32 devices in a mesh: dp: 8 (over z, core), tensor: 4 (over y, x).
Axes of the slice: x: 2, y: 2, z: 4, core: 2. Of those that a mesh axis runs over, the one named last changes fastest.
Arguments:
- layer_in: bfloat16 [8192, 2304], P(('dp', 'tensor')), may hold values from -6 to 6
- cotangent: bfloat16 [8192, 2304], P(('dp', 'tensor')), may hold values from -6 to 6
- lengths: int32 [8], P('dp'), may hold values from 256 to 1024, as said below
- adapter_ids: int32 [8, 1], P('dp'), may hold values from 0 to 7
- norm_gains: float32 [4, 2304], replicated, may hold values from 0.1 to 1.9
- query_weight: bfloat16 [2304, 2048], P('dp', 'tensor'), may hold values from -0.125 to 0.125
- key_weight: bfloat16 [2304, 1024], P('dp'), may hold values from -0.125 to 0.125
- value_weight: bfloat16 [2304, 1024], P('dp'), may hold values from -0.125 to 0.125
- out_weight: bfloat16 [2048, 2304], P('tensor', 'dp'), may hold values from -0.125 to 0.125
- gate_weight: bfloat16 [2304, 9216], P('dp', 'tensor'), may hold values from -0.125 to 0.125
- up_weight: bfloat16 [2304, 9216], P('dp', 'tensor'), may hold values from -0.125 to 0.125
- down_weight: bfloat16 [9216, 2304], P('tensor', 'dp'), may hold values from -0.0625 to 0.0625
- adapt_in: bfloat16 [8, 2304, 80], P(None, ('dp', 'tensor')), may hold values from -0.125 to 0.125
- adapt_heads: bfloat16 [8, 2048, 16], P(None, ('dp', 'tensor')), may hold values from -0.125 to 0.125
- adapt_hidden: bfloat16 [8, 9216, 16], P(None, ('dp', 'tensor')), may hold values from -0.0625 to 0.0625
- lift_query: bfloat16 [8, 16, 2048], P(None, None, ('dp', 'tensor')), may hold values from -0.75 to 0.75
- lift_keyval: bfloat16 [8, 2, 16, 1024], P(None, None, None, ('dp', 'tensor')), may hold values from -0.75 to 0.75
- lift_gateup: bfloat16 [8, 2, 16, 9216], P(None, None, None, ('dp', 'tensor')), may hold values from -0.75 to 0.75
- lift_resid: bfloat16 [8, 2, 16, 2304], P(None, None, None, ('dp', 'tensor')), may hold values from -0.75 to 0.75
Outputs:
- layer_out: bfloat16 [8192, 2304], P(('dp', 'tensor'))
- input_grad: bfloat16 [8192, 2304], P(('dp', 'tensor'))
- adapt_in_grad: float32 [8, 2304, 80], P(None, ('dp', 'tensor'))
- adapt_heads_grad: float32 [8, 2048, 16], P(None, ('dp', 'tensor'))
- adapt_hidden_grad: float32 [8, 9216, 16], P(None, ('dp', 'tensor'))
- lift_query_grad: float32 [8, 16, 2048], P(None, None, ('dp', 'tensor'))
- lift_keyval_grad: float32 [8, 2, 16, 1024], P(None, None, None, ('dp', 'tensor'))
- lift_gateup_grad: float32 [8, 2, 16, 9216], P(None, None, None, ('dp', 'tensor'))
- lift_resid_grad: float32 [8, 2, 16, 2304], P(None, None, None, ('dp', 'tensor'))
The draws below stay inside these ranges and needn't reach their ends.
Inputs may be any that keep to these rules, and one draw needn't show every extreme that they name: `lengths`: a sequence's real tokens stand at its start and the rest of its 1024 slots are padding; at least one sequence is full. `adapter_ids`: one adapter per sequence; every one of the 8 adapters serves some sequence.
All inputs are finite; a program needn't handle non-finite values.
Results may differ from the reference program's by a relative error of at most 0.025.
Values may be sent and summed in bfloat16 or wider, within the bound.
A program may use at most 320 MiB of HBM per device.

```python
import jax
import jax.numpy as jnp
from jax import lax

D = 2304
HQ = 8
KV = 4
HD = 256
FF = 9216
NA = 8
ADAPTER_RANK = 16
LEN = 1024
NSEQ = 8
TOKENS = 8192


def draw_lengths(key, part):
    drawn = jax.random.randint(key, (NSEQ,), LEN // 4, LEN + 1)
    return drawn.at[0].set(LEN).astype(jnp.int32)


def block_levels(key, dims, cuts, least, largest):
    def one(dim, blocks):
        steps = jax.random.uniform(jax.random.fold_in(jax.random.fold_in(key, 6), dim), (blocks,), jnp.float32, least / len(cuts), largest / len(cuts))
        return jnp.repeat(jnp.exp(steps), dims[dim] // blocks).reshape((-1,) + (1,) * (len(dims) - dim - 1))

    level = one(*cuts[0])
    for cut in cuts[1:]:
        level = level * one(*cut)
    return level


def choose_distinct(rng, rows, number_of, top, lift):
    ranking = jax.random.permutation(jax.random.fold_in(rng, 1), number_of)
    favour = ranking
    for power in range(3):
        favour = favour * favour // number_of
    favour = favour * lift // number_of
    lots = jax.random.randint(jax.random.fold_in(rng, 2), (rows, number_of), 0, 4096) + favour
    fixed_rows = jax.random.permutation(jax.random.fold_in(rng, 3), rows)[jnp.arange(number_of) % rows]
    lots = jnp.where(jnp.arange(rows)[:, None] == fixed_rows[None, :], 1 << 14, lots)
    merit = lots * number_of + jnp.arange(number_of)
    return lax.top_k(merit.astype(jnp.int32), top)[1].astype(jnp.int32)


def gaussian(stream_key, extent, scale, limit, cuts=(), kind=jnp.bfloat16):
    values = jax.random.normal(stream_key, extent, jnp.float32) * scale
    if len(cuts) > 0:
        values = block_levels(stream_key, extent, cuts, -0.22, 0.18) * values
    return jnp.clip(values, min=-limit, max=limit).astype(kind)


def setup_inputs(seed: int = 0) -> dict:
    splits = jax.random.split(jax.random.key(seed), 20)
    layer_in = gaussian(splits[0], (TOKENS, D), 1.0, 6.0, ((0, 32),))
    cotangent = gaussian(splits[1], (TOKENS, D), 1.0, 6.0, ((0, 32),))
    lengths = draw_lengths(jax.random.fold_in(splits[19], 71), 0)
    adapter_ids = choose_distinct(splits[3], NSEQ, NA, 1, 0)
    norm_gains = jnp.clip(1.0 + 0.18 * jax.random.normal(splits[4], (4, D), jnp.float32), 0.1, 1.9)
    query_weight = gaussian(splits[5], (D, HQ * HD), D ** -0.5, 0.125, ((0, 8), (1, 4)))
    key_weight = gaussian(splits[6], (D, KV * HD), D ** -0.5, 0.125, ((0, 8),))
    value_weight = gaussian(splits[7], (D, KV * HD), D ** -0.5, 0.125, ((0, 8),))
    out_weight = gaussian(splits[8], (HQ * HD, D), (HQ * HD) ** -0.5, 0.125, ((0, 4), (1, 8)))
    gate_weight = gaussian(splits[9], (D, FF), D ** -0.5, 0.125, ((0, 8), (1, 4)))
    up_weight = gaussian(splits[10], (D, FF), D ** -0.5, 0.125, ((0, 8), (1, 4)))
    down_weight = gaussian(splits[11], (FF, D), FF ** -0.5, 0.0625, ((0, 4), (1, 8)))
    adapt_in = gaussian(splits[12], (NA, D, 5 * ADAPTER_RANK), D ** -0.5, 0.125, ((1, 32),))
    adapt_heads = gaussian(splits[13], (NA, HQ * HD, ADAPTER_RANK), (HQ * HD) ** -0.5, 0.125, ((1, 32),))
    adapt_hidden = gaussian(splits[14], (NA, FF, ADAPTER_RANK), FF ** -0.5, 0.0625, ((1, 32),))
    lift_query = gaussian(splits[15], (NA, ADAPTER_RANK, HQ * HD), (4 * ADAPTER_RANK) ** -0.5, 0.75, ((2, 32),))
    lift_keyval = gaussian(splits[16], (NA, 2, ADAPTER_RANK, KV * HD), (4 * ADAPTER_RANK) ** -0.5, 0.75, ((3, 32),))
    lift_gateup = gaussian(splits[17], (NA, 2, ADAPTER_RANK, FF), (4 * ADAPTER_RANK) ** -0.5, 0.75, ((3, 32),))
    lift_resid = gaussian(splits[18], (NA, 2, ADAPTER_RANK, D), (4 * ADAPTER_RANK) ** -0.5, 0.75, ((3, 32),))
    return {"layer_in": layer_in, "cotangent": cotangent, "lengths": lengths, "adapter_ids": adapter_ids, "norm_gains": norm_gains, "query_weight": query_weight, "key_weight": key_weight, "value_weight": value_weight, "out_weight": out_weight, "gate_weight": gate_weight, "up_weight": up_weight, "down_weight": down_weight, "adapt_in": adapt_in, "adapt_heads": adapt_heads, "adapt_hidden": adapt_hidden, "lift_query": lift_query, "lift_keyval": lift_keyval, "lift_gateup": lift_gateup, "lift_resid": lift_resid}


EPSILON = 1e-06
SOFT_CAP = 50.0
MASKED = -1e+30
FULL_PRECISION = lax.Precision.HIGHEST

@jax.custom_vjp
def rank_projection(v):
    return lax.optimization_barrier(v.astype(jnp.bfloat16)).astype(jnp.float32)

@jax.custom_vjp
def rank_projection_back(v):
    return v

def low_keep(v):
    return (rank_projection(v), None)

def low_pass(kept, grad):
    return (grad,)

def back_keep(v):
    return (v, None)

def back_low(kept, grad):
    return (rank_projection(grad),)
rank_projection.defvjp(low_keep, low_pass)
rank_projection_back.defvjp(back_keep, back_low)

def rms_norm(values, gain_row):
    return values * lax.rsqrt(lax.optimization_barrier(jnp.mean(values * values, axis=-1, keepdims=True)) + EPSILON) * gain_row

def tables(length, size):
    half_size = size // 2
    frequency = 10000.0 ** (-2.0 * jnp.arange(half_size, dtype=jnp.float32) / size)
    angles = jnp.arange(length, dtype=jnp.float32)[:, None] * frequency[None, :]
    return (jnp.cos(angles)[:, None, :], jnp.sin(angles)[:, None, :])

def rotate(values, cosine, sine):
    half_size = values.shape[-1] // 2
    first_half = values[..., :half_size]
    second_half = values[..., half_size:]
    return jnp.concatenate([first_half * cosine - second_half * sine, second_half * cosine + first_half * sine], axis=-1)

def attend(inputs):
    queries, keys, values, key_ok = inputs
    length = queries.shape[0]
    raw_scores = rank_projection_back(jnp.einsum('qhd,khd->hqk', queries, keys, precision=FULL_PRECISION))
    capped = SOFT_CAP * jnp.tanh(raw_scores / SOFT_CAP)
    causal = jnp.arange(length)[:, None] >= jnp.arange(length)[None, :]
    allowed = causal[None] & key_ok[None, None, :]
    softmax_out = rank_projection(jax.nn.softmax(jnp.where(allowed, capped, MASKED), axis=-1))
    return jnp.einsum('hqk,khd->qhd', softmax_out, values, precision=FULL_PRECISION)

def pick_adapter(onehot, table_in):
    return jnp.einsum('sa,a...->s...', onehot, table_in, precision=FULL_PRECISION)

def block_forward(layer_in, adapters, frozen, onehot, key_ok, valid_rows):
    adapt_in, adapt_heads, adapt_hidden, lift_query, lift_keyval, lift_gateup, lift_resid = adapters
    gains, w_query, w_key, w_value, output_matrix, gate_matrix, up_matrix, down_matrix = frozen
    seq_count = layer_in.shape[0]
    length = layer_in.shape[1]
    attention_input_normed = rank_projection(rms_norm(layer_in, gains[0]))
    select_input_adapter = pick_adapter(onehot, adapt_in)
    rank_query_key_value = rank_projection(rank_projection_back(jnp.einsum('xpt,xtv->xpv', attention_input_normed, select_input_adapter[:, :, :3 * ADAPTER_RANK], precision=FULL_PRECISION)))
    pick_query = pick_adapter(onehot, lift_query)
    pick_keyval = pick_adapter(onehot, lift_keyval)

    def project(weight_matrix, lift_table, low_rows):
        dense_portion = jnp.einsum('rti,iv->rtv', attention_input_normed, weight_matrix, precision=FULL_PRECISION)
        return dense_portion + jnp.einsum('slr,sre->sle', low_rows, lift_table, precision=FULL_PRECISION)
    query_pre = rank_projection_back(project(w_query, pick_query, rank_query_key_value[..., :ADAPTER_RANK]).reshape(seq_count, length, HQ, HD))
    key_pre = project(w_key, pick_keyval[:, 0], rank_query_key_value[..., ADAPTER_RANK:2 * ADAPTER_RANK]).reshape(seq_count, length, KV, HD)
    value_pre = project(w_value, pick_keyval[:, 1], rank_query_key_value[..., 2 * ADAPTER_RANK:]).reshape(seq_count, length, KV, HD)
    key_pre = rank_projection_back(jnp.repeat(key_pre, HQ // KV, axis=2))
    value_pre = rank_projection_back(jnp.repeat(value_pre, HQ // KV, axis=2))
    cosine, sine = tables(length, HD)
    queries = rank_projection(rotate(query_pre, cosine, sine) * HD ** (-0.5))
    keys = rank_projection(rotate(key_pre, cosine, sine))
    values = rank_projection(value_pre)
    attention_output = lax.map(jax.checkpoint(attend), (queries, keys, values, key_ok))
    attention_output = rank_projection(rank_projection_back(attention_output.reshape(seq_count, length, HQ * HD)))
    rank_output_projection = rank_projection(rank_projection_back(jnp.einsum('sle,ser->slr', attention_output, pick_adapter(onehot, adapt_heads), precision=FULL_PRECISION)))
    select_residual_adapter = pick_adapter(onehot, lift_resid)
    attention_total = jnp.einsum('bok,ki->boi', attention_output, output_matrix, precision=FULL_PRECISION)
    attention_total = rank_projection_back(attention_total + jnp.einsum('ypm,ymn->ypn', rank_output_projection, select_residual_adapter[:, 0], precision=FULL_PRECISION))
    resid_mid = layer_in + rms_norm(attention_total, gains[1])
    feedforward_input_normed = rank_projection(rms_norm(resid_mid, gains[2]))
    rank_gate_up_projection = rank_projection(rank_projection_back(jnp.einsum('xpt,xtv->xpv', feedforward_input_normed, select_input_adapter[:, :, 3 * ADAPTER_RANK:], precision=FULL_PRECISION)))
    pick_gu = pick_adapter(onehot, lift_gateup)
    gate_preactivation = jnp.einsum('zvp,pj->zvj', feedforward_input_normed, gate_matrix, precision=FULL_PRECISION)
    gate_preactivation = rank_projection_back(gate_preactivation + jnp.einsum('slr,srf->slf', rank_gate_up_projection[..., :ADAPTER_RANK], pick_gu[:, 0], precision=FULL_PRECISION))
    up_preactivation = jnp.einsum('zvp,pj->zvj', feedforward_input_normed, up_matrix, precision=FULL_PRECISION)
    up_preactivation = rank_projection_back(up_preactivation + jnp.einsum('slr,srf->slf', rank_gate_up_projection[..., ADAPTER_RANK:], pick_gu[:, 1], precision=FULL_PRECISION))
    hidden_state = rank_projection(jax.nn.gelu(gate_preactivation, approximate=True) * up_preactivation)
    rank_down_projection = rank_projection(rank_projection_back(jnp.einsum('slf,sfr->slr', hidden_state, pick_adapter(onehot, adapt_hidden), precision=FULL_PRECISION)))
    feedforward_total = jnp.einsum('rgw,wo->rgo', hidden_state, down_matrix, precision=FULL_PRECISION)
    feedforward_total = rank_projection_back(feedforward_total + jnp.einsum('ypm,ymn->ypn', rank_down_projection, select_residual_adapter[:, 1], precision=FULL_PRECISION))
    return valid_rows * (resid_mid + rms_norm(feedforward_total, gains[3]))

def reference(layer_in, cotangent, lengths, adapter_ids, norm_gains, query_weight, key_weight, value_weight, out_weight, gate_weight, up_weight, down_weight, adapt_in, adapt_heads, adapt_hidden, lift_query, lift_keyval, lift_gateup, lift_resid):
    frozen = (norm_gains.astype(jnp.float32), query_weight.astype(jnp.float32), key_weight.astype(jnp.float32), value_weight.astype(jnp.float32), out_weight.astype(jnp.float32), gate_weight.astype(jnp.float32), up_weight.astype(jnp.float32), down_weight.astype(jnp.float32))
    adapters = (adapt_in.astype(jnp.float32), adapt_heads.astype(jnp.float32), adapt_hidden.astype(jnp.float32), lift_query.astype(jnp.float32), lift_keyval.astype(jnp.float32), lift_gateup.astype(jnp.float32), lift_resid.astype(jnp.float32))
    block_seqs = 4
    block_count = NSEQ // block_seqs
    blocks_in = layer_in.astype(jnp.float32).reshape(block_count, block_seqs, LEN, D)
    blocks_cot = cotangent.astype(jnp.float32).reshape(block_count, block_seqs, LEN, D)
    block_lengths = lengths.reshape(block_count, block_seqs)
    block_ids = adapter_ids.reshape(block_count, block_seqs)

    def block_step(carried, inputs):
        values_in, values_cot, length_row, id_row = inputs
        onehot = (id_row[:, None] == jnp.arange(NA, dtype=jnp.int32)[None, :]).astype(jnp.float32)
        key_ok = jnp.arange(LEN, dtype=jnp.int32)[None, :] < length_row[:, None]
        valid_rows = key_ok.astype(jnp.float32)[..., None]

        def forward_fn(inner_value, *inner_adapters):
            return block_forward(inner_value, inner_adapters, frozen, onehot, key_ok, valid_rows)
        output_value, pullback = jax.vjp(forward_fn, values_in, *adapters)
        gradients = pullback(values_cot)
        updated = tuple((carried_one + grad_one for carried_one, grad_one in zip(carried, gradients[1:])))
        return (updated, (output_value.astype(jnp.bfloat16), gradients[0].astype(jnp.bfloat16)))
    initial = tuple((jnp.zeros(table_one.shape, jnp.float32) for table_one in adapters))
    totals, outputs = lax.scan(block_step, initial, (blocks_in, blocks_cot, block_lengths, block_ids))
    return (outputs[0].reshape(TOKENS, D), outputs[1].reshape(TOKENS, D), totals[0], totals[1], totals[2], totals[3], totals[4], totals[5], totals[6])
```

```python
import functools

import jax
import jax.numpy as jnp
from jax import lax
from jax.experimental import pallas as pl
from jax.experimental.pallas import tpu as pltpu
from jax.sharding import PartitionSpec as P

D = 2304
HQ = 8
KV = 4
HD = 256
FF = 9216
NA = 8
RANK = 16
LEN = 1024
LANES = 128

EPSILON = 1e-06
SOFT_CAP = 50.0
MESH = pl.DeviceIdType.MESH
BF16 = jnp.bfloat16
F32 = jnp.float32
VMEM_LIMIT = 48 * 1024 * 1024


def rms_norm(values, gain_row):
    return (
        values * lax.rsqrt(jnp.mean(values * values, axis=-1, keepdims=True) + EPSILON) * gain_row
    )


def norm_back(values, gain_row, gradient):
    inverse = lax.rsqrt(jnp.mean(values * values, axis=-1, keepdims=True) + EPSILON)
    scaled = gradient * gain_row
    normed = values * inverse
    return inverse * (scaled - normed * jnp.mean(scaled * normed, axis=-1, keepdims=True))


def gated_gelu(gate_in, up_in):
    return jax.nn.gelu(gate_in, approximate=True) * up_in


def tables(length, size):
    half_size = size // 2
    frequency = 10000.0 ** (-2.0 * jnp.arange(half_size, dtype=F32) / size)
    angles = jnp.arange(length, dtype=F32)[:, None] * frequency[None, :]
    return (jnp.cos(angles)[:, None, :], jnp.sin(angles)[:, None, :])


def rotate(values, cosine, sine):
    half_size = values.shape[-1] // 2
    first_half = values[..., :half_size]
    second_half = values[..., half_size:]
    return jnp.concatenate(
        [first_half * cosine - second_half * sine, second_half * cosine + first_half * sine],
        axis=-1,
    )


def nn(a, b):
    return lax.dot_general(a, b, (((1,), (0,)), ((), ())), preferred_element_type=F32)


def nt(a, b):
    return lax.dot_general(a, b, (((1,), (1,)), ((), ())), preferred_element_type=F32)


def tn(a, b):
    return lax.dot_general(a, b, (((0,), (0,)), ((), ())), preferred_element_type=F32)


def pad_lanes(values):
    return jnp.pad(values, [(0, 0)] * (values.ndim - 1) + [(0, LANES - values.shape[-1])])


def greet(peers):
    barrier = pltpu.get_barrier_semaphore()
    for peer in peers:
        pl.semaphore_signal(barrier, inc=1, device_id=peer, device_id_type=MESH)
    pl.semaphore_wait(barrier, len(peers))


def square_peers(index):
    return index + 1 - 2 * lax.rem(index, 2), lax.rem(index + 2, 4), 3 - index


def remote(source, target, send_sem, recv_sem, peer):
    return pltpu.make_async_remote_copy(
        src_ref=source,
        dst_ref=target,
        send_sem=send_sem,
        recv_sem=recv_sem,
        device_id={"tensor": peer},
        device_id_type=MESH,
    )


def gather_kernel(count, rows, x_ref, o_ref, local_sem, send_sem, recv_sem):
    me = lax.axis_index("tensor")
    if count == 4:
        across, down, _ = square_peers(me)
        greet([{"tensor": across}, {"tensor": down}])
        own = pltpu.make_async_copy(x_ref, o_ref.at[pl.ds(me * rows, rows)], local_sem)
        own.start()
        half = rows // 2
        links = (across, down)
        first = [[None, None], [None, None]]
        for order in range(2):
            for link in range(2):
                part = order if link == 0 else 1 - order
                target = o_ref.at[pl.ds(me * rows + part * half, half)]
                copy = remote(
                    x_ref.at[pl.ds(part * half, half)],
                    target,
                    send_sem.at[link, part],
                    recv_sem.at[link, part],
                    links[link],
                )
                copy.start()
                first[link][part] = copy
        second = []
        for link in range(2):
            first[link][link].wait_recv()
            block = o_ref.at[pl.ds(links[link] * rows + link * half, half)]
            copy = remote(
                block, block, send_sem.at[2, link], recv_sem.at[2, link], links[1 - link]
            )
            copy.start()
            second.append(copy)
        for link in range(2):
            first[link][1 - link].wait_recv()
        for copy in second:
            copy.wait_recv()
        own.wait()
        for link in range(2):
            for part in range(2):
                first[link][part].wait_send()
        for copy in second:
            copy.wait_send()
    else:
        peers = [lax.rem(me + step, count) for step in range(1, count)]
        greet([{"tensor": peer} for peer in peers])
        own = pltpu.make_async_copy(x_ref, o_ref.at[pl.ds(me * rows, rows)], local_sem)
        own.start()
        copies = []
        for step, peer in enumerate(peers):
            copy = remote(
                x_ref,
                o_ref.at[pl.ds(me * rows, rows)],
                send_sem.at[0, step],
                recv_sem.at[0, step],
                peer,
            )
            copy.start()
            copies.append(copy)
        own.wait()
        for copy in copies:
            copy.wait()


def tensor_gather(values, count):
    rows, width = values.shape
    slots = max(2, count - 1)
    return pl.pallas_call(
        functools.partial(gather_kernel, count, rows),
        out_shape=jax.ShapeDtypeStruct((count * rows, width), values.dtype),
        in_specs=[pl.BlockSpec(memory_space=pl.ANY)],
        out_specs=pl.BlockSpec(memory_space=pl.ANY),
        scratch_shapes=[
            pltpu.SemaphoreType.DMA,
            pltpu.SemaphoreType.DMA((3, slots)),
            pltpu.SemaphoreType.DMA((3, slots)),
        ],
        compiler_params=pltpu.CompilerParams(
            collective_id=1, has_side_effects=True, vmem_limit_bytes=VMEM_LIMIT
        ),
        name="tensor_gather",
    )(values)


def scatter_kernel(count, rows, p_ref, q_ref, o_ref, l_ref, *scratch):
    me = lax.axis_index("tensor")
    payload = ((p_ref, o_ref), (q_ref, l_ref))
    if count == 4:
        across, down, far = square_peers(me)
        greet([{"tensor": across}, {"tensor": down}])
        half = rows // 2
        first = scratch[0:2]
        sums = scratch[2:4]
        second = scratch[4:6]
        send_sem, recv_sem = scratch[6], scratch[7]
        links = (across, down)
        copies = {}
        for which in (1, 0):
            for link in range(2):
                block = far if which == 1 else links[link]
                for item in range(2):
                    copy = remote(
                        payload[item][0].at[pl.ds(block * rows + link * half, half)],
                        first[item].at[link, which],
                        send_sem.at[item, link, which],
                        recv_sem.at[item, link, which],
                        links[link],
                    )
                    copy.start()
                    copies[item, link, which] = copy
        for link in range(2):
            block = links[1 - link]
            for item in range(2):
                copies[item, link, 1].wait_recv()
                mine = payload[item][0][pl.ds(block * rows + link * half, half), :]
                sums[item][link] = (
                    mine.astype(F32) + first[item][link, 1].astype(F32)
                ).astype(BF16)
                copy = remote(
                    sums[item].at[link],
                    second[item].at[link],
                    send_sem.at[item, link, 2],
                    recv_sem.at[item, link, 2],
                    links[1 - link],
                )
                copy.start()
                copies[item, link, 2] = copy
        for link in range(2):
            for item in range(2):
                copies[item, link, 0].wait_recv()
                mine = payload[item][0][pl.ds(me * rows + link * half, half), :]
                payload[item][1][pl.ds(link * half, half), :] = mine.astype(F32) + first[item][
                    link, 0
                ].astype(F32)
        for link in range(2):
            for item in range(2):
                copies[item, link, 2].wait_recv()
                payload[item][1][pl.ds(link * half, half), :] += second[item][link].astype(F32)
        for copy in copies.values():
            copy.wait_send()
    else:
        peers = [lax.rem(me + step, count) for step in range(1, count)]
        greet([{"tensor": peer} for peer in peers])
        first = scratch[0:2]
        send_sem, recv_sem = scratch[2], scratch[3]
        copies = []
        for step, peer in enumerate(peers):
            for item in range(2):
                copy = remote(
                    payload[item][0].at[pl.ds(peer * rows, rows)],
                    first[item].at[step],
                    send_sem.at[item, step],
                    recv_sem.at[item, step],
                    peer,
                )
                copy.start()
                copies.append((item, step, copy))
        for item in range(2):
            payload[item][1][...] = payload[item][0][pl.ds(me * rows, rows), :].astype(F32)
        for item, step, copy in copies:
            copy.wait()
            payload[item][1][...] += first[item][step].astype(F32)


def tensor_scatter(values, narrow, count):
    rows = values.shape[0] // count
    widths = (values.shape[1], narrow.shape[1])
    if count == 4:
        half = rows // 2
        scratch = [pltpu.VMEM((2, 2, half, width), BF16) for width in widths]
        scratch += [pltpu.VMEM((2, half, width), BF16) for width in widths]
        scratch += [pltpu.VMEM((2, half, width), BF16) for width in widths]
        scratch += [pltpu.SemaphoreType.DMA((2, 2, 3)), pltpu.SemaphoreType.DMA((2, 2, 3))]
    else:
        scratch = [pltpu.VMEM((count - 1, rows, width), BF16) for width in widths]
        scratch += [pltpu.SemaphoreType.DMA((2, count - 1))] * 2
    vmem = pl.BlockSpec(memory_space=pltpu.VMEM)
    return pl.pallas_call(
        functools.partial(scatter_kernel, count, rows),
        out_shape=tuple(jax.ShapeDtypeStruct((rows, width), F32) for width in widths),
        in_specs=[vmem, vmem],
        out_specs=(vmem, vmem),
        scratch_shapes=scratch,
        compiler_params=pltpu.CompilerParams(
            collective_id=2, has_side_effects=True, vmem_limit_bytes=VMEM_LIMIT
        ),
        name="tensor_scatter",
    )(values, narrow)


class Layout:
    def __init__(self):
        self.dp = lax.axis_size("dp")
        self.tensor = lax.axis_size("tensor")
        self.total = self.dp * self.tensor
        self.d = lax.axis_index("dp")
        self.t = lax.axis_index("tensor")
        self.me = self.d * self.tensor + self.t
        self.heads_here = HQ // self.tensor
        self.ratio = HQ // KV
        self.share = max(1, self.tensor // KV)
        self.kv_owners = self.total // KV
        self.kv_head = self.t * self.heads_here // self.ratio
        self.user = self.me // self.dp
        self.kv_slice_head = self.me // self.kv_owners

    def device(self, flat):
        return {"dp": flat // self.tensor, "tensor": lax.rem(flat, self.tensor)}


def greet_all(lay):
    barrier = pltpu.get_barrier_semaphore()

    def signal(step, unused):
        peer = lax.rem(lay.me + step, lay.total)
        pl.semaphore_signal(
            barrier, inc=1, device_id=lay.device(peer), device_id_type=MESH
        )
        return unused

    lax.fori_loop(1, lay.total, signal, 0)
    pl.semaphore_wait(barrier, lay.total - 1)


def send_or_keep(lay, sends, source, target, send_sem, recv_sem, flat, maybe_own):
    def far():
        return pltpu.make_async_remote_copy(
            src_ref=source,
            dst_ref=target,
            send_sem=send_sem,
            recv_sem=recv_sem,
            device_id=lay.device(flat),
            device_id_type=MESH,
        )

    if maybe_own is None:
        copy = far()
        copy.start()
        sends.append((None, copy))
        return

    @pl.when(maybe_own)
    def _():
        pltpu.make_async_copy(source, target, recv_sem).start()

    @pl.when(jnp.logical_not(maybe_own))
    def _():
        far().start()

    sends.append((maybe_own, far()))


def finish(sends, received):
    for own, copy in sends:
        if own is None:
            copy.wait_send()
        else:

            @pl.when(jnp.logical_not(own))
            def _(copy=copy):
                copy.wait_send()

    for target, sem in received:
        pltpu.make_async_copy(target, target, sem).wait()


def tables_kernel(d_ref, f_ref, h_ref, k_ref, do_ref, fo_ref, ho_ref, ko_ref, *sems):
    lay = Layout()
    send_sems, recv_sem = sems[:4], sems[4]
    greet_all(lay)
    sends = []
    for step in range(lay.dp):
        group = lax.rem(lay.d + step, lay.dp)
        flat = group * lay.tensor + lay.user
        own = (lay.user == lay.t) if step == 0 else None
        for item, (source, target) in enumerate(((f_ref, fo_ref), (h_ref, ho_ref))):
            send_or_keep(
                lay,
                sends,
                source.at[group],
                target.at[lax.rem(lay.me, lay.dp)],
                send_sems[item].at[step],
                recv_sem.at[item],
                flat,
                own,
            )
        for extra in range(lay.share):
            user = lay.kv_slice_head * lay.share + extra
            flat = group * lay.tensor + user
            send_or_keep(
                lay,
                sends,
                k_ref.at[group],
                ko_ref.at[lax.rem(lay.me, lay.kv_owners)],
                send_sems[2].at[step, extra],
                recv_sem.at[2],
                flat,
                (user == lay.t) if step == 0 else None,
            )
    pltpu.make_async_copy(d_ref.at[lay.d], do_ref.at[lay.me], recv_sem.at[3]).start()
    for step in range(1, lay.total):
        flat = lax.rem(lay.me + step, lay.total)
        send_or_keep(
            lay,
            sends,
            d_ref.at[flat // lay.tensor],
            do_ref.at[lay.me],
            send_sems[3].at[step],
            recv_sem.at[3],
            flat,
            None,
        )
    finish(
        sends,
        (
            (fo_ref, recv_sem.at[0]),
            (ho_ref, recv_sem.at[1]),
            (ko_ref, recv_sem.at[2]),
            (do_ref, recv_sem.at[3]),
        ),
    )


def grads_kernel(d_ref, f_ref, h_ref, k_ref, do_ref, fo_ref, ho_ref, ko_ref, *sems):
    lay = Layout()
    send_sems, recv_sem = sems[:4], sems[4]
    greet_all(lay)
    sends = []
    for step in range(lay.dp):
        slot = lax.rem(lay.d + step, lay.dp)
        flat = lay.t * lay.dp + slot
        for item, (source, target) in enumerate(((f_ref, fo_ref), (h_ref, ho_ref))):
            send_or_keep(
                lay,
                sends,
                source.at[slot],
                target.at[lay.d],
                send_sems[item].at[step],
                recv_sem.at[item],
                flat,
                flat == lay.me,
            )
    for step in range(lay.kv_owners):
        slot = lax.rem(lay.d + step, lay.kv_owners)
        flat = lay.kv_head * lay.kv_owners + slot
        send_or_keep(
            lay,
            sends,
            k_ref.at[slot],
            ko_ref.at[lay.d * lay.share + lax.rem(lay.t, lay.share)],
            send_sems[2].at[step // lay.share, step % lay.share],
            recv_sem.at[2],
            flat,
            flat == lay.me,
        )
    pltpu.make_async_copy(d_ref.at[lay.me], do_ref.at[lay.me], recv_sem.at[3]).start()
    for step in range(1, lay.total):
        flat = lax.rem(lay.me + step, lay.total)
        send_or_keep(
            lay,
            sends,
            d_ref.at[flat],
            do_ref.at[lay.me],
            send_sems[3].at[step],
            recv_sem.at[3],
            flat,
            None,
        )
    finish(
        sends,
        (
            (fo_ref, recv_sem.at[0]),
            (ho_ref, recv_sem.at[1]),
            (ko_ref, recv_sem.at[2]),
            (do_ref, recv_sem.at[3]),
        ),
    )


def exchange(kernel, name, number, arrays, outs, dp, total, share):
    anywhere = pl.BlockSpec(memory_space=pl.ANY)
    return pl.pallas_call(
        kernel,
        out_shape=tuple(jax.ShapeDtypeStruct(shape, BF16) for shape in outs),
        in_specs=[anywhere] * 4,
        out_specs=(anywhere,) * 4,
        scratch_shapes=[
            pltpu.SemaphoreType.DMA((dp,)),
            pltpu.SemaphoreType.DMA((dp,)),
            pltpu.SemaphoreType.DMA((dp, share)),
            pltpu.SemaphoreType.DMA((total,)),
            pltpu.SemaphoreType.DMA((4,)),
        ],
        compiler_params=pltpu.CompilerParams(
            collective_id=number, has_side_effects=True, vmem_limit_bytes=VMEM_LIMIT
        ),
        name=name,
    )(*arrays)


def per_device(
    layer_in,
    cotangent,
    lengths,
    adapter_ids,
    norm_gains,
    query_weight,
    key_weight,
    value_weight,
    out_weight,
    gate_weight,
    up_weight,
    down_weight,
    adapt_in,
    adapt_heads,
    adapt_hidden,
    lift_query,
    lift_keyval,
    lift_gateup,
    lift_resid,
):
    lay = Layout()
    count = lay.tensor
    rows = layer_in.shape[0]
    group_rows = rows * count
    assert lengths.shape[0] == 1 and group_rows == LEN
    heads_here = lay.heads_here
    head_width = heads_here * HD
    hidden_here = FF // count
    assert lay.ratio % heads_here == 0

    key_cols = lax.dynamic_slice_in_dim(key_weight, lay.kv_head * HD, HD, 1)
    value_cols = lax.dynamic_slice_in_dim(value_weight, lay.kv_head * HD, HD, 1)
    attn_shard = jnp.concatenate([query_weight, key_cols, value_cols, out_weight.T], axis=1)
    attn_w = lax.all_gather(attn_shard, "dp", axis=0, tiled=True)
    gate_up_shard = jnp.concatenate([gate_weight, up_weight], axis=1)
    down_shard = down_weight.T
    attn_shard, gate_up_shard, down_shard = lax.optimization_barrier(
        (attn_shard, gate_up_shard, down_shard)
    )
    gate_up_w = lax.all_gather(gate_up_shard, "dp", axis=0, tiled=True)
    down_w = lax.all_gather(down_shard, "dp", axis=0, tiled=True)
    qkv_width = head_width + 2 * HD

    all_ids = lax.all_gather(adapter_ids[:, 0], "dp", axis=0, tiled=True)
    group_hot = (all_ids[:, None] == jnp.arange(NA, dtype=jnp.int32)[None, :]).astype(BF16)

    def rows_of(table):
        moved = jnp.moveaxis(table, -1, 1)
        return moved.reshape(NA, moved.shape[1], -1)

    def choose(*parts):
        packed = pad_lanes(jnp.concatenate(parts, axis=-1))
        return lax.dot_general(
            group_hot, packed, (((1,), (0,)), ((), ())), preferred_element_type=F32
        ).astype(BF16)

    d_send = choose(adapt_in, rows_of(lift_resid))
    f_send = choose(adapt_hidden, rows_of(lift_gateup))
    h_send = choose(adapt_heads, rows_of(lift_query))
    k_send = choose(rows_of(lift_keyval))
    d_rows, f_rows, h_rows, k_rows = (item.shape[1] for item in (d_send, f_send, h_send, k_send))
    d_tab, f_tab, h_tab, k_tab = exchange(
        tables_kernel,
        "adapter_tables",
        3,
        (d_send, f_send, h_send, k_send),
        (
            (lay.total, d_rows, LANES),
            (lay.dp, f_rows, LANES),
            (lay.dp, h_rows, LANES),
            (lay.kv_owners, k_rows, LANES),
        ),
        lay.dp,
        lay.total,
        lay.share,
    )
    d_tab = d_tab.reshape(D, LANES)
    f_tab = f_tab.reshape(hidden_here, LANES)
    h_tab = h_tab.reshape(head_width, LANES)
    k_tab = k_tab.reshape(HD, LANES)
    in_qkv, in_gu = d_tab[:, : 3 * RANK], d_tab[:, 3 * RANK : 5 * RANK]
    lift_out, lift_down = d_tab[:, 5 * RANK : 6 * RANK], d_tab[:, 6 * RANK : 7 * RANK]
    map_hidden, lift_gate, lift_up = (f_tab[:, i * RANK : (i + 1) * RANK] for i in range(3))
    map_heads, lift_q = h_tab[:, :RANK], h_tab[:, RANK : 2 * RANK]
    lift_k, lift_v = k_tab[:, :RANK], k_tab[:, RANK : 2 * RANK]

    row_start = lay.t * rows
    length = lengths[0]
    row_valid = ((row_start + jnp.arange(rows, dtype=jnp.int32)) < length).astype(F32)[:, None]
    cosine, sine = tables(LEN, HD)
    place = jnp.arange(LEN, dtype=jnp.int32)
    allowed = (place[:, None] >= place[None, :]) & (place[None, :] < length)

    resid_in = layer_in.astype(F32)
    normed_attn = rms_norm(resid_in, norm_gains[0]).astype(BF16)
    seq_attn = tensor_gather(normed_attn, count)
    low_qkv = nn(seq_attn, in_qkv).astype(BF16)
    low_q, low_k, low_v = (low_qkv[:, i * RANK : (i + 1) * RANK] for i in range(3))
    qkv = nn(seq_attn, attn_w[:, :qkv_width])
    query_pre = (qkv[:, :head_width] + nt(low_q, lift_q)).reshape(LEN, heads_here, HD)
    key_pre = (qkv[:, head_width : head_width + HD] + nt(low_k, lift_k)).reshape(LEN, 1, HD)
    value_pre = qkv[:, head_width + HD :] + nt(low_v, lift_v)
    queries = (rotate(query_pre, cosine, sine) * HD ** (-0.5)).astype(BF16)
    keys = rotate(key_pre, cosine, sine).astype(BF16).reshape(LEN, HD)
    values = value_pre.astype(BF16)

    def scores_of():
        raw = jnp.einsum("qhd,kd->hqk", queries, keys, preferred_element_type=F32)
        squash = jnp.tanh(raw / SOFT_CAP)
        return squash, jnp.where(allowed[None], jnp.exp(SOFT_CAP * squash), 0.0)

    squash, weights = scores_of()
    inverse_total = 1.0 / jnp.sum(weights, axis=-1, keepdims=True)
    attended = jnp.einsum(
        "hqk,kd->qhd", (weights * inverse_total).astype(BF16), values, preferred_element_type=F32
    )
    attended = attended.astype(BF16).reshape(LEN, head_width)
    w_out = attn_w[:, qkv_width:]
    out_part = nt(attended, w_out).astype(BF16)
    low_out_part = pad_lanes(nn(attended, map_heads).astype(BF16))
    attn_main, low_out = tensor_scatter(out_part, low_out_part, count)
    low_out = low_out[:, :RANK].astype(BF16)
    attn_total = attn_main + nt(low_out, lift_out)
    resid_mid = resid_in + rms_norm(attn_total, norm_gains[1])

    normed_mlp = rms_norm(resid_mid, norm_gains[2]).astype(BF16)
    seq_mlp = tensor_gather(normed_mlp, count)
    low_gu = nn(seq_mlp, in_gu).astype(BF16)
    low_g, low_u = low_gu[:, :RANK], low_gu[:, RANK:]
    w_gate, w_up = gate_up_w[:, :hidden_here], gate_up_w[:, hidden_here:]
    gate = nn(seq_mlp, w_gate) + nt(low_g, lift_gate)
    up = nn(seq_mlp, w_up) + nt(low_u, lift_up)
    hidden = gated_gelu(gate, up).astype(BF16)
    down_part = nt(hidden, down_w).astype(BF16)
    low_down_part = pad_lanes(nn(hidden, map_hidden).astype(BF16))
    mlp_main, low_down = tensor_scatter(down_part, low_down_part, count)
    low_down = low_down[:, :RANK].astype(BF16)
    mlp_total = mlp_main + nt(low_down, lift_down)
    layer_out = (row_valid * (resid_mid + rms_norm(mlp_total, norm_gains[3]))).astype(BF16)

    grad_out = cotangent.astype(F32) * row_valid
    grad_mlp = norm_back(mlp_total, norm_gains[3], grad_out).astype(BF16)
    seq_grad_mlp = tensor_gather(grad_mlp, count)
    grad_low_down = nn(seq_grad_mlp, lift_down).astype(BF16)
    grad_hidden = nn(seq_grad_mlp, down_w) + nt(grad_low_down, map_hidden)
    unused, pull = jax.vjp(gated_gelu, gate, up)
    grad_gate, grad_up = pull(grad_hidden)
    grad_gate, grad_up = grad_gate.astype(BF16), grad_up.astype(BF16)
    low_gu_part = pad_lanes(
        jnp.concatenate([nn(grad_gate, lift_gate), nn(grad_up, lift_up)], axis=1).astype(BF16)
    )
    mlp_back_part = (nt(grad_gate, w_gate) + nt(grad_up, w_up)).astype(BF16)
    mlp_back, grad_low_gu = tensor_scatter(mlp_back_part, low_gu_part, count)
    grad_low_gu = grad_low_gu[:, : 2 * RANK].astype(BF16)
    grad_normed_mlp = mlp_back + nt(grad_low_gu, in_gu)
    grad_mid = grad_out + norm_back(resid_mid, norm_gains[2], grad_normed_mlp)

    grad_attn = norm_back(attn_total, norm_gains[1], grad_mid).astype(BF16)
    seq_grad_attn = tensor_gather(grad_attn, count)
    grad_low_out = nn(seq_grad_attn, lift_out).astype(BF16)
    grad_attended = (nn(seq_grad_attn, w_out) + nt(grad_low_out, map_heads)).astype(BF16)
    grad_heads = grad_attended.reshape(LEN, heads_here, HD)
    probs = weights * inverse_total
    probs_low = probs.astype(BF16)
    grad_probs = jnp.einsum("qhd,kd->hqk", grad_heads, values, preferred_element_type=F32)
    grad_value = jnp.einsum("hqk,qhd->kd", probs_low, grad_heads, preferred_element_type=F32)
    grad_capped = probs * (grad_probs - jnp.sum(probs * grad_probs, axis=-1, keepdims=True))
    grad_raw = (grad_capped * (1.0 - squash * squash)).astype(BF16)
    grad_query = jnp.einsum("hqk,kd->qhd", grad_raw, keys, preferred_element_type=F32)
    grad_key = jnp.einsum("hqk,qhd->kd", grad_raw, queries, preferred_element_type=F32)
    grad_q_pre = rotate(grad_query * HD ** (-0.5), cosine, -sine).astype(BF16)
    grad_q_pre = grad_q_pre.reshape(LEN, head_width)
    grad_k_pre = rotate(grad_key.reshape(LEN, 1, HD), cosine, -sine).astype(BF16)
    grad_k_pre = grad_k_pre.reshape(LEN, HD)
    grad_v_pre = grad_value.astype(BF16)
    low_qkv_part = pad_lanes(
        jnp.concatenate(
            [nn(grad_q_pre, lift_q), nn(grad_k_pre, lift_k), nn(grad_v_pre, lift_v)], axis=1
        ).astype(BF16)
    )
    grad_qkv = jnp.concatenate([grad_q_pre, grad_k_pre, grad_v_pre], axis=1)
    attn_back_part = nt(grad_qkv, attn_w[:, :qkv_width]).astype(BF16)
    attn_back, grad_low_qkv = tensor_scatter(attn_back_part, low_qkv_part, count)
    grad_low_qkv = grad_low_qkv[:, : 3 * RANK].astype(BF16)
    grad_normed_attn = attn_back + nt(grad_low_qkv, in_qkv)
    input_grad = (grad_mid + norm_back(resid_in, norm_gains[0], grad_normed_attn)).astype(BF16)

    def packed(parts, blocks):
        return pad_lanes(jnp.concatenate(parts, axis=1).astype(BF16)).reshape(
            blocks, -1, LANES
        )

    d_grad = packed(
        [
            tn(normed_attn, grad_low_qkv),
            tn(normed_mlp, grad_low_gu),
            tn(grad_attn, low_out),
            tn(grad_mlp, low_down),
        ],
        lay.total,
    )
    f_grad = packed(
        [tn(hidden, grad_low_down), tn(grad_gate, low_g), tn(grad_up, low_u)], lay.dp
    )
    h_grad = packed([tn(attended, grad_low_out), tn(grad_q_pre, low_q)], lay.dp)
    k_grad = packed([tn(grad_k_pre, low_k), tn(grad_v_pre, low_v)], lay.kv_owners)
    d_all, f_all, h_all, k_all = exchange(
        grads_kernel,
        "adapter_grads",
        4,
        (d_grad, f_grad, h_grad, k_grad),
        (
            (lay.total, d_rows, LANES),
            (lay.dp, f_rows, LANES),
            (lay.dp, h_rows, LANES),
            (lay.dp * lay.share, k_rows, LANES),
        ),
        lay.dp,
        lay.total,
        lay.share,
    )

    def collect(received):
        repeats = received.shape[0] // lay.dp
        hot = jnp.repeat(group_hot, repeats, axis=0)
        return lax.dot_general(
            hot, received, (((0,), (0,)), ((), ())), preferred_element_type=F32
        )

    d_all, f_all, h_all, k_all = (collect(item) for item in (d_all, f_all, h_all, k_all))

    def lift_form(values, shape):
        return jnp.moveaxis(values, 1, 2).reshape(shape)

    return (
        layer_out,
        input_grad,
        d_all[:, :, : 5 * RANK],
        h_all[:, :, :RANK],
        f_all[:, :, :RANK],
        lift_form(h_all[:, :, RANK : 2 * RANK], lift_query.shape),
        lift_form(k_all[:, :, : 2 * RANK], lift_keyval.shape),
        lift_form(f_all[:, :, RANK : 3 * RANK], lift_gateup.shape),
        lift_form(d_all[:, :, 5 * RANK : 7 * RANK], lift_resid.shape),
    )


def solution(mesh):
    return jax.shard_map(
        per_device,
        mesh=mesh,
        in_specs=(
            P(("dp", "tensor"), None),
            P(("dp", "tensor"), None),
            P("dp"),
            P("dp", None),
            P(),
            P("dp", "tensor"),
            P("dp", None),
            P("dp", None),
            P("tensor", "dp"),
            P("dp", "tensor"),
            P("dp", "tensor"),
            P("tensor", "dp"),
            P(None, ("dp", "tensor"), None),
            P(None, ("dp", "tensor"), None),
            P(None, ("dp", "tensor"), None),
            P(None, None, ("dp", "tensor")),
            P(None, None, None, ("dp", "tensor")),
            P(None, None, None, ("dp", "tensor")),
            P(None, None, None, ("dp", "tensor")),
        ),
        out_specs=(
            P(("dp", "tensor"), None),
            P(("dp", "tensor"), None),
            P(None, ("dp", "tensor"), None),
            P(None, ("dp", "tensor"), None),
            P(None, ("dp", "tensor"), None),
            P(None, None, ("dp", "tensor")),
            P(None, None, None, ("dp", "tensor")),
            P(None, None, None, ("dp", "tensor")),
            P(None, None, None, ("dp", "tensor")),
        ),
        check_vma=False,
    )
```

```python
import functools

import jax
import jax.numpy as jnp
from jax import lax
from jax.experimental import pallas as pl
from jax.experimental.pallas import tpu as pltpu
from jax.sharding import PartitionSpec as P

D = 2304
HQ = 8
KV = 4
HD = 256
FF = 9216
NA = 8
RANK = 16
LEN = 1024
LANES = 128

EPSILON = 1e-06
SOFT_CAP = 50.0
MESH = pl.DeviceIdType.MESH
BF16 = jnp.bfloat16
F32 = jnp.float32
VMEM_LIMIT = 48 * 1024 * 1024


def rms_norm(values, gain_row):
    return (
        values * lax.rsqrt(jnp.mean(values * values, axis=-1, keepdims=True) + EPSILON) * gain_row
    )


def norm_back(values, gain_row, gradient):
    inverse = lax.rsqrt(jnp.mean(values * values, axis=-1, keepdims=True) + EPSILON)
    scaled = gradient * gain_row
    normed = values * inverse
    return inverse * (scaled - normed * jnp.mean(scaled * normed, axis=-1, keepdims=True))


def gelu_parts(gate, up):
    scale = (2.0 / jnp.pi) ** 0.5
    square = gate * gate
    bend = jnp.tanh(scale * gate * (1.0 + 0.044715 * square))
    low = 0.5 * (1.0 + bend)
    gelu = gate * low
    slope = low + 0.5 * gate * (1.0 - bend * bend) * (scale * (1.0 + 3.0 * 0.044715 * square))
    return (gelu * up).astype(BF16), (slope * up).astype(BF16), gelu.astype(BF16)


def tables(length, size):
    half_size = size // 2
    frequency = 10000.0 ** (-2.0 * jnp.arange(half_size, dtype=F32) / size)
    angles = jnp.arange(length, dtype=F32)[:, None] * frequency[None, :]
    return (jnp.cos(angles)[:, None, :], jnp.sin(angles)[:, None, :])


def rotate(values, cosine, sine):
    half_size = values.shape[-1] // 2
    first_half = values[..., :half_size]
    second_half = values[..., half_size:]
    return jnp.concatenate(
        [first_half * cosine - second_half * sine, second_half * cosine + first_half * sine],
        axis=-1,
    )


def nn(a, b):
    return lax.dot_general(a, b, (((1,), (0,)), ((), ())), preferred_element_type=F32)


def nt(a, b):
    return lax.dot_general(a, b, (((1,), (1,)), ((), ())), preferred_element_type=F32)


def tn(a, b):
    return lax.dot_general(a, b, (((0,), (0,)), ((), ())), preferred_element_type=F32)


def pad_lanes(values):
    return jnp.pad(values, [(0, 0)] * (values.ndim - 1) + [(0, LANES - values.shape[-1])])


def greet(peers):
    barrier = pltpu.get_barrier_semaphore()
    for peer in peers:
        pl.semaphore_signal(barrier, inc=1, device_id=peer, device_id_type=MESH)
    pl.semaphore_wait(barrier, len(peers))


def square_peers(index):
    return index + 1 - 2 * lax.rem(index, 2), lax.rem(index + 2, 4), 3 - index


def remote(source, target, send_sem, recv_sem, peer):
    return pltpu.make_async_remote_copy(
        src_ref=source,
        dst_ref=target,
        send_sem=send_sem,
        recv_sem=recv_sem,
        device_id={"tensor": peer},
        device_id_type=MESH,
    )


def gather_kernel(count, rows, x_ref, o_ref, local_sem, send_sem, recv_sem):
    me = lax.axis_index("tensor")
    if count == 4:
        across, down, _ = square_peers(me)
        greet([{"tensor": across}, {"tensor": down}])
        own = pltpu.make_async_copy(x_ref, o_ref.at[pl.ds(me * rows, rows)], local_sem)
        own.start()
        half = rows // 2
        links = (across, down)
        first = [[None, None], [None, None]]
        for order in range(2):
            for link in range(2):
                part = order if link == 0 else 1 - order
                target = o_ref.at[pl.ds(me * rows + part * half, half)]
                copy = remote(
                    x_ref.at[pl.ds(part * half, half)],
                    target,
                    send_sem.at[link, part],
                    recv_sem.at[link, part],
                    links[link],
                )
                copy.start()
                first[link][part] = copy
        second = []
        for link in range(2):
            first[link][link].wait_recv()
            block = o_ref.at[pl.ds(links[link] * rows + link * half, half)]
            copy = remote(
                block, block, send_sem.at[2, link], recv_sem.at[2, link], links[1 - link]
            )
            copy.start()
            second.append(copy)
        for link in range(2):
            first[link][1 - link].wait_recv()
        for copy in second:
            copy.wait_recv()
        own.wait()
        for link in range(2):
            for part in range(2):
                first[link][part].wait_send()
        for copy in second:
            copy.wait_send()
    else:
        peers = [lax.rem(me + step, count) for step in range(1, count)]
        greet([{"tensor": peer} for peer in peers])
        own = pltpu.make_async_copy(x_ref, o_ref.at[pl.ds(me * rows, rows)], local_sem)
        own.start()
        copies = []
        for step, peer in enumerate(peers):
            copy = remote(
                x_ref,
                o_ref.at[pl.ds(me * rows, rows)],
                send_sem.at[0, step],
                recv_sem.at[0, step],
                peer,
            )
            copy.start()
            copies.append(copy)
        own.wait()
        for copy in copies:
            copy.wait()


def tensor_gather(values, count):
    rows, width = values.shape
    slots = max(2, count - 1)
    return pl.pallas_call(
        functools.partial(gather_kernel, count, rows),
        out_shape=jax.ShapeDtypeStruct((count * rows, width), values.dtype),
        in_specs=[pl.BlockSpec(memory_space=pl.ANY)],
        out_specs=pl.BlockSpec(memory_space=pl.ANY),
        scratch_shapes=[
            pltpu.SemaphoreType.DMA,
            pltpu.SemaphoreType.DMA((3, slots)),
            pltpu.SemaphoreType.DMA((3, slots)),
        ],
        compiler_params=pltpu.CompilerParams(
            collective_id=1, has_side_effects=True, vmem_limit_bytes=VMEM_LIMIT
        ),
        name="tensor_gather",
    )(values)


def scatter_kernel(count, rows, p_ref, q_ref, o_ref, l_ref, *scratch):
    me = lax.axis_index("tensor")
    payload = ((p_ref, o_ref), (q_ref, l_ref))
    if count == 4:
        across, down, far = square_peers(me)
        greet([{"tensor": across}, {"tensor": down}])
        half = rows // 2
        first = scratch[0:2]
        sums = scratch[2:4]
        second = scratch[4:6]
        send_sem, recv_sem = scratch[6], scratch[7]
        links = (across, down)
        copies = {}
        for which in (1, 0):
            for link in range(2):
                block = far if which == 1 else links[link]
                for item in range(2):
                    copy = remote(
                        payload[item][0].at[pl.ds(block * rows + link * half, half)],
                        first[item].at[link, which],
                        send_sem.at[item, link, which],
                        recv_sem.at[item, link, which],
                        links[link],
                    )
                    copy.start()
                    copies[item, link, which] = copy
        for link in range(2):
            block = links[1 - link]
            for item in range(2):
                copies[item, link, 1].wait_recv()
                mine = payload[item][0][pl.ds(block * rows + link * half, half), :]
                sums[item][link] = (
                    mine.astype(F32) + first[item][link, 1].astype(F32)
                ).astype(BF16)
                copy = remote(
                    sums[item].at[link],
                    second[item].at[link],
                    send_sem.at[item, link, 2],
                    recv_sem.at[item, link, 2],
                    links[1 - link],
                )
                copy.start()
                copies[item, link, 2] = copy
        for link in range(2):
            for item in range(2):
                copies[item, link, 0].wait_recv()
                mine = payload[item][0][pl.ds(me * rows + link * half, half), :]
                payload[item][1][pl.ds(link * half, half), :] = mine.astype(F32) + first[item][
                    link, 0
                ].astype(F32)
        for link in range(2):
            for item in range(2):
                copies[item, link, 2].wait_recv()
                payload[item][1][pl.ds(link * half, half), :] += second[item][link].astype(F32)
        for copy in copies.values():
            copy.wait_send()
    else:
        peers = [lax.rem(me + step, count) for step in range(1, count)]
        greet([{"tensor": peer} for peer in peers])
        first = scratch[0:2]
        send_sem, recv_sem = scratch[2], scratch[3]
        copies = []
        for step, peer in enumerate(peers):
            for item in range(2):
                copy = remote(
                    payload[item][0].at[pl.ds(peer * rows, rows)],
                    first[item].at[step],
                    send_sem.at[item, step],
                    recv_sem.at[item, step],
                    peer,
                )
                copy.start()
                copies.append((item, step, copy))
        for item in range(2):
            payload[item][1][...] = payload[item][0][pl.ds(me * rows, rows), :].astype(F32)
        for item, step, copy in copies:
            copy.wait()
            payload[item][1][...] += first[item][step].astype(F32)


def tensor_scatter(values, narrow, count):
    rows = values.shape[0] // count
    widths = (values.shape[1], narrow.shape[1])
    if count == 4:
        half = rows // 2
        scratch = [pltpu.VMEM((2, 2, half, width), BF16) for width in widths]
        scratch += [pltpu.VMEM((2, half, width), BF16) for width in widths]
        scratch += [pltpu.VMEM((2, half, width), BF16) for width in widths]
        scratch += [pltpu.SemaphoreType.DMA((2, 2, 3)), pltpu.SemaphoreType.DMA((2, 2, 3))]
    else:
        scratch = [pltpu.VMEM((count - 1, rows, width), BF16) for width in widths]
        scratch += [pltpu.SemaphoreType.DMA((2, count - 1))] * 2
    vmem = pl.BlockSpec(memory_space=pltpu.VMEM)
    return pl.pallas_call(
        functools.partial(scatter_kernel, count, rows),
        out_shape=tuple(jax.ShapeDtypeStruct((rows, width), F32) for width in widths),
        in_specs=[vmem, vmem],
        out_specs=(vmem, vmem),
        scratch_shapes=scratch,
        compiler_params=pltpu.CompilerParams(
            collective_id=2, has_side_effects=True, vmem_limit_bytes=VMEM_LIMIT
        ),
        name="tensor_scatter",
    )(values, narrow)


class Square:
    def __init__(self, rows):
        self.rows = rows
        self.half = rows // 2
        self.me = lax.axis_index("tensor")
        self.across, self.down, self.far = square_peers(self.me)
        self.links = (self.across, self.down)

    def greet(self):
        greet([{"tensor": self.across}, {"tensor": self.down}])

    def pieces(self, chunk):
        block = {0: self.me, 3: self.far}.get(chunk)
        if block is not None:
            starts = (block * self.rows, block * self.rows + self.half)
        elif chunk == 1:
            starts = (self.across * self.rows, self.down * self.rows + self.half)
        else:
            starts = (self.across * self.rows + self.half, self.down * self.rows)
        return tuple((start, part * self.half) for part, start in enumerate(starts))


class ChunkGather:
    def __init__(self, sq, source, buf, send_sem, recv_sem):
        half = sq.half
        self.first, self.second, self.onward = [], [], []
        for link in range(2):
            for order in range(2):
                part = link if order == 0 else 1 - link
                copy = remote(
                    source.at[pl.ds(part * half, half)],
                    buf.at[1 + order, pl.ds(link * half, half)],
                    send_sem.at[2 * order + link],
                    recv_sem.at[2 * order + link],
                    sq.links[link],
                )
                (self.first if order == 0 else self.second).append(copy)
            self.onward.append(
                remote(
                    buf.at[1, pl.ds(link * half, half)],
                    buf.at[3, pl.ds(link * half, half)],
                    send_sem.at[4 + link],
                    recv_sem.at[4 + link],
                    sq.links[1 - link],
                )
            )

    def start(self):
        for copy in self.first + self.second:
            copy.start()

    def wait_chunk(self, chunk):
        if chunk == 1:
            for copy in self.first:
                copy.wait_recv()
            for copy in self.onward:
                copy.start()
        if chunk == 2:
            for copy in self.second:
                copy.wait_recv()
        if chunk == 3:
            for copy in self.onward:
                copy.wait_recv()

    def finish(self):
        for copy in self.first + self.second + self.onward:
            copy.wait_send()


class ChunkScatter:
    def __init__(self, sq, part, landing, passed, send_sem, recv_sem):
        half = sq.half
        self.half, self.part, self.landing, self.passed = half, part, landing, passed
        self.own, self.far, self.last = [], [], []
        for link in range(2):
            rows = pl.ds(link * half, half)
            for kind, chunk, group in ((0, 1, self.own), (1, 3, self.far)):
                slot = 2 * kind + link
                group.append(
                    remote(
                        part.at[chunk, rows],
                        landing.at[slot],
                        send_sem.at[slot],
                        recv_sem.at[slot],
                        sq.links[link],
                    )
                )
            self.last.append(
                remote(
                    passed.at[link],
                    landing.at[4 + link],
                    send_sem.at[4 + link],
                    recv_sem.at[4 + link],
                    sq.links[1 - link],
                )
            )

    def send_own(self):
        for copy in self.own:
            copy.start()

    def send_far(self):
        for copy in self.far:
            copy.start()

    def pass_on(self, link):
        self.far[link].wait_recv()
        rows = pl.ds((1 - link) * self.half, self.half)
        mine = self.part[2, rows, :].astype(F32)
        self.passed[link] = (mine + self.landing[2 + link].astype(F32)).astype(BF16)
        self.last[link].start()

    def collect(self, out_ref):
        for link in range(2):
            self.own[link].wait_recv()
            self.last[link].wait_recv()
            rows = pl.ds(link * self.half, self.half)
            out_ref[rows, :] = (
                self.part[0, rows, :].astype(F32)
                + self.landing[link].astype(F32)
                + self.landing[4 + link].astype(F32)
            )

    def finish(self):
        for copy in self.own + self.far + self.last:
            copy.wait_send()


def scatter_scratch(rows, width):
    half = rows // 2
    return [
        pltpu.VMEM((4, rows, width), BF16),
        pltpu.VMEM((6, half, width), BF16),
        pltpu.VMEM((2, half, width), BF16),
        pltpu.SemaphoreType.DMA((6,)),
        pltpu.SemaphoreType.DMA((6,)),
    ]


def tile_of(width):
    return 768 if width % 768 == 0 else 384


def columns(step, tile, base=0):
    return pl.ds(pl.multiple_of(base + step * tile, LANES), tile)


def mlp_back_kernel(
    rows,
    g_ref,
    down_hbm,
    gu_hbm,
    slope_hbm,
    gelu_hbm,
    hidden_hbm,
    low_hbm,
    lift_down_ref,
    map_ref,
    lift_gu_ref,
    o_ref,
    l_ref,
    f_ref,
    down_w,
    gu_w,
    buf,
    slope,
    gelu,
    hidden,
    low,
    grads,
    weight_sem,
    load_sem,
    own_sem,
    gather_send,
    gather_recv,
    *scratch,
):
    sq = Square(rows)
    half = sq.half
    width = hidden.shape[-1]
    model = o_ref.shape[-1]
    down_load = pltpu.make_async_copy(down_hbm, down_w, weight_sem.at[0])
    gu_load = pltpu.make_async_copy(gu_hbm, gu_w, weight_sem.at[1])
    own_load = pltpu.make_async_copy(g_ref, buf.at[0], own_sem)

    def loads(chunk):
        slot = chunk % 2
        copies = []
        for part, (start, place) in enumerate(sq.pieces(chunk)):
            for item, (source, target) in enumerate(
                ((slope_hbm, slope), (gelu_hbm, gelu), (hidden_hbm, hidden), (low_hbm, low))
            ):
                copies.append(
                    pltpu.make_async_copy(
                        source.at[pl.ds(start, half)],
                        target.at[slot, pl.ds(place, half)],
                        load_sem.at[slot, item, part],
                    )
                )
        return copies

    down_load.start()
    own_load.start()
    for copy in loads(0):
        copy.start()
    sq.greet()
    gather = ChunkGather(sq, g_ref, buf, gather_send, gather_recv)
    gather.start()
    gu_load.start()
    part, part_low = scratch[0], scratch[5]
    scatters = (ChunkScatter(sq, *scratch[:5]), ChunkScatter(sq, *scratch[5:10]))
    f_ref[...] = jnp.zeros_like(f_ref)
    own_load.wait()
    down_load.wait()

    @pl.loop(0, 4)
    def _(chunk):
        slot = lax.rem(chunk, 2)
        for step in range(4):

            @pl.when(chunk == step)
            def _(step=step):
                gather.wait_chunk(step)
                for copy in loads(step):
                    copy.wait()
                if step < 3:
                    for copy in loads(step + 1):
                        copy.start()

        incoming = buf.at[chunk]
        low_down = nn(incoming[...], lift_down_ref[...]).astype(BF16)
        tile = tile_of(width)

        @pl.loop(0, width // tile)
        def _(step):
            here = columns(step, tile)
            grad = nn(incoming[...], down_w[:, here]) + nt(low_down, map_ref[here, :])
            grads[:, here] = (grad * slope[slot, :, here].astype(F32)).astype(BF16)
            grads[:, columns(step, tile, width)] = (
                grad * gelu[slot, :, here].astype(F32)
            ).astype(BF16)

        @pl.when(chunk == 0)
        def _():
            gu_load.wait()

        part_low[chunk] = nn(grads[...], lift_gu_ref[...]).astype(BF16)
        wide = tile_of(model)

        @pl.loop(0, model // wide)
        def _(step):
            here = columns(step, wide)
            part[chunk, :, here] = nt(grads[...], gu_w[here, :]).astype(BF16)

        @pl.when(chunk == 1)
        def _():
            for scatter in scatters:
                scatter.send_own()

        @pl.when(chunk == 3)
        def _():
            for scatter in scatters:
                scatter.send_far()

        low_turned = low_down.astype(F32).T[:RANK].astype(BF16)
        gu_turned = low[slot].astype(F32).T.astype(BF16)
        f_ref[:RANK, :] += nn(low_turned, hidden[slot])
        f_ref[RANK : 2 * RANK, :] += nn(gu_turned[:RANK], grads[:, :width])
        f_ref[2 * RANK : 3 * RANK, :] += nn(gu_turned[RANK : 2 * RANK], grads[:, width:])

    for link in range(2):
        for scatter in scatters:
            scatter.pass_on(link)
    gather.finish()
    scatters[0].collect(o_ref)
    scatters[1].collect(l_ref)
    for scatter in scatters:
        scatter.finish()


def mlp_back_fused(grad, down_w, gu_w, slope, gelu, hidden, low, lift_down, map_hidden, lift_gu):
    rows, model = grad.shape
    width = hidden.shape[1]
    anywhere = pl.BlockSpec(memory_space=pl.ANY)
    vmem = pl.BlockSpec(memory_space=pltpu.VMEM)
    return pl.pallas_call(
        functools.partial(mlp_back_kernel, rows),
        out_shape=(
            jax.ShapeDtypeStruct((rows, model), F32),
            jax.ShapeDtypeStruct((rows, LANES), F32),
            jax.ShapeDtypeStruct((3 * RANK, width), F32),
        ),
        in_specs=[vmem] + [anywhere] * 6 + [vmem] * 3,
        out_specs=(vmem,) * 3,
        scratch_shapes=[
            pltpu.VMEM((model, width), BF16),
            pltpu.VMEM((model, 2 * width), BF16),
            pltpu.VMEM((4, rows, model), BF16),
            pltpu.VMEM((2, rows, width), BF16),
            pltpu.VMEM((2, rows, width), BF16),
            pltpu.VMEM((2, rows, width), BF16),
            pltpu.VMEM((2, rows, LANES), BF16),
            pltpu.VMEM((rows, 2 * width), BF16),
            pltpu.SemaphoreType.DMA((2,)),
            pltpu.SemaphoreType.DMA((2, 4, 2)),
            pltpu.SemaphoreType.DMA,
            pltpu.SemaphoreType.DMA((6,)),
            pltpu.SemaphoreType.DMA((6,)),
        ]
        + scatter_scratch(rows, model)
        + scatter_scratch(rows, LANES),
        compiler_params=pltpu.CompilerParams(
            collective_id=5, has_side_effects=True, vmem_limit_bytes=62 * 1024 * 1024
        ),
        name="mlp_back",
    )(grad, down_w, gu_w, slope, gelu, hidden, low, lift_down, map_hidden, lift_gu)


class Layout:
    def __init__(self):
        self.dp = lax.axis_size("dp")
        self.tensor = lax.axis_size("tensor")
        self.total = self.dp * self.tensor
        self.d = lax.axis_index("dp")
        self.t = lax.axis_index("tensor")
        self.me = self.d * self.tensor + self.t
        self.heads_here = HQ // self.tensor
        self.ratio = HQ // KV
        self.share = max(1, self.tensor // KV)
        self.kv_owners = self.total // KV
        self.kv_head = self.t * self.heads_here // self.ratio
        self.user = self.me // self.dp
        self.kv_slice_head = self.me // self.kv_owners

    def device(self, flat):
        return {"dp": flat // self.tensor, "tensor": lax.rem(flat, self.tensor)}


def greet_all(lay):
    barrier = pltpu.get_barrier_semaphore()

    def signal(step, unused):
        peer = lax.rem(lay.me + step, lay.total)
        pl.semaphore_signal(
            barrier, inc=1, device_id=lay.device(peer), device_id_type=MESH
        )
        return unused

    lax.fori_loop(1, lay.total, signal, 0)
    pl.semaphore_wait(barrier, lay.total - 1)


def send_or_keep(lay, sends, source, target, send_sem, recv_sem, flat, maybe_own):
    def far():
        return pltpu.make_async_remote_copy(
            src_ref=source,
            dst_ref=target,
            send_sem=send_sem,
            recv_sem=recv_sem,
            device_id=lay.device(flat),
            device_id_type=MESH,
        )

    if maybe_own is None:
        copy = far()
        copy.start()
        sends.append((None, copy))
        return

    @pl.when(maybe_own)
    def _():
        pltpu.make_async_copy(source, target, recv_sem).start()

    @pl.when(jnp.logical_not(maybe_own))
    def _():
        far().start()

    sends.append((maybe_own, far()))


def finish(sends, received):
    for own, copy in sends:
        if own is None:
            copy.wait_send()
        else:

            @pl.when(jnp.logical_not(own))
            def _(copy=copy):
                copy.wait_send()

    for target, sem in received:
        pltpu.make_async_copy(target, target, sem).wait()


def tables_kernel(d_ref, f_ref, h_ref, k_ref, do_ref, fo_ref, ho_ref, ko_ref, *sems):
    lay = Layout()
    send_sems, recv_sem = sems[:4], sems[4]
    greet_all(lay)
    sends = []
    for step in range(lay.dp):
        group = lax.rem(lay.d + step, lay.dp)
        flat = group * lay.tensor + lay.user
        own = (lay.user == lay.t) if step == 0 else None
        for item, (source, target) in enumerate(((f_ref, fo_ref), (h_ref, ho_ref))):
            send_or_keep(
                lay,
                sends,
                source.at[group],
                target.at[lax.rem(lay.me, lay.dp)],
                send_sems[item].at[step],
                recv_sem.at[item],
                flat,
                own,
            )
        for extra in range(lay.share):
            user = lay.kv_slice_head * lay.share + extra
            flat = group * lay.tensor + user
            send_or_keep(
                lay,
                sends,
                k_ref.at[group],
                ko_ref.at[lax.rem(lay.me, lay.kv_owners)],
                send_sems[2].at[step, extra],
                recv_sem.at[2],
                flat,
                (user == lay.t) if step == 0 else None,
            )
    pltpu.make_async_copy(d_ref.at[lay.d], do_ref.at[lay.me], recv_sem.at[3]).start()
    for step in range(1, lay.total):
        flat = lax.rem(lay.me + step, lay.total)
        send_or_keep(
            lay,
            sends,
            d_ref.at[flat // lay.tensor],
            do_ref.at[lay.me],
            send_sems[3].at[step],
            recv_sem.at[3],
            flat,
            None,
        )
    finish(
        sends,
        (
            (fo_ref, recv_sem.at[0]),
            (ho_ref, recv_sem.at[1]),
            (ko_ref, recv_sem.at[2]),
            (do_ref, recv_sem.at[3]),
        ),
    )


def grads_kernel(d_ref, f_ref, h_ref, k_ref, do_ref, fo_ref, ho_ref, ko_ref, *sems):
    lay = Layout()
    send_sems, recv_sem = sems[:4], sems[4]
    greet_all(lay)
    sends = []
    for step in range(lay.dp):
        slot = lax.rem(lay.d + step, lay.dp)
        flat = lay.t * lay.dp + slot
        for item, (source, target) in enumerate(((f_ref, fo_ref), (h_ref, ho_ref))):
            send_or_keep(
                lay,
                sends,
                source.at[slot],
                target.at[lay.d],
                send_sems[item].at[step],
                recv_sem.at[item],
                flat,
                flat == lay.me,
            )
    for step in range(lay.kv_owners):
        slot = lax.rem(lay.d + step, lay.kv_owners)
        flat = lay.kv_head * lay.kv_owners + slot
        send_or_keep(
            lay,
            sends,
            k_ref.at[slot],
            ko_ref.at[lay.d * lay.share + lax.rem(lay.t, lay.share)],
            send_sems[2].at[step // lay.share, step % lay.share],
            recv_sem.at[2],
            flat,
            flat == lay.me,
        )
    pltpu.make_async_copy(d_ref.at[lay.me], do_ref.at[lay.me], recv_sem.at[3]).start()
    for step in range(1, lay.total):
        flat = lax.rem(lay.me + step, lay.total)
        send_or_keep(
            lay,
            sends,
            d_ref.at[flat],
            do_ref.at[lay.me],
            send_sems[3].at[step],
            recv_sem.at[3],
            flat,
            None,
        )
    finish(
        sends,
        (
            (fo_ref, recv_sem.at[0]),
            (ho_ref, recv_sem.at[1]),
            (ko_ref, recv_sem.at[2]),
            (do_ref, recv_sem.at[3]),
        ),
    )


def exchange(kernel, name, number, arrays, outs, dp, total, share):
    anywhere = pl.BlockSpec(memory_space=pl.ANY)
    return pl.pallas_call(
        kernel,
        out_shape=tuple(jax.ShapeDtypeStruct(shape, BF16) for shape in outs),
        in_specs=[anywhere] * 4,
        out_specs=(anywhere,) * 4,
        scratch_shapes=[
            pltpu.SemaphoreType.DMA((dp,)),
            pltpu.SemaphoreType.DMA((dp,)),
            pltpu.SemaphoreType.DMA((dp, share)),
            pltpu.SemaphoreType.DMA((total,)),
            pltpu.SemaphoreType.DMA((4,)),
        ],
        compiler_params=pltpu.CompilerParams(
            collective_id=number, has_side_effects=True, vmem_limit_bytes=VMEM_LIMIT
        ),
        name=name,
    )(*arrays)


def per_device(
    layer_in,
    cotangent,
    lengths,
    adapter_ids,
    norm_gains,
    query_weight,
    key_weight,
    value_weight,
    out_weight,
    gate_weight,
    up_weight,
    down_weight,
    adapt_in,
    adapt_heads,
    adapt_hidden,
    lift_query,
    lift_keyval,
    lift_gateup,
    lift_resid,
):
    lay = Layout()
    count = lay.tensor
    rows = layer_in.shape[0]
    group_rows = rows * count
    assert lengths.shape[0] == 1 and group_rows == LEN
    heads_here = lay.heads_here
    head_width = heads_here * HD
    hidden_here = FF // count
    assert lay.ratio % heads_here == 0

    key_cols = lax.dynamic_slice_in_dim(key_weight, lay.kv_head * HD, HD, 1)
    value_cols = lax.dynamic_slice_in_dim(value_weight, lay.kv_head * HD, HD, 1)
    attn_shard = jnp.concatenate([query_weight, key_cols, value_cols, out_weight.T], axis=1)
    attn_w = lax.all_gather(attn_shard, "dp", axis=0, tiled=True)
    gate_up_shard = jnp.concatenate([gate_weight, up_weight], axis=1)
    down_shard = down_weight.T
    attn_shard, gate_up_shard, down_shard = lax.optimization_barrier(
        (attn_shard, gate_up_shard, down_shard)
    )
    gate_up_w = lax.all_gather(gate_up_shard, "dp", axis=0, tiled=True)
    down_w = lax.all_gather(down_shard, "dp", axis=0, tiled=True)
    qkv_width = head_width + 2 * HD

    all_ids = lax.all_gather(adapter_ids[:, 0], "dp", axis=0, tiled=True)
    group_hot = (all_ids[:, None] == jnp.arange(NA, dtype=jnp.int32)[None, :]).astype(BF16)

    def rows_of(table):
        moved = jnp.moveaxis(table, -1, 1)
        return moved.reshape(NA, moved.shape[1], -1)

    def choose(*parts):
        packed = pad_lanes(jnp.concatenate(parts, axis=-1))
        return lax.dot_general(
            group_hot, packed, (((1,), (0,)), ((), ())), preferred_element_type=F32
        ).astype(BF16)

    d_send = choose(adapt_in, rows_of(lift_resid))
    f_send = choose(adapt_hidden, rows_of(lift_gateup))
    h_send = choose(adapt_heads, rows_of(lift_query))
    k_send = choose(rows_of(lift_keyval))
    d_rows, f_rows, h_rows, k_rows = (item.shape[1] for item in (d_send, f_send, h_send, k_send))
    d_tab, f_tab, h_tab, k_tab = exchange(
        tables_kernel,
        "adapter_tables",
        3,
        (d_send, f_send, h_send, k_send),
        (
            (lay.total, d_rows, LANES),
            (lay.dp, f_rows, LANES),
            (lay.dp, h_rows, LANES),
            (lay.kv_owners, k_rows, LANES),
        ),
        lay.dp,
        lay.total,
        lay.share,
    )
    d_tab = d_tab.reshape(D, LANES)
    f_tab = f_tab.reshape(hidden_here, LANES)
    h_tab = h_tab.reshape(head_width, LANES)
    k_tab = k_tab.reshape(HD, LANES)
    in_qkv, in_gu = d_tab[:, : 3 * RANK], d_tab[:, 3 * RANK : 5 * RANK]
    lift_out, lift_down = d_tab[:, 5 * RANK : 6 * RANK], d_tab[:, 6 * RANK : 7 * RANK]
    map_hidden, lift_gate, lift_up = (f_tab[:, i * RANK : (i + 1) * RANK] for i in range(3))
    map_heads, lift_q = h_tab[:, :RANK], h_tab[:, RANK : 2 * RANK]
    lift_k, lift_v = k_tab[:, :RANK], k_tab[:, RANK : 2 * RANK]

    row_start = lay.t * rows
    length = lengths[0]
    row_valid = ((row_start + jnp.arange(rows, dtype=jnp.int32)) < length).astype(F32)[:, None]
    cosine, sine = tables(LEN, HD)
    place = jnp.arange(LEN, dtype=jnp.int32)
    allowed = (place[:, None] >= place[None, :]) & (place[None, :] < length)

    resid_in = layer_in.astype(F32)
    normed_attn = rms_norm(resid_in, norm_gains[0]).astype(BF16)
    seq_attn = tensor_gather(normed_attn, count)
    low_qkv = nn(seq_attn, in_qkv).astype(BF16)
    low_q, low_k, low_v = (low_qkv[:, i * RANK : (i + 1) * RANK] for i in range(3))
    qkv = nn(seq_attn, attn_w[:, :qkv_width])
    query_pre = (qkv[:, :head_width] + nt(low_q, lift_q)).reshape(LEN, heads_here, HD)
    key_pre = (qkv[:, head_width : head_width + HD] + nt(low_k, lift_k)).reshape(LEN, 1, HD)
    value_pre = qkv[:, head_width + HD :] + nt(low_v, lift_v)
    queries = (rotate(query_pre, cosine, sine) * HD ** (-0.5)).astype(BF16)
    keys = rotate(key_pre, cosine, sine).astype(BF16).reshape(LEN, HD)
    values = value_pre.astype(BF16)

    def scores_of():
        raw = jnp.einsum("qhd,kd->hqk", queries, keys, preferred_element_type=F32)
        squash = jnp.tanh(raw / SOFT_CAP)
        return squash, jnp.where(allowed[None], jnp.exp(SOFT_CAP * squash), 0.0)

    squash, weights = scores_of()
    inverse_total = 1.0 / jnp.sum(weights, axis=-1, keepdims=True)
    attended = jnp.einsum(
        "hqk,kd->qhd", (weights * inverse_total).astype(BF16), values, preferred_element_type=F32
    )
    attended = attended.astype(BF16).reshape(LEN, head_width)
    w_out = attn_w[:, qkv_width:]
    out_part = nt(attended, w_out).astype(BF16)
    low_out_part = pad_lanes(nn(attended, map_heads).astype(BF16))
    attn_main, low_out = tensor_scatter(out_part, low_out_part, count)
    low_out = low_out[:, :RANK].astype(BF16)
    attn_total = attn_main + nt(low_out, lift_out)
    resid_mid = resid_in + rms_norm(attn_total, norm_gains[1])

    normed_mlp = rms_norm(resid_mid, norm_gains[2]).astype(BF16)
    seq_mlp = tensor_gather(normed_mlp, count)
    low_gu = nn(seq_mlp, in_gu).astype(BF16)
    low_g, low_u = low_gu[:, :RANK], low_gu[:, RANK:]
    w_gate, w_up = gate_up_w[:, :hidden_here], gate_up_w[:, hidden_here:]
    gate = nn(seq_mlp, w_gate) + nt(low_g, lift_gate)
    up = nn(seq_mlp, w_up) + nt(low_u, lift_up)
    hidden, slope, gelu = gelu_parts(gate, up)
    down_part = nt(hidden, down_w).astype(BF16)
    low_down_part = pad_lanes(nn(hidden, map_hidden).astype(BF16))
    mlp_main, low_down = tensor_scatter(down_part, low_down_part, count)
    low_down = low_down[:, :RANK].astype(BF16)
    mlp_total = mlp_main + nt(low_down, lift_down)
    layer_out = (row_valid * (resid_mid + rms_norm(mlp_total, norm_gains[3]))).astype(BF16)

    grad_out = cotangent.astype(F32) * row_valid
    grad_mlp = norm_back(mlp_total, norm_gains[3], grad_out).astype(BF16)
    if count == 4:
        lift_gu = jnp.concatenate(
            [pad_lanes(lift_gate), jnp.pad(lift_up, ((0, 0), (RANK, LANES - 2 * RANK)))], axis=0
        )
        mlp_back, grad_low_gu, f_turned = mlp_back_fused(
            grad_mlp,
            down_w,
            gate_up_w,
            slope,
            gelu,
            hidden,
            pad_lanes(low_gu),
            pad_lanes(lift_down),
            pad_lanes(map_hidden),
            lift_gu,
        )
        f_parts = [f_turned.T]
    else:
        seq_grad_mlp = tensor_gather(grad_mlp, count)
        grad_low_down = nn(seq_grad_mlp, lift_down).astype(BF16)
        grad_hidden = nn(seq_grad_mlp, down_w) + nt(grad_low_down, map_hidden)
        grad_gate = (grad_hidden * slope.astype(F32)).astype(BF16)
        grad_up = (grad_hidden * gelu.astype(F32)).astype(BF16)
        low_gu_part = pad_lanes(
            jnp.concatenate([nn(grad_gate, lift_gate), nn(grad_up, lift_up)], axis=1).astype(BF16)
        )
        mlp_back_part = (nt(grad_gate, w_gate) + nt(grad_up, w_up)).astype(BF16)
        mlp_back, grad_low_gu = tensor_scatter(mlp_back_part, low_gu_part, count)
        f_parts = [tn(hidden, grad_low_down), tn(grad_gate, low_g), tn(grad_up, low_u)]
    grad_low_gu = grad_low_gu[:, : 2 * RANK].astype(BF16)
    grad_normed_mlp = mlp_back + nt(grad_low_gu, in_gu)
    grad_mid = grad_out + norm_back(resid_mid, norm_gains[2], grad_normed_mlp)

    grad_attn = norm_back(attn_total, norm_gains[1], grad_mid).astype(BF16)
    seq_grad_attn = tensor_gather(grad_attn, count)
    grad_low_out = nn(seq_grad_attn, lift_out).astype(BF16)
    grad_attended = (nn(seq_grad_attn, w_out) + nt(grad_low_out, map_heads)).astype(BF16)
    grad_heads = grad_attended.reshape(LEN, heads_here, HD)
    probs = weights * inverse_total
    probs_low = probs.astype(BF16)
    grad_probs = jnp.einsum("qhd,kd->hqk", grad_heads, values, preferred_element_type=F32)
    grad_value = jnp.einsum("hqk,qhd->kd", probs_low, grad_heads, preferred_element_type=F32)
    grad_capped = probs * (grad_probs - jnp.sum(probs * grad_probs, axis=-1, keepdims=True))
    grad_raw = (grad_capped * (1.0 - squash * squash)).astype(BF16)
    grad_query = jnp.einsum("hqk,kd->qhd", grad_raw, keys, preferred_element_type=F32)
    grad_key = jnp.einsum("hqk,qhd->kd", grad_raw, queries, preferred_element_type=F32)
    grad_q_pre = rotate(grad_query * HD ** (-0.5), cosine, -sine).astype(BF16)
    grad_q_pre = grad_q_pre.reshape(LEN, head_width)
    grad_k_pre = rotate(grad_key.reshape(LEN, 1, HD), cosine, -sine).astype(BF16)
    grad_k_pre = grad_k_pre.reshape(LEN, HD)
    grad_v_pre = grad_value.astype(BF16)
    low_qkv_part = pad_lanes(
        jnp.concatenate(
            [nn(grad_q_pre, lift_q), nn(grad_k_pre, lift_k), nn(grad_v_pre, lift_v)], axis=1
        ).astype(BF16)
    )
    grad_qkv = jnp.concatenate([grad_q_pre, grad_k_pre, grad_v_pre], axis=1)
    attn_back_part = nt(grad_qkv, attn_w[:, :qkv_width]).astype(BF16)
    attn_back, grad_low_qkv = tensor_scatter(attn_back_part, low_qkv_part, count)
    grad_low_qkv = grad_low_qkv[:, : 3 * RANK].astype(BF16)
    grad_normed_attn = attn_back + nt(grad_low_qkv, in_qkv)
    input_grad = (grad_mid + norm_back(resid_in, norm_gains[0], grad_normed_attn)).astype(BF16)

    def packed(parts, blocks):
        return pad_lanes(jnp.concatenate(parts, axis=1).astype(BF16)).reshape(
            blocks, -1, LANES
        )

    d_grad = packed(
        [
            tn(normed_attn, grad_low_qkv),
            tn(normed_mlp, grad_low_gu),
            tn(grad_attn, low_out),
            tn(grad_mlp, low_down),
        ],
        lay.total,
    )
    f_grad = packed(f_parts, lay.dp)
    h_grad = packed([tn(attended, grad_low_out), tn(grad_q_pre, low_q)], lay.dp)
    k_grad = packed([tn(grad_k_pre, low_k), tn(grad_v_pre, low_v)], lay.kv_owners)
    d_all, f_all, h_all, k_all = exchange(
        grads_kernel,
        "adapter_grads",
        4,
        (d_grad, f_grad, h_grad, k_grad),
        (
            (lay.total, d_rows, LANES),
            (lay.dp, f_rows, LANES),
            (lay.dp, h_rows, LANES),
            (lay.dp * lay.share, k_rows, LANES),
        ),
        lay.dp,
        lay.total,
        lay.share,
    )

    def collect(received):
        repeats = received.shape[0] // lay.dp
        hot = jnp.repeat(group_hot, repeats, axis=0)
        return lax.dot_general(
            hot, received, (((0,), (0,)), ((), ())), preferred_element_type=F32
        )

    d_all, f_all, h_all, k_all = (collect(item) for item in (d_all, f_all, h_all, k_all))

    def lift_form(values, shape):
        return jnp.moveaxis(values, 1, 2).reshape(shape)

    return (
        layer_out,
        input_grad,
        d_all[:, :, : 5 * RANK],
        h_all[:, :, :RANK],
        f_all[:, :, :RANK],
        lift_form(h_all[:, :, RANK : 2 * RANK], lift_query.shape),
        lift_form(k_all[:, :, : 2 * RANK], lift_keyval.shape),
        lift_form(f_all[:, :, RANK : 3 * RANK], lift_gateup.shape),
        lift_form(d_all[:, :, 5 * RANK : 7 * RANK], lift_resid.shape),
    )


def solution(mesh):
    return jax.shard_map(
        per_device,
        mesh=mesh,
        in_specs=(
            P(("dp", "tensor"), None),
            P(("dp", "tensor"), None),
            P("dp"),
            P("dp", None),
            P(),
            P("dp", "tensor"),
            P("dp", None),
            P("dp", None),
            P("tensor", "dp"),
            P("dp", "tensor"),
            P("dp", "tensor"),
            P("tensor", "dp"),
            P(None, ("dp", "tensor"), None),
            P(None, ("dp", "tensor"), None),
            P(None, ("dp", "tensor"), None),
            P(None, None, ("dp", "tensor")),
            P(None, None, None, ("dp", "tensor")),
            P(None, None, None, ("dp", "tensor")),
            P(None, None, None, ("dp", "tensor")),
        ),
        out_specs=(
            P(("dp", "tensor"), None),
            P(("dp", "tensor"), None),
            P(None, ("dp", "tensor"), None),
            P(None, ("dp", "tensor"), None),
            P(None, ("dp", "tensor"), None),
            P(None, None, ("dp", "tensor")),
            P(None, None, None, ("dp", "tensor")),
            P(None, None, None, ("dp", "tensor")),
            P(None, None, None, ("dp", "tensor")),
        ),
        check_vma=False,
    )
```

```python
import functools

import jax
import jax.numpy as jnp
from jax import lax
from jax.experimental import pallas as pl
from jax.experimental.pallas import tpu as pltpu
from jax.sharding import PartitionSpec as P

D = 2304
HQ = 8
KV = 4
HD = 256
FF = 9216
NA = 8
RANK = 16
LEN = 1024
LANES = 128

EPSILON = 1e-06
SOFT_CAP = 50.0
MESH = pl.DeviceIdType.MESH
BF16 = jnp.bfloat16
F32 = jnp.float32
VMEM_LIMIT = 48 * 1024 * 1024


def rms_norm(values, gain_row):
    return (
        values * lax.rsqrt(jnp.mean(values * values, axis=-1, keepdims=True) + EPSILON) * gain_row
    )


def norm_back(values, gain_row, gradient):
    inverse = lax.rsqrt(jnp.mean(values * values, axis=-1, keepdims=True) + EPSILON)
    scaled = gradient * gain_row
    normed = values * inverse
    return inverse * (scaled - normed * jnp.mean(scaled * normed, axis=-1, keepdims=True))


def gelu_parts(gate, up):
    scale = (2.0 / jnp.pi) ** 0.5
    square = gate * gate
    bend = jnp.tanh(scale * gate * (1.0 + 0.044715 * square))
    low = 0.5 * (1.0 + bend)
    gelu = gate * low
    slope = low + 0.5 * gate * (1.0 - bend * bend) * (scale * (1.0 + 3.0 * 0.044715 * square))
    return (gelu * up).astype(BF16), (slope * up).astype(BF16), gelu.astype(BF16)


def tables(length, size):
    half_size = size // 2
    frequency = 10000.0 ** (-2.0 * jnp.arange(half_size, dtype=F32) / size)
    angles = jnp.arange(length, dtype=F32)[:, None] * frequency[None, :]
    return (jnp.cos(angles)[:, None, :], jnp.sin(angles)[:, None, :])


def rotate(values, cosine, sine):
    half_size = values.shape[-1] // 2
    first_half = values[..., :half_size]
    second_half = values[..., half_size:]
    return jnp.concatenate(
        [first_half * cosine - second_half * sine, second_half * cosine + first_half * sine],
        axis=-1,
    )


def nn(a, b):
    return lax.dot_general(a, b, (((1,), (0,)), ((), ())), preferred_element_type=F32)


def nt(a, b):
    return lax.dot_general(a, b, (((1,), (1,)), ((), ())), preferred_element_type=F32)


def tn(a, b):
    return lax.dot_general(a, b, (((0,), (0,)), ((), ())), preferred_element_type=F32)


def pad_lanes(values):
    return jnp.pad(values, [(0, 0)] * (values.ndim - 1) + [(0, LANES - values.shape[-1])])


def greet(peers):
    barrier = pltpu.get_barrier_semaphore()
    for peer in peers:
        pl.semaphore_signal(barrier, inc=1, device_id=peer, device_id_type=MESH)
    pl.semaphore_wait(barrier, len(peers))


def square_peers(index):
    return index + 1 - 2 * lax.rem(index, 2), lax.rem(index + 2, 4), 3 - index


def remote(source, target, send_sem, recv_sem, peer):
    return pltpu.make_async_remote_copy(
        src_ref=source,
        dst_ref=target,
        send_sem=send_sem,
        recv_sem=recv_sem,
        device_id={"tensor": peer},
        device_id_type=MESH,
    )


def gather_kernel(count, rows, x_ref, o_ref, local_sem, send_sem, recv_sem):
    me = lax.axis_index("tensor")
    if count == 4:
        across, down, _ = square_peers(me)
        greet([{"tensor": across}, {"tensor": down}])
        own = pltpu.make_async_copy(x_ref, o_ref.at[pl.ds(me * rows, rows)], local_sem)
        own.start()
        half = rows // 2
        links = (across, down)
        first = [[None, None], [None, None]]
        for order in range(2):
            for link in range(2):
                part = order if link == 0 else 1 - order
                target = o_ref.at[pl.ds(me * rows + part * half, half)]
                copy = remote(
                    x_ref.at[pl.ds(part * half, half)],
                    target,
                    send_sem.at[link, part],
                    recv_sem.at[link, part],
                    links[link],
                )
                copy.start()
                first[link][part] = copy
        second = []
        for link in range(2):
            first[link][link].wait_recv()
            block = o_ref.at[pl.ds(links[link] * rows + link * half, half)]
            copy = remote(
                block, block, send_sem.at[2, link], recv_sem.at[2, link], links[1 - link]
            )
            copy.start()
            second.append(copy)
        for link in range(2):
            first[link][1 - link].wait_recv()
        for copy in second:
            copy.wait_recv()
        own.wait()
        for link in range(2):
            for part in range(2):
                first[link][part].wait_send()
        for copy in second:
            copy.wait_send()
    else:
        peers = [lax.rem(me + step, count) for step in range(1, count)]
        greet([{"tensor": peer} for peer in peers])
        own = pltpu.make_async_copy(x_ref, o_ref.at[pl.ds(me * rows, rows)], local_sem)
        own.start()
        copies = []
        for step, peer in enumerate(peers):
            copy = remote(
                x_ref,
                o_ref.at[pl.ds(me * rows, rows)],
                send_sem.at[0, step],
                recv_sem.at[0, step],
                peer,
            )
            copy.start()
            copies.append(copy)
        own.wait()
        for copy in copies:
            copy.wait()


def tensor_gather(values, count):
    rows, width = values.shape
    slots = max(2, count - 1)
    return pl.pallas_call(
        functools.partial(gather_kernel, count, rows),
        out_shape=jax.ShapeDtypeStruct((count * rows, width), values.dtype),
        in_specs=[pl.BlockSpec(memory_space=pl.ANY)],
        out_specs=pl.BlockSpec(memory_space=pl.ANY),
        scratch_shapes=[
            pltpu.SemaphoreType.DMA,
            pltpu.SemaphoreType.DMA((3, slots)),
            pltpu.SemaphoreType.DMA((3, slots)),
        ],
        compiler_params=pltpu.CompilerParams(
            collective_id=1, has_side_effects=True, vmem_limit_bytes=VMEM_LIMIT
        ),
        name="tensor_gather",
    )(values)


def scatter_kernel(count, rows, p_ref, q_ref, o_ref, l_ref, *scratch):
    me = lax.axis_index("tensor")
    payload = ((p_ref, o_ref), (q_ref, l_ref))
    if count == 4:
        across, down, far = square_peers(me)
        greet([{"tensor": across}, {"tensor": down}])
        half = rows // 2
        first = scratch[0:2]
        sums = scratch[2:4]
        second = scratch[4:6]
        send_sem, recv_sem = scratch[6], scratch[7]
        links = (across, down)
        copies = {}
        for which in (1, 0):
            for link in range(2):
                block = far if which == 1 else links[link]
                for item in range(2):
                    copy = remote(
                        payload[item][0].at[pl.ds(block * rows + link * half, half)],
                        first[item].at[link, which],
                        send_sem.at[item, link, which],
                        recv_sem.at[item, link, which],
                        links[link],
                    )
                    copy.start()
                    copies[item, link, which] = copy
        for link in range(2):
            block = links[1 - link]
            for item in range(2):
                copies[item, link, 1].wait_recv()
                mine = payload[item][0][pl.ds(block * rows + link * half, half), :]
                sums[item][link] = (
                    mine.astype(F32) + first[item][link, 1].astype(F32)
                ).astype(BF16)
                copy = remote(
                    sums[item].at[link],
                    second[item].at[link],
                    send_sem.at[item, link, 2],
                    recv_sem.at[item, link, 2],
                    links[1 - link],
                )
                copy.start()
                copies[item, link, 2] = copy
        for link in range(2):
            for item in range(2):
                copies[item, link, 0].wait_recv()
                mine = payload[item][0][pl.ds(me * rows + link * half, half), :]
                payload[item][1][pl.ds(link * half, half), :] = mine.astype(F32) + first[item][
                    link, 0
                ].astype(F32)
        for link in range(2):
            for item in range(2):
                copies[item, link, 2].wait_recv()
                payload[item][1][pl.ds(link * half, half), :] += second[item][link].astype(F32)
        for copy in copies.values():
            copy.wait_send()
    else:
        peers = [lax.rem(me + step, count) for step in range(1, count)]
        greet([{"tensor": peer} for peer in peers])
        first = scratch[0:2]
        send_sem, recv_sem = scratch[2], scratch[3]
        copies = []
        for step, peer in enumerate(peers):
            for item in range(2):
                copy = remote(
                    payload[item][0].at[pl.ds(peer * rows, rows)],
                    first[item].at[step],
                    send_sem.at[item, step],
                    recv_sem.at[item, step],
                    peer,
                )
                copy.start()
                copies.append((item, step, copy))
        for item in range(2):
            payload[item][1][...] = payload[item][0][pl.ds(me * rows, rows), :].astype(F32)
        for item, step, copy in copies:
            copy.wait()
            payload[item][1][...] += first[item][step].astype(F32)


def tensor_scatter(values, narrow, count):
    rows = values.shape[0] // count
    widths = (values.shape[1], narrow.shape[1])
    if count == 4:
        half = rows // 2
        scratch = [pltpu.VMEM((2, 2, half, width), BF16) for width in widths]
        scratch += [pltpu.VMEM((2, half, width), BF16) for width in widths]
        scratch += [pltpu.VMEM((2, half, width), BF16) for width in widths]
        scratch += [pltpu.SemaphoreType.DMA((2, 2, 3)), pltpu.SemaphoreType.DMA((2, 2, 3))]
    else:
        scratch = [pltpu.VMEM((count - 1, rows, width), BF16) for width in widths]
        scratch += [pltpu.SemaphoreType.DMA((2, count - 1))] * 2
    vmem = pl.BlockSpec(memory_space=pltpu.VMEM)
    return pl.pallas_call(
        functools.partial(scatter_kernel, count, rows),
        out_shape=tuple(jax.ShapeDtypeStruct((rows, width), F32) for width in widths),
        in_specs=[vmem, vmem],
        out_specs=(vmem, vmem),
        scratch_shapes=scratch,
        compiler_params=pltpu.CompilerParams(
            collective_id=2, has_side_effects=True, vmem_limit_bytes=VMEM_LIMIT
        ),
        name="tensor_scatter",
    )(values, narrow)


class Square:
    def __init__(self, rows):
        self.rows = rows
        self.half = rows // 2
        self.me = lax.axis_index("tensor")
        self.across, self.down, self.far = square_peers(self.me)
        self.links = (self.across, self.down)

    def greet(self):
        greet([{"tensor": self.across}, {"tensor": self.down}])

    def pieces(self, chunk):
        block = {0: self.me, 3: self.far}.get(chunk)
        if block is not None:
            starts = (block * self.rows, block * self.rows + self.half)
        elif chunk == 1:
            starts = (self.across * self.rows, self.down * self.rows + self.half)
        else:
            starts = (self.across * self.rows + self.half, self.down * self.rows)
        return tuple((start, part * self.half) for part, start in enumerate(starts))


class ChunkGather:
    def __init__(self, sq, source, buf, send_sem, recv_sem):
        half = sq.half
        self.first, self.second, self.onward = [], [], []
        for link in range(2):
            for order in range(2):
                part = link if order == 0 else 1 - link
                copy = remote(
                    source.at[pl.ds(part * half, half)],
                    buf.at[1 + order, pl.ds(link * half, half)],
                    send_sem.at[2 * order + link],
                    recv_sem.at[2 * order + link],
                    sq.links[link],
                )
                (self.first if order == 0 else self.second).append(copy)
            self.onward.append(
                remote(
                    buf.at[1, pl.ds(link * half, half)],
                    buf.at[3, pl.ds(link * half, half)],
                    send_sem.at[4 + link],
                    recv_sem.at[4 + link],
                    sq.links[1 - link],
                )
            )

    def start(self):
        for copy in self.first + self.second:
            copy.start()

    def wait_chunk(self, chunk):
        if chunk == 1:
            for copy in self.first:
                copy.wait_recv()
            for copy in self.onward:
                copy.start()
        if chunk == 2:
            for copy in self.second:
                copy.wait_recv()
        if chunk == 3:
            for copy in self.onward:
                copy.wait_recv()

    def finish(self):
        for copy in self.first + self.second + self.onward:
            copy.wait_send()


class ChunkScatter:
    def __init__(self, sq, part, landing, passed, send_sem, recv_sem):
        half = sq.half
        self.half, self.part, self.landing, self.passed = half, part, landing, passed
        self.own, self.far, self.last = [], [], []
        for link in range(2):
            rows = pl.ds(link * half, half)
            for kind, chunk, group in ((0, 1, self.own), (1, 3, self.far)):
                slot = 2 * kind + link
                group.append(
                    remote(
                        part.at[chunk, rows],
                        landing.at[slot],
                        send_sem.at[slot],
                        recv_sem.at[slot],
                        sq.links[link],
                    )
                )
            self.last.append(
                remote(
                    passed.at[link],
                    landing.at[4 + link],
                    send_sem.at[4 + link],
                    recv_sem.at[4 + link],
                    sq.links[1 - link],
                )
            )

    def send_own(self):
        for copy in self.own:
            copy.start()

    def send_far(self):
        for copy in self.far:
            copy.start()

    def pass_on(self, link):
        self.far[link].wait_recv()
        rows = pl.ds((1 - link) * self.half, self.half)
        mine = self.part[2, rows, :].astype(F32)
        self.passed[link] = (mine + self.landing[2 + link].astype(F32)).astype(BF16)
        self.last[link].start()

    def collect(self, out_ref):
        for link in range(2):
            self.own[link].wait_recv()
            self.last[link].wait_recv()
            rows = pl.ds(link * self.half, self.half)
            out_ref[rows, :] = (
                self.part[0, rows, :].astype(F32)
                + self.landing[link].astype(F32)
                + self.landing[4 + link].astype(F32)
            )

    def finish(self):
        for copy in self.own + self.far + self.last:
            copy.wait_send()


def scatter_scratch(rows, width):
    half = rows // 2
    return [
        pltpu.VMEM((4, rows, width), BF16),
        pltpu.VMEM((6, half, width), BF16),
        pltpu.VMEM((2, half, width), BF16),
        pltpu.SemaphoreType.DMA((6,)),
        pltpu.SemaphoreType.DMA((6,)),
    ]


def tile_of(width):
    return 768 if width % 768 == 0 else 384


def columns(step, tile, base=0):
    return pl.ds(pl.multiple_of(base + step * tile, LANES), tile)


def mlp_back_kernel(
    rows,
    g_ref,
    down_hbm,
    gu_hbm,
    slope_hbm,
    gelu_hbm,
    hidden_hbm,
    low_hbm,
    lift_down_ref,
    map_ref,
    lift_gu_ref,
    o_ref,
    l_ref,
    f_out,
    f_ref,
    down_w,
    gu_w,
    buf,
    slope,
    gelu,
    hidden,
    low,
    grads,
    weight_sem,
    load_sem,
    own_sem,
    gather_send,
    gather_recv,
    *scratch,
):
    sq = Square(rows)
    half = sq.half
    width = hidden.shape[-1]
    model = o_ref.shape[-1]
    down_load = pltpu.make_async_copy(down_hbm, down_w, weight_sem.at[0])
    gu_load = pltpu.make_async_copy(gu_hbm, gu_w, weight_sem.at[1])
    own_load = pltpu.make_async_copy(g_ref, buf.at[0], own_sem)

    def loads(chunk):
        slot = chunk % 2
        copies = []
        for part, (start, place) in enumerate(sq.pieces(chunk)):
            for item, (source, target) in enumerate(
                ((slope_hbm, slope), (gelu_hbm, gelu), (hidden_hbm, hidden), (low_hbm, low))
            ):
                copies.append(
                    pltpu.make_async_copy(
                        source.at[pl.ds(start, half)],
                        target.at[slot, pl.ds(place, half)],
                        load_sem.at[slot, item, part],
                    )
                )
        return copies

    down_load.start()
    own_load.start()
    for copy in loads(0):
        copy.start()
    sq.greet()
    gather = ChunkGather(sq, g_ref, buf, gather_send, gather_recv)
    gather.start()
    gu_load.start()
    part, part_low = scratch[0], scratch[5]
    scatters = (ChunkScatter(sq, *scratch[:5]), ChunkScatter(sq, *scratch[5:10]))
    f_ref[...] = jnp.zeros_like(f_ref)
    own_load.wait()
    down_load.wait()

    @pl.loop(0, 4)
    def _(chunk):
        slot = lax.rem(chunk, 2)
        for step in range(4):

            @pl.when(chunk == step)
            def _(step=step):
                gather.wait_chunk(step)
                for copy in loads(step):
                    copy.wait()
                if step < 3:
                    for copy in loads(step + 1):
                        copy.start()

        incoming = buf.at[chunk]
        low_down = nn(incoming[...], lift_down_ref[...]).astype(BF16)
        tile = tile_of(width)

        @pl.loop(0, width // tile)
        def _(step):
            here = columns(step, tile)
            grad = nn(incoming[...], down_w[:, here]) + nt(low_down, map_ref[here, :])
            grads[:, here] = (grad * slope[slot, :, here].astype(F32)).astype(BF16)
            grads[:, columns(step, tile, width)] = (
                grad * gelu[slot, :, here].astype(F32)
            ).astype(BF16)

        @pl.when(chunk == 0)
        def _():
            gu_load.wait()

        part_low[chunk] = nn(grads[...], lift_gu_ref[...]).astype(BF16)
        wide = tile_of(model)

        @pl.loop(0, model // wide)
        def _(step):
            here = columns(step, wide)
            part[chunk, :, here] = nt(grads[...], gu_w[here, :]).astype(BF16)

        @pl.when(chunk == 1)
        def _():
            for scatter in scatters:
                scatter.send_own()

        @pl.when(chunk == 3)
        def _():
            for scatter in scatters:
                scatter.send_far()

        low_turned = low_down.astype(F32).T[:RANK].astype(BF16)
        gu_turned = low[slot].astype(F32).T.astype(BF16)
        f_ref[:RANK, :] += nn(low_turned, hidden[slot])
        f_ref[RANK : 2 * RANK, :] += nn(gu_turned[:RANK], grads[:, :width])
        f_ref[2 * RANK : 3 * RANK, :] += nn(gu_turned[RANK : 2 * RANK], grads[:, width:])

    @pl.loop(0, width // LANES)
    def _(step):
        here = columns(step, LANES)
        f_out[here, :] = jnp.concatenate(
            [f_ref[:, here], jnp.zeros((LANES - 4 * RANK, LANES), F32)], axis=0
        ).T.astype(BF16)

    for link in range(2):
        for scatter in scatters:
            scatter.pass_on(link)
    gather.finish()
    scatters[0].collect(o_ref)
    scatters[1].collect(l_ref)
    for scatter in scatters:
        scatter.finish()


def mlp_back_fused(grad, down_w, gu_w, slope, gelu, hidden, low, lift_down, map_hidden, lift_gu):
    rows, model = grad.shape
    width = hidden.shape[1]
    anywhere = pl.BlockSpec(memory_space=pl.ANY)
    vmem = pl.BlockSpec(memory_space=pltpu.VMEM)
    return pl.pallas_call(
        functools.partial(mlp_back_kernel, rows),
        out_shape=(
            jax.ShapeDtypeStruct((rows, model), F32),
            jax.ShapeDtypeStruct((rows, LANES), F32),
            jax.ShapeDtypeStruct((width, LANES), BF16),
        ),
        in_specs=[vmem] + [anywhere] * 6 + [vmem] * 3,
        out_specs=(vmem,) * 3,
        scratch_shapes=[
            pltpu.VMEM((4 * RANK, width), F32),
            pltpu.VMEM((model, width), BF16),
            pltpu.VMEM((model, 2 * width), BF16),
            pltpu.VMEM((4, rows, model), BF16),
            pltpu.VMEM((2, rows, width), BF16),
            pltpu.VMEM((2, rows, width), BF16),
            pltpu.VMEM((2, rows, width), BF16),
            pltpu.VMEM((2, rows, LANES), BF16),
            pltpu.VMEM((rows, 2 * width), BF16),
            pltpu.SemaphoreType.DMA((2,)),
            pltpu.SemaphoreType.DMA((2, 4, 2)),
            pltpu.SemaphoreType.DMA,
            pltpu.SemaphoreType.DMA((6,)),
            pltpu.SemaphoreType.DMA((6,)),
        ]
        + scatter_scratch(rows, model)
        + scatter_scratch(rows, LANES),
        compiler_params=pltpu.CompilerParams(
            collective_id=5, has_side_effects=True, vmem_limit_bytes=62 * 1024 * 1024
        ),
        name="mlp_back",
    )(grad, down_w, gu_w, slope, gelu, hidden, low, lift_down, map_hidden, lift_gu)


class Layout:
    def __init__(self):
        self.dp = lax.axis_size("dp")
        self.tensor = lax.axis_size("tensor")
        self.total = self.dp * self.tensor
        self.d = lax.axis_index("dp")
        self.t = lax.axis_index("tensor")
        self.me = self.d * self.tensor + self.t
        self.heads_here = HQ // self.tensor
        self.ratio = HQ // KV
        self.share = max(1, self.tensor // KV)
        self.kv_owners = self.total // KV
        self.kv_head = self.t * self.heads_here // self.ratio
        self.user = self.me // self.dp
        self.kv_slice_head = self.me // self.kv_owners

    def device(self, flat):
        return {"dp": flat // self.tensor, "tensor": lax.rem(flat, self.tensor)}


def greet_all(lay):
    barrier = pltpu.get_barrier_semaphore()

    def signal(step, unused):
        peer = lax.rem(lay.me + step, lay.total)
        pl.semaphore_signal(
            barrier, inc=1, device_id=lay.device(peer), device_id_type=MESH
        )
        return unused

    lax.fori_loop(1, lay.total, signal, 0)
    pl.semaphore_wait(barrier, lay.total - 1)


def send_or_keep(lay, sends, source, target, send_sem, recv_sem, flat, maybe_own):
    def far():
        return pltpu.make_async_remote_copy(
            src_ref=source,
            dst_ref=target,
            send_sem=send_sem,
            recv_sem=recv_sem,
            device_id=lay.device(flat),
            device_id_type=MESH,
        )

    if maybe_own is None:
        copy = far()
        copy.start()
        sends.append((None, copy))
        return

    @pl.when(maybe_own)
    def _():
        pltpu.make_async_copy(source, target, recv_sem).start()

    @pl.when(jnp.logical_not(maybe_own))
    def _():
        far().start()

    sends.append((maybe_own, far()))


def finish(sends, received):
    for own, copy in sends:
        if own is None:
            copy.wait_send()
        else:

            @pl.when(jnp.logical_not(own))
            def _(copy=copy):
                copy.wait_send()

    for target, sem in received:
        pltpu.make_async_copy(target, target, sem).wait()


def tables_kernel(d_ref, f_ref, h_ref, k_ref, do_ref, fo_ref, ho_ref, ko_ref, *sems):
    lay = Layout()
    send_sems, recv_sem = sems[:4], sems[4]
    greet_all(lay)
    sends = []
    for step in range(lay.dp):
        group = lax.rem(lay.d + step, lay.dp)
        flat = group * lay.tensor + lay.user
        own = (lay.user == lay.t) if step == 0 else None
        for item, (source, target) in enumerate(((f_ref, fo_ref), (h_ref, ho_ref))):
            send_or_keep(
                lay,
                sends,
                source.at[group],
                target.at[lax.rem(lay.me, lay.dp)],
                send_sems[item].at[step],
                recv_sem.at[item],
                flat,
                own,
            )
        for extra in range(lay.share):
            user = lay.kv_slice_head * lay.share + extra
            flat = group * lay.tensor + user
            send_or_keep(
                lay,
                sends,
                k_ref.at[group],
                ko_ref.at[lax.rem(lay.me, lay.kv_owners)],
                send_sems[2].at[step, extra],
                recv_sem.at[2],
                flat,
                (user == lay.t) if step == 0 else None,
            )
    pltpu.make_async_copy(d_ref.at[lay.d], do_ref.at[lay.me], recv_sem.at[3]).start()
    for step in range(1, lay.total):
        flat = lax.rem(lay.me + step, lay.total)
        send_or_keep(
            lay,
            sends,
            d_ref.at[flat // lay.tensor],
            do_ref.at[lay.me],
            send_sems[3].at[step],
            recv_sem.at[3],
            flat,
            None,
        )
    finish(
        sends,
        (
            (fo_ref, recv_sem.at[0]),
            (ho_ref, recv_sem.at[1]),
            (ko_ref, recv_sem.at[2]),
            (do_ref, recv_sem.at[3]),
        ),
    )


def grads_kernel(d_ref, f_ref, h_ref, k_ref, do_ref, fo_ref, ho_ref, ko_ref, *sems):
    lay = Layout()
    send_sems, recv_sem = sems[:4], sems[4]
    greet_all(lay)
    sends = []
    for step in range(lay.dp):
        slot = lax.rem(lay.d + step, lay.dp)
        flat = lay.t * lay.dp + slot
        for item, (source, target) in enumerate(((f_ref, fo_ref), (h_ref, ho_ref))):
            send_or_keep(
                lay,
                sends,
                source.at[slot],
                target.at[lay.d],
                send_sems[item].at[step],
                recv_sem.at[item],
                flat,
                flat == lay.me,
            )
    for step in range(lay.kv_owners):
        slot = lax.rem(lay.d + step, lay.kv_owners)
        flat = lay.kv_head * lay.kv_owners + slot
        send_or_keep(
            lay,
            sends,
            k_ref.at[slot],
            ko_ref.at[lay.d * lay.share + lax.rem(lay.t, lay.share)],
            send_sems[2].at[step // lay.share, step % lay.share],
            recv_sem.at[2],
            flat,
            flat == lay.me,
        )
    pltpu.make_async_copy(d_ref.at[lay.me], do_ref.at[lay.me], recv_sem.at[3]).start()
    for step in range(1, lay.total):
        flat = lax.rem(lay.me + step, lay.total)
        send_or_keep(
            lay,
            sends,
            d_ref.at[flat],
            do_ref.at[lay.me],
            send_sems[3].at[step],
            recv_sem.at[3],
            flat,
            None,
        )
    finish(
        sends,
        (
            (fo_ref, recv_sem.at[0]),
            (ho_ref, recv_sem.at[1]),
            (ko_ref, recv_sem.at[2]),
            (do_ref, recv_sem.at[3]),
        ),
    )


def exchange(kernel, name, number, arrays, outs, dp, total, share):
    anywhere = pl.BlockSpec(memory_space=pl.ANY)
    return pl.pallas_call(
        kernel,
        out_shape=tuple(jax.ShapeDtypeStruct(shape, BF16) for shape in outs),
        in_specs=[anywhere] * 4,
        out_specs=(anywhere,) * 4,
        scratch_shapes=[
            pltpu.SemaphoreType.DMA((dp,)),
            pltpu.SemaphoreType.DMA((dp,)),
            pltpu.SemaphoreType.DMA((dp, share)),
            pltpu.SemaphoreType.DMA((total,)),
            pltpu.SemaphoreType.DMA((4,)),
        ],
        compiler_params=pltpu.CompilerParams(
            collective_id=number, has_side_effects=True, vmem_limit_bytes=VMEM_LIMIT
        ),
        name=name,
    )(*arrays)


def chunk_start(sq, chunk, part):
    is_own = (3 - chunk) // 3
    is_far = chunk // 3
    near = 1 - is_own - is_far
    neighbour = sq.down if part == 1 else sq.across
    block = sq.me * is_own + sq.far * is_far + neighbour * near
    other_half = chunk // 2 - is_far
    half = 1 - other_half if part == 1 else other_half
    return pl.multiple_of(block * sq.rows + half * sq.half, sq.half)


def rotate_back(values, cosine, sine):
    first, second = values[:, : HD // 2], values[:, HD // 2 :]
    return jnp.concatenate([first * cosine + second * sine, second * cosine - first * sine], axis=1)


def attn_back_kernel(
    rows,
    ids_ref,
    length_ref,
    g_ref,
    weight_hbm,
    seq_hbm,
    q_ref,
    k_ref,
    kt_ref,
    v_ref,
    attended_ref,
    inverse_ref,
    cos_ref,
    sin_ref,
    low_ref,
    lift_out_ref,
    map_ref,
    lift_qkv_ref,
    normed_ref,
    grad_gu_ref,
    low_out_ref,
    grad_mlp_ref,
    low_down_ref,
    f_hbm,
    o_ref,
    l_ref,
    in_out,
    heads_out,
    hidden_out,
    query_out,
    keyval_out,
    gateup_out,
    resid_out,
    weight,
    seq,
    buf,
    att,
    q_grad,
    k_sum,
    v_sum,
    kv_grad,
    joined,
    d_turned,
    h_turned,
    k_turned,
    d_send,
    h_send,
    k_send,
    d_recv,
    f_recv,
    h_recv,
    k_recv,
    load_sem,
    own_sem,
    gather_send,
    gather_recv,
    d_sem,
    f_sem,
    h_sem,
    k_sem,
    recv_sem,
    *scratch,
):
    sq = Square(rows)
    lay = Layout()
    half = sq.half
    model = o_ref.shape[-1]
    weight_load = pltpu.make_async_copy(weight_hbm, weight, load_sem.at[0])
    seq_load = pltpu.make_async_copy(seq_hbm, seq, load_sem.at[1])
    own_load = pltpu.make_async_copy(g_ref, buf.at[0], own_sem)
    weight_load.start()
    own_load.start()
    greet_all(lay)
    gather = ChunkGather(sq, g_ref, buf, gather_send, gather_recv)
    gather.start()
    seq_load.start()
    sends = []
    for step in range(lay.dp):
        slot = lax.rem(lay.d + step, lay.dp)
        flat = lay.t * lay.dp + slot
        send_or_keep(
            lay,
            sends,
            f_hbm.at[slot],
            f_recv.at[lay.d],
            f_sem.at[step],
            recv_sem.at[0],
            flat,
            flat == lay.me,
        )
    part, part_low = scratch[0], scratch[5]
    scatters = (ChunkScatter(sq, *scratch[:5]), ChunkScatter(sq, *scratch[5:10]))

    def turned(values):
        return values.astype(F32).T.astype(BF16)

    d_turned[...] = jnp.zeros_like(d_turned)
    wide = tile_of(model)
    low_grads = (
        (turned(grad_gu_ref[...]), normed_ref, 3 * RANK, 2 * RANK),
        (turned(low_out_ref[...]), g_ref, 5 * RANK, RANK),
        (turned(low_down_ref[...]), grad_mlp_ref, 6 * RANK, RANK),
    )

    @pl.loop(0, model // wide)
    def _(step):
        here = columns(step, wide)
        for low, source, first, count in low_grads:
            d_turned[pl.ds(first, count), here] = nn(low[:count], source[:, here])

    h_turned[...] = jnp.zeros_like(h_turned)
    k_turned[...] = jnp.zeros_like(k_turned)
    k_sum[...] = jnp.zeros_like(k_sum)
    v_sum[...] = jnp.zeros_like(v_sum)
    own_load.wait()
    weight_load.wait()
    q_width = q_ref.shape[1]
    qkv_width = q_width + 2 * HD
    heads = q_width // HD
    stacked = heads * half

    @pl.loop(0, 4)
    def _(chunk):
        for step in range(4):

            @pl.when(chunk == step)
            def _(step=step):
                gather.wait_chunk(step)

        incoming = buf.at[chunk]
        low_out = nn(incoming[...], lift_out_ref[...]).astype(BF16)
        att[...] = (
            nn(incoming[...], weight[:, qkv_width:]) + nt(low_out, map_ref[...])
        ).astype(BF16)
        low_turned = turned(low_out)[:RANK]
        for side in range(2):
            start = chunk_start(sq, chunk, side)
            here = pl.ds(start, half)
            place = pl.ds(side * half, half)
            h_turned[:RANK, :] += nn(
                low_turned[:, side * half : (side + 1) * half], attended_ref[here, :]
            )
            queries = jnp.concatenate(
                [q_ref[here, h * HD : (h + 1) * HD] for h in range(heads)], axis=0
            )
            grads = jnp.concatenate(
                [att[place, h * HD : (h + 1) * HD] for h in range(heads)], axis=0
            )
            inverse = jnp.concatenate([inverse_ref[h : h + 1, here] for h in range(heads)], axis=1)
            key_at = lax.broadcasted_iota(jnp.int32, (LEN, stacked), 0)
            query_at = lax.rem(lax.broadcasted_iota(jnp.int32, (LEN, stacked), 1), half) + start
            allowed = (key_at <= query_at) & (key_at < length_ref[0])
            squash = jnp.tanh(nt(k_ref[...], queries) * (1.0 / SOFT_CAP))
            probs = jnp.where(allowed, jnp.exp(SOFT_CAP * squash) * inverse, 0.0)
            grad_probs = nt(v_ref[...], grads)
            mean = jnp.sum(probs * grad_probs, axis=0, keepdims=True)
            grad_raw = (probs * (grad_probs - mean) * (1.0 - squash * squash)).astype(BF16)
            k_sum[...] += nn(grad_raw, queries)
            v_sum[...] += nn(probs.astype(BF16), grads)
            q_back = nn(kt_ref[...], grad_raw).T * HD ** (-0.5)
            for h in range(heads):
                q_grad[chunk, place, h * HD : (h + 1) * HD] = rotate_back(
                    q_back[h * half : (h + 1) * half], cos_ref[here, :], sin_ref[here, :]
                ).astype(BF16)

    kv_grad[:, :HD] = rotate_back(k_sum[...], cos_ref[...], sin_ref[...]).astype(BF16)
    kv_grad[:, HD:] = v_sum[...].astype(BF16)

    @pl.loop(0, 4)
    def _(step):
        chunk = step + 3 * ((3 - step) // 3) - 3 * (step // 3)
        joined[chunk, :, :q_width] = q_grad[chunk]
        for side in range(2):
            here = pl.ds(chunk_start(sq, chunk, side), half)
            joined[chunk, pl.ds(side * half, half), q_width:] = kv_grad[here, :]
        part_low[chunk] = nn(joined[chunk], lift_qkv_ref[...]).astype(BF16)

        @pl.loop(0, model // wide)
        def _(tile):
            here = columns(tile, wide)
            part[chunk, :, here] = nt(joined[chunk], weight[here, :qkv_width]).astype(BF16)

        @pl.when(step == 0)
        def _():
            for scatter in scatters:
                scatter.send_far()

        @pl.when(step == 1)
        def _():
            for scatter in scatters:
                scatter.send_own()

    seq_load.wait()

    @pl.loop(0, 4)
    def _(chunk):
        grad_turned = turned(part_low[chunk])[: 3 * RANK]
        for side in range(2):
            here = pl.ds(chunk_start(sq, chunk, side), half)
            place = slice(side * half, (side + 1) * half)
            low_turned = turned(low_ref[here, :])
            mine = joined.at[chunk, pl.ds(side * half, half)]
            h_turned[RANK : 2 * RANK, :] += nn(low_turned[:RANK], mine[:, :q_width])
            k_turned[:RANK, :] += nn(
                low_turned[RANK : 2 * RANK], mine[:, q_width : q_width + HD]
            )
            k_turned[RANK : 2 * RANK, :] += nn(
                low_turned[2 * RANK : 3 * RANK], mine[:, q_width + HD :]
            )

            @pl.loop(0, model // wide)
            def _(tile):
                where = columns(tile, wide)
                d_turned[: 3 * RANK, where] += nn(grad_turned[:, place], seq[here, where])

    @pl.loop(0, model // LANES)
    def _(step):
        here = columns(step, LANES)
        d_send[here, :] = d_turned[:, here].T.astype(BF16)

    h_send[...] = h_turned[...].T.astype(BF16)
    k_send[...] = k_turned[...].T.astype(BF16)
    d_rows, h_rows, k_rows = d_recv.shape[1], h_recv.shape[1], k_recv.shape[1]
    for step in range(lay.dp):
        slot = lax.rem(lay.d + step, lay.dp)
        flat = lay.t * lay.dp + slot
        for item, (source, size, target, sem) in enumerate(
            ((h_send, h_rows, h_recv, h_sem), (k_send, k_rows, k_recv, k_sem))
        ):
            send_or_keep(
                lay,
                sends,
                source.at[pl.ds(pl.multiple_of(slot * size, size), size)],
                target.at[lay.d],
                sem.at[step],
                recv_sem.at[1 + item],
                flat,
                flat == lay.me,
            )
    pltpu.make_async_copy(
        d_send.at[pl.ds(pl.multiple_of(lay.me * d_rows, 8), d_rows)],
        d_recv.at[lay.me],
        recv_sem.at[3],
    ).start()
    for step in range(1, lay.total):
        flat = lax.rem(lay.me + step, lay.total)
        send_or_keep(
            lay,
            sends,
            d_send.at[pl.ds(pl.multiple_of(flat * d_rows, 8), d_rows)],
            d_recv.at[lay.me],
            d_sem.at[step],
            recv_sem.at[3],
            flat,
            None,
        )
    for link in range(2):
        for scatter in scatters:
            scatter.pass_on(link)
    scatters[0].collect(o_ref)
    scatters[1].collect(l_ref)
    finish(
        sends,
        (
            (f_recv, recv_sem.at[0]),
            (h_recv, recv_sem.at[1]),
            (k_recv, recv_sem.at[2]),
            (d_recv, recv_sem.at[3]),
        ),
    )

    @pl.loop(0, NA)
    def _(adapter):
        def pick(parts):
            total = None
            for group in range(lay.dp):
                mine = jnp.where(ids_ref[group] == adapter, parts(group), 0.0)
                total = mine if total is None else total + mine
            return total

        def d_part(group):
            return sum(
                d_recv[group * lay.tensor + t].astype(F32) for t in range(lay.tensor)
            )

        d_all = pick(d_part)
        in_out[adapter] = d_all[:, : 5 * RANK]
        d_flip = d_all.T
        f_all = pick(lambda group: f_recv[group].astype(F32))
        hidden_out[adapter] = f_all[:, :RANK]
        f_flip = f_all.T
        h_all = pick(lambda group: h_recv[group].astype(F32))
        heads_out[adapter] = h_all[:, :RANK]
        query_out[adapter] = h_all.T[RANK : 2 * RANK]
        k_flip = pick(lambda group: k_recv[group].astype(F32)).T
        for which in range(2):
            band = slice(which * RANK, (which + 1) * RANK)
            keyval_out[adapter, which] = k_flip[band]
            gateup_out[adapter, which] = f_flip[RANK:][band]
            resid_out[adapter, which] = d_flip[5 * RANK :][band]

    gather.finish()
    for scatter in scatters:
        scatter.finish()


def attn_back_fused(scalars, arrays, grad_shapes, dp, total):
    (g, weight, seq, q) = arrays[:4]
    rows, model = g.shape
    f_send = arrays[-1]
    anywhere = pl.BlockSpec(memory_space=pl.ANY)
    vmem = pl.BlockSpec(memory_space=pltpu.VMEM)
    smem = pl.BlockSpec(memory_space=pltpu.SMEM)
    q_width = q.shape[1]
    specs = [smem, smem] + [vmem] * len(arrays)
    specs[3] = specs[4] = specs[-1] = anywhere
    outs = [jax.ShapeDtypeStruct((rows, model), F32), jax.ShapeDtypeStruct((rows, LANES), F32)]
    outs += [jax.ShapeDtypeStruct(shape, F32) for shape in grad_shapes]
    d_rows, h_rows = model // total, q_width // dp
    k_rows = HD // dp
    return pl.pallas_call(
        functools.partial(attn_back_kernel, rows),
        out_shape=tuple(outs),
        in_specs=specs,
        out_specs=(vmem,) * len(outs),
        scratch_shapes=[
            pltpu.VMEM(weight.shape, BF16),
            pltpu.VMEM(seq.shape, BF16),
            pltpu.VMEM((4, rows, model), BF16),
            pltpu.VMEM((rows, q_width), BF16),
            pltpu.VMEM((4, rows, q_width), BF16),
            pltpu.VMEM((LEN, HD), F32),
            pltpu.VMEM((LEN, HD), F32),
            pltpu.VMEM((LEN, 2 * HD), BF16),
            pltpu.VMEM((4, rows, q_width + 2 * HD), BF16),
            pltpu.VMEM((LANES, model), F32),
            pltpu.VMEM((LANES, q_width), F32),
            pltpu.VMEM((LANES, HD), F32),
            pltpu.VMEM((model, LANES), BF16),
            pltpu.VMEM((q_width, LANES), BF16),
            pltpu.VMEM((HD, LANES), BF16),
            pltpu.VMEM((total, d_rows, LANES), BF16),
            pltpu.VMEM(f_send.shape, BF16),
            pltpu.VMEM((dp, h_rows, LANES), BF16),
            pltpu.VMEM((dp, k_rows, LANES), BF16),
            pltpu.SemaphoreType.DMA((2,)),
            pltpu.SemaphoreType.DMA,
            pltpu.SemaphoreType.DMA((6,)),
            pltpu.SemaphoreType.DMA((6,)),
            pltpu.SemaphoreType.DMA((total,)),
            pltpu.SemaphoreType.DMA((dp,)),
            pltpu.SemaphoreType.DMA((dp,)),
            pltpu.SemaphoreType.DMA((dp,)),
            pltpu.SemaphoreType.DMA((4,)),
        ]
        + scatter_scratch(rows, model)
        + scatter_scratch(rows, LANES),
        compiler_params=pltpu.CompilerParams(
            collective_id=6, has_side_effects=True, vmem_limit_bytes=62 * 1024 * 1024
        ),
        name="attn_back",
    )(*scalars, *arrays)


def per_device(
    layer_in,
    cotangent,
    lengths,
    adapter_ids,
    norm_gains,
    query_weight,
    key_weight,
    value_weight,
    out_weight,
    gate_weight,
    up_weight,
    down_weight,
    adapt_in,
    adapt_heads,
    adapt_hidden,
    lift_query,
    lift_keyval,
    lift_gateup,
    lift_resid,
):
    lay = Layout()
    count = lay.tensor
    rows = layer_in.shape[0]
    group_rows = rows * count
    assert lengths.shape[0] == 1 and group_rows == LEN
    heads_here = lay.heads_here
    head_width = heads_here * HD
    hidden_here = FF // count
    assert lay.ratio % heads_here == 0

    key_cols = lax.dynamic_slice_in_dim(key_weight, lay.kv_head * HD, HD, 1)
    value_cols = lax.dynamic_slice_in_dim(value_weight, lay.kv_head * HD, HD, 1)
    attn_shard = jnp.concatenate([query_weight, key_cols, value_cols, out_weight.T], axis=1)
    attn_w = lax.all_gather(attn_shard, "dp", axis=0, tiled=True)
    gate_up_shard = jnp.concatenate([gate_weight, up_weight], axis=1)
    down_shard = down_weight.T
    attn_shard, gate_up_shard, down_shard = lax.optimization_barrier(
        (attn_shard, gate_up_shard, down_shard)
    )
    gate_up_w = lax.all_gather(gate_up_shard, "dp", axis=0, tiled=True)
    down_w = lax.all_gather(down_shard, "dp", axis=0, tiled=True)
    qkv_width = head_width + 2 * HD

    all_ids = lax.all_gather(adapter_ids[:, 0], "dp", axis=0, tiled=True)
    group_hot = (all_ids[:, None] == jnp.arange(NA, dtype=jnp.int32)[None, :]).astype(BF16)

    def rows_of(table):
        moved = jnp.moveaxis(table, -1, 1)
        return moved.reshape(NA, moved.shape[1], -1)

    def choose(*parts):
        packed = pad_lanes(jnp.concatenate(parts, axis=-1))
        return lax.dot_general(
            group_hot, packed, (((1,), (0,)), ((), ())), preferred_element_type=F32
        ).astype(BF16)

    d_send = choose(adapt_in, rows_of(lift_resid))
    f_send = choose(adapt_hidden, rows_of(lift_gateup))
    h_send = choose(adapt_heads, rows_of(lift_query))
    k_send = choose(rows_of(lift_keyval))
    d_rows, f_rows, h_rows, k_rows = (item.shape[1] for item in (d_send, f_send, h_send, k_send))
    d_tab, f_tab, h_tab, k_tab = exchange(
        tables_kernel,
        "adapter_tables",
        3,
        (d_send, f_send, h_send, k_send),
        (
            (lay.total, d_rows, LANES),
            (lay.dp, f_rows, LANES),
            (lay.dp, h_rows, LANES),
            (lay.kv_owners, k_rows, LANES),
        ),
        lay.dp,
        lay.total,
        lay.share,
    )
    d_tab = d_tab.reshape(D, LANES)
    f_tab = f_tab.reshape(hidden_here, LANES)
    h_tab = h_tab.reshape(head_width, LANES)
    k_tab = k_tab.reshape(HD, LANES)
    in_qkv, in_gu = d_tab[:, : 3 * RANK], d_tab[:, 3 * RANK : 5 * RANK]
    lift_out, lift_down = d_tab[:, 5 * RANK : 6 * RANK], d_tab[:, 6 * RANK : 7 * RANK]
    map_hidden, lift_gate, lift_up = (f_tab[:, i * RANK : (i + 1) * RANK] for i in range(3))
    map_heads, lift_q = h_tab[:, :RANK], h_tab[:, RANK : 2 * RANK]
    lift_k, lift_v = k_tab[:, :RANK], k_tab[:, RANK : 2 * RANK]

    row_start = lay.t * rows
    length = lengths[0]
    row_valid = ((row_start + jnp.arange(rows, dtype=jnp.int32)) < length).astype(F32)[:, None]
    cosine, sine = tables(LEN, HD)
    place = jnp.arange(LEN, dtype=jnp.int32)
    allowed = (place[:, None] >= place[None, :]) & (place[None, :] < length)

    resid_in = layer_in.astype(F32)
    normed_attn = rms_norm(resid_in, norm_gains[0]).astype(BF16)
    seq_attn = tensor_gather(normed_attn, count)
    low_qkv = nn(seq_attn, in_qkv).astype(BF16)
    low_q, low_k, low_v = (low_qkv[:, i * RANK : (i + 1) * RANK] for i in range(3))
    qkv = nn(seq_attn, attn_w[:, :qkv_width])
    query_pre = (qkv[:, :head_width] + nt(low_q, lift_q)).reshape(LEN, heads_here, HD)
    key_pre = (qkv[:, head_width : head_width + HD] + nt(low_k, lift_k)).reshape(LEN, 1, HD)
    value_pre = qkv[:, head_width + HD :] + nt(low_v, lift_v)
    queries = (rotate(query_pre, cosine, sine) * HD ** (-0.5)).astype(BF16)
    keys = rotate(key_pre, cosine, sine).astype(BF16).reshape(LEN, HD)
    values = value_pre.astype(BF16)

    def scores_of():
        raw = jnp.einsum("qhd,kd->hqk", queries, keys, preferred_element_type=F32)
        squash = jnp.tanh(raw / SOFT_CAP)
        return squash, jnp.where(allowed[None], jnp.exp(SOFT_CAP * squash), 0.0)

    squash, weights = scores_of()
    inverse_total = 1.0 / jnp.sum(weights, axis=-1, keepdims=True)
    attended = jnp.einsum(
        "hqk,kd->qhd", (weights * inverse_total).astype(BF16), values, preferred_element_type=F32
    )
    attended = attended.astype(BF16).reshape(LEN, head_width)
    w_out = attn_w[:, qkv_width:]
    out_part = nt(attended, w_out).astype(BF16)
    low_out_part = pad_lanes(nn(attended, map_heads).astype(BF16))
    attn_main, low_out = tensor_scatter(out_part, low_out_part, count)
    low_out = low_out[:, :RANK].astype(BF16)
    attn_total = attn_main + nt(low_out, lift_out)
    resid_mid = resid_in + rms_norm(attn_total, norm_gains[1])

    normed_mlp = rms_norm(resid_mid, norm_gains[2]).astype(BF16)
    seq_mlp = tensor_gather(normed_mlp, count)
    low_gu = nn(seq_mlp, in_gu).astype(BF16)
    low_g, low_u = low_gu[:, :RANK], low_gu[:, RANK:]
    w_gate, w_up = gate_up_w[:, :hidden_here], gate_up_w[:, hidden_here:]
    gate = nn(seq_mlp, w_gate) + nt(low_g, lift_gate)
    up = nn(seq_mlp, w_up) + nt(low_u, lift_up)
    hidden, slope, gelu = gelu_parts(gate, up)
    down_part = nt(hidden, down_w).astype(BF16)
    low_down_part = pad_lanes(nn(hidden, map_hidden).astype(BF16))
    mlp_main, low_down = tensor_scatter(down_part, low_down_part, count)
    low_down = low_down[:, :RANK].astype(BF16)
    mlp_total = mlp_main + nt(low_down, lift_down)
    layer_out = (row_valid * (resid_mid + rms_norm(mlp_total, norm_gains[3]))).astype(BF16)

    grad_out = cotangent.astype(F32) * row_valid
    grad_mlp = norm_back(mlp_total, norm_gains[3], grad_out).astype(BF16)
    if count == 4:
        lift_gu = jnp.concatenate(
            [pad_lanes(lift_gate), jnp.pad(lift_up, ((0, 0), (RANK, LANES - 2 * RANK)))], axis=0
        )
        mlp_back, grad_low_gu, f_grad = mlp_back_fused(
            grad_mlp,
            down_w,
            gate_up_w,
            slope,
            gelu,
            hidden,
            pad_lanes(low_gu),
            pad_lanes(lift_down),
            pad_lanes(map_hidden),
            lift_gu,
        )
    else:
        seq_grad_mlp = tensor_gather(grad_mlp, count)
        grad_low_down = nn(seq_grad_mlp, lift_down).astype(BF16)
        grad_hidden = nn(seq_grad_mlp, down_w) + nt(grad_low_down, map_hidden)
        grad_gate = (grad_hidden * slope.astype(F32)).astype(BF16)
        grad_up = (grad_hidden * gelu.astype(F32)).astype(BF16)
        low_gu_part = pad_lanes(
            jnp.concatenate([nn(grad_gate, lift_gate), nn(grad_up, lift_up)], axis=1).astype(BF16)
        )
        mlp_back_part = (nt(grad_gate, w_gate) + nt(grad_up, w_up)).astype(BF16)
        mlp_back, grad_low_gu = tensor_scatter(mlp_back_part, low_gu_part, count)
        f_parts = [tn(hidden, grad_low_down), tn(grad_gate, low_g), tn(grad_up, low_u)]
    grad_low_gu = grad_low_gu[:, : 2 * RANK].astype(BF16)
    grad_normed_mlp = mlp_back + nt(grad_low_gu, in_gu)
    grad_mid = grad_out + norm_back(resid_mid, norm_gains[2], grad_normed_mlp)

    grad_attn = norm_back(attn_total, norm_gains[1], grad_mid).astype(BF16)
    grad_shapes = tuple(
        table.shape
        for table in (
            adapt_in,
            adapt_heads,
            adapt_hidden,
            lift_query,
            lift_keyval,
            lift_gateup,
            lift_resid,
        )
    )
    if count == 4:
        lift_qkv = jnp.concatenate(
            [
                pad_lanes(lift_q),
                jnp.pad(lift_k, ((0, 0), (RANK, LANES - 2 * RANK))),
                jnp.pad(lift_v, ((0, 0), (2 * RANK, LANES - 3 * RANK))),
            ],
            axis=0,
        )
        attn_back, grad_low_qkv, *adapter_grads = attn_back_fused(
            (all_ids, lengths),
            (
                grad_attn,
                attn_w,
                seq_attn,
                queries.reshape(LEN, head_width),
                keys,
                keys.T,
                values,
                attended,
                inverse_total.reshape(heads_here, LEN),
                cosine.reshape(LEN, HD // 2),
                sine.reshape(LEN, HD // 2),
                pad_lanes(low_qkv),
                pad_lanes(lift_out),
                pad_lanes(map_heads),
                lift_qkv,
                normed_mlp,
                pad_lanes(grad_low_gu),
                pad_lanes(low_out),
                grad_mlp,
                pad_lanes(low_down),
                f_grad.reshape(lay.dp, -1, LANES),
            ),
            grad_shapes,
            lay.dp,
            lay.total,
        )
    else:
        seq_grad_attn = tensor_gather(grad_attn, count)
        grad_low_out = nn(seq_grad_attn, lift_out).astype(BF16)
        grad_attended = (nn(seq_grad_attn, w_out) + nt(grad_low_out, map_heads)).astype(BF16)
        grad_heads = grad_attended.reshape(LEN, heads_here, HD)
        probs = weights * inverse_total
        probs_low = probs.astype(BF16)
        grad_probs = jnp.einsum("qhd,kd->hqk", grad_heads, values, preferred_element_type=F32)
        grad_value = jnp.einsum("hqk,qhd->kd", probs_low, grad_heads, preferred_element_type=F32)
        grad_capped = probs * (grad_probs - jnp.sum(probs * grad_probs, axis=-1, keepdims=True))
        grad_raw = (grad_capped * (1.0 - squash * squash)).astype(BF16)
        grad_query = jnp.einsum("hqk,kd->qhd", grad_raw, keys, preferred_element_type=F32)
        grad_key = jnp.einsum("hqk,qhd->kd", grad_raw, queries, preferred_element_type=F32)
        grad_q_pre = rotate(grad_query * HD ** (-0.5), cosine, -sine).astype(BF16)
        grad_q_pre = grad_q_pre.reshape(LEN, head_width)
        grad_k_pre = rotate(grad_key.reshape(LEN, 1, HD), cosine, -sine).astype(BF16)
        grad_k_pre = grad_k_pre.reshape(LEN, HD)
        grad_v_pre = grad_value.astype(BF16)
        low_qkv_part = pad_lanes(
            jnp.concatenate(
                [nn(grad_q_pre, lift_q), nn(grad_k_pre, lift_k), nn(grad_v_pre, lift_v)], axis=1
            ).astype(BF16)
        )
        grad_qkv = jnp.concatenate([grad_q_pre, grad_k_pre, grad_v_pre], axis=1)
        attn_back_part = nt(grad_qkv, attn_w[:, :qkv_width]).astype(BF16)
        attn_back, grad_low_qkv = tensor_scatter(attn_back_part, low_qkv_part, count)
    grad_low_qkv = grad_low_qkv[:, : 3 * RANK].astype(BF16)
    grad_normed_attn = attn_back + nt(grad_low_qkv, in_qkv)
    input_grad = (grad_mid + norm_back(resid_in, norm_gains[0], grad_normed_attn)).astype(BF16)

    if count == 4:
        return (layer_out, input_grad, *adapter_grads)

    def packed(parts, blocks):
        return pad_lanes(jnp.concatenate(parts, axis=1).astype(BF16)).reshape(
            blocks, -1, LANES
        )

    d_grad = packed(
        [
            tn(normed_attn, grad_low_qkv),
            tn(normed_mlp, grad_low_gu),
            tn(grad_attn, low_out),
            tn(grad_mlp, low_down),
        ],
        lay.total,
    )
    f_grad = packed(f_parts, lay.dp)
    h_grad = packed([tn(attended, grad_low_out), tn(grad_q_pre, low_q)], lay.dp)
    k_grad = packed([tn(grad_k_pre, low_k), tn(grad_v_pre, low_v)], lay.kv_owners)
    d_all, f_all, h_all, k_all = exchange(
        grads_kernel,
        "adapter_grads",
        4,
        (d_grad, f_grad, h_grad, k_grad),
        (
            (lay.total, d_rows, LANES),
            (lay.dp, f_rows, LANES),
            (lay.dp, h_rows, LANES),
            (lay.dp * lay.share, k_rows, LANES),
        ),
        lay.dp,
        lay.total,
        lay.share,
    )

    def collect(received):
        repeats = received.shape[0] // lay.dp
        hot = jnp.repeat(group_hot, repeats, axis=0)
        return lax.dot_general(
            hot, received, (((0,), (0,)), ((), ())), preferred_element_type=F32
        )

    d_all, f_all, h_all, k_all = (collect(item) for item in (d_all, f_all, h_all, k_all))

    def lift_form(values, shape):
        return jnp.moveaxis(values, 1, 2).reshape(shape)

    return (
        layer_out,
        input_grad,
        d_all[:, :, : 5 * RANK],
        h_all[:, :, :RANK],
        f_all[:, :, :RANK],
        lift_form(h_all[:, :, RANK : 2 * RANK], lift_query.shape),
        lift_form(k_all[:, :, : 2 * RANK], lift_keyval.shape),
        lift_form(f_all[:, :, RANK : 3 * RANK], lift_gateup.shape),
        lift_form(d_all[:, :, 5 * RANK : 7 * RANK], lift_resid.shape),
    )


def solution(mesh):
    return jax.shard_map(
        per_device,
        mesh=mesh,
        in_specs=(
            P(("dp", "tensor"), None),
            P(("dp", "tensor"), None),
            P("dp"),
            P("dp", None),
            P(),
            P("dp", "tensor"),
            P("dp", None),
            P("dp", None),
            P("tensor", "dp"),
            P("dp", "tensor"),
            P("dp", "tensor"),
            P("tensor", "dp"),
            P(None, ("dp", "tensor"), None),
            P(None, ("dp", "tensor"), None),
            P(None, ("dp", "tensor"), None),
            P(None, None, ("dp", "tensor")),
            P(None, None, None, ("dp", "tensor")),
            P(None, None, None, ("dp", "tensor")),
            P(None, None, None, ("dp", "tensor")),
        ),
        out_specs=(
            P(("dp", "tensor"), None),
            P(("dp", "tensor"), None),
            P(None, ("dp", "tensor"), None),
            P(None, ("dp", "tensor"), None),
            P(None, ("dp", "tensor"), None),
            P(None, None, ("dp", "tensor")),
            P(None, None, None, ("dp", "tensor")),
            P(None, None, None, ("dp", "tensor")),
            P(None, None, None, ("dp", "tensor")),
        ),
        check_vma=False,
    )
```

```python
import functools

import jax
import jax.numpy as jnp
from jax import lax
from jax.experimental import pallas as pl
from jax.experimental.pallas import tpu as pltpu
from jax.sharding import PartitionSpec as P

D = 2304
HQ = 8
KV = 4
HD = 256
FF = 9216
NA = 8
RANK = 16
LEN = 1024
LANES = 128

EPSILON = 1e-06
SOFT_CAP = 50.0
MESH = pl.DeviceIdType.MESH
BF16 = jnp.bfloat16
F32 = jnp.float32
VMEM_LIMIT = 48 * 1024 * 1024


def rms_norm(values, gain_row):
    return (
        values * lax.rsqrt(jnp.mean(values * values, axis=-1, keepdims=True) + EPSILON) * gain_row
    )


def norm_back(values, gain_row, gradient):
    inverse = lax.rsqrt(jnp.mean(values * values, axis=-1, keepdims=True) + EPSILON)
    scaled = gradient * gain_row
    normed = values * inverse
    return inverse * (scaled - normed * jnp.mean(scaled * normed, axis=-1, keepdims=True))


def gelu_parts(gate, up):
    scale = (2.0 / jnp.pi) ** 0.5
    square = gate * gate
    bend = jnp.tanh(scale * gate * (1.0 + 0.044715 * square))
    low = 0.5 * (1.0 + bend)
    gelu = gate * low
    slope = low + 0.5 * gate * (1.0 - bend * bend) * (scale * (1.0 + 3.0 * 0.044715 * square))
    return (gelu * up).astype(BF16), (slope * up).astype(BF16), gelu.astype(BF16)


def tables(length, size):
    half_size = size // 2
    frequency = 10000.0 ** (-2.0 * jnp.arange(half_size, dtype=F32) / size)
    angles = jnp.arange(length, dtype=F32)[:, None] * frequency[None, :]
    return (jnp.cos(angles)[:, None, :], jnp.sin(angles)[:, None, :])


def rotate(values, cosine, sine):
    half_size = values.shape[-1] // 2
    first_half = values[..., :half_size]
    second_half = values[..., half_size:]
    return jnp.concatenate(
        [first_half * cosine - second_half * sine, second_half * cosine + first_half * sine],
        axis=-1,
    )


def nn(a, b):
    return lax.dot_general(a, b, (((1,), (0,)), ((), ())), preferred_element_type=F32)


def nt(a, b):
    return lax.dot_general(a, b, (((1,), (1,)), ((), ())), preferred_element_type=F32)


def tn(a, b):
    return lax.dot_general(a, b, (((0,), (0,)), ((), ())), preferred_element_type=F32)


def pad_lanes(values):
    return jnp.pad(values, [(0, 0)] * (values.ndim - 1) + [(0, LANES - values.shape[-1])])


def greet(peers):
    barrier = pltpu.get_barrier_semaphore()
    for peer in peers:
        pl.semaphore_signal(barrier, inc=1, device_id=peer, device_id_type=MESH)
    pl.semaphore_wait(barrier, len(peers))


def square_peers(index):
    return index + 1 - 2 * lax.rem(index, 2), lax.rem(index + 2, 4), 3 - index


def remote(source, target, send_sem, recv_sem, peer):
    return pltpu.make_async_remote_copy(
        src_ref=source,
        dst_ref=target,
        send_sem=send_sem,
        recv_sem=recv_sem,
        device_id={"tensor": peer},
        device_id_type=MESH,
    )


def gather_kernel(count, rows, x_ref, o_ref, local_sem, send_sem, recv_sem):
    me = lax.axis_index("tensor")
    if count == 4:
        across, down, _ = square_peers(me)
        greet([{"tensor": across}, {"tensor": down}])
        own = pltpu.make_async_copy(x_ref, o_ref.at[pl.ds(me * rows, rows)], local_sem)
        own.start()
        half = rows // 2
        links = (across, down)
        first = [[None, None], [None, None]]
        for order in range(2):
            for link in range(2):
                part = order if link == 0 else 1 - order
                target = o_ref.at[pl.ds(me * rows + part * half, half)]
                copy = remote(
                    x_ref.at[pl.ds(part * half, half)],
                    target,
                    send_sem.at[link, part],
                    recv_sem.at[link, part],
                    links[link],
                )
                copy.start()
                first[link][part] = copy
        second = []
        for link in range(2):
            first[link][link].wait_recv()
            block = o_ref.at[pl.ds(links[link] * rows + link * half, half)]
            copy = remote(
                block, block, send_sem.at[2, link], recv_sem.at[2, link], links[1 - link]
            )
            copy.start()
            second.append(copy)
        for link in range(2):
            first[link][1 - link].wait_recv()
        for copy in second:
            copy.wait_recv()
        own.wait()
        for link in range(2):
            for part in range(2):
                first[link][part].wait_send()
        for copy in second:
            copy.wait_send()
    else:
        peers = [lax.rem(me + step, count) for step in range(1, count)]
        greet([{"tensor": peer} for peer in peers])
        own = pltpu.make_async_copy(x_ref, o_ref.at[pl.ds(me * rows, rows)], local_sem)
        own.start()
        copies = []
        for step, peer in enumerate(peers):
            copy = remote(
                x_ref,
                o_ref.at[pl.ds(me * rows, rows)],
                send_sem.at[0, step],
                recv_sem.at[0, step],
                peer,
            )
            copy.start()
            copies.append(copy)
        own.wait()
        for copy in copies:
            copy.wait()


def tensor_gather(values, count):
    rows, width = values.shape
    slots = max(2, count - 1)
    return pl.pallas_call(
        functools.partial(gather_kernel, count, rows),
        out_shape=jax.ShapeDtypeStruct((count * rows, width), values.dtype),
        in_specs=[pl.BlockSpec(memory_space=pl.ANY)],
        out_specs=pl.BlockSpec(memory_space=pl.ANY),
        scratch_shapes=[
            pltpu.SemaphoreType.DMA,
            pltpu.SemaphoreType.DMA((3, slots)),
            pltpu.SemaphoreType.DMA((3, slots)),
        ],
        compiler_params=pltpu.CompilerParams(
            collective_id=1, has_side_effects=True, vmem_limit_bytes=VMEM_LIMIT
        ),
        name="tensor_gather",
    )(values)


def scatter_kernel(count, rows, p_ref, q_ref, o_ref, l_ref, *scratch):
    me = lax.axis_index("tensor")
    payload = ((p_ref, o_ref), (q_ref, l_ref))
    if count == 4:
        across, down, far = square_peers(me)
        greet([{"tensor": across}, {"tensor": down}])
        half = rows // 2
        first = scratch[0:2]
        sums = scratch[2:4]
        second = scratch[4:6]
        send_sem, recv_sem = scratch[6], scratch[7]
        links = (across, down)
        copies = {}
        for which in (1, 0):
            for link in range(2):
                block = far if which == 1 else links[link]
                for item in range(2):
                    copy = remote(
                        payload[item][0].at[pl.ds(block * rows + link * half, half)],
                        first[item].at[link, which],
                        send_sem.at[item, link, which],
                        recv_sem.at[item, link, which],
                        links[link],
                    )
                    copy.start()
                    copies[item, link, which] = copy
        for link in range(2):
            block = links[1 - link]
            for item in range(2):
                copies[item, link, 1].wait_recv()
                mine = payload[item][0][pl.ds(block * rows + link * half, half), :]
                sums[item][link] = (
                    mine.astype(F32) + first[item][link, 1].astype(F32)
                ).astype(BF16)
                copy = remote(
                    sums[item].at[link],
                    second[item].at[link],
                    send_sem.at[item, link, 2],
                    recv_sem.at[item, link, 2],
                    links[1 - link],
                )
                copy.start()
                copies[item, link, 2] = copy
        for link in range(2):
            for item in range(2):
                copies[item, link, 0].wait_recv()
                mine = payload[item][0][pl.ds(me * rows + link * half, half), :]
                payload[item][1][pl.ds(link * half, half), :] = mine.astype(F32) + first[item][
                    link, 0
                ].astype(F32)
        for link in range(2):
            for item in range(2):
                copies[item, link, 2].wait_recv()
                payload[item][1][pl.ds(link * half, half), :] += second[item][link].astype(F32)
        for copy in copies.values():
            copy.wait_send()
    else:
        peers = [lax.rem(me + step, count) for step in range(1, count)]
        greet([{"tensor": peer} for peer in peers])
        first = scratch[0:2]
        send_sem, recv_sem = scratch[2], scratch[3]
        copies = []
        for step, peer in enumerate(peers):
            for item in range(2):
                copy = remote(
                    payload[item][0].at[pl.ds(peer * rows, rows)],
                    first[item].at[step],
                    send_sem.at[item, step],
                    recv_sem.at[item, step],
                    peer,
                )
                copy.start()
                copies.append((item, step, copy))
        for item in range(2):
            payload[item][1][...] = payload[item][0][pl.ds(me * rows, rows), :].astype(F32)
        for item, step, copy in copies:
            copy.wait()
            payload[item][1][...] += first[item][step].astype(F32)


def tensor_scatter(values, narrow, count):
    rows = values.shape[0] // count
    widths = (values.shape[1], narrow.shape[1])
    if count == 4:
        half = rows // 2
        scratch = [pltpu.VMEM((2, 2, half, width), BF16) for width in widths]
        scratch += [pltpu.VMEM((2, half, width), BF16) for width in widths]
        scratch += [pltpu.VMEM((2, half, width), BF16) for width in widths]
        scratch += [pltpu.SemaphoreType.DMA((2, 2, 3)), pltpu.SemaphoreType.DMA((2, 2, 3))]
    else:
        scratch = [pltpu.VMEM((count - 1, rows, width), BF16) for width in widths]
        scratch += [pltpu.SemaphoreType.DMA((2, count - 1))] * 2
    vmem = pl.BlockSpec(memory_space=pltpu.VMEM)
    return pl.pallas_call(
        functools.partial(scatter_kernel, count, rows),
        out_shape=tuple(jax.ShapeDtypeStruct((rows, width), F32) for width in widths),
        in_specs=[vmem, vmem],
        out_specs=(vmem, vmem),
        scratch_shapes=scratch,
        compiler_params=pltpu.CompilerParams(
            collective_id=2, has_side_effects=True, vmem_limit_bytes=VMEM_LIMIT
        ),
        name="tensor_scatter",
    )(values, narrow)


class Square:
    def __init__(self, rows):
        self.rows = rows
        self.half = rows // 2
        self.me = lax.axis_index("tensor")
        self.across, self.down, self.far = square_peers(self.me)
        self.links = (self.across, self.down)

    def greet(self):
        greet([{"tensor": self.across}, {"tensor": self.down}])


class ChunkGather:
    def __init__(self, sq, source, buf, send_sem, recv_sem):
        half = sq.half
        self.first, self.second, self.onward = [], [], []
        for link in range(2):
            for order in range(2):
                part = link if order == 0 else 1 - link
                copy = remote(
                    source.at[pl.ds(part * half, half)],
                    buf.at[1 + order, pl.ds(link * half, half)],
                    send_sem.at[2 * order + link],
                    recv_sem.at[2 * order + link],
                    sq.links[link],
                )
                (self.first if order == 0 else self.second).append(copy)
            self.onward.append(
                remote(
                    buf.at[1, pl.ds(link * half, half)],
                    buf.at[3, pl.ds(link * half, half)],
                    send_sem.at[4 + link],
                    recv_sem.at[4 + link],
                    sq.links[1 - link],
                )
            )

    def start(self):
        for copy in self.first + self.second:
            copy.start()

    def wait_chunk(self, chunk):
        if chunk == 1:
            for copy in self.first:
                copy.wait_recv()
            for copy in self.onward:
                copy.start()
        if chunk == 2:
            for copy in self.second:
                copy.wait_recv()
        if chunk == 3:
            for copy in self.onward:
                copy.wait_recv()

    def finish(self):
        for copy in self.first + self.second + self.onward:
            copy.wait_send()


class ChunkScatter:
    def __init__(self, sq, part, landing, passed, send_sem, recv_sem):
        self.sq, self.half = sq, sq.half
        self.part, self.landing, self.passed = part, landing, passed
        self.send_sem, self.recv_sem = send_sem, recv_sem

    def copy(self, kind, link):
        rows = pl.ds(link * self.half, self.half)
        source = (
            self.passed.at[link] if kind == 2 else self.part.at[1 + 2 * kind, rows]
        )
        slot = 2 * kind + link
        return remote(
            source,
            self.landing.at[slot],
            self.send_sem.at[slot],
            self.recv_sem.at[slot],
            self.sq.links[1 - link if kind == 2 else link],
        )

    def send_own(self):
        for link in range(2):
            self.copy(0, link).start()

    def send_far(self):
        for link in range(2):
            self.copy(1, link).start()

    def pass_on(self, link):
        self.copy(1, link).wait_recv()
        rows = pl.ds((1 - link) * self.half, self.half)
        mine = self.part[2, rows, :].astype(F32)
        self.passed[link] = (mine + self.landing[2 + link].astype(F32)).astype(BF16)
        self.copy(2, link).start()

    def collect(self, out_ref, first=0):
        for link in range(2):
            self.copy(0, link).wait_recv()
            self.copy(2, link).wait_recv()
            rows = pl.ds(link * self.half, self.half)
            out_ref[rows, first : first + self.part.shape[-1]] = (
                self.part[0, rows, :].astype(F32)
                + self.landing[link].astype(F32)
                + self.landing[4 + link].astype(F32)
            )

    def finish(self):
        for kind in range(3):
            for link in range(2):
                self.copy(kind, link).wait_send()


def scatter_scratch(rows, width):
    half = rows // 2
    return [
        pltpu.VMEM((4, rows, width), BF16),
        pltpu.VMEM((6, half, width), BF16),
        pltpu.VMEM((2, half, width), BF16),
        pltpu.SemaphoreType.DMA((6,)),
        pltpu.SemaphoreType.DMA((6,)),
    ]


def tile_of(width):
    return 768 if width % 768 == 0 else 384


def columns(step, tile, base=0):
    return pl.ds(pl.multiple_of(base + step * tile, LANES), tile)


def mlp_back_kernel(
    rows,
    g_ref,
    down_hbm,
    gu_hbm,
    slope_hbm,
    gelu_hbm,
    hidden_hbm,
    low_hbm,
    lift_down_ref,
    map_ref,
    lift_gu_ref,
    o_ref,
    l_ref,
    f_out,
    f_ref,
    down_w,
    gu_w,
    buf,
    slope,
    gelu,
    hidden,
    low,
    grads,
    weight_sem,
    load_sem,
    own_sem,
    gather_send,
    gather_recv,
    *scratch,
):
    sq = Square(rows)
    width = hidden.shape[-1]
    model = o_ref.shape[-1]
    down_load = pltpu.make_async_copy(down_hbm, down_w, weight_sem.at[0])
    gu_load = pltpu.make_async_copy(gu_hbm, gu_w, weight_sem.at[1])
    own_load = pltpu.make_async_copy(g_ref, buf.at[0], own_sem)

    def loads(chunk):
        slot = chunk % 2
        return [
            pltpu.make_async_copy(source.at[chunk], target.at[slot], load_sem.at[slot, item])
            for item, (source, target) in enumerate(
                ((slope_hbm, slope), (gelu_hbm, gelu), (hidden_hbm, hidden), (low_hbm, low))
            )
        ]

    down_load.start()
    own_load.start()
    for copy in loads(0):
        copy.start()
    sq.greet()
    gather = ChunkGather(sq, g_ref, buf, gather_send, gather_recv)
    gather.start()
    gu_load.start()
    part, part_low = scratch[0], scratch[5]
    scatters = (ChunkScatter(sq, *scratch[:5]), ChunkScatter(sq, *scratch[5:10]))
    f_ref[...] = jnp.zeros_like(f_ref)
    own_load.wait()
    down_load.wait()

    @pl.loop(0, 4)
    def _(chunk):
        slot = lax.rem(chunk, 2)
        for step in range(4):

            @pl.when(chunk == step)
            def _(step=step):
                gather.wait_chunk(step)
                for copy in loads(step):
                    copy.wait()
                if step < 3:
                    for copy in loads(step + 1):
                        copy.start()

        incoming = buf.at[chunk]
        low_down = nn(incoming[...], lift_down_ref[...]).astype(BF16)
        tile = tile_of(width)

        @pl.loop(0, width // tile)
        def _(step):
            here = columns(step, tile)
            grad = nn(incoming[...], down_w[:, here]) + nt(low_down, map_ref[here, :])
            grads[:, here] = (grad * slope[slot, :, here].astype(F32)).astype(BF16)
            grads[:, columns(step, tile, width)] = (
                grad * gelu[slot, :, here].astype(F32)
            ).astype(BF16)

        @pl.when(chunk == 0)
        def _():
            gu_load.wait()

        part_low[chunk] = nn(grads[...], lift_gu_ref[...]).astype(BF16)
        wide = tile_of(model)

        @pl.loop(0, model // wide)
        def _(step):
            here = columns(step, wide)
            part[chunk, :, here] = nt(grads[...], gu_w[here, :]).astype(BF16)

        @pl.when(chunk == 1)
        def _():
            for scatter in scatters:
                scatter.send_own()

        @pl.when(chunk == 3)
        def _():
            for scatter in scatters:
                scatter.send_far()

        low_turned = low_down.astype(F32).T[:RANK].astype(BF16)
        gu_turned = low[slot].astype(F32).T.astype(BF16)
        f_ref[:RANK, :] += nn(low_turned, hidden[slot])
        f_ref[RANK : 2 * RANK, :] += nn(gu_turned[:RANK], grads[:, :width])
        f_ref[2 * RANK : 3 * RANK, :] += nn(gu_turned[RANK : 2 * RANK], grads[:, width:])

    @pl.loop(0, width // LANES)
    def _(step):
        here = columns(step, LANES)
        f_out[here, :] = jnp.concatenate(
            [f_ref[:, here], jnp.zeros((LANES - 4 * RANK, LANES), F32)], axis=0
        ).T.astype(BF16)

    for link in range(2):
        for scatter in scatters:
            scatter.pass_on(link)
    gather.finish()
    scatters[0].collect(o_ref)
    scatters[1].collect(l_ref)
    for scatter in scatters:
        scatter.finish()


def mlp_back_fused(grad, down_w, gu_w, slope, gelu, hidden, low, lift_down, map_hidden, lift_gu):
    rows, model = grad.shape
    width = hidden.shape[2]
    anywhere = pl.BlockSpec(memory_space=pl.ANY)
    vmem = pl.BlockSpec(memory_space=pltpu.VMEM)
    return pl.pallas_call(
        functools.partial(mlp_back_kernel, rows),
        out_shape=(
            jax.ShapeDtypeStruct((rows, model), F32),
            jax.ShapeDtypeStruct((rows, LANES), F32),
            jax.ShapeDtypeStruct((width, LANES), BF16),
        ),
        in_specs=[vmem] + [anywhere] * 6 + [vmem] * 3,
        out_specs=(vmem,) * 3,
        scratch_shapes=[
            pltpu.VMEM((4 * RANK, width), F32),
            pltpu.VMEM((model, width), BF16),
            pltpu.VMEM((model, 2 * width), BF16),
            pltpu.VMEM((4, rows, model), BF16),
            pltpu.VMEM((2, rows, width), BF16),
            pltpu.VMEM((2, rows, width), BF16),
            pltpu.VMEM((2, rows, width), BF16),
            pltpu.VMEM((2, rows, LANES), BF16),
            pltpu.VMEM((rows, 2 * width), BF16),
            pltpu.SemaphoreType.DMA((2,)),
            pltpu.SemaphoreType.DMA((2, 4)),
            pltpu.SemaphoreType.DMA,
            pltpu.SemaphoreType.DMA((6,)),
            pltpu.SemaphoreType.DMA((6,)),
        ]
        + scatter_scratch(rows, model)
        + scatter_scratch(rows, LANES),
        compiler_params=pltpu.CompilerParams(
            collective_id=5, has_side_effects=True, vmem_limit_bytes=62 * 1024 * 1024
        ),
        name="mlp_back",
    )(grad, down_w, gu_w, slope, gelu, hidden, low, lift_down, map_hidden, lift_gu)


class Line:
    def __init__(self, slots, send_sem, recv_sem):
        self.d = lax.axis_index("dp")
        self.places = lax.axis_size("dp") // 2
        self.core = lax.rem(self.d, 2)
        self.z = self.d // 2
        self.sibling = self.d + 1 - 2 * self.core
        self.slots, self.send_sem, self.recv_sem = slots, send_sem, recv_sem

    def greet(self, others):
        barrier = pltpu.get_barrier_semaphore()
        for peer in others + [{"dp": self.sibling}]:
            pl.semaphore_signal(barrier, inc=1, device_id=peer, device_id_type=MESH)

        @pl.when(self.z > 0)
        def _():
            pl.semaphore_signal(
                barrier, inc=1, device_id={"dp": self.d - 2}, device_id_type=MESH
            )

        @pl.when(self.z < self.places - 1)
        def _():
            pl.semaphore_signal(
                barrier, inc=1, device_id={"dp": self.d + 2}, device_id_type=MESH
            )

        last = self.places - 1
        ends = (last - self.z) // last + self.z // last
        pl.semaphore_wait(barrier, len(others) + 3 - ends)

    def copy(self, place, kind):
        target = (self.d + 2, self.d - 2, self.sibling)[kind]
        slot = 2 * place + self.core
        return pltpu.make_async_remote_copy(
            src_ref=self.slots.at[slot],
            dst_ref=self.slots.at[slot],
            send_sem=self.send_sem.at[kind, place],
            recv_sem=self.recv_sem.at[slot],
            device_id={"dp": target},
            device_id_type=MESH,
        )

    def send_up(self, place):
        @pl.when(self.z < self.places - 1)
        def _():
            self.copy(place, 0).start()

    def send_down(self, place):
        @pl.when(self.z > 0)
        def _():
            self.copy(place, 1).start()

    def start(self):
        self.send_up(self.z)
        self.send_down(self.z)
        self.copy(self.z, 2).start()

    def arrive(self, distance):
        @pl.when(self.z >= distance)
        def _():
            place = self.z - distance
            self.copy(place, 2).wait_recv()
            self.send_up(place)
            self.copy(place, 2).start()

        @pl.when(self.z + distance < self.places)
        def _():
            place = self.z + distance
            self.copy(place, 2).wait_recv()
            self.send_down(place)
            self.copy(place, 2).start()

    def wait_sibling(self, place):
        slot = self.slots.at[2 * place + 1 - self.core]
        pltpu.make_async_copy(
            slot, slot, self.recv_sem.at[2 * place + 1 - self.core]
        ).wait()

    def finish(self):
        for place in range(self.places):

            @pl.when((self.z >= place) & (self.z < self.places - 1))
            def _(place=place):
                self.copy(place, 0).wait_send()

            @pl.when((self.z <= place) & (self.z > 0))
            def _(place=place):
                self.copy(place, 1).wait_send()

            self.copy(place, 2).wait_send()


ARRIVALS = ((0, 1, 2, 3), (1, 0, 2, 3), (2, 1, 3, 0), (3, 2, 1, 0))


def mlp_kernel(
    rows,
    x_hbm,
    gu_hbm,
    shard_hbm,
    low_ref,
    lift_gu_ref,
    map_ref,
    o_ref,
    l_ref,
    hidden_out,
    slope_out,
    gelu_out,
    down_out,
    seq,
    tiles,
    hidden,
    slope,
    gelu,
    down,
    load_sem,
    tile_sem,
    store_sem,
    keep_sem,
    line_send,
    line_recv,
    part,
    landing,
    passed,
    part_send,
    part_recv,
    *low_scratch,
):
    sq = Square(rows)
    line = Line(down, line_send, line_recv)
    width = hidden.shape[-1]
    tile = tiles.shape[-1] // 2
    steps = width // tile
    own_shard = pltpu.make_async_copy(shard_hbm, down.at[line.d], load_sem.at[0])
    seq_load = pltpu.make_async_copy(x_hbm, seq, load_sem.at[1])

    def tile_loads(step, slot):
        return [
            pltpu.make_async_copy(
                gu_hbm.at[:, columns(step, tile, which * width)],
                tiles.at[slot, :, pl.ds(which * tile, tile)],
                tile_sem.at[slot, which],
            )
            for which in range(2)
        ]

    def stores(step, slot):
        here = columns(step, tile)
        return [
            pltpu.make_async_copy(
                source.at[slot], target.at[:, :, here], store_sem.at[slot, which]
            )
            for which, (source, target) in enumerate(((slope, slope_out), (gelu, gelu_out)))
        ]

    own_shard.start()
    seq_load.start()
    for copy in tile_loads(0, 0):
        copy.start()
    line.greet([{"tensor": sq.across}, {"tensor": sq.down}])
    own_shard.wait()
    line.start()
    seq_load.wait()

    @pl.loop(0, steps)
    def _(step):
        slot = lax.rem(step, 2)
        for copy in tile_loads(step, slot):
            copy.wait()

        @pl.when(step + 1 < steps)
        def _():
            for copy in tile_loads(step + 1, 1 - slot):
                copy.start()

        @pl.when(step >= 2)
        def _():
            for copy in stores(step - 2, slot):
                copy.wait()

        here = columns(step, tile)

        @pl.loop(0, 4)
        def _(chunk):
            both = nn(seq[chunk], tiles[slot])
            gate = both[:, :tile] + nt(low_ref[chunk], lift_gu_ref[here, :])
            up = both[:, tile:] + nt(low_ref[chunk], lift_gu_ref[columns(step, tile, width), :])
            hidden[chunk, :, here], slope[slot, chunk], gelu[slot, chunk] = gelu_parts(gate, up)

        for copy in stores(step, slot):
            copy.start()

        @pl.when(step == steps - 2)
        def _():
            line.arrive(1)

    keep_hidden = pltpu.make_async_copy(hidden, hidden_out, keep_sem.at[0])
    keep_hidden.start()
    last = line.places - 1
    is_first, is_last = (last - line.z) // last, line.z // last
    is_third = line.z // 2 - is_last
    is_here = (is_first, 1 - is_first - is_third - is_last, is_third, is_last)
    order = [sum(flag * ARRIVALS[z][i] for z, flag in enumerate(is_here)) for i in range(4)]

    def scatter_at(place):
        return ChunkScatter(
            sq,
            part.at[place],
            landing.at[place],
            passed.at[place],
            part_send.at[place],
            part_recv.at[place],
        )

    low_scatter = ChunkScatter(sq, *low_scratch)

    @pl.loop(0, 4)
    def _(chunk):
        low_scratch[0][chunk] = nn(hidden[chunk], map_ref[...]).astype(BF16)

    low_scatter.send_far()
    low_scatter.send_own()
    keeps = []
    for step in range(4):
        if step >= 2:
            line.arrive(step)
        place = order[step]
        line.wait_sibling(place)
        pair = pl.ds(2 * place, 2)
        keep = pltpu.make_async_copy(down.at[pair], down_out.at[pair], keep_sem.at[1 + step])
        keep.start()
        keeps.append(keep)
        scatter = scatter_at(place)
        shard_rows = down.shape[1]

        @pl.loop(0, 4)
        def _(turn, place=place, scatter=scatter):
            chunk = turn + 3 * ((3 - turn) // 3) - 3 * (turn // 3)
            for core in range(2):
                part[place, chunk, :, core * shard_rows : (core + 1) * shard_rows] = nt(
                    hidden[chunk], down[2 * place + core]
                ).astype(BF16)

            @pl.when(turn == 0)
            def _():
                scatter.send_far()

            @pl.when(turn == 1)
            def _():
                scatter.send_own()

        if step > 0:
            for link in range(2):
                scatter_at(order[step - 1]).pass_on(link)
        else:
            for link in range(2):
                low_scatter.pass_on(link)
    for link in range(2):
        scatter_at(order[3]).pass_on(link)
    wide = part.shape[-1]
    low_scatter.collect(l_ref)
    for place in range(4):
        scatter_at(place).collect(o_ref, place * wide)
    for place in range(4):
        scatter_at(place).finish()
    low_scatter.finish()
    line.finish()
    for step in (steps - 2, steps - 1):
        for copy in stores(step, step % 2):
            copy.wait()
    keep_hidden.wait()
    for keep in keeps:
        keep.wait()


def mlp_fused(seq, gu_w, shard, low, lift_gu, map_hidden, dp):
    chunks, rows, model = seq.shape
    width = shard.shape[1]
    tile = 384
    wide = model // (dp // 2)
    half = rows // 2
    anywhere = pl.BlockSpec(memory_space=pl.ANY)
    vmem = pl.BlockSpec(memory_space=pltpu.VMEM)
    saved = jax.ShapeDtypeStruct((4, rows, width), BF16)
    return pl.pallas_call(
        functools.partial(mlp_kernel, rows),
        out_shape=(
            jax.ShapeDtypeStruct((rows, model), F32),
            jax.ShapeDtypeStruct((rows, LANES), F32),
            saved,
            saved,
            saved,
            jax.ShapeDtypeStruct((dp,) + shard.shape, BF16),
        ),
        in_specs=[anywhere] * 3 + [vmem] * 3,
        out_specs=(vmem, vmem) + (anywhere,) * 4,
        scratch_shapes=[
            pltpu.VMEM((4, rows, model), BF16),
            pltpu.VMEM((2, model, 2 * tile), BF16),
            pltpu.VMEM((4, rows, width), BF16),
            pltpu.VMEM((2, 4, rows, tile), BF16),
            pltpu.VMEM((2, 4, rows, tile), BF16),
            pltpu.VMEM((dp,) + shard.shape, BF16),
            pltpu.SemaphoreType.DMA((2,)),
            pltpu.SemaphoreType.DMA((2, 2)),
            pltpu.SemaphoreType.DMA((2, 2)),
            pltpu.SemaphoreType.DMA((5,)),
            pltpu.SemaphoreType.DMA((3, dp // 2)),
            pltpu.SemaphoreType.DMA((dp,)),
            pltpu.VMEM((4, 4, rows, wide), BF16),
            pltpu.VMEM((4, 6, half, wide), BF16),
            pltpu.VMEM((4, 2, half, wide), BF16),
            pltpu.SemaphoreType.DMA((4, 6)),
            pltpu.SemaphoreType.DMA((4, 6)),
        ]
        + scatter_scratch(rows, LANES),
        compiler_params=pltpu.CompilerParams(
            collective_id=7, has_side_effects=True, vmem_limit_bytes=62 * 1024 * 1024
        ),
        name="mlp",
    )(seq, gu_w, shard, low, lift_gu, map_hidden)


def chunk_gather_kernel(rows, x_ref, o_ref, own_sem, send_sem, recv_sem):
    sq = Square(rows)
    sq.greet()
    gather = ChunkGather(sq, x_ref, o_ref, send_sem, recv_sem)
    gather.start()
    own = pltpu.make_async_copy(x_ref, o_ref.at[0], own_sem)
    own.start()
    for chunk in range(1, 4):
        gather.wait_chunk(chunk)
    own.wait()
    gather.finish()


def chunk_gather(values):
    rows, width = values.shape
    anywhere = pl.BlockSpec(memory_space=pl.ANY)
    return pl.pallas_call(
        functools.partial(chunk_gather_kernel, rows),
        out_shape=jax.ShapeDtypeStruct((4, rows, width), values.dtype),
        in_specs=[anywhere],
        out_specs=anywhere,
        scratch_shapes=[
            pltpu.SemaphoreType.DMA,
            pltpu.SemaphoreType.DMA((6,)),
            pltpu.SemaphoreType.DMA((6,)),
        ],
        compiler_params=pltpu.CompilerParams(
            collective_id=8, has_side_effects=True, vmem_limit_bytes=VMEM_LIMIT
        ),
        name="chunk_gather",
    )(values)


class Layout:
    def __init__(self):
        self.dp = lax.axis_size("dp")
        self.tensor = lax.axis_size("tensor")
        self.total = self.dp * self.tensor
        self.d = lax.axis_index("dp")
        self.t = lax.axis_index("tensor")
        self.me = self.d * self.tensor + self.t
        self.heads_here = HQ // self.tensor
        self.ratio = HQ // KV
        self.share = max(1, self.tensor // KV)
        self.kv_owners = self.total // KV
        self.kv_head = self.t * self.heads_here // self.ratio
        self.user = self.me // self.dp
        self.kv_slice_head = self.me // self.kv_owners

    def device(self, flat):
        return {"dp": flat // self.tensor, "tensor": lax.rem(flat, self.tensor)}


def greet_all(lay):
    barrier = pltpu.get_barrier_semaphore()

    def signal(step, unused):
        peer = lax.rem(lay.me + step, lay.total)
        pl.semaphore_signal(
            barrier, inc=1, device_id=lay.device(peer), device_id_type=MESH
        )
        return unused

    lax.fori_loop(1, lay.total, signal, 0)
    pl.semaphore_wait(barrier, lay.total - 1)


def send_or_keep(lay, sends, source, target, send_sem, recv_sem, flat, maybe_own):
    def far():
        return pltpu.make_async_remote_copy(
            src_ref=source,
            dst_ref=target,
            send_sem=send_sem,
            recv_sem=recv_sem,
            device_id=lay.device(flat),
            device_id_type=MESH,
        )

    if maybe_own is None:
        copy = far()
        copy.start()
        sends.append((None, copy))
        return

    @pl.when(maybe_own)
    def _():
        pltpu.make_async_copy(source, target, recv_sem).start()

    @pl.when(jnp.logical_not(maybe_own))
    def _():
        far().start()

    sends.append((maybe_own, far()))


def finish(sends, received):
    for own, copy in sends:
        if own is None:
            copy.wait_send()
        else:

            @pl.when(jnp.logical_not(own))
            def _(copy=copy):
                copy.wait_send()

    for target, sem in received:
        pltpu.make_async_copy(target, target, sem).wait()


def tables_kernel(d_ref, f_ref, h_ref, k_ref, do_ref, fo_ref, ho_ref, ko_ref, *sems):
    lay = Layout()
    send_sems, recv_sem = sems[:4], sems[4]
    greet_all(lay)
    sends = []
    for step in range(lay.dp):
        group = lax.rem(lay.d + step, lay.dp)
        flat = group * lay.tensor + lay.user
        own = (lay.user == lay.t) if step == 0 else None
        for item, (source, target) in enumerate(((f_ref, fo_ref), (h_ref, ho_ref))):
            send_or_keep(
                lay,
                sends,
                source.at[group],
                target.at[lax.rem(lay.me, lay.dp)],
                send_sems[item].at[step],
                recv_sem.at[item],
                flat,
                own,
            )
        for extra in range(lay.share):
            user = lay.kv_slice_head * lay.share + extra
            flat = group * lay.tensor + user
            send_or_keep(
                lay,
                sends,
                k_ref.at[group],
                ko_ref.at[lax.rem(lay.me, lay.kv_owners)],
                send_sems[2].at[step, extra],
                recv_sem.at[2],
                flat,
                (user == lay.t) if step == 0 else None,
            )
    pltpu.make_async_copy(d_ref.at[lay.d], do_ref.at[lay.me], recv_sem.at[3]).start()
    for step in range(1, lay.total):
        flat = lax.rem(lay.me + step, lay.total)
        send_or_keep(
            lay,
            sends,
            d_ref.at[flat // lay.tensor],
            do_ref.at[lay.me],
            send_sems[3].at[step],
            recv_sem.at[3],
            flat,
            None,
        )
    finish(
        sends,
        (
            (fo_ref, recv_sem.at[0]),
            (ho_ref, recv_sem.at[1]),
            (ko_ref, recv_sem.at[2]),
            (do_ref, recv_sem.at[3]),
        ),
    )


def grads_kernel(d_ref, f_ref, h_ref, k_ref, do_ref, fo_ref, ho_ref, ko_ref, *sems):
    lay = Layout()
    send_sems, recv_sem = sems[:4], sems[4]
    greet_all(lay)
    sends = []
    for step in range(lay.dp):
        slot = lax.rem(lay.d + step, lay.dp)
        flat = lay.t * lay.dp + slot
        for item, (source, target) in enumerate(((f_ref, fo_ref), (h_ref, ho_ref))):
            send_or_keep(
                lay,
                sends,
                source.at[slot],
                target.at[lay.d],
                send_sems[item].at[step],
                recv_sem.at[item],
                flat,
                flat == lay.me,
            )
    for step in range(lay.kv_owners):
        slot = lax.rem(lay.d + step, lay.kv_owners)
        flat = lay.kv_head * lay.kv_owners + slot
        send_or_keep(
            lay,
            sends,
            k_ref.at[slot],
            ko_ref.at[lay.d * lay.share + lax.rem(lay.t, lay.share)],
            send_sems[2].at[step // lay.share, step % lay.share],
            recv_sem.at[2],
            flat,
            flat == lay.me,
        )
    pltpu.make_async_copy(d_ref.at[lay.me], do_ref.at[lay.me], recv_sem.at[3]).start()
    for step in range(1, lay.total):
        flat = lax.rem(lay.me + step, lay.total)
        send_or_keep(
            lay,
            sends,
            d_ref.at[flat],
            do_ref.at[lay.me],
            send_sems[3].at[step],
            recv_sem.at[3],
            flat,
            None,
        )
    finish(
        sends,
        (
            (fo_ref, recv_sem.at[0]),
            (ho_ref, recv_sem.at[1]),
            (ko_ref, recv_sem.at[2]),
            (do_ref, recv_sem.at[3]),
        ),
    )


def exchange(kernel, name, number, arrays, outs, dp, total, share):
    anywhere = pl.BlockSpec(memory_space=pl.ANY)
    return pl.pallas_call(
        kernel,
        out_shape=tuple(jax.ShapeDtypeStruct(shape, BF16) for shape in outs),
        in_specs=[anywhere] * 4,
        out_specs=(anywhere,) * 4,
        scratch_shapes=[
            pltpu.SemaphoreType.DMA((dp,)),
            pltpu.SemaphoreType.DMA((dp,)),
            pltpu.SemaphoreType.DMA((dp, share)),
            pltpu.SemaphoreType.DMA((total,)),
            pltpu.SemaphoreType.DMA((4,)),
        ],
        compiler_params=pltpu.CompilerParams(
            collective_id=number, has_side_effects=True, vmem_limit_bytes=VMEM_LIMIT
        ),
        name=name,
    )(*arrays)


def chunk_start(sq, chunk, part):
    is_own = (3 - chunk) // 3
    is_far = chunk // 3
    near = 1 - is_own - is_far
    neighbour = sq.down if part == 1 else sq.across
    block = sq.me * is_own + sq.far * is_far + neighbour * near
    other_half = chunk // 2 - is_far
    half = 1 - other_half if part == 1 else other_half
    return pl.multiple_of(block * sq.rows + half * sq.half, sq.half)


def rotate_back(values, cosine, sine):
    first, second = values[:, : HD // 2], values[:, HD // 2 :]
    return jnp.concatenate([first * cosine + second * sine, second * cosine - first * sine], axis=1)


def attn_back_kernel(
    rows,
    ids_ref,
    length_ref,
    g_ref,
    weight_hbm,
    seq_hbm,
    q_ref,
    k_ref,
    kt_ref,
    v_ref,
    attended_ref,
    inverse_ref,
    cos_ref,
    sin_ref,
    low_ref,
    lift_out_ref,
    map_ref,
    lift_qkv_ref,
    normed_ref,
    grad_gu_ref,
    low_out_ref,
    grad_mlp_ref,
    low_down_ref,
    f_hbm,
    o_ref,
    l_ref,
    in_out,
    heads_out,
    hidden_out,
    query_out,
    keyval_out,
    gateup_out,
    resid_out,
    weight,
    seq,
    buf,
    att,
    q_grad,
    k_sum,
    v_sum,
    kv_grad,
    joined,
    d_turned,
    h_turned,
    k_turned,
    d_send,
    h_send,
    k_send,
    d_recv,
    f_recv,
    h_recv,
    k_recv,
    load_sem,
    own_sem,
    gather_send,
    gather_recv,
    d_sem,
    f_sem,
    h_sem,
    k_sem,
    recv_sem,
    *scratch,
):
    sq = Square(rows)
    lay = Layout()
    half = sq.half
    model = o_ref.shape[-1]
    weight_load = pltpu.make_async_copy(weight_hbm, weight, load_sem.at[0])
    seq_load = pltpu.make_async_copy(seq_hbm, seq, load_sem.at[1])
    own_load = pltpu.make_async_copy(g_ref, buf.at[0], own_sem)
    weight_load.start()
    own_load.start()
    greet_all(lay)
    gather = ChunkGather(sq, g_ref, buf, gather_send, gather_recv)
    gather.start()
    seq_load.start()
    sends = []
    for step in range(lay.dp):
        slot = lax.rem(lay.d + step, lay.dp)
        flat = lay.t * lay.dp + slot
        send_or_keep(
            lay,
            sends,
            f_hbm.at[slot],
            f_recv.at[lay.d],
            f_sem.at[step],
            recv_sem.at[0],
            flat,
            flat == lay.me,
        )
    part, part_low = scratch[0], scratch[5]
    scatters = (ChunkScatter(sq, *scratch[:5]), ChunkScatter(sq, *scratch[5:10]))

    def turned(values):
        return values.astype(F32).T.astype(BF16)

    d_turned[...] = jnp.zeros_like(d_turned)
    wide = tile_of(model)
    low_grads = (
        (turned(grad_gu_ref[...]), normed_ref, 3 * RANK, 2 * RANK),
        (turned(low_out_ref[...]), g_ref, 5 * RANK, RANK),
        (turned(low_down_ref[...]), grad_mlp_ref, 6 * RANK, RANK),
    )

    @pl.loop(0, model // wide)
    def _(step):
        here = columns(step, wide)
        for low, source, first, count in low_grads:
            d_turned[pl.ds(first, count), here] = nn(low[:count], source[:, here])

    h_turned[...] = jnp.zeros_like(h_turned)
    k_turned[...] = jnp.zeros_like(k_turned)
    k_sum[...] = jnp.zeros_like(k_sum)
    v_sum[...] = jnp.zeros_like(v_sum)
    own_load.wait()
    weight_load.wait()
    q_width = q_ref.shape[1]
    qkv_width = q_width + 2 * HD
    heads = q_width // HD
    stacked = heads * half

    @pl.loop(0, 4)
    def _(chunk):
        for step in range(4):

            @pl.when(chunk == step)
            def _(step=step):
                gather.wait_chunk(step)

        incoming = buf.at[chunk]
        low_out = nn(incoming[...], lift_out_ref[...]).astype(BF16)
        att[...] = (
            nn(incoming[...], weight[:, qkv_width:]) + nt(low_out, map_ref[...])
        ).astype(BF16)
        low_turned = turned(low_out)[:RANK]
        for side in range(2):
            start = chunk_start(sq, chunk, side)
            here = pl.ds(start, half)
            place = pl.ds(side * half, half)
            h_turned[:RANK, :] += nn(
                low_turned[:, side * half : (side + 1) * half], attended_ref[here, :]
            )
            queries = jnp.concatenate(
                [q_ref[here, h * HD : (h + 1) * HD] for h in range(heads)], axis=0
            )
            grads = jnp.concatenate(
                [att[place, h * HD : (h + 1) * HD] for h in range(heads)], axis=0
            )
            inverse = jnp.concatenate([inverse_ref[h : h + 1, here] for h in range(heads)], axis=1)
            key_at = lax.broadcasted_iota(jnp.int32, (LEN, stacked), 0)
            query_at = lax.rem(lax.broadcasted_iota(jnp.int32, (LEN, stacked), 1), half) + start
            allowed = (key_at <= query_at) & (key_at < length_ref[0])
            squash = jnp.tanh(nt(k_ref[...], queries) * (1.0 / SOFT_CAP))
            probs = jnp.where(allowed, jnp.exp(SOFT_CAP * squash) * inverse, 0.0)
            grad_probs = nt(v_ref[...], grads)
            mean = jnp.sum(probs * grad_probs, axis=0, keepdims=True)
            grad_raw = (probs * (grad_probs - mean) * (1.0 - squash * squash)).astype(BF16)
            k_sum[...] += nn(grad_raw, queries)
            v_sum[...] += nn(probs.astype(BF16), grads)
            q_back = nn(kt_ref[...], grad_raw).T * HD ** (-0.5)
            for h in range(heads):
                q_grad[chunk, place, h * HD : (h + 1) * HD] = rotate_back(
                    q_back[h * half : (h + 1) * half], cos_ref[here, :], sin_ref[here, :]
                ).astype(BF16)

    kv_grad[:, :HD] = rotate_back(k_sum[...], cos_ref[...], sin_ref[...]).astype(BF16)
    kv_grad[:, HD:] = v_sum[...].astype(BF16)

    @pl.loop(0, 4)
    def _(step):
        chunk = step + 3 * ((3 - step) // 3) - 3 * (step // 3)
        joined[chunk, :, :q_width] = q_grad[chunk]
        for side in range(2):
            here = pl.ds(chunk_start(sq, chunk, side), half)
            joined[chunk, pl.ds(side * half, half), q_width:] = kv_grad[here, :]
        part_low[chunk] = nn(joined[chunk], lift_qkv_ref[...]).astype(BF16)

        @pl.loop(0, model // wide)
        def _(tile):
            here = columns(tile, wide)
            part[chunk, :, here] = nt(joined[chunk], weight[here, :qkv_width]).astype(BF16)

        @pl.when(step == 0)
        def _():
            for scatter in scatters:
                scatter.send_far()

        @pl.when(step == 1)
        def _():
            for scatter in scatters:
                scatter.send_own()

    seq_load.wait()

    @pl.loop(0, 4)
    def _(chunk):
        grad_turned = turned(part_low[chunk])[: 3 * RANK]
        for side in range(2):
            here = pl.ds(chunk_start(sq, chunk, side), half)
            place = slice(side * half, (side + 1) * half)
            low_turned = turned(low_ref[here, :])
            mine = joined.at[chunk, pl.ds(side * half, half)]
            h_turned[RANK : 2 * RANK, :] += nn(low_turned[:RANK], mine[:, :q_width])
            k_turned[:RANK, :] += nn(
                low_turned[RANK : 2 * RANK], mine[:, q_width : q_width + HD]
            )
            k_turned[RANK : 2 * RANK, :] += nn(
                low_turned[2 * RANK : 3 * RANK], mine[:, q_width + HD :]
            )

            @pl.loop(0, model // wide)
            def _(tile):
                where = columns(tile, wide)
                d_turned[: 3 * RANK, where] += nn(grad_turned[:, place], seq[here, where])

    @pl.loop(0, model // LANES)
    def _(step):
        here = columns(step, LANES)
        d_send[here, :] = d_turned[:, here].T.astype(BF16)

    h_send[...] = h_turned[...].T.astype(BF16)
    k_send[...] = k_turned[...].T.astype(BF16)
    d_rows, h_rows, k_rows = d_recv.shape[1], h_recv.shape[1], k_recv.shape[1]
    for step in range(lay.dp):
        slot = lax.rem(lay.d + step, lay.dp)
        flat = lay.t * lay.dp + slot
        for item, (source, size, target, sem) in enumerate(
            ((h_send, h_rows, h_recv, h_sem), (k_send, k_rows, k_recv, k_sem))
        ):
            send_or_keep(
                lay,
                sends,
                source.at[pl.ds(pl.multiple_of(slot * size, size), size)],
                target.at[lay.d],
                sem.at[step],
                recv_sem.at[1 + item],
                flat,
                flat == lay.me,
            )
    pltpu.make_async_copy(
        d_send.at[pl.ds(pl.multiple_of(lay.me * d_rows, 8), d_rows)],
        d_recv.at[lay.me],
        recv_sem.at[3],
    ).start()
    for step in range(1, lay.total):
        flat = lax.rem(lay.me + step, lay.total)
        send_or_keep(
            lay,
            sends,
            d_send.at[pl.ds(pl.multiple_of(flat * d_rows, 8), d_rows)],
            d_recv.at[lay.me],
            d_sem.at[step],
            recv_sem.at[3],
            flat,
            None,
        )
    for link in range(2):
        for scatter in scatters:
            scatter.pass_on(link)
    scatters[0].collect(o_ref)
    scatters[1].collect(l_ref)
    finish(
        sends,
        (
            (f_recv, recv_sem.at[0]),
            (h_recv, recv_sem.at[1]),
            (k_recv, recv_sem.at[2]),
            (d_recv, recv_sem.at[3]),
        ),
    )

    @pl.loop(0, NA)
    def _(adapter):
        def pick(parts):
            total = None
            for group in range(lay.dp):
                mine = jnp.where(ids_ref[group] == adapter, parts(group), 0.0)
                total = mine if total is None else total + mine
            return total

        def d_part(group):
            return sum(
                d_recv[group * lay.tensor + t].astype(F32) for t in range(lay.tensor)
            )

        d_all = pick(d_part)
        in_out[adapter] = d_all[:, : 5 * RANK]
        d_flip = d_all.T
        f_all = pick(lambda group: f_recv[group].astype(F32))
        hidden_out[adapter] = f_all[:, :RANK]
        f_flip = f_all.T
        h_all = pick(lambda group: h_recv[group].astype(F32))
        heads_out[adapter] = h_all[:, :RANK]
        query_out[adapter] = h_all.T[RANK : 2 * RANK]
        k_flip = pick(lambda group: k_recv[group].astype(F32)).T
        for which in range(2):
            band = slice(which * RANK, (which + 1) * RANK)
            keyval_out[adapter, which] = k_flip[band]
            gateup_out[adapter, which] = f_flip[RANK:][band]
            resid_out[adapter, which] = d_flip[5 * RANK :][band]

    gather.finish()
    for scatter in scatters:
        scatter.finish()


def attn_back_fused(scalars, arrays, grad_shapes, dp, total):
    (g, weight, seq, q) = arrays[:4]
    rows, model = g.shape
    f_send = arrays[-1]
    anywhere = pl.BlockSpec(memory_space=pl.ANY)
    vmem = pl.BlockSpec(memory_space=pltpu.VMEM)
    smem = pl.BlockSpec(memory_space=pltpu.SMEM)
    q_width = q.shape[1]
    specs = [smem, smem] + [vmem] * len(arrays)
    specs[3] = specs[4] = specs[-1] = anywhere
    outs = [jax.ShapeDtypeStruct((rows, model), F32), jax.ShapeDtypeStruct((rows, LANES), F32)]
    outs += [jax.ShapeDtypeStruct(shape, F32) for shape in grad_shapes]
    d_rows, h_rows = model // total, q_width // dp
    k_rows = HD // dp
    return pl.pallas_call(
        functools.partial(attn_back_kernel, rows),
        out_shape=tuple(outs),
        in_specs=specs,
        out_specs=(vmem,) * len(outs),
        scratch_shapes=[
            pltpu.VMEM(weight.shape, BF16),
            pltpu.VMEM(seq.shape, BF16),
            pltpu.VMEM((4, rows, model), BF16),
            pltpu.VMEM((rows, q_width), BF16),
            pltpu.VMEM((4, rows, q_width), BF16),
            pltpu.VMEM((LEN, HD), F32),
            pltpu.VMEM((LEN, HD), F32),
            pltpu.VMEM((LEN, 2 * HD), BF16),
            pltpu.VMEM((4, rows, q_width + 2 * HD), BF16),
            pltpu.VMEM((LANES, model), F32),
            pltpu.VMEM((LANES, q_width), F32),
            pltpu.VMEM((LANES, HD), F32),
            pltpu.VMEM((model, LANES), BF16),
            pltpu.VMEM((q_width, LANES), BF16),
            pltpu.VMEM((HD, LANES), BF16),
            pltpu.VMEM((total, d_rows, LANES), BF16),
            pltpu.VMEM(f_send.shape, BF16),
            pltpu.VMEM((dp, h_rows, LANES), BF16),
            pltpu.VMEM((dp, k_rows, LANES), BF16),
            pltpu.SemaphoreType.DMA((2,)),
            pltpu.SemaphoreType.DMA,
            pltpu.SemaphoreType.DMA((6,)),
            pltpu.SemaphoreType.DMA((6,)),
            pltpu.SemaphoreType.DMA((total,)),
            pltpu.SemaphoreType.DMA((dp,)),
            pltpu.SemaphoreType.DMA((dp,)),
            pltpu.SemaphoreType.DMA((dp,)),
            pltpu.SemaphoreType.DMA((4,)),
        ]
        + scatter_scratch(rows, model)
        + scatter_scratch(rows, LANES),
        compiler_params=pltpu.CompilerParams(
            collective_id=6, has_side_effects=True, vmem_limit_bytes=62 * 1024 * 1024
        ),
        name="attn_back",
    )(*scalars, *arrays)


def per_device(
    layer_in,
    cotangent,
    lengths,
    adapter_ids,
    norm_gains,
    query_weight,
    key_weight,
    value_weight,
    out_weight,
    gate_weight,
    up_weight,
    down_weight,
    adapt_in,
    adapt_heads,
    adapt_hidden,
    lift_query,
    lift_keyval,
    lift_gateup,
    lift_resid,
):
    lay = Layout()
    count = lay.tensor
    rows = layer_in.shape[0]
    group_rows = rows * count
    assert lengths.shape[0] == 1 and group_rows == LEN
    heads_here = lay.heads_here
    head_width = heads_here * HD
    hidden_here = FF // count
    assert lay.ratio % heads_here == 0

    key_cols = lax.dynamic_slice_in_dim(key_weight, lay.kv_head * HD, HD, 1)
    value_cols = lax.dynamic_slice_in_dim(value_weight, lay.kv_head * HD, HD, 1)
    attn_shard = jnp.concatenate([query_weight, key_cols, value_cols, out_weight.T], axis=1)
    attn_w = lax.all_gather(attn_shard, "dp", axis=0, tiled=True)
    gate_up_shard = jnp.concatenate([gate_weight, up_weight], axis=1)
    down_shard = down_weight.T
    attn_shard, gate_up_shard, down_shard = lax.optimization_barrier(
        (attn_shard, gate_up_shard, down_shard)
    )
    gate_up_w = lax.all_gather(gate_up_shard, "dp", axis=0, tiled=True)
    qkv_width = head_width + 2 * HD

    all_ids = lax.all_gather(adapter_ids[:, 0], "dp", axis=0, tiled=True)
    group_hot = (all_ids[:, None] == jnp.arange(NA, dtype=jnp.int32)[None, :]).astype(BF16)

    def rows_of(table):
        moved = jnp.moveaxis(table, -1, 1)
        return moved.reshape(NA, moved.shape[1], -1)

    def choose(*parts):
        packed = pad_lanes(jnp.concatenate(parts, axis=-1))
        return lax.dot_general(
            group_hot, packed, (((1,), (0,)), ((), ())), preferred_element_type=F32
        ).astype(BF16)

    d_send = choose(adapt_in, rows_of(lift_resid))
    f_send = choose(adapt_hidden, rows_of(lift_gateup))
    h_send = choose(adapt_heads, rows_of(lift_query))
    k_send = choose(rows_of(lift_keyval))
    d_rows, f_rows, h_rows, k_rows = (item.shape[1] for item in (d_send, f_send, h_send, k_send))
    d_tab, f_tab, h_tab, k_tab = exchange(
        tables_kernel,
        "adapter_tables",
        3,
        (d_send, f_send, h_send, k_send),
        (
            (lay.total, d_rows, LANES),
            (lay.dp, f_rows, LANES),
            (lay.dp, h_rows, LANES),
            (lay.kv_owners, k_rows, LANES),
        ),
        lay.dp,
        lay.total,
        lay.share,
    )
    d_tab = d_tab.reshape(D, LANES)
    f_tab = f_tab.reshape(hidden_here, LANES)
    h_tab = h_tab.reshape(head_width, LANES)
    k_tab = k_tab.reshape(HD, LANES)
    in_qkv, in_gu = d_tab[:, : 3 * RANK], d_tab[:, 3 * RANK : 5 * RANK]
    lift_out, lift_down = d_tab[:, 5 * RANK : 6 * RANK], d_tab[:, 6 * RANK : 7 * RANK]
    map_hidden, lift_gate, lift_up = (f_tab[:, i * RANK : (i + 1) * RANK] for i in range(3))
    map_heads, lift_q = h_tab[:, :RANK], h_tab[:, RANK : 2 * RANK]
    lift_k, lift_v = k_tab[:, :RANK], k_tab[:, RANK : 2 * RANK]

    row_start = lay.t * rows
    length = lengths[0]
    row_valid = ((row_start + jnp.arange(rows, dtype=jnp.int32)) < length).astype(F32)[:, None]
    cosine, sine = tables(LEN, HD)
    place = jnp.arange(LEN, dtype=jnp.int32)
    allowed = (place[:, None] >= place[None, :]) & (place[None, :] < length)

    resid_in = layer_in.astype(F32)
    normed_attn = rms_norm(resid_in, norm_gains[0]).astype(BF16)
    seq_attn = tensor_gather(normed_attn, count)
    low_qkv = nn(seq_attn, in_qkv).astype(BF16)
    low_q, low_k, low_v = (low_qkv[:, i * RANK : (i + 1) * RANK] for i in range(3))
    qkv = nn(seq_attn, attn_w[:, :qkv_width])
    query_pre = (qkv[:, :head_width] + nt(low_q, lift_q)).reshape(LEN, heads_here, HD)
    key_pre = (qkv[:, head_width : head_width + HD] + nt(low_k, lift_k)).reshape(LEN, 1, HD)
    value_pre = qkv[:, head_width + HD :] + nt(low_v, lift_v)
    queries = (rotate(query_pre, cosine, sine) * HD ** (-0.5)).astype(BF16)
    keys = rotate(key_pre, cosine, sine).astype(BF16).reshape(LEN, HD)
    values = value_pre.astype(BF16)

    def scores_of():
        raw = jnp.einsum("qhd,kd->hqk", queries, keys, preferred_element_type=F32)
        squash = jnp.tanh(raw / SOFT_CAP)
        return squash, jnp.where(allowed[None], jnp.exp(SOFT_CAP * squash), 0.0)

    squash, weights = scores_of()
    inverse_total = 1.0 / jnp.sum(weights, axis=-1, keepdims=True)
    attended = jnp.einsum(
        "hqk,kd->qhd", (weights * inverse_total).astype(BF16), values, preferred_element_type=F32
    )
    attended = attended.astype(BF16).reshape(LEN, head_width)
    w_out = attn_w[:, qkv_width:]
    out_part = nt(attended, w_out).astype(BF16)
    low_out_part = pad_lanes(nn(attended, map_heads).astype(BF16))
    attn_main, low_out = tensor_scatter(out_part, low_out_part, count)
    low_out = low_out[:, :RANK].astype(BF16)
    attn_total = attn_main + nt(low_out, lift_out)
    resid_mid = resid_in + rms_norm(attn_total, norm_gains[1])

    normed_mlp = rms_norm(resid_mid, norm_gains[2]).astype(BF16)
    line_of_four = count == 4 and lay.dp == 8
    if line_of_four:
        seq_mlp = chunk_gather(normed_mlp)
        low_gu = pad_lanes(nn(seq_mlp.reshape(LEN, D), in_gu).astype(BF16)).reshape(4, rows, LANES)
        lift_gu = jnp.concatenate(
            [pad_lanes(lift_gate), jnp.pad(lift_up, ((0, 0), (RANK, LANES - 2 * RANK)))], axis=0
        )
        mlp_main, low_down, hidden, slope, gelu, down_w = mlp_fused(
            seq_mlp, gate_up_w, down_shard, low_gu, lift_gu, pad_lanes(map_hidden), lay.dp
        )
        down_w = down_w.reshape(D, hidden_here)
    else:
        seq_mlp = tensor_gather(normed_mlp, count)
        low_gu = nn(seq_mlp, in_gu).astype(BF16)
        low_g, low_u = low_gu[:, :RANK], low_gu[:, RANK:]
        w_gate, w_up = gate_up_w[:, :hidden_here], gate_up_w[:, hidden_here:]
        gate = nn(seq_mlp, w_gate) + nt(low_g, lift_gate)
        up = nn(seq_mlp, w_up) + nt(low_u, lift_up)
        hidden, slope, gelu = gelu_parts(gate, up)
        down_w = lax.all_gather(down_shard, "dp", axis=0, tiled=True)
        down_part = nt(hidden, down_w).astype(BF16)
        low_down_part = pad_lanes(nn(hidden, map_hidden).astype(BF16))
        mlp_main, low_down = tensor_scatter(down_part, low_down_part, count)
    low_down = low_down[:, :RANK].astype(BF16)
    mlp_total = mlp_main + nt(low_down, lift_down)
    layer_out = (row_valid * (resid_mid + rms_norm(mlp_total, norm_gains[3]))).astype(BF16)

    grad_out = cotangent.astype(F32) * row_valid
    grad_mlp = norm_back(mlp_total, norm_gains[3], grad_out).astype(BF16)
    if line_of_four:
        mlp_back, grad_low_gu, f_grad = mlp_back_fused(
            grad_mlp,
            down_w,
            gate_up_w,
            slope,
            gelu,
            hidden,
            low_gu,
            pad_lanes(lift_down),
            pad_lanes(map_hidden),
            lift_gu,
        )
    else:
        seq_grad_mlp = tensor_gather(grad_mlp, count)
        grad_low_down = nn(seq_grad_mlp, lift_down).astype(BF16)
        grad_hidden = nn(seq_grad_mlp, down_w) + nt(grad_low_down, map_hidden)
        grad_gate = (grad_hidden * slope.astype(F32)).astype(BF16)
        grad_up = (grad_hidden * gelu.astype(F32)).astype(BF16)
        low_gu_part = pad_lanes(
            jnp.concatenate([nn(grad_gate, lift_gate), nn(grad_up, lift_up)], axis=1).astype(BF16)
        )
        mlp_back_part = (nt(grad_gate, w_gate) + nt(grad_up, w_up)).astype(BF16)
        mlp_back, grad_low_gu = tensor_scatter(mlp_back_part, low_gu_part, count)
        f_parts = [tn(hidden, grad_low_down), tn(grad_gate, low_g), tn(grad_up, low_u)]
    grad_low_gu = grad_low_gu[:, : 2 * RANK].astype(BF16)
    grad_normed_mlp = mlp_back + nt(grad_low_gu, in_gu)
    grad_mid = grad_out + norm_back(resid_mid, norm_gains[2], grad_normed_mlp)

    grad_attn = norm_back(attn_total, norm_gains[1], grad_mid).astype(BF16)
    grad_shapes = tuple(
        table.shape
        for table in (
            adapt_in,
            adapt_heads,
            adapt_hidden,
            lift_query,
            lift_keyval,
            lift_gateup,
            lift_resid,
        )
    )
    if line_of_four:
        lift_qkv = jnp.concatenate(
            [
                pad_lanes(lift_q),
                jnp.pad(lift_k, ((0, 0), (RANK, LANES - 2 * RANK))),
                jnp.pad(lift_v, ((0, 0), (2 * RANK, LANES - 3 * RANK))),
            ],
            axis=0,
        )
        attn_back, grad_low_qkv, *adapter_grads = attn_back_fused(
            (all_ids, lengths),
            (
                grad_attn,
                attn_w,
                seq_attn,
                queries.reshape(LEN, head_width),
                keys,
                keys.T,
                values,
                attended,
                inverse_total.reshape(heads_here, LEN),
                cosine.reshape(LEN, HD // 2),
                sine.reshape(LEN, HD // 2),
                pad_lanes(low_qkv),
                pad_lanes(lift_out),
                pad_lanes(map_heads),
                lift_qkv,
                normed_mlp,
                pad_lanes(grad_low_gu),
                pad_lanes(low_out),
                grad_mlp,
                pad_lanes(low_down),
                f_grad.reshape(lay.dp, -1, LANES),
            ),
            grad_shapes,
            lay.dp,
            lay.total,
        )
    else:
        seq_grad_attn = tensor_gather(grad_attn, count)
        grad_low_out = nn(seq_grad_attn, lift_out).astype(BF16)
        grad_attended = (nn(seq_grad_attn, w_out) + nt(grad_low_out, map_heads)).astype(BF16)
        grad_heads = grad_attended.reshape(LEN, heads_here, HD)
        probs = weights * inverse_total
        probs_low = probs.astype(BF16)
        grad_probs = jnp.einsum("qhd,kd->hqk", grad_heads, values, preferred_element_type=F32)
        grad_value = jnp.einsum("hqk,qhd->kd", probs_low, grad_heads, preferred_element_type=F32)
        grad_capped = probs * (grad_probs - jnp.sum(probs * grad_probs, axis=-1, keepdims=True))
        grad_raw = (grad_capped * (1.0 - squash * squash)).astype(BF16)
        grad_query = jnp.einsum("hqk,kd->qhd", grad_raw, keys, preferred_element_type=F32)
        grad_key = jnp.einsum("hqk,qhd->kd", grad_raw, queries, preferred_element_type=F32)
        grad_q_pre = rotate(grad_query * HD ** (-0.5), cosine, -sine).astype(BF16)
        grad_q_pre = grad_q_pre.reshape(LEN, head_width)
        grad_k_pre = rotate(grad_key.reshape(LEN, 1, HD), cosine, -sine).astype(BF16)
        grad_k_pre = grad_k_pre.reshape(LEN, HD)
        grad_v_pre = grad_value.astype(BF16)
        low_qkv_part = pad_lanes(
            jnp.concatenate(
                [nn(grad_q_pre, lift_q), nn(grad_k_pre, lift_k), nn(grad_v_pre, lift_v)], axis=1
            ).astype(BF16)
        )
        grad_qkv = jnp.concatenate([grad_q_pre, grad_k_pre, grad_v_pre], axis=1)
        attn_back_part = nt(grad_qkv, attn_w[:, :qkv_width]).astype(BF16)
        attn_back, grad_low_qkv = tensor_scatter(attn_back_part, low_qkv_part, count)
    grad_low_qkv = grad_low_qkv[:, : 3 * RANK].astype(BF16)
    grad_normed_attn = attn_back + nt(grad_low_qkv, in_qkv)
    input_grad = (grad_mid + norm_back(resid_in, norm_gains[0], grad_normed_attn)).astype(BF16)

    if line_of_four:
        return (layer_out, input_grad, *adapter_grads)

    def packed(parts, blocks):
        return pad_lanes(jnp.concatenate(parts, axis=1).astype(BF16)).reshape(
            blocks, -1, LANES
        )

    d_grad = packed(
        [
            tn(normed_attn, grad_low_qkv),
            tn(normed_mlp, grad_low_gu),
            tn(grad_attn, low_out),
            tn(grad_mlp, low_down),
        ],
        lay.total,
    )
    f_grad = packed(f_parts, lay.dp)
    h_grad = packed([tn(attended, grad_low_out), tn(grad_q_pre, low_q)], lay.dp)
    k_grad = packed([tn(grad_k_pre, low_k), tn(grad_v_pre, low_v)], lay.kv_owners)
    d_all, f_all, h_all, k_all = exchange(
        grads_kernel,
        "adapter_grads",
        4,
        (d_grad, f_grad, h_grad, k_grad),
        (
            (lay.total, d_rows, LANES),
            (lay.dp, f_rows, LANES),
            (lay.dp, h_rows, LANES),
            (lay.dp * lay.share, k_rows, LANES),
        ),
        lay.dp,
        lay.total,
        lay.share,
    )

    def collect(received):
        repeats = received.shape[0] // lay.dp
        hot = jnp.repeat(group_hot, repeats, axis=0)
        return lax.dot_general(
            hot, received, (((0,), (0,)), ((), ())), preferred_element_type=F32
        )

    d_all, f_all, h_all, k_all = (collect(item) for item in (d_all, f_all, h_all, k_all))

    def lift_form(values, shape):
        return jnp.moveaxis(values, 1, 2).reshape(shape)

    return (
        layer_out,
        input_grad,
        d_all[:, :, : 5 * RANK],
        h_all[:, :, :RANK],
        f_all[:, :, :RANK],
        lift_form(h_all[:, :, RANK : 2 * RANK], lift_query.shape),
        lift_form(k_all[:, :, : 2 * RANK], lift_keyval.shape),
        lift_form(f_all[:, :, RANK : 3 * RANK], lift_gateup.shape),
        lift_form(d_all[:, :, 5 * RANK : 7 * RANK], lift_resid.shape),
    )


def solution(mesh):
    return jax.shard_map(
        per_device,
        mesh=mesh,
        in_specs=(
            P(("dp", "tensor"), None),
            P(("dp", "tensor"), None),
            P("dp"),
            P("dp", None),
            P(),
            P("dp", "tensor"),
            P("dp", None),
            P("dp", None),
            P("tensor", "dp"),
            P("dp", "tensor"),
            P("dp", "tensor"),
            P("tensor", "dp"),
            P(None, ("dp", "tensor"), None),
            P(None, ("dp", "tensor"), None),
            P(None, ("dp", "tensor"), None),
            P(None, None, ("dp", "tensor")),
            P(None, None, None, ("dp", "tensor")),
            P(None, None, None, ("dp", "tensor")),
            P(None, None, None, ("dp", "tensor")),
        ),
        out_specs=(
            P(("dp", "tensor"), None),
            P(("dp", "tensor"), None),
            P(None, ("dp", "tensor"), None),
            P(None, ("dp", "tensor"), None),
            P(None, ("dp", "tensor"), None),
            P(None, None, ("dp", "tensor")),
            P(None, None, None, ("dp", "tensor")),
            P(None, None, None, ("dp", "tensor")),
            P(None, None, None, ("dp", "tensor")),
        ),
        check_vma=False,
    )
```

```python
import functools

import jax
import jax.numpy as jnp
from jax import lax
from jax.experimental import pallas as pl
from jax.experimental.pallas import tpu as pltpu
from jax.sharding import PartitionSpec as P

D = 2304
HQ = 8
KV = 4
HD = 256
FF = 9216
NA = 8
RANK = 16
LEN = 1024
LANES = 128

EPSILON = 1e-06
SOFT_CAP = 50.0
MESH = pl.DeviceIdType.MESH
BF16 = jnp.bfloat16
F32 = jnp.float32
VMEM_LIMIT = 48 * 1024 * 1024
BLOCK = 32


def rms_norm(values, gain_row):
    return (
        values * lax.rsqrt(jnp.mean(values * values, axis=-1, keepdims=True) + EPSILON) * gain_row
    )


def norm_back(values, gain_row, gradient):
    inverse = lax.rsqrt(jnp.mean(values * values, axis=-1, keepdims=True) + EPSILON)
    scaled = gradient * gain_row
    normed = values * inverse
    return inverse * (scaled - normed * jnp.mean(scaled * normed, axis=-1, keepdims=True))


def gelu_parts(gate, up):
    scale = (2.0 / jnp.pi) ** 0.5
    square = gate * gate
    bend = jnp.tanh(scale * gate * (1.0 + 0.044715 * square))
    low = 0.5 * (1.0 + bend)
    gelu = gate * low
    slope = low + 0.5 * gate * (1.0 - bend * bend) * (scale * (1.0 + 3.0 * 0.044715 * square))
    return (gelu * up).astype(BF16), (slope * up).astype(BF16), gelu.astype(BF16)


def tables(length, size):
    half_size = size // 2
    frequency = 10000.0 ** (-2.0 * jnp.arange(half_size, dtype=F32) / size)
    angles = jnp.arange(length, dtype=F32)[:, None] * frequency[None, :]
    return (jnp.cos(angles)[:, None, :], jnp.sin(angles)[:, None, :])


def rotate(values, cosine, sine):
    half_size = values.shape[-1] // 2
    first_half = values[..., :half_size]
    second_half = values[..., half_size:]
    return jnp.concatenate(
        [first_half * cosine - second_half * sine, second_half * cosine + first_half * sine],
        axis=-1,
    )


def nn(a, b):
    return lax.dot_general(a, b, (((1,), (0,)), ((), ())), preferred_element_type=F32)


def nt(a, b):
    return lax.dot_general(a, b, (((1,), (1,)), ((), ())), preferred_element_type=F32)


def tn(a, b):
    return lax.dot_general(a, b, (((0,), (0,)), ((), ())), preferred_element_type=F32)


def pad_lanes(values):
    return jnp.pad(values, [(0, 0)] * (values.ndim - 1) + [(0, LANES - values.shape[-1])])


QUERY, KEY, VALUE, GATE, UP, OUT, DOWN = (
    slice(i * RANK, (i + 1) * RANK) for i in range(7)
)


def band(values, first, last=None):
    lane = lax.broadcasted_iota(jnp.int32, values.shape, 1)
    keep = (lane >= first.start) & (lane < (last or first).stop)
    return jnp.where(keep, values, 0.0)


def lanes(*parts):
    pieces, at = [], 0
    for place, values in parts:
        if place.start > at:
            pieces.append(jnp.zeros(values.shape[:-1] + (place.start - at,), values.dtype))
        pieces.append(values)
        at = place.start + values.shape[-1]
    last = parts[-1][1]
    pieces.append(jnp.zeros(last.shape[:-1] + (LANES - at,), last.dtype))
    return jnp.concatenate(pieces, axis=-1)


def call(peers):
    barrier = pltpu.get_barrier_semaphore()
    for peer in peers:
        pl.semaphore_signal(barrier, inc=1, device_id=peer, device_id_type=MESH)


def greet(peers):
    call(peers)
    pl.semaphore_wait(pltpu.get_barrier_semaphore(), len(peers))


def square_peers(index):
    return index + 1 - 2 * lax.rem(index, 2), lax.rem(index + 2, 4), 3 - index


def remote(source, target, send_sem, recv_sem, peer):
    return pltpu.make_async_remote_copy(
        src_ref=source,
        dst_ref=target,
        send_sem=send_sem,
        recv_sem=recv_sem,
        device_id={"tensor": peer},
        device_id_type=MESH,
    )


def gather_kernel(count, rows, x_ref, o_ref, local_sem, send_sem, recv_sem):
    me = lax.axis_index("tensor")
    if count == 4:
        across, down, _ = square_peers(me)
        greet([{"tensor": across}, {"tensor": down}])
        own = pltpu.make_async_copy(x_ref, o_ref.at[pl.ds(me * rows, rows)], local_sem)
        own.start()
        half = rows // 2
        links = (across, down)
        first = [[None, None], [None, None]]
        for order in range(2):
            for link in range(2):
                part = order if link == 0 else 1 - order
                target = o_ref.at[pl.ds(me * rows + part * half, half)]
                copy = remote(
                    x_ref.at[pl.ds(part * half, half)],
                    target,
                    send_sem.at[link, part],
                    recv_sem.at[link, part],
                    links[link],
                )
                copy.start()
                first[link][part] = copy
        second = []
        for link in range(2):
            first[link][link].wait_recv()
            block = o_ref.at[pl.ds(links[link] * rows + link * half, half)]
            copy = remote(
                block, block, send_sem.at[2, link], recv_sem.at[2, link], links[1 - link]
            )
            copy.start()
            second.append(copy)
        for link in range(2):
            first[link][1 - link].wait_recv()
        for copy in second:
            copy.wait_recv()
        own.wait()
        for link in range(2):
            for part in range(2):
                first[link][part].wait_send()
        for copy in second:
            copy.wait_send()
    else:
        peers = [lax.rem(me + step, count) for step in range(1, count)]
        greet([{"tensor": peer} for peer in peers])
        own = pltpu.make_async_copy(x_ref, o_ref.at[pl.ds(me * rows, rows)], local_sem)
        own.start()
        copies = []
        for step, peer in enumerate(peers):
            copy = remote(
                x_ref,
                o_ref.at[pl.ds(me * rows, rows)],
                send_sem.at[0, step],
                recv_sem.at[0, step],
                peer,
            )
            copy.start()
            copies.append(copy)
        own.wait()
        for copy in copies:
            copy.wait()


def tensor_gather(values, count):
    rows, width = values.shape
    slots = max(2, count - 1)
    return pl.pallas_call(
        functools.partial(gather_kernel, count, rows),
        out_shape=jax.ShapeDtypeStruct((count * rows, width), values.dtype),
        in_specs=[pl.BlockSpec(memory_space=pl.ANY)],
        out_specs=pl.BlockSpec(memory_space=pl.ANY),
        scratch_shapes=[
            pltpu.SemaphoreType.DMA,
            pltpu.SemaphoreType.DMA((3, slots)),
            pltpu.SemaphoreType.DMA((3, slots)),
        ],
        compiler_params=pltpu.CompilerParams(
            collective_id=1, has_side_effects=True, vmem_limit_bytes=VMEM_LIMIT
        ),
        name="tensor_gather",
    )(values)


def scatter_kernel(count, rows, p_ref, q_ref, o_ref, l_ref, *scratch):
    me = lax.axis_index("tensor")
    payload = ((p_ref, o_ref), (q_ref, l_ref))
    if count == 4:
        across, down, far = square_peers(me)
        greet([{"tensor": across}, {"tensor": down}])
        half = rows // 2
        first = scratch[0:2]
        sums = scratch[2:4]
        second = scratch[4:6]
        send_sem, recv_sem = scratch[6], scratch[7]
        links = (across, down)
        copies = {}
        for which in (1, 0):
            for link in range(2):
                block = far if which == 1 else links[link]
                for item in range(2):
                    copy = remote(
                        payload[item][0].at[pl.ds(block * rows + link * half, half)],
                        first[item].at[link, which],
                        send_sem.at[item, link, which],
                        recv_sem.at[item, link, which],
                        links[link],
                    )
                    copy.start()
                    copies[item, link, which] = copy
        for link in range(2):
            block = links[1 - link]
            for item in range(2):
                copies[item, link, 1].wait_recv()
                mine = payload[item][0][pl.ds(block * rows + link * half, half), :]
                sums[item][link] = (
                    mine.astype(F32) + first[item][link, 1].astype(F32)
                ).astype(BF16)
                copy = remote(
                    sums[item].at[link],
                    second[item].at[link],
                    send_sem.at[item, link, 2],
                    recv_sem.at[item, link, 2],
                    links[1 - link],
                )
                copy.start()
                copies[item, link, 2] = copy
        for link in range(2):
            for item in range(2):
                copies[item, link, 0].wait_recv()
                mine = payload[item][0][pl.ds(me * rows + link * half, half), :]
                payload[item][1][pl.ds(link * half, half), :] = mine.astype(F32) + first[item][
                    link, 0
                ].astype(F32)
        for link in range(2):
            for item in range(2):
                copies[item, link, 2].wait_recv()
                payload[item][1][pl.ds(link * half, half), :] += second[item][link].astype(F32)
        for copy in copies.values():
            copy.wait_send()
    else:
        peers = [lax.rem(me + step, count) for step in range(1, count)]
        greet([{"tensor": peer} for peer in peers])
        first = scratch[0:2]
        send_sem, recv_sem = scratch[2], scratch[3]
        copies = []
        for step, peer in enumerate(peers):
            for item in range(2):
                copy = remote(
                    payload[item][0].at[pl.ds(peer * rows, rows)],
                    first[item].at[step],
                    send_sem.at[item, step],
                    recv_sem.at[item, step],
                    peer,
                )
                copy.start()
                copies.append((item, step, copy))
        for item in range(2):
            payload[item][1][...] = payload[item][0][pl.ds(me * rows, rows), :].astype(F32)
        for item, step, copy in copies:
            copy.wait()
            payload[item][1][...] += first[item][step].astype(F32)


def tensor_scatter(values, narrow, count):
    rows = values.shape[0] // count
    widths = (values.shape[1], narrow.shape[1])
    if count == 4:
        half = rows // 2
        scratch = [pltpu.VMEM((2, 2, half, width), BF16) for width in widths]
        scratch += [pltpu.VMEM((2, half, width), BF16) for width in widths]
        scratch += [pltpu.VMEM((2, half, width), BF16) for width in widths]
        scratch += [pltpu.SemaphoreType.DMA((2, 2, 3)), pltpu.SemaphoreType.DMA((2, 2, 3))]
    else:
        scratch = [pltpu.VMEM((count - 1, rows, width), BF16) for width in widths]
        scratch += [pltpu.SemaphoreType.DMA((2, count - 1))] * 2
    vmem = pl.BlockSpec(memory_space=pltpu.VMEM)
    return pl.pallas_call(
        functools.partial(scatter_kernel, count, rows),
        out_shape=tuple(jax.ShapeDtypeStruct((rows, width), F32) for width in widths),
        in_specs=[vmem, vmem],
        out_specs=(vmem, vmem),
        scratch_shapes=scratch,
        compiler_params=pltpu.CompilerParams(
            collective_id=2, has_side_effects=True, vmem_limit_bytes=VMEM_LIMIT
        ),
        name="tensor_scatter",
    )(values, narrow)


class Square:
    def __init__(self, rows):
        self.rows = rows
        self.half = rows // 2
        self.me = lax.axis_index("tensor")
        self.across, self.down, self.far = square_peers(self.me)
        self.links = (self.across, self.down)

    def greet(self, far=False):
        greet([{"tensor": peer} for peer in (self.across, self.down) + ((self.far,) if far else ())])

    def spread(self, source_at, target, send_sem, recv_sem):
        copies = [pltpu.make_async_copy(source_at(self.me), target.at[self.me], recv_sem.at[0])]
        for which, peer in enumerate((self.across, self.down, self.far)):
            copies.append(
                remote(
                    source_at(peer),
                    target.at[self.me],
                    send_sem.at[which],
                    recv_sem.at[1 + which],
                    peer,
                )
            )
        return copies


class ChunkGather:
    def __init__(self, sq, source, buf, send_sem, recv_sem):
        half = sq.half
        self.first, self.second, self.onward = [], [], []
        for link in range(2):
            for order in range(2):
                part = link if order == 0 else 1 - link
                copy = remote(
                    source.at[pl.ds(part * half, half)],
                    buf.at[1 + order, pl.ds(link * half, half)],
                    send_sem.at[2 * order + link],
                    recv_sem.at[2 * order + link],
                    sq.links[link],
                )
                (self.first if order == 0 else self.second).append(copy)
            self.onward.append(
                remote(
                    buf.at[1, pl.ds(link * half, half)],
                    buf.at[3, pl.ds(link * half, half)],
                    send_sem.at[4 + link],
                    recv_sem.at[4 + link],
                    sq.links[1 - link],
                )
            )

    def start(self):
        for copy in self.first + self.second:
            copy.start()

    def wait_chunk(self, chunk):
        if chunk == 1:
            for copy in self.first:
                copy.wait_recv()
            for copy in self.onward:
                copy.start()
        if chunk == 2:
            for copy in self.second:
                copy.wait_recv()
        if chunk == 3:
            for copy in self.onward:
                copy.wait_recv()

    def finish(self):
        for copy in self.first + self.second + self.onward:
            copy.wait_send()


class ChunkScatter:
    def __init__(self, sq, part, landing, passed, send_sem, recv_sem):
        self.sq, self.half = sq, sq.half
        self.part, self.landing, self.passed = part, landing, passed
        self.send_sem, self.recv_sem = send_sem, recv_sem

    def copy(self, kind, link):
        rows = pl.ds(link * self.half, self.half)
        source = (
            self.passed.at[link] if kind == 2 else self.part.at[1 + 2 * kind, rows]
        )
        slot = 2 * kind + link
        return remote(
            source,
            self.landing.at[slot],
            self.send_sem.at[slot],
            self.recv_sem.at[slot],
            self.sq.links[1 - link if kind == 2 else link],
        )

    def send_own(self):
        for link in range(2):
            self.copy(0, link).start()

    def send_far(self):
        for link in range(2):
            self.copy(1, link).start()

    def pass_on(self, link):
        self.copy(1, link).wait_recv()
        rows = pl.ds((1 - link) * self.half, self.half)
        mine = self.part[2, rows, :].astype(F32)
        self.passed[link] = (mine + self.landing[2 + link].astype(F32)).astype(BF16)
        self.copy(2, link).start()

    def collect(self, out_ref, first=0):
        for link in range(2):
            self.copy(0, link).wait_recv()
            self.copy(2, link).wait_recv()
            rows = pl.ds(link * self.half, self.half)
            out_ref[rows, first : first + self.part.shape[-1]] = (
                self.part[0, rows, :].astype(F32)
                + self.landing[link].astype(F32)
                + self.landing[4 + link].astype(F32)
            )

    def finish(self):
        for kind in range(3):
            for link in range(2):
                self.copy(kind, link).wait_send()


def scatter_scratch(rows, width):
    half = rows // 2
    return [
        pltpu.VMEM((4, rows, width), BF16),
        pltpu.VMEM((6, half, width), BF16),
        pltpu.VMEM((2, half, width), BF16),
        pltpu.SemaphoreType.DMA((6,)),
        pltpu.SemaphoreType.DMA((6,)),
    ]


def tile_of(width):
    return 768 if width % 768 == 0 else 384


def columns(step, tile, base=0):
    return pl.ds(pl.multiple_of(base + step * tile, LANES), tile)


def mlp_back_kernel(
    rows,
    g_ref,
    down_hbm,
    gu_hbm,
    slope_hbm,
    gelu_hbm,
    hidden_hbm,
    low_hbm,
    d_ref,
    f_table,
    o_ref,
    l_ref,
    f_out,
    f_ref,
    f_send,
    down_w,
    gu_w,
    buf,
    slope,
    gelu,
    hidden,
    low,
    grads,
    weight_sem,
    load_sem,
    own_sem,
    gather_send,
    gather_recv,
    spread_send,
    spread_recv,
    *scratch,
):
    sq = Square(rows)
    width = hidden.shape[-1]
    model = o_ref.shape[-1]
    down_load = pltpu.make_async_copy(down_hbm, down_w, weight_sem.at[0])
    gu_load = pltpu.make_async_copy(gu_hbm, gu_w, weight_sem.at[1])
    own_load = pltpu.make_async_copy(g_ref, buf.at[0], own_sem)

    def loads(chunk):
        slot = chunk % 2
        return [
            pltpu.make_async_copy(source.at[chunk], target.at[slot], load_sem.at[slot, item])
            for item, (source, target) in enumerate(
                ((slope_hbm, slope), (gelu_hbm, gelu), (hidden_hbm, hidden), (low_hbm, low))
            )
        ]

    down_load.start()
    own_load.start()
    for copy in loads(0):
        copy.start()
    sq.greet(far=True)
    gather = ChunkGather(sq, g_ref, buf, gather_send, gather_recv)
    gather.start()
    gu_load.start()
    part, part_low = scratch[0], scratch[5]
    scatters = (ChunkScatter(sq, *scratch[:5]), ChunkScatter(sq, *scratch[5:10]))
    f_ref[...] = jnp.zeros_like(f_ref)
    own_load.wait()
    down_load.wait()

    @pl.loop(0, 4)
    def _(chunk):
        slot = lax.rem(chunk, 2)
        for step in range(4):

            @pl.when(chunk == step)
            def _(step=step):
                gather.wait_chunk(step)
                for copy in loads(step):
                    copy.wait()
                if step < 3:
                    for copy in loads(step + 1):
                        copy.start()

        incoming = buf.at[chunk]
        low_down = band(nn(incoming[...], d_ref[...]), DOWN).astype(BF16)
        tile = tile_of(width)

        @pl.loop(0, width // tile)
        def _(step):
            here = columns(step, tile)
            grad = nn(incoming[...], down_w[:, here]) + nt(low_down, f_table[here, :])
            grads[:, here] = (grad * slope[slot, :, here].astype(F32)).astype(BF16)
            grads[:, columns(step, tile, width)] = (
                grad * gelu[slot, :, here].astype(F32)
            ).astype(BF16)

        @pl.when(chunk == 0)
        def _():
            gu_load.wait()

        part_low[chunk] = (
            band(nn(grads[:, :width], f_table[...]), GATE)
            + band(nn(grads[:, width:], f_table[...]), UP)
        ).astype(BF16)
        wide = tile_of(model)

        @pl.loop(0, model // wide)
        def _(step):
            here = columns(step, wide)
            part[chunk, :, here] = nt(grads[...], gu_w[here, :]).astype(BF16)

        @pl.when(chunk == 1)
        def _():
            for scatter in scatters:
                scatter.send_own()

        @pl.when(chunk == 3)
        def _():
            for scatter in scatters:
                scatter.send_far()

        low_turned = low_down.astype(F32).T.astype(BF16)
        gu_turned = low[slot].astype(F32).T.astype(BF16)
        f_ref[:RANK, :] += nn(low_turned[DOWN], hidden[slot])
        f_ref[RANK : 2 * RANK, :] += nn(gu_turned[GATE], grads[:, :width])
        f_ref[2 * RANK : 3 * RANK, :] += nn(gu_turned[UP], grads[:, width:])

    cores, slices = f_send.shape[:2]
    size = width // (cores * slices)
    for core in range(cores):
        for peer in range(slices):
            first = (core * slices + peer) * size
            f_send[core, peer] = f_ref[: 3 * RANK, first : first + size].astype(BF16)
    spread = sq.spread(lambda peer: f_send.at[:, peer], f_out, spread_send, spread_recv)
    for copy in spread:
        copy.start()
    for link in range(2):
        for scatter in scatters:
            scatter.pass_on(link)
    gather.finish()
    scatters[0].collect(o_ref)
    scatters[1].collect(l_ref)
    for scatter in scatters:
        scatter.finish()
    for copy in spread:
        copy.wait()


def mlp_back_fused(grad, down_w, gu_w, slope, gelu, hidden, low, d_tab, f_tab, dp):
    rows, model = grad.shape
    width = hidden.shape[2]
    messages = (dp // 4, 4, 3 * RANK, width // dp)
    anywhere = pl.BlockSpec(memory_space=pl.ANY)
    vmem = pl.BlockSpec(memory_space=pltpu.VMEM)
    return pl.pallas_call(
        functools.partial(mlp_back_kernel, rows),
        out_shape=(
            jax.ShapeDtypeStruct((rows, model), F32),
            jax.ShapeDtypeStruct((rows, LANES), F32),
            jax.ShapeDtypeStruct((4, dp // 4, 3 * RANK, width // dp), BF16),
        ),
        in_specs=[vmem] + [anywhere] * 6 + [vmem] * 2,
        out_specs=(vmem,) * 3,
        scratch_shapes=[
            pltpu.VMEM((3 * RANK, width), F32),
            pltpu.VMEM(messages, BF16),
            pltpu.VMEM((model, width), BF16),
            pltpu.VMEM((model, 2 * width), BF16),
            pltpu.VMEM((4, rows, model), BF16),
            pltpu.VMEM((2, rows, width), BF16),
            pltpu.VMEM((2, rows, width), BF16),
            pltpu.VMEM((2, rows, width), BF16),
            pltpu.VMEM((2, rows, LANES), BF16),
            pltpu.VMEM((rows, 2 * width), BF16),
            pltpu.SemaphoreType.DMA((2,)),
            pltpu.SemaphoreType.DMA((2, 4)),
            pltpu.SemaphoreType.DMA,
            pltpu.SemaphoreType.DMA((6,)),
            pltpu.SemaphoreType.DMA((6,)),
            pltpu.SemaphoreType.DMA((3,)),
            pltpu.SemaphoreType.DMA((4,)),
        ]
        + scatter_scratch(rows, model)
        + scatter_scratch(rows, LANES),
        compiler_params=pltpu.CompilerParams(
            collective_id=5, has_side_effects=True, vmem_limit_bytes=62 * 1024 * 1024
        ),
        name="mlp_back",
    )(grad, down_w, gu_w, slope, gelu, hidden, low, d_tab, f_tab)


class Line:
    def __init__(self, slots, send_sem, recv_sem):
        self.d = lax.axis_index("dp")
        self.places = lax.axis_size("dp") // 2
        self.core = lax.rem(self.d, 2)
        self.z = self.d // 2
        self.sibling = self.d + 1 - 2 * self.core
        self.slots, self.send_sem, self.recv_sem = slots, send_sem, recv_sem

    def greet(self, others):
        barrier = pltpu.get_barrier_semaphore()
        for peer in others + [{"dp": self.sibling}]:
            pl.semaphore_signal(barrier, inc=1, device_id=peer, device_id_type=MESH)

        @pl.when(self.z > 0)
        def _():
            pl.semaphore_signal(
                barrier, inc=1, device_id={"dp": self.d - 2}, device_id_type=MESH
            )

        @pl.when(self.z < self.places - 1)
        def _():
            pl.semaphore_signal(
                barrier, inc=1, device_id={"dp": self.d + 2}, device_id_type=MESH
            )

        last = self.places - 1
        ends = (last - self.z) // last + self.z // last
        pl.semaphore_wait(barrier, len(others) + 3 - ends)

    def copy(self, place, kind):
        target = (self.d + 2, self.d - 2, self.sibling)[kind]
        slot = 2 * place + self.core
        return pltpu.make_async_remote_copy(
            src_ref=self.slots.at[slot],
            dst_ref=self.slots.at[slot],
            send_sem=self.send_sem.at[kind, place],
            recv_sem=self.recv_sem.at[slot],
            device_id={"dp": target},
            device_id_type=MESH,
        )

    def send_up(self, place):
        @pl.when(self.z < self.places - 1)
        def _():
            self.copy(place, 0).start()

    def send_down(self, place):
        @pl.when(self.z > 0)
        def _():
            self.copy(place, 1).start()

    def start(self):
        self.send_up(self.z)
        self.send_down(self.z)
        self.copy(self.z, 2).start()

    def arrive(self, distance):
        @pl.when(self.z >= distance)
        def _():
            place = self.z - distance
            self.copy(place, 2).wait_recv()
            self.send_up(place)
            self.copy(place, 2).start()

        @pl.when(self.z + distance < self.places)
        def _():
            place = self.z + distance
            self.copy(place, 2).wait_recv()
            self.send_down(place)
            self.copy(place, 2).start()

    def wait_sibling(self, place):
        slot = self.slots.at[2 * place + 1 - self.core]
        pltpu.make_async_copy(
            slot, slot, self.recv_sem.at[2 * place + 1 - self.core]
        ).wait()

    def finish(self):
        for place in range(self.places):

            @pl.when((self.z >= place) & (self.z < self.places - 1))
            def _(place=place):
                self.copy(place, 0).wait_send()

            @pl.when((self.z <= place) & (self.z > 0))
            def _(place=place):
                self.copy(place, 1).wait_send()

            self.copy(place, 2).wait_send()


ARRIVALS = ((0, 1, 2, 3), (1, 0, 2, 3), (2, 1, 3, 0), (3, 2, 1, 0))


def mlp_kernel(
    rows,
    length_ref,
    x_hbm,
    gu_hbm,
    shard_hbm,
    d_ref,
    f_table,
    resid_ref,
    cot_ref,
    gains_ref,
    layer_ref,
    grad_ref,
    low_ref,
    low_down_ref,
    hidden_out,
    slope_out,
    gelu_out,
    down_out,
    work,
    low_sum,
    lows,
    seq,
    tiles,
    hidden,
    slope,
    gelu,
    down,
    load_sem,
    tile_sem,
    store_sem,
    keep_sem,
    line_send,
    line_recv,
    part,
    landing,
    passed,
    part_send,
    part_recv,
    *low_scratch,
):
    sq = Square(rows)
    line = Line(down, line_send, line_recv)
    width = hidden.shape[-1]
    tile = tiles.shape[-1] // 2
    steps = width // tile
    own_shard = pltpu.make_async_copy(shard_hbm, down.at[line.d], load_sem.at[0])
    seq_load = pltpu.make_async_copy(x_hbm, seq, load_sem.at[1])

    def tile_loads(step, slot):
        return [
            pltpu.make_async_copy(
                gu_hbm.at[:, columns(step, tile, which * width)],
                tiles.at[slot, :, pl.ds(which * tile, tile)],
                tile_sem.at[slot, which],
            )
            for which in range(2)
        ]

    def stores(step, slot):
        here = columns(step, tile)
        return [
            pltpu.make_async_copy(
                source.at[slot], target.at[:, :, here], store_sem.at[slot, which]
            )
            for which, (source, target) in enumerate(((slope, slope_out), (gelu, gelu_out)))
        ]

    own_shard.start()
    seq_load.start()
    for copy in tile_loads(0, 0):
        copy.start()
    line.greet([{"tensor": sq.across}, {"tensor": sq.down}])
    own_shard.wait()
    line.start()
    seq_load.wait()

    @pl.loop(0, 4)
    def _(chunk):
        low = nn(seq[chunk], d_ref[...])
        lows[0, chunk] = band(low, GATE).astype(BF16)
        lows[1, chunk] = band(low, UP).astype(BF16)
        low_ref[chunk] = band(low, GATE, UP).astype(BF16)

    @pl.loop(0, steps)
    def _(step):
        slot = lax.rem(step, 2)
        for copy in tile_loads(step, slot):
            copy.wait()

        @pl.when(step + 1 < steps)
        def _():
            for copy in tile_loads(step + 1, 1 - slot):
                copy.start()

        @pl.when(step >= 2)
        def _():
            for copy in stores(step - 2, slot):
                copy.wait()

        here = columns(step, tile)

        @pl.loop(0, 4)
        def _(chunk):
            both = nn(seq[chunk], tiles[slot])
            gate = both[:, :tile] + nt(lows[0, chunk], f_table[here, :])
            up = both[:, tile:] + nt(lows[1, chunk], f_table[here, :])
            hidden[chunk, :, here], slope[slot, chunk], gelu[slot, chunk] = gelu_parts(gate, up)

        for copy in stores(step, slot):
            copy.start()

        @pl.when(step == steps - 2)
        def _():
            line.arrive(1)

    keep_hidden = pltpu.make_async_copy(hidden, hidden_out, keep_sem.at[0])
    keep_hidden.start()
    last = line.places - 1
    is_first, is_last = (last - line.z) // last, line.z // last
    is_third = line.z // 2 - is_last
    is_here = (is_first, 1 - is_first - is_third - is_last, is_third, is_last)
    order = [sum(flag * ARRIVALS[z][i] for z, flag in enumerate(is_here)) for i in range(4)]

    def scatter_at(place):
        return ChunkScatter(
            sq,
            part.at[place],
            landing.at[place],
            passed.at[place],
            part_send.at[place],
            part_recv.at[place],
        )

    low_scatter = ChunkScatter(sq, *low_scratch)

    @pl.loop(0, 4)
    def _(chunk):
        low_scratch[0][chunk] = band(nn(hidden[chunk], f_table[...]), DOWN).astype(BF16)

    low_scatter.send_far()
    low_scatter.send_own()
    keeps = []
    for step in range(4):
        if step >= 2:
            line.arrive(step)
        place = order[step]
        line.wait_sibling(place)
        pair = pl.ds(2 * place, 2)
        keep = pltpu.make_async_copy(down.at[pair], down_out.at[pair], keep_sem.at[1 + step])
        keep.start()
        keeps.append(keep)
        scatter = scatter_at(place)
        shard_rows = down.shape[1]

        @pl.loop(0, 4)
        def _(turn, place=place, scatter=scatter):
            chunk = turn + 3 * ((3 - turn) // 3) - 3 * (turn // 3)
            for core in range(2):
                part[place, chunk, :, core * shard_rows : (core + 1) * shard_rows] = nt(
                    hidden[chunk], down[2 * place + core]
                ).astype(BF16)

            @pl.when(turn == 0)
            def _():
                scatter.send_far()

            @pl.when(turn == 1)
            def _():
                scatter.send_own()

        if step > 0:
            for link in range(2):
                scatter_at(order[step - 1]).pass_on(link)
        else:
            for link in range(2):
                low_scatter.pass_on(link)
    for link in range(2):
        scatter_at(order[3]).pass_on(link)
    wide = part.shape[-1]
    low_scatter.collect(low_sum)
    low_down_ref[...] = low_sum[...].astype(BF16)
    for place in range(4):
        scatter_at(place).collect(work, place * wide)
    add_lifted(work, low_down_ref, d_ref)

    @pl.loop(0, rows // BLOCK)
    def _(step):
        here = pl.ds(pl.multiple_of(step * BLOCK, BLOCK), BLOCK)
        at = sq.me * rows + step * BLOCK + lax.broadcasted_iota(jnp.int32, (BLOCK, 1), 0)
        valid = (at < length_ref[0]).astype(F32)
        total = work[here, :]
        gain = gains_ref[3:4, :]
        layer_ref[here, :] = (valid * (resid_ref[here, :] + rms_norm(total, gain))).astype(BF16)
        grad_ref[here, :] = norm_back(total, gain, cot_ref[here, :].astype(F32) * valid).astype(
            BF16
        )

    for place in range(4):
        scatter_at(place).finish()
    low_scatter.finish()
    line.finish()
    for step in (steps - 2, steps - 1):
        for copy in stores(step, step % 2):
            copy.wait()
    keep_hidden.wait()
    for keep in keeps:
        keep.wait()


def add_lifted(work, low, table):
    wide = tile_of(work.shape[1])

    @pl.loop(0, work.shape[1] // wide)
    def _(step):
        here = columns(step, wide)
        work[:, here] += nt(low[...], table[here, :])


def mlp_fused(lengths, seq, gu_w, shard, d_tab, f_tab, resid, cotangent, gains, dp):
    chunks, rows, model = seq.shape
    width = shard.shape[1]
    tile = 384
    wide = model // (dp // 2)
    half = rows // 2
    anywhere = pl.BlockSpec(memory_space=pl.ANY)
    vmem = pl.BlockSpec(memory_space=pltpu.VMEM)
    saved = jax.ShapeDtypeStruct((4, rows, width), BF16)
    return pl.pallas_call(
        functools.partial(mlp_kernel, rows),
        out_shape=(
            jax.ShapeDtypeStruct((rows, model), BF16),
            jax.ShapeDtypeStruct((rows, model), BF16),
            jax.ShapeDtypeStruct((4, rows, LANES), BF16),
            jax.ShapeDtypeStruct((rows, LANES), BF16),
            saved,
            saved,
            saved,
            jax.ShapeDtypeStruct((dp,) + shard.shape, BF16),
        ),
        in_specs=[pl.BlockSpec(memory_space=pltpu.SMEM)] + [anywhere] * 3 + [vmem] * 5,
        out_specs=(vmem,) * 4 + (anywhere,) * 4,
        scratch_shapes=[
            pltpu.VMEM((rows, model), F32),
            pltpu.VMEM((rows, LANES), F32),
            pltpu.VMEM((2, 4, rows, LANES), BF16),
            pltpu.VMEM((4, rows, model), BF16),
            pltpu.VMEM((2, model, 2 * tile), BF16),
            pltpu.VMEM((4, rows, width), BF16),
            pltpu.VMEM((2, 4, rows, tile), BF16),
            pltpu.VMEM((2, 4, rows, tile), BF16),
            pltpu.VMEM((dp,) + shard.shape, BF16),
            pltpu.SemaphoreType.DMA((2,)),
            pltpu.SemaphoreType.DMA((2, 2)),
            pltpu.SemaphoreType.DMA((2, 2)),
            pltpu.SemaphoreType.DMA((5,)),
            pltpu.SemaphoreType.DMA((3, dp // 2)),
            pltpu.SemaphoreType.DMA((dp,)),
            pltpu.VMEM((4, 4, rows, wide), BF16),
            pltpu.VMEM((4, 6, half, wide), BF16),
            pltpu.VMEM((4, 2, half, wide), BF16),
            pltpu.SemaphoreType.DMA((4, 6)),
            pltpu.SemaphoreType.DMA((4, 6)),
        ]
        + scatter_scratch(rows, LANES),
        compiler_params=pltpu.CompilerParams(
            collective_id=7, has_side_effects=True, vmem_limit_bytes=62 * 1024 * 1024
        ),
        name="mlp",
    )(lengths, seq, gu_w, shard, d_tab, f_tab, resid, cotangent, gains)


def chunk_gather_kernel(rows, x_ref, o_ref, own_sem, send_sem, recv_sem):
    sq = Square(rows)
    sq.greet()
    gather = ChunkGather(sq, x_ref, o_ref, send_sem, recv_sem)
    gather.start()
    own = pltpu.make_async_copy(x_ref, o_ref.at[0], own_sem)
    own.start()
    for chunk in range(1, 4):
        gather.wait_chunk(chunk)
    own.wait()
    gather.finish()


def chunk_gather(values):
    rows, width = values.shape
    anywhere = pl.BlockSpec(memory_space=pl.ANY)
    return pl.pallas_call(
        functools.partial(chunk_gather_kernel, rows),
        out_shape=jax.ShapeDtypeStruct((4, rows, width), values.dtype),
        in_specs=[anywhere],
        out_specs=anywhere,
        scratch_shapes=[
            pltpu.SemaphoreType.DMA,
            pltpu.SemaphoreType.DMA((6,)),
            pltpu.SemaphoreType.DMA((6,)),
        ],
        compiler_params=pltpu.CompilerParams(
            collective_id=8, has_side_effects=True, vmem_limit_bytes=VMEM_LIMIT
        ),
        name="chunk_gather",
    )(values)


class Layout:
    def __init__(self):
        self.dp = lax.axis_size("dp")
        self.tensor = lax.axis_size("tensor")
        self.total = self.dp * self.tensor
        self.d = lax.axis_index("dp")
        self.t = lax.axis_index("tensor")
        self.me = self.d * self.tensor + self.t
        self.heads_here = HQ // self.tensor
        self.ratio = HQ // KV
        self.share = max(1, self.tensor // KV)
        self.kv_owners = self.total // KV
        self.kv_head = self.t * self.heads_here // self.ratio
        self.user = self.me // self.dp
        self.kv_slice_head = self.me // self.kv_owners

    def device(self, flat):
        return {"dp": flat // self.tensor, "tensor": lax.rem(flat, self.tensor)}


def greet_all(lay):
    barrier = pltpu.get_barrier_semaphore()

    def signal(step, unused):
        peer = lax.rem(lay.me + step, lay.total)
        pl.semaphore_signal(
            barrier, inc=1, device_id=lay.device(peer), device_id_type=MESH
        )
        return unused

    lax.fori_loop(1, lay.total, signal, 0)
    pl.semaphore_wait(barrier, lay.total - 1)


def send_or_keep(lay, sends, source, target, send_sem, recv_sem, flat, maybe_own):
    def far():
        return pltpu.make_async_remote_copy(
            src_ref=source,
            dst_ref=target,
            send_sem=send_sem,
            recv_sem=recv_sem,
            device_id=lay.device(flat),
            device_id_type=MESH,
        )

    if maybe_own is None:
        copy = far()
        copy.start()
        sends.append((None, copy))
        return

    @pl.when(maybe_own)
    def _():
        pltpu.make_async_copy(source, target, recv_sem).start()

    @pl.when(jnp.logical_not(maybe_own))
    def _():
        far().start()

    sends.append((maybe_own, far()))


def finish(sends, received):
    for own, copy in sends:
        if own is None:
            copy.wait_send()
        else:

            @pl.when(jnp.logical_not(own))
            def _(copy=copy):
                copy.wait_send()

    for target, sem in received:
        pltpu.make_async_copy(target, target, sem).wait()


def tables_kernel(d_ref, f_ref, h_ref, k_ref, do_ref, fo_ref, ho_ref, ko_ref, *sems):
    lay = Layout()
    send_sems, recv_sem = sems[:4], sems[4]
    greet_all(lay)
    sends = []
    for step in range(lay.dp):
        group = lax.rem(lay.d + step, lay.dp)
        flat = group * lay.tensor + lay.user
        own = (lay.user == lay.t) if step == 0 else None
        for item, (source, target) in enumerate(((f_ref, fo_ref), (h_ref, ho_ref))):
            send_or_keep(
                lay,
                sends,
                source.at[group],
                target.at[lax.rem(lay.me, lay.dp)],
                send_sems[item].at[step],
                recv_sem.at[item],
                flat,
                own,
            )
        for extra in range(lay.share):
            user = lay.kv_slice_head * lay.share + extra
            flat = group * lay.tensor + user
            send_or_keep(
                lay,
                sends,
                k_ref.at[group],
                ko_ref.at[lax.rem(lay.me, lay.kv_owners)],
                send_sems[2].at[step, extra],
                recv_sem.at[2],
                flat,
                (user == lay.t) if step == 0 else None,
            )
    pltpu.make_async_copy(d_ref.at[lay.d], do_ref.at[lay.me], recv_sem.at[3]).start()
    for step in range(1, lay.total):
        flat = lax.rem(lay.me + step, lay.total)
        send_or_keep(
            lay,
            sends,
            d_ref.at[flat // lay.tensor],
            do_ref.at[lay.me],
            send_sems[3].at[step],
            recv_sem.at[3],
            flat,
            None,
        )
    finish(
        sends,
        (
            (fo_ref, recv_sem.at[0]),
            (ho_ref, recv_sem.at[1]),
            (ko_ref, recv_sem.at[2]),
            (do_ref, recv_sem.at[3]),
        ),
    )


def grads_kernel(d_ref, f_ref, h_ref, k_ref, do_ref, fo_ref, ho_ref, ko_ref, *sems):
    lay = Layout()
    send_sems, recv_sem = sems[:4], sems[4]
    greet_all(lay)
    sends = []
    for step in range(lay.dp):
        slot = lax.rem(lay.d + step, lay.dp)
        flat = lay.t * lay.dp + slot
        for item, (source, target) in enumerate(((f_ref, fo_ref), (h_ref, ho_ref))):
            send_or_keep(
                lay,
                sends,
                source.at[slot],
                target.at[lay.d],
                send_sems[item].at[step],
                recv_sem.at[item],
                flat,
                flat == lay.me,
            )
    for step in range(lay.kv_owners):
        slot = lax.rem(lay.d + step, lay.kv_owners)
        flat = lay.kv_head * lay.kv_owners + slot
        send_or_keep(
            lay,
            sends,
            k_ref.at[slot],
            ko_ref.at[lay.d * lay.share + lax.rem(lay.t, lay.share)],
            send_sems[2].at[step // lay.share, step % lay.share],
            recv_sem.at[2],
            flat,
            flat == lay.me,
        )
    pltpu.make_async_copy(d_ref.at[lay.me], do_ref.at[lay.me], recv_sem.at[3]).start()
    for step in range(1, lay.total):
        flat = lax.rem(lay.me + step, lay.total)
        send_or_keep(
            lay,
            sends,
            d_ref.at[flat],
            do_ref.at[lay.me],
            send_sems[3].at[step],
            recv_sem.at[3],
            flat,
            None,
        )
    finish(
        sends,
        (
            (fo_ref, recv_sem.at[0]),
            (ho_ref, recv_sem.at[1]),
            (ko_ref, recv_sem.at[2]),
            (do_ref, recv_sem.at[3]),
        ),
    )


def exchange(kernel, name, number, arrays, outs, dp, total, share):
    anywhere = pl.BlockSpec(memory_space=pl.ANY)
    return pl.pallas_call(
        kernel,
        out_shape=tuple(jax.ShapeDtypeStruct(shape, BF16) for shape in outs),
        in_specs=[anywhere] * 4,
        out_specs=(anywhere,) * 4,
        scratch_shapes=[
            pltpu.SemaphoreType.DMA((dp,)),
            pltpu.SemaphoreType.DMA((dp,)),
            pltpu.SemaphoreType.DMA((dp, share)),
            pltpu.SemaphoreType.DMA((total,)),
            pltpu.SemaphoreType.DMA((4,)),
        ],
        compiler_params=pltpu.CompilerParams(
            collective_id=number, has_side_effects=True, vmem_limit_bytes=VMEM_LIMIT
        ),
        name=name,
    )(*arrays)


def chunk_start(sq, chunk, part):
    is_own = (3 - chunk) // 3
    is_far = chunk // 3
    near = 1 - is_own - is_far
    neighbour = sq.down if part == 1 else sq.across
    block = sq.me * is_own + sq.far * is_far + neighbour * near
    other_half = chunk // 2 - is_far
    half = 1 - other_half if part == 1 else other_half
    return pl.multiple_of(block * sq.rows + half * sq.half, sq.half)


def rotate_back(values, cosine, sine):
    first, second = values[:, : HD // 2], values[:, HD // 2 :]
    return jnp.concatenate([first * cosine + second * sine, second * cosine - first * sine], axis=1)


def attn_back_kernel(
    rows,
    ids_ref,
    length_ref,
    back_ref,
    low_gu_ref,
    resid_ref,
    total_ref,
    cot_ref,
    layer_ref,
    gains_ref,
    weight_hbm,
    seq_hbm,
    q_ref,
    k_ref,
    kt_ref,
    v_ref,
    attended_ref,
    inverse_ref,
    cos_ref,
    sin_ref,
    low_ref,
    d_table,
    h_table,
    k_table,
    normed_ref,
    low_out_ref,
    grad_mlp_ref,
    low_down_ref,
    f_ref,
    o_ref,
    in_out,
    heads_out,
    hidden_out,
    query_out,
    keyval_out,
    gateup_out,
    resid_out,
    weight,
    work,
    g_ref,
    low_sum,
    buf,
    att,
    q_grad,
    k_sum,
    v_sum,
    kv_grad,
    joined,
    d_turned,
    h_turned,
    k_turned,
    d_send,
    d_land,
    d_sum,
    d_recv,
    f_recv,
    hk_send,
    hk_land,
    hk_recv,
    load_sem,
    own_sem,
    gather_send,
    gather_recv,
    f_sem,
    d_sem,
    hk_sem,
    group_send,
    group_recv,
    line_recv,
    *scratch,
):
    sq = Square(rows)
    dp = lax.axis_size("dp")
    d = lax.axis_index("dp")
    model = o_ref.shape[-1]
    half = sq.half
    wide = tile_of(model)
    weight_load = pltpu.make_async_copy(weight_hbm, weight, load_sem.at[0])
    seq_load = pltpu.make_async_copy(seq_hbm, buf, load_sem.at[1])
    weight_load.start()
    peers = [{"tensor": peer} for peer in (sq.across, sq.down, sq.far)]
    peers += [{"dp": lax.rem(d + step, dp)} for step in range(1, dp)]
    call(peers)

    def turned(values):
        return values.astype(F32).T.astype(BF16)

    low_gu = low_gu_ref[...].astype(BF16)

    @pl.loop(0, model // wide)
    def _(step):
        here = columns(step, wide)
        work[:, here] = back_ref[:, here] + nt(low_gu, d_table[here, :])

    @pl.loop(0, rows // BLOCK)
    def _(step):
        here = pl.ds(pl.multiple_of(step * BLOCK, BLOCK), BLOCK)
        at = sq.me * rows + step * BLOCK + lax.broadcasted_iota(jnp.int32, (BLOCK, 1), 0)
        valid = (at < length_ref[0]).astype(F32)
        mid = cot_ref[here, :].astype(F32) * valid + norm_back(
            resid_ref[here, :], gains_ref[2:3, :], work[here, :]
        )
        work[here, :] = mid
        g_ref[here, :] = norm_back(total_ref[here, :], gains_ref[1:2, :], mid).astype(BF16)

    own_load = pltpu.make_async_copy(g_ref, buf.at[0], own_sem)
    own_load.start()
    pl.semaphore_wait(pltpu.get_barrier_semaphore(), len(peers))
    gather = ChunkGather(sq, g_ref, buf, gather_send, gather_recv)
    gather.start()
    line = []

    def along(source_at, target, send_sem, recv_sem):
        own = pltpu.make_async_copy(source_at(d), target.at[d], recv_sem)
        own.start()
        for step in range(1, dp):
            peer = lax.rem(d + step, dp)
            copy = pltpu.make_async_remote_copy(
                src_ref=source_at(peer),
                dst_ref=target.at[d],
                send_sem=send_sem.at[step],
                recv_sem=recv_sem,
                device_id={"dp": peer},
                device_id_type=MESH,
            )
            copy.start()
            line.append(copy)

    along(lambda k: f_ref.at[k // 2, lax.rem(k, 2)], f_recv, f_sem, line_recv.at[0])
    part, part_low = scratch[0], scratch[5]
    scatters = (ChunkScatter(sq, *scratch[:5]), ChunkScatter(sq, *scratch[5:10]))

    d_turned[...] = jnp.zeros_like(d_turned)
    low_grads = (
        (turned(low_gu)[GATE.start : UP.stop], normed_ref, slice(GATE.start, UP.stop)),
        (turned(low_out_ref[...])[OUT], g_ref, OUT),
        (turned(low_down_ref[...])[DOWN], grad_mlp_ref, DOWN),
    )

    @pl.loop(0, model // wide)
    def _(step):
        here = columns(step, wide)
        for low, source, place in low_grads:
            d_turned[place, here] = nn(low, source[:, here])

    h_turned[...] = jnp.zeros_like(h_turned)
    k_turned[...] = jnp.zeros_like(k_turned)
    k_sum[...] = jnp.zeros_like(k_sum)
    v_sum[...] = jnp.zeros_like(v_sum)
    own_load.wait()
    weight_load.wait()
    q_width = q_ref.shape[1]
    qkv_width = q_width + 2 * HD
    heads = q_width // HD
    stacked = heads * half

    @pl.loop(0, 4)
    def _(chunk):
        for step in range(4):

            @pl.when(chunk == step)
            def _(step=step):
                gather.wait_chunk(step)

        incoming = buf.at[chunk]
        low_out = band(nn(incoming[...], d_table[...]), OUT).astype(BF16)
        att[...] = (
            nn(incoming[...], weight[:, qkv_width:]) + nt(low_out, h_table[...])
        ).astype(BF16)
        low_turned = turned(low_out)[OUT]
        for side in range(2):
            start = chunk_start(sq, chunk, side)
            here = pl.ds(start, half)
            place = pl.ds(side * half, half)
            h_turned[:RANK, :] += nn(
                low_turned[:, side * half : (side + 1) * half], attended_ref[here, :]
            )
            queries = jnp.concatenate(
                [q_ref[here, h * HD : (h + 1) * HD] for h in range(heads)], axis=0
            )
            grads = jnp.concatenate(
                [att[place, h * HD : (h + 1) * HD] for h in range(heads)], axis=0
            )
            inverse = jnp.concatenate([inverse_ref[h : h + 1, here] for h in range(heads)], axis=1)
            key_at = lax.broadcasted_iota(jnp.int32, (LEN, stacked), 0)
            query_at = lax.rem(lax.broadcasted_iota(jnp.int32, (LEN, stacked), 1), half) + start
            allowed = (key_at <= query_at) & (key_at < length_ref[0])
            squash = jnp.tanh(nt(k_ref[...], queries) * (1.0 / SOFT_CAP))
            probs = jnp.where(allowed, jnp.exp(SOFT_CAP * squash) * inverse, 0.0)
            grad_probs = nt(v_ref[...], grads)
            mean = jnp.sum(probs * grad_probs, axis=0, keepdims=True)
            grad_raw = (probs * (grad_probs - mean) * (1.0 - squash * squash)).astype(BF16)
            k_sum[...] += nn(grad_raw, queries)
            v_sum[...] += nn(probs.astype(BF16), grads)
            q_back = nn(kt_ref[...], grad_raw).T * HD ** (-0.5)
            for h in range(heads):
                q_grad[chunk, place, h * HD : (h + 1) * HD] = rotate_back(
                    q_back[h * half : (h + 1) * half], cos_ref[here, :], sin_ref[here, :]
                ).astype(BF16)

    gather.finish()
    seq_load.start()
    kv_grad[:, :HD] = rotate_back(k_sum[...], cos_ref[...], sin_ref[...]).astype(BF16)
    kv_grad[:, HD:] = v_sum[...].astype(BF16)

    @pl.loop(0, 4)
    def _(step):
        chunk = step + 3 * ((3 - step) // 3) - 3 * (step // 3)
        joined[chunk, :, :q_width] = q_grad[chunk]
        for side in range(2):
            here = pl.ds(chunk_start(sq, chunk, side), half)
            joined[chunk, pl.ds(side * half, half), q_width:] = kv_grad[here, :]
        part_low[chunk] = (
            band(nn(joined[chunk, :, :q_width], h_table[...]), QUERY)
            + band(nn(joined[chunk, :, q_width : q_width + HD], k_table[...]), KEY)
            + band(nn(joined[chunk, :, q_width + HD :], k_table[...]), VALUE)
        ).astype(BF16)

        @pl.loop(0, model // wide)
        def _(tile):
            here = columns(tile, wide)
            part[chunk, :, here] = nt(joined[chunk], weight[here, :qkv_width]).astype(BF16)

        @pl.when(step == 0)
        def _():
            for scatter in scatters:
                scatter.send_far()

        @pl.when(step == 1)
        def _():
            for scatter in scatters:
                scatter.send_own()

    seq_load.wait()

    @pl.loop(0, 4)
    def _(chunk):
        grad_turned = turned(part_low[chunk])[: VALUE.stop]
        for side in range(2):
            here = pl.ds(chunk_start(sq, chunk, side), half)
            place = slice(side * half, (side + 1) * half)
            low_turned = turned(low_ref[here, :])
            mine = joined.at[chunk, pl.ds(side * half, half)]
            h_turned[RANK : 2 * RANK, :] += nn(low_turned[QUERY], mine[:, :q_width])
            k_turned[:RANK, :] += nn(low_turned[KEY], mine[:, q_width : q_width + HD])
            k_turned[RANK : 2 * RANK, :] += nn(low_turned[VALUE], mine[:, q_width + HD :])
            where_from = chunk_start(sq, chunk, side)
            block = where_from // rows
            inside = pl.ds(pl.multiple_of(where_from - block * rows, half), half)

            @pl.loop(0, model // wide)
            def _(tile):
                where = columns(tile, wide)
                d_turned[: VALUE.stop, where] += nn(
                    grad_turned[:, place],
                    buf[block, inside, where],
                )

    @pl.loop(0, model // LANES)
    def _(step):
        here = columns(step, LANES)
        d_send[here, :] = d_turned[:, here].T.astype(BF16)

    d_rows = d_sum.shape[1]
    spread = []
    for k in range(dp):
        spread.append(
            sq.spread(
                lambda peer, k=k: d_send.at[pl.ds(pl.multiple_of((k * 4 + peer) * d_rows, 8), d_rows)],
                d_land.at[k],
                group_send.at[k],
                group_recv.at[k],
            )
        )
    cores = hk_send.shape[0]
    h_size, k_size = q_width // dp, HD // dp
    hk_send[...] = jnp.zeros_like(hk_send)
    for core in range(cores):
        for peer in range(4):
            at = core * 4 + peer
            hk_send[core, peer, : 2 * RANK, :h_size] = h_turned[
                : 2 * RANK, at * h_size : (at + 1) * h_size
            ].astype(BF16)
            hk_send[core, peer, 2 * RANK :, :k_size] = k_turned[
                : 2 * RANK, at * k_size : (at + 1) * k_size
            ].astype(BF16)
    spread.append(
        sq.spread(lambda peer: hk_send.at[:, peer], hk_land, group_send.at[dp], group_recv.at[dp])
    )
    for copies in spread:
        for copy in copies:
            copy.start()
    for link in range(2):
        for scatter in scatters:
            scatter.pass_on(link)
    for copies in spread:
        copies[0].wait()
        for copy in copies[1:]:
            copy.wait_recv()
    for k in range(dp):
        d_sum[k] = sum(d_land[k, t].astype(F32) for t in range(4)).astype(BF16)
    along(lambda k: d_sum.at[k], d_recv, d_sem, line_recv.at[1])
    along(lambda k: hk_land.at[k // 2, lax.rem(k, 2)], hk_recv, hk_sem, line_recv.at[2])
    scatters[1].collect(low_sum)
    low_qkv = low_sum[...].astype(BF16)
    for link in range(2):
        scatters[0].copy(0, link).wait_recv()
        scatters[0].copy(2, link).wait_recv()
    landing = scratch[1]
    low_sum[...] = low_qkv.astype(F32)

    @pl.loop(0, rows // BLOCK)
    def _(step):
        here = pl.ds(pl.multiple_of(step * BLOCK, BLOCK), BLOCK)
        link = (step * BLOCK) // half
        there = pl.ds(pl.multiple_of(step * BLOCK - link * half, BLOCK), BLOCK)
        total = (
            part[0, here, :].astype(F32)
            + landing[link, there, :].astype(F32)
            + landing[4 + link, there, :].astype(F32)
            + nt(low_sum[here, :].astype(BF16), d_table[...])
        )
        o_ref[here, :] = (
            work[here, :] + norm_back(layer_ref[here, :].astype(F32), gains_ref[0:1, :], total)
        ).astype(BF16)

    for item, target in enumerate((f_recv, d_recv, hk_recv)):
        pltpu.make_async_copy(target, target, line_recv.at[item]).wait()

    @pl.loop(0, NA)
    def _(adapter):
        def pick(received):
            total = None
            for group in range(dp):
                mine = jnp.where(
                    ids_ref[group] == adapter, received[group].astype(F32), 0.0
                )
                total = mine if total is None else total + mine
            return total

        d_all = pick(d_recv)
        in_out[adapter] = d_all[:, : 5 * RANK]
        d_flip = d_all.T
        f_all = pick(f_recv)
        hidden_out[adapter] = f_all[:RANK].T
        hk_all = pick(hk_recv)
        heads_out[adapter] = hk_all[:RANK, :h_size].T
        query_out[adapter] = hk_all[RANK : 2 * RANK, :h_size]
        for which in range(2):
            first = (which + 2) * RANK
            keyval_out[adapter, which] = hk_all[first : first + RANK, :k_size]
            first = (which + 1) * RANK
            gateup_out[adapter, which] = f_all[first : first + RANK]
            first = (which + 5) * RANK
            resid_out[adapter, which] = d_flip[first : first + RANK]

    for copies in spread:
        for copy in copies[1:]:
            copy.wait_send()
    for copy in line:
        copy.wait_send()
    for scatter in scatters:
        scatter.finish()


def attn_back_fused(scalars, arrays, grad_shapes, dp, total):
    anywhere = pl.BlockSpec(memory_space=pl.ANY)
    vmem = pl.BlockSpec(memory_space=pltpu.VMEM)
    smem = pl.BlockSpec(memory_space=pltpu.SMEM)
    rows, model = arrays[0].shape
    weight, seq, q, f_in = arrays[7], arrays[8], arrays[9], arrays[-1]
    q_width = q.shape[1]
    specs = [smem, smem] + [vmem] * len(arrays)
    specs[9] = specs[10] = anywhere
    outs = [jax.ShapeDtypeStruct((rows, model), BF16)]
    outs += [jax.ShapeDtypeStruct(shape, F32) for shape in grad_shapes]
    d_rows = model // total
    messages = f_in.shape[2:]
    return pl.pallas_call(
        functools.partial(attn_back_kernel, rows),
        out_shape=tuple(outs),
        in_specs=specs,
        out_specs=(vmem,) * len(outs),
        scratch_shapes=[
            pltpu.VMEM(weight.shape, BF16),
            pltpu.VMEM((rows, model), F32),
            pltpu.VMEM((rows, model), BF16),
            pltpu.VMEM((rows, LANES), F32),
            pltpu.VMEM((4, rows, model), BF16),
            pltpu.VMEM((rows, q_width), BF16),
            pltpu.VMEM((4, rows, q_width), BF16),
            pltpu.VMEM((LEN, HD), F32),
            pltpu.VMEM((LEN, HD), F32),
            pltpu.VMEM((LEN, 2 * HD), BF16),
            pltpu.VMEM((4, rows, q_width + 2 * HD), BF16),
            pltpu.VMEM((LANES, model), F32),
            pltpu.VMEM((2 * RANK, q_width), F32),
            pltpu.VMEM((2 * RANK, HD), F32),
            pltpu.VMEM((model, LANES), BF16),
            pltpu.VMEM((dp, 4, d_rows, LANES), BF16),
            pltpu.VMEM((dp, d_rows, LANES), BF16),
            pltpu.VMEM((dp, d_rows, LANES), BF16),
            pltpu.VMEM((dp,) + messages, BF16),
            pltpu.VMEM((dp // 4, 4, 4 * RANK, LANES), BF16),
            pltpu.VMEM((4, dp // 4, 4 * RANK, LANES), BF16),
            pltpu.VMEM((dp, 4 * RANK, LANES), BF16),
            pltpu.SemaphoreType.DMA((2,)),
            pltpu.SemaphoreType.DMA,
            pltpu.SemaphoreType.DMA((6,)),
            pltpu.SemaphoreType.DMA((6,)),
            pltpu.SemaphoreType.DMA((dp,)),
            pltpu.SemaphoreType.DMA((dp,)),
            pltpu.SemaphoreType.DMA((dp,)),
            pltpu.SemaphoreType.DMA((dp + 1, 3)),
            pltpu.SemaphoreType.DMA((dp + 1, 4)),
            pltpu.SemaphoreType.DMA((3,)),
        ]
        + scatter_scratch(rows, model)
        + scatter_scratch(rows, LANES),
        compiler_params=pltpu.CompilerParams(
            collective_id=6, has_side_effects=True, vmem_limit_bytes=62 * 1024 * 1024
        ),
        name="attn_back",
    )(*scalars, *arrays)


def per_device(
    layer_in,
    cotangent,
    lengths,
    adapter_ids,
    norm_gains,
    query_weight,
    key_weight,
    value_weight,
    out_weight,
    gate_weight,
    up_weight,
    down_weight,
    adapt_in,
    adapt_heads,
    adapt_hidden,
    lift_query,
    lift_keyval,
    lift_gateup,
    lift_resid,
):
    lay = Layout()
    count = lay.tensor
    rows = layer_in.shape[0]
    group_rows = rows * count
    assert lengths.shape[0] == 1 and group_rows == LEN
    heads_here = lay.heads_here
    head_width = heads_here * HD
    hidden_here = FF // count
    assert lay.ratio % heads_here == 0

    key_cols = lax.dynamic_slice_in_dim(key_weight, lay.kv_head * HD, HD, 1)
    value_cols = lax.dynamic_slice_in_dim(value_weight, lay.kv_head * HD, HD, 1)
    attn_shard = jnp.concatenate([query_weight, key_cols, value_cols, out_weight.T], axis=1)
    attn_w = lax.all_gather(attn_shard, "dp", axis=0, tiled=True)
    gate_up_shard = jnp.concatenate([gate_weight, up_weight], axis=1)
    down_shard = down_weight.T
    attn_shard, gate_up_shard, down_shard = lax.optimization_barrier(
        (attn_shard, gate_up_shard, down_shard)
    )
    gate_up_w = lax.all_gather(gate_up_shard, "dp", axis=0, tiled=True)
    qkv_width = head_width + 2 * HD

    all_ids = lax.all_gather(adapter_ids[:, 0], "dp", axis=0, tiled=True)
    group_hot = (all_ids[:, None] == jnp.arange(NA, dtype=jnp.int32)[None, :]).astype(BF16)

    def rows_of(table):
        moved = jnp.moveaxis(table, -1, 1)
        return moved.reshape(NA, moved.shape[1], -1)

    def choose(*parts):
        packed = lanes(*parts)
        return lax.dot_general(
            group_hot, packed, (((1,), (0,)), ((), ())), preferred_element_type=F32
        ).astype(BF16)

    d_send = choose((QUERY, adapt_in), (OUT, rows_of(lift_resid)))
    f_send = choose((GATE, rows_of(lift_gateup)), (DOWN, adapt_hidden))
    h_send = choose((QUERY, rows_of(lift_query)), (OUT, adapt_heads))
    k_send = choose((KEY, rows_of(lift_keyval)))
    d_rows, f_rows, h_rows, k_rows = (item.shape[1] for item in (d_send, f_send, h_send, k_send))
    d_tab, f_tab, h_tab, k_tab = exchange(
        tables_kernel,
        "adapter_tables",
        3,
        (d_send, f_send, h_send, k_send),
        (
            (lay.total, d_rows, LANES),
            (lay.dp, f_rows, LANES),
            (lay.dp, h_rows, LANES),
            (lay.kv_owners, k_rows, LANES),
        ),
        lay.dp,
        lay.total,
        lay.share,
    )
    d_tab = d_tab.reshape(D, LANES)
    f_tab = f_tab.reshape(hidden_here, LANES)
    h_tab = h_tab.reshape(head_width, LANES)
    k_tab = k_tab.reshape(HD, LANES)
    in_qkv, in_gu = d_tab[:, : 3 * RANK], d_tab[:, 3 * RANK : 5 * RANK]
    lift_out, lift_down = d_tab[:, OUT], d_tab[:, DOWN]
    map_hidden, lift_gate, lift_up = f_tab[:, DOWN], f_tab[:, GATE], f_tab[:, UP]
    map_heads, lift_q = h_tab[:, OUT], h_tab[:, QUERY]
    lift_k, lift_v = k_tab[:, KEY], k_tab[:, VALUE]

    row_start = lay.t * rows
    length = lengths[0]
    row_valid = ((row_start + jnp.arange(rows, dtype=jnp.int32)) < length).astype(F32)[:, None]
    cosine, sine = tables(LEN, HD)
    place = jnp.arange(LEN, dtype=jnp.int32)
    allowed = (place[:, None] >= place[None, :]) & (place[None, :] < length)

    resid_in = layer_in.astype(F32)
    normed_attn = rms_norm(resid_in, norm_gains[0]).astype(BF16)
    seq_attn = tensor_gather(normed_attn, count)
    low_qkv = nn(seq_attn, in_qkv).astype(BF16)
    low_q, low_k, low_v = (low_qkv[:, i * RANK : (i + 1) * RANK] for i in range(3))
    qkv = nn(seq_attn, attn_w[:, :qkv_width])
    query_pre = (qkv[:, :head_width] + nt(low_q, lift_q)).reshape(LEN, heads_here, HD)
    key_pre = (qkv[:, head_width : head_width + HD] + nt(low_k, lift_k)).reshape(LEN, 1, HD)
    value_pre = qkv[:, head_width + HD :] + nt(low_v, lift_v)
    queries = (rotate(query_pre, cosine, sine) * HD ** (-0.5)).astype(BF16)
    keys = rotate(key_pre, cosine, sine).astype(BF16).reshape(LEN, HD)
    values = value_pre.astype(BF16)

    def scores_of():
        raw = jnp.einsum("qhd,kd->hqk", queries, keys, preferred_element_type=F32)
        squash = jnp.tanh(raw / SOFT_CAP)
        return squash, jnp.where(allowed[None], jnp.exp(SOFT_CAP * squash), 0.0)

    squash, weights = scores_of()
    inverse_total = 1.0 / jnp.sum(weights, axis=-1, keepdims=True)
    attended = jnp.einsum(
        "hqk,kd->qhd", (weights * inverse_total).astype(BF16), values, preferred_element_type=F32
    )
    attended = attended.astype(BF16).reshape(LEN, head_width)
    w_out = attn_w[:, qkv_width:]
    out_part = nt(attended, w_out).astype(BF16)
    low_out_part = pad_lanes(nn(attended, map_heads).astype(BF16))
    attn_main, low_out = tensor_scatter(out_part, low_out_part, count)
    low_out = low_out[:, :RANK].astype(BF16)
    attn_total = attn_main + nt(low_out, lift_out)
    resid_mid = resid_in + rms_norm(attn_total, norm_gains[1])

    normed_mlp = rms_norm(resid_mid, norm_gains[2]).astype(BF16)
    if count == 4 and lay.dp == 8:
        layer_out, grad_mlp, low_gu, low_down, hidden, slope, gelu, down_w = mlp_fused(
            lengths,
            chunk_gather(normed_mlp),
            gate_up_w,
            down_shard,
            d_tab,
            f_tab,
            resid_mid,
            cotangent,
            norm_gains,
            lay.dp,
        )
        mlp_back, grad_low_gu, f_grad = mlp_back_fused(
            grad_mlp,
            down_w.reshape(D, hidden_here),
            gate_up_w,
            slope,
            gelu,
            hidden,
            low_gu,
            d_tab,
            f_tab,
            lay.dp,
        )
        return (
            layer_out,
            *attn_back_fused(
                (all_ids, lengths),
                (
                    mlp_back,
                    grad_low_gu,
                    resid_mid,
                    attn_total,
                    cotangent,
                    layer_in,
                    norm_gains,
                    attn_w,
                    seq_attn.reshape(count, rows, D),
                    queries.reshape(LEN, head_width),
                    keys,
                    keys.T,
                    values,
                    attended,
                    inverse_total.reshape(heads_here, LEN),
                    cosine.reshape(LEN, HD // 2),
                    sine.reshape(LEN, HD // 2),
                    pad_lanes(low_qkv),
                    d_tab,
                    h_tab,
                    k_tab,
                    normed_mlp,
                    lanes((OUT, low_out)),
                    grad_mlp,
                    low_down,
                    f_grad,
                ),
                tuple(
                    table.shape
                    for table in (
                        adapt_in,
                        adapt_heads,
                        adapt_hidden,
                        lift_query,
                        lift_keyval,
                        lift_gateup,
                        lift_resid,
                    )
                ),
                lay.dp,
                lay.total,
            ),
        )

    seq_mlp = tensor_gather(normed_mlp, count)
    low_gu = nn(seq_mlp, in_gu).astype(BF16)
    low_g, low_u = low_gu[:, :RANK], low_gu[:, RANK:]
    w_gate, w_up = gate_up_w[:, :hidden_here], gate_up_w[:, hidden_here:]
    gate = nn(seq_mlp, w_gate) + nt(low_g, lift_gate)
    up = nn(seq_mlp, w_up) + nt(low_u, lift_up)
    hidden, slope, gelu = gelu_parts(gate, up)
    down_w = lax.all_gather(down_shard, "dp", axis=0, tiled=True)
    down_part = nt(hidden, down_w).astype(BF16)
    low_down_part = pad_lanes(nn(hidden, map_hidden).astype(BF16))
    mlp_main, low_down = tensor_scatter(down_part, low_down_part, count)
    low_down = low_down[:, :RANK].astype(BF16)
    mlp_total = mlp_main + nt(low_down, lift_down)
    layer_out = (row_valid * (resid_mid + rms_norm(mlp_total, norm_gains[3]))).astype(BF16)

    grad_out = cotangent.astype(F32) * row_valid
    grad_mlp = norm_back(mlp_total, norm_gains[3], grad_out).astype(BF16)
    seq_grad_mlp = tensor_gather(grad_mlp, count)
    grad_low_down = nn(seq_grad_mlp, lift_down).astype(BF16)
    grad_hidden = nn(seq_grad_mlp, down_w) + nt(grad_low_down, map_hidden)
    grad_gate = (grad_hidden * slope.astype(F32)).astype(BF16)
    grad_up = (grad_hidden * gelu.astype(F32)).astype(BF16)
    low_gu_part = pad_lanes(
        jnp.concatenate([nn(grad_gate, lift_gate), nn(grad_up, lift_up)], axis=1).astype(BF16)
    )
    mlp_back_part = (nt(grad_gate, w_gate) + nt(grad_up, w_up)).astype(BF16)
    mlp_back, grad_low_gu = tensor_scatter(mlp_back_part, low_gu_part, count)
    f_parts = [tn(hidden, grad_low_down), tn(grad_gate, low_g), tn(grad_up, low_u)]
    grad_low_gu = grad_low_gu[:, : 2 * RANK].astype(BF16)
    grad_normed_mlp = mlp_back + nt(grad_low_gu, in_gu)
    grad_mid = grad_out + norm_back(resid_mid, norm_gains[2], grad_normed_mlp)

    grad_attn = norm_back(attn_total, norm_gains[1], grad_mid).astype(BF16)
    seq_grad_attn = tensor_gather(grad_attn, count)
    grad_low_out = nn(seq_grad_attn, lift_out).astype(BF16)
    grad_attended = (nn(seq_grad_attn, w_out) + nt(grad_low_out, map_heads)).astype(BF16)
    grad_heads = grad_attended.reshape(LEN, heads_here, HD)
    probs = weights * inverse_total
    probs_low = probs.astype(BF16)
    grad_probs = jnp.einsum("qhd,kd->hqk", grad_heads, values, preferred_element_type=F32)
    grad_value = jnp.einsum("hqk,qhd->kd", probs_low, grad_heads, preferred_element_type=F32)
    grad_capped = probs * (grad_probs - jnp.sum(probs * grad_probs, axis=-1, keepdims=True))
    grad_raw = (grad_capped * (1.0 - squash * squash)).astype(BF16)
    grad_query = jnp.einsum("hqk,kd->qhd", grad_raw, keys, preferred_element_type=F32)
    grad_key = jnp.einsum("hqk,qhd->kd", grad_raw, queries, preferred_element_type=F32)
    grad_q_pre = rotate(grad_query * HD ** (-0.5), cosine, -sine).astype(BF16)
    grad_q_pre = grad_q_pre.reshape(LEN, head_width)
    grad_k_pre = rotate(grad_key.reshape(LEN, 1, HD), cosine, -sine).astype(BF16)
    grad_k_pre = grad_k_pre.reshape(LEN, HD)
    grad_v_pre = grad_value.astype(BF16)
    low_qkv_part = pad_lanes(
        jnp.concatenate(
            [nn(grad_q_pre, lift_q), nn(grad_k_pre, lift_k), nn(grad_v_pre, lift_v)], axis=1
        ).astype(BF16)
    )
    grad_qkv = jnp.concatenate([grad_q_pre, grad_k_pre, grad_v_pre], axis=1)
    attn_back_part = nt(grad_qkv, attn_w[:, :qkv_width]).astype(BF16)
    attn_back, grad_low_qkv = tensor_scatter(attn_back_part, low_qkv_part, count)
    grad_low_qkv = grad_low_qkv[:, : 3 * RANK].astype(BF16)
    grad_normed_attn = attn_back + nt(grad_low_qkv, in_qkv)
    input_grad = (grad_mid + norm_back(resid_in, norm_gains[0], grad_normed_attn)).astype(BF16)

    def packed(parts, blocks):
        return pad_lanes(jnp.concatenate(parts, axis=1).astype(BF16)).reshape(
            blocks, -1, LANES
        )

    d_grad = packed(
        [
            tn(normed_attn, grad_low_qkv),
            tn(normed_mlp, grad_low_gu),
            tn(grad_attn, low_out),
            tn(grad_mlp, low_down),
        ],
        lay.total,
    )
    f_grad = packed(f_parts, lay.dp)
    h_grad = packed([tn(attended, grad_low_out), tn(grad_q_pre, low_q)], lay.dp)
    k_grad = packed([tn(grad_k_pre, low_k), tn(grad_v_pre, low_v)], lay.kv_owners)
    d_all, f_all, h_all, k_all = exchange(
        grads_kernel,
        "adapter_grads",
        4,
        (d_grad, f_grad, h_grad, k_grad),
        (
            (lay.total, d_rows, LANES),
            (lay.dp, f_rows, LANES),
            (lay.dp, h_rows, LANES),
            (lay.dp * lay.share, k_rows, LANES),
        ),
        lay.dp,
        lay.total,
        lay.share,
    )

    def collect(received):
        repeats = received.shape[0] // lay.dp
        hot = jnp.repeat(group_hot, repeats, axis=0)
        return lax.dot_general(
            hot, received, (((0,), (0,)), ((), ())), preferred_element_type=F32
        )

    d_all, f_all, h_all, k_all = (collect(item) for item in (d_all, f_all, h_all, k_all))

    def lift_form(values, shape):
        return jnp.moveaxis(values, 1, 2).reshape(shape)

    return (
        layer_out,
        input_grad,
        d_all[:, :, : 5 * RANK],
        h_all[:, :, :RANK],
        f_all[:, :, :RANK],
        lift_form(h_all[:, :, RANK : 2 * RANK], lift_query.shape),
        lift_form(k_all[:, :, : 2 * RANK], lift_keyval.shape),
        lift_form(f_all[:, :, RANK : 3 * RANK], lift_gateup.shape),
        lift_form(d_all[:, :, 5 * RANK : 7 * RANK], lift_resid.shape),
    )


def solution(mesh):
    return jax.shard_map(
        per_device,
        mesh=mesh,
        in_specs=(
            P(("dp", "tensor"), None),
            P(("dp", "tensor"), None),
            P("dp"),
            P("dp", None),
            P(),
            P("dp", "tensor"),
            P("dp", None),
            P("dp", None),
            P("tensor", "dp"),
            P("dp", "tensor"),
            P("dp", "tensor"),
            P("tensor", "dp"),
            P(None, ("dp", "tensor"), None),
            P(None, ("dp", "tensor"), None),
            P(None, ("dp", "tensor"), None),
            P(None, None, ("dp", "tensor")),
            P(None, None, None, ("dp", "tensor")),
            P(None, None, None, ("dp", "tensor")),
            P(None, None, None, ("dp", "tensor")),
        ),
        out_specs=(
            P(("dp", "tensor"), None),
            P(("dp", "tensor"), None),
            P(None, ("dp", "tensor"), None),
            P(None, ("dp", "tensor"), None),
            P(None, ("dp", "tensor"), None),
            P(None, None, ("dp", "tensor")),
            P(None, None, None, ("dp", "tensor")),
            P(None, None, None, ("dp", "tensor")),
            P(None, None, None, ("dp", "tensor")),
        ),
        check_vma=False,
    )
```

```python
import functools

import jax
import jax.numpy as jnp
from jax import lax
from jax.experimental import pallas as pl
from jax.experimental.pallas import tpu as pltpu
from jax.sharding import PartitionSpec as P

D = 2304
HQ = 8
KV = 4
HD = 256
FF = 9216
NA = 8
RANK = 16
LEN = 1024
LANES = 128

EPSILON = 1e-06
SOFT_CAP = 50.0
MESH = pl.DeviceIdType.MESH
BF16 = jnp.bfloat16
F32 = jnp.float32
VMEM_LIMIT = 48 * 1024 * 1024
BLOCK = 32


def rms_norm(values, gain_row):
    return (
        values * lax.rsqrt(jnp.mean(values * values, axis=-1, keepdims=True) + EPSILON) * gain_row
    )


def norm_back(values, gain_row, gradient):
    inverse = lax.rsqrt(jnp.mean(values * values, axis=-1, keepdims=True) + EPSILON)
    scaled = gradient * gain_row
    normed = values * inverse
    return inverse * (scaled - normed * jnp.mean(scaled * normed, axis=-1, keepdims=True))


def gelu_parts(gate, up):
    scale = (2.0 / jnp.pi) ** 0.5
    square = gate * gate
    bend = jnp.tanh(scale * gate * (1.0 + 0.044715 * square))
    low = 0.5 * (1.0 + bend)
    gelu = gate * low
    slope = low + 0.5 * gate * (1.0 - bend * bend) * (scale * (1.0 + 3.0 * 0.044715 * square))
    return (gelu * up).astype(BF16), (slope * up).astype(BF16), gelu.astype(BF16)


def tables(length, size):
    half_size = size // 2
    frequency = 10000.0 ** (-2.0 * jnp.arange(half_size, dtype=F32) / size)
    angles = jnp.arange(length, dtype=F32)[:, None] * frequency[None, :]
    return (jnp.cos(angles)[:, None, :], jnp.sin(angles)[:, None, :])


def rotate(values, cosine, sine):
    half_size = values.shape[-1] // 2
    first_half = values[..., :half_size]
    second_half = values[..., half_size:]
    return jnp.concatenate(
        [first_half * cosine - second_half * sine, second_half * cosine + first_half * sine],
        axis=-1,
    )


def nn(a, b):
    return lax.dot_general(a, b, (((1,), (0,)), ((), ())), preferred_element_type=F32)


def nt(a, b):
    return lax.dot_general(a, b, (((1,), (1,)), ((), ())), preferred_element_type=F32)


def tn(a, b):
    return lax.dot_general(a, b, (((0,), (0,)), ((), ())), preferred_element_type=F32)


def pad_lanes(values):
    return jnp.pad(values, [(0, 0)] * (values.ndim - 1) + [(0, LANES - values.shape[-1])])


QUERY, KEY, VALUE, GATE, UP, OUT, DOWN = (
    slice(i * RANK, (i + 1) * RANK) for i in range(7)
)


def band(values, first, last=None):
    lane = lax.broadcasted_iota(jnp.int32, values.shape, 1)
    keep = (lane >= first.start) & (lane < (last or first).stop)
    return jnp.where(keep, values, 0.0)


def lanes(*parts):
    pieces, at = [], 0
    for place, values in parts:
        if place.start > at:
            pieces.append(jnp.zeros(values.shape[:-1] + (place.start - at,), values.dtype))
        pieces.append(values)
        at = place.start + values.shape[-1]
    last = parts[-1][1]
    pieces.append(jnp.zeros(last.shape[:-1] + (LANES - at,), last.dtype))
    return jnp.concatenate(pieces, axis=-1)


def call(peers):
    barrier = pltpu.get_barrier_semaphore()
    for peer in peers:
        pl.semaphore_signal(barrier, inc=1, device_id=peer, device_id_type=MESH)


def greet(peers):
    call(peers)
    pl.semaphore_wait(pltpu.get_barrier_semaphore(), len(peers))


def square_peers(index):
    return index + 1 - 2 * lax.rem(index, 2), lax.rem(index + 2, 4), 3 - index


def remote(source, target, send_sem, recv_sem, peer):
    return pltpu.make_async_remote_copy(
        src_ref=source,
        dst_ref=target,
        send_sem=send_sem,
        recv_sem=recv_sem,
        device_id={"tensor": peer},
        device_id_type=MESH,
    )


class PlainGather:
    def __init__(self, me, x_ref, o_ref, local_sem, send_sem, recv_sem):
        rows = x_ref.shape[0]
        half = rows // 2
        links = square_peers(me)[:2]
        self.own = pltpu.make_async_copy(x_ref, o_ref.at[pl.ds(me * rows, rows)], local_sem)
        self.first, self.second, self.onward = [], [], []
        for order, group in enumerate((self.first, self.second)):
            for link in range(2):
                part = link if order == 0 else 1 - link
                group.append(
                    remote(
                        x_ref.at[pl.ds(part * half, half)],
                        o_ref.at[pl.ds(me * rows + part * half, half)],
                        send_sem.at[link, part],
                        recv_sem.at[link, part],
                        links[link],
                    )
                )
        for link in range(2):
            block = o_ref.at[pl.ds(links[link] * rows + link * half, half)]
            self.onward.append(
                remote(block, block, send_sem.at[2, link], recv_sem.at[2, link], links[1 - link])
            )

    def start(self):
        self.own.start()
        for copy in self.first + self.second:
            copy.start()

    def forward(self):
        for copy, onward in zip(self.first, self.onward):
            copy.wait_recv()
            onward.start()

    def finish(self):
        for copy in self.second + self.onward:
            copy.wait_recv()
        self.own.wait()
        for copy in self.first + self.second + self.onward:
            copy.wait_send()


def gather_kernel(count, rows, x_ref, o_ref, local_sem, send_sem, recv_sem):
    me = lax.axis_index("tensor")
    if count == 4:
        across, down, _ = square_peers(me)
        greet([{"tensor": across}, {"tensor": down}])
        gather = PlainGather(me, x_ref, o_ref, local_sem, send_sem, recv_sem)
        gather.start()
        gather.forward()
        gather.finish()
    else:
        peers = [lax.rem(me + step, count) for step in range(1, count)]
        greet([{"tensor": peer} for peer in peers])
        own = pltpu.make_async_copy(x_ref, o_ref.at[pl.ds(me * rows, rows)], local_sem)
        own.start()
        copies = []
        for step, peer in enumerate(peers):
            copy = remote(
                x_ref,
                o_ref.at[pl.ds(me * rows, rows)],
                send_sem.at[0, step],
                recv_sem.at[0, step],
                peer,
            )
            copy.start()
            copies.append(copy)
        own.wait()
        for copy in copies:
            copy.wait()


def tensor_gather(values, count):
    rows, width = values.shape
    slots = max(2, count - 1)
    return pl.pallas_call(
        functools.partial(gather_kernel, count, rows),
        out_shape=jax.ShapeDtypeStruct((count * rows, width), values.dtype),
        in_specs=[pl.BlockSpec(memory_space=pl.ANY)],
        out_specs=pl.BlockSpec(memory_space=pl.ANY),
        scratch_shapes=[
            pltpu.SemaphoreType.DMA,
            pltpu.SemaphoreType.DMA((3, slots)),
            pltpu.SemaphoreType.DMA((3, slots)),
        ],
        compiler_params=pltpu.CompilerParams(
            collective_id=1, has_side_effects=True, vmem_limit_bytes=VMEM_LIMIT
        ),
        name="tensor_gather",
    )(values)


def scatter_kernel(count, rows, p_ref, q_ref, o_ref, l_ref, *scratch):
    me = lax.axis_index("tensor")
    payload = ((p_ref, o_ref), (q_ref, l_ref))
    if count == 4:
        across, down, far = square_peers(me)
        greet([{"tensor": across}, {"tensor": down}])
        half = rows // 2
        first = scratch[0:2]
        sums = scratch[2:4]
        second = scratch[4:6]
        send_sem, recv_sem = scratch[6], scratch[7]
        links = (across, down)
        copies = {}
        for which in (1, 0):
            for link in range(2):
                block = far if which == 1 else links[link]
                for item in range(2):
                    copy = remote(
                        payload[item][0].at[pl.ds(block * rows + link * half, half)],
                        first[item].at[link, which],
                        send_sem.at[item, link, which],
                        recv_sem.at[item, link, which],
                        links[link],
                    )
                    copy.start()
                    copies[item, link, which] = copy
        for link in range(2):
            block = links[1 - link]
            for item in range(2):
                copies[item, link, 1].wait_recv()
                mine = payload[item][0][pl.ds(block * rows + link * half, half), :]
                sums[item][link] = (
                    mine.astype(F32) + first[item][link, 1].astype(F32)
                ).astype(BF16)
                copy = remote(
                    sums[item].at[link],
                    second[item].at[link],
                    send_sem.at[item, link, 2],
                    recv_sem.at[item, link, 2],
                    links[1 - link],
                )
                copy.start()
                copies[item, link, 2] = copy
        for link in range(2):
            for item in range(2):
                copies[item, link, 0].wait_recv()
                mine = payload[item][0][pl.ds(me * rows + link * half, half), :]
                payload[item][1][pl.ds(link * half, half), :] = mine.astype(F32) + first[item][
                    link, 0
                ].astype(F32)
        for link in range(2):
            for item in range(2):
                copies[item, link, 2].wait_recv()
                payload[item][1][pl.ds(link * half, half), :] += second[item][link].astype(F32)
        for copy in copies.values():
            copy.wait_send()
    else:
        peers = [lax.rem(me + step, count) for step in range(1, count)]
        greet([{"tensor": peer} for peer in peers])
        first = scratch[0:2]
        send_sem, recv_sem = scratch[2], scratch[3]
        copies = []
        for step, peer in enumerate(peers):
            for item in range(2):
                copy = remote(
                    payload[item][0].at[pl.ds(peer * rows, rows)],
                    first[item].at[step],
                    send_sem.at[item, step],
                    recv_sem.at[item, step],
                    peer,
                )
                copy.start()
                copies.append((item, step, copy))
        for item in range(2):
            payload[item][1][...] = payload[item][0][pl.ds(me * rows, rows), :].astype(F32)
        for item, step, copy in copies:
            copy.wait()
            payload[item][1][...] += first[item][step].astype(F32)


def tensor_scatter(values, narrow, count):
    rows = values.shape[0] // count
    widths = (values.shape[1], narrow.shape[1])
    if count == 4:
        half = rows // 2
        scratch = [pltpu.VMEM((2, 2, half, width), BF16) for width in widths]
        scratch += [pltpu.VMEM((2, half, width), BF16) for width in widths]
        scratch += [pltpu.VMEM((2, half, width), BF16) for width in widths]
        scratch += [pltpu.SemaphoreType.DMA((2, 2, 3)), pltpu.SemaphoreType.DMA((2, 2, 3))]
    else:
        scratch = [pltpu.VMEM((count - 1, rows, width), BF16) for width in widths]
        scratch += [pltpu.SemaphoreType.DMA((2, count - 1))] * 2
    vmem = pl.BlockSpec(memory_space=pltpu.VMEM)
    return pl.pallas_call(
        functools.partial(scatter_kernel, count, rows),
        out_shape=tuple(jax.ShapeDtypeStruct((rows, width), F32) for width in widths),
        in_specs=[vmem, vmem],
        out_specs=(vmem, vmem),
        scratch_shapes=scratch,
        compiler_params=pltpu.CompilerParams(
            collective_id=2, has_side_effects=True, vmem_limit_bytes=VMEM_LIMIT
        ),
        name="tensor_scatter",
    )(values, narrow)


class Square:
    def __init__(self, rows):
        self.rows = rows
        self.half = rows // 2
        self.me = lax.axis_index("tensor")
        self.across, self.down, self.far = square_peers(self.me)
        self.links = (self.across, self.down)

    def greet(self, far=False):
        greet([{"tensor": peer} for peer in (self.across, self.down) + ((self.far,) if far else ())])

    def spread(self, source_at, target, send_sem, recv_sem):
        copies = [pltpu.make_async_copy(source_at(self.me), target.at[self.me], recv_sem.at[0])]
        for which, peer in enumerate((self.across, self.down, self.far)):
            copies.append(
                remote(
                    source_at(peer),
                    target.at[self.me],
                    send_sem.at[which],
                    recv_sem.at[1 + which],
                    peer,
                )
            )
        return copies


def along(source_at, target, send_sem, recv_sem):
    dp = lax.axis_size("dp")
    d = lax.axis_index("dp")
    pltpu.make_async_copy(source_at(d), target.at[d], recv_sem).start()
    copies = []
    for step in range(1, dp):
        peer = lax.rem(d + step, dp)
        copy = pltpu.make_async_remote_copy(
            src_ref=source_at(peer),
            dst_ref=target.at[d],
            send_sem=send_sem.at[step],
            recv_sem=recv_sem,
            device_id={"dp": peer},
            device_id_type=MESH,
        )
        copy.start()
        copies.append(copy)
    return copies


class ChunkGather:
    def __init__(self, sq, source, buf, send_sem, recv_sem):
        half = sq.half
        self.first, self.second, self.onward = [], [], []
        for link in range(2):
            for order in range(2):
                part = link if order == 0 else 1 - link
                copy = remote(
                    source.at[pl.ds(part * half, half)],
                    buf.at[1 + order, pl.ds(link * half, half)],
                    send_sem.at[2 * order + link],
                    recv_sem.at[2 * order + link],
                    sq.links[link],
                )
                (self.first if order == 0 else self.second).append(copy)
            self.onward.append(
                remote(
                    buf.at[1, pl.ds(link * half, half)],
                    buf.at[3, pl.ds(link * half, half)],
                    send_sem.at[4 + link],
                    recv_sem.at[4 + link],
                    sq.links[1 - link],
                )
            )

    def start(self):
        for copy in self.first + self.second:
            copy.start()

    def wait_chunk(self, chunk):
        if chunk == 1:
            for copy in self.first:
                copy.wait_recv()
            for copy in self.onward:
                copy.start()
        if chunk == 2:
            for copy in self.second:
                copy.wait_recv()
        if chunk == 3:
            for copy in self.onward:
                copy.wait_recv()

    def finish(self):
        for copy in self.first + self.second + self.onward:
            copy.wait_send()


class ChunkScatter:
    def __init__(self, sq, part, landing, passed, send_sem, recv_sem):
        self.sq, self.half = sq, sq.half
        self.part, self.landing, self.passed = part, landing, passed
        self.send_sem, self.recv_sem = send_sem, recv_sem

    def copy(self, kind, link):
        rows = pl.ds(link * self.half, self.half)
        source = (
            self.passed.at[link] if kind == 2 else self.part.at[1 + 2 * kind, rows]
        )
        slot = 2 * kind + link
        return remote(
            source,
            self.landing.at[slot],
            self.send_sem.at[slot],
            self.recv_sem.at[slot],
            self.sq.links[1 - link if kind == 2 else link],
        )

    def send_own(self):
        for link in range(2):
            self.copy(0, link).start()

    def send_far(self):
        for link in range(2):
            self.copy(1, link).start()

    def pass_on(self, link):
        self.copy(1, link).wait_recv()
        rows = pl.ds((1 - link) * self.half, self.half)
        mine = self.part[2, rows, :].astype(F32)
        self.passed[link] = (mine + self.landing[2 + link].astype(F32)).astype(BF16)
        self.copy(2, link).start()

    def collect(self, out_ref, first=0):
        for link in range(2):
            self.copy(0, link).wait_recv()
            self.copy(2, link).wait_recv()
            rows = pl.ds(link * self.half, self.half)
            out_ref[rows, first : first + self.part.shape[-1]] = (
                self.part[0, rows, :].astype(F32)
                + self.landing[link].astype(F32)
                + self.landing[4 + link].astype(F32)
            )

    def finish(self):
        for kind in range(3):
            for link in range(2):
                self.copy(kind, link).wait_send()


def scatter_scratch(rows, width):
    half = rows // 2
    return [
        pltpu.VMEM((4, rows, width), BF16),
        pltpu.VMEM((6, half, width), BF16),
        pltpu.VMEM((2, half, width), BF16),
        pltpu.SemaphoreType.DMA((6,)),
        pltpu.SemaphoreType.DMA((6,)),
    ]


def tile_of(width):
    return 768 if width % 768 == 0 else 384


def columns(step, tile, base=0):
    return pl.ds(pl.multiple_of(base + step * tile, LANES), tile)


def mlp_back_kernel(
    rows,
    g_ref,
    down_hbm,
    gu_hbm,
    slope_hbm,
    gelu_hbm,
    hidden_hbm,
    low_hbm,
    d_ref,
    f_table,
    o_ref,
    l_ref,
    f_out,
    f_ref,
    f_send,
    down_w,
    gu_w,
    buf,
    slope,
    gelu,
    hidden,
    low,
    grads,
    weight_sem,
    load_sem,
    own_sem,
    gather_send,
    gather_recv,
    spread_send,
    spread_recv,
    *scratch,
):
    sq = Square(rows)
    width = hidden.shape[-1]
    model = o_ref.shape[-1]
    down_load = pltpu.make_async_copy(down_hbm, down_w, weight_sem.at[0])
    gu_load = pltpu.make_async_copy(gu_hbm, gu_w, weight_sem.at[1])
    own_load = pltpu.make_async_copy(g_ref, buf.at[0], own_sem)

    def loads(chunk):
        slot = chunk % 2
        return [
            pltpu.make_async_copy(source.at[chunk], target.at[slot], load_sem.at[slot, item])
            for item, (source, target) in enumerate(
                ((slope_hbm, slope), (gelu_hbm, gelu), (hidden_hbm, hidden), (low_hbm, low))
            )
        ]

    down_load.start()
    own_load.start()
    for copy in loads(0):
        copy.start()
    sq.greet(far=True)
    gather = ChunkGather(sq, g_ref, buf, gather_send, gather_recv)
    gather.start()
    gu_load.start()
    part, part_low = scratch[0], scratch[5]
    scatters = (ChunkScatter(sq, *scratch[:5]), ChunkScatter(sq, *scratch[5:10]))
    f_ref[...] = jnp.zeros_like(f_ref)
    own_load.wait()
    down_load.wait()

    @pl.loop(0, 4)
    def _(chunk):
        slot = lax.rem(chunk, 2)
        for step in range(4):

            @pl.when(chunk == step)
            def _(step=step):
                gather.wait_chunk(step)
                for copy in loads(step):
                    copy.wait()
                if step < 3:
                    for copy in loads(step + 1):
                        copy.start()

        incoming = buf.at[chunk]
        low_down = band(nn(incoming[...], d_ref[...]), DOWN).astype(BF16)
        tile = tile_of(width)

        @pl.loop(0, width // tile)
        def _(step):
            here = columns(step, tile)
            grad = nn(incoming[...], down_w[:, here]) + nt(low_down, f_table[here, :])
            grads[:, here] = (grad * slope[slot, :, here].astype(F32)).astype(BF16)
            grads[:, columns(step, tile, width)] = (
                grad * gelu[slot, :, here].astype(F32)
            ).astype(BF16)

        @pl.when(chunk == 0)
        def _():
            gu_load.wait()

        part_low[chunk] = (
            band(nn(grads[:, :width], f_table[...]), GATE)
            + band(nn(grads[:, width:], f_table[...]), UP)
        ).astype(BF16)
        wide = tile_of(model)

        @pl.loop(0, model // wide)
        def _(step):
            here = columns(step, wide)
            part[chunk, :, here] = nt(grads[...], gu_w[here, :]).astype(BF16)

        @pl.when(chunk == 1)
        def _():
            for scatter in scatters:
                scatter.send_own()

        @pl.when(chunk == 3)
        def _():
            for scatter in scatters:
                scatter.send_far()

        low_turned = low_down.astype(F32).T.astype(BF16)
        gu_turned = low[slot].astype(F32).T.astype(BF16)
        f_ref[:RANK, :] += nn(low_turned[DOWN], hidden[slot])
        f_ref[RANK : 2 * RANK, :] += nn(gu_turned[GATE], grads[:, :width])
        f_ref[2 * RANK : 3 * RANK, :] += nn(gu_turned[UP], grads[:, width:])

    cores, slices = f_send.shape[:2]
    size = width // (cores * slices)
    for core in range(cores):
        for peer in range(slices):
            first = (core * slices + peer) * size
            f_send[core, peer] = f_ref[: 3 * RANK, first : first + size].astype(BF16)
    spread = sq.spread(lambda peer: f_send.at[:, peer], f_out, spread_send, spread_recv)
    for copy in spread:
        copy.start()
    for link in range(2):
        for scatter in scatters:
            scatter.pass_on(link)
    gather.finish()
    scatters[0].collect(o_ref)
    scatters[1].collect(l_ref)
    for scatter in scatters:
        scatter.finish()
    for copy in spread:
        copy.wait()


def mlp_back_fused(grad, down_w, gu_w, slope, gelu, hidden, low, d_tab, f_tab, dp):
    rows, model = grad.shape
    width = hidden.shape[2]
    messages = (dp // 4, 4, 3 * RANK, width // dp)
    anywhere = pl.BlockSpec(memory_space=pl.ANY)
    vmem = pl.BlockSpec(memory_space=pltpu.VMEM)
    return pl.pallas_call(
        functools.partial(mlp_back_kernel, rows),
        out_shape=(
            jax.ShapeDtypeStruct((rows, model), F32),
            jax.ShapeDtypeStruct((rows, LANES), F32),
            jax.ShapeDtypeStruct((4, dp // 4, 3 * RANK, width // dp), BF16),
        ),
        in_specs=[vmem] + [anywhere] * 6 + [vmem] * 2,
        out_specs=(vmem,) * 3,
        scratch_shapes=[
            pltpu.VMEM((3 * RANK, width), F32),
            pltpu.VMEM(messages, BF16),
            pltpu.VMEM((model, width), BF16),
            pltpu.VMEM((model, 2 * width), BF16),
            pltpu.VMEM((4, rows, model), BF16),
            pltpu.VMEM((2, rows, width), BF16),
            pltpu.VMEM((2, rows, width), BF16),
            pltpu.VMEM((2, rows, width), BF16),
            pltpu.VMEM((2, rows, LANES), BF16),
            pltpu.VMEM((rows, 2 * width), BF16),
            pltpu.SemaphoreType.DMA((2,)),
            pltpu.SemaphoreType.DMA((2, 4)),
            pltpu.SemaphoreType.DMA,
            pltpu.SemaphoreType.DMA((6,)),
            pltpu.SemaphoreType.DMA((6,)),
            pltpu.SemaphoreType.DMA((3,)),
            pltpu.SemaphoreType.DMA((4,)),
        ]
        + scatter_scratch(rows, model)
        + scatter_scratch(rows, LANES),
        compiler_params=pltpu.CompilerParams(
            collective_id=5, has_side_effects=True, vmem_limit_bytes=62 * 1024 * 1024
        ),
        name="mlp_back",
    )(grad, down_w, gu_w, slope, gelu, hidden, low, d_tab, f_tab)


def front_kernel(
    ids_ref,
    layer_ref,
    gains_ref,
    f_all,
    d_all,
    hk_all,
    seq_out,
    ids_out,
    d_out,
    f_out,
    h_out,
    k_out,
    normed,
    ids_land,
    f_pick,
    d_pick,
    hk_pick,
    f_mid,
    d_mid,
    hk_mid,
    d_join,
    f_land,
    d_land,
    hk_land,
    d_flip,
    f_flip,
    h_flip,
    k_flip,
    local_sem,
    gather_send,
    gather_recv,
    line_send,
    line_recv,
    group_send,
    group_recv,
):
    rows = layer_ref.shape[0]
    sq = Square(rows)
    dp = lax.axis_size("dp")
    d = lax.axis_index("dp")
    peers = [{"tensor": peer} for peer in (sq.across, sq.down, sq.far)]
    peers += [{"dp": lax.rem(d + step, dp)} for step in range(1, dp)]
    call(peers)

    @pl.loop(0, rows // BLOCK)
    def _(step):
        here = pl.ds(pl.multiple_of(step * BLOCK, BLOCK), BLOCK)
        normed[here, :] = rms_norm(layer_ref[here, :].astype(F32), gains_ref[0:1, :]).astype(BF16)

    pl.semaphore_wait(pltpu.get_barrier_semaphore(), len(peers))
    line = along(lambda k: ids_ref, ids_land, line_send.at[0], line_recv.at[0])
    gather = PlainGather(sq.me, normed, seq_out, local_sem, gather_send, gather_recv)
    gather.start()
    pltpu.make_async_copy(ids_land, ids_land, line_recv.at[0]).wait()
    ids_out[...] = ids_land[...]

    @pl.loop(0, dp)
    def _(k):
        for source, target in ((f_all, f_pick), (d_all, d_pick), (hk_all, hk_pick)):
            total = None
            for adapter in range(NA):
                hit = jnp.broadcast_to(ids_land[k, 0:1, 0:1], source.shape[1:]) == adapter
                mine = jnp.where(hit, source[adapter].astype(F32), 0.0)
                total = mine if total is None else total + mine
            target[k] = total.astype(BF16)

    lands = (f_mid, d_mid, hk_mid)
    for item, (source, target) in enumerate(zip((f_pick, d_pick, hk_pick), lands)):
        line += along(
            lambda k, source=source: source.at[k],
            target,
            line_send.at[1 + item],
            line_recv.at[1 + item],
        )
    gather.forward()
    for flip in (d_flip, f_flip, h_flip, k_flip):
        flip[...] = jnp.zeros_like(flip)
    for item, target in enumerate(lands):
        pltpu.make_async_copy(target, target, line_recv.at[1 + item]).wait()
    size = d_mid.shape[2]
    for k in range(dp):
        d_join[:, k * size : (k + 1) * size] = d_mid[k]
    per_user = dp // 4
    spread = [
        sq.spread(lambda peer: d_join, d_land, group_send.at[0], group_recv.at[0]),
        sq.spread(
            lambda peer: f_mid.at[pl.ds(peer * per_user, per_user)],
            f_land,
            group_send.at[1],
            group_recv.at[1],
        ),
        sq.spread(
            lambda peer: hk_mid.at[pl.ds(peer * per_user, per_user)],
            hk_land,
            group_send.at[2],
            group_recv.at[2],
        ),
    ]
    for copies in spread:
        for copy in copies:
            copy.start()
    for copies in spread:
        copies[0].wait()
        for copy in copies[1:]:
            copy.wait_recv()
    f_size, h_size, k_size = f_mid.shape[2], h_out.shape[0] // dp, k_out.shape[0] // dp
    for t in range(4):
        for k in range(dp):
            at = (k * 4 + t) * size
            d_flip[: DOWN.stop, at : at + size] = d_land[
                t, :, k * size : (k + 1) * size
            ].astype(F32)
        for core in range(per_user):
            at = (core * 4 + t) * f_size
            piece = f_land[t, core].astype(F32)
            f_flip[GATE.start : UP.stop, at : at + f_size] = piece[: 2 * RANK]
            f_flip[DOWN, at : at + f_size] = piece[2 * RANK :]
            piece = hk_land[t, core].astype(F32)
            at = (core * 4 + t) * h_size
            h_flip[OUT, at : at + h_size] = piece[:RANK, :h_size]
            h_flip[QUERY, at : at + h_size] = piece[RANK : 2 * RANK, :h_size]
            at = (core * 4 + t) * k_size
            k_flip[KEY.start : VALUE.stop, at : at + k_size] = piece[2 * RANK :, :k_size]
    for flip, out in ((d_flip, d_out), (f_flip, f_out), (h_flip, h_out), (k_flip, k_out)):

        @pl.loop(0, out.shape[0] // LANES)
        def _(step, flip=flip, out=out):
            here = columns(step, LANES)
            out[here, :] = flip[:, here].T.astype(BF16)

    gather.finish()
    for copies in spread:
        for copy in copies[1:]:
            copy.wait_send()
    for copy in line:
        copy.wait_send()


def front(ids, layer_in, gains, f_all, d_all, hk_all, dp, widths):
    rows, model = layer_in.shape
    anywhere = pl.BlockSpec(memory_space=pl.ANY)
    vmem = pl.BlockSpec(memory_space=pltpu.VMEM)
    tables_in = (f_all, d_all, hk_all)
    shapes = [(dp,) + table.shape[1:] for table in tables_in]
    joined = (shapes[1][1], dp * shapes[1][2])
    return pl.pallas_call(
        front_kernel,
        out_shape=(
            jax.ShapeDtypeStruct((4 * rows, model), BF16),
            jax.ShapeDtypeStruct((dp,) + ids.shape, jnp.int32),
        )
        + tuple(jax.ShapeDtypeStruct((width, LANES), BF16) for width in widths),
        in_specs=[vmem] * 6,
        out_specs=(anywhere,) + (vmem,) * 5,
        scratch_shapes=[
            pltpu.VMEM((rows, model), BF16),
            pltpu.VMEM((dp,) + ids.shape, jnp.int32),
        ]
        + [pltpu.VMEM(shape, BF16) for shape in shapes] * 2
        + [
            pltpu.VMEM(joined, BF16),
            pltpu.VMEM((4, dp // 4) + shapes[0][1:], BF16),
            pltpu.VMEM((4,) + joined, BF16),
            pltpu.VMEM((4, dp // 4) + shapes[2][1:], BF16),
        ]
        + [pltpu.VMEM((LANES, width), F32) for width in widths]
        + [
            pltpu.SemaphoreType.DMA,
            pltpu.SemaphoreType.DMA((3, 2)),
            pltpu.SemaphoreType.DMA((3, 2)),
            pltpu.SemaphoreType.DMA((4, dp)),
            pltpu.SemaphoreType.DMA((4,)),
            pltpu.SemaphoreType.DMA((3, 3)),
            pltpu.SemaphoreType.DMA((3, 4)),
        ],
        compiler_params=pltpu.CompilerParams(
            collective_id=9, has_side_effects=True, vmem_limit_bytes=VMEM_LIMIT
        ),
        name="front",
    )(ids, layer_in, gains, *tables_in)


class Line:
    def __init__(self, slots, send_sem, recv_sem):
        self.d = lax.axis_index("dp")
        self.places = lax.axis_size("dp") // 2
        self.core = lax.rem(self.d, 2)
        self.z = self.d // 2
        self.sibling = self.d + 1 - 2 * self.core
        self.slots, self.send_sem, self.recv_sem = slots, send_sem, recv_sem

    def greet(self, others):
        barrier = pltpu.get_barrier_semaphore()
        for peer in others + [{"dp": self.sibling}]:
            pl.semaphore_signal(barrier, inc=1, device_id=peer, device_id_type=MESH)

        @pl.when(self.z > 0)
        def _():
            pl.semaphore_signal(
                barrier, inc=1, device_id={"dp": self.d - 2}, device_id_type=MESH
            )

        @pl.when(self.z < self.places - 1)
        def _():
            pl.semaphore_signal(
                barrier, inc=1, device_id={"dp": self.d + 2}, device_id_type=MESH
            )

        last = self.places - 1
        ends = (last - self.z) // last + self.z // last
        pl.semaphore_wait(barrier, len(others) + 3 - ends)

    def copy(self, place, kind):
        target = (self.d + 2, self.d - 2, self.sibling)[kind]
        slot = 2 * place + self.core
        return pltpu.make_async_remote_copy(
            src_ref=self.slots.at[slot],
            dst_ref=self.slots.at[slot],
            send_sem=self.send_sem.at[kind, place],
            recv_sem=self.recv_sem.at[slot],
            device_id={"dp": target},
            device_id_type=MESH,
        )

    def send_up(self, place):
        @pl.when(self.z < self.places - 1)
        def _():
            self.copy(place, 0).start()

    def send_down(self, place):
        @pl.when(self.z > 0)
        def _():
            self.copy(place, 1).start()

    def start(self):
        self.send_up(self.z)
        self.send_down(self.z)
        self.copy(self.z, 2).start()

    def arrive(self, distance):
        @pl.when(self.z >= distance)
        def _():
            place = self.z - distance
            self.copy(place, 2).wait_recv()
            self.send_up(place)
            self.copy(place, 2).start()

        @pl.when(self.z + distance < self.places)
        def _():
            place = self.z + distance
            self.copy(place, 2).wait_recv()
            self.send_down(place)
            self.copy(place, 2).start()

    def wait_sibling(self, place):
        slot = self.slots.at[2 * place + 1 - self.core]
        pltpu.make_async_copy(
            slot, slot, self.recv_sem.at[2 * place + 1 - self.core]
        ).wait()

    def finish(self):
        for place in range(self.places):

            @pl.when((self.z >= place) & (self.z < self.places - 1))
            def _(place=place):
                self.copy(place, 0).wait_send()

            @pl.when((self.z <= place) & (self.z > 0))
            def _(place=place):
                self.copy(place, 1).wait_send()

            self.copy(place, 2).wait_send()


ARRIVALS = ((0, 1, 2, 3), (1, 0, 2, 3), (2, 1, 3, 0), (3, 2, 1, 0))


def mlp_kernel(
    rows,
    length_ref,
    x_hbm,
    gu_hbm,
    shard_hbm,
    d_ref,
    f_table,
    resid_ref,
    cot_ref,
    gains_ref,
    layer_ref,
    grad_ref,
    low_ref,
    low_down_ref,
    hidden_out,
    slope_out,
    gelu_out,
    down_out,
    work,
    low_sum,
    lows,
    seq,
    tiles,
    hidden,
    slope,
    gelu,
    down,
    load_sem,
    tile_sem,
    store_sem,
    keep_sem,
    line_send,
    line_recv,
    part,
    landing,
    passed,
    part_send,
    part_recv,
    *low_scratch,
):
    sq = Square(rows)
    line = Line(down, line_send, line_recv)
    width = hidden.shape[-1]
    tile = tiles.shape[-1] // 2
    steps = width // tile
    own_shard = pltpu.make_async_copy(shard_hbm, down.at[line.d], load_sem.at[0])
    seq_load = pltpu.make_async_copy(x_hbm, seq, load_sem.at[1])

    def tile_loads(step, slot):
        return [
            pltpu.make_async_copy(
                gu_hbm.at[:, columns(step, tile, which * width)],
                tiles.at[slot, :, pl.ds(which * tile, tile)],
                tile_sem.at[slot, which],
            )
            for which in range(2)
        ]

    def stores(step, slot):
        here = columns(step, tile)
        return [
            pltpu.make_async_copy(
                source.at[slot], target.at[:, :, here], store_sem.at[slot, which]
            )
            for which, (source, target) in enumerate(((slope, slope_out), (gelu, gelu_out)))
        ]

    own_shard.start()
    seq_load.start()
    for copy in tile_loads(0, 0):
        copy.start()
    line.greet([{"tensor": sq.across}, {"tensor": sq.down}])
    own_shard.wait()
    line.start()
    seq_load.wait()

    @pl.loop(0, 4)
    def _(chunk):
        low = nn(seq[chunk], d_ref[...])
        lows[0, chunk] = band(low, GATE).astype(BF16)
        lows[1, chunk] = band(low, UP).astype(BF16)
        low_ref[chunk] = band(low, GATE, UP).astype(BF16)

    @pl.loop(0, steps)
    def _(step):
        slot = lax.rem(step, 2)
        for copy in tile_loads(step, slot):
            copy.wait()

        @pl.when(step + 1 < steps)
        def _():
            for copy in tile_loads(step + 1, 1 - slot):
                copy.start()

        @pl.when(step >= 2)
        def _():
            for copy in stores(step - 2, slot):
                copy.wait()

        here = columns(step, tile)

        @pl.loop(0, 4)
        def _(chunk):
            both = nn(seq[chunk], tiles[slot])
            gate = both[:, :tile] + nt(lows[0, chunk], f_table[here, :])
            up = both[:, tile:] + nt(lows[1, chunk], f_table[here, :])
            hidden[chunk, :, here], slope[slot, chunk], gelu[slot, chunk] = gelu_parts(gate, up)

        for copy in stores(step, slot):
            copy.start()

        @pl.when(step == steps - 2)
        def _():
            line.arrive(1)

    keep_hidden = pltpu.make_async_copy(hidden, hidden_out, keep_sem.at[0])
    keep_hidden.start()
    last = line.places - 1
    is_first, is_last = (last - line.z) // last, line.z // last
    is_third = line.z // 2 - is_last
    is_here = (is_first, 1 - is_first - is_third - is_last, is_third, is_last)
    order = [sum(flag * ARRIVALS[z][i] for z, flag in enumerate(is_here)) for i in range(4)]

    def scatter_at(place):
        return ChunkScatter(
            sq,
            part.at[place],
            landing.at[place],
            passed.at[place],
            part_send.at[place],
            part_recv.at[place],
        )

    low_scatter = ChunkScatter(sq, *low_scratch)

    @pl.loop(0, 4)
    def _(chunk):
        low_scratch[0][chunk] = band(nn(hidden[chunk], f_table[...]), DOWN).astype(BF16)

    low_scatter.send_far()
    low_scatter.send_own()
    keeps = []
    for step in range(4):
        if step >= 2:
            line.arrive(step)
        place = order[step]
        line.wait_sibling(place)
        pair = pl.ds(2 * place, 2)
        keep = pltpu.make_async_copy(down.at[pair], down_out.at[pair], keep_sem.at[1 + step])
        keep.start()
        keeps.append(keep)
        scatter = scatter_at(place)
        shard_rows = down.shape[1]

        @pl.loop(0, 4)
        def _(turn, place=place, scatter=scatter):
            chunk = turn + 3 * ((3 - turn) // 3) - 3 * (turn // 3)
            for core in range(2):
                part[place, chunk, :, core * shard_rows : (core + 1) * shard_rows] = nt(
                    hidden[chunk], down[2 * place + core]
                ).astype(BF16)

            @pl.when(turn == 0)
            def _():
                scatter.send_far()

            @pl.when(turn == 1)
            def _():
                scatter.send_own()

        if step > 0:
            for link in range(2):
                scatter_at(order[step - 1]).pass_on(link)
        else:
            for link in range(2):
                low_scatter.pass_on(link)
    for link in range(2):
        scatter_at(order[3]).pass_on(link)
    wide = part.shape[-1]
    low_scatter.collect(low_sum)
    low_down_ref[...] = low_sum[...].astype(BF16)
    for place in range(4):
        scatter_at(place).collect(work, place * wide)
    add_lifted(work, low_down_ref, d_ref)

    @pl.loop(0, rows // BLOCK)
    def _(step):
        here = pl.ds(pl.multiple_of(step * BLOCK, BLOCK), BLOCK)
        at = sq.me * rows + step * BLOCK + lax.broadcasted_iota(jnp.int32, (BLOCK, 1), 0)
        valid = (at < length_ref[0]).astype(F32)
        total = work[here, :]
        gain = gains_ref[3:4, :]
        layer_ref[here, :] = (valid * (resid_ref[here, :] + rms_norm(total, gain))).astype(BF16)
        grad_ref[here, :] = norm_back(total, gain, cot_ref[here, :].astype(F32) * valid).astype(
            BF16
        )

    for place in range(4):
        scatter_at(place).finish()
    low_scatter.finish()
    line.finish()
    for step in (steps - 2, steps - 1):
        for copy in stores(step, step % 2):
            copy.wait()
    keep_hidden.wait()
    for keep in keeps:
        keep.wait()


def add_lifted(work, low, table):
    wide = tile_of(work.shape[1])

    @pl.loop(0, work.shape[1] // wide)
    def _(step):
        here = columns(step, wide)
        work[:, here] += nt(low[...], table[here, :])


def mlp_fused(lengths, seq, gu_w, shard, d_tab, f_tab, resid, cotangent, gains, dp):
    chunks, rows, model = seq.shape
    width = shard.shape[1]
    tile = 384
    wide = model // (dp // 2)
    half = rows // 2
    anywhere = pl.BlockSpec(memory_space=pl.ANY)
    vmem = pl.BlockSpec(memory_space=pltpu.VMEM)
    saved = jax.ShapeDtypeStruct((4, rows, width), BF16)
    return pl.pallas_call(
        functools.partial(mlp_kernel, rows),
        out_shape=(
            jax.ShapeDtypeStruct((rows, model), BF16),
            jax.ShapeDtypeStruct((rows, model), BF16),
            jax.ShapeDtypeStruct((4, rows, LANES), BF16),
            jax.ShapeDtypeStruct((rows, LANES), BF16),
            saved,
            saved,
            saved,
            jax.ShapeDtypeStruct((dp,) + shard.shape, BF16),
        ),
        in_specs=[pl.BlockSpec(memory_space=pltpu.SMEM)] + [anywhere] * 3 + [vmem] * 5,
        out_specs=(vmem,) * 4 + (anywhere,) * 4,
        scratch_shapes=[
            pltpu.VMEM((rows, model), F32),
            pltpu.VMEM((rows, LANES), F32),
            pltpu.VMEM((2, 4, rows, LANES), BF16),
            pltpu.VMEM((4, rows, model), BF16),
            pltpu.VMEM((2, model, 2 * tile), BF16),
            pltpu.VMEM((4, rows, width), BF16),
            pltpu.VMEM((2, 4, rows, tile), BF16),
            pltpu.VMEM((2, 4, rows, tile), BF16),
            pltpu.VMEM((dp,) + shard.shape, BF16),
            pltpu.SemaphoreType.DMA((2,)),
            pltpu.SemaphoreType.DMA((2, 2)),
            pltpu.SemaphoreType.DMA((2, 2)),
            pltpu.SemaphoreType.DMA((5,)),
            pltpu.SemaphoreType.DMA((3, dp // 2)),
            pltpu.SemaphoreType.DMA((dp,)),
            pltpu.VMEM((4, 4, rows, wide), BF16),
            pltpu.VMEM((4, 6, half, wide), BF16),
            pltpu.VMEM((4, 2, half, wide), BF16),
            pltpu.SemaphoreType.DMA((4, 6)),
            pltpu.SemaphoreType.DMA((4, 6)),
        ]
        + scatter_scratch(rows, LANES),
        compiler_params=pltpu.CompilerParams(
            collective_id=7, has_side_effects=True, vmem_limit_bytes=62 * 1024 * 1024
        ),
        name="mlp",
    )(lengths, seq, gu_w, shard, d_tab, f_tab, resid, cotangent, gains)


class Layout:
    def __init__(self):
        self.dp = lax.axis_size("dp")
        self.tensor = lax.axis_size("tensor")
        self.total = self.dp * self.tensor
        self.d = lax.axis_index("dp")
        self.t = lax.axis_index("tensor")
        self.me = self.d * self.tensor + self.t
        self.heads_here = HQ // self.tensor
        self.ratio = HQ // KV
        self.share = max(1, self.tensor // KV)
        self.kv_owners = self.total // KV
        self.kv_head = self.t * self.heads_here // self.ratio
        self.user = self.me // self.dp
        self.kv_slice_head = self.me // self.kv_owners

    def device(self, flat):
        return {"dp": flat // self.tensor, "tensor": lax.rem(flat, self.tensor)}


def greet_all(lay):
    barrier = pltpu.get_barrier_semaphore()

    def signal(step, unused):
        peer = lax.rem(lay.me + step, lay.total)
        pl.semaphore_signal(
            barrier, inc=1, device_id=lay.device(peer), device_id_type=MESH
        )
        return unused

    lax.fori_loop(1, lay.total, signal, 0)
    pl.semaphore_wait(barrier, lay.total - 1)


def send_or_keep(lay, sends, source, target, send_sem, recv_sem, flat, maybe_own):
    def far():
        return pltpu.make_async_remote_copy(
            src_ref=source,
            dst_ref=target,
            send_sem=send_sem,
            recv_sem=recv_sem,
            device_id=lay.device(flat),
            device_id_type=MESH,
        )

    if maybe_own is None:
        copy = far()
        copy.start()
        sends.append((None, copy))
        return

    @pl.when(maybe_own)
    def _():
        pltpu.make_async_copy(source, target, recv_sem).start()

    @pl.when(jnp.logical_not(maybe_own))
    def _():
        far().start()

    sends.append((maybe_own, far()))


def finish(sends, received):
    for own, copy in sends:
        if own is None:
            copy.wait_send()
        else:

            @pl.when(jnp.logical_not(own))
            def _(copy=copy):
                copy.wait_send()

    for target, sem in received:
        pltpu.make_async_copy(target, target, sem).wait()


def tables_kernel(d_ref, f_ref, h_ref, k_ref, do_ref, fo_ref, ho_ref, ko_ref, *sems):
    lay = Layout()
    send_sems, recv_sem = sems[:4], sems[4]
    greet_all(lay)
    sends = []
    for step in range(lay.dp):
        group = lax.rem(lay.d + step, lay.dp)
        flat = group * lay.tensor + lay.user
        own = (lay.user == lay.t) if step == 0 else None
        for item, (source, target) in enumerate(((f_ref, fo_ref), (h_ref, ho_ref))):
            send_or_keep(
                lay,
                sends,
                source.at[group],
                target.at[lax.rem(lay.me, lay.dp)],
                send_sems[item].at[step],
                recv_sem.at[item],
                flat,
                own,
            )
        for extra in range(lay.share):
            user = lay.kv_slice_head * lay.share + extra
            flat = group * lay.tensor + user
            send_or_keep(
                lay,
                sends,
                k_ref.at[group],
                ko_ref.at[lax.rem(lay.me, lay.kv_owners)],
                send_sems[2].at[step, extra],
                recv_sem.at[2],
                flat,
                (user == lay.t) if step == 0 else None,
            )
    pltpu.make_async_copy(d_ref.at[lay.d], do_ref.at[lay.me], recv_sem.at[3]).start()
    for step in range(1, lay.total):
        flat = lax.rem(lay.me + step, lay.total)
        send_or_keep(
            lay,
            sends,
            d_ref.at[flat // lay.tensor],
            do_ref.at[lay.me],
            send_sems[3].at[step],
            recv_sem.at[3],
            flat,
            None,
        )
    finish(
        sends,
        (
            (fo_ref, recv_sem.at[0]),
            (ho_ref, recv_sem.at[1]),
            (ko_ref, recv_sem.at[2]),
            (do_ref, recv_sem.at[3]),
        ),
    )


def grads_kernel(d_ref, f_ref, h_ref, k_ref, do_ref, fo_ref, ho_ref, ko_ref, *sems):
    lay = Layout()
    send_sems, recv_sem = sems[:4], sems[4]
    greet_all(lay)
    sends = []
    for step in range(lay.dp):
        slot = lax.rem(lay.d + step, lay.dp)
        flat = lay.t * lay.dp + slot
        for item, (source, target) in enumerate(((f_ref, fo_ref), (h_ref, ho_ref))):
            send_or_keep(
                lay,
                sends,
                source.at[slot],
                target.at[lay.d],
                send_sems[item].at[step],
                recv_sem.at[item],
                flat,
                flat == lay.me,
            )
    for step in range(lay.kv_owners):
        slot = lax.rem(lay.d + step, lay.kv_owners)
        flat = lay.kv_head * lay.kv_owners + slot
        send_or_keep(
            lay,
            sends,
            k_ref.at[slot],
            ko_ref.at[lay.d * lay.share + lax.rem(lay.t, lay.share)],
            send_sems[2].at[step // lay.share, step % lay.share],
            recv_sem.at[2],
            flat,
            flat == lay.me,
        )
    pltpu.make_async_copy(d_ref.at[lay.me], do_ref.at[lay.me], recv_sem.at[3]).start()
    for step in range(1, lay.total):
        flat = lax.rem(lay.me + step, lay.total)
        send_or_keep(
            lay,
            sends,
            d_ref.at[flat],
            do_ref.at[lay.me],
            send_sems[3].at[step],
            recv_sem.at[3],
            flat,
            None,
        )
    finish(
        sends,
        (
            (fo_ref, recv_sem.at[0]),
            (ho_ref, recv_sem.at[1]),
            (ko_ref, recv_sem.at[2]),
            (do_ref, recv_sem.at[3]),
        ),
    )


def exchange(kernel, name, number, arrays, outs, dp, total, share):
    anywhere = pl.BlockSpec(memory_space=pl.ANY)
    return pl.pallas_call(
        kernel,
        out_shape=tuple(jax.ShapeDtypeStruct(shape, BF16) for shape in outs),
        in_specs=[anywhere] * 4,
        out_specs=(anywhere,) * 4,
        scratch_shapes=[
            pltpu.SemaphoreType.DMA((dp,)),
            pltpu.SemaphoreType.DMA((dp,)),
            pltpu.SemaphoreType.DMA((dp, share)),
            pltpu.SemaphoreType.DMA((total,)),
            pltpu.SemaphoreType.DMA((4,)),
        ],
        compiler_params=pltpu.CompilerParams(
            collective_id=number, has_side_effects=True, vmem_limit_bytes=VMEM_LIMIT
        ),
        name=name,
    )(*arrays)


def chunk_start(sq, chunk, part):
    is_own = (3 - chunk) // 3
    is_far = chunk // 3
    near = 1 - is_own - is_far
    neighbour = sq.down if part == 1 else sq.across
    block = sq.me * is_own + sq.far * is_far + neighbour * near
    other_half = chunk // 2 - is_far
    half = 1 - other_half if part == 1 else other_half
    return pl.multiple_of(block * sq.rows + half * sq.half, sq.half)


def rotate_back(values, cosine, sine):
    first, second = values[:, : HD // 2], values[:, HD // 2 :]
    return jnp.concatenate([first * cosine + second * sine, second * cosine - first * sine], axis=1)


def turned(values):
    return values.astype(F32).T.astype(BF16)


def rotate_rows(values, cosine, sine):
    first, second = values[:, : HD // 2], values[:, HD // 2 :]
    return jnp.concatenate([first * cosine - second * sine, second * cosine + first * sine], axis=1)


def softmax_weights(keys, queries, start, half, length):
    shape = (keys.shape[0], queries.shape[0])
    key_at = lax.broadcasted_iota(jnp.int32, shape, 0)
    query_at = lax.rem(lax.broadcasted_iota(jnp.int32, shape, 1), half) + start
    allowed = (key_at <= query_at) & (key_at < length)
    squash = jnp.tanh(nt(keys, queries) * (1.0 / SOFT_CAP))
    return squash, jnp.where(allowed, jnp.exp(SOFT_CAP * squash), 0.0)


def stack_heads(ref, here, heads):
    return jnp.concatenate([ref[here, h * HD : (h + 1) * HD] for h in range(heads)], axis=0)


def far_first(step):
    return step + 3 * ((3 - step) // 3) - 3 * (step // 3)


def attn_kernel(
    rows,
    length_ref,
    seq_hbm,
    weight_hbm,
    d_table,
    h_table,
    k_table,
    cos_ref,
    sin_ref,
    layer_ref,
    gains_ref,
    q_ref,
    k_ref,
    kt_ref,
    v_ref,
    attended_ref,
    inverse_ref,
    low_ref,
    low_out_ref,
    total_ref,
    resid_ref,
    normed_ref,
    mlp_out,
    w_out_all,
    h_all,
    seq,
    weight,
    vt,
    low_sum,
    load_sem,
    own_sem,
    gather_send,
    gather_recv,
    w_send,
    w_recv,
    *scratch,
):
    sq = Square(rows)
    half = sq.half
    model = total_ref.shape[-1]
    q_width = q_ref.shape[1]
    qkv_width = q_width + 2 * HD
    heads = q_width // HD
    wide = tile_of(model)
    core = lax.rem(lax.axis_index("dp"), 2)
    sibling = lax.axis_index("dp") + 1 - 2 * core
    weight_load = pltpu.make_async_copy(weight_hbm, weight, load_sem.at[0])
    seq_load = pltpu.make_async_copy(seq_hbm, seq, load_sem.at[1])
    weight_load.start()
    seq_load.start()
    greet([{"tensor": peer} for peer in (sq.across, sq.down, sq.far)] + [{"dp": sibling}])

    share = model // 2
    mine = pl.ds(pl.multiple_of(core * share, 8), share)
    own_h = pltpu.make_async_copy(h_table, h_all.at[sq.me], own_sem.at[1])
    own_h.start()
    taken, passed_on = [], []
    for which, peer in enumerate((sq.across, sq.down, sq.far)):
        taken.append(
            (
                remote(
                    weight_hbm.at[mine, pl.ds(qkv_width, q_width)],
                    w_out_all.at[sq.me, mine],
                    w_send.at[0, which],
                    w_recv.at[0, which],
                    peer,
                ),
                remote(
                    h_table, h_all.at[sq.me], w_send.at[1, which], w_recv.at[1, which], peer
                ),
            )
        )
        block = w_out_all.at[peer, mine]
        passed_on.append(
            pltpu.make_async_remote_copy(
                src_ref=block,
                dst_ref=block,
                send_sem=w_send.at[2, which],
                recv_sem=w_recv.at[2, which],
                device_id={"dp": sibling},
                device_id_type=MESH,
            )
        )
    weight_load.wait()
    seq_load.wait()

    @pl.loop(0, 4)
    def _(block):
        here = pl.ds(pl.multiple_of(block * rows, rows), rows)
        low = band(nn(seq[block], d_table[...]), QUERY, VALUE).astype(BF16)
        low_ref[here, :] = low
        cosine, sine = cos_ref[here, :], sin_ref[here, :]
        for h in range(heads):
            column = slice(h * HD, (h + 1) * HD)
            query = nn(seq[block], weight[:, column]) + nt(
                band(low.astype(F32), QUERY).astype(BF16), h_table[column, :]
            )
            q_ref[here, column] = (rotate_rows(query, cosine, sine) * HD ** (-0.5)).astype(BF16)
        key = nn(seq[block], weight[:, q_width : q_width + HD]) + nt(
            band(low.astype(F32), KEY).astype(BF16), k_table[...]
        )
        key = rotate_rows(key, cosine, sine)
        k_ref[here, :] = key.astype(BF16)
        kt_ref[:, here] = key.T.astype(BF16)
        value = nn(seq[block], weight[:, q_width + HD : qkv_width]) + nt(
            band(low.astype(F32), VALUE).astype(BF16), k_table[...]
        )
        v_ref[here, :] = value.astype(BF16)
        vt[:, here] = value.T.astype(BF16)

    for copies in taken:
        for copy in copies:
            copy.start()
    part, part_low = scratch[0], scratch[5]
    scatters = (ChunkScatter(sq, *scratch[:5]), ChunkScatter(sq, *scratch[5:10]))

    @pl.loop(0, 4)
    def _(step):
        chunk = far_first(step)
        for side in range(2):
            start = chunk_start(sq, chunk, side)
            here = pl.ds(start, half)
            unused, weights = softmax_weights(
                k_ref[...], stack_heads(q_ref, here, heads), start, half, length_ref[0]
            )
            inverse = 1.0 / jnp.sum(weights, axis=0, keepdims=True)
            mixed = nn(vt[...], (weights * inverse).astype(BF16)).T.astype(BF16)
            for h in range(heads):
                inverse_ref[h : h + 1, here] = inverse[:, h * half : (h + 1) * half]
                attended_ref[here, h * HD : (h + 1) * HD] = mixed[h * half : (h + 1) * half]

        attended = jnp.concatenate(
            [attended_ref[pl.ds(chunk_start(sq, chunk, side), half), :] for side in range(2)],
            axis=0,
        )
        part_low[chunk] = band(nn(attended, h_table[...]), OUT).astype(BF16)

        @pl.loop(0, model // wide)
        def _(tile):
            here = columns(tile, wide)
            part[chunk, :, here] = nt(attended, weight[here, qkv_width:]).astype(BF16)

        @pl.when(step == 0)
        def _():
            for scatter in scatters:
                scatter.send_far()

        @pl.when(step == 1)
        def _():
            for scatter in scatters:
                scatter.send_own()

    for link in range(2):
        for scatter in scatters:
            scatter.pass_on(link)
    scatters[1].collect(low_sum)
    low_out_ref[...] = low_sum[...].astype(BF16)
    scatters[0].collect(total_ref)
    add_lifted(total_ref, low_out_ref, d_table)

    @pl.loop(0, rows // BLOCK)
    def _(step):
        here = pl.ds(pl.multiple_of(step * BLOCK, BLOCK), BLOCK)
        resid = layer_ref[here, :].astype(F32) + rms_norm(total_ref[here, :], gains_ref[1:2, :])
        resid_ref[here, :] = resid
        normed_ref[here, :] = rms_norm(resid, gains_ref[2:3, :]).astype(BF16)

    gather = ChunkGather(sq, normed_ref, mlp_out, gather_send, gather_recv)
    gather.start()
    own = pltpu.make_async_copy(normed_ref, mlp_out.at[0], own_sem.at[0])
    own.start()
    for chunk in range(1, 4):
        gather.wait_chunk(chunk)
    for copies, onward in zip(taken, passed_on):
        for copy in copies:
            copy.wait_recv()
        onward.start()
    for copies, onward in zip(taken, passed_on):
        for copy in copies:
            copy.wait_send()
        onward.wait()
    own.wait()
    own_h.wait()
    gather.finish()
    for scatter in scatters:
        scatter.finish()


def attn_fused(lengths, seq, weight, d_tab, h_tab, k_tab, cosine, sine, layer_in, gains):
    rows, model = layer_in.shape
    q_width = weight.shape[1] - 2 * HD
    q_width //= 2
    qkv_width = q_width + 2 * HD
    anywhere = pl.BlockSpec(memory_space=pl.ANY)
    vmem = pl.BlockSpec(memory_space=pltpu.VMEM)
    narrow = jax.ShapeDtypeStruct((LEN, HD), BF16)
    return pl.pallas_call(
        functools.partial(attn_kernel, rows),
        out_shape=(
            jax.ShapeDtypeStruct((LEN, q_width), BF16),
            narrow,
            jax.ShapeDtypeStruct((HD, LEN), BF16),
            narrow,
            jax.ShapeDtypeStruct((LEN, q_width), BF16),
            jax.ShapeDtypeStruct((q_width // HD, LEN), F32),
            jax.ShapeDtypeStruct((LEN, LANES), BF16),
            jax.ShapeDtypeStruct((rows, LANES), BF16),
            jax.ShapeDtypeStruct((rows, model), F32),
            jax.ShapeDtypeStruct((rows, model), F32),
            jax.ShapeDtypeStruct((rows, model), BF16),
            jax.ShapeDtypeStruct((4, rows, model), BF16),
            jax.ShapeDtypeStruct((4, model, q_width), BF16),
            jax.ShapeDtypeStruct((4, q_width, LANES), BF16),
        ),
        in_specs=[pl.BlockSpec(memory_space=pltpu.SMEM)] + [anywhere] * 2 + [vmem] * 7,
        out_specs=(vmem,) * 11 + (anywhere,) * 3,
        scratch_shapes=[
            pltpu.VMEM((4, rows, model), BF16),
            pltpu.VMEM(weight.shape, BF16),
            pltpu.VMEM((HD, LEN), BF16),
            pltpu.VMEM((rows, LANES), F32),
            pltpu.SemaphoreType.DMA((2,)),
            pltpu.SemaphoreType.DMA((2,)),
            pltpu.SemaphoreType.DMA((6,)),
            pltpu.SemaphoreType.DMA((6,)),
            pltpu.SemaphoreType.DMA((3, 3)),
            pltpu.SemaphoreType.DMA((3, 3)),
        ]
        + scatter_scratch(rows, model)
        + scatter_scratch(rows, LANES),
        compiler_params=pltpu.CompilerParams(
            collective_id=8, has_side_effects=True, vmem_limit_bytes=62 * 1024 * 1024
        ),
        name="attn",
    )(lengths, seq, weight, d_tab, h_tab, k_tab, cosine, sine, layer_in, gains)


def attn_back_kernel(
    rows,
    ids_ref,
    length_ref,
    back_ref,
    low_gu_ref,
    resid_ref,
    total_ref,
    cot_ref,
    layer_ref,
    gains_ref,
    weight_hbm,
    w_out_hbm,
    seq_hbm,
    q_ref,
    k_ref,
    kt_ref,
    v_ref,
    attended_ref,
    inverse_ref,
    cos_ref,
    sin_ref,
    low_ref,
    d_table,
    h_all,
    k_table,
    normed_ref,
    low_out_ref,
    grad_mlp_ref,
    low_down_ref,
    f_ref,
    o_ref,
    in_out,
    heads_out,
    hidden_out,
    query_out,
    keyval_out,
    gateup_out,
    resid_out,
    weight,
    w_out,
    work,
    g_ref,
    low_sum,
    buf,
    att_send,
    att,
    low_own,
    low_all,
    q_grad,
    k_sum,
    v_sum,
    kv_grad,
    joined,
    d_turned,
    h_turned,
    k_turned,
    d_send,
    d_land,
    d_sum,
    d_recv,
    f_recv,
    hk_send,
    hk_land,
    hk_recv,
    load_sem,
    att_sends,
    att_recvs,
    f_sem,
    d_sem,
    hk_sem,
    group_send,
    group_recv,
    line_recv,
    *scratch,
):
    sq = Square(rows)
    dp = lax.axis_size("dp")
    d = lax.axis_index("dp")
    model = o_ref.shape[-1]
    half = sq.half
    wide = tile_of(model)
    q_width = q_ref.shape[1]
    qkv_width = q_width + 2 * HD
    others = (sq.far, sq.across, sq.down)
    sources = [w_out_hbm.at[peer] for peer in others]
    sources.append(weight_hbm.at[:, pl.ds(qkv_width, q_width)])
    loads = [
        pltpu.make_async_copy(source, w_out.at[which % 2], load_sem.at[2 + which])
        for which, source in enumerate(sources)
    ]
    weight_load = pltpu.make_async_copy(
        weight_hbm.at[:, pl.ds(0, qkv_width)], weight, load_sem.at[0]
    )
    seq_load = pltpu.make_async_copy(seq_hbm, buf, load_sem.at[1])
    loads[0].start()
    loads[1].start()
    weight_load.start()
    seq_load.start()
    peers = [{"tensor": peer} for peer in (sq.across, sq.down, sq.far)]
    peers += [{"dp": lax.rem(d + step, dp)} for step in range(1, dp)]
    call(peers)

    low_gu = low_gu_ref[...].astype(BF16)

    @pl.loop(0, model // wide)
    def _(step):
        here = columns(step, wide)
        work[:, here] = back_ref[:, here] + nt(low_gu, d_table[here, :])

    @pl.loop(0, rows // BLOCK)
    def _(step):
        here = pl.ds(pl.multiple_of(step * BLOCK, BLOCK), BLOCK)
        at = sq.me * rows + step * BLOCK + lax.broadcasted_iota(jnp.int32, (BLOCK, 1), 0)
        valid = (at < length_ref[0]).astype(F32)
        mid = cot_ref[here, :].astype(F32) * valid + norm_back(
            resid_ref[here, :], gains_ref[2:3, :], work[here, :]
        )
        work[here, :] = mid
        g_ref[here, :] = norm_back(total_ref[here, :], gains_ref[1:2, :], mid).astype(BF16)

    low_own[...] = band(nn(g_ref[...], d_table[...]), OUT).astype(BF16)
    pl.semaphore_wait(pltpu.get_barrier_semaphore(), len(peers))
    heads_out_copies = []
    for which, peer in enumerate(others + (sq.me,)):
        loads[which].wait()
        grads = (nn(g_ref[...], w_out[which % 2]) + nt(low_own[...], h_all[peer])).astype(BF16)
        if which < 2:
            loads[which + 2].start()
        if which == 3:
            att[sq.me] = grads
            low_all[sq.me] = low_own[...]
            continue
        att_send[which] = grads
        copies = (
            remote(
                att_send.at[which],
                att.at[sq.me],
                att_sends.at[which, 0],
                att_recvs.at[which, 0],
                peer,
            ),
            remote(
                low_own,
                low_all.at[sq.me],
                att_sends.at[which, 1],
                att_recvs.at[which, 1],
                peer,
            ),
        )
        for copy in copies:
            copy.start()
        heads_out_copies.append(copies)
    line = []
    line += along(lambda k: f_ref.at[k // 2, lax.rem(k, 2)], f_recv, f_sem, line_recv.at[0])
    part, part_low = scratch[0], scratch[5]
    scatters = (ChunkScatter(sq, *scratch[:5]), ChunkScatter(sq, *scratch[5:10]))

    d_turned[...] = jnp.zeros_like(d_turned)
    low_grads = (
        (turned(low_gu)[GATE.start : UP.stop], normed_ref, slice(GATE.start, UP.stop)),
        (turned(low_out_ref[...])[OUT], g_ref, OUT),
        (turned(low_down_ref[...])[DOWN], grad_mlp_ref, DOWN),
    )

    @pl.loop(0, model // wide)
    def _(step):
        here = columns(step, wide)
        for low, source, place in low_grads:
            d_turned[place, here] = nn(low, source[:, here])

    h_turned[...] = jnp.zeros_like(h_turned)
    k_turned[...] = jnp.zeros_like(k_turned)
    k_sum[...] = jnp.zeros_like(k_sum)
    v_sum[...] = jnp.zeros_like(v_sum)
    heads = q_width // HD
    stacked = heads * half

    @pl.loop(0, 4)
    def _(turn):
        for step, which in ((1, 1), (2, 2), (3, 0)):

            @pl.when(turn == step)
            def _(which=which):
                for copy in heads_out_copies[which]:
                    copy.wait_recv()

        is_own, is_far = (3 - turn) // 3, turn // 3
        is_down = turn // 2 - is_far
        block = (
            sq.me * is_own
            + sq.far * is_far
            + sq.down * is_down
            + sq.across * (1 - is_own - is_far - is_down)
        )
        low_turned = turned(low_all[block])[OUT]
        for side in range(2):
            start = pl.multiple_of(block * rows + side * half, half)
            here = pl.ds(start, half)
            place = pl.ds(side * half, half)
            h_turned[:RANK, :] += nn(
                low_turned[:, side * half : (side + 1) * half], attended_ref[here, :]
            )
            queries = stack_heads(q_ref, here, heads)
            grads = jnp.concatenate(
                [att[block, place, h * HD : (h + 1) * HD] for h in range(heads)], axis=0
            )
            inverse = jnp.concatenate([inverse_ref[h : h + 1, here] for h in range(heads)], axis=1)
            squash, weights = softmax_weights(k_ref[...], queries, start, half, length_ref[0])
            probs = weights * inverse
            grad_probs = nt(v_ref[...], grads)
            mean = jnp.sum(probs * grad_probs, axis=0, keepdims=True)
            grad_raw = (probs * (grad_probs - mean) * (1.0 - squash * squash)).astype(BF16)
            k_sum[...] += nn(grad_raw, queries)
            v_sum[...] += nn(probs.astype(BF16), grads)
            q_back = nn(kt_ref[...], grad_raw).T * HD ** (-0.5)
            for h in range(heads):
                q_grad[here, h * HD : (h + 1) * HD] = rotate_back(
                    q_back[h * half : (h + 1) * half], cos_ref[here, :], sin_ref[here, :]
                ).astype(BF16)

    weight_load.wait()
    kv_grad[:, :HD] = rotate_back(k_sum[...], cos_ref[...], sin_ref[...]).astype(BF16)
    kv_grad[:, HD:] = v_sum[...].astype(BF16)

    @pl.loop(0, 4)
    def _(step):
        chunk = far_first(step)
        for side in range(2):
            here = pl.ds(chunk_start(sq, chunk, side), half)
            place = pl.ds(side * half, half)
            joined[chunk, place, :q_width] = q_grad[here, :]
            joined[chunk, place, q_width:] = kv_grad[here, :]
        part_low[chunk] = (
            band(nn(joined[chunk, :, :q_width], h_all[sq.me]), QUERY)
            + band(nn(joined[chunk, :, q_width : q_width + HD], k_table[...]), KEY)
            + band(nn(joined[chunk, :, q_width + HD :], k_table[...]), VALUE)
        ).astype(BF16)

        @pl.loop(0, model // wide)
        def _(tile):
            here = columns(tile, wide)
            part[chunk, :, here] = nt(joined[chunk], weight[here, :]).astype(BF16)

        @pl.when(step == 0)
        def _():
            for scatter in scatters:
                scatter.send_far()

        @pl.when(step == 1)
        def _():
            for scatter in scatters:
                scatter.send_own()

    seq_load.wait()

    @pl.loop(0, 4)
    def _(chunk):
        grad_turned = turned(part_low[chunk])[: VALUE.stop]
        for side in range(2):
            here = pl.ds(chunk_start(sq, chunk, side), half)
            place = slice(side * half, (side + 1) * half)
            low_turned = turned(low_ref[here, :])
            mine = joined.at[chunk, pl.ds(side * half, half)]
            h_turned[RANK : 2 * RANK, :] += nn(low_turned[QUERY], mine[:, :q_width])
            k_turned[:RANK, :] += nn(low_turned[KEY], mine[:, q_width : q_width + HD])
            k_turned[RANK : 2 * RANK, :] += nn(low_turned[VALUE], mine[:, q_width + HD :])
            where_from = chunk_start(sq, chunk, side)
            block = where_from // rows
            inside = pl.ds(pl.multiple_of(where_from - block * rows, half), half)

            @pl.loop(0, model // wide)
            def _(tile):
                where = columns(tile, wide)
                d_turned[: VALUE.stop, where] += nn(
                    grad_turned[:, place],
                    buf[block, inside, where],
                )

    @pl.loop(0, model // LANES)
    def _(step):
        here = columns(step, LANES)
        d_send[here, :] = d_turned[:, here].T.astype(BF16)

    d_rows = d_sum.shape[1]
    spread = []
    for k in range(dp):
        spread.append(
            sq.spread(
                lambda peer, k=k: d_send.at[pl.ds(pl.multiple_of((k * 4 + peer) * d_rows, 8), d_rows)],
                d_land.at[k],
                group_send.at[k],
                group_recv.at[k],
            )
        )
    cores = hk_send.shape[0]
    h_size, k_size = q_width // dp, HD // dp
    hk_send[...] = jnp.zeros_like(hk_send)
    for core in range(cores):
        for peer in range(4):
            at = core * 4 + peer
            hk_send[core, peer, : 2 * RANK, :h_size] = h_turned[
                : 2 * RANK, at * h_size : (at + 1) * h_size
            ].astype(BF16)
            hk_send[core, peer, 2 * RANK :, :k_size] = k_turned[
                : 2 * RANK, at * k_size : (at + 1) * k_size
            ].astype(BF16)
    spread.append(
        sq.spread(lambda peer: hk_send.at[:, peer], hk_land, group_send.at[dp], group_recv.at[dp])
    )
    for copies in spread:
        for copy in copies:
            copy.start()
    for link in range(2):
        for scatter in scatters:
            scatter.pass_on(link)
    for copies in spread:
        copies[0].wait()
        for copy in copies[1:]:
            copy.wait_recv()
    for k in range(dp):
        d_sum[k] = sum(d_land[k, t].astype(F32) for t in range(4)).astype(BF16)
    line += along(lambda k: d_sum.at[k], d_recv, d_sem, line_recv.at[1])
    line += along(lambda k: hk_land.at[k // 2, lax.rem(k, 2)], hk_recv, hk_sem, line_recv.at[2])
    scatters[1].collect(low_sum)
    low_qkv = low_sum[...].astype(BF16)
    for link in range(2):
        scatters[0].copy(0, link).wait_recv()
        scatters[0].copy(2, link).wait_recv()
    landing = scratch[1]
    low_sum[...] = low_qkv.astype(F32)

    @pl.loop(0, rows // BLOCK)
    def _(step):
        here = pl.ds(pl.multiple_of(step * BLOCK, BLOCK), BLOCK)
        link = (step * BLOCK) // half
        there = pl.ds(pl.multiple_of(step * BLOCK - link * half, BLOCK), BLOCK)
        total = (
            part[0, here, :].astype(F32)
            + landing[link, there, :].astype(F32)
            + landing[4 + link, there, :].astype(F32)
            + nt(low_sum[here, :].astype(BF16), d_table[...])
        )
        o_ref[here, :] = (
            work[here, :] + norm_back(layer_ref[here, :].astype(F32), gains_ref[0:1, :], total)
        ).astype(BF16)

    for item, target in enumerate((f_recv, d_recv, hk_recv)):
        pltpu.make_async_copy(target, target, line_recv.at[item]).wait()

    @pl.loop(0, NA)
    def _(adapter):
        def pick(received):
            total = None
            for group in range(dp):
                mine = jnp.where(
                    ids_ref[group] == adapter, received[group].astype(F32), 0.0
                )
                total = mine if total is None else total + mine
            return total

        d_all = pick(d_recv)
        in_out[adapter] = d_all[:, : 5 * RANK]
        d_flip = d_all.T
        f_all = pick(f_recv)
        hidden_out[adapter] = f_all[:RANK]
        hk_all = pick(hk_recv)
        heads_out[adapter] = hk_all[:RANK, :h_size]
        query_out[adapter] = hk_all[RANK : 2 * RANK, :h_size]
        for which in range(2):
            first = (which + 2) * RANK
            keyval_out[adapter, which] = hk_all[first : first + RANK, :k_size]
            first = (which + 1) * RANK
            gateup_out[adapter, which] = f_all[first : first + RANK]
            first = (which + 5) * RANK
            resid_out[adapter, which] = d_flip[first : first + RANK]

    for copies in spread:
        for copy in copies[1:]:
            copy.wait_send()
    for copies in heads_out_copies:
        for copy in copies:
            copy.wait_send()
    for copy in line:
        copy.wait_send()
    for scatter in scatters:
        scatter.finish()


def attn_back_fused(scalars, arrays, grad_shapes, dp, total):
    anywhere = pl.BlockSpec(memory_space=pl.ANY)
    vmem = pl.BlockSpec(memory_space=pltpu.VMEM)
    smem = pl.BlockSpec(memory_space=pltpu.SMEM)
    rows, model = arrays[0].shape
    weight, q, f_in = arrays[7], arrays[10], arrays[-1]
    q_width = q.shape[1]
    specs = [smem, smem] + [vmem] * len(arrays)
    specs[9] = specs[10] = specs[11] = anywhere
    outs = [jax.ShapeDtypeStruct((rows, model), BF16)]
    outs += [jax.ShapeDtypeStruct(shape, F32) for shape in grad_shapes]
    d_rows = model // total
    messages = f_in.shape[2:]
    return pl.pallas_call(
        functools.partial(attn_back_kernel, rows),
        out_shape=tuple(outs),
        in_specs=specs,
        out_specs=(vmem,) * len(outs),
        scratch_shapes=[
            pltpu.VMEM((model, q_width + 2 * HD), BF16),
            pltpu.VMEM((2, model, q_width), BF16),
            pltpu.VMEM((rows, model), F32),
            pltpu.VMEM((rows, model), BF16),
            pltpu.VMEM((rows, LANES), F32),
            pltpu.VMEM((4, rows, model), BF16),
            pltpu.VMEM((3, rows, q_width), BF16),
            pltpu.VMEM((4, rows, q_width), BF16),
            pltpu.VMEM((rows, LANES), BF16),
            pltpu.VMEM((4, rows, LANES), BF16),
            pltpu.VMEM((LEN, q_width), BF16),
            pltpu.VMEM((LEN, HD), F32),
            pltpu.VMEM((LEN, HD), F32),
            pltpu.VMEM((LEN, 2 * HD), BF16),
            pltpu.VMEM((4, rows, q_width + 2 * HD), BF16),
            pltpu.VMEM((LANES, model), F32),
            pltpu.VMEM((2 * RANK, q_width), F32),
            pltpu.VMEM((2 * RANK, HD), F32),
            pltpu.VMEM((model, LANES), BF16),
            pltpu.VMEM((dp, 4, d_rows, LANES), BF16),
            pltpu.VMEM((dp, d_rows, LANES), BF16),
            pltpu.VMEM((dp, d_rows, LANES), BF16),
            pltpu.VMEM((dp,) + messages, BF16),
            pltpu.VMEM((dp // 4, 4, 4 * RANK, LANES), BF16),
            pltpu.VMEM((4, dp // 4, 4 * RANK, LANES), BF16),
            pltpu.VMEM((dp, 4 * RANK, LANES), BF16),
            pltpu.SemaphoreType.DMA((6,)),
            pltpu.SemaphoreType.DMA((3, 2)),
            pltpu.SemaphoreType.DMA((3, 2)),
            pltpu.SemaphoreType.DMA((dp,)),
            pltpu.SemaphoreType.DMA((dp,)),
            pltpu.SemaphoreType.DMA((dp,)),
            pltpu.SemaphoreType.DMA((dp + 1, 3)),
            pltpu.SemaphoreType.DMA((dp + 1, 4)),
            pltpu.SemaphoreType.DMA((3,)),
        ]
        + scatter_scratch(rows, model)
        + scatter_scratch(rows, LANES),
        compiler_params=pltpu.CompilerParams(
            collective_id=6, has_side_effects=True, vmem_limit_bytes=62 * 1024 * 1024
        ),
        name="attn_back",
    )(*scalars, *arrays)


def per_device(
    layer_in,
    cotangent,
    lengths,
    adapter_ids,
    norm_gains,
    query_weight,
    key_weight,
    value_weight,
    out_weight,
    gate_weight,
    up_weight,
    down_weight,
    adapt_in,
    adapt_heads,
    adapt_hidden,
    lift_query,
    lift_keyval,
    lift_gateup,
    lift_resid,
):
    lay = Layout()
    count = lay.tensor
    rows = layer_in.shape[0]
    group_rows = rows * count
    assert lengths.shape[0] == 1 and group_rows == LEN
    heads_here = lay.heads_here
    head_width = heads_here * HD
    hidden_here = FF // count
    assert lay.ratio % heads_here == 0

    key_cols = lax.dynamic_slice_in_dim(key_weight, lay.kv_head * HD, HD, 1)
    value_cols = lax.dynamic_slice_in_dim(value_weight, lay.kv_head * HD, HD, 1)
    attn_shard = jnp.concatenate([query_weight, key_cols, value_cols, out_weight.T], axis=1)
    attn_w = lax.all_gather(attn_shard, "dp", axis=0, tiled=True)
    gate_up_shard = jnp.concatenate([gate_weight, up_weight], axis=1)
    down_shard = down_weight.T
    attn_shard, gate_up_shard, down_shard = lax.optimization_barrier(
        (attn_shard, gate_up_shard, down_shard)
    )
    gate_up_w = lax.all_gather(gate_up_shard, "dp", axis=0, tiled=True)
    qkv_width = head_width + 2 * HD

    cosine, sine = tables(LEN, HD)
    if count == 4 and lay.dp == 8:
        seq_attn, all_ids, d_tab, f_tab, h_tab, k_tab = front(
            jnp.broadcast_to(adapter_ids, (8, LANES)),
            layer_in,
            norm_gains,
            jnp.concatenate(
                [
                    lift_gateup.reshape(NA, 2 * RANK, -1),
                    jnp.swapaxes(adapt_hidden, 1, 2),
                ],
                axis=1,
            ),
            jnp.concatenate(
                [jnp.swapaxes(adapt_in, 1, 2), lift_resid.reshape(NA, 2 * RANK, -1)], axis=1
            ),
            jnp.concatenate(
                [
                    jnp.swapaxes(adapt_heads, 1, 2),
                    lift_query,
                    jnp.pad(
                        lift_keyval.reshape(NA, 2 * RANK, -1),
                        ((0, 0), (0, 0), (0, lift_query.shape[2] - lift_keyval.shape[3])),
                    ),
                ],
                axis=1,
            ),
            lay.dp,
            (D, hidden_here, head_width, HD),
        )
        (
            queries,
            keys,
            keys_turned,
            values,
            attended,
            inverse,
            low_qkv,
            low_out,
            attn_total,
            resid_mid,
            normed_mlp,
            seq_mlp,
            w_out_all,
            h_all,
        ) = attn_fused(
            lengths,
            seq_attn.reshape(count, rows, D),
            attn_w,
            d_tab,
            h_tab,
            k_tab,
            cosine.reshape(LEN, HD // 2),
            sine.reshape(LEN, HD // 2),
            layer_in,
            norm_gains,
        )
        layer_out, grad_mlp, low_gu, low_down, hidden, slope, gelu, down_w = mlp_fused(
            lengths,
            seq_mlp,
            gate_up_w,
            down_shard,
            d_tab,
            f_tab,
            resid_mid,
            cotangent,
            norm_gains,
            lay.dp,
        )
        mlp_back, grad_low_gu, f_grad = mlp_back_fused(
            grad_mlp,
            down_w.reshape(D, hidden_here),
            gate_up_w,
            slope,
            gelu,
            hidden,
            low_gu,
            d_tab,
            f_tab,
            lay.dp,
        )
        grad_shapes = [
            table.shape
            for table in (
                adapt_in,
                adapt_heads,
                adapt_hidden,
                lift_query,
                lift_keyval,
                lift_gateup,
                lift_resid,
            )
        ]
        for which in (1, 2):
            shape = grad_shapes[which]
            grad_shapes[which] = (shape[0], shape[2], shape[1])
        grads = list(
            attn_back_fused(
                (all_ids[:, 0, 0], lengths),
                (
                    mlp_back,
                    grad_low_gu,
                    resid_mid,
                    attn_total,
                    cotangent,
                    layer_in,
                    norm_gains,
                    attn_w,
                    w_out_all,
                    seq_attn.reshape(count, rows, D),
                    queries,
                    keys,
                    keys_turned,
                    values,
                    attended,
                    inverse,
                    cosine.reshape(LEN, HD // 2),
                    sine.reshape(LEN, HD // 2),
                    low_qkv,
                    d_tab,
                    h_all,
                    k_tab,
                    normed_mlp,
                    low_out,
                    grad_mlp,
                    low_down,
                    f_grad,
                ),
                tuple(grad_shapes),
                lay.dp,
                lay.total,
            )
        )
        for which in (2, 3):
            grads[which] = jnp.swapaxes(grads[which], 1, 2)
        return (layer_out, *grads)

    all_ids = lax.all_gather(adapter_ids[:, 0], "dp", axis=0, tiled=True)
    group_hot = (all_ids[:, None] == jnp.arange(NA, dtype=jnp.int32)[None, :]).astype(BF16)

    def rows_of(table):
        moved = jnp.moveaxis(table, -1, 1)
        return moved.reshape(NA, moved.shape[1], -1)

    def choose(*parts):
        packed = lanes(*parts)
        return lax.dot_general(
            group_hot, packed, (((1,), (0,)), ((), ())), preferred_element_type=F32
        ).astype(BF16)

    d_send = choose((QUERY, adapt_in), (OUT, rows_of(lift_resid)))
    f_send = choose((GATE, rows_of(lift_gateup)), (DOWN, adapt_hidden))
    h_send = choose((QUERY, rows_of(lift_query)), (OUT, adapt_heads))
    k_send = choose((KEY, rows_of(lift_keyval)))
    d_rows, f_rows, h_rows, k_rows = (item.shape[1] for item in (d_send, f_send, h_send, k_send))
    d_tab, f_tab, h_tab, k_tab = exchange(
        tables_kernel,
        "adapter_tables",
        3,
        (d_send, f_send, h_send, k_send),
        (
            (lay.total, d_rows, LANES),
            (lay.dp, f_rows, LANES),
            (lay.dp, h_rows, LANES),
            (lay.kv_owners, k_rows, LANES),
        ),
        lay.dp,
        lay.total,
        lay.share,
    )
    d_tab = d_tab.reshape(D, LANES)
    f_tab = f_tab.reshape(hidden_here, LANES)
    h_tab = h_tab.reshape(head_width, LANES)
    k_tab = k_tab.reshape(HD, LANES)
    in_qkv, in_gu = d_tab[:, : 3 * RANK], d_tab[:, 3 * RANK : 5 * RANK]
    lift_out, lift_down = d_tab[:, OUT], d_tab[:, DOWN]
    map_hidden, lift_gate, lift_up = f_tab[:, DOWN], f_tab[:, GATE], f_tab[:, UP]
    map_heads, lift_q = h_tab[:, OUT], h_tab[:, QUERY]
    lift_k, lift_v = k_tab[:, KEY], k_tab[:, VALUE]

    row_start = lay.t * rows
    length = lengths[0]
    row_valid = ((row_start + jnp.arange(rows, dtype=jnp.int32)) < length).astype(F32)[:, None]
    place = jnp.arange(LEN, dtype=jnp.int32)
    allowed = (place[:, None] >= place[None, :]) & (place[None, :] < length)

    resid_in = layer_in.astype(F32)
    normed_attn = rms_norm(resid_in, norm_gains[0]).astype(BF16)
    seq_attn = tensor_gather(normed_attn, count)
    low_qkv = nn(seq_attn, in_qkv).astype(BF16)
    low_q, low_k, low_v = (low_qkv[:, i * RANK : (i + 1) * RANK] for i in range(3))
    qkv = nn(seq_attn, attn_w[:, :qkv_width])
    query_pre = (qkv[:, :head_width] + nt(low_q, lift_q)).reshape(LEN, heads_here, HD)
    key_pre = (qkv[:, head_width : head_width + HD] + nt(low_k, lift_k)).reshape(LEN, 1, HD)
    value_pre = qkv[:, head_width + HD :] + nt(low_v, lift_v)
    queries = (rotate(query_pre, cosine, sine) * HD ** (-0.5)).astype(BF16)
    keys = rotate(key_pre, cosine, sine).astype(BF16).reshape(LEN, HD)
    values = value_pre.astype(BF16)

    def scores_of():
        raw = jnp.einsum("qhd,kd->hqk", queries, keys, preferred_element_type=F32)
        squash = jnp.tanh(raw / SOFT_CAP)
        return squash, jnp.where(allowed[None], jnp.exp(SOFT_CAP * squash), 0.0)

    squash, weights = scores_of()
    inverse_total = 1.0 / jnp.sum(weights, axis=-1, keepdims=True)
    attended = jnp.einsum(
        "hqk,kd->qhd", (weights * inverse_total).astype(BF16), values, preferred_element_type=F32
    )
    attended = attended.astype(BF16).reshape(LEN, head_width)
    w_out = attn_w[:, qkv_width:]
    out_part = nt(attended, w_out).astype(BF16)
    low_out_part = pad_lanes(nn(attended, map_heads).astype(BF16))
    attn_main, low_out = tensor_scatter(out_part, low_out_part, count)
    low_out = low_out[:, :RANK].astype(BF16)
    attn_total = attn_main + nt(low_out, lift_out)
    resid_mid = resid_in + rms_norm(attn_total, norm_gains[1])

    normed_mlp = rms_norm(resid_mid, norm_gains[2]).astype(BF16)
    seq_mlp = tensor_gather(normed_mlp, count)
    low_gu = nn(seq_mlp, in_gu).astype(BF16)
    low_g, low_u = low_gu[:, :RANK], low_gu[:, RANK:]
    w_gate, w_up = gate_up_w[:, :hidden_here], gate_up_w[:, hidden_here:]
    gate = nn(seq_mlp, w_gate) + nt(low_g, lift_gate)
    up = nn(seq_mlp, w_up) + nt(low_u, lift_up)
    hidden, slope, gelu = gelu_parts(gate, up)
    down_w = lax.all_gather(down_shard, "dp", axis=0, tiled=True)
    down_part = nt(hidden, down_w).astype(BF16)
    low_down_part = pad_lanes(nn(hidden, map_hidden).astype(BF16))
    mlp_main, low_down = tensor_scatter(down_part, low_down_part, count)
    low_down = low_down[:, :RANK].astype(BF16)
    mlp_total = mlp_main + nt(low_down, lift_down)
    layer_out = (row_valid * (resid_mid + rms_norm(mlp_total, norm_gains[3]))).astype(BF16)

    grad_out = cotangent.astype(F32) * row_valid
    grad_mlp = norm_back(mlp_total, norm_gains[3], grad_out).astype(BF16)
    seq_grad_mlp = tensor_gather(grad_mlp, count)
    grad_low_down = nn(seq_grad_mlp, lift_down).astype(BF16)
    grad_hidden = nn(seq_grad_mlp, down_w) + nt(grad_low_down, map_hidden)
    grad_gate = (grad_hidden * slope.astype(F32)).astype(BF16)
    grad_up = (grad_hidden * gelu.astype(F32)).astype(BF16)
    low_gu_part = pad_lanes(
        jnp.concatenate([nn(grad_gate, lift_gate), nn(grad_up, lift_up)], axis=1).astype(BF16)
    )
    mlp_back_part = (nt(grad_gate, w_gate) + nt(grad_up, w_up)).astype(BF16)
    mlp_back, grad_low_gu = tensor_scatter(mlp_back_part, low_gu_part, count)
    f_parts = [tn(hidden, grad_low_down), tn(grad_gate, low_g), tn(grad_up, low_u)]
    grad_low_gu = grad_low_gu[:, : 2 * RANK].astype(BF16)
    grad_normed_mlp = mlp_back + nt(grad_low_gu, in_gu)
    grad_mid = grad_out + norm_back(resid_mid, norm_gains[2], grad_normed_mlp)

    grad_attn = norm_back(attn_total, norm_gains[1], grad_mid).astype(BF16)
    seq_grad_attn = tensor_gather(grad_attn, count)
    grad_low_out = nn(seq_grad_attn, lift_out).astype(BF16)
    grad_attended = (nn(seq_grad_attn, w_out) + nt(grad_low_out, map_heads)).astype(BF16)
    grad_heads = grad_attended.reshape(LEN, heads_here, HD)
    probs = weights * inverse_total
    probs_low = probs.astype(BF16)
    grad_probs = jnp.einsum("qhd,kd->hqk", grad_heads, values, preferred_element_type=F32)
    grad_value = jnp.einsum("hqk,qhd->kd", probs_low, grad_heads, preferred_element_type=F32)
    grad_capped = probs * (grad_probs - jnp.sum(probs * grad_probs, axis=-1, keepdims=True))
    grad_raw = (grad_capped * (1.0 - squash * squash)).astype(BF16)
    grad_query = jnp.einsum("hqk,kd->qhd", grad_raw, keys, preferred_element_type=F32)
    grad_key = jnp.einsum("hqk,qhd->kd", grad_raw, queries, preferred_element_type=F32)
    grad_q_pre = rotate(grad_query * HD ** (-0.5), cosine, -sine).astype(BF16)
    grad_q_pre = grad_q_pre.reshape(LEN, head_width)
    grad_k_pre = rotate(grad_key.reshape(LEN, 1, HD), cosine, -sine).astype(BF16)
    grad_k_pre = grad_k_pre.reshape(LEN, HD)
    grad_v_pre = grad_value.astype(BF16)
    low_qkv_part = pad_lanes(
        jnp.concatenate(
            [nn(grad_q_pre, lift_q), nn(grad_k_pre, lift_k), nn(grad_v_pre, lift_v)], axis=1
        ).astype(BF16)
    )
    grad_qkv = jnp.concatenate([grad_q_pre, grad_k_pre, grad_v_pre], axis=1)
    attn_back_part = nt(grad_qkv, attn_w[:, :qkv_width]).astype(BF16)
    attn_back, grad_low_qkv = tensor_scatter(attn_back_part, low_qkv_part, count)
    grad_low_qkv = grad_low_qkv[:, : 3 * RANK].astype(BF16)
    grad_normed_attn = attn_back + nt(grad_low_qkv, in_qkv)
    input_grad = (grad_mid + norm_back(resid_in, norm_gains[0], grad_normed_attn)).astype(BF16)

    def packed(parts, blocks):
        return pad_lanes(jnp.concatenate(parts, axis=1).astype(BF16)).reshape(
            blocks, -1, LANES
        )

    d_grad = packed(
        [
            tn(normed_attn, grad_low_qkv),
            tn(normed_mlp, grad_low_gu),
            tn(grad_attn, low_out),
            tn(grad_mlp, low_down),
        ],
        lay.total,
    )
    f_grad = packed(f_parts, lay.dp)
    h_grad = packed([tn(attended, grad_low_out), tn(grad_q_pre, low_q)], lay.dp)
    k_grad = packed([tn(grad_k_pre, low_k), tn(grad_v_pre, low_v)], lay.kv_owners)
    d_all, f_all, h_all, k_all = exchange(
        grads_kernel,
        "adapter_grads",
        4,
        (d_grad, f_grad, h_grad, k_grad),
        (
            (lay.total, d_rows, LANES),
            (lay.dp, f_rows, LANES),
            (lay.dp, h_rows, LANES),
            (lay.dp * lay.share, k_rows, LANES),
        ),
        lay.dp,
        lay.total,
        lay.share,
    )

    def collect(received):
        repeats = received.shape[0] // lay.dp
        hot = jnp.repeat(group_hot, repeats, axis=0)
        return lax.dot_general(
            hot, received, (((0,), (0,)), ((), ())), preferred_element_type=F32
        )

    d_all, f_all, h_all, k_all = (collect(item) for item in (d_all, f_all, h_all, k_all))

    def lift_form(values, shape):
        return jnp.moveaxis(values, 1, 2).reshape(shape)

    return (
        layer_out,
        input_grad,
        d_all[:, :, : 5 * RANK],
        h_all[:, :, :RANK],
        f_all[:, :, :RANK],
        lift_form(h_all[:, :, RANK : 2 * RANK], lift_query.shape),
        lift_form(k_all[:, :, : 2 * RANK], lift_keyval.shape),
        lift_form(f_all[:, :, RANK : 3 * RANK], lift_gateup.shape),
        lift_form(d_all[:, :, 5 * RANK : 7 * RANK], lift_resid.shape),
    )


def solution(mesh):
    return jax.shard_map(
        per_device,
        mesh=mesh,
        in_specs=(
            P(("dp", "tensor"), None),
            P(("dp", "tensor"), None),
            P("dp"),
            P("dp", None),
            P(),
            P("dp", "tensor"),
            P("dp", None),
            P("dp", None),
            P("tensor", "dp"),
            P("dp", "tensor"),
            P("dp", "tensor"),
            P("tensor", "dp"),
            P(None, ("dp", "tensor"), None),
            P(None, ("dp", "tensor"), None),
            P(None, ("dp", "tensor"), None),
            P(None, None, ("dp", "tensor")),
            P(None, None, None, ("dp", "tensor")),
            P(None, None, None, ("dp", "tensor")),
            P(None, None, None, ("dp", "tensor")),
        ),
        out_specs=(
            P(("dp", "tensor"), None),
            P(("dp", "tensor"), None),
            P(None, ("dp", "tensor"), None),
            P(None, ("dp", "tensor"), None),
            P(None, ("dp", "tensor"), None),
            P(None, None, ("dp", "tensor")),
            P(None, None, None, ("dp", "tensor")),
            P(None, None, None, ("dp", "tensor")),
            P(None, None, None, ("dp", "tensor")),
        ),
        check_vma=False,
    )
```

```python
import functools

import jax
import jax.numpy as jnp
from jax import lax
from jax.experimental import pallas as pl
from jax.experimental.pallas import tpu as pltpu
from jax.sharding import PartitionSpec as P

D = 2304
HQ = 8
KV = 4
HD = 256
FF = 9216
NA = 8
RANK = 16
LEN = 1024
LANES = 128

EPSILON = 1e-06
SOFT_CAP = 50.0
MESH = pl.DeviceIdType.MESH
BF16 = jnp.bfloat16
F32 = jnp.float32
VMEM_LIMIT = 48 * 1024 * 1024
BLOCK = 32


def rms_norm(values, gain_row):
    return (
        values * lax.rsqrt(jnp.mean(values * values, axis=-1, keepdims=True) + EPSILON) * gain_row
    )


def norm_back(values, gain_row, gradient):
    inverse = lax.rsqrt(jnp.mean(values * values, axis=-1, keepdims=True) + EPSILON)
    scaled = gradient * gain_row
    normed = values * inverse
    return inverse * (scaled - normed * jnp.mean(scaled * normed, axis=-1, keepdims=True))


def gelu_parts(gate, up):
    scale = (2.0 / jnp.pi) ** 0.5
    square = gate * gate
    bend = jnp.tanh(scale * gate * (1.0 + 0.044715 * square))
    low = 0.5 * (1.0 + bend)
    gelu = gate * low
    slope = low + 0.5 * gate * (1.0 - bend * bend) * (scale * (1.0 + 3.0 * 0.044715 * square))
    return (gelu * up).astype(BF16), (slope * up).astype(BF16), gelu.astype(BF16)


def tables(length, size):
    half_size = size // 2
    frequency = 10000.0 ** (-2.0 * jnp.arange(half_size, dtype=F32) / size)
    angles = jnp.arange(length, dtype=F32)[:, None] * frequency[None, :]
    return (jnp.cos(angles)[:, None, :], jnp.sin(angles)[:, None, :])


def rotate(values, cosine, sine):
    half_size = values.shape[-1] // 2
    first_half = values[..., :half_size]
    second_half = values[..., half_size:]
    return jnp.concatenate(
        [first_half * cosine - second_half * sine, second_half * cosine + first_half * sine],
        axis=-1,
    )


def nn(a, b):
    return lax.dot_general(a, b, (((1,), (0,)), ((), ())), preferred_element_type=F32)


def nt(a, b):
    return lax.dot_general(a, b, (((1,), (1,)), ((), ())), preferred_element_type=F32)


def tn(a, b):
    return lax.dot_general(a, b, (((0,), (0,)), ((), ())), preferred_element_type=F32)


def pad_lanes(values):
    return jnp.pad(values, [(0, 0)] * (values.ndim - 1) + [(0, LANES - values.shape[-1])])


QUERY, KEY, VALUE, GATE, UP, OUT, DOWN = (
    slice(i * RANK, (i + 1) * RANK) for i in range(7)
)


def band(values, first, last=None):
    lane = lax.broadcasted_iota(jnp.int32, values.shape, 1)
    keep = (lane >= first.start) & (lane < (last or first).stop)
    return jnp.where(keep, values, 0.0)


def lanes(*parts):
    pieces, at = [], 0
    for place, values in parts:
        if place.start > at:
            pieces.append(jnp.zeros(values.shape[:-1] + (place.start - at,), values.dtype))
        pieces.append(values)
        at = place.start + values.shape[-1]
    last = parts[-1][1]
    pieces.append(jnp.zeros(last.shape[:-1] + (LANES - at,), last.dtype))
    return jnp.concatenate(pieces, axis=-1)


def call(peers):
    barrier = pltpu.get_barrier_semaphore()
    for peer in peers:
        pl.semaphore_signal(barrier, inc=1, device_id=peer, device_id_type=MESH)


def greet(peers):
    call(peers)
    pl.semaphore_wait(pltpu.get_barrier_semaphore(), len(peers))


def square_peers(index):
    return index + 1 - 2 * lax.rem(index, 2), lax.rem(index + 2, 4), 3 - index


def remote(source, target, send_sem, recv_sem, peer):
    return pltpu.make_async_remote_copy(
        src_ref=source,
        dst_ref=target,
        send_sem=send_sem,
        recv_sem=recv_sem,
        device_id={"tensor": peer},
        device_id_type=MESH,
    )


class PlainGather:
    def __init__(self, me, x_ref, o_ref, local_sem, send_sem, recv_sem):
        rows = x_ref.shape[0]
        half = rows // 2
        links = square_peers(me)[:2]
        self.own = pltpu.make_async_copy(x_ref, o_ref.at[pl.ds(me * rows, rows)], local_sem)
        self.first, self.second, self.onward = [], [], []
        for order, group in enumerate((self.first, self.second)):
            for link in range(2):
                part = link if order == 0 else 1 - link
                group.append(
                    remote(
                        x_ref.at[pl.ds(part * half, half)],
                        o_ref.at[pl.ds(me * rows + part * half, half)],
                        send_sem.at[link, part],
                        recv_sem.at[link, part],
                        links[link],
                    )
                )
        for link in range(2):
            block = o_ref.at[pl.ds(links[link] * rows + link * half, half)]
            self.onward.append(
                remote(block, block, send_sem.at[2, link], recv_sem.at[2, link], links[1 - link])
            )

    def start(self):
        self.own.start()
        for copy in self.first + self.second:
            copy.start()

    def forward(self):
        for copy, onward in zip(self.first, self.onward):
            copy.wait_recv()
            onward.start()

    def finish(self):
        for copy in self.second + self.onward:
            copy.wait_recv()
        self.own.wait()
        for copy in self.first + self.second + self.onward:
            copy.wait_send()


def gather_kernel(count, rows, x_ref, o_ref, local_sem, send_sem, recv_sem):
    me = lax.axis_index("tensor")
    if count == 4:
        across, down, _ = square_peers(me)
        greet([{"tensor": across}, {"tensor": down}])
        gather = PlainGather(me, x_ref, o_ref, local_sem, send_sem, recv_sem)
        gather.start()
        gather.forward()
        gather.finish()
    else:
        peers = [lax.rem(me + step, count) for step in range(1, count)]
        greet([{"tensor": peer} for peer in peers])
        own = pltpu.make_async_copy(x_ref, o_ref.at[pl.ds(me * rows, rows)], local_sem)
        own.start()
        copies = []
        for step, peer in enumerate(peers):
            copy = remote(
                x_ref,
                o_ref.at[pl.ds(me * rows, rows)],
                send_sem.at[0, step],
                recv_sem.at[0, step],
                peer,
            )
            copy.start()
            copies.append(copy)
        own.wait()
        for copy in copies:
            copy.wait()


def tensor_gather(values, count):
    rows, width = values.shape
    slots = max(2, count - 1)
    return pl.pallas_call(
        functools.partial(gather_kernel, count, rows),
        out_shape=jax.ShapeDtypeStruct((count * rows, width), values.dtype),
        in_specs=[pl.BlockSpec(memory_space=pl.ANY)],
        out_specs=pl.BlockSpec(memory_space=pl.ANY),
        scratch_shapes=[
            pltpu.SemaphoreType.DMA,
            pltpu.SemaphoreType.DMA((3, slots)),
            pltpu.SemaphoreType.DMA((3, slots)),
        ],
        compiler_params=pltpu.CompilerParams(
            collective_id=1, has_side_effects=True, vmem_limit_bytes=VMEM_LIMIT
        ),
        name="tensor_gather",
    )(values)


def scatter_kernel(count, rows, p_ref, q_ref, o_ref, l_ref, *scratch):
    me = lax.axis_index("tensor")
    payload = ((p_ref, o_ref), (q_ref, l_ref))
    if count == 4:
        across, down, far = square_peers(me)
        greet([{"tensor": across}, {"tensor": down}])
        half = rows // 2
        first = scratch[0:2]
        sums = scratch[2:4]
        second = scratch[4:6]
        send_sem, recv_sem = scratch[6], scratch[7]
        links = (across, down)
        copies = {}
        for which in (1, 0):
            for link in range(2):
                block = far if which == 1 else links[link]
                for item in range(2):
                    copy = remote(
                        payload[item][0].at[pl.ds(block * rows + link * half, half)],
                        first[item].at[link, which],
                        send_sem.at[item, link, which],
                        recv_sem.at[item, link, which],
                        links[link],
                    )
                    copy.start()
                    copies[item, link, which] = copy
        for link in range(2):
            block = links[1 - link]
            for item in range(2):
                copies[item, link, 1].wait_recv()
                mine = payload[item][0][pl.ds(block * rows + link * half, half), :]
                sums[item][link] = (
                    mine.astype(F32) + first[item][link, 1].astype(F32)
                ).astype(BF16)
                copy = remote(
                    sums[item].at[link],
                    second[item].at[link],
                    send_sem.at[item, link, 2],
                    recv_sem.at[item, link, 2],
                    links[1 - link],
                )
                copy.start()
                copies[item, link, 2] = copy
        for link in range(2):
            for item in range(2):
                copies[item, link, 0].wait_recv()
                mine = payload[item][0][pl.ds(me * rows + link * half, half), :]
                payload[item][1][pl.ds(link * half, half), :] = mine.astype(F32) + first[item][
                    link, 0
                ].astype(F32)
        for link in range(2):
            for item in range(2):
                copies[item, link, 2].wait_recv()
                payload[item][1][pl.ds(link * half, half), :] += second[item][link].astype(F32)
        for copy in copies.values():
            copy.wait_send()
    else:
        peers = [lax.rem(me + step, count) for step in range(1, count)]
        greet([{"tensor": peer} for peer in peers])
        first = scratch[0:2]
        send_sem, recv_sem = scratch[2], scratch[3]
        copies = []
        for step, peer in enumerate(peers):
            for item in range(2):
                copy = remote(
                    payload[item][0].at[pl.ds(peer * rows, rows)],
                    first[item].at[step],
                    send_sem.at[item, step],
                    recv_sem.at[item, step],
                    peer,
                )
                copy.start()
                copies.append((item, step, copy))
        for item in range(2):
            payload[item][1][...] = payload[item][0][pl.ds(me * rows, rows), :].astype(F32)
        for item, step, copy in copies:
            copy.wait()
            payload[item][1][...] += first[item][step].astype(F32)


def tensor_scatter(values, narrow, count):
    rows = values.shape[0] // count
    widths = (values.shape[1], narrow.shape[1])
    if count == 4:
        half = rows // 2
        scratch = [pltpu.VMEM((2, 2, half, width), BF16) for width in widths]
        scratch += [pltpu.VMEM((2, half, width), BF16) for width in widths]
        scratch += [pltpu.VMEM((2, half, width), BF16) for width in widths]
        scratch += [pltpu.SemaphoreType.DMA((2, 2, 3)), pltpu.SemaphoreType.DMA((2, 2, 3))]
    else:
        scratch = [pltpu.VMEM((count - 1, rows, width), BF16) for width in widths]
        scratch += [pltpu.SemaphoreType.DMA((2, count - 1))] * 2
    vmem = pl.BlockSpec(memory_space=pltpu.VMEM)
    return pl.pallas_call(
        functools.partial(scatter_kernel, count, rows),
        out_shape=tuple(jax.ShapeDtypeStruct((rows, width), F32) for width in widths),
        in_specs=[vmem, vmem],
        out_specs=(vmem, vmem),
        scratch_shapes=scratch,
        compiler_params=pltpu.CompilerParams(
            collective_id=2, has_side_effects=True, vmem_limit_bytes=VMEM_LIMIT
        ),
        name="tensor_scatter",
    )(values, narrow)


class Square:
    def __init__(self, rows):
        self.rows = rows
        self.half = rows // 2
        self.me = lax.axis_index("tensor")
        self.across, self.down, self.far = square_peers(self.me)
        self.links = (self.across, self.down)

    def greet(self, far=False):
        greet([{"tensor": peer} for peer in (self.across, self.down) + ((self.far,) if far else ())])

    def spread(self, source_at, target, send_sem, recv_sem):
        copies = [pltpu.make_async_copy(source_at(self.me), target.at[self.me], recv_sem.at[0])]
        for which, peer in enumerate((self.across, self.down, self.far)):
            copies.append(
                remote(
                    source_at(peer),
                    target.at[self.me],
                    send_sem.at[which],
                    recv_sem.at[1 + which],
                    peer,
                )
            )
        return copies


def along(source_at, target, send_sem, recv_sem):
    dp = lax.axis_size("dp")
    d = lax.axis_index("dp")
    pltpu.make_async_copy(source_at(d), target.at[d], recv_sem).start()
    copies = []
    for step in range(1, dp):
        peer = lax.rem(d + step, dp)
        copy = pltpu.make_async_remote_copy(
            src_ref=source_at(peer),
            dst_ref=target.at[d],
            send_sem=send_sem.at[step],
            recv_sem=recv_sem,
            device_id={"dp": peer},
            device_id_type=MESH,
        )
        copy.start()
        copies.append(copy)
    return copies


class ChunkGather:
    def __init__(self, sq, source, buf, send_sem, recv_sem):
        half = sq.half
        self.first, self.second, self.onward = [], [], []
        for link in range(2):
            for order in range(2):
                part = link if order == 0 else 1 - link
                copy = remote(
                    source.at[pl.ds(part * half, half)],
                    buf.at[1 + order, pl.ds(link * half, half)],
                    send_sem.at[2 * order + link],
                    recv_sem.at[2 * order + link],
                    sq.links[link],
                )
                (self.first if order == 0 else self.second).append(copy)
            self.onward.append(
                remote(
                    buf.at[1, pl.ds(link * half, half)],
                    buf.at[3, pl.ds(link * half, half)],
                    send_sem.at[4 + link],
                    recv_sem.at[4 + link],
                    sq.links[1 - link],
                )
            )

    def start(self):
        for copy in self.first + self.second:
            copy.start()

    def wait_chunk(self, chunk):
        if chunk == 1:
            for copy in self.first:
                copy.wait_recv()
            for copy in self.onward:
                copy.start()
        if chunk == 2:
            for copy in self.second:
                copy.wait_recv()
        if chunk == 3:
            for copy in self.onward:
                copy.wait_recv()

    def finish(self):
        for copy in self.first + self.second + self.onward:
            copy.wait_send()


class ChunkScatter:
    def __init__(self, sq, part, landing, passed, send_sem, recv_sem):
        self.sq, self.half = sq, sq.half
        self.part, self.landing, self.passed = part, landing, passed
        self.send_sem, self.recv_sem = send_sem, recv_sem
        self.tiles = send_sem.shape[-1]
        self.width = part.shape[-1] // self.tiles

    def columns(self, tile):
        if self.tiles == 1:
            return pl.ds(0, self.width)
        return columns(tile, self.width)

    def copy(self, kind, link, tile):
        rows = pl.ds(link * self.half, self.half)
        cols = self.columns(tile)
        source = (
            self.passed.at[link, :, cols]
            if kind == 2
            else self.part.at[1 + 2 * kind, rows, cols]
        )
        slot = 2 * kind + link
        return remote(
            source,
            self.landing.at[slot, :, cols],
            self.send_sem.at[slot, tile],
            self.recv_sem.at[slot, tile],
            self.sq.links[1 - link if kind == 2 else link],
        )

    def send(self, kind, tile):
        for link in range(2):
            self.copy(kind, link, tile).start()

    def send_own(self):
        for tile in range(self.tiles):
            self.send(0, tile)

    def send_far(self):
        for tile in range(self.tiles):
            self.send(1, tile)

    def pass_on(self):
        for tile in range(self.tiles):
            cols = self.columns(tile)
            for link in range(2):
                self.copy(1, link, tile).wait_recv()
                rows = pl.ds((1 - link) * self.half, self.half)
                mine = self.part[2, rows, cols].astype(F32)
                self.passed[link, :, cols] = (
                    mine + self.landing[2 + link, :, cols].astype(F32)
                ).astype(BF16)
                self.copy(2, link, tile).start()

    def arrived(self):
        for kind in (0, 2):
            for tile in range(self.tiles):
                for link in range(2):
                    self.copy(kind, link, tile).wait_recv()

    def collect(self, out_ref, places=((0, 0),)):
        self.arrived()
        for link in range(2):
            rows = pl.ds(link * self.half, self.half)
            total = (
                self.part[0, rows, :].astype(F32)
                + self.landing[link].astype(F32)
                + self.landing[4 + link].astype(F32)
            )
            size = self.part.shape[-1] // len(places)
            for source, target in places:
                out_ref[rows, target : target + size] = total[:, source : source + size]

    def finish(self):
        for kind in range(3):
            for tile in range(self.tiles):
                for link in range(2):
                    self.copy(kind, link, tile).wait_send()


def scatter_scratch(rows, width, tiles=1):
    half = rows // 2
    return [
        pltpu.VMEM((4, rows, width), BF16),
        pltpu.VMEM((6, half, width), BF16),
        pltpu.VMEM((2, half, width), BF16),
        pltpu.SemaphoreType.DMA((6, tiles)),
        pltpu.SemaphoreType.DMA((6, tiles)),
    ]


def tile_of(width):
    return 768 if width % 768 == 0 else 384


def columns(step, tile, base=0):
    return pl.ds(pl.multiple_of(base + step * tile, LANES), tile)


def mlp_back_kernel(
    rows,
    g_ref,
    down_hbm,
    gu_hbm,
    slope_hbm,
    gelu_hbm,
    hidden_hbm,
    low_hbm,
    d_ref,
    f_table,
    o_ref,
    l_ref,
    f_out,
    f_ref,
    f_send,
    down_w,
    gu_w,
    buf,
    slope,
    gelu,
    hidden,
    low,
    grads,
    weight_sem,
    load_sem,
    own_sem,
    gather_send,
    gather_recv,
    spread_send,
    spread_recv,
    *scratch,
):
    sq = Square(rows)
    width = hidden.shape[-1]
    model = o_ref.shape[-1]
    down_load = pltpu.make_async_copy(down_hbm, down_w, weight_sem.at[0])
    gu_load = pltpu.make_async_copy(gu_hbm, gu_w, weight_sem.at[1])
    own_load = pltpu.make_async_copy(g_ref, buf.at[0], own_sem)

    def loads(chunk):
        slot = chunk % 2
        return [
            pltpu.make_async_copy(source.at[chunk], target.at[slot], load_sem.at[slot, item])
            for item, (source, target) in enumerate(
                ((slope_hbm, slope), (gelu_hbm, gelu), (hidden_hbm, hidden), (low_hbm, low))
            )
        ]

    down_load.start()
    own_load.start()
    for copy in loads(0):
        copy.start()
    sq.greet(far=True)
    gather = ChunkGather(sq, g_ref, buf, gather_send, gather_recv)
    gather.start()
    gu_load.start()
    part, part_low = scratch[0], scratch[5]
    scatters = (ChunkScatter(sq, *scratch[:5]), ChunkScatter(sq, *scratch[5:10]))
    f_ref[...] = jnp.zeros_like(f_ref)
    own_load.wait()
    down_load.wait()

    @pl.loop(0, 4)
    def _(chunk):
        slot = lax.rem(chunk, 2)
        for step in range(4):

            @pl.when(chunk == step)
            def _(step=step):
                gather.wait_chunk(step)
                for copy in loads(step):
                    copy.wait()
                if step < 3:
                    for copy in loads(step + 1):
                        copy.start()

        incoming = buf.at[chunk]
        low_down = band(nn(incoming[...], d_ref[...]), DOWN).astype(BF16)
        tile = tile_of(width)

        @pl.loop(0, width // tile)
        def _(step):
            here = columns(step, tile)
            grad = nn(incoming[...], down_w[:, here]) + nt(low_down, f_table[here, :])
            grads[:, here] = (grad * slope[slot, :, here].astype(F32)).astype(BF16)
            grads[:, columns(step, tile, width)] = (
                grad * gelu[slot, :, here].astype(F32)
            ).astype(BF16)

        @pl.when(chunk == 0)
        def _():
            gu_load.wait()

        part_low[chunk] = (
            band(nn(grads[:, :width], f_table[...]), GATE)
            + band(nn(grads[:, width:], f_table[...]), UP)
        ).astype(BF16)
        wide = tile_of(model)

        @pl.loop(0, model // wide)
        def _(step):
            here = columns(step, wide)
            part[chunk, :, here] = nt(grads[...], gu_w[here, :]).astype(BF16)

            @pl.when(chunk == 1)
            def _():
                scatters[0].send(0, step)

            @pl.when(chunk == 3)
            def _():
                scatters[0].send(1, step)

        @pl.when(chunk == 1)
        def _():
            scatters[1].send_own()

        @pl.when(chunk == 3)
        def _():
            scatters[1].send_far()

        low_turned = low_down.astype(F32).T.astype(BF16)
        gu_turned = low[slot].astype(F32).T.astype(BF16)
        f_ref[:RANK, :] += nn(low_turned[DOWN], hidden[slot])
        f_ref[RANK : 2 * RANK, :] += nn(gu_turned[GATE], grads[:, :width])
        f_ref[2 * RANK : 3 * RANK, :] += nn(gu_turned[UP], grads[:, width:])

    cores, slices = f_send.shape[:2]
    size = width // (cores * slices)
    for core in range(cores):
        for peer in range(slices):
            first = (core * slices + peer) * size
            f_send[core, peer] = f_ref[: 3 * RANK, first : first + size].astype(BF16)
    spread = sq.spread(lambda peer: f_send.at[:, peer], f_out, spread_send, spread_recv)
    for copy in spread:
        copy.start()
    for scatter in scatters:
        scatter.pass_on()
    gather.finish()
    scatters[0].collect(o_ref)
    scatters[1].collect(l_ref)
    for scatter in scatters:
        scatter.finish()
    for copy in spread:
        copy.wait()


def mlp_back_fused(grad, down_w, gu_w, slope, gelu, hidden, low, d_tab, f_tab, dp):
    rows, model = grad.shape
    width = hidden.shape[2]
    messages = (dp // 4, 4, 3 * RANK, width // dp)
    anywhere = pl.BlockSpec(memory_space=pl.ANY)
    vmem = pl.BlockSpec(memory_space=pltpu.VMEM)
    return pl.pallas_call(
        functools.partial(mlp_back_kernel, rows),
        out_shape=(
            jax.ShapeDtypeStruct((rows, model), F32),
            jax.ShapeDtypeStruct((rows, LANES), F32),
            jax.ShapeDtypeStruct((4, dp // 4, 3 * RANK, width // dp), BF16),
        ),
        in_specs=[vmem] + [anywhere] * 6 + [vmem] * 2,
        out_specs=(vmem,) * 3,
        scratch_shapes=[
            pltpu.VMEM((3 * RANK, width), F32),
            pltpu.VMEM(messages, BF16),
            pltpu.VMEM((model, width), BF16),
            pltpu.VMEM((model, 2 * width), BF16),
            pltpu.VMEM((4, rows, model), BF16),
            pltpu.VMEM((2, rows, width), BF16),
            pltpu.VMEM((2, rows, width), BF16),
            pltpu.VMEM((2, rows, width), BF16),
            pltpu.VMEM((2, rows, LANES), BF16),
            pltpu.VMEM((rows, 2 * width), BF16),
            pltpu.SemaphoreType.DMA((2,)),
            pltpu.SemaphoreType.DMA((2, 4)),
            pltpu.SemaphoreType.DMA,
            pltpu.SemaphoreType.DMA((6,)),
            pltpu.SemaphoreType.DMA((6,)),
            pltpu.SemaphoreType.DMA((3,)),
            pltpu.SemaphoreType.DMA((4,)),
        ]
        + scatter_scratch(rows, model, model // tile_of(model))
        + scatter_scratch(rows, LANES),
        compiler_params=pltpu.CompilerParams(
            collective_id=5, has_side_effects=True, vmem_limit_bytes=62 * 1024 * 1024
        ),
        name="mlp_back",
    )(grad, down_w, gu_w, slope, gelu, hidden, low, d_tab, f_tab)


def front_kernel(
    ids_ref,
    layer_ref,
    gains_ref,
    f_all,
    d_all,
    hk_all,
    seq_out,
    ids_out,
    d_out,
    f_out,
    h_out,
    k_out,
    normed,
    ids_land,
    f_pick,
    d_pick,
    hk_pick,
    f_mid,
    d_mid,
    hk_mid,
    d_join,
    f_land,
    d_land,
    hk_land,
    d_flip,
    f_flip,
    h_flip,
    k_flip,
    local_sem,
    gather_send,
    gather_recv,
    line_send,
    line_recv,
    group_send,
    group_recv,
):
    rows = layer_ref.shape[0]
    sq = Square(rows)
    dp = lax.axis_size("dp")
    d = lax.axis_index("dp")
    peers = [{"tensor": peer} for peer in (sq.across, sq.down, sq.far)]
    peers += [{"dp": lax.rem(d + step, dp)} for step in range(1, dp)]
    call(peers)

    @pl.loop(0, rows // BLOCK)
    def _(step):
        here = pl.ds(pl.multiple_of(step * BLOCK, BLOCK), BLOCK)
        normed[here, :] = rms_norm(layer_ref[here, :].astype(F32), gains_ref[0:1, :]).astype(BF16)

    pl.semaphore_wait(pltpu.get_barrier_semaphore(), len(peers))
    line = along(lambda k: ids_ref, ids_land, line_send.at[0], line_recv.at[0])
    gather = PlainGather(sq.me, normed, seq_out, local_sem, gather_send, gather_recv)
    gather.start()
    pltpu.make_async_copy(ids_land, ids_land, line_recv.at[0]).wait()
    ids_out[...] = ids_land[...]

    @pl.loop(0, dp)
    def _(k):
        for source, target in ((f_all, f_pick), (d_all, d_pick), (hk_all, hk_pick)):
            total = None
            for adapter in range(NA):
                hit = jnp.broadcast_to(ids_land[k, 0:1, 0:1], source.shape[1:]) == adapter
                mine = jnp.where(hit, source[adapter].astype(F32), 0.0)
                total = mine if total is None else total + mine
            target[k] = total.astype(BF16)

    lands = (f_mid, d_mid, hk_mid)
    for item, (source, target) in enumerate(zip((f_pick, d_pick, hk_pick), lands)):
        line += along(
            lambda k, source=source: source.at[k],
            target,
            line_send.at[1 + item],
            line_recv.at[1 + item],
        )
    gather.forward()
    for flip in (d_flip, f_flip, h_flip, k_flip):
        flip[...] = jnp.zeros_like(flip)
    for item, target in enumerate(lands):
        pltpu.make_async_copy(target, target, line_recv.at[1 + item]).wait()
    size = d_mid.shape[2]
    for k in range(dp):
        d_join[:, k * size : (k + 1) * size] = d_mid[k]
    per_user = dp // 4
    spread = [
        sq.spread(lambda peer: d_join, d_land, group_send.at[0], group_recv.at[0]),
        sq.spread(
            lambda peer: f_mid.at[pl.ds(peer * per_user, per_user)],
            f_land,
            group_send.at[1],
            group_recv.at[1],
        ),
        sq.spread(
            lambda peer: hk_mid.at[pl.ds(peer * per_user, per_user)],
            hk_land,
            group_send.at[2],
            group_recv.at[2],
        ),
    ]
    for copies in spread:
        for copy in copies:
            copy.start()
    for copies in spread:
        copies[0].wait()
        for copy in copies[1:]:
            copy.wait_recv()
    f_size, h_size, k_size = f_mid.shape[2], h_out.shape[0] // dp, k_out.shape[0] // dp
    for t in range(4):
        for k in range(dp):
            at = (k * 4 + t) * size
            d_flip[: DOWN.stop, at : at + size] = d_land[
                t, :, k * size : (k + 1) * size
            ].astype(F32)
        for core in range(per_user):
            at = (core * 4 + t) * f_size
            piece = f_land[t, core].astype(F32)
            f_flip[GATE.start : UP.stop, at : at + f_size] = piece[: 2 * RANK]
            f_flip[DOWN, at : at + f_size] = piece[2 * RANK :]
            piece = hk_land[t, core].astype(F32)
            at = (core * 4 + t) * h_size
            h_flip[OUT, at : at + h_size] = piece[:RANK, :h_size]
            h_flip[QUERY, at : at + h_size] = piece[RANK : 2 * RANK, :h_size]
            at = (core * 4 + t) * k_size
            k_flip[KEY.start : VALUE.stop, at : at + k_size] = piece[2 * RANK :, :k_size]
    for flip, out in ((d_flip, d_out), (f_flip, f_out), (h_flip, h_out), (k_flip, k_out)):

        @pl.loop(0, out.shape[0] // LANES)
        def _(step, flip=flip, out=out):
            here = columns(step, LANES)
            out[here, :] = flip[:, here].T.astype(BF16)

    gather.finish()
    for copies in spread:
        for copy in copies[1:]:
            copy.wait_send()
    for copy in line:
        copy.wait_send()


def front(ids, layer_in, gains, f_all, d_all, hk_all, dp, widths):
    rows, model = layer_in.shape
    anywhere = pl.BlockSpec(memory_space=pl.ANY)
    vmem = pl.BlockSpec(memory_space=pltpu.VMEM)
    tables_in = (f_all, d_all, hk_all)
    shapes = [(dp,) + table.shape[1:] for table in tables_in]
    joined = (shapes[1][1], dp * shapes[1][2])
    return pl.pallas_call(
        front_kernel,
        out_shape=(
            jax.ShapeDtypeStruct((4 * rows, model), BF16),
            jax.ShapeDtypeStruct((dp,) + ids.shape, jnp.int32),
        )
        + tuple(jax.ShapeDtypeStruct((width, LANES), BF16) for width in widths),
        in_specs=[vmem] * 6,
        out_specs=(anywhere,) + (vmem,) * 5,
        scratch_shapes=[
            pltpu.VMEM((rows, model), BF16),
            pltpu.VMEM((dp,) + ids.shape, jnp.int32),
        ]
        + [pltpu.VMEM(shape, BF16) for shape in shapes] * 2
        + [
            pltpu.VMEM(joined, BF16),
            pltpu.VMEM((4, dp // 4) + shapes[0][1:], BF16),
            pltpu.VMEM((4,) + joined, BF16),
            pltpu.VMEM((4, dp // 4) + shapes[2][1:], BF16),
        ]
        + [pltpu.VMEM((LANES, width), F32) for width in widths]
        + [
            pltpu.SemaphoreType.DMA,
            pltpu.SemaphoreType.DMA((3, 2)),
            pltpu.SemaphoreType.DMA((3, 2)),
            pltpu.SemaphoreType.DMA((4, dp)),
            pltpu.SemaphoreType.DMA((4,)),
            pltpu.SemaphoreType.DMA((3, 3)),
            pltpu.SemaphoreType.DMA((3, 4)),
        ],
        compiler_params=pltpu.CompilerParams(
            collective_id=9, has_side_effects=True, vmem_limit_bytes=VMEM_LIMIT
        ),
        name="front",
    )(ids, layer_in, gains, *tables_in)


class Line:
    def __init__(self, slots, send_sem, recv_sem):
        self.d = lax.axis_index("dp")
        self.places = lax.axis_size("dp") // 2
        self.core = lax.rem(self.d, 2)
        self.z = self.d // 2
        self.sibling = self.d + 1 - 2 * self.core
        self.slots, self.send_sem, self.recv_sem = slots, send_sem, recv_sem

    def greet(self, others):
        barrier = pltpu.get_barrier_semaphore()
        for peer in others + [{"dp": self.sibling}]:
            pl.semaphore_signal(barrier, inc=1, device_id=peer, device_id_type=MESH)

        @pl.when(self.z > 0)
        def _():
            pl.semaphore_signal(
                barrier, inc=1, device_id={"dp": self.d - 2}, device_id_type=MESH
            )

        @pl.when(self.z < self.places - 1)
        def _():
            pl.semaphore_signal(
                barrier, inc=1, device_id={"dp": self.d + 2}, device_id_type=MESH
            )

        last = self.places - 1
        ends = (last - self.z) // last + self.z // last
        pl.semaphore_wait(barrier, len(others) + 3 - ends)

    def copy(self, place, kind, part):
        target = (self.d + 2, self.d - 2, self.sibling)[kind]
        slot = 2 * place + self.core
        half = self.slots.shape[1] // 2
        block = self.slots.at[slot, pl.ds(part * half, half)]
        return pltpu.make_async_remote_copy(
            src_ref=block,
            dst_ref=block,
            send_sem=self.send_sem.at[kind, place, part],
            recv_sem=self.recv_sem.at[slot, part],
            device_id={"dp": target},
            device_id_type=MESH,
        )

    def send_up(self, place, part):
        @pl.when(self.z < self.places - 1)
        def _():
            self.copy(place, 0, part).start()

    def send_down(self, place, part):
        @pl.when(self.z > 0)
        def _():
            self.copy(place, 1, part).start()

    def start(self):
        for part in range(2):
            self.send_up(self.z, part)
            self.send_down(self.z, part)
            self.copy(self.z, 2, part).start()

    def arrive(self, distance, part):
        @pl.when(self.z >= distance)
        def _():
            place = self.z - distance
            self.copy(place, 2, part).wait_recv()
            self.send_up(place, part)
            self.copy(place, 2, part).start()

        @pl.when(self.z + distance < self.places)
        def _():
            place = self.z + distance
            self.copy(place, 2, part).wait_recv()
            self.send_down(place, part)
            self.copy(place, 2, part).start()

    def wait_sibling(self, place, part):
        half = self.slots.shape[1] // 2
        other = 2 * place + 1 - self.core
        block = self.slots.at[other, pl.ds(part * half, half)]
        pltpu.make_async_copy(block, block, self.recv_sem.at[other, part]).wait()

    def finish(self):
        for place in range(self.places):
            for part in range(2):

                @pl.when((self.z >= place) & (self.z < self.places - 1))
                def _(place=place, part=part):
                    self.copy(place, 0, part).wait_send()

                @pl.when((self.z <= place) & (self.z > 0))
                def _(place=place, part=part):
                    self.copy(place, 1, part).wait_send()

                self.copy(place, 2, part).wait_send()


ARRIVALS = ((0, 1, 2, 3), (1, 0, 2, 3), (2, 1, 3, 0), (3, 2, 1, 0))


def mlp_kernel(
    rows,
    length_ref,
    x_hbm,
    gu_hbm,
    shard_hbm,
    d_ref,
    f_table,
    resid_ref,
    cot_ref,
    gains_ref,
    layer_ref,
    grad_ref,
    low_ref,
    low_down_ref,
    hidden_out,
    slope_out,
    gelu_out,
    down_out,
    work,
    low_sum,
    lows,
    seq,
    tiles,
    hidden,
    slope,
    gelu,
    down,
    load_sem,
    tile_sem,
    store_sem,
    keep_sem,
    line_send,
    line_recv,
    part,
    landing,
    passed,
    part_send,
    part_recv,
    *low_scratch,
):
    sq = Square(rows)
    line = Line(down, line_send, line_recv)
    width = hidden.shape[-1]
    tile = tiles.shape[-1] // 2
    steps = width // tile
    own_shard = pltpu.make_async_copy(shard_hbm, down.at[line.d], load_sem.at[0])
    seq_load = pltpu.make_async_copy(x_hbm, seq, load_sem.at[1])

    def tile_loads(step, slot):
        return [
            pltpu.make_async_copy(
                gu_hbm.at[:, columns(step, tile, which * width)],
                tiles.at[slot, :, pl.ds(which * tile, tile)],
                tile_sem.at[slot, which],
            )
            for which in range(2)
        ]

    def stores(step, slot):
        here = columns(step, tile)
        return [
            pltpu.make_async_copy(
                source.at[slot], target.at[:, :, here], store_sem.at[slot, which]
            )
            for which, (source, target) in enumerate(((slope, slope_out), (gelu, gelu_out)))
        ]

    own_shard.start()
    seq_load.start()
    for copy in tile_loads(0, 0):
        copy.start()
    line.greet([{"tensor": sq.across}, {"tensor": sq.down}])
    own_shard.wait()
    line.start()
    seq_load.wait()

    @pl.loop(0, 4)
    def _(chunk):
        low = nn(seq[chunk], d_ref[...])
        lows[0, chunk] = band(low, GATE).astype(BF16)
        lows[1, chunk] = band(low, UP).astype(BF16)
        low_ref[chunk] = band(low, GATE, UP).astype(BF16)

    @pl.loop(0, steps)
    def _(step):
        slot = lax.rem(step, 2)
        for copy in tile_loads(step, slot):
            copy.wait()

        @pl.when(step + 1 < steps)
        def _():
            for copy in tile_loads(step + 1, 1 - slot):
                copy.start()

        @pl.when(step >= 2)
        def _():
            for copy in stores(step - 2, slot):
                copy.wait()

        here = columns(step, tile)

        @pl.loop(0, 4)
        def _(chunk):
            both = nn(seq[chunk], tiles[slot])
            gate = both[:, :tile] + nt(lows[0, chunk], f_table[here, :])
            up = both[:, tile:] + nt(lows[1, chunk], f_table[here, :])
            hidden[chunk, :, here], slope[slot, chunk], gelu[slot, chunk] = gelu_parts(gate, up)

        for copy in stores(step, slot):
            copy.start()

        for part_at, part_of in ((steps // 2 - 1, 0), (steps - 2, 1)):

            @pl.when(step == part_at)
            def _(part_of=part_of):
                line.arrive(1, part_of)

    keep_hidden = pltpu.make_async_copy(hidden, hidden_out, keep_sem.at[0])
    keep_hidden.start()
    last = line.places - 1
    is_first, is_last = (last - line.z) // last, line.z // last
    is_third = line.z // 2 - is_last
    is_here = (is_first, 1 - is_first - is_third - is_last, is_third, is_last)
    order = [sum(flag * ARRIVALS[z][i] for z, flag in enumerate(is_here)) for i in range(4)]

    def scatter_at(place, half):
        at = 2 * place + half
        return ChunkScatter(
            sq, part.at[at], landing.at[at], passed.at[at], part_send.at[at], part_recv.at[at]
        )

    low_scatter = ChunkScatter(sq, *low_scratch)

    @pl.loop(0, 4)
    def _(chunk):
        low_scratch[0][chunk] = band(nn(hidden[chunk], f_table[...]), DOWN).astype(BF16)

    low_scatter.send_far()
    low_scatter.send_own()
    keeps = []
    earlier = low_scatter
    half_rows = down.shape[1] // 2
    arrivals = {(1, 0): ((2, 0),), (2, 0): ((2, 1),), (3, 0): ((3, 0),), (3, 1): ((3, 1),)}
    for turn in range(4):
        place = order[turn]
        for half in range(2):
            for distance, piece in arrivals.get((turn, half), ()):
                line.arrive(distance, piece)
            line.wait_sibling(place, half)
            scatter = scatter_at(place, half)

            @pl.loop(0, 4)
            def _(step, place=place, half=half, scatter=scatter):
                chunk = far_first(step)
                for core in range(2):
                    part[
                        2 * place + half, chunk, :, core * half_rows : (core + 1) * half_rows
                    ] = nt(
                        hidden[chunk],
                        down[2 * place + core, half * half_rows : (half + 1) * half_rows],
                    ).astype(BF16)

                @pl.when(step == 0)
                def _():
                    scatter.send_far()

                @pl.when(step == 1)
                def _():
                    scatter.send_own()

            earlier.pass_on()
            earlier = scatter
        pair = pl.ds(2 * place, 2)
        keep = pltpu.make_async_copy(down.at[pair], down_out.at[pair], keep_sem.at[1 + turn])
        keep.start()
        keeps.append(keep)
    low_scatter.collect(low_sum)
    low_down_ref[...] = low_sum[...].astype(BF16)
    earlier.pass_on()
    everything = [(place, half) for place in range(4) for half in range(2)]
    for place, half in everything:
        first = 2 * place * down.shape[1] + half * half_rows
        scatter_at(place, half).collect(
            work, ((0, first), (half_rows, first + down.shape[1]))
        )
    add_lifted(work, low_down_ref, d_ref)

    @pl.loop(0, rows // BLOCK)
    def _(step):
        here = pl.ds(pl.multiple_of(step * BLOCK, BLOCK), BLOCK)
        at = sq.me * rows + step * BLOCK + lax.broadcasted_iota(jnp.int32, (BLOCK, 1), 0)
        valid = (at < length_ref[0]).astype(F32)
        total = work[here, :]
        gain = gains_ref[3:4, :]
        layer_ref[here, :] = (valid * (resid_ref[here, :] + rms_norm(total, gain))).astype(BF16)
        grad_ref[here, :] = norm_back(total, gain, cot_ref[here, :].astype(F32) * valid).astype(
            BF16
        )

    for place, half in everything:
        scatter_at(place, half).finish()
    low_scatter.finish()
    line.finish()
    for step in (steps - 2, steps - 1):
        for copy in stores(step, step % 2):
            copy.wait()
    keep_hidden.wait()
    for keep in keeps:
        keep.wait()


def add_lifted(work, low, table):
    wide = tile_of(work.shape[1])

    @pl.loop(0, work.shape[1] // wide)
    def _(step):
        here = columns(step, wide)
        work[:, here] += nt(low[...], table[here, :])


def mlp_fused(lengths, seq, gu_w, shard, d_tab, f_tab, resid, cotangent, gains, dp):
    chunks, rows, model = seq.shape
    width = shard.shape[1]
    tile = 384
    wide = model // dp
    half = rows // 2
    anywhere = pl.BlockSpec(memory_space=pl.ANY)
    vmem = pl.BlockSpec(memory_space=pltpu.VMEM)
    saved = jax.ShapeDtypeStruct((4, rows, width), BF16)
    return pl.pallas_call(
        functools.partial(mlp_kernel, rows),
        out_shape=(
            jax.ShapeDtypeStruct((rows, model), BF16),
            jax.ShapeDtypeStruct((rows, model), BF16),
            jax.ShapeDtypeStruct((4, rows, LANES), BF16),
            jax.ShapeDtypeStruct((rows, LANES), BF16),
            saved,
            saved,
            saved,
            jax.ShapeDtypeStruct((dp,) + shard.shape, BF16),
        ),
        in_specs=[pl.BlockSpec(memory_space=pltpu.SMEM)] + [anywhere] * 3 + [vmem] * 5,
        out_specs=(vmem,) * 4 + (anywhere,) * 4,
        scratch_shapes=[
            pltpu.VMEM((rows, model), F32),
            pltpu.VMEM((rows, LANES), F32),
            pltpu.VMEM((2, 4, rows, LANES), BF16),
            pltpu.VMEM((4, rows, model), BF16),
            pltpu.VMEM((2, model, 2 * tile), BF16),
            pltpu.VMEM((4, rows, width), BF16),
            pltpu.VMEM((2, 4, rows, tile), BF16),
            pltpu.VMEM((2, 4, rows, tile), BF16),
            pltpu.VMEM((dp,) + shard.shape, BF16),
            pltpu.SemaphoreType.DMA((2,)),
            pltpu.SemaphoreType.DMA((2, 2)),
            pltpu.SemaphoreType.DMA((2, 2)),
            pltpu.SemaphoreType.DMA((5,)),
            pltpu.SemaphoreType.DMA((3, dp // 2, 2)),
            pltpu.SemaphoreType.DMA((dp, 2)),
            pltpu.VMEM((dp, 4, rows, wide), BF16),
            pltpu.VMEM((dp, 6, half, wide), BF16),
            pltpu.VMEM((dp, 2, half, wide), BF16),
            pltpu.SemaphoreType.DMA((dp, 6, 1)),
            pltpu.SemaphoreType.DMA((dp, 6, 1)),
        ]
        + scatter_scratch(rows, LANES),
        compiler_params=pltpu.CompilerParams(
            collective_id=7, has_side_effects=True, vmem_limit_bytes=62 * 1024 * 1024
        ),
        name="mlp",
    )(lengths, seq, gu_w, shard, d_tab, f_tab, resid, cotangent, gains)


class Layout:
    def __init__(self):
        self.dp = lax.axis_size("dp")
        self.tensor = lax.axis_size("tensor")
        self.total = self.dp * self.tensor
        self.d = lax.axis_index("dp")
        self.t = lax.axis_index("tensor")
        self.me = self.d * self.tensor + self.t
        self.heads_here = HQ // self.tensor
        self.ratio = HQ // KV
        self.share = max(1, self.tensor // KV)
        self.kv_owners = self.total // KV
        self.kv_head = self.t * self.heads_here // self.ratio
        self.user = self.me // self.dp
        self.kv_slice_head = self.me // self.kv_owners

    def device(self, flat):
        return {"dp": flat // self.tensor, "tensor": lax.rem(flat, self.tensor)}


def greet_all(lay):
    barrier = pltpu.get_barrier_semaphore()

    def signal(step, unused):
        peer = lax.rem(lay.me + step, lay.total)
        pl.semaphore_signal(
            barrier, inc=1, device_id=lay.device(peer), device_id_type=MESH
        )
        return unused

    lax.fori_loop(1, lay.total, signal, 0)
    pl.semaphore_wait(barrier, lay.total - 1)


def send_or_keep(lay, sends, source, target, send_sem, recv_sem, flat, maybe_own):
    def far():
        return pltpu.make_async_remote_copy(
            src_ref=source,
            dst_ref=target,
            send_sem=send_sem,
            recv_sem=recv_sem,
            device_id=lay.device(flat),
            device_id_type=MESH,
        )

    if maybe_own is None:
        copy = far()
        copy.start()
        sends.append((None, copy))
        return

    @pl.when(maybe_own)
    def _():
        pltpu.make_async_copy(source, target, recv_sem).start()

    @pl.when(jnp.logical_not(maybe_own))
    def _():
        far().start()

    sends.append((maybe_own, far()))


def finish(sends, received):
    for own, copy in sends:
        if own is None:
            copy.wait_send()
        else:

            @pl.when(jnp.logical_not(own))
            def _(copy=copy):
                copy.wait_send()

    for target, sem in received:
        pltpu.make_async_copy(target, target, sem).wait()


def tables_kernel(d_ref, f_ref, h_ref, k_ref, do_ref, fo_ref, ho_ref, ko_ref, *sems):
    lay = Layout()
    send_sems, recv_sem = sems[:4], sems[4]
    greet_all(lay)
    sends = []
    for step in range(lay.dp):
        group = lax.rem(lay.d + step, lay.dp)
        flat = group * lay.tensor + lay.user
        own = (lay.user == lay.t) if step == 0 else None
        for item, (source, target) in enumerate(((f_ref, fo_ref), (h_ref, ho_ref))):
            send_or_keep(
                lay,
                sends,
                source.at[group],
                target.at[lax.rem(lay.me, lay.dp)],
                send_sems[item].at[step],
                recv_sem.at[item],
                flat,
                own,
            )
        for extra in range(lay.share):
            user = lay.kv_slice_head * lay.share + extra
            flat = group * lay.tensor + user
            send_or_keep(
                lay,
                sends,
                k_ref.at[group],
                ko_ref.at[lax.rem(lay.me, lay.kv_owners)],
                send_sems[2].at[step, extra],
                recv_sem.at[2],
                flat,
                (user == lay.t) if step == 0 else None,
            )
    pltpu.make_async_copy(d_ref.at[lay.d], do_ref.at[lay.me], recv_sem.at[3]).start()
    for step in range(1, lay.total):
        flat = lax.rem(lay.me + step, lay.total)
        send_or_keep(
            lay,
            sends,
            d_ref.at[flat // lay.tensor],
            do_ref.at[lay.me],
            send_sems[3].at[step],
            recv_sem.at[3],
            flat,
            None,
        )
    finish(
        sends,
        (
            (fo_ref, recv_sem.at[0]),
            (ho_ref, recv_sem.at[1]),
            (ko_ref, recv_sem.at[2]),
            (do_ref, recv_sem.at[3]),
        ),
    )


def grads_kernel(d_ref, f_ref, h_ref, k_ref, do_ref, fo_ref, ho_ref, ko_ref, *sems):
    lay = Layout()
    send_sems, recv_sem = sems[:4], sems[4]
    greet_all(lay)
    sends = []
    for step in range(lay.dp):
        slot = lax.rem(lay.d + step, lay.dp)
        flat = lay.t * lay.dp + slot
        for item, (source, target) in enumerate(((f_ref, fo_ref), (h_ref, ho_ref))):
            send_or_keep(
                lay,
                sends,
                source.at[slot],
                target.at[lay.d],
                send_sems[item].at[step],
                recv_sem.at[item],
                flat,
                flat == lay.me,
            )
    for step in range(lay.kv_owners):
        slot = lax.rem(lay.d + step, lay.kv_owners)
        flat = lay.kv_head * lay.kv_owners + slot
        send_or_keep(
            lay,
            sends,
            k_ref.at[slot],
            ko_ref.at[lay.d * lay.share + lax.rem(lay.t, lay.share)],
            send_sems[2].at[step // lay.share, step % lay.share],
            recv_sem.at[2],
            flat,
            flat == lay.me,
        )
    pltpu.make_async_copy(d_ref.at[lay.me], do_ref.at[lay.me], recv_sem.at[3]).start()
    for step in range(1, lay.total):
        flat = lax.rem(lay.me + step, lay.total)
        send_or_keep(
            lay,
            sends,
            d_ref.at[flat],
            do_ref.at[lay.me],
            send_sems[3].at[step],
            recv_sem.at[3],
            flat,
            None,
        )
    finish(
        sends,
        (
            (fo_ref, recv_sem.at[0]),
            (ho_ref, recv_sem.at[1]),
            (ko_ref, recv_sem.at[2]),
            (do_ref, recv_sem.at[3]),
        ),
    )


def exchange(kernel, name, number, arrays, outs, dp, total, share):
    anywhere = pl.BlockSpec(memory_space=pl.ANY)
    return pl.pallas_call(
        kernel,
        out_shape=tuple(jax.ShapeDtypeStruct(shape, BF16) for shape in outs),
        in_specs=[anywhere] * 4,
        out_specs=(anywhere,) * 4,
        scratch_shapes=[
            pltpu.SemaphoreType.DMA((dp,)),
            pltpu.SemaphoreType.DMA((dp,)),
            pltpu.SemaphoreType.DMA((dp, share)),
            pltpu.SemaphoreType.DMA((total,)),
            pltpu.SemaphoreType.DMA((4,)),
        ],
        compiler_params=pltpu.CompilerParams(
            collective_id=number, has_side_effects=True, vmem_limit_bytes=VMEM_LIMIT
        ),
        name=name,
    )(*arrays)


def chunk_start(sq, chunk, part):
    is_own = (3 - chunk) // 3
    is_far = chunk // 3
    near = 1 - is_own - is_far
    neighbour = sq.down if part == 1 else sq.across
    block = sq.me * is_own + sq.far * is_far + neighbour * near
    other_half = chunk // 2 - is_far
    half = 1 - other_half if part == 1 else other_half
    return pl.multiple_of(block * sq.rows + half * sq.half, sq.half)


def rotate_back(values, cosine, sine):
    first, second = values[:, : HD // 2], values[:, HD // 2 :]
    return jnp.concatenate([first * cosine + second * sine, second * cosine - first * sine], axis=1)


def turned(values):
    return values.astype(F32).T.astype(BF16)


def rotate_rows(values, cosine, sine):
    first, second = values[:, : HD // 2], values[:, HD // 2 :]
    return jnp.concatenate([first * cosine - second * sine, second * cosine + first * sine], axis=1)


def softmax_weights(keys, queries, start, half, length):
    shape = (keys.shape[0], queries.shape[0])
    key_at = lax.broadcasted_iota(jnp.int32, shape, 0)
    query_at = lax.rem(lax.broadcasted_iota(jnp.int32, shape, 1), half) + start
    allowed = (key_at <= query_at) & (key_at < length)
    squash = jnp.tanh(nt(keys, queries) * (1.0 / SOFT_CAP))
    return squash, jnp.where(allowed, jnp.exp(SOFT_CAP * squash), 0.0)


def stack_heads(ref, here, heads):
    return jnp.concatenate([ref[here, h * HD : (h + 1) * HD] for h in range(heads)], axis=0)


def far_first(step):
    return step + 3 * ((3 - step) // 3) - 3 * (step // 3)


def attn_kernel(
    rows,
    length_ref,
    seq_hbm,
    weight_hbm,
    d_table,
    h_table,
    k_table,
    cos_ref,
    sin_ref,
    layer_ref,
    gains_ref,
    q_ref,
    k_ref,
    kt_ref,
    v_ref,
    attended_ref,
    inverse_ref,
    low_ref,
    low_out_ref,
    total_ref,
    resid_ref,
    normed_ref,
    mlp_out,
    w_out_all,
    h_all,
    seq,
    weight,
    vt,
    low_sum,
    load_sem,
    own_sem,
    gather_send,
    gather_recv,
    w_send,
    w_recv,
    *scratch,
):
    sq = Square(rows)
    half = sq.half
    model = total_ref.shape[-1]
    q_width = q_ref.shape[1]
    qkv_width = q_width + 2 * HD
    heads = q_width // HD
    wide = tile_of(model)
    core = lax.rem(lax.axis_index("dp"), 2)
    sibling = lax.axis_index("dp") + 1 - 2 * core
    weight_load = pltpu.make_async_copy(weight_hbm, weight, load_sem.at[0])
    seq_load = pltpu.make_async_copy(seq_hbm, seq, load_sem.at[1])
    weight_load.start()
    seq_load.start()
    greet([{"tensor": peer} for peer in (sq.across, sq.down, sq.far)] + [{"dp": sibling}])

    share = model // 2
    mine = pl.ds(pl.multiple_of(core * share, 8), share)
    own_h = pltpu.make_async_copy(h_table, h_all.at[sq.me], own_sem.at[1])
    own_h.start()
    taken, passed_on = [], []
    for which, peer in enumerate((sq.across, sq.down, sq.far)):
        taken.append(
            (
                remote(
                    weight_hbm.at[mine, pl.ds(qkv_width, q_width)],
                    w_out_all.at[sq.me, mine],
                    w_send.at[0, which],
                    w_recv.at[0, which],
                    peer,
                ),
                remote(
                    h_table, h_all.at[sq.me], w_send.at[1, which], w_recv.at[1, which], peer
                ),
            )
        )
        block = w_out_all.at[peer, mine]
        passed_on.append(
            pltpu.make_async_remote_copy(
                src_ref=block,
                dst_ref=block,
                send_sem=w_send.at[2, which],
                recv_sem=w_recv.at[2, which],
                device_id={"dp": sibling},
                device_id_type=MESH,
            )
        )
    weight_load.wait()
    seq_load.wait()

    @pl.loop(0, 4)
    def _(block):
        here = pl.ds(pl.multiple_of(block * rows, rows), rows)
        low = band(nn(seq[block], d_table[...]), QUERY, VALUE).astype(BF16)
        low_ref[here, :] = low
        cosine, sine = cos_ref[here, :], sin_ref[here, :]
        for h in range(heads):
            column = slice(h * HD, (h + 1) * HD)
            query = nn(seq[block], weight[:, column]) + nt(
                band(low.astype(F32), QUERY).astype(BF16), h_table[column, :]
            )
            q_ref[here, column] = (rotate_rows(query, cosine, sine) * HD ** (-0.5)).astype(BF16)
        key = nn(seq[block], weight[:, q_width : q_width + HD]) + nt(
            band(low.astype(F32), KEY).astype(BF16), k_table[...]
        )
        key = rotate_rows(key, cosine, sine)
        k_ref[here, :] = key.astype(BF16)
        kt_ref[:, here] = key.T.astype(BF16)
        value = nn(seq[block], weight[:, q_width + HD : qkv_width]) + nt(
            band(low.astype(F32), VALUE).astype(BF16), k_table[...]
        )
        v_ref[here, :] = value.astype(BF16)
        vt[:, here] = value.T.astype(BF16)

    for copies in taken:
        for copy in copies:
            copy.start()
    part, part_low = scratch[0], scratch[5]
    scatters = (ChunkScatter(sq, *scratch[:5]), ChunkScatter(sq, *scratch[5:10]))

    @pl.loop(0, 4)
    def _(step):
        chunk = far_first(step)
        for side in range(2):
            start = chunk_start(sq, chunk, side)
            here = pl.ds(start, half)
            unused, weights = softmax_weights(
                k_ref[...], stack_heads(q_ref, here, heads), start, half, length_ref[0]
            )
            inverse = 1.0 / jnp.sum(weights, axis=0, keepdims=True)
            mixed = nn(vt[...], (weights * inverse).astype(BF16)).T.astype(BF16)
            for h in range(heads):
                inverse_ref[h : h + 1, here] = inverse[:, h * half : (h + 1) * half]
                attended_ref[here, h * HD : (h + 1) * HD] = mixed[h * half : (h + 1) * half]

        attended = jnp.concatenate(
            [attended_ref[pl.ds(chunk_start(sq, chunk, side), half), :] for side in range(2)],
            axis=0,
        )
        part_low[chunk] = band(nn(attended, h_table[...]), OUT).astype(BF16)

        @pl.loop(0, model // wide)
        def _(tile):
            here = columns(tile, wide)
            part[chunk, :, here] = nt(attended, weight[here, qkv_width:]).astype(BF16)

            @pl.when(step == 0)
            def _():
                scatters[0].send(1, tile)

            @pl.when(step == 1)
            def _():
                scatters[0].send(0, tile)

        @pl.when(step == 0)
        def _():
            scatters[1].send_far()

        @pl.when(step == 1)
        def _():
            scatters[1].send_own()

    for scatter in scatters:
        scatter.pass_on()
    scatters[1].collect(low_sum)
    low_out_ref[...] = low_sum[...].astype(BF16)
    scatters[0].collect(total_ref)
    add_lifted(total_ref, low_out_ref, d_table)

    @pl.loop(0, rows // BLOCK)
    def _(step):
        here = pl.ds(pl.multiple_of(step * BLOCK, BLOCK), BLOCK)
        resid = layer_ref[here, :].astype(F32) + rms_norm(total_ref[here, :], gains_ref[1:2, :])
        resid_ref[here, :] = resid
        normed_ref[here, :] = rms_norm(resid, gains_ref[2:3, :]).astype(BF16)

    gather = ChunkGather(sq, normed_ref, mlp_out, gather_send, gather_recv)
    gather.start()
    own = pltpu.make_async_copy(normed_ref, mlp_out.at[0], own_sem.at[0])
    own.start()
    for chunk in range(1, 4):
        gather.wait_chunk(chunk)
    for copies, onward in zip(taken, passed_on):
        for copy in copies:
            copy.wait_recv()
        onward.start()
    for copies, onward in zip(taken, passed_on):
        for copy in copies:
            copy.wait_send()
        onward.wait()
    own.wait()
    own_h.wait()
    gather.finish()
    for scatter in scatters:
        scatter.finish()


def attn_fused(lengths, seq, weight, d_tab, h_tab, k_tab, cosine, sine, layer_in, gains):
    rows, model = layer_in.shape
    q_width = weight.shape[1] - 2 * HD
    q_width //= 2
    qkv_width = q_width + 2 * HD
    anywhere = pl.BlockSpec(memory_space=pl.ANY)
    vmem = pl.BlockSpec(memory_space=pltpu.VMEM)
    narrow = jax.ShapeDtypeStruct((LEN, HD), BF16)
    return pl.pallas_call(
        functools.partial(attn_kernel, rows),
        out_shape=(
            jax.ShapeDtypeStruct((LEN, q_width), BF16),
            narrow,
            jax.ShapeDtypeStruct((HD, LEN), BF16),
            narrow,
            jax.ShapeDtypeStruct((LEN, q_width), BF16),
            jax.ShapeDtypeStruct((q_width // HD, LEN), F32),
            jax.ShapeDtypeStruct((LEN, LANES), BF16),
            jax.ShapeDtypeStruct((rows, LANES), BF16),
            jax.ShapeDtypeStruct((rows, model), F32),
            jax.ShapeDtypeStruct((rows, model), F32),
            jax.ShapeDtypeStruct((rows, model), BF16),
            jax.ShapeDtypeStruct((4, rows, model), BF16),
            jax.ShapeDtypeStruct((4, model, q_width), BF16),
            jax.ShapeDtypeStruct((4, q_width, LANES), BF16),
        ),
        in_specs=[pl.BlockSpec(memory_space=pltpu.SMEM)] + [anywhere] * 2 + [vmem] * 7,
        out_specs=(vmem,) * 11 + (anywhere,) * 3,
        scratch_shapes=[
            pltpu.VMEM((4, rows, model), BF16),
            pltpu.VMEM(weight.shape, BF16),
            pltpu.VMEM((HD, LEN), BF16),
            pltpu.VMEM((rows, LANES), F32),
            pltpu.SemaphoreType.DMA((2,)),
            pltpu.SemaphoreType.DMA((2,)),
            pltpu.SemaphoreType.DMA((6,)),
            pltpu.SemaphoreType.DMA((6,)),
            pltpu.SemaphoreType.DMA((3, 3)),
            pltpu.SemaphoreType.DMA((3, 3)),
        ]
        + scatter_scratch(rows, model, model // tile_of(model))
        + scatter_scratch(rows, LANES),
        compiler_params=pltpu.CompilerParams(
            collective_id=8, has_side_effects=True, vmem_limit_bytes=62 * 1024 * 1024
        ),
        name="attn",
    )(lengths, seq, weight, d_tab, h_tab, k_tab, cosine, sine, layer_in, gains)


def attn_back_kernel(
    rows,
    ids_ref,
    length_ref,
    back_ref,
    low_gu_ref,
    resid_ref,
    total_ref,
    cot_ref,
    layer_ref,
    gains_ref,
    weight_hbm,
    w_out_hbm,
    seq_hbm,
    q_ref,
    k_ref,
    kt_ref,
    v_ref,
    attended_ref,
    inverse_ref,
    cos_ref,
    sin_ref,
    low_ref,
    d_table,
    h_all,
    k_table,
    normed_ref,
    low_out_ref,
    grad_mlp_ref,
    low_down_ref,
    f_ref,
    o_ref,
    in_out,
    heads_out,
    hidden_out,
    query_out,
    keyval_out,
    gateup_out,
    resid_out,
    weight,
    w_out,
    work,
    g_ref,
    low_sum,
    buf,
    att_send,
    att,
    low_own,
    low_all,
    q_grad,
    k_sum,
    v_sum,
    kv_grad,
    joined,
    d_turned,
    h_turned,
    k_turned,
    d_send,
    d_land,
    d_sum,
    d_recv,
    f_recv,
    hk_send,
    hk_land,
    hk_recv,
    load_sem,
    att_sends,
    att_recvs,
    f_sem,
    d_sem,
    hk_sem,
    group_send,
    group_recv,
    line_recv,
    *scratch,
):
    sq = Square(rows)
    dp = lax.axis_size("dp")
    d = lax.axis_index("dp")
    model = o_ref.shape[-1]
    half = sq.half
    wide = tile_of(model)
    q_width = q_ref.shape[1]
    qkv_width = q_width + 2 * HD
    others = (sq.far, sq.across, sq.down)
    sources = [w_out_hbm.at[peer] for peer in others]
    sources.append(weight_hbm.at[:, pl.ds(qkv_width, q_width)])
    loads = [
        pltpu.make_async_copy(source, w_out.at[which % 2], load_sem.at[2 + which])
        for which, source in enumerate(sources)
    ]
    weight_load = pltpu.make_async_copy(
        weight_hbm.at[:, pl.ds(0, qkv_width)], weight, load_sem.at[0]
    )
    seq_load = pltpu.make_async_copy(seq_hbm, buf, load_sem.at[1])
    loads[0].start()
    loads[1].start()
    weight_load.start()
    seq_load.start()
    peers = [{"tensor": peer} for peer in (sq.across, sq.down, sq.far)]
    peers += [{"dp": lax.rem(d + step, dp)} for step in range(1, dp)]
    call(peers)

    low_gu = low_gu_ref[...].astype(BF16)

    @pl.loop(0, model // wide)
    def _(step):
        here = columns(step, wide)
        work[:, here] = back_ref[:, here] + nt(low_gu, d_table[here, :])

    @pl.loop(0, rows // BLOCK)
    def _(step):
        here = pl.ds(pl.multiple_of(step * BLOCK, BLOCK), BLOCK)
        at = sq.me * rows + step * BLOCK + lax.broadcasted_iota(jnp.int32, (BLOCK, 1), 0)
        valid = (at < length_ref[0]).astype(F32)
        mid = cot_ref[here, :].astype(F32) * valid + norm_back(
            resid_ref[here, :], gains_ref[2:3, :], work[here, :]
        )
        work[here, :] = mid
        g_ref[here, :] = norm_back(total_ref[here, :], gains_ref[1:2, :], mid).astype(BF16)

    low_own[...] = band(nn(g_ref[...], d_table[...]), OUT).astype(BF16)
    pl.semaphore_wait(pltpu.get_barrier_semaphore(), len(peers))
    heads_out_copies = []
    for which, peer in enumerate(others + (sq.me,)):
        loads[which].wait()
        grads = (nn(g_ref[...], w_out[which % 2]) + nt(low_own[...], h_all[peer])).astype(BF16)
        if which < 2:
            loads[which + 2].start()
        if which == 3:
            att[sq.me] = grads
            low_all[sq.me] = low_own[...]
            continue
        att_send[which] = grads
        copies = (
            remote(
                att_send.at[which],
                att.at[sq.me],
                att_sends.at[which, 0],
                att_recvs.at[which, 0],
                peer,
            ),
            remote(
                low_own,
                low_all.at[sq.me],
                att_sends.at[which, 1],
                att_recvs.at[which, 1],
                peer,
            ),
        )
        for copy in copies:
            copy.start()
        heads_out_copies.append(copies)
    line = []
    line += along(lambda k: f_ref.at[k // 2, lax.rem(k, 2)], f_recv, f_sem, line_recv.at[0])
    part, part_low = scratch[0], scratch[5]
    scatters = (ChunkScatter(sq, *scratch[:5]), ChunkScatter(sq, *scratch[5:10]))

    d_turned[...] = jnp.zeros_like(d_turned)
    low_grads = (
        (turned(low_gu)[GATE.start : UP.stop], normed_ref, slice(GATE.start, UP.stop)),
        (turned(low_out_ref[...])[OUT], g_ref, OUT),
        (turned(low_down_ref[...])[DOWN], grad_mlp_ref, DOWN),
    )

    @pl.loop(0, model // wide)
    def _(step):
        here = columns(step, wide)
        for low, source, place in low_grads:
            d_turned[place, here] = nn(low, source[:, here])

    h_turned[...] = jnp.zeros_like(h_turned)
    k_turned[...] = jnp.zeros_like(k_turned)
    k_sum[...] = jnp.zeros_like(k_sum)
    v_sum[...] = jnp.zeros_like(v_sum)
    heads = q_width // HD
    stacked = heads * half

    @pl.loop(0, 4)
    def _(turn):
        for step, which in ((1, 1), (2, 2), (3, 0)):

            @pl.when(turn == step)
            def _(which=which):
                for copy in heads_out_copies[which]:
                    copy.wait_recv()

        is_own, is_far = (3 - turn) // 3, turn // 3
        is_down = turn // 2 - is_far
        block = (
            sq.me * is_own
            + sq.far * is_far
            + sq.down * is_down
            + sq.across * (1 - is_own - is_far - is_down)
        )
        low_turned = turned(low_all[block])[OUT]
        h_turned[:RANK, :] += nn(
            low_turned, attended_ref[pl.ds(pl.multiple_of(block * rows, rows), rows), :]
        )
        for last in range(4):

            @pl.when(block == last)
            def _(last=last):
                seen = slice(0, (last + 1) * rows)

                @pl.loop(0, 2)
                def _(side):
                    start = pl.multiple_of(last * rows + side * half, half)
                    here = pl.ds(start, half)
                    place = pl.ds(pl.multiple_of(side * half, half), half)
                    queries = stack_heads(q_ref, here, heads)
                    grads = jnp.concatenate(
                        [att[last, place, h * HD : (h + 1) * HD] for h in range(heads)], axis=0
                    )
                    inverse = jnp.concatenate(
                        [inverse_ref[h : h + 1, here] for h in range(heads)], axis=1
                    )
                    squash, weights = softmax_weights(
                        k_ref[seen, :], queries, start, half, length_ref[0]
                    )
                    probs = weights * inverse
                    grad_probs = nt(v_ref[seen, :], grads)
                    mean = jnp.sum(probs * grad_probs, axis=0, keepdims=True)
                    grad_raw = (probs * (grad_probs - mean) * (1.0 - squash * squash)).astype(BF16)
                    k_sum[seen, :] += nn(grad_raw, queries)
                    v_sum[seen, :] += nn(probs.astype(BF16), grads)
                    q_back = nn(kt_ref[:, seen], grad_raw).T * HD ** (-0.5)
                    for h in range(heads):
                        q_grad[here, h * HD : (h + 1) * HD] = rotate_back(
                            q_back[h * half : (h + 1) * half], cos_ref[here, :], sin_ref[here, :]
                        ).astype(BF16)

    weight_load.wait()
    kv_grad[:, :HD] = rotate_back(k_sum[...], cos_ref[...], sin_ref[...]).astype(BF16)
    kv_grad[:, HD:] = v_sum[...].astype(BF16)

    @pl.loop(0, 4)
    def _(step):
        chunk = far_first(step)
        for side in range(2):
            here = pl.ds(chunk_start(sq, chunk, side), half)
            place = pl.ds(side * half, half)
            joined[chunk, place, :q_width] = q_grad[here, :]
            joined[chunk, place, q_width:] = kv_grad[here, :]
        part_low[chunk] = (
            band(nn(joined[chunk, :, :q_width], h_all[sq.me]), QUERY)
            + band(nn(joined[chunk, :, q_width : q_width + HD], k_table[...]), KEY)
            + band(nn(joined[chunk, :, q_width + HD :], k_table[...]), VALUE)
        ).astype(BF16)

        @pl.loop(0, model // wide)
        def _(tile):
            here = columns(tile, wide)
            part[chunk, :, here] = nt(joined[chunk], weight[here, :]).astype(BF16)

            @pl.when(step == 0)
            def _():
                scatters[0].send(1, tile)

            @pl.when(step == 1)
            def _():
                scatters[0].send(0, tile)

        @pl.when(step == 0)
        def _():
            scatters[1].send_far()

        @pl.when(step == 1)
        def _():
            scatters[1].send_own()

    seq_load.wait()

    @pl.loop(0, 4)
    def _(chunk):
        grad_turned = turned(part_low[chunk])[: VALUE.stop]
        for side in range(2):
            here = pl.ds(chunk_start(sq, chunk, side), half)
            place = slice(side * half, (side + 1) * half)
            low_turned = turned(low_ref[here, :])
            mine = joined.at[chunk, pl.ds(side * half, half)]
            h_turned[RANK : 2 * RANK, :] += nn(low_turned[QUERY], mine[:, :q_width])
            k_turned[:RANK, :] += nn(low_turned[KEY], mine[:, q_width : q_width + HD])
            k_turned[RANK : 2 * RANK, :] += nn(low_turned[VALUE], mine[:, q_width + HD :])
            where_from = chunk_start(sq, chunk, side)
            block = where_from // rows
            inside = pl.ds(pl.multiple_of(where_from - block * rows, half), half)

            @pl.loop(0, model // wide)
            def _(tile):
                where = columns(tile, wide)
                d_turned[: VALUE.stop, where] += nn(
                    grad_turned[:, place],
                    buf[block, inside, where],
                )

    @pl.loop(0, model // LANES)
    def _(step):
        here = columns(step, LANES)
        d_send[here, :] = d_turned[:, here].T.astype(BF16)

    d_rows = d_sum.shape[1]
    spread = []
    for k in range(dp):
        spread.append(
            sq.spread(
                lambda peer, k=k: d_send.at[pl.ds(pl.multiple_of((k * 4 + peer) * d_rows, 8), d_rows)],
                d_land.at[k],
                group_send.at[k],
                group_recv.at[k],
            )
        )
    cores = hk_send.shape[0]
    h_size, k_size = q_width // dp, HD // dp
    hk_send[...] = jnp.zeros_like(hk_send)
    for core in range(cores):
        for peer in range(4):
            at = core * 4 + peer
            hk_send[core, peer, : 2 * RANK, :h_size] = h_turned[
                : 2 * RANK, at * h_size : (at + 1) * h_size
            ].astype(BF16)
            hk_send[core, peer, 2 * RANK :, :k_size] = k_turned[
                : 2 * RANK, at * k_size : (at + 1) * k_size
            ].astype(BF16)
    spread.append(
        sq.spread(lambda peer: hk_send.at[:, peer], hk_land, group_send.at[dp], group_recv.at[dp])
    )
    for copies in spread:
        for copy in copies:
            copy.start()
    for scatter in scatters:
        scatter.pass_on()
    for copies in spread:
        copies[0].wait()
        for copy in copies[1:]:
            copy.wait_recv()
    for k in range(dp):
        d_sum[k] = sum(d_land[k, t].astype(F32) for t in range(4)).astype(BF16)
    line += along(lambda k: d_sum.at[k], d_recv, d_sem, line_recv.at[1])
    line += along(lambda k: hk_land.at[k // 2, lax.rem(k, 2)], hk_recv, hk_sem, line_recv.at[2])
    scatters[1].collect(low_sum)
    low_qkv = low_sum[...].astype(BF16)
    scatters[0].arrived()
    landing = scratch[1]
    low_sum[...] = low_qkv.astype(F32)

    @pl.loop(0, rows // BLOCK)
    def _(step):
        here = pl.ds(pl.multiple_of(step * BLOCK, BLOCK), BLOCK)
        link = (step * BLOCK) // half
        there = pl.ds(pl.multiple_of(step * BLOCK - link * half, BLOCK), BLOCK)
        total = (
            part[0, here, :].astype(F32)
            + landing[link, there, :].astype(F32)
            + landing[4 + link, there, :].astype(F32)
            + nt(low_sum[here, :].astype(BF16), d_table[...])
        )
        o_ref[here, :] = (
            work[here, :] + norm_back(layer_ref[here, :].astype(F32), gains_ref[0:1, :], total)
        ).astype(BF16)

    for item, target in enumerate((f_recv, d_recv, hk_recv)):
        pltpu.make_async_copy(target, target, line_recv.at[item]).wait()

    @pl.loop(0, NA)
    def _(adapter):
        def pick(received):
            total = None
            for group in range(dp):
                mine = jnp.where(
                    ids_ref[group] == adapter, received[group].astype(F32), 0.0
                )
                total = mine if total is None else total + mine
            return total

        d_all = pick(d_recv)
        in_out[adapter] = d_all[:, : 5 * RANK]
        d_flip = d_all.T
        f_all = pick(f_recv)
        hidden_out[adapter] = f_all[:RANK]
        hk_all = pick(hk_recv)
        heads_out[adapter] = hk_all[:RANK, :h_size]
        query_out[adapter] = hk_all[RANK : 2 * RANK, :h_size]
        for which in range(2):
            first = (which + 2) * RANK
            keyval_out[adapter, which] = hk_all[first : first + RANK, :k_size]
            first = (which + 1) * RANK
            gateup_out[adapter, which] = f_all[first : first + RANK]
            first = (which + 5) * RANK
            resid_out[adapter, which] = d_flip[first : first + RANK]

    for copies in spread:
        for copy in copies[1:]:
            copy.wait_send()
    for copies in heads_out_copies:
        for copy in copies:
            copy.wait_send()
    for copy in line:
        copy.wait_send()
    for scatter in scatters:
        scatter.finish()


def attn_back_fused(scalars, arrays, grad_shapes, dp, total):
    anywhere = pl.BlockSpec(memory_space=pl.ANY)
    vmem = pl.BlockSpec(memory_space=pltpu.VMEM)
    smem = pl.BlockSpec(memory_space=pltpu.SMEM)
    rows, model = arrays[0].shape
    weight, q, f_in = arrays[7], arrays[10], arrays[-1]
    q_width = q.shape[1]
    specs = [smem, smem] + [vmem] * len(arrays)
    specs[9] = specs[10] = specs[11] = anywhere
    outs = [jax.ShapeDtypeStruct((rows, model), BF16)]
    outs += [jax.ShapeDtypeStruct(shape, F32) for shape in grad_shapes]
    d_rows = model // total
    messages = f_in.shape[2:]
    return pl.pallas_call(
        functools.partial(attn_back_kernel, rows),
        out_shape=tuple(outs),
        in_specs=specs,
        out_specs=(vmem,) * len(outs),
        scratch_shapes=[
            pltpu.VMEM((model, q_width + 2 * HD), BF16),
            pltpu.VMEM((2, model, q_width), BF16),
            pltpu.VMEM((rows, model), F32),
            pltpu.VMEM((rows, model), BF16),
            pltpu.VMEM((rows, LANES), F32),
            pltpu.VMEM((4, rows, model), BF16),
            pltpu.VMEM((3, rows, q_width), BF16),
            pltpu.VMEM((4, rows, q_width), BF16),
            pltpu.VMEM((rows, LANES), BF16),
            pltpu.VMEM((4, rows, LANES), BF16),
            pltpu.VMEM((LEN, q_width), BF16),
            pltpu.VMEM((LEN, HD), F32),
            pltpu.VMEM((LEN, HD), F32),
            pltpu.VMEM((LEN, 2 * HD), BF16),
            pltpu.VMEM((4, rows, q_width + 2 * HD), BF16),
            pltpu.VMEM((LANES, model), F32),
            pltpu.VMEM((2 * RANK, q_width), F32),
            pltpu.VMEM((2 * RANK, HD), F32),
            pltpu.VMEM((model, LANES), BF16),
            pltpu.VMEM((dp, 4, d_rows, LANES), BF16),
            pltpu.VMEM((dp, d_rows, LANES), BF16),
            pltpu.VMEM((dp, d_rows, LANES), BF16),
            pltpu.VMEM((dp,) + messages, BF16),
            pltpu.VMEM((dp // 4, 4, 4 * RANK, LANES), BF16),
            pltpu.VMEM((4, dp // 4, 4 * RANK, LANES), BF16),
            pltpu.VMEM((dp, 4 * RANK, LANES), BF16),
            pltpu.SemaphoreType.DMA((6,)),
            pltpu.SemaphoreType.DMA((3, 2)),
            pltpu.SemaphoreType.DMA((3, 2)),
            pltpu.SemaphoreType.DMA((dp,)),
            pltpu.SemaphoreType.DMA((dp,)),
            pltpu.SemaphoreType.DMA((dp,)),
            pltpu.SemaphoreType.DMA((dp + 1, 3)),
            pltpu.SemaphoreType.DMA((dp + 1, 4)),
            pltpu.SemaphoreType.DMA((3,)),
        ]
        + scatter_scratch(rows, model, model // tile_of(model))
        + scatter_scratch(rows, LANES),
        compiler_params=pltpu.CompilerParams(
            collective_id=6, has_side_effects=True, vmem_limit_bytes=62 * 1024 * 1024
        ),
        name="attn_back",
    )(*scalars, *arrays)


def per_device(
    layer_in,
    cotangent,
    lengths,
    adapter_ids,
    norm_gains,
    query_weight,
    key_weight,
    value_weight,
    out_weight,
    gate_weight,
    up_weight,
    down_weight,
    adapt_in,
    adapt_heads,
    adapt_hidden,
    lift_query,
    lift_keyval,
    lift_gateup,
    lift_resid,
):
    lay = Layout()
    count = lay.tensor
    rows = layer_in.shape[0]
    group_rows = rows * count
    assert lengths.shape[0] == 1 and group_rows == LEN
    heads_here = lay.heads_here
    head_width = heads_here * HD
    hidden_here = FF // count
    assert lay.ratio % heads_here == 0

    key_cols = lax.dynamic_slice_in_dim(key_weight, lay.kv_head * HD, HD, 1)
    value_cols = lax.dynamic_slice_in_dim(value_weight, lay.kv_head * HD, HD, 1)
    attn_shard = jnp.concatenate([query_weight, key_cols, value_cols, out_weight.T], axis=1)
    attn_w = lax.all_gather(attn_shard, "dp", axis=0, tiled=True)
    gate_up_shard = jnp.concatenate([gate_weight, up_weight], axis=1)
    down_shard = down_weight.T
    attn_shard, gate_up_shard, down_shard = lax.optimization_barrier(
        (attn_shard, gate_up_shard, down_shard)
    )
    gate_up_w = lax.all_gather(gate_up_shard, "dp", axis=0, tiled=True)
    qkv_width = head_width + 2 * HD

    cosine, sine = tables(LEN, HD)
    if count == 4 and lay.dp == 8:
        seq_attn, all_ids, d_tab, f_tab, h_tab, k_tab = front(
            jnp.broadcast_to(adapter_ids, (8, LANES)),
            layer_in,
            norm_gains,
            jnp.concatenate(
                [
                    lift_gateup.reshape(NA, 2 * RANK, -1),
                    jnp.swapaxes(adapt_hidden, 1, 2),
                ],
                axis=1,
            ),
            jnp.concatenate(
                [jnp.swapaxes(adapt_in, 1, 2), lift_resid.reshape(NA, 2 * RANK, -1)], axis=1
            ),
            jnp.concatenate(
                [
                    jnp.swapaxes(adapt_heads, 1, 2),
                    lift_query,
                    jnp.pad(
                        lift_keyval.reshape(NA, 2 * RANK, -1),
                        ((0, 0), (0, 0), (0, lift_query.shape[2] - lift_keyval.shape[3])),
                    ),
                ],
                axis=1,
            ),
            lay.dp,
            (D, hidden_here, head_width, HD),
        )
        (
            queries,
            keys,
            keys_turned,
            values,
            attended,
            inverse,
            low_qkv,
            low_out,
            attn_total,
            resid_mid,
            normed_mlp,
            seq_mlp,
            w_out_all,
            h_all,
        ) = attn_fused(
            lengths,
            seq_attn.reshape(count, rows, D),
            attn_w,
            d_tab,
            h_tab,
            k_tab,
            cosine.reshape(LEN, HD // 2),
            sine.reshape(LEN, HD // 2),
            layer_in,
            norm_gains,
        )
        layer_out, grad_mlp, low_gu, low_down, hidden, slope, gelu, down_w = mlp_fused(
            lengths,
            seq_mlp,
            gate_up_w,
            down_shard,
            d_tab,
            f_tab,
            resid_mid,
            cotangent,
            norm_gains,
            lay.dp,
        )
        mlp_back, grad_low_gu, f_grad = mlp_back_fused(
            grad_mlp,
            down_w.reshape(D, hidden_here),
            gate_up_w,
            slope,
            gelu,
            hidden,
            low_gu,
            d_tab,
            f_tab,
            lay.dp,
        )
        grad_shapes = [
            table.shape
            for table in (
                adapt_in,
                adapt_heads,
                adapt_hidden,
                lift_query,
                lift_keyval,
                lift_gateup,
                lift_resid,
            )
        ]
        for which in (1, 2):
            shape = grad_shapes[which]
            grad_shapes[which] = (shape[0], shape[2], shape[1])
        grads = list(
            attn_back_fused(
                (all_ids[:, 0, 0], lengths),
                (
                    mlp_back,
                    grad_low_gu,
                    resid_mid,
                    attn_total,
                    cotangent,
                    layer_in,
                    norm_gains,
                    attn_w,
                    w_out_all,
                    seq_attn.reshape(count, rows, D),
                    queries,
                    keys,
                    keys_turned,
                    values,
                    attended,
                    inverse,
                    cosine.reshape(LEN, HD // 2),
                    sine.reshape(LEN, HD // 2),
                    low_qkv,
                    d_tab,
                    h_all,
                    k_tab,
                    normed_mlp,
                    low_out,
                    grad_mlp,
                    low_down,
                    f_grad,
                ),
                tuple(grad_shapes),
                lay.dp,
                lay.total,
            )
        )
        for which in (2, 3):
            grads[which] = jnp.swapaxes(grads[which], 1, 2)
        return (layer_out, *grads)

    all_ids = lax.all_gather(adapter_ids[:, 0], "dp", axis=0, tiled=True)
    group_hot = (all_ids[:, None] == jnp.arange(NA, dtype=jnp.int32)[None, :]).astype(BF16)

    def rows_of(table):
        moved = jnp.moveaxis(table, -1, 1)
        return moved.reshape(NA, moved.shape[1], -1)

    def choose(*parts):
        packed = lanes(*parts)
        return lax.dot_general(
            group_hot, packed, (((1,), (0,)), ((), ())), preferred_element_type=F32
        ).astype(BF16)

    d_send = choose((QUERY, adapt_in), (OUT, rows_of(lift_resid)))
    f_send = choose((GATE, rows_of(lift_gateup)), (DOWN, adapt_hidden))
    h_send = choose((QUERY, rows_of(lift_query)), (OUT, adapt_heads))
    k_send = choose((KEY, rows_of(lift_keyval)))
    d_rows, f_rows, h_rows, k_rows = (item.shape[1] for item in (d_send, f_send, h_send, k_send))
    d_tab, f_tab, h_tab, k_tab = exchange(
        tables_kernel,
        "adapter_tables",
        3,
        (d_send, f_send, h_send, k_send),
        (
            (lay.total, d_rows, LANES),
            (lay.dp, f_rows, LANES),
            (lay.dp, h_rows, LANES),
            (lay.kv_owners, k_rows, LANES),
        ),
        lay.dp,
        lay.total,
        lay.share,
    )
    d_tab = d_tab.reshape(D, LANES)
    f_tab = f_tab.reshape(hidden_here, LANES)
    h_tab = h_tab.reshape(head_width, LANES)
    k_tab = k_tab.reshape(HD, LANES)
    in_qkv, in_gu = d_tab[:, : 3 * RANK], d_tab[:, 3 * RANK : 5 * RANK]
    lift_out, lift_down = d_tab[:, OUT], d_tab[:, DOWN]
    map_hidden, lift_gate, lift_up = f_tab[:, DOWN], f_tab[:, GATE], f_tab[:, UP]
    map_heads, lift_q = h_tab[:, OUT], h_tab[:, QUERY]
    lift_k, lift_v = k_tab[:, KEY], k_tab[:, VALUE]

    row_start = lay.t * rows
    length = lengths[0]
    row_valid = ((row_start + jnp.arange(rows, dtype=jnp.int32)) < length).astype(F32)[:, None]
    place = jnp.arange(LEN, dtype=jnp.int32)
    allowed = (place[:, None] >= place[None, :]) & (place[None, :] < length)

    resid_in = layer_in.astype(F32)
    normed_attn = rms_norm(resid_in, norm_gains[0]).astype(BF16)
    seq_attn = tensor_gather(normed_attn, count)
    low_qkv = nn(seq_attn, in_qkv).astype(BF16)
    low_q, low_k, low_v = (low_qkv[:, i * RANK : (i + 1) * RANK] for i in range(3))
    qkv = nn(seq_attn, attn_w[:, :qkv_width])
    query_pre = (qkv[:, :head_width] + nt(low_q, lift_q)).reshape(LEN, heads_here, HD)
    key_pre = (qkv[:, head_width : head_width + HD] + nt(low_k, lift_k)).reshape(LEN, 1, HD)
    value_pre = qkv[:, head_width + HD :] + nt(low_v, lift_v)
    queries = (rotate(query_pre, cosine, sine) * HD ** (-0.5)).astype(BF16)
    keys = rotate(key_pre, cosine, sine).astype(BF16).reshape(LEN, HD)
    values = value_pre.astype(BF16)

    def scores_of():
        raw = jnp.einsum("qhd,kd->hqk", queries, keys, preferred_element_type=F32)
        squash = jnp.tanh(raw / SOFT_CAP)
        return squash, jnp.where(allowed[None], jnp.exp(SOFT_CAP * squash), 0.0)

    squash, weights = scores_of()
    inverse_total = 1.0 / jnp.sum(weights, axis=-1, keepdims=True)
    attended = jnp.einsum(
        "hqk,kd->qhd", (weights * inverse_total).astype(BF16), values, preferred_element_type=F32
    )
    attended = attended.astype(BF16).reshape(LEN, head_width)
    w_out = attn_w[:, qkv_width:]
    out_part = nt(attended, w_out).astype(BF16)
    low_out_part = pad_lanes(nn(attended, map_heads).astype(BF16))
    attn_main, low_out = tensor_scatter(out_part, low_out_part, count)
    low_out = low_out[:, :RANK].astype(BF16)
    attn_total = attn_main + nt(low_out, lift_out)
    resid_mid = resid_in + rms_norm(attn_total, norm_gains[1])

    normed_mlp = rms_norm(resid_mid, norm_gains[2]).astype(BF16)
    seq_mlp = tensor_gather(normed_mlp, count)
    low_gu = nn(seq_mlp, in_gu).astype(BF16)
    low_g, low_u = low_gu[:, :RANK], low_gu[:, RANK:]
    w_gate, w_up = gate_up_w[:, :hidden_here], gate_up_w[:, hidden_here:]
    gate = nn(seq_mlp, w_gate) + nt(low_g, lift_gate)
    up = nn(seq_mlp, w_up) + nt(low_u, lift_up)
    hidden, slope, gelu = gelu_parts(gate, up)
    down_w = lax.all_gather(down_shard, "dp", axis=0, tiled=True)
    down_part = nt(hidden, down_w).astype(BF16)
    low_down_part = pad_lanes(nn(hidden, map_hidden).astype(BF16))
    mlp_main, low_down = tensor_scatter(down_part, low_down_part, count)
    low_down = low_down[:, :RANK].astype(BF16)
    mlp_total = mlp_main + nt(low_down, lift_down)
    layer_out = (row_valid * (resid_mid + rms_norm(mlp_total, norm_gains[3]))).astype(BF16)

    grad_out = cotangent.astype(F32) * row_valid
    grad_mlp = norm_back(mlp_total, norm_gains[3], grad_out).astype(BF16)
    seq_grad_mlp = tensor_gather(grad_mlp, count)
    grad_low_down = nn(seq_grad_mlp, lift_down).astype(BF16)
    grad_hidden = nn(seq_grad_mlp, down_w) + nt(grad_low_down, map_hidden)
    grad_gate = (grad_hidden * slope.astype(F32)).astype(BF16)
    grad_up = (grad_hidden * gelu.astype(F32)).astype(BF16)
    low_gu_part = pad_lanes(
        jnp.concatenate([nn(grad_gate, lift_gate), nn(grad_up, lift_up)], axis=1).astype(BF16)
    )
    mlp_back_part = (nt(grad_gate, w_gate) + nt(grad_up, w_up)).astype(BF16)
    mlp_back, grad_low_gu = tensor_scatter(mlp_back_part, low_gu_part, count)
    f_parts = [tn(hidden, grad_low_down), tn(grad_gate, low_g), tn(grad_up, low_u)]
    grad_low_gu = grad_low_gu[:, : 2 * RANK].astype(BF16)
    grad_normed_mlp = mlp_back + nt(grad_low_gu, in_gu)
    grad_mid = grad_out + norm_back(resid_mid, norm_gains[2], grad_normed_mlp)

    grad_attn = norm_back(attn_total, norm_gains[1], grad_mid).astype(BF16)
    seq_grad_attn = tensor_gather(grad_attn, count)
    grad_low_out = nn(seq_grad_attn, lift_out).astype(BF16)
    grad_attended = (nn(seq_grad_attn, w_out) + nt(grad_low_out, map_heads)).astype(BF16)
    grad_heads = grad_attended.reshape(LEN, heads_here, HD)
    probs = weights * inverse_total
    probs_low = probs.astype(BF16)
    grad_probs = jnp.einsum("qhd,kd->hqk", grad_heads, values, preferred_element_type=F32)
    grad_value = jnp.einsum("hqk,qhd->kd", probs_low, grad_heads, preferred_element_type=F32)
    grad_capped = probs * (grad_probs - jnp.sum(probs * grad_probs, axis=-1, keepdims=True))
    grad_raw = (grad_capped * (1.0 - squash * squash)).astype(BF16)
    grad_query = jnp.einsum("hqk,kd->qhd", grad_raw, keys, preferred_element_type=F32)
    grad_key = jnp.einsum("hqk,qhd->kd", grad_raw, queries, preferred_element_type=F32)
    grad_q_pre = rotate(grad_query * HD ** (-0.5), cosine, -sine).astype(BF16)
    grad_q_pre = grad_q_pre.reshape(LEN, head_width)
    grad_k_pre = rotate(grad_key.reshape(LEN, 1, HD), cosine, -sine).astype(BF16)
    grad_k_pre = grad_k_pre.reshape(LEN, HD)
    grad_v_pre = grad_value.astype(BF16)
    low_qkv_part = pad_lanes(
        jnp.concatenate(
            [nn(grad_q_pre, lift_q), nn(grad_k_pre, lift_k), nn(grad_v_pre, lift_v)], axis=1
        ).astype(BF16)
    )
    grad_qkv = jnp.concatenate([grad_q_pre, grad_k_pre, grad_v_pre], axis=1)
    attn_back_part = nt(grad_qkv, attn_w[:, :qkv_width]).astype(BF16)
    attn_back, grad_low_qkv = tensor_scatter(attn_back_part, low_qkv_part, count)
    grad_low_qkv = grad_low_qkv[:, : 3 * RANK].astype(BF16)
    grad_normed_attn = attn_back + nt(grad_low_qkv, in_qkv)
    input_grad = (grad_mid + norm_back(resid_in, norm_gains[0], grad_normed_attn)).astype(BF16)

    def packed(parts, blocks):
        return pad_lanes(jnp.concatenate(parts, axis=1).astype(BF16)).reshape(
            blocks, -1, LANES
        )

    d_grad = packed(
        [
            tn(normed_attn, grad_low_qkv),
            tn(normed_mlp, grad_low_gu),
            tn(grad_attn, low_out),
            tn(grad_mlp, low_down),
        ],
        lay.total,
    )
    f_grad = packed(f_parts, lay.dp)
    h_grad = packed([tn(attended, grad_low_out), tn(grad_q_pre, low_q)], lay.dp)
    k_grad = packed([tn(grad_k_pre, low_k), tn(grad_v_pre, low_v)], lay.kv_owners)
    d_all, f_all, h_all, k_all = exchange(
        grads_kernel,
        "adapter_grads",
        4,
        (d_grad, f_grad, h_grad, k_grad),
        (
            (lay.total, d_rows, LANES),
            (lay.dp, f_rows, LANES),
            (lay.dp, h_rows, LANES),
            (lay.dp * lay.share, k_rows, LANES),
        ),
        lay.dp,
        lay.total,
        lay.share,
    )

    def collect(received):
        repeats = received.shape[0] // lay.dp
        hot = jnp.repeat(group_hot, repeats, axis=0)
        return lax.dot_general(
            hot, received, (((0,), (0,)), ((), ())), preferred_element_type=F32
        )

    d_all, f_all, h_all, k_all = (collect(item) for item in (d_all, f_all, h_all, k_all))

    def lift_form(values, shape):
        return jnp.moveaxis(values, 1, 2).reshape(shape)

    return (
        layer_out,
        input_grad,
        d_all[:, :, : 5 * RANK],
        h_all[:, :, :RANK],
        f_all[:, :, :RANK],
        lift_form(h_all[:, :, RANK : 2 * RANK], lift_query.shape),
        lift_form(k_all[:, :, : 2 * RANK], lift_keyval.shape),
        lift_form(f_all[:, :, RANK : 3 * RANK], lift_gateup.shape),
        lift_form(d_all[:, :, 5 * RANK : 7 * RANK], lift_resid.shape),
    )


def solution(mesh):
    return jax.shard_map(
        per_device,
        mesh=mesh,
        in_specs=(
            P(("dp", "tensor"), None),
            P(("dp", "tensor"), None),
            P("dp"),
            P("dp", None),
            P(),
            P("dp", "tensor"),
            P("dp", None),
            P("dp", None),
            P("tensor", "dp"),
            P("dp", "tensor"),
            P("dp", "tensor"),
            P("tensor", "dp"),
            P(None, ("dp", "tensor"), None),
            P(None, ("dp", "tensor"), None),
            P(None, ("dp", "tensor"), None),
            P(None, None, ("dp", "tensor")),
            P(None, None, None, ("dp", "tensor")),
            P(None, None, None, ("dp", "tensor")),
            P(None, None, None, ("dp", "tensor")),
        ),
        out_specs=(
            P(("dp", "tensor"), None),
            P(("dp", "tensor"), None),
            P(None, ("dp", "tensor"), None),
            P(None, ("dp", "tensor"), None),
            P(None, ("dp", "tensor"), None),
            P(None, None, ("dp", "tensor")),
            P(None, None, None, ("dp", "tensor")),
            P(None, None, None, ("dp", "tensor")),
            P(None, None, None, ("dp", "tensor")),
        ),
        check_vma=False,
    )
```

```python
import functools

import jax
import jax.numpy as jnp
from jax import lax
from jax.experimental import pallas as pl
from jax.experimental.pallas import tpu as pltpu
from jax.sharding import PartitionSpec as P

D = 2304
HQ = 8
KV = 4
HD = 256
FF = 9216
NA = 8
RANK = 16
LEN = 1024
LANES = 128

EPSILON = 1e-06
SOFT_CAP = 50.0
MESH = pl.DeviceIdType.MESH
BF16 = jnp.bfloat16
F32 = jnp.float32
VMEM_LIMIT = 48 * 1024 * 1024
BLOCK = 32


def rms_norm(values, gain_row):
    return (
        values * lax.rsqrt(jnp.mean(values * values, axis=-1, keepdims=True) + EPSILON) * gain_row
    )


def norm_back(values, gain_row, gradient):
    inverse = lax.rsqrt(jnp.mean(values * values, axis=-1, keepdims=True) + EPSILON)
    scaled = gradient * gain_row
    normed = values * inverse
    return inverse * (scaled - normed * jnp.mean(scaled * normed, axis=-1, keepdims=True))


def gelu_parts(gate, up):
    scale = (2.0 / jnp.pi) ** 0.5
    square = gate * gate
    bend = jnp.tanh(scale * gate * (1.0 + 0.044715 * square))
    low = 0.5 * (1.0 + bend)
    gelu = gate * low
    slope = low + 0.5 * gate * (1.0 - bend * bend) * (scale * (1.0 + 3.0 * 0.044715 * square))
    return (gelu * up).astype(BF16), (slope * up).astype(BF16), gelu.astype(BF16)


def tables(length, size):
    half_size = size // 2
    frequency = 10000.0 ** (-2.0 * jnp.arange(half_size, dtype=F32) / size)
    angles = jnp.arange(length, dtype=F32)[:, None] * frequency[None, :]
    return (jnp.cos(angles)[:, None, :], jnp.sin(angles)[:, None, :])


def rotate(values, cosine, sine):
    half_size = values.shape[-1] // 2
    first_half = values[..., :half_size]
    second_half = values[..., half_size:]
    return jnp.concatenate(
        [first_half * cosine - second_half * sine, second_half * cosine + first_half * sine],
        axis=-1,
    )


def nn(a, b):
    return lax.dot_general(a, b, (((1,), (0,)), ((), ())), preferred_element_type=F32)


def nt(a, b):
    return lax.dot_general(a, b, (((1,), (1,)), ((), ())), preferred_element_type=F32)


def tn(a, b):
    return lax.dot_general(a, b, (((0,), (0,)), ((), ())), preferred_element_type=F32)


def pad_lanes(values):
    return jnp.pad(values, [(0, 0)] * (values.ndim - 1) + [(0, LANES - values.shape[-1])])


QUERY, KEY, VALUE, GATE, UP, OUT, DOWN = (
    slice(i * RANK, (i + 1) * RANK) for i in range(7)
)


def band(values, first, last=None):
    lane = lax.broadcasted_iota(jnp.int32, values.shape, 1)
    keep = (lane >= first.start) & (lane < (last or first).stop)
    return jnp.where(keep, values, 0.0)


def lanes(*parts):
    pieces, at = [], 0
    for place, values in parts:
        if place.start > at:
            pieces.append(jnp.zeros(values.shape[:-1] + (place.start - at,), values.dtype))
        pieces.append(values)
        at = place.start + values.shape[-1]
    last = parts[-1][1]
    pieces.append(jnp.zeros(last.shape[:-1] + (LANES - at,), last.dtype))
    return jnp.concatenate(pieces, axis=-1)


def call(peers):
    barrier = pltpu.get_barrier_semaphore()
    for peer in peers:
        pl.semaphore_signal(barrier, inc=1, device_id=peer, device_id_type=MESH)


def greet(peers):
    call(peers)
    pl.semaphore_wait(pltpu.get_barrier_semaphore(), len(peers))


def square_peers(index):
    return index + 1 - 2 * lax.rem(index, 2), lax.rem(index + 2, 4), 3 - index


def remote(source, target, send_sem, recv_sem, peer):
    return pltpu.make_async_remote_copy(
        src_ref=source,
        dst_ref=target,
        send_sem=send_sem,
        recv_sem=recv_sem,
        device_id={"tensor": peer},
        device_id_type=MESH,
    )


class PlainGather:
    def __init__(self, me, x_ref, o_ref, local_sem, send_sem, recv_sem):
        rows = x_ref.shape[0]
        half = rows // 2
        links = square_peers(me)[:2]
        self.own = pltpu.make_async_copy(x_ref, o_ref.at[pl.ds(me * rows, rows)], local_sem)
        self.first, self.second, self.onward = [], [], []
        for order, group in enumerate((self.first, self.second)):
            for link in range(2):
                part = link if order == 0 else 1 - link
                group.append(
                    remote(
                        x_ref.at[pl.ds(part * half, half)],
                        o_ref.at[pl.ds(me * rows + part * half, half)],
                        send_sem.at[link, part],
                        recv_sem.at[link, part],
                        links[link],
                    )
                )
        for link in range(2):
            block = o_ref.at[pl.ds(links[link] * rows + link * half, half)]
            self.onward.append(
                remote(block, block, send_sem.at[2, link], recv_sem.at[2, link], links[1 - link])
            )

    def start(self):
        self.own.start()
        for copy in self.first + self.second:
            copy.start()

    def forward(self):
        for copy, onward in zip(self.first, self.onward):
            copy.wait_recv()
            onward.start()

    def finish(self):
        for copy in self.second + self.onward:
            copy.wait_recv()
        self.own.wait()
        for copy in self.first + self.second + self.onward:
            copy.wait_send()


def gather_kernel(count, rows, x_ref, o_ref, local_sem, send_sem, recv_sem):
    me = lax.axis_index("tensor")
    if count == 4:
        across, down, _ = square_peers(me)
        greet([{"tensor": across}, {"tensor": down}])
        gather = PlainGather(me, x_ref, o_ref, local_sem, send_sem, recv_sem)
        gather.start()
        gather.forward()
        gather.finish()
    else:
        peers = [lax.rem(me + step, count) for step in range(1, count)]
        greet([{"tensor": peer} for peer in peers])
        own = pltpu.make_async_copy(x_ref, o_ref.at[pl.ds(me * rows, rows)], local_sem)
        own.start()
        copies = []
        for step, peer in enumerate(peers):
            copy = remote(
                x_ref,
                o_ref.at[pl.ds(me * rows, rows)],
                send_sem.at[0, step],
                recv_sem.at[0, step],
                peer,
            )
            copy.start()
            copies.append(copy)
        own.wait()
        for copy in copies:
            copy.wait()


def tensor_gather(values, count):
    rows, width = values.shape
    slots = max(2, count - 1)
    return pl.pallas_call(
        functools.partial(gather_kernel, count, rows),
        out_shape=jax.ShapeDtypeStruct((count * rows, width), values.dtype),
        in_specs=[pl.BlockSpec(memory_space=pl.ANY)],
        out_specs=pl.BlockSpec(memory_space=pl.ANY),
        scratch_shapes=[
            pltpu.SemaphoreType.DMA,
            pltpu.SemaphoreType.DMA((3, slots)),
            pltpu.SemaphoreType.DMA((3, slots)),
        ],
        compiler_params=pltpu.CompilerParams(
            collective_id=1, has_side_effects=True, vmem_limit_bytes=VMEM_LIMIT
        ),
        name="tensor_gather",
    )(values)


def scatter_kernel(count, rows, p_ref, q_ref, o_ref, l_ref, *scratch):
    me = lax.axis_index("tensor")
    payload = ((p_ref, o_ref), (q_ref, l_ref))
    if count == 4:
        across, down, far = square_peers(me)
        greet([{"tensor": across}, {"tensor": down}])
        half = rows // 2
        first = scratch[0:2]
        sums = scratch[2:4]
        second = scratch[4:6]
        send_sem, recv_sem = scratch[6], scratch[7]
        links = (across, down)
        copies = {}
        for which in (1, 0):
            for link in range(2):
                block = far if which == 1 else links[link]
                for item in range(2):
                    copy = remote(
                        payload[item][0].at[pl.ds(block * rows + link * half, half)],
                        first[item].at[link, which],
                        send_sem.at[item, link, which],
                        recv_sem.at[item, link, which],
                        links[link],
                    )
                    copy.start()
                    copies[item, link, which] = copy
        for link in range(2):
            block = links[1 - link]
            for item in range(2):
                copies[item, link, 1].wait_recv()
                mine = payload[item][0][pl.ds(block * rows + link * half, half), :]
                sums[item][link] = (
                    mine.astype(F32) + first[item][link, 1].astype(F32)
                ).astype(BF16)
                copy = remote(
                    sums[item].at[link],
                    second[item].at[link],
                    send_sem.at[item, link, 2],
                    recv_sem.at[item, link, 2],
                    links[1 - link],
                )
                copy.start()
                copies[item, link, 2] = copy
        for link in range(2):
            for item in range(2):
                copies[item, link, 0].wait_recv()
                mine = payload[item][0][pl.ds(me * rows + link * half, half), :]
                payload[item][1][pl.ds(link * half, half), :] = mine.astype(F32) + first[item][
                    link, 0
                ].astype(F32)
        for link in range(2):
            for item in range(2):
                copies[item, link, 2].wait_recv()
                payload[item][1][pl.ds(link * half, half), :] += second[item][link].astype(F32)
        for copy in copies.values():
            copy.wait_send()
    else:
        peers = [lax.rem(me + step, count) for step in range(1, count)]
        greet([{"tensor": peer} for peer in peers])
        first = scratch[0:2]
        send_sem, recv_sem = scratch[2], scratch[3]
        copies = []
        for step, peer in enumerate(peers):
            for item in range(2):
                copy = remote(
                    payload[item][0].at[pl.ds(peer * rows, rows)],
                    first[item].at[step],
                    send_sem.at[item, step],
                    recv_sem.at[item, step],
                    peer,
                )
                copy.start()
                copies.append((item, step, copy))
        for item in range(2):
            payload[item][1][...] = payload[item][0][pl.ds(me * rows, rows), :].astype(F32)
        for item, step, copy in copies:
            copy.wait()
            payload[item][1][...] += first[item][step].astype(F32)


def tensor_scatter(values, narrow, count):
    rows = values.shape[0] // count
    widths = (values.shape[1], narrow.shape[1])
    if count == 4:
        half = rows // 2
        scratch = [pltpu.VMEM((2, 2, half, width), BF16) for width in widths]
        scratch += [pltpu.VMEM((2, half, width), BF16) for width in widths]
        scratch += [pltpu.VMEM((2, half, width), BF16) for width in widths]
        scratch += [pltpu.SemaphoreType.DMA((2, 2, 3)), pltpu.SemaphoreType.DMA((2, 2, 3))]
    else:
        scratch = [pltpu.VMEM((count - 1, rows, width), BF16) for width in widths]
        scratch += [pltpu.SemaphoreType.DMA((2, count - 1))] * 2
    vmem = pl.BlockSpec(memory_space=pltpu.VMEM)
    return pl.pallas_call(
        functools.partial(scatter_kernel, count, rows),
        out_shape=tuple(jax.ShapeDtypeStruct((rows, width), F32) for width in widths),
        in_specs=[vmem, vmem],
        out_specs=(vmem, vmem),
        scratch_shapes=scratch,
        compiler_params=pltpu.CompilerParams(
            collective_id=2, has_side_effects=True, vmem_limit_bytes=VMEM_LIMIT
        ),
        name="tensor_scatter",
    )(values, narrow)


class Square:
    def __init__(self, rows):
        self.rows = rows
        self.half = rows // 2
        self.me = lax.axis_index("tensor")
        self.across, self.down, self.far = square_peers(self.me)
        self.links = (self.across, self.down)

    def greet(self, far=False):
        greet([{"tensor": peer} for peer in (self.across, self.down) + ((self.far,) if far else ())])

    def spread(self, source_at, target, send_sem, recv_sem):
        copies = [pltpu.make_async_copy(source_at(self.me), target.at[self.me], recv_sem.at[0])]
        for which, peer in enumerate((self.across, self.down, self.far)):
            copies.append(
                remote(
                    source_at(peer),
                    target.at[self.me],
                    send_sem.at[which],
                    recv_sem.at[1 + which],
                    peer,
                )
            )
        return copies


def along(source_at, target, send_sem, recv_sem):
    dp = lax.axis_size("dp")
    d = lax.axis_index("dp")
    pltpu.make_async_copy(source_at(d), target.at[d], recv_sem).start()
    copies = []
    for step in range(1, dp):
        peer = lax.rem(d + step, dp)
        copy = pltpu.make_async_remote_copy(
            src_ref=source_at(peer),
            dst_ref=target.at[d],
            send_sem=send_sem.at[step],
            recv_sem=recv_sem,
            device_id={"dp": peer},
            device_id_type=MESH,
        )
        copy.start()
        copies.append(copy)
    return copies


class ChunkGather:
    def __init__(self, sq, source, buf, send_sem, recv_sem):
        half = sq.half
        self.first, self.second, self.onward = [], [], []
        for link in range(2):
            for order in range(2):
                part = link if order == 0 else 1 - link
                copy = remote(
                    source.at[pl.ds(part * half, half)],
                    buf.at[1 + order, pl.ds(link * half, half)],
                    send_sem.at[2 * order + link],
                    recv_sem.at[2 * order + link],
                    sq.links[link],
                )
                (self.first if order == 0 else self.second).append(copy)
            self.onward.append(
                remote(
                    buf.at[1, pl.ds(link * half, half)],
                    buf.at[3, pl.ds(link * half, half)],
                    send_sem.at[4 + link],
                    recv_sem.at[4 + link],
                    sq.links[1 - link],
                )
            )

    def start(self):
        for copy in self.first + self.second:
            copy.start()

    def wait_chunk(self, chunk):
        if chunk == 1:
            for copy in self.first:
                copy.wait_recv()
            for copy in self.onward:
                copy.start()
        if chunk == 2:
            for copy in self.second:
                copy.wait_recv()
        if chunk == 3:
            for copy in self.onward:
                copy.wait_recv()

    def finish(self):
        for copy in self.first + self.second + self.onward:
            copy.wait_send()


class ChunkScatter:
    def __init__(self, sq, part, landing, passed, send_sem, recv_sem):
        self.sq, self.half = sq, sq.half
        self.part, self.landing, self.passed = part, landing, passed
        self.send_sem, self.recv_sem = send_sem, recv_sem
        self.tiles = send_sem.shape[-1]
        self.width = part.shape[-1] // self.tiles

    def columns(self, tile):
        if self.tiles == 1:
            return pl.ds(0, self.width)
        return columns(tile, self.width)

    def copy(self, kind, link, tile):
        rows = pl.ds(link * self.half, self.half)
        cols = self.columns(tile)
        source = (
            self.passed.at[link, :, cols]
            if kind == 2
            else self.part.at[1 + 2 * kind, rows, cols]
        )
        slot = 2 * kind + link
        return remote(
            source,
            self.landing.at[slot, :, cols],
            self.send_sem.at[slot, tile],
            self.recv_sem.at[slot, tile],
            self.sq.links[1 - link if kind == 2 else link],
        )

    def send(self, kind, tile):
        for link in range(2):
            self.copy(kind, link, tile).start()

    def send_own(self):
        for tile in range(self.tiles):
            self.send(0, tile)

    def send_far(self):
        for tile in range(self.tiles):
            self.send(1, tile)

    def pass_on(self):
        for tile in range(self.tiles):
            cols = self.columns(tile)
            for link in range(2):
                self.copy(1, link, tile).wait_recv()
                rows = pl.ds((1 - link) * self.half, self.half)
                mine = self.part[2, rows, cols].astype(F32)
                self.passed[link, :, cols] = (
                    mine + self.landing[2 + link, :, cols].astype(F32)
                ).astype(BF16)
                self.copy(2, link, tile).start()

    def arrived(self):
        for kind in (0, 2):
            for tile in range(self.tiles):
                for link in range(2):
                    self.copy(kind, link, tile).wait_recv()

    def collect(self, out_ref, places=((0, 0),)):
        self.arrived()
        for link in range(2):
            rows = pl.ds(link * self.half, self.half)
            total = (
                self.part[0, rows, :].astype(F32)
                + self.landing[link].astype(F32)
                + self.landing[4 + link].astype(F32)
            )
            size = self.part.shape[-1] // len(places)
            for source, target in places:
                out_ref[rows, target : target + size] = total[:, source : source + size]

    def finish(self):
        for kind in range(3):
            for tile in range(self.tiles):
                for link in range(2):
                    self.copy(kind, link, tile).wait_send()


def scatter_scratch(rows, width, tiles=1):
    half = rows // 2
    return [
        pltpu.VMEM((4, rows, width), BF16),
        pltpu.VMEM((6, half, width), BF16),
        pltpu.VMEM((2, half, width), BF16),
        pltpu.SemaphoreType.DMA((6, tiles)),
        pltpu.SemaphoreType.DMA((6, tiles)),
    ]


def tile_of(width):
    return 768 if width % 768 == 0 else 384


def columns(step, tile, base=0):
    return pl.ds(pl.multiple_of(base + step * tile, LANES), tile)


def mlp_back_kernel(
    rows,
    g_ref,
    down_hbm,
    gu_hbm,
    slope_hbm,
    gelu_hbm,
    hidden_hbm,
    low_hbm,
    d_ref,
    f_table,
    o_ref,
    l_ref,
    f_out,
    f_ref,
    f_send,
    down_w,
    gu_w,
    buf,
    slope,
    gelu,
    hidden,
    low,
    grads,
    weight_sem,
    load_sem,
    own_sem,
    gather_send,
    gather_recv,
    spread_send,
    spread_recv,
    *scratch,
):
    sq = Square(rows)
    width = hidden.shape[-1]
    model = o_ref.shape[-1]
    down_load = pltpu.make_async_copy(down_hbm, down_w, weight_sem.at[0])
    gu_load = pltpu.make_async_copy(gu_hbm, gu_w, weight_sem.at[1])
    own_load = pltpu.make_async_copy(g_ref, buf.at[0], own_sem)

    def loads(chunk):
        slot = chunk % 2
        return [
            pltpu.make_async_copy(source.at[chunk], target.at[slot], load_sem.at[slot, item])
            for item, (source, target) in enumerate(
                ((slope_hbm, slope), (gelu_hbm, gelu), (hidden_hbm, hidden), (low_hbm, low))
            )
        ]

    down_load.start()
    own_load.start()
    for copy in loads(0):
        copy.start()
    sq.greet(far=True)
    gather = ChunkGather(sq, g_ref, buf, gather_send, gather_recv)
    gather.start()
    gu_load.start()
    part, part_low = scratch[0], scratch[5]
    scatters = (ChunkScatter(sq, *scratch[:5]), ChunkScatter(sq, *scratch[5:10]))
    f_ref[...] = jnp.zeros_like(f_ref)
    own_load.wait()
    down_load.wait()

    @pl.loop(0, 4)
    def _(chunk):
        slot = lax.rem(chunk, 2)
        for step in range(4):

            @pl.when(chunk == step)
            def _(step=step):
                gather.wait_chunk(step)
                for copy in loads(step):
                    copy.wait()
                if step < 3:
                    for copy in loads(step + 1):
                        copy.start()

        incoming = buf.at[chunk]
        low_down = band(nn(incoming[...], d_ref[...]), DOWN).astype(BF16)
        tile = tile_of(width)

        @pl.loop(0, width // tile)
        def _(step):
            here = columns(step, tile)
            grad = nn(incoming[...], down_w[:, here]) + nt(low_down, f_table[here, :])
            grads[:, here] = (grad * slope[slot, :, here].astype(F32)).astype(BF16)
            grads[:, columns(step, tile, width)] = (
                grad * gelu[slot, :, here].astype(F32)
            ).astype(BF16)

        @pl.when(chunk == 0)
        def _():
            gu_load.wait()

        part_low[chunk] = (
            band(nn(grads[:, :width], f_table[...]), GATE)
            + band(nn(grads[:, width:], f_table[...]), UP)
        ).astype(BF16)
        wide = tile_of(model)

        @pl.loop(0, model // wide)
        def _(step):
            here = columns(step, wide)
            part[chunk, :, here] = nt(grads[...], gu_w[here, :]).astype(BF16)

            @pl.when(chunk == 1)
            def _():
                scatters[0].send(0, step)

            @pl.when(chunk == 3)
            def _():
                scatters[0].send(1, step)

        @pl.when(chunk == 1)
        def _():
            scatters[1].send_own()

        @pl.when(chunk == 3)
        def _():
            scatters[1].send_far()

        low_turned = low_down.astype(F32).T.astype(BF16)
        gu_turned = low[slot].astype(F32).T.astype(BF16)
        f_ref[:RANK, :] += nn(low_turned[DOWN], hidden[slot])
        f_ref[RANK : 2 * RANK, :] += nn(gu_turned[GATE], grads[:, :width])
        f_ref[2 * RANK : 3 * RANK, :] += nn(gu_turned[UP], grads[:, width:])

    cores, slices = f_send.shape[:2]
    size = width // (cores * slices)
    for core in range(cores):
        for peer in range(slices):
            first = (core * slices + peer) * size
            f_send[core, peer] = f_ref[: 3 * RANK, first : first + size].astype(BF16)
    spread = sq.spread(lambda peer: f_send.at[:, peer], f_out, spread_send, spread_recv)
    for copy in spread:
        copy.start()
    for scatter in scatters:
        scatter.pass_on()
    gather.finish()
    scatters[0].collect(o_ref)
    scatters[1].collect(l_ref)
    for scatter in scatters:
        scatter.finish()
    for copy in spread:
        copy.wait()


def mlp_back_fused(grad, down_w, gu_w, slope, gelu, hidden, low, d_tab, f_tab, dp):
    rows, model = grad.shape
    width = hidden.shape[2]
    messages = (dp // 4, 4, 3 * RANK, width // dp)
    anywhere = pl.BlockSpec(memory_space=pl.ANY)
    vmem = pl.BlockSpec(memory_space=pltpu.VMEM)
    return pl.pallas_call(
        functools.partial(mlp_back_kernel, rows),
        out_shape=(
            jax.ShapeDtypeStruct((rows, model), F32),
            jax.ShapeDtypeStruct((rows, LANES), F32),
            jax.ShapeDtypeStruct((4, dp // 4, 3 * RANK, width // dp), BF16),
        ),
        in_specs=[vmem] + [anywhere] * 6 + [vmem] * 2,
        out_specs=(vmem,) * 3,
        scratch_shapes=[
            pltpu.VMEM((3 * RANK, width), F32),
            pltpu.VMEM(messages, BF16),
            pltpu.VMEM((model, width), BF16),
            pltpu.VMEM((model, 2 * width), BF16),
            pltpu.VMEM((4, rows, model), BF16),
            pltpu.VMEM((2, rows, width), BF16),
            pltpu.VMEM((2, rows, width), BF16),
            pltpu.VMEM((2, rows, width), BF16),
            pltpu.VMEM((2, rows, LANES), BF16),
            pltpu.VMEM((rows, 2 * width), BF16),
            pltpu.SemaphoreType.DMA((2,)),
            pltpu.SemaphoreType.DMA((2, 4)),
            pltpu.SemaphoreType.DMA,
            pltpu.SemaphoreType.DMA((6,)),
            pltpu.SemaphoreType.DMA((6,)),
            pltpu.SemaphoreType.DMA((3,)),
            pltpu.SemaphoreType.DMA((4,)),
        ]
        + scatter_scratch(rows, model, model // tile_of(model))
        + scatter_scratch(rows, LANES),
        compiler_params=pltpu.CompilerParams(
            collective_id=5, has_side_effects=True, vmem_limit_bytes=62 * 1024 * 1024
        ),
        name="mlp_back",
    )(grad, down_w, gu_w, slope, gelu, hidden, low, d_tab, f_tab)


def front_kernel(
    ids_ref,
    layer_ref,
    gains_ref,
    f_all,
    d_all,
    hk_all,
    shard_hbm,
    seq_out,
    ids_out,
    d_out,
    f_out,
    h_out,
    k_out,
    weight_out,
    normed,
    ids_land,
    f_pick,
    d_pick,
    hk_pick,
    f_mid,
    d_mid,
    hk_mid,
    d_join,
    f_land,
    d_land,
    hk_land,
    d_flip,
    f_flip,
    h_flip,
    k_flip,
    local_sem,
    gather_send,
    gather_recv,
    line_send,
    line_recv,
    group_send,
    group_recv,
    shard_sem,
    shard_send,
    shard_recv,
):
    rows = layer_ref.shape[0]
    sq = Square(rows)
    dp = lax.axis_size("dp")
    d = lax.axis_index("dp")
    peers = [{"tensor": peer} for peer in (sq.across, sq.down, sq.far)]
    peers += [{"dp": lax.rem(d + step, dp)} for step in range(1, dp)]
    call(peers)
    shards = Line(weight_out, shard_send, shard_recv)
    own_shard = pltpu.make_async_copy(shard_hbm, weight_out.at[d], shard_sem)
    own_shard.start()

    @pl.loop(0, rows // BLOCK)
    def _(step):
        here = pl.ds(pl.multiple_of(step * BLOCK, BLOCK), BLOCK)
        normed[here, :] = rms_norm(layer_ref[here, :].astype(F32), gains_ref[0:1, :]).astype(BF16)

    pl.semaphore_wait(pltpu.get_barrier_semaphore(), len(peers))
    line = along(lambda k: ids_ref, ids_land, line_send.at[0], line_recv.at[0])
    own_shard.wait()
    shards.start()
    gather = PlainGather(sq.me, normed, seq_out, local_sem, gather_send, gather_recv)
    gather.start()
    pltpu.make_async_copy(ids_land, ids_land, line_recv.at[0]).wait()
    ids_out[...] = ids_land[...]

    @pl.loop(0, dp)
    def _(k):
        for source, target in ((f_all, f_pick), (d_all, d_pick), (hk_all, hk_pick)):
            total = None
            for adapter in range(NA):
                hit = jnp.broadcast_to(ids_land[k, 0:1, 0:1], source.shape[1:]) == adapter
                mine = jnp.where(hit, source[adapter].astype(F32), 0.0)
                total = mine if total is None else total + mine
            target[k] = total.astype(BF16)

    lands = (f_mid, d_mid, hk_mid)
    for item, (source, target) in enumerate(zip((f_pick, d_pick, hk_pick), lands)):
        line += along(
            lambda k, source=source: source.at[k],
            target,
            line_send.at[1 + item],
            line_recv.at[1 + item],
        )
    shards.arrive(1, 0)
    gather.forward()
    for flip in (d_flip, f_flip, h_flip, k_flip):
        flip[...] = jnp.zeros_like(flip)
    for item, target in enumerate(lands):
        pltpu.make_async_copy(target, target, line_recv.at[1 + item]).wait()
    shards.arrive(1, 1)
    size = d_mid.shape[2]
    for k in range(dp):
        d_join[:, k * size : (k + 1) * size] = d_mid[k]
    per_user = dp // 4
    spread = [
        sq.spread(lambda peer: d_join, d_land, group_send.at[0], group_recv.at[0]),
        sq.spread(
            lambda peer: f_mid.at[pl.ds(peer * per_user, per_user)],
            f_land,
            group_send.at[1],
            group_recv.at[1],
        ),
        sq.spread(
            lambda peer: hk_mid.at[pl.ds(peer * per_user, per_user)],
            hk_land,
            group_send.at[2],
            group_recv.at[2],
        ),
    ]
    for copies in spread:
        for copy in copies:
            copy.start()
    shards.arrive(2, 0)
    for copies in spread:
        copies[0].wait()
        for copy in copies[1:]:
            copy.wait_recv()
    shards.arrive(2, 1)
    f_size, h_size, k_size = f_mid.shape[2], h_out.shape[0] // dp, k_out.shape[0] // dp
    for t in range(4):
        for k in range(dp):
            at = (k * 4 + t) * size
            d_flip[: DOWN.stop, at : at + size] = d_land[
                t, :, k * size : (k + 1) * size
            ].astype(F32)
        for core in range(per_user):
            at = (core * 4 + t) * f_size
            piece = f_land[t, core].astype(F32)
            f_flip[GATE.start : UP.stop, at : at + f_size] = piece[: 2 * RANK]
            f_flip[DOWN, at : at + f_size] = piece[2 * RANK :]
            piece = hk_land[t, core].astype(F32)
            at = (core * 4 + t) * h_size
            h_flip[OUT, at : at + h_size] = piece[:RANK, :h_size]
            h_flip[QUERY, at : at + h_size] = piece[RANK : 2 * RANK, :h_size]
            at = (core * 4 + t) * k_size
            k_flip[KEY.start : VALUE.stop, at : at + k_size] = piece[2 * RANK :, :k_size]
    for flip, out in ((d_flip, d_out), (f_flip, f_out), (h_flip, h_out), (k_flip, k_out)):

        @pl.loop(0, out.shape[0] // LANES)
        def _(step, flip=flip, out=out):
            here = columns(step, LANES)
            out[here, :] = flip[:, here].T.astype(BF16)

    shards.arrive(3, 0)
    gather.finish()
    shards.arrive(3, 1)
    for place in range(dp // 2):
        for part in range(2):
            shards.wait_sibling(place, part)
    shards.finish()
    for copies in spread:
        for copy in copies[1:]:
            copy.wait_send()
    for copy in line:
        copy.wait_send()


def front(ids, layer_in, gains, f_all, d_all, hk_all, shard, dp, widths):
    rows, model = layer_in.shape
    anywhere = pl.BlockSpec(memory_space=pl.ANY)
    vmem = pl.BlockSpec(memory_space=pltpu.VMEM)
    tables_in = (f_all, d_all, hk_all)
    shapes = [(dp,) + table.shape[1:] for table in tables_in]
    joined = (shapes[1][1], dp * shapes[1][2])
    return pl.pallas_call(
        front_kernel,
        out_shape=(
            jax.ShapeDtypeStruct((4 * rows, model), BF16),
            jax.ShapeDtypeStruct((dp,) + ids.shape, jnp.int32),
        )
        + tuple(jax.ShapeDtypeStruct((width, LANES), BF16) for width in widths)
        + (jax.ShapeDtypeStruct((dp,) + shard.shape, BF16),),
        in_specs=[vmem] * 6 + [anywhere],
        out_specs=(anywhere,) + (vmem,) * 5 + (anywhere,),
        scratch_shapes=[
            pltpu.VMEM((rows, model), BF16),
            pltpu.VMEM((dp,) + ids.shape, jnp.int32),
        ]
        + [pltpu.VMEM(shape, BF16) for shape in shapes] * 2
        + [
            pltpu.VMEM(joined, BF16),
            pltpu.VMEM((4, dp // 4) + shapes[0][1:], BF16),
            pltpu.VMEM((4,) + joined, BF16),
            pltpu.VMEM((4, dp // 4) + shapes[2][1:], BF16),
        ]
        + [pltpu.VMEM((LANES, width), F32) for width in widths]
        + [
            pltpu.SemaphoreType.DMA,
            pltpu.SemaphoreType.DMA((3, 2)),
            pltpu.SemaphoreType.DMA((3, 2)),
            pltpu.SemaphoreType.DMA((4, dp)),
            pltpu.SemaphoreType.DMA((4,)),
            pltpu.SemaphoreType.DMA((3, 3)),
            pltpu.SemaphoreType.DMA((3, 4)),
            pltpu.SemaphoreType.DMA,
            pltpu.SemaphoreType.DMA((3, dp // 2, 2)),
            pltpu.SemaphoreType.DMA((dp, 2)),
        ],
        compiler_params=pltpu.CompilerParams(
            collective_id=9, has_side_effects=True, vmem_limit_bytes=VMEM_LIMIT
        ),
        name="front",
    )(ids, layer_in, gains, *tables_in, shard)


class Line:
    def __init__(self, slots, send_sem, recv_sem):
        self.d = lax.axis_index("dp")
        self.places = lax.axis_size("dp") // 2
        self.core = lax.rem(self.d, 2)
        self.z = self.d // 2
        self.sibling = self.d + 1 - 2 * self.core
        self.slots, self.send_sem, self.recv_sem = slots, send_sem, recv_sem

    def greet(self, others):
        barrier = pltpu.get_barrier_semaphore()
        for peer in others + [{"dp": self.sibling}]:
            pl.semaphore_signal(barrier, inc=1, device_id=peer, device_id_type=MESH)

        @pl.when(self.z > 0)
        def _():
            pl.semaphore_signal(
                barrier, inc=1, device_id={"dp": self.d - 2}, device_id_type=MESH
            )

        @pl.when(self.z < self.places - 1)
        def _():
            pl.semaphore_signal(
                barrier, inc=1, device_id={"dp": self.d + 2}, device_id_type=MESH
            )

        last = self.places - 1
        ends = (last - self.z) // last + self.z // last
        pl.semaphore_wait(barrier, len(others) + 3 - ends)

    def copy(self, place, kind, part):
        target = (self.d + 2, self.d - 2, self.sibling)[kind]
        slot = 2 * place + self.core
        half = self.slots.shape[1] // 2
        block = self.slots.at[slot, pl.ds(part * half, half)]
        return pltpu.make_async_remote_copy(
            src_ref=block,
            dst_ref=block,
            send_sem=self.send_sem.at[kind, place, part],
            recv_sem=self.recv_sem.at[slot, part],
            device_id={"dp": target},
            device_id_type=MESH,
        )

    def send_up(self, place, part):
        @pl.when(self.z < self.places - 1)
        def _():
            self.copy(place, 0, part).start()

    def send_down(self, place, part):
        @pl.when(self.z > 0)
        def _():
            self.copy(place, 1, part).start()

    def start(self):
        for part in range(2):
            self.send_up(self.z, part)
            self.send_down(self.z, part)
            self.copy(self.z, 2, part).start()

    def arrive(self, distance, part):
        @pl.when(self.z >= distance)
        def _():
            place = self.z - distance
            self.copy(place, 2, part).wait_recv()
            self.send_up(place, part)
            self.copy(place, 2, part).start()

        @pl.when(self.z + distance < self.places)
        def _():
            place = self.z + distance
            self.copy(place, 2, part).wait_recv()
            self.send_down(place, part)
            self.copy(place, 2, part).start()

    def wait_sibling(self, place, part):
        half = self.slots.shape[1] // 2
        other = 2 * place + 1 - self.core
        block = self.slots.at[other, pl.ds(part * half, half)]
        pltpu.make_async_copy(block, block, self.recv_sem.at[other, part]).wait()

    def finish(self):
        for place in range(self.places):
            for part in range(2):

                @pl.when((self.z >= place) & (self.z < self.places - 1))
                def _(place=place, part=part):
                    self.copy(place, 0, part).wait_send()

                @pl.when((self.z <= place) & (self.z > 0))
                def _(place=place, part=part):
                    self.copy(place, 1, part).wait_send()

                self.copy(place, 2, part).wait_send()


class WeightSpread:
    def __init__(self, sq, line, weight_hbm, h_table, w_out_all, h_all, own_sem, send_sem, recv_sem):
        model, q_width = w_out_all.shape[1:]
        share = model // 2
        mine = pl.ds(pl.multiple_of(line.core * share, 8), share)
        first = weight_hbm.shape[1] - q_width
        self.own = pltpu.make_async_copy(h_table, h_all.at[sq.me], own_sem)
        self.taken, self.onward = [], []
        for which, peer in enumerate((sq.across, sq.down, sq.far)):
            pairs = (
                (weight_hbm.at[mine, pl.ds(first, q_width)], w_out_all.at[sq.me, mine]),
                (h_table, h_all.at[sq.me]),
            )
            self.taken.append(
                [
                    remote(
                        source, target, send_sem.at[item, which], recv_sem.at[item, which], peer
                    )
                    for item, (source, target) in enumerate(pairs)
                ]
            )
            block = w_out_all.at[peer, mine]
            self.onward.append(
                pltpu.make_async_remote_copy(
                    src_ref=block,
                    dst_ref=block,
                    send_sem=send_sem.at[2, which],
                    recv_sem=recv_sem.at[2, which],
                    device_id={"dp": line.sibling},
                    device_id_type=MESH,
                )
            )

    def start(self):
        self.own.start()
        for copies in self.taken:
            for copy in copies:
                copy.start()

    def pass_on(self, which):
        for copy in self.taken[which]:
            copy.wait_recv()
        self.onward[which].start()

    def finish(self):
        self.own.wait()
        for copies, onward in zip(self.taken, self.onward):
            for copy in copies:
                copy.wait_send()
            onward.wait()


ARRIVALS = ((0, 1, 2, 3), (1, 0, 2, 3), (2, 1, 3, 0), (3, 2, 1, 0))


def mlp_kernel(
    rows,
    length_ref,
    x_hbm,
    gu_hbm,
    shard_hbm,
    d_ref,
    f_table,
    resid_ref,
    cot_ref,
    gains_ref,
    layer_ref,
    grad_ref,
    low_ref,
    low_down_ref,
    hidden_out,
    slope_out,
    gelu_out,
    down_out,
    work,
    low_sum,
    lows,
    seq,
    tiles,
    hidden,
    slope,
    gelu,
    down,
    load_sem,
    tile_sem,
    store_sem,
    keep_sem,
    line_send,
    line_recv,
    part,
    landing,
    passed,
    part_send,
    part_recv,
    *low_scratch,
):
    sq = Square(rows)
    line = Line(down, line_send, line_recv)
    width = hidden.shape[-1]
    tile = tiles.shape[-1] // 2
    steps = width // tile
    own_shard = pltpu.make_async_copy(shard_hbm, down.at[line.d], load_sem.at[0])
    seq_load = pltpu.make_async_copy(x_hbm, seq, load_sem.at[1])

    def tile_loads(step, slot):
        return [
            pltpu.make_async_copy(
                gu_hbm.at[:, columns(step, tile, which * width)],
                tiles.at[slot, :, pl.ds(which * tile, tile)],
                tile_sem.at[slot, which],
            )
            for which in range(2)
        ]

    def stores(step, slot):
        here = columns(step, tile)
        return [
            pltpu.make_async_copy(
                source.at[slot], target.at[:, :, here], store_sem.at[slot, which]
            )
            for which, (source, target) in enumerate(((slope, slope_out), (gelu, gelu_out)))
        ]

    own_shard.start()
    seq_load.start()
    for copy in tile_loads(0, 0):
        copy.start()
    line.greet([{"tensor": sq.across}, {"tensor": sq.down}])
    own_shard.wait()
    line.start()
    seq_load.wait()

    @pl.loop(0, 4)
    def _(chunk):
        low = nn(seq[chunk], d_ref[...])
        lows[0, chunk] = band(low, GATE).astype(BF16)
        lows[1, chunk] = band(low, UP).astype(BF16)
        low_ref[chunk] = band(low, GATE, UP).astype(BF16)

    @pl.loop(0, steps)
    def _(step):
        slot = lax.rem(step, 2)
        for copy in tile_loads(step, slot):
            copy.wait()

        @pl.when(step + 1 < steps)
        def _():
            for copy in tile_loads(step + 1, 1 - slot):
                copy.start()

        @pl.when(step >= 2)
        def _():
            for copy in stores(step - 2, slot):
                copy.wait()

        here = columns(step, tile)

        @pl.loop(0, 4)
        def _(chunk):
            both = nn(seq[chunk], tiles[slot])
            gate = both[:, :tile] + nt(lows[0, chunk], f_table[here, :])
            up = both[:, tile:] + nt(lows[1, chunk], f_table[here, :])
            hidden[chunk, :, here], slope[slot, chunk], gelu[slot, chunk] = gelu_parts(gate, up)

        for copy in stores(step, slot):
            copy.start()

        for part_at, part_of in ((steps // 2 - 1, 0), (steps - 2, 1)):

            @pl.when(step == part_at)
            def _(part_of=part_of):
                line.arrive(1, part_of)

    keep_hidden = pltpu.make_async_copy(hidden, hidden_out, keep_sem.at[0])
    keep_hidden.start()
    last = line.places - 1
    is_first, is_last = (last - line.z) // last, line.z // last
    is_third = line.z // 2 - is_last
    is_here = (is_first, 1 - is_first - is_third - is_last, is_third, is_last)
    order = [sum(flag * ARRIVALS[z][i] for z, flag in enumerate(is_here)) for i in range(4)]

    def scatter_at(place, half):
        at = 2 * place + half
        return ChunkScatter(
            sq, part.at[at], landing.at[at], passed.at[at], part_send.at[at], part_recv.at[at]
        )

    low_scatter = ChunkScatter(sq, *low_scratch)

    @pl.loop(0, 4)
    def _(chunk):
        low_scratch[0][chunk] = band(nn(hidden[chunk], f_table[...]), DOWN).astype(BF16)

    low_scatter.send_far()
    low_scatter.send_own()
    keeps = []
    earlier = low_scatter
    half_rows = down.shape[1] // 2
    arrivals = {(1, 0): ((2, 0),), (2, 0): ((2, 1),), (3, 0): ((3, 0),), (3, 1): ((3, 1),)}
    for turn in range(4):
        place = order[turn]
        for half in range(2):
            for distance, piece in arrivals.get((turn, half), ()):
                line.arrive(distance, piece)
            line.wait_sibling(place, half)
            scatter = scatter_at(place, half)

            @pl.loop(0, 4)
            def _(step, place=place, half=half, scatter=scatter):
                chunk = far_first(step)
                for core in range(2):
                    part[
                        2 * place + half, chunk, :, core * half_rows : (core + 1) * half_rows
                    ] = nt(
                        hidden[chunk],
                        down[2 * place + core, half * half_rows : (half + 1) * half_rows],
                    ).astype(BF16)

                @pl.when(step == 0)
                def _():
                    scatter.send_far()

                @pl.when(step == 1)
                def _():
                    scatter.send_own()

            earlier.pass_on()
            earlier = scatter
        pair = pl.ds(2 * place, 2)
        keep = pltpu.make_async_copy(down.at[pair], down_out.at[pair], keep_sem.at[1 + turn])
        keep.start()
        keeps.append(keep)
    low_scatter.collect(low_sum)
    low_down_ref[...] = low_sum[...].astype(BF16)
    earlier.pass_on()
    everything = [(place, half) for place in range(4) for half in range(2)]
    for place, half in everything:
        first = 2 * place * down.shape[1] + half * half_rows
        scatter_at(place, half).collect(
            work, ((0, first), (half_rows, first + down.shape[1]))
        )
    add_lifted(work, low_down_ref, d_ref)

    @pl.loop(0, rows // BLOCK)
    def _(step):
        here = pl.ds(pl.multiple_of(step * BLOCK, BLOCK), BLOCK)
        at = sq.me * rows + step * BLOCK + lax.broadcasted_iota(jnp.int32, (BLOCK, 1), 0)
        valid = (at < length_ref[0]).astype(F32)
        total = work[here, :]
        gain = gains_ref[3:4, :]
        layer_ref[here, :] = (valid * (resid_ref[here, :] + rms_norm(total, gain))).astype(BF16)
        grad_ref[here, :] = norm_back(total, gain, cot_ref[here, :].astype(F32) * valid).astype(
            BF16
        )

    for place, half in everything:
        scatter_at(place, half).finish()
    low_scatter.finish()
    line.finish()
    for step in (steps - 2, steps - 1):
        for copy in stores(step, step % 2):
            copy.wait()
    keep_hidden.wait()
    for keep in keeps:
        keep.wait()


def add_lifted(work, low, table):
    wide = tile_of(work.shape[1])

    @pl.loop(0, work.shape[1] // wide)
    def _(step):
        here = columns(step, wide)
        work[:, here] += nt(low[...], table[here, :])


def mlp_fused(lengths, seq, gu_w, shard, d_tab, f_tab, resid, cotangent, gains, dp):
    chunks, rows, model = seq.shape
    width = shard.shape[1]
    tile = 384
    wide = model // dp
    half = rows // 2
    anywhere = pl.BlockSpec(memory_space=pl.ANY)
    vmem = pl.BlockSpec(memory_space=pltpu.VMEM)
    saved = jax.ShapeDtypeStruct((4, rows, width), BF16)
    return pl.pallas_call(
        functools.partial(mlp_kernel, rows),
        out_shape=(
            jax.ShapeDtypeStruct((rows, model), BF16),
            jax.ShapeDtypeStruct((rows, model), BF16),
            jax.ShapeDtypeStruct((4, rows, LANES), BF16),
            jax.ShapeDtypeStruct((rows, LANES), BF16),
            saved,
            saved,
            saved,
            jax.ShapeDtypeStruct((dp,) + shard.shape, BF16),
        ),
        in_specs=[pl.BlockSpec(memory_space=pltpu.SMEM)] + [anywhere] * 3 + [vmem] * 5,
        out_specs=(vmem,) * 4 + (anywhere,) * 4,
        scratch_shapes=[
            pltpu.VMEM((rows, model), F32),
            pltpu.VMEM((rows, LANES), F32),
            pltpu.VMEM((2, 4, rows, LANES), BF16),
            pltpu.VMEM((4, rows, model), BF16),
            pltpu.VMEM((2, model, 2 * tile), BF16),
            pltpu.VMEM((4, rows, width), BF16),
            pltpu.VMEM((2, 4, rows, tile), BF16),
            pltpu.VMEM((2, 4, rows, tile), BF16),
            pltpu.VMEM((dp,) + shard.shape, BF16),
            pltpu.SemaphoreType.DMA((2,)),
            pltpu.SemaphoreType.DMA((2, 2)),
            pltpu.SemaphoreType.DMA((2, 2)),
            pltpu.SemaphoreType.DMA((5,)),
            pltpu.SemaphoreType.DMA((3, dp // 2, 2)),
            pltpu.SemaphoreType.DMA((dp, 2)),
            pltpu.VMEM((dp, 4, rows, wide), BF16),
            pltpu.VMEM((dp, 6, half, wide), BF16),
            pltpu.VMEM((dp, 2, half, wide), BF16),
            pltpu.SemaphoreType.DMA((dp, 6, 1)),
            pltpu.SemaphoreType.DMA((dp, 6, 1)),
        ]
        + scatter_scratch(rows, LANES),
        compiler_params=pltpu.CompilerParams(
            collective_id=7, has_side_effects=True, vmem_limit_bytes=62 * 1024 * 1024
        ),
        name="mlp",
    )(lengths, seq, gu_w, shard, d_tab, f_tab, resid, cotangent, gains)


class Layout:
    def __init__(self):
        self.dp = lax.axis_size("dp")
        self.tensor = lax.axis_size("tensor")
        self.total = self.dp * self.tensor
        self.d = lax.axis_index("dp")
        self.t = lax.axis_index("tensor")
        self.me = self.d * self.tensor + self.t
        self.heads_here = HQ // self.tensor
        self.ratio = HQ // KV
        self.share = max(1, self.tensor // KV)
        self.kv_owners = self.total // KV
        self.kv_head = self.t * self.heads_here // self.ratio
        self.user = self.me // self.dp
        self.kv_slice_head = self.me // self.kv_owners

    def device(self, flat):
        return {"dp": flat // self.tensor, "tensor": lax.rem(flat, self.tensor)}


def greet_all(lay):
    barrier = pltpu.get_barrier_semaphore()

    def signal(step, unused):
        peer = lax.rem(lay.me + step, lay.total)
        pl.semaphore_signal(
            barrier, inc=1, device_id=lay.device(peer), device_id_type=MESH
        )
        return unused

    lax.fori_loop(1, lay.total, signal, 0)
    pl.semaphore_wait(barrier, lay.total - 1)


def send_or_keep(lay, sends, source, target, send_sem, recv_sem, flat, maybe_own):
    def far():
        return pltpu.make_async_remote_copy(
            src_ref=source,
            dst_ref=target,
            send_sem=send_sem,
            recv_sem=recv_sem,
            device_id=lay.device(flat),
            device_id_type=MESH,
        )

    if maybe_own is None:
        copy = far()
        copy.start()
        sends.append((None, copy))
        return

    @pl.when(maybe_own)
    def _():
        pltpu.make_async_copy(source, target, recv_sem).start()

    @pl.when(jnp.logical_not(maybe_own))
    def _():
        far().start()

    sends.append((maybe_own, far()))


def finish(sends, received):
    for own, copy in sends:
        if own is None:
            copy.wait_send()
        else:

            @pl.when(jnp.logical_not(own))
            def _(copy=copy):
                copy.wait_send()

    for target, sem in received:
        pltpu.make_async_copy(target, target, sem).wait()


def tables_kernel(d_ref, f_ref, h_ref, k_ref, do_ref, fo_ref, ho_ref, ko_ref, *sems):
    lay = Layout()
    send_sems, recv_sem = sems[:4], sems[4]
    greet_all(lay)
    sends = []
    for step in range(lay.dp):
        group = lax.rem(lay.d + step, lay.dp)
        flat = group * lay.tensor + lay.user
        own = (lay.user == lay.t) if step == 0 else None
        for item, (source, target) in enumerate(((f_ref, fo_ref), (h_ref, ho_ref))):
            send_or_keep(
                lay,
                sends,
                source.at[group],
                target.at[lax.rem(lay.me, lay.dp)],
                send_sems[item].at[step],
                recv_sem.at[item],
                flat,
                own,
            )
        for extra in range(lay.share):
            user = lay.kv_slice_head * lay.share + extra
            flat = group * lay.tensor + user
            send_or_keep(
                lay,
                sends,
                k_ref.at[group],
                ko_ref.at[lax.rem(lay.me, lay.kv_owners)],
                send_sems[2].at[step, extra],
                recv_sem.at[2],
                flat,
                (user == lay.t) if step == 0 else None,
            )
    pltpu.make_async_copy(d_ref.at[lay.d], do_ref.at[lay.me], recv_sem.at[3]).start()
    for step in range(1, lay.total):
        flat = lax.rem(lay.me + step, lay.total)
        send_or_keep(
            lay,
            sends,
            d_ref.at[flat // lay.tensor],
            do_ref.at[lay.me],
            send_sems[3].at[step],
            recv_sem.at[3],
            flat,
            None,
        )
    finish(
        sends,
        (
            (fo_ref, recv_sem.at[0]),
            (ho_ref, recv_sem.at[1]),
            (ko_ref, recv_sem.at[2]),
            (do_ref, recv_sem.at[3]),
        ),
    )


def grads_kernel(d_ref, f_ref, h_ref, k_ref, do_ref, fo_ref, ho_ref, ko_ref, *sems):
    lay = Layout()
    send_sems, recv_sem = sems[:4], sems[4]
    greet_all(lay)
    sends = []
    for step in range(lay.dp):
        slot = lax.rem(lay.d + step, lay.dp)
        flat = lay.t * lay.dp + slot
        for item, (source, target) in enumerate(((f_ref, fo_ref), (h_ref, ho_ref))):
            send_or_keep(
                lay,
                sends,
                source.at[slot],
                target.at[lay.d],
                send_sems[item].at[step],
                recv_sem.at[item],
                flat,
                flat == lay.me,
            )
    for step in range(lay.kv_owners):
        slot = lax.rem(lay.d + step, lay.kv_owners)
        flat = lay.kv_head * lay.kv_owners + slot
        send_or_keep(
            lay,
            sends,
            k_ref.at[slot],
            ko_ref.at[lay.d * lay.share + lax.rem(lay.t, lay.share)],
            send_sems[2].at[step // lay.share, step % lay.share],
            recv_sem.at[2],
            flat,
            flat == lay.me,
        )
    pltpu.make_async_copy(d_ref.at[lay.me], do_ref.at[lay.me], recv_sem.at[3]).start()
    for step in range(1, lay.total):
        flat = lax.rem(lay.me + step, lay.total)
        send_or_keep(
            lay,
            sends,
            d_ref.at[flat],
            do_ref.at[lay.me],
            send_sems[3].at[step],
            recv_sem.at[3],
            flat,
            None,
        )
    finish(
        sends,
        (
            (fo_ref, recv_sem.at[0]),
            (ho_ref, recv_sem.at[1]),
            (ko_ref, recv_sem.at[2]),
            (do_ref, recv_sem.at[3]),
        ),
    )


def exchange(kernel, name, number, arrays, outs, dp, total, share):
    anywhere = pl.BlockSpec(memory_space=pl.ANY)
    return pl.pallas_call(
        kernel,
        out_shape=tuple(jax.ShapeDtypeStruct(shape, BF16) for shape in outs),
        in_specs=[anywhere] * 4,
        out_specs=(anywhere,) * 4,
        scratch_shapes=[
            pltpu.SemaphoreType.DMA((dp,)),
            pltpu.SemaphoreType.DMA((dp,)),
            pltpu.SemaphoreType.DMA((dp, share)),
            pltpu.SemaphoreType.DMA((total,)),
            pltpu.SemaphoreType.DMA((4,)),
        ],
        compiler_params=pltpu.CompilerParams(
            collective_id=number, has_side_effects=True, vmem_limit_bytes=VMEM_LIMIT
        ),
        name=name,
    )(*arrays)


def chunk_start(sq, chunk, part):
    is_own = (3 - chunk) // 3
    is_far = chunk // 3
    near = 1 - is_own - is_far
    neighbour = sq.down if part == 1 else sq.across
    block = sq.me * is_own + sq.far * is_far + neighbour * near
    other_half = chunk // 2 - is_far
    half = 1 - other_half if part == 1 else other_half
    return pl.multiple_of(block * sq.rows + half * sq.half, sq.half)


def rotate_back(values, cosine, sine):
    first, second = values[:, : HD // 2], values[:, HD // 2 :]
    return jnp.concatenate([first * cosine + second * sine, second * cosine - first * sine], axis=1)


def turned(values):
    return values.astype(F32).T.astype(BF16)


def rotate_rows(values, cosine, sine):
    first, second = values[:, : HD // 2], values[:, HD // 2 :]
    return jnp.concatenate([first * cosine - second * sine, second * cosine + first * sine], axis=1)


def softmax_weights(keys, queries, start, half, length):
    shape = (keys.shape[0], queries.shape[0])
    key_at = lax.broadcasted_iota(jnp.int32, shape, 0)
    query_at = lax.rem(lax.broadcasted_iota(jnp.int32, shape, 1), half) + start
    allowed = (key_at <= query_at) & (key_at < length)
    squash = jnp.tanh(nt(keys, queries) * (1.0 / SOFT_CAP))
    return squash, jnp.where(allowed, jnp.exp(SOFT_CAP * squash), 0.0)


def stack_heads(ref, here, heads):
    return jnp.concatenate([ref[here, h * HD : (h + 1) * HD] for h in range(heads)], axis=0)


def far_first(step):
    return step + 3 * ((3 - step) // 3) - 3 * (step // 3)


def attn_kernel(
    rows,
    length_ref,
    seq_hbm,
    weight_hbm,
    d_table,
    h_table,
    k_table,
    cos_ref,
    sin_ref,
    layer_ref,
    gains_ref,
    q_ref,
    k_ref,
    kt_ref,
    v_ref,
    attended_ref,
    inverse_ref,
    low_ref,
    low_out_ref,
    total_ref,
    resid_ref,
    normed_ref,
    mlp_out,
    w_out_all,
    h_all,
    seq,
    weight,
    vt,
    low_sum,
    load_sem,
    own_sem,
    gather_send,
    gather_recv,
    w_own,
    w_send,
    w_recv,
    *scratch,
):
    sq = Square(rows)
    half = sq.half
    model = total_ref.shape[-1]
    q_width = q_ref.shape[1]
    qkv_width = q_width + 2 * HD
    heads = q_width // HD
    wide = tile_of(model)
    weight_load = pltpu.make_async_copy(weight_hbm, weight, load_sem.at[0])
    seq_load = pltpu.make_async_copy(seq_hbm, seq, load_sem.at[1])
    weight_load.start()
    seq_load.start()
    line = Line(None, None, None)
    greet(
        [{"tensor": peer} for peer in (sq.across, sq.down, sq.far)] + [{"dp": line.sibling}]
    )
    weight_load.wait()
    seq_load.wait()

    @pl.loop(0, 4)
    def _(block):
        here = pl.ds(pl.multiple_of(block * rows, rows), rows)
        low = band(nn(seq[block], d_table[...]), QUERY, VALUE).astype(BF16)
        low_ref[here, :] = low
        cosine, sine = cos_ref[here, :], sin_ref[here, :]
        for h in range(heads):
            column = slice(h * HD, (h + 1) * HD)
            query = nn(seq[block], weight[:, column]) + nt(
                band(low.astype(F32), QUERY).astype(BF16), h_table[column, :]
            )
            q_ref[here, column] = (rotate_rows(query, cosine, sine) * HD ** (-0.5)).astype(BF16)
        key = nn(seq[block], weight[:, q_width : q_width + HD]) + nt(
            band(low.astype(F32), KEY).astype(BF16), k_table[...]
        )
        key = rotate_rows(key, cosine, sine)
        k_ref[here, :] = key.astype(BF16)
        kt_ref[:, here] = key.T.astype(BF16)
        value = nn(seq[block], weight[:, q_width + HD : qkv_width]) + nt(
            band(low.astype(F32), VALUE).astype(BF16), k_table[...]
        )
        v_ref[here, :] = value.astype(BF16)
        vt[:, here] = value.T.astype(BF16)

    part, part_low = scratch[0], scratch[5]
    scatters = (ChunkScatter(sq, *scratch[:5]), ChunkScatter(sq, *scratch[5:10]))

    @pl.loop(0, 4)
    def _(step):
        chunk = far_first(step)
        for side in range(2):
            start = chunk_start(sq, chunk, side)
            here = pl.ds(start, half)
            unused, weights = softmax_weights(
                k_ref[...], stack_heads(q_ref, here, heads), start, half, length_ref[0]
            )
            inverse = 1.0 / jnp.sum(weights, axis=0, keepdims=True)
            mixed = nn(vt[...], (weights * inverse).astype(BF16)).T.astype(BF16)
            for h in range(heads):
                inverse_ref[h : h + 1, here] = inverse[:, h * half : (h + 1) * half]
                attended_ref[here, h * HD : (h + 1) * HD] = mixed[h * half : (h + 1) * half]

        attended = jnp.concatenate(
            [attended_ref[pl.ds(chunk_start(sq, chunk, side), half), :] for side in range(2)],
            axis=0,
        )
        part_low[chunk] = band(nn(attended, h_table[...]), OUT).astype(BF16)

        @pl.loop(0, model // wide)
        def _(tile):
            here = columns(tile, wide)
            part[chunk, :, here] = nt(attended, weight[here, qkv_width:]).astype(BF16)

            @pl.when(step == 0)
            def _():
                scatters[0].send(1, tile)

            @pl.when(step == 1)
            def _():
                scatters[0].send(0, tile)

        @pl.when(step == 0)
        def _():
            scatters[1].send_far()

        @pl.when(step == 1)
        def _():
            scatters[1].send_own()

    for scatter in scatters:
        scatter.pass_on()
    scatters[1].collect(low_sum)
    low_out_ref[...] = low_sum[...].astype(BF16)
    scatters[0].collect(total_ref)
    add_lifted(total_ref, low_out_ref, d_table)

    @pl.loop(0, rows // BLOCK)
    def _(step):
        here = pl.ds(pl.multiple_of(step * BLOCK, BLOCK), BLOCK)
        resid = layer_ref[here, :].astype(F32) + rms_norm(total_ref[here, :], gains_ref[1:2, :])
        resid_ref[here, :] = resid
        normed_ref[here, :] = rms_norm(resid, gains_ref[2:3, :]).astype(BF16)

    gather = ChunkGather(sq, normed_ref, mlp_out, gather_send, gather_recv)
    gather.start()
    own = pltpu.make_async_copy(normed_ref, mlp_out.at[0], own_sem)
    own.start()
    gather.wait_chunk(1)
    weights = WeightSpread(
        sq, line, weight_hbm, h_table, w_out_all, h_all, w_own, w_send, w_recv
    )
    weights.start()
    for chunk in range(2, 4):
        gather.wait_chunk(chunk)
    own.wait()
    for which in range(3):
        weights.pass_on(which)
    weights.finish()
    gather.finish()
    for scatter in scatters:
        scatter.finish()


def attn_fused(lengths, seq, weight, d_tab, h_tab, k_tab, cosine, sine, layer_in, gains):
    rows, model = layer_in.shape
    q_width = weight.shape[1] - 2 * HD
    q_width //= 2
    qkv_width = q_width + 2 * HD
    anywhere = pl.BlockSpec(memory_space=pl.ANY)
    vmem = pl.BlockSpec(memory_space=pltpu.VMEM)
    narrow = jax.ShapeDtypeStruct((LEN, HD), BF16)
    return pl.pallas_call(
        functools.partial(attn_kernel, rows),
        out_shape=(
            jax.ShapeDtypeStruct((LEN, q_width), BF16),
            narrow,
            jax.ShapeDtypeStruct((HD, LEN), BF16),
            narrow,
            jax.ShapeDtypeStruct((LEN, q_width), BF16),
            jax.ShapeDtypeStruct((q_width // HD, LEN), F32),
            jax.ShapeDtypeStruct((LEN, LANES), BF16),
            jax.ShapeDtypeStruct((rows, LANES), BF16),
            jax.ShapeDtypeStruct((rows, model), F32),
            jax.ShapeDtypeStruct((rows, model), F32),
            jax.ShapeDtypeStruct((rows, model), BF16),
            jax.ShapeDtypeStruct((4, rows, model), BF16),
            jax.ShapeDtypeStruct((4, model, q_width), BF16),
            jax.ShapeDtypeStruct((4, q_width, LANES), BF16),
        ),
        in_specs=[pl.BlockSpec(memory_space=pltpu.SMEM)] + [anywhere] * 2 + [vmem] * 7,
        out_specs=(vmem,) * 11 + (anywhere,) * 3,
        scratch_shapes=[
            pltpu.VMEM((4, rows, model), BF16),
            pltpu.VMEM(weight.shape, BF16),
            pltpu.VMEM((HD, LEN), BF16),
            pltpu.VMEM((rows, LANES), F32),
            pltpu.SemaphoreType.DMA((2,)),
            pltpu.SemaphoreType.DMA,
            pltpu.SemaphoreType.DMA((6,)),
            pltpu.SemaphoreType.DMA((6,)),
            pltpu.SemaphoreType.DMA,
            pltpu.SemaphoreType.DMA((3, 3)),
            pltpu.SemaphoreType.DMA((3, 3)),
        ]
        + scatter_scratch(rows, model, model // tile_of(model))
        + scatter_scratch(rows, LANES),
        compiler_params=pltpu.CompilerParams(
            collective_id=8, has_side_effects=True, vmem_limit_bytes=62 * 1024 * 1024
        ),
        name="attn",
    )(lengths, seq, weight, d_tab, h_tab, k_tab, cosine, sine, layer_in, gains)


def attn_back_kernel(
    rows,
    ids_ref,
    length_ref,
    back_ref,
    low_gu_ref,
    resid_ref,
    total_ref,
    cot_ref,
    layer_hbm,
    gains_ref,
    weight_hbm,
    w_out_hbm,
    seq_hbm,
    q_hbm,
    k_hbm,
    kt_hbm,
    v_hbm,
    attended_hbm,
    inverse_ref,
    cos_hbm,
    sin_hbm,
    low_hbm,
    d_table,
    h_all,
    k_table,
    normed_hbm,
    low_out_ref,
    grad_mlp_hbm,
    low_down_ref,
    f_ref,
    o_ref,
    in_out,
    heads_out,
    hidden_out,
    query_out,
    keyval_out,
    gateup_out,
    resid_out,
    q_ref,
    k_ref,
    kt_ref,
    v_ref,
    attended_ref,
    cos_ref,
    sin_ref,
    low_ref,
    normed_ref,
    grad_mlp_ref,
    layer_ref,
    weight,
    w_out,
    work,
    g_ref,
    low_sum,
    buf,
    att_send,
    att,
    low_own,
    low_all,
    q_grad,
    k_sum,
    v_sum,
    kv_grad,
    joined,
    d_turned,
    h_turned,
    k_turned,
    d_send,
    d_land,
    d_sum,
    d_recv,
    f_recv,
    hk_send,
    hk_land,
    hk_recv,
    load_sem,
    late_sem,
    att_sends,
    att_recvs,
    f_sem,
    d_sem,
    hk_sem,
    group_send,
    group_recv,
    line_recv,
    *scratch,
):
    sq = Square(rows)
    dp = lax.axis_size("dp")
    d = lax.axis_index("dp")
    model = o_ref.shape[-1]
    half = sq.half
    wide = tile_of(model)
    q_width = q_ref.shape[1]
    qkv_width = q_width + 2 * HD
    others = (sq.far, sq.across, sq.down)
    sources = [w_out_hbm.at[peer] for peer in others]
    sources.append(weight_hbm.at[:, pl.ds(qkv_width, q_width)])
    loads = [
        pltpu.make_async_copy(source, w_out.at[which % 2], load_sem.at[2 + which])
        for which, source in enumerate(sources)
    ]
    weight_load = pltpu.make_async_copy(
        weight_hbm.at[:, pl.ds(0, qkv_width)], weight, load_sem.at[0]
    )
    seq_load = pltpu.make_async_copy(seq_hbm, buf, load_sem.at[1])
    late = [
        pltpu.make_async_copy(source, target, late_sem.at[which])
        for which, (source, target) in enumerate(
            (
                (q_hbm, q_ref),
                (k_hbm, k_ref),
                (kt_hbm, kt_ref),
                (v_hbm, v_ref),
                (attended_hbm, attended_ref),
                (cos_hbm, cos_ref),
                (sin_hbm, sin_ref),
                (low_hbm, low_ref),
                (normed_hbm, normed_ref),
                (grad_mlp_hbm, grad_mlp_ref),
                (layer_hbm, layer_ref),
            )
        )
    ]
    loads[0].start()
    loads[1].start()
    for copy in late:
        copy.start()
    weight_load.start()
    seq_load.start()
    peers = [{"tensor": peer} for peer in (sq.across, sq.down, sq.far)]
    peers += [{"dp": lax.rem(d + step, dp)} for step in range(1, dp)]
    call(peers)

    low_gu = low_gu_ref[...].astype(BF16)

    @pl.loop(0, model // wide)
    def _(step):
        here = columns(step, wide)
        work[:, here] = back_ref[:, here] + nt(low_gu, d_table[here, :])

    @pl.loop(0, rows // BLOCK)
    def _(step):
        here = pl.ds(pl.multiple_of(step * BLOCK, BLOCK), BLOCK)
        at = sq.me * rows + step * BLOCK + lax.broadcasted_iota(jnp.int32, (BLOCK, 1), 0)
        valid = (at < length_ref[0]).astype(F32)
        mid = cot_ref[here, :].astype(F32) * valid + norm_back(
            resid_ref[here, :], gains_ref[2:3, :], work[here, :]
        )
        work[here, :] = mid
        g_ref[here, :] = norm_back(total_ref[here, :], gains_ref[1:2, :], mid).astype(BF16)

    low_own[...] = band(nn(g_ref[...], d_table[...]), OUT).astype(BF16)
    pl.semaphore_wait(pltpu.get_barrier_semaphore(), len(peers))
    heads_out_copies = []
    for which, peer in enumerate(others + (sq.me,)):
        loads[which].wait()
        grads = (nn(g_ref[...], w_out[which % 2]) + nt(low_own[...], h_all[peer])).astype(BF16)
        if which < 2:
            loads[which + 2].start()
        if which == 3:
            att[sq.me] = grads
            low_all[sq.me] = low_own[...]
            continue
        att_send[which] = grads
        copies = (
            remote(
                att_send.at[which],
                att.at[sq.me],
                att_sends.at[which, 0],
                att_recvs.at[which, 0],
                peer,
            ),
            remote(
                low_own,
                low_all.at[sq.me],
                att_sends.at[which, 1],
                att_recvs.at[which, 1],
                peer,
            ),
        )
        for copy in copies:
            copy.start()
        heads_out_copies.append(copies)
    line = []
    line += along(lambda k: f_ref.at[k // 2, lax.rem(k, 2)], f_recv, f_sem, line_recv.at[0])
    part, part_low = scratch[0], scratch[5]
    scatters = (ChunkScatter(sq, *scratch[:5]), ChunkScatter(sq, *scratch[5:10]))

    for copy in late:
        copy.wait()
    d_turned[...] = jnp.zeros_like(d_turned)
    low_grads = (
        (turned(low_gu)[GATE.start : UP.stop], normed_ref, slice(GATE.start, UP.stop)),
        (turned(low_out_ref[...])[OUT], g_ref, OUT),
        (turned(low_down_ref[...])[DOWN], grad_mlp_ref, DOWN),
    )

    @pl.loop(0, model // wide)
    def _(step):
        here = columns(step, wide)
        for low, source, place in low_grads:
            d_turned[place, here] = nn(low, source[:, here])

    h_turned[...] = jnp.zeros_like(h_turned)
    k_turned[...] = jnp.zeros_like(k_turned)
    k_sum[...] = jnp.zeros_like(k_sum)
    v_sum[...] = jnp.zeros_like(v_sum)
    heads = q_width // HD
    stacked = heads * half

    @pl.loop(0, 4)
    def _(turn):
        for step, which in ((1, 1), (2, 2), (3, 0)):

            @pl.when(turn == step)
            def _(which=which):
                for copy in heads_out_copies[which]:
                    copy.wait_recv()

        is_own, is_far = (3 - turn) // 3, turn // 3
        is_down = turn // 2 - is_far
        block = (
            sq.me * is_own
            + sq.far * is_far
            + sq.down * is_down
            + sq.across * (1 - is_own - is_far - is_down)
        )
        low_turned = turned(low_all[block])[OUT]
        h_turned[:RANK, :] += nn(
            low_turned, attended_ref[pl.ds(pl.multiple_of(block * rows, rows), rows), :]
        )
        for last in range(4):

            @pl.when(block == last)
            def _(last=last):
                seen = slice(0, (last + 1) * rows)

                @pl.loop(0, 2)
                def _(side):
                    start = pl.multiple_of(last * rows + side * half, half)
                    here = pl.ds(start, half)
                    place = pl.ds(pl.multiple_of(side * half, half), half)
                    queries = stack_heads(q_ref, here, heads)
                    grads = jnp.concatenate(
                        [att[last, place, h * HD : (h + 1) * HD] for h in range(heads)], axis=0
                    )
                    inverse = jnp.concatenate(
                        [inverse_ref[h : h + 1, here] for h in range(heads)], axis=1
                    )
                    squash, weights = softmax_weights(
                        k_ref[seen, :], queries, start, half, length_ref[0]
                    )
                    probs = weights * inverse
                    grad_probs = nt(v_ref[seen, :], grads)
                    mean = jnp.sum(probs * grad_probs, axis=0, keepdims=True)
                    grad_raw = (probs * (grad_probs - mean) * (1.0 - squash * squash)).astype(BF16)
                    k_sum[seen, :] += nn(grad_raw, queries)
                    v_sum[seen, :] += nn(probs.astype(BF16), grads)
                    q_back = nn(kt_ref[:, seen], grad_raw).T * HD ** (-0.5)
                    for h in range(heads):
                        q_grad[here, h * HD : (h + 1) * HD] = rotate_back(
                            q_back[h * half : (h + 1) * half], cos_ref[here, :], sin_ref[here, :]
                        ).astype(BF16)

    weight_load.wait()
    kv_grad[:, :HD] = rotate_back(k_sum[...], cos_ref[...], sin_ref[...]).astype(BF16)
    kv_grad[:, HD:] = v_sum[...].astype(BF16)

    @pl.loop(0, 4)
    def _(step):
        chunk = far_first(step)
        for side in range(2):
            here = pl.ds(chunk_start(sq, chunk, side), half)
            place = pl.ds(side * half, half)
            joined[chunk, place, :q_width] = q_grad[here, :]
            joined[chunk, place, q_width:] = kv_grad[here, :]
        part_low[chunk] = (
            band(nn(joined[chunk, :, :q_width], h_all[sq.me]), QUERY)
            + band(nn(joined[chunk, :, q_width : q_width + HD], k_table[...]), KEY)
            + band(nn(joined[chunk, :, q_width + HD :], k_table[...]), VALUE)
        ).astype(BF16)

        @pl.loop(0, model // wide)
        def _(tile):
            here = columns(tile, wide)
            part[chunk, :, here] = nt(joined[chunk], weight[here, :]).astype(BF16)

            @pl.when(step == 0)
            def _():
                scatters[0].send(1, tile)

            @pl.when(step == 1)
            def _():
                scatters[0].send(0, tile)

        @pl.when(step == 0)
        def _():
            scatters[1].send_far()

        @pl.when(step == 1)
        def _():
            scatters[1].send_own()

    seq_load.wait()

    @pl.loop(0, 4)
    def _(chunk):
        grad_turned = turned(part_low[chunk])[: VALUE.stop]
        for side in range(2):
            here = pl.ds(chunk_start(sq, chunk, side), half)
            place = slice(side * half, (side + 1) * half)
            low_turned = turned(low_ref[here, :])
            mine = joined.at[chunk, pl.ds(side * half, half)]
            h_turned[RANK : 2 * RANK, :] += nn(low_turned[QUERY], mine[:, :q_width])
            k_turned[:RANK, :] += nn(low_turned[KEY], mine[:, q_width : q_width + HD])
            k_turned[RANK : 2 * RANK, :] += nn(low_turned[VALUE], mine[:, q_width + HD :])
            where_from = chunk_start(sq, chunk, side)
            block = where_from // rows
            inside = pl.ds(pl.multiple_of(where_from - block * rows, half), half)

            @pl.loop(0, model // wide)
            def _(tile):
                where = columns(tile, wide)
                d_turned[: VALUE.stop, where] += nn(
                    grad_turned[:, place],
                    buf[block, inside, where],
                )

    @pl.loop(0, model // LANES)
    def _(step):
        here = columns(step, LANES)
        d_send[here, :] = d_turned[:, here].T.astype(BF16)

    d_rows = d_sum.shape[1]
    spread = []
    for k in range(dp):
        spread.append(
            sq.spread(
                lambda peer, k=k: d_send.at[pl.ds(pl.multiple_of((k * 4 + peer) * d_rows, 8), d_rows)],
                d_land.at[k],
                group_send.at[k],
                group_recv.at[k],
            )
        )
    cores = hk_send.shape[0]
    h_size, k_size = q_width // dp, HD // dp
    hk_send[...] = jnp.zeros_like(hk_send)
    for core in range(cores):
        for peer in range(4):
            at = core * 4 + peer
            hk_send[core, peer, : 2 * RANK, :h_size] = h_turned[
                : 2 * RANK, at * h_size : (at + 1) * h_size
            ].astype(BF16)
            hk_send[core, peer, 2 * RANK :, :k_size] = k_turned[
                : 2 * RANK, at * k_size : (at + 1) * k_size
            ].astype(BF16)
    spread.append(
        sq.spread(lambda peer: hk_send.at[:, peer], hk_land, group_send.at[dp], group_recv.at[dp])
    )
    for copies in spread:
        for copy in copies:
            copy.start()
    for scatter in scatters:
        scatter.pass_on()
    for copies in spread:
        copies[0].wait()
        for copy in copies[1:]:
            copy.wait_recv()
    for k in range(dp):
        d_sum[k] = sum(d_land[k, t].astype(F32) for t in range(4)).astype(BF16)
    line += along(lambda k: d_sum.at[k], d_recv, d_sem, line_recv.at[1])
    line += along(lambda k: hk_land.at[k // 2, lax.rem(k, 2)], hk_recv, hk_sem, line_recv.at[2])
    scatters[1].collect(low_sum)
    low_qkv = low_sum[...].astype(BF16)
    scatters[0].arrived()
    landing = scratch[1]
    low_sum[...] = low_qkv.astype(F32)

    @pl.loop(0, rows // BLOCK)
    def _(step):
        here = pl.ds(pl.multiple_of(step * BLOCK, BLOCK), BLOCK)
        link = (step * BLOCK) // half
        there = pl.ds(pl.multiple_of(step * BLOCK - link * half, BLOCK), BLOCK)
        total = (
            part[0, here, :].astype(F32)
            + landing[link, there, :].astype(F32)
            + landing[4 + link, there, :].astype(F32)
            + nt(low_sum[here, :].astype(BF16), d_table[...])
        )
        o_ref[here, :] = (
            work[here, :] + norm_back(layer_ref[here, :].astype(F32), gains_ref[0:1, :], total)
        ).astype(BF16)

    for item, target in enumerate((f_recv, d_recv, hk_recv)):
        pltpu.make_async_copy(target, target, line_recv.at[item]).wait()

    @pl.loop(0, NA)
    def _(adapter):
        def pick(received):
            total = None
            for group in range(dp):
                mine = jnp.where(
                    ids_ref[group] == adapter, received[group].astype(F32), 0.0
                )
                total = mine if total is None else total + mine
            return total

        d_all = pick(d_recv)
        in_out[adapter] = d_all[:, : 5 * RANK]
        d_flip = d_all.T
        f_all = pick(f_recv)
        hidden_out[adapter] = f_all[:RANK]
        hk_all = pick(hk_recv)
        heads_out[adapter] = hk_all[:RANK, :h_size]
        query_out[adapter] = hk_all[RANK : 2 * RANK, :h_size]
        for which in range(2):
            first = (which + 2) * RANK
            keyval_out[adapter, which] = hk_all[first : first + RANK, :k_size]
            first = (which + 1) * RANK
            gateup_out[adapter, which] = f_all[first : first + RANK]
            first = (which + 5) * RANK
            resid_out[adapter, which] = d_flip[first : first + RANK]

    for copies in spread:
        for copy in copies[1:]:
            copy.wait_send()
    for copies in heads_out_copies:
        for copy in copies:
            copy.wait_send()
    for copy in line:
        copy.wait_send()
    for scatter in scatters:
        scatter.finish()


LATE = (10, 11, 12, 13, 14, 16, 17, 18, 22, 24, 5)


def attn_back_fused(scalars, arrays, grad_shapes, dp, total):
    anywhere = pl.BlockSpec(memory_space=pl.ANY)
    vmem = pl.BlockSpec(memory_space=pltpu.VMEM)
    smem = pl.BlockSpec(memory_space=pltpu.SMEM)
    rows, model = arrays[0].shape
    weight, q, f_in = arrays[7], arrays[10], arrays[-1]
    q_width = q.shape[1]
    specs = [smem, smem] + [vmem] * len(arrays)
    late = [arrays[which] for which in LATE]
    for which in LATE + (7, 8, 9):
        specs[2 + which] = anywhere
    outs = [jax.ShapeDtypeStruct((rows, model), BF16)]
    outs += [jax.ShapeDtypeStruct(shape, F32) for shape in grad_shapes]
    d_rows = model // total
    messages = f_in.shape[2:]
    return pl.pallas_call(
        functools.partial(attn_back_kernel, rows),
        out_shape=tuple(outs),
        in_specs=specs,
        out_specs=(vmem,) * len(outs),
        scratch_shapes=[
            *(pltpu.VMEM(array.shape, array.dtype) for array in late),
            pltpu.VMEM((model, q_width + 2 * HD), BF16),
            pltpu.VMEM((2, model, q_width), BF16),
            pltpu.VMEM((rows, model), F32),
            pltpu.VMEM((rows, model), BF16),
            pltpu.VMEM((rows, LANES), F32),
            pltpu.VMEM((4, rows, model), BF16),
            pltpu.VMEM((3, rows, q_width), BF16),
            pltpu.VMEM((4, rows, q_width), BF16),
            pltpu.VMEM((rows, LANES), BF16),
            pltpu.VMEM((4, rows, LANES), BF16),
            pltpu.VMEM((LEN, q_width), BF16),
            pltpu.VMEM((LEN, HD), F32),
            pltpu.VMEM((LEN, HD), F32),
            pltpu.VMEM((LEN, 2 * HD), BF16),
            pltpu.VMEM((4, rows, q_width + 2 * HD), BF16),
            pltpu.VMEM((LANES, model), F32),
            pltpu.VMEM((2 * RANK, q_width), F32),
            pltpu.VMEM((2 * RANK, HD), F32),
            pltpu.VMEM((model, LANES), BF16),
            pltpu.VMEM((dp, 4, d_rows, LANES), BF16),
            pltpu.VMEM((dp, d_rows, LANES), BF16),
            pltpu.VMEM((dp, d_rows, LANES), BF16),
            pltpu.VMEM((dp,) + messages, BF16),
            pltpu.VMEM((dp // 4, 4, 4 * RANK, LANES), BF16),
            pltpu.VMEM((4, dp // 4, 4 * RANK, LANES), BF16),
            pltpu.VMEM((dp, 4 * RANK, LANES), BF16),
            pltpu.SemaphoreType.DMA((6,)),
            pltpu.SemaphoreType.DMA((len(late),)),
            pltpu.SemaphoreType.DMA((3, 2)),
            pltpu.SemaphoreType.DMA((3, 2)),
            pltpu.SemaphoreType.DMA((dp,)),
            pltpu.SemaphoreType.DMA((dp,)),
            pltpu.SemaphoreType.DMA((dp,)),
            pltpu.SemaphoreType.DMA((dp + 1, 3)),
            pltpu.SemaphoreType.DMA((dp + 1, 4)),
            pltpu.SemaphoreType.DMA((3,)),
        ]
        + scatter_scratch(rows, model, model // tile_of(model))
        + scatter_scratch(rows, LANES),
        compiler_params=pltpu.CompilerParams(
            collective_id=6, has_side_effects=True, vmem_limit_bytes=62 * 1024 * 1024
        ),
        name="attn_back",
    )(*scalars, *arrays)


def per_device(
    layer_in,
    cotangent,
    lengths,
    adapter_ids,
    norm_gains,
    query_weight,
    key_weight,
    value_weight,
    out_weight,
    gate_weight,
    up_weight,
    down_weight,
    adapt_in,
    adapt_heads,
    adapt_hidden,
    lift_query,
    lift_keyval,
    lift_gateup,
    lift_resid,
):
    lay = Layout()
    count = lay.tensor
    rows = layer_in.shape[0]
    group_rows = rows * count
    assert lengths.shape[0] == 1 and group_rows == LEN
    heads_here = lay.heads_here
    head_width = heads_here * HD
    hidden_here = FF // count
    assert lay.ratio % heads_here == 0

    key_cols = lax.dynamic_slice_in_dim(key_weight, lay.kv_head * HD, HD, 1)
    value_cols = lax.dynamic_slice_in_dim(value_weight, lay.kv_head * HD, HD, 1)
    attn_shard = jnp.concatenate([query_weight, key_cols, value_cols, out_weight.T], axis=1)
    gate_up_shard = jnp.concatenate([gate_weight, up_weight], axis=1)
    down_shard = down_weight.T
    attn_shard, gate_up_shard, down_shard = lax.optimization_barrier(
        (attn_shard, gate_up_shard, down_shard)
    )
    qkv_width = head_width + 2 * HD

    cosine, sine = tables(LEN, HD)
    if count == 4 and lay.dp == 8:
        seq_attn, all_ids, d_tab, f_tab, h_tab, k_tab, attn_w = front(
            jnp.broadcast_to(adapter_ids, (8, LANES)),
            layer_in,
            norm_gains,
            jnp.concatenate(
                [
                    lift_gateup.reshape(NA, 2 * RANK, -1),
                    jnp.swapaxes(adapt_hidden, 1, 2),
                ],
                axis=1,
            ),
            jnp.concatenate(
                [jnp.swapaxes(adapt_in, 1, 2), lift_resid.reshape(NA, 2 * RANK, -1)], axis=1
            ),
            jnp.concatenate(
                [
                    jnp.swapaxes(adapt_heads, 1, 2),
                    lift_query,
                    jnp.pad(
                        lift_keyval.reshape(NA, 2 * RANK, -1),
                        ((0, 0), (0, 0), (0, lift_query.shape[2] - lift_keyval.shape[3])),
                    ),
                ],
                axis=1,
            ),
            attn_shard,
            lay.dp,
            (D, hidden_here, head_width, HD),
        )
        attn_w = attn_w.reshape(D, -1)
        gate_up_shard, attn_w = lax.optimization_barrier((gate_up_shard, attn_w))
        gate_up_w = lax.all_gather(gate_up_shard, "dp", axis=0, tiled=True)
        (
            queries,
            keys,
            keys_turned,
            values,
            attended,
            inverse,
            low_qkv,
            low_out,
            attn_total,
            resid_mid,
            normed_mlp,
            seq_mlp,
            w_out_all,
            h_all,
        ) = attn_fused(
            lengths,
            seq_attn.reshape(count, rows, D),
            attn_w,
            d_tab,
            h_tab,
            k_tab,
            cosine.reshape(LEN, HD // 2),
            sine.reshape(LEN, HD // 2),
            layer_in,
            norm_gains,
        )
        (
            layer_out,
            grad_mlp,
            low_gu,
            low_down,
            hidden,
            slope,
            gelu,
            down_w,
        ) = mlp_fused(
            lengths,
            seq_mlp,
            gate_up_w,
            down_shard,
            d_tab,
            f_tab,
            resid_mid,
            cotangent,
            norm_gains,
            lay.dp,
        )
        mlp_back, grad_low_gu, f_grad = mlp_back_fused(
            grad_mlp,
            down_w.reshape(D, hidden_here),
            gate_up_w,
            slope,
            gelu,
            hidden,
            low_gu,
            d_tab,
            f_tab,
            lay.dp,
        )
        grad_shapes = [
            table.shape
            for table in (
                adapt_in,
                adapt_heads,
                adapt_hidden,
                lift_query,
                lift_keyval,
                lift_gateup,
                lift_resid,
            )
        ]
        for which in (1, 2):
            shape = grad_shapes[which]
            grad_shapes[which] = (shape[0], shape[2], shape[1])
        grads = list(
            attn_back_fused(
                (all_ids[:, 0, 0], lengths),
                (
                    mlp_back,
                    grad_low_gu,
                    resid_mid,
                    attn_total,
                    cotangent,
                    layer_in,
                    norm_gains,
                    attn_w,
                    w_out_all,
                    seq_attn.reshape(count, rows, D),
                    queries,
                    keys,
                    keys_turned,
                    values,
                    attended,
                    inverse,
                    cosine.reshape(LEN, HD // 2),
                    sine.reshape(LEN, HD // 2),
                    low_qkv,
                    d_tab,
                    h_all,
                    k_tab,
                    normed_mlp,
                    low_out,
                    grad_mlp,
                    low_down,
                    f_grad,
                ),
                tuple(grad_shapes),
                lay.dp,
                lay.total,
            )
        )
        for which in (2, 3):
            grads[which] = jnp.swapaxes(grads[which], 1, 2)
        return (layer_out, *grads)

    attn_w = lax.all_gather(attn_shard, "dp", axis=0, tiled=True)
    gate_up_w = lax.all_gather(gate_up_shard, "dp", axis=0, tiled=True)

    all_ids = lax.all_gather(adapter_ids[:, 0], "dp", axis=0, tiled=True)
    group_hot = (all_ids[:, None] == jnp.arange(NA, dtype=jnp.int32)[None, :]).astype(BF16)

    def rows_of(table):
        moved = jnp.moveaxis(table, -1, 1)
        return moved.reshape(NA, moved.shape[1], -1)

    def choose(*parts):
        packed = lanes(*parts)
        return lax.dot_general(
            group_hot, packed, (((1,), (0,)), ((), ())), preferred_element_type=F32
        ).astype(BF16)

    d_send = choose((QUERY, adapt_in), (OUT, rows_of(lift_resid)))
    f_send = choose((GATE, rows_of(lift_gateup)), (DOWN, adapt_hidden))
    h_send = choose((QUERY, rows_of(lift_query)), (OUT, adapt_heads))
    k_send = choose((KEY, rows_of(lift_keyval)))
    d_rows, f_rows, h_rows, k_rows = (item.shape[1] for item in (d_send, f_send, h_send, k_send))
    d_tab, f_tab, h_tab, k_tab = exchange(
        tables_kernel,
        "adapter_tables",
        3,
        (d_send, f_send, h_send, k_send),
        (
            (lay.total, d_rows, LANES),
            (lay.dp, f_rows, LANES),
            (lay.dp, h_rows, LANES),
            (lay.kv_owners, k_rows, LANES),
        ),
        lay.dp,
        lay.total,
        lay.share,
    )
    d_tab = d_tab.reshape(D, LANES)
    f_tab = f_tab.reshape(hidden_here, LANES)
    h_tab = h_tab.reshape(head_width, LANES)
    k_tab = k_tab.reshape(HD, LANES)
    in_qkv, in_gu = d_tab[:, : 3 * RANK], d_tab[:, 3 * RANK : 5 * RANK]
    lift_out, lift_down = d_tab[:, OUT], d_tab[:, DOWN]
    map_hidden, lift_gate, lift_up = f_tab[:, DOWN], f_tab[:, GATE], f_tab[:, UP]
    map_heads, lift_q = h_tab[:, OUT], h_tab[:, QUERY]
    lift_k, lift_v = k_tab[:, KEY], k_tab[:, VALUE]

    row_start = lay.t * rows
    length = lengths[0]
    row_valid = ((row_start + jnp.arange(rows, dtype=jnp.int32)) < length).astype(F32)[:, None]
    place = jnp.arange(LEN, dtype=jnp.int32)
    allowed = (place[:, None] >= place[None, :]) & (place[None, :] < length)

    resid_in = layer_in.astype(F32)
    normed_attn = rms_norm(resid_in, norm_gains[0]).astype(BF16)
    seq_attn = tensor_gather(normed_attn, count)
    low_qkv = nn(seq_attn, in_qkv).astype(BF16)
    low_q, low_k, low_v = (low_qkv[:, i * RANK : (i + 1) * RANK] for i in range(3))
    qkv = nn(seq_attn, attn_w[:, :qkv_width])
    query_pre = (qkv[:, :head_width] + nt(low_q, lift_q)).reshape(LEN, heads_here, HD)
    key_pre = (qkv[:, head_width : head_width + HD] + nt(low_k, lift_k)).reshape(LEN, 1, HD)
    value_pre = qkv[:, head_width + HD :] + nt(low_v, lift_v)
    queries = (rotate(query_pre, cosine, sine) * HD ** (-0.5)).astype(BF16)
    keys = rotate(key_pre, cosine, sine).astype(BF16).reshape(LEN, HD)
    values = value_pre.astype(BF16)

    def scores_of():
        raw = jnp.einsum("qhd,kd->hqk", queries, keys, preferred_element_type=F32)
        squash = jnp.tanh(raw / SOFT_CAP)
        return squash, jnp.where(allowed[None], jnp.exp(SOFT_CAP * squash), 0.0)

    squash, weights = scores_of()
    inverse_total = 1.0 / jnp.sum(weights, axis=-1, keepdims=True)
    attended = jnp.einsum(
        "hqk,kd->qhd", (weights * inverse_total).astype(BF16), values, preferred_element_type=F32
    )
    attended = attended.astype(BF16).reshape(LEN, head_width)
    w_out = attn_w[:, qkv_width:]
    out_part = nt(attended, w_out).astype(BF16)
    low_out_part = pad_lanes(nn(attended, map_heads).astype(BF16))
    attn_main, low_out = tensor_scatter(out_part, low_out_part, count)
    low_out = low_out[:, :RANK].astype(BF16)
    attn_total = attn_main + nt(low_out, lift_out)
    resid_mid = resid_in + rms_norm(attn_total, norm_gains[1])

    normed_mlp = rms_norm(resid_mid, norm_gains[2]).astype(BF16)
    seq_mlp = tensor_gather(normed_mlp, count)
    low_gu = nn(seq_mlp, in_gu).astype(BF16)
    low_g, low_u = low_gu[:, :RANK], low_gu[:, RANK:]
    w_gate, w_up = gate_up_w[:, :hidden_here], gate_up_w[:, hidden_here:]
    gate = nn(seq_mlp, w_gate) + nt(low_g, lift_gate)
    up = nn(seq_mlp, w_up) + nt(low_u, lift_up)
    hidden, slope, gelu = gelu_parts(gate, up)
    down_w = lax.all_gather(down_shard, "dp", axis=0, tiled=True)
    down_part = nt(hidden, down_w).astype(BF16)
    low_down_part = pad_lanes(nn(hidden, map_hidden).astype(BF16))
    mlp_main, low_down = tensor_scatter(down_part, low_down_part, count)
    low_down = low_down[:, :RANK].astype(BF16)
    mlp_total = mlp_main + nt(low_down, lift_down)
    layer_out = (row_valid * (resid_mid + rms_norm(mlp_total, norm_gains[3]))).astype(BF16)

    grad_out = cotangent.astype(F32) * row_valid
    grad_mlp = norm_back(mlp_total, norm_gains[3], grad_out).astype(BF16)
    seq_grad_mlp = tensor_gather(grad_mlp, count)
    grad_low_down = nn(seq_grad_mlp, lift_down).astype(BF16)
    grad_hidden = nn(seq_grad_mlp, down_w) + nt(grad_low_down, map_hidden)
    grad_gate = (grad_hidden * slope.astype(F32)).astype(BF16)
    grad_up = (grad_hidden * gelu.astype(F32)).astype(BF16)
    low_gu_part = pad_lanes(
        jnp.concatenate([nn(grad_gate, lift_gate), nn(grad_up, lift_up)], axis=1).astype(BF16)
    )
    mlp_back_part = (nt(grad_gate, w_gate) + nt(grad_up, w_up)).astype(BF16)
    mlp_back, grad_low_gu = tensor_scatter(mlp_back_part, low_gu_part, count)
    f_parts = [tn(hidden, grad_low_down), tn(grad_gate, low_g), tn(grad_up, low_u)]
    grad_low_gu = grad_low_gu[:, : 2 * RANK].astype(BF16)
    grad_normed_mlp = mlp_back + nt(grad_low_gu, in_gu)
    grad_mid = grad_out + norm_back(resid_mid, norm_gains[2], grad_normed_mlp)

    grad_attn = norm_back(attn_total, norm_gains[1], grad_mid).astype(BF16)
    seq_grad_attn = tensor_gather(grad_attn, count)
    grad_low_out = nn(seq_grad_attn, lift_out).astype(BF16)
    grad_attended = (nn(seq_grad_attn, w_out) + nt(grad_low_out, map_heads)).astype(BF16)
    grad_heads = grad_attended.reshape(LEN, heads_here, HD)
    probs = weights * inverse_total
    probs_low = probs.astype(BF16)
    grad_probs = jnp.einsum("qhd,kd->hqk", grad_heads, values, preferred_element_type=F32)
    grad_value = jnp.einsum("hqk,qhd->kd", probs_low, grad_heads, preferred_element_type=F32)
    grad_capped = probs * (grad_probs - jnp.sum(probs * grad_probs, axis=-1, keepdims=True))
    grad_raw = (grad_capped * (1.0 - squash * squash)).astype(BF16)
    grad_query = jnp.einsum("hqk,kd->qhd", grad_raw, keys, preferred_element_type=F32)
    grad_key = jnp.einsum("hqk,qhd->kd", grad_raw, queries, preferred_element_type=F32)
    grad_q_pre = rotate(grad_query * HD ** (-0.5), cosine, -sine).astype(BF16)
    grad_q_pre = grad_q_pre.reshape(LEN, head_width)
    grad_k_pre = rotate(grad_key.reshape(LEN, 1, HD), cosine, -sine).astype(BF16)
    grad_k_pre = grad_k_pre.reshape(LEN, HD)
    grad_v_pre = grad_value.astype(BF16)
    low_qkv_part = pad_lanes(
        jnp.concatenate(
            [nn(grad_q_pre, lift_q), nn(grad_k_pre, lift_k), nn(grad_v_pre, lift_v)], axis=1
        ).astype(BF16)
    )
    grad_qkv = jnp.concatenate([grad_q_pre, grad_k_pre, grad_v_pre], axis=1)
    attn_back_part = nt(grad_qkv, attn_w[:, :qkv_width]).astype(BF16)
    attn_back, grad_low_qkv = tensor_scatter(attn_back_part, low_qkv_part, count)
    grad_low_qkv = grad_low_qkv[:, : 3 * RANK].astype(BF16)
    grad_normed_attn = attn_back + nt(grad_low_qkv, in_qkv)
    input_grad = (grad_mid + norm_back(resid_in, norm_gains[0], grad_normed_attn)).astype(BF16)

    def packed(parts, blocks):
        return pad_lanes(jnp.concatenate(parts, axis=1).astype(BF16)).reshape(
            blocks, -1, LANES
        )

    d_grad = packed(
        [
            tn(normed_attn, grad_low_qkv),
            tn(normed_mlp, grad_low_gu),
            tn(grad_attn, low_out),
            tn(grad_mlp, low_down),
        ],
        lay.total,
    )
    f_grad = packed(f_parts, lay.dp)
    h_grad = packed([tn(attended, grad_low_out), tn(grad_q_pre, low_q)], lay.dp)
    k_grad = packed([tn(grad_k_pre, low_k), tn(grad_v_pre, low_v)], lay.kv_owners)
    d_all, f_all, h_all, k_all = exchange(
        grads_kernel,
        "adapter_grads",
        4,
        (d_grad, f_grad, h_grad, k_grad),
        (
            (lay.total, d_rows, LANES),
            (lay.dp, f_rows, LANES),
            (lay.dp, h_rows, LANES),
            (lay.dp * lay.share, k_rows, LANES),
        ),
        lay.dp,
        lay.total,
        lay.share,
    )

    def collect(received):
        repeats = received.shape[0] // lay.dp
        hot = jnp.repeat(group_hot, repeats, axis=0)
        return lax.dot_general(
            hot, received, (((0,), (0,)), ((), ())), preferred_element_type=F32
        )

    d_all, f_all, h_all, k_all = (collect(item) for item in (d_all, f_all, h_all, k_all))

    def lift_form(values, shape):
        return jnp.moveaxis(values, 1, 2).reshape(shape)

    return (
        layer_out,
        input_grad,
        d_all[:, :, : 5 * RANK],
        h_all[:, :, :RANK],
        f_all[:, :, :RANK],
        lift_form(h_all[:, :, RANK : 2 * RANK], lift_query.shape),
        lift_form(k_all[:, :, : 2 * RANK], lift_keyval.shape),
        lift_form(f_all[:, :, RANK : 3 * RANK], lift_gateup.shape),
        lift_form(d_all[:, :, 5 * RANK : 7 * RANK], lift_resid.shape),
    )


def solution(mesh):
    return jax.shard_map(
        per_device,
        mesh=mesh,
        in_specs=(
            P(("dp", "tensor"), None),
            P(("dp", "tensor"), None),
            P("dp"),
            P("dp", None),
            P(),
            P("dp", "tensor"),
            P("dp", None),
            P("dp", None),
            P("tensor", "dp"),
            P("dp", "tensor"),
            P("dp", "tensor"),
            P("tensor", "dp"),
            P(None, ("dp", "tensor"), None),
            P(None, ("dp", "tensor"), None),
            P(None, ("dp", "tensor"), None),
            P(None, None, ("dp", "tensor")),
            P(None, None, None, ("dp", "tensor")),
            P(None, None, None, ("dp", "tensor")),
            P(None, None, None, ("dp", "tensor")),
        ),
        out_specs=(
            P(("dp", "tensor"), None),
            P(("dp", "tensor"), None),
            P(None, ("dp", "tensor"), None),
            P(None, ("dp", "tensor"), None),
            P(None, ("dp", "tensor"), None),
            P(None, None, ("dp", "tensor")),
            P(None, None, None, ("dp", "tensor")),
            P(None, None, None, ("dp", "tensor")),
            P(None, None, None, ("dp", "tensor")),
        ),
        check_vma=False,
    )
```

```python
import functools

import jax
import jax.numpy as jnp
from jax import lax
from jax.experimental import pallas as pl
from jax.experimental.pallas import tpu as pltpu
from jax.sharding import PartitionSpec as P

D = 2304
HQ = 8
KV = 4
HD = 256
FF = 9216
NA = 8
RANK = 16
LEN = 1024
LANES = 128

EPSILON = 1e-06
SOFT_CAP = 50.0
MESH = pl.DeviceIdType.MESH
BF16 = jnp.bfloat16
F32 = jnp.float32
VMEM_LIMIT = 48 * 1024 * 1024
BLOCK = 32


def rms_norm(values, gain_row):
    return (
        values * lax.rsqrt(jnp.mean(values * values, axis=-1, keepdims=True) + EPSILON) * gain_row
    )


def norm_back(values, gain_row, gradient):
    inverse = lax.rsqrt(jnp.mean(values * values, axis=-1, keepdims=True) + EPSILON)
    scaled = gradient * gain_row
    normed = values * inverse
    return inverse * (scaled - normed * jnp.mean(scaled * normed, axis=-1, keepdims=True))


def gelu_parts(gate, up):
    scale = (2.0 / jnp.pi) ** 0.5
    square = gate * gate
    bend = jnp.tanh(scale * gate * (1.0 + 0.044715 * square))
    low = 0.5 * (1.0 + bend)
    gelu = gate * low
    slope = low + 0.5 * gate * (1.0 - bend * bend) * (scale * (1.0 + 3.0 * 0.044715 * square))
    return (gelu * up).astype(BF16), (slope * up).astype(BF16), gelu.astype(BF16)


def tables(length, size):
    half_size = size // 2
    frequency = 10000.0 ** (-2.0 * jnp.arange(half_size, dtype=F32) / size)
    angles = jnp.arange(length, dtype=F32)[:, None] * frequency[None, :]
    return (jnp.cos(angles)[:, None, :], jnp.sin(angles)[:, None, :])


def rotate(values, cosine, sine):
    half_size = values.shape[-1] // 2
    first_half = values[..., :half_size]
    second_half = values[..., half_size:]
    return jnp.concatenate(
        [first_half * cosine - second_half * sine, second_half * cosine + first_half * sine],
        axis=-1,
    )


def nn(a, b):
    return lax.dot_general(a, b, (((1,), (0,)), ((), ())), preferred_element_type=F32)


def nt(a, b):
    return lax.dot_general(a, b, (((1,), (1,)), ((), ())), preferred_element_type=F32)


def tn(a, b):
    return lax.dot_general(a, b, (((0,), (0,)), ((), ())), preferred_element_type=F32)


def pad_lanes(values):
    return jnp.pad(values, [(0, 0)] * (values.ndim - 1) + [(0, LANES - values.shape[-1])])


QUERY, KEY, VALUE, GATE, UP, OUT, DOWN = (
    slice(i * RANK, (i + 1) * RANK) for i in range(7)
)


def band(values, first, last=None):
    lane = lax.broadcasted_iota(jnp.int32, values.shape, 1)
    keep = (lane >= first.start) & (lane < (last or first).stop)
    return jnp.where(keep, values, 0.0)


def lanes(*parts):
    pieces, at = [], 0
    for place, values in parts:
        if place.start > at:
            pieces.append(jnp.zeros(values.shape[:-1] + (place.start - at,), values.dtype))
        pieces.append(values)
        at = place.start + values.shape[-1]
    last = parts[-1][1]
    pieces.append(jnp.zeros(last.shape[:-1] + (LANES - at,), last.dtype))
    return jnp.concatenate(pieces, axis=-1)


def call(peers):
    barrier = pltpu.get_barrier_semaphore()
    for peer in peers:
        pl.semaphore_signal(barrier, inc=1, device_id=peer, device_id_type=MESH)


def greet(peers):
    call(peers)
    pl.semaphore_wait(pltpu.get_barrier_semaphore(), len(peers))


def square_peers(index):
    return index + 1 - 2 * lax.rem(index, 2), lax.rem(index + 2, 4), 3 - index


def remote(source, target, send_sem, recv_sem, peer):
    return pltpu.make_async_remote_copy(
        src_ref=source,
        dst_ref=target,
        send_sem=send_sem,
        recv_sem=recv_sem,
        device_id={"tensor": peer},
        device_id_type=MESH,
    )


class PlainGather:
    def __init__(self, me, x_ref, o_ref, local_sem, send_sem, recv_sem):
        rows = x_ref.shape[0]
        half = rows // 2
        links = square_peers(me)[:2]
        self.own = pltpu.make_async_copy(x_ref, o_ref.at[pl.ds(me * rows, rows)], local_sem)
        self.first, self.second, self.onward = [], [], []
        for order, group in enumerate((self.first, self.second)):
            for link in range(2):
                part = link if order == 0 else 1 - link
                group.append(
                    remote(
                        x_ref.at[pl.ds(part * half, half)],
                        o_ref.at[pl.ds(me * rows + part * half, half)],
                        send_sem.at[link, part],
                        recv_sem.at[link, part],
                        links[link],
                    )
                )
        for link in range(2):
            block = o_ref.at[pl.ds(links[link] * rows + link * half, half)]
            self.onward.append(
                remote(block, block, send_sem.at[2, link], recv_sem.at[2, link], links[1 - link])
            )

    def start(self):
        self.own.start()
        for copy in self.first + self.second:
            copy.start()

    def forward(self):
        for copy, onward in zip(self.first, self.onward):
            copy.wait_recv()
            onward.start()

    def finish(self):
        for copy in self.second + self.onward:
            copy.wait_recv()
        self.own.wait()
        for copy in self.first + self.second + self.onward:
            copy.wait_send()


def gather_kernel(count, rows, x_ref, o_ref, local_sem, send_sem, recv_sem):
    me = lax.axis_index("tensor")
    if count == 4:
        across, down, _ = square_peers(me)
        greet([{"tensor": across}, {"tensor": down}])
        gather = PlainGather(me, x_ref, o_ref, local_sem, send_sem, recv_sem)
        gather.start()
        gather.forward()
        gather.finish()
    else:
        peers = [lax.rem(me + step, count) for step in range(1, count)]
        greet([{"tensor": peer} for peer in peers])
        own = pltpu.make_async_copy(x_ref, o_ref.at[pl.ds(me * rows, rows)], local_sem)
        own.start()
        copies = []
        for step, peer in enumerate(peers):
            copy = remote(
                x_ref,
                o_ref.at[pl.ds(me * rows, rows)],
                send_sem.at[0, step],
                recv_sem.at[0, step],
                peer,
            )
            copy.start()
            copies.append(copy)
        own.wait()
        for copy in copies:
            copy.wait()


def tensor_gather(values, count):
    rows, width = values.shape
    slots = max(2, count - 1)
    return pl.pallas_call(
        functools.partial(gather_kernel, count, rows),
        out_shape=jax.ShapeDtypeStruct((count * rows, width), values.dtype),
        in_specs=[pl.BlockSpec(memory_space=pl.ANY)],
        out_specs=pl.BlockSpec(memory_space=pl.ANY),
        scratch_shapes=[
            pltpu.SemaphoreType.DMA,
            pltpu.SemaphoreType.DMA((3, slots)),
            pltpu.SemaphoreType.DMA((3, slots)),
        ],
        compiler_params=pltpu.CompilerParams(
            collective_id=1, has_side_effects=True, vmem_limit_bytes=VMEM_LIMIT
        ),
        name="tensor_gather",
    )(values)


def scatter_kernel(count, rows, p_ref, q_ref, o_ref, l_ref, *scratch):
    me = lax.axis_index("tensor")
    payload = ((p_ref, o_ref), (q_ref, l_ref))
    if count == 4:
        across, down, far = square_peers(me)
        greet([{"tensor": across}, {"tensor": down}])
        half = rows // 2
        first = scratch[0:2]
        sums = scratch[2:4]
        second = scratch[4:6]
        send_sem, recv_sem = scratch[6], scratch[7]
        links = (across, down)
        copies = {}
        for which in (1, 0):
            for link in range(2):
                block = far if which == 1 else links[link]
                for item in range(2):
                    copy = remote(
                        payload[item][0].at[pl.ds(block * rows + link * half, half)],
                        first[item].at[link, which],
                        send_sem.at[item, link, which],
                        recv_sem.at[item, link, which],
                        links[link],
                    )
                    copy.start()
                    copies[item, link, which] = copy
        for link in range(2):
            block = links[1 - link]
            for item in range(2):
                copies[item, link, 1].wait_recv()
                mine = payload[item][0][pl.ds(block * rows + link * half, half), :]
                sums[item][link] = (
                    mine.astype(F32) + first[item][link, 1].astype(F32)
                ).astype(BF16)
                copy = remote(
                    sums[item].at[link],
                    second[item].at[link],
                    send_sem.at[item, link, 2],
                    recv_sem.at[item, link, 2],
                    links[1 - link],
                )
                copy.start()
                copies[item, link, 2] = copy
        for link in range(2):
            for item in range(2):
                copies[item, link, 0].wait_recv()
                mine = payload[item][0][pl.ds(me * rows + link * half, half), :]
                payload[item][1][pl.ds(link * half, half), :] = mine.astype(F32) + first[item][
                    link, 0
                ].astype(F32)
        for link in range(2):
            for item in range(2):
                copies[item, link, 2].wait_recv()
                payload[item][1][pl.ds(link * half, half), :] += second[item][link].astype(F32)
        for copy in copies.values():
            copy.wait_send()
    else:
        peers = [lax.rem(me + step, count) for step in range(1, count)]
        greet([{"tensor": peer} for peer in peers])
        first = scratch[0:2]
        send_sem, recv_sem = scratch[2], scratch[3]
        copies = []
        for step, peer in enumerate(peers):
            for item in range(2):
                copy = remote(
                    payload[item][0].at[pl.ds(peer * rows, rows)],
                    first[item].at[step],
                    send_sem.at[item, step],
                    recv_sem.at[item, step],
                    peer,
                )
                copy.start()
                copies.append((item, step, copy))
        for item in range(2):
            payload[item][1][...] = payload[item][0][pl.ds(me * rows, rows), :].astype(F32)
        for item, step, copy in copies:
            copy.wait()
            payload[item][1][...] += first[item][step].astype(F32)


def tensor_scatter(values, narrow, count):
    rows = values.shape[0] // count
    widths = (values.shape[1], narrow.shape[1])
    if count == 4:
        half = rows // 2
        scratch = [pltpu.VMEM((2, 2, half, width), BF16) for width in widths]
        scratch += [pltpu.VMEM((2, half, width), BF16) for width in widths]
        scratch += [pltpu.VMEM((2, half, width), BF16) for width in widths]
        scratch += [pltpu.SemaphoreType.DMA((2, 2, 3)), pltpu.SemaphoreType.DMA((2, 2, 3))]
    else:
        scratch = [pltpu.VMEM((count - 1, rows, width), BF16) for width in widths]
        scratch += [pltpu.SemaphoreType.DMA((2, count - 1))] * 2
    vmem = pl.BlockSpec(memory_space=pltpu.VMEM)
    return pl.pallas_call(
        functools.partial(scatter_kernel, count, rows),
        out_shape=tuple(jax.ShapeDtypeStruct((rows, width), F32) for width in widths),
        in_specs=[vmem, vmem],
        out_specs=(vmem, vmem),
        scratch_shapes=scratch,
        compiler_params=pltpu.CompilerParams(
            collective_id=2, has_side_effects=True, vmem_limit_bytes=VMEM_LIMIT
        ),
        name="tensor_scatter",
    )(values, narrow)


class Square:
    def __init__(self, rows):
        self.rows = rows
        self.half = rows // 2
        self.me = lax.axis_index("tensor")
        self.across, self.down, self.far = square_peers(self.me)
        self.links = (self.across, self.down)

    def greet(self, far=False):
        greet([{"tensor": peer} for peer in (self.across, self.down) + ((self.far,) if far else ())])

    def spread(self, source_at, target, send_sem, recv_sem):
        copies = [pltpu.make_async_copy(source_at(self.me), target.at[self.me], recv_sem.at[0])]
        for which, peer in enumerate((self.across, self.down, self.far)):
            copies.append(
                remote(
                    source_at(peer),
                    target.at[self.me],
                    send_sem.at[which],
                    recv_sem.at[1 + which],
                    peer,
                )
            )
        return copies


def along(source_at, target, send_sem, recv_sem):
    dp = lax.axis_size("dp")
    d = lax.axis_index("dp")
    pltpu.make_async_copy(source_at(d), target.at[d], recv_sem).start()
    copies = []
    for step in range(1, dp):
        peer = lax.rem(d + step, dp)
        copy = pltpu.make_async_remote_copy(
            src_ref=source_at(peer),
            dst_ref=target.at[d],
            send_sem=send_sem.at[step],
            recv_sem=recv_sem,
            device_id={"dp": peer},
            device_id_type=MESH,
        )
        copy.start()
        copies.append(copy)
    return copies


class ChunkGather:
    def __init__(self, sq, source, buf, send_sem, recv_sem):
        half = sq.half
        self.first, self.second, self.onward = [], [], []
        for link in range(2):
            for order in range(2):
                part = link if order == 0 else 1 - link
                copy = remote(
                    source.at[pl.ds(part * half, half)],
                    buf.at[1 + order, pl.ds(link * half, half)],
                    send_sem.at[2 * order + link],
                    recv_sem.at[2 * order + link],
                    sq.links[link],
                )
                (self.first if order == 0 else self.second).append(copy)
            self.onward.append(
                remote(
                    buf.at[1, pl.ds(link * half, half)],
                    buf.at[3, pl.ds(link * half, half)],
                    send_sem.at[4 + link],
                    recv_sem.at[4 + link],
                    sq.links[1 - link],
                )
            )

    def start(self):
        for copy in self.first + self.second:
            copy.start()

    def wait_chunk(self, chunk):
        if chunk == 1:
            for copy in self.first:
                copy.wait_recv()
            for copy in self.onward:
                copy.start()
        if chunk == 2:
            for copy in self.second:
                copy.wait_recv()
        if chunk == 3:
            for copy in self.onward:
                copy.wait_recv()

    def finish(self):
        for copy in self.first + self.second + self.onward:
            copy.wait_send()


class ChunkScatter:
    def __init__(self, sq, part, landing, passed, send_sem, recv_sem):
        self.sq, self.half = sq, sq.half
        self.part, self.landing, self.passed = part, landing, passed
        self.send_sem, self.recv_sem = send_sem, recv_sem
        self.tiles = send_sem.shape[-1]
        self.width = part.shape[-1] // self.tiles

    def columns(self, tile):
        if self.tiles == 1:
            return pl.ds(0, self.width)
        return columns(tile, self.width)

    def copy(self, kind, link, tile):
        rows = pl.ds(link * self.half, self.half)
        cols = self.columns(tile)
        source = (
            self.passed.at[link, :, cols]
            if kind == 2
            else self.part.at[1 + 2 * kind, rows, cols]
        )
        slot = 2 * kind + link
        return remote(
            source,
            self.landing.at[slot, :, cols],
            self.send_sem.at[slot, tile],
            self.recv_sem.at[slot, tile],
            self.sq.links[1 - link if kind == 2 else link],
        )

    def send(self, kind, tile):
        for link in range(2):
            self.copy(kind, link, tile).start()

    def send_own(self):
        for tile in range(self.tiles):
            self.send(0, tile)

    def send_far(self):
        for tile in range(self.tiles):
            self.send(1, tile)

    def pass_on(self):
        for tile in range(self.tiles):
            cols = self.columns(tile)
            for link in range(2):
                self.copy(1, link, tile).wait_recv()
                rows = pl.ds((1 - link) * self.half, self.half)
                mine = self.part[2, rows, cols].astype(F32)
                self.passed[link, :, cols] = (
                    mine + self.landing[2 + link, :, cols].astype(F32)
                ).astype(BF16)
                self.copy(2, link, tile).start()

    def arrived(self):
        for kind in (0, 2):
            for tile in range(self.tiles):
                for link in range(2):
                    self.copy(kind, link, tile).wait_recv()

    def collect(self, out_ref, places=((0, 0),)):
        self.arrived()
        for link in range(2):
            rows = pl.ds(link * self.half, self.half)
            total = (
                self.part[0, rows, :].astype(F32)
                + self.landing[link].astype(F32)
                + self.landing[4 + link].astype(F32)
            )
            size = self.part.shape[-1] // len(places)
            for source, target in places:
                out_ref[rows, target : target + size] = total[:, source : source + size]

    def finish(self):
        for kind in range(3):
            for tile in range(self.tiles):
                for link in range(2):
                    self.copy(kind, link, tile).wait_send()


def scatter_scratch(rows, width, tiles=1):
    half = rows // 2
    return [
        pltpu.VMEM((4, rows, width), BF16),
        pltpu.VMEM((6, half, width), BF16),
        pltpu.VMEM((2, half, width), BF16),
        pltpu.SemaphoreType.DMA((6, tiles)),
        pltpu.SemaphoreType.DMA((6, tiles)),
    ]


def tile_of(width):
    return 768 if width % 768 == 0 else 384


def columns(step, tile, base=0):
    return pl.ds(pl.multiple_of(base + step * tile, LANES), tile)


def mlp_back_kernel(
    rows,
    g_ref,
    down_hbm,
    gu_hbm,
    slope_hbm,
    gelu_hbm,
    hidden_hbm,
    low_hbm,
    d_ref,
    f_table,
    o_ref,
    l_ref,
    f_out,
    f_ref,
    f_send,
    down_w,
    gu_w,
    buf,
    slope,
    gelu,
    hidden,
    low,
    grads,
    weight_sem,
    load_sem,
    own_sem,
    gather_send,
    gather_recv,
    spread_send,
    spread_recv,
    *scratch,
):
    sq = Square(rows)
    width = hidden.shape[-1]
    model = o_ref.shape[-1]
    down_load = pltpu.make_async_copy(down_hbm, down_w, weight_sem.at[0])
    gu_load = pltpu.make_async_copy(gu_hbm, gu_w, weight_sem.at[1])
    own_load = pltpu.make_async_copy(g_ref, buf.at[0], own_sem)

    def loads(chunk):
        slot = chunk % 2
        return [
            pltpu.make_async_copy(source.at[chunk], target.at[slot], load_sem.at[slot, item])
            for item, (source, target) in enumerate(
                ((slope_hbm, slope), (gelu_hbm, gelu), (hidden_hbm, hidden), (low_hbm, low))
            )
        ]

    down_load.start()
    own_load.start()
    for copy in loads(0):
        copy.start()
    sq.greet(far=True)
    gather = ChunkGather(sq, g_ref, buf, gather_send, gather_recv)
    gather.start()
    gu_load.start()
    part, part_low = scratch[0], scratch[5]
    scatters = (ChunkScatter(sq, *scratch[:5]), ChunkScatter(sq, *scratch[5:10]))
    f_ref[...] = jnp.zeros_like(f_ref)
    own_load.wait()
    down_load.wait()

    @pl.loop(0, 4)
    def _(chunk):
        slot = lax.rem(chunk, 2)
        for step in range(4):

            @pl.when(chunk == step)
            def _(step=step):
                gather.wait_chunk(step)
                for copy in loads(step):
                    copy.wait()
                if step < 3:
                    for copy in loads(step + 1):
                        copy.start()

        incoming = buf.at[chunk]
        low_down = band(nn(incoming[...], d_ref[...]), DOWN).astype(BF16)
        tile = tile_of(width)

        @pl.loop(0, width // tile)
        def _(step):
            here = columns(step, tile)
            grad = nn(incoming[...], down_w[:, here]) + nt(low_down, f_table[here, :])
            grads[:, here] = (grad * slope[slot, :, here].astype(F32)).astype(BF16)
            grads[:, columns(step, tile, width)] = (
                grad * gelu[slot, :, here].astype(F32)
            ).astype(BF16)

        @pl.when(chunk == 0)
        def _():
            gu_load.wait()

        part_low[chunk] = (
            band(nn(grads[:, :width], f_table[...]), GATE)
            + band(nn(grads[:, width:], f_table[...]), UP)
        ).astype(BF16)
        wide = tile_of(model)

        @pl.loop(0, model // wide)
        def _(step):
            here = columns(step, wide)
            part[chunk, :, here] = nt(grads[...], gu_w[here, :]).astype(BF16)

            @pl.when(chunk == 1)
            def _():
                scatters[0].send(0, step)

            @pl.when(chunk == 3)
            def _():
                scatters[0].send(1, step)

        @pl.when(chunk == 1)
        def _():
            scatters[1].send_own()

        @pl.when(chunk == 3)
        def _():
            scatters[1].send_far()

        low_turned = low_down.astype(F32).T.astype(BF16)
        gu_turned = low[slot].astype(F32).T.astype(BF16)
        f_ref[:RANK, :] += nn(low_turned[DOWN], hidden[slot])
        f_ref[RANK : 2 * RANK, :] += nn(gu_turned[GATE], grads[:, :width])
        f_ref[2 * RANK : 3 * RANK, :] += nn(gu_turned[UP], grads[:, width:])

    cores, slices = f_send.shape[:2]
    size = width // (cores * slices)
    for core in range(cores):
        for peer in range(slices):
            first = (core * slices + peer) * size
            f_send[core, peer] = f_ref[: 3 * RANK, first : first + size].astype(BF16)
    spread = sq.spread(lambda peer: f_send.at[:, peer], f_out, spread_send, spread_recv)
    for copy in spread:
        copy.start()
    for scatter in scatters:
        scatter.pass_on()
    gather.finish()
    scatters[0].collect(o_ref)
    scatters[1].collect(l_ref)
    for scatter in scatters:
        scatter.finish()
    for copy in spread:
        copy.wait()


def mlp_back_fused(grad, down_w, gu_w, slope, gelu, hidden, low, d_tab, f_tab, dp):
    rows, model = grad.shape
    width = hidden.shape[2]
    messages = (dp // 4, 4, 3 * RANK, width // dp)
    anywhere = pl.BlockSpec(memory_space=pl.ANY)
    vmem = pl.BlockSpec(memory_space=pltpu.VMEM)
    return pl.pallas_call(
        functools.partial(mlp_back_kernel, rows),
        out_shape=(
            jax.ShapeDtypeStruct((rows, model), F32),
            jax.ShapeDtypeStruct((rows, LANES), F32),
            jax.ShapeDtypeStruct((4, dp // 4, 3 * RANK, width // dp), BF16),
        ),
        in_specs=[vmem] + [anywhere] * 6 + [vmem] * 2,
        out_specs=(vmem,) * 3,
        scratch_shapes=[
            pltpu.VMEM((3 * RANK, width), F32),
            pltpu.VMEM(messages, BF16),
            pltpu.VMEM((model, width), BF16),
            pltpu.VMEM((model, 2 * width), BF16),
            pltpu.VMEM((4, rows, model), BF16),
            pltpu.VMEM((2, rows, width), BF16),
            pltpu.VMEM((2, rows, width), BF16),
            pltpu.VMEM((2, rows, width), BF16),
            pltpu.VMEM((2, rows, LANES), BF16),
            pltpu.VMEM((rows, 2 * width), BF16),
            pltpu.SemaphoreType.DMA((2,)),
            pltpu.SemaphoreType.DMA((2, 4)),
            pltpu.SemaphoreType.DMA,
            pltpu.SemaphoreType.DMA((6,)),
            pltpu.SemaphoreType.DMA((6,)),
            pltpu.SemaphoreType.DMA((3,)),
            pltpu.SemaphoreType.DMA((4,)),
        ]
        + scatter_scratch(rows, model, model // tile_of(model))
        + scatter_scratch(rows, LANES),
        compiler_params=pltpu.CompilerParams(
            collective_id=5, has_side_effects=True, vmem_limit_bytes=62 * 1024 * 1024
        ),
        name="mlp_back",
    )(grad, down_w, gu_w, slope, gelu, hidden, low, d_tab, f_tab)


def front_kernel(
    ids_ref,
    layer_ref,
    gains_ref,
    f_all,
    d_all,
    hk_all,
    shard_hbm,
    seq_out,
    ids_out,
    d_out,
    f_out,
    h_out,
    k_out,
    weight_out,
    normed,
    ids_land,
    f_pick,
    d_pick,
    hk_pick,
    f_mid,
    d_mid,
    hk_mid,
    d_join,
    f_land,
    d_land,
    hk_land,
    d_flip,
    f_flip,
    h_flip,
    k_flip,
    local_sem,
    gather_send,
    gather_recv,
    line_send,
    line_recv,
    group_send,
    group_recv,
    shard_sem,
    shard_send,
    shard_recv,
):
    rows = layer_ref.shape[0]
    sq = Square(rows)
    dp = lax.axis_size("dp")
    d = lax.axis_index("dp")
    peers = [{"tensor": peer} for peer in (sq.across, sq.down, sq.far)]
    peers += [{"dp": lax.rem(d + step, dp)} for step in range(1, dp)]
    call(peers)
    shards = Line(weight_out, shard_send, shard_recv)
    own_shard = pltpu.make_async_copy(shard_hbm, weight_out.at[d], shard_sem)
    own_shard.start()

    @pl.loop(0, rows // BLOCK)
    def _(step):
        here = pl.ds(pl.multiple_of(step * BLOCK, BLOCK), BLOCK)
        normed[here, :] = rms_norm(layer_ref[here, :].astype(F32), gains_ref[0:1, :]).astype(BF16)

    pl.semaphore_wait(pltpu.get_barrier_semaphore(), len(peers))
    line = along(lambda k: ids_ref, ids_land, line_send.at[0], line_recv.at[0])
    own_shard.wait()
    shards.start()
    gather = PlainGather(sq.me, normed, seq_out, local_sem, gather_send, gather_recv)
    gather.start()
    pltpu.make_async_copy(ids_land, ids_land, line_recv.at[0]).wait()
    ids_out[...] = ids_land[...]

    @pl.loop(0, dp)
    def _(k):
        for source, target in ((f_all, f_pick), (d_all, d_pick), (hk_all, hk_pick)):
            total = None
            for adapter in range(NA):
                hit = jnp.broadcast_to(ids_land[k, 0:1, 0:1], source.shape[1:]) == adapter
                mine = jnp.where(hit, source[adapter].astype(F32), 0.0)
                total = mine if total is None else total + mine
            target[k] = total.astype(BF16)

    lands = (f_mid, d_mid, hk_mid)
    for item, (source, target) in enumerate(zip((f_pick, d_pick, hk_pick), lands)):
        line += along(
            lambda k, source=source: source.at[k],
            target,
            line_send.at[1 + item],
            line_recv.at[1 + item],
        )
    shards.arrive(1, 0)
    gather.forward()
    for flip in (d_flip, f_flip, h_flip, k_flip):
        flip[...] = jnp.zeros_like(flip)
    for item, target in enumerate(lands):
        pltpu.make_async_copy(target, target, line_recv.at[1 + item]).wait()
    shards.arrive(1, 1)
    size = d_mid.shape[2]
    for k in range(dp):
        d_join[:, k * size : (k + 1) * size] = d_mid[k]
    per_user = dp // 4
    spread = [
        sq.spread(lambda peer: d_join, d_land, group_send.at[0], group_recv.at[0]),
        sq.spread(
            lambda peer: f_mid.at[pl.ds(peer * per_user, per_user)],
            f_land,
            group_send.at[1],
            group_recv.at[1],
        ),
        sq.spread(
            lambda peer: hk_mid.at[pl.ds(peer * per_user, per_user)],
            hk_land,
            group_send.at[2],
            group_recv.at[2],
        ),
    ]
    for copies in spread:
        for copy in copies:
            copy.start()
    shards.arrive(2, 0)
    for copies in spread:
        copies[0].wait()
        for copy in copies[1:]:
            copy.wait_recv()
    shards.arrive(2, 1)
    f_size, h_size, k_size = f_mid.shape[2], h_out.shape[0] // dp, k_out.shape[0] // dp
    for t in range(4):
        for k in range(dp):
            at = (k * 4 + t) * size
            d_flip[: DOWN.stop, at : at + size] = d_land[
                t, :, k * size : (k + 1) * size
            ].astype(F32)
        for core in range(per_user):
            at = (core * 4 + t) * f_size
            piece = f_land[t, core].astype(F32)
            f_flip[GATE.start : UP.stop, at : at + f_size] = piece[: 2 * RANK]
            f_flip[DOWN, at : at + f_size] = piece[2 * RANK :]
            piece = hk_land[t, core].astype(F32)
            at = (core * 4 + t) * h_size
            h_flip[OUT, at : at + h_size] = piece[:RANK, :h_size]
            h_flip[QUERY, at : at + h_size] = piece[RANK : 2 * RANK, :h_size]
            at = (core * 4 + t) * k_size
            k_flip[KEY.start : VALUE.stop, at : at + k_size] = piece[2 * RANK :, :k_size]
    for flip, out in ((d_flip, d_out), (f_flip, f_out), (h_flip, h_out), (k_flip, k_out)):

        @pl.loop(0, out.shape[0] // LANES)
        def _(step, flip=flip, out=out):
            here = columns(step, LANES)
            out[here, :] = flip[:, here].T.astype(BF16)

    shards.arrive(3, 0)
    gather.finish()
    shards.arrive(3, 1)
    for place in range(dp // 2):
        for part in range(2):
            shards.wait_sibling(place, part)
    shards.finish()
    for copies in spread:
        for copy in copies[1:]:
            copy.wait_send()
    for copy in line:
        copy.wait_send()


def front(ids, layer_in, gains, f_all, d_all, hk_all, shard, dp, widths):
    rows, model = layer_in.shape
    anywhere = pl.BlockSpec(memory_space=pl.ANY)
    vmem = pl.BlockSpec(memory_space=pltpu.VMEM)
    tables_in = (f_all, d_all, hk_all)
    shapes = [(dp,) + table.shape[1:] for table in tables_in]
    joined = (shapes[1][1], dp * shapes[1][2])
    return pl.pallas_call(
        front_kernel,
        out_shape=(
            jax.ShapeDtypeStruct((4 * rows, model), BF16),
            jax.ShapeDtypeStruct((dp,) + ids.shape, jnp.int32),
        )
        + tuple(jax.ShapeDtypeStruct((width, LANES), BF16) for width in widths)
        + (jax.ShapeDtypeStruct((dp,) + shard.shape, BF16),),
        in_specs=[vmem] * 6 + [anywhere],
        out_specs=(anywhere,) + (vmem,) * 5 + (anywhere,),
        scratch_shapes=[
            pltpu.VMEM((rows, model), BF16),
            pltpu.VMEM((dp,) + ids.shape, jnp.int32),
        ]
        + [pltpu.VMEM(shape, BF16) for shape in shapes] * 2
        + [
            pltpu.VMEM(joined, BF16),
            pltpu.VMEM((4, dp // 4) + shapes[0][1:], BF16),
            pltpu.VMEM((4,) + joined, BF16),
            pltpu.VMEM((4, dp // 4) + shapes[2][1:], BF16),
        ]
        + [pltpu.VMEM((LANES, width), F32) for width in widths]
        + [
            pltpu.SemaphoreType.DMA,
            pltpu.SemaphoreType.DMA((3, 2)),
            pltpu.SemaphoreType.DMA((3, 2)),
            pltpu.SemaphoreType.DMA((4, dp)),
            pltpu.SemaphoreType.DMA((4,)),
            pltpu.SemaphoreType.DMA((3, 3)),
            pltpu.SemaphoreType.DMA((3, 4)),
            pltpu.SemaphoreType.DMA,
            pltpu.SemaphoreType.DMA((3, dp // 2, 2)),
            pltpu.SemaphoreType.DMA((dp, 2)),
        ],
        compiler_params=pltpu.CompilerParams(
            collective_id=9, has_side_effects=True, vmem_limit_bytes=VMEM_LIMIT
        ),
        name="front",
    )(ids, layer_in, gains, *tables_in, shard)


class Line:
    def __init__(self, slots, send_sem, recv_sem):
        self.d = lax.axis_index("dp")
        self.places = lax.axis_size("dp") // 2
        self.core = lax.rem(self.d, 2)
        self.z = self.d // 2
        self.sibling = self.d + 1 - 2 * self.core
        self.slots, self.send_sem, self.recv_sem = slots, send_sem, recv_sem

    def greet(self, others):
        barrier = pltpu.get_barrier_semaphore()
        for peer in others + [{"dp": self.sibling}]:
            pl.semaphore_signal(barrier, inc=1, device_id=peer, device_id_type=MESH)

        @pl.when(self.z > 0)
        def _():
            pl.semaphore_signal(
                barrier, inc=1, device_id={"dp": self.d - 2}, device_id_type=MESH
            )

        @pl.when(self.z < self.places - 1)
        def _():
            pl.semaphore_signal(
                barrier, inc=1, device_id={"dp": self.d + 2}, device_id_type=MESH
            )

        last = self.places - 1
        ends = (last - self.z) // last + self.z // last
        pl.semaphore_wait(barrier, len(others) + 3 - ends)

    def copy(self, place, kind, part):
        target = (self.d + 2, self.d - 2, self.sibling)[kind]
        slot = 2 * place + self.core
        half = self.slots.shape[1] // 2
        block = self.slots.at[slot, pl.ds(part * half, half)]
        return pltpu.make_async_remote_copy(
            src_ref=block,
            dst_ref=block,
            send_sem=self.send_sem.at[kind, place, part],
            recv_sem=self.recv_sem.at[slot, part],
            device_id={"dp": target},
            device_id_type=MESH,
        )

    def send_up(self, place, part):
        @pl.when(self.z < self.places - 1)
        def _():
            self.copy(place, 0, part).start()

    def send_down(self, place, part):
        @pl.when(self.z > 0)
        def _():
            self.copy(place, 1, part).start()

    def start(self):
        for part in range(2):
            self.send_up(self.z, part)
            self.send_down(self.z, part)
            self.copy(self.z, 2, part).start()

    def arrive(self, distance, part):
        @pl.when(self.z >= distance)
        def _():
            place = self.z - distance
            self.copy(place, 2, part).wait_recv()
            self.send_up(place, part)
            self.copy(place, 2, part).start()

        @pl.when(self.z + distance < self.places)
        def _():
            place = self.z + distance
            self.copy(place, 2, part).wait_recv()
            self.send_down(place, part)
            self.copy(place, 2, part).start()

    def wait_sibling(self, place, part):
        half = self.slots.shape[1] // 2
        other = 2 * place + 1 - self.core
        block = self.slots.at[other, pl.ds(part * half, half)]
        pltpu.make_async_copy(block, block, self.recv_sem.at[other, part]).wait()

    def finish(self):
        for place in range(self.places):
            for part in range(2):

                @pl.when((self.z >= place) & (self.z < self.places - 1))
                def _(place=place, part=part):
                    self.copy(place, 0, part).wait_send()

                @pl.when((self.z <= place) & (self.z > 0))
                def _(place=place, part=part):
                    self.copy(place, 1, part).wait_send()

                self.copy(place, 2, part).wait_send()


class HalfSpread:
    def __init__(self, sq, line, weight, columns_from, target, send_sem, recv_sem):
        model, width = target.shape[1:]
        share, part_rows = model // 2, model // 4
        cols = pl.ds(columns_from, width)

        def rows(part):
            return pl.ds(pl.multiple_of(line.core * share + part * part_rows, 8), part_rows)

        self.first, self.second, self.onward, self.sibling = [], [], [], []
        for order, group in enumerate((self.first, self.second)):
            for link in range(2):
                part = link if order == 0 else 1 - link
                sem = 2 * order + link
                group.append(
                    remote(
                        weight.at[rows(part), cols],
                        target.at[sq.me, rows(part)],
                        send_sem.at[sem],
                        recv_sem.at[sem],
                        sq.links[link],
                    )
                )
        for link in range(2):
            block = target.at[sq.links[link], rows(link)]
            self.onward.append(
                remote(
                    block, block, send_sem.at[4 + link], recv_sem.at[4 + link], sq.links[1 - link]
                )
            )
        mine = pl.ds(pl.multiple_of(line.core * share, 8), share)
        for which, peer in enumerate((sq.across, sq.down, sq.far)):
            block = target.at[peer, mine]
            self.sibling.append(
                pltpu.make_async_remote_copy(
                    src_ref=block,
                    dst_ref=block,
                    send_sem=send_sem.at[6 + which],
                    recv_sem=recv_sem.at[6 + which],
                    device_id={"dp": line.sibling},
                    device_id_type=MESH,
                )
            )

    def start(self):
        for copy in self.first + self.second:
            copy.start()

    def forward(self):
        for copy, onward in zip(self.first, self.onward):
            copy.wait_recv()
            onward.start()

    def share(self):
        for copy in self.second + self.onward:
            copy.wait_recv()
        for copy in self.sibling:
            copy.start()

    def finish(self):
        for copy in self.first + self.second + self.onward:
            copy.wait_send()
        for copy in self.sibling:
            copy.wait()


ARRIVALS = ((0, 1, 2, 3), (1, 0, 2, 3), (2, 1, 3, 0), (3, 2, 1, 0))


def mlp_kernel(
    rows,
    length_ref,
    x_hbm,
    gu_hbm,
    shard_hbm,
    weight_hbm,
    d_ref,
    f_table,
    resid_ref,
    cot_ref,
    gains_ref,
    layer_ref,
    grad_ref,
    low_ref,
    low_down_ref,
    hidden_out,
    slope_out,
    gelu_out,
    down_out,
    w_kv_all,
    work,
    low_sum,
    lows,
    seq,
    tiles,
    hidden,
    slope,
    gelu,
    down,
    load_sem,
    tile_sem,
    store_sem,
    keep_sem,
    line_send,
    line_recv,
    part,
    landing,
    passed,
    part_send,
    part_recv,
    w_send,
    w_recv,
    *low_scratch,
):
    sq = Square(rows)
    line = Line(down, line_send, line_recv)
    width = hidden.shape[-1]
    tile = tiles.shape[-1] // 2
    steps = width // tile
    own_shard = pltpu.make_async_copy(shard_hbm, down.at[line.d], load_sem.at[0])
    seq_load = pltpu.make_async_copy(x_hbm, seq, load_sem.at[1])

    def tile_loads(step, slot):
        return [
            pltpu.make_async_copy(
                gu_hbm.at[:, columns(step, tile, which * width)],
                tiles.at[slot, :, pl.ds(which * tile, tile)],
                tile_sem.at[slot, which],
            )
            for which in range(2)
        ]

    def stores(step, slot):
        here = columns(step, tile)
        return [
            pltpu.make_async_copy(
                source.at[slot], target.at[:, :, here], store_sem.at[slot, which]
            )
            for which, (source, target) in enumerate(((slope, slope_out), (gelu, gelu_out)))
        ]

    own_shard.start()
    seq_load.start()
    for copy in tile_loads(0, 0):
        copy.start()
    line.greet([{"tensor": sq.across}, {"tensor": sq.down}])
    own_shard.wait()
    line.start()
    keys_from = (weight_hbm.shape[1] - w_kv_all.shape[2]) // 2
    spread = HalfSpread(sq, line, weight_hbm, keys_from, w_kv_all, w_send, w_recv)
    spread.start()
    seq_load.wait()

    @pl.loop(0, 4)
    def _(chunk):
        low = nn(seq[chunk], d_ref[...])
        lows[0, chunk] = band(low, GATE).astype(BF16)
        lows[1, chunk] = band(low, UP).astype(BF16)
        low_ref[chunk] = band(low, GATE, UP).astype(BF16)

    @pl.loop(0, steps)
    def _(step):
        slot = lax.rem(step, 2)
        for copy in tile_loads(step, slot):
            copy.wait()

        @pl.when(step + 1 < steps)
        def _():
            for copy in tile_loads(step + 1, 1 - slot):
                copy.start()

        @pl.when(step >= 2)
        def _():
            for copy in stores(step - 2, slot):
                copy.wait()

        here = columns(step, tile)

        @pl.loop(0, 4)
        def _(chunk):
            both = nn(seq[chunk], tiles[slot])
            gate = both[:, :tile] + nt(lows[0, chunk], f_table[here, :])
            up = both[:, tile:] + nt(lows[1, chunk], f_table[here, :])
            hidden[chunk, :, here], slope[slot, chunk], gelu[slot, chunk] = gelu_parts(gate, up)

        for copy in stores(step, slot):
            copy.start()

        for part_at, part_of in ((steps // 2 - 1, 0), (steps - 2, 1)):

            @pl.when(step == part_at)
            def _(part_of=part_of):
                line.arrive(1, part_of)
                if part_of == 0:
                    spread.forward()

    keep_hidden = pltpu.make_async_copy(hidden, hidden_out, keep_sem.at[0])
    keep_hidden.start()
    last = line.places - 1
    is_first, is_last = (last - line.z) // last, line.z // last
    is_third = line.z // 2 - is_last
    is_here = (is_first, 1 - is_first - is_third - is_last, is_third, is_last)
    order = [sum(flag * ARRIVALS[z][i] for z, flag in enumerate(is_here)) for i in range(4)]

    def scatter_at(place, half):
        at = 2 * place + half
        return ChunkScatter(
            sq, part.at[at], landing.at[at], passed.at[at], part_send.at[at], part_recv.at[at]
        )

    low_scatter = ChunkScatter(sq, *low_scratch)

    @pl.loop(0, 4)
    def _(chunk):
        low_scratch[0][chunk] = band(nn(hidden[chunk], f_table[...]), DOWN).astype(BF16)

    low_scatter.send_far()
    low_scatter.send_own()
    keeps = []
    earlier = low_scatter
    half_rows = down.shape[1] // 2
    arrivals = {(1, 0): ((2, 0),), (2, 0): ((2, 1),), (3, 0): ((3, 0),), (3, 1): ((3, 1),)}
    for turn in range(4):
        place = order[turn]
        for half in range(2):
            for distance, piece in arrivals.get((turn, half), ()):
                line.arrive(distance, piece)
            if (turn, half) == (1, 0):
                spread.share()
            line.wait_sibling(place, half)
            scatter = scatter_at(place, half)

            @pl.loop(0, 4)
            def _(step, place=place, half=half, scatter=scatter):
                chunk = far_first(step)
                for core in range(2):
                    part[
                        2 * place + half, chunk, :, core * half_rows : (core + 1) * half_rows
                    ] = nt(
                        hidden[chunk],
                        down[2 * place + core, half * half_rows : (half + 1) * half_rows],
                    ).astype(BF16)

                @pl.when(step == 0)
                def _():
                    scatter.send_far()

                @pl.when(step == 1)
                def _():
                    scatter.send_own()

            earlier.pass_on()
            earlier = scatter
        pair = pl.ds(2 * place, 2)
        keep = pltpu.make_async_copy(down.at[pair], down_out.at[pair], keep_sem.at[1 + turn])
        keep.start()
        keeps.append(keep)
    low_scatter.collect(low_sum)
    low_down_ref[...] = low_sum[...].astype(BF16)
    earlier.pass_on()
    everything = [(place, half) for place in range(4) for half in range(2)]
    for place, half in everything:
        first = 2 * place * down.shape[1] + half * half_rows
        scatter_at(place, half).collect(
            work, ((0, first), (half_rows, first + down.shape[1]))
        )
    add_lifted(work, low_down_ref, d_ref)

    @pl.loop(0, rows // BLOCK)
    def _(step):
        here = pl.ds(pl.multiple_of(step * BLOCK, BLOCK), BLOCK)
        at = sq.me * rows + step * BLOCK + lax.broadcasted_iota(jnp.int32, (BLOCK, 1), 0)
        valid = (at < length_ref[0]).astype(F32)
        total = work[here, :]
        gain = gains_ref[3:4, :]
        layer_ref[here, :] = (valid * (resid_ref[here, :] + rms_norm(total, gain))).astype(BF16)
        grad_ref[here, :] = norm_back(total, gain, cot_ref[here, :].astype(F32) * valid).astype(
            BF16
        )

    for place, half in everything:
        scatter_at(place, half).finish()
    low_scatter.finish()
    line.finish()
    spread.finish()
    for step in (steps - 2, steps - 1):
        for copy in stores(step, step % 2):
            copy.wait()
    keep_hidden.wait()
    for keep in keeps:
        keep.wait()


def add_lifted(work, low, table):
    wide = tile_of(work.shape[1])

    @pl.loop(0, work.shape[1] // wide)
    def _(step):
        here = columns(step, wide)
        work[:, here] += nt(low[...], table[here, :])


def mlp_fused(lengths, seq, gu_w, shard, attn_w, d_tab, f_tab, resid, cotangent, gains, dp):
    chunks, rows, model = seq.shape
    width = shard.shape[1]
    tile = 384
    wide = model // dp
    half = rows // 2
    anywhere = pl.BlockSpec(memory_space=pl.ANY)
    vmem = pl.BlockSpec(memory_space=pltpu.VMEM)
    saved = jax.ShapeDtypeStruct((4, rows, width), BF16)
    return pl.pallas_call(
        functools.partial(mlp_kernel, rows),
        out_shape=(
            jax.ShapeDtypeStruct((rows, model), BF16),
            jax.ShapeDtypeStruct((rows, model), BF16),
            jax.ShapeDtypeStruct((4, rows, LANES), BF16),
            jax.ShapeDtypeStruct((rows, LANES), BF16),
            saved,
            saved,
            saved,
            jax.ShapeDtypeStruct((dp,) + shard.shape, BF16),
            jax.ShapeDtypeStruct((4, model, 2 * HD), BF16),
        ),
        in_specs=[pl.BlockSpec(memory_space=pltpu.SMEM)] + [anywhere] * 4 + [vmem] * 5,
        out_specs=(vmem,) * 4 + (anywhere,) * 5,
        scratch_shapes=[
            pltpu.VMEM((rows, model), F32),
            pltpu.VMEM((rows, LANES), F32),
            pltpu.VMEM((2, 4, rows, LANES), BF16),
            pltpu.VMEM((4, rows, model), BF16),
            pltpu.VMEM((2, model, 2 * tile), BF16),
            pltpu.VMEM((4, rows, width), BF16),
            pltpu.VMEM((2, 4, rows, tile), BF16),
            pltpu.VMEM((2, 4, rows, tile), BF16),
            pltpu.VMEM((dp,) + shard.shape, BF16),
            pltpu.SemaphoreType.DMA((2,)),
            pltpu.SemaphoreType.DMA((2, 2)),
            pltpu.SemaphoreType.DMA((2, 2)),
            pltpu.SemaphoreType.DMA((5,)),
            pltpu.SemaphoreType.DMA((3, dp // 2, 2)),
            pltpu.SemaphoreType.DMA((dp, 2)),
            pltpu.VMEM((dp, 4, rows, wide), BF16),
            pltpu.VMEM((dp, 6, half, wide), BF16),
            pltpu.VMEM((dp, 2, half, wide), BF16),
            pltpu.SemaphoreType.DMA((dp, 6, 1)),
            pltpu.SemaphoreType.DMA((dp, 6, 1)),
            pltpu.SemaphoreType.DMA((9,)),
            pltpu.SemaphoreType.DMA((9,)),
        ]
        + scatter_scratch(rows, LANES),
        compiler_params=pltpu.CompilerParams(
            collective_id=7, has_side_effects=True, vmem_limit_bytes=62 * 1024 * 1024
        ),
        name="mlp",
    )(lengths, seq, gu_w, shard, attn_w, d_tab, f_tab, resid, cotangent, gains)


class Layout:
    def __init__(self):
        self.dp = lax.axis_size("dp")
        self.tensor = lax.axis_size("tensor")
        self.total = self.dp * self.tensor
        self.d = lax.axis_index("dp")
        self.t = lax.axis_index("tensor")
        self.me = self.d * self.tensor + self.t
        self.heads_here = HQ // self.tensor
        self.ratio = HQ // KV
        self.share = max(1, self.tensor // KV)
        self.kv_owners = self.total // KV
        self.kv_head = self.t * self.heads_here // self.ratio
        self.user = self.me // self.dp
        self.kv_slice_head = self.me // self.kv_owners

    def device(self, flat):
        return {"dp": flat // self.tensor, "tensor": lax.rem(flat, self.tensor)}


def greet_all(lay):
    barrier = pltpu.get_barrier_semaphore()

    def signal(step, unused):
        peer = lax.rem(lay.me + step, lay.total)
        pl.semaphore_signal(
            barrier, inc=1, device_id=lay.device(peer), device_id_type=MESH
        )
        return unused

    lax.fori_loop(1, lay.total, signal, 0)
    pl.semaphore_wait(barrier, lay.total - 1)


def send_or_keep(lay, sends, source, target, send_sem, recv_sem, flat, maybe_own):
    def far():
        return pltpu.make_async_remote_copy(
            src_ref=source,
            dst_ref=target,
            send_sem=send_sem,
            recv_sem=recv_sem,
            device_id=lay.device(flat),
            device_id_type=MESH,
        )

    if maybe_own is None:
        copy = far()
        copy.start()
        sends.append((None, copy))
        return

    @pl.when(maybe_own)
    def _():
        pltpu.make_async_copy(source, target, recv_sem).start()

    @pl.when(jnp.logical_not(maybe_own))
    def _():
        far().start()

    sends.append((maybe_own, far()))


def finish(sends, received):
    for own, copy in sends:
        if own is None:
            copy.wait_send()
        else:

            @pl.when(jnp.logical_not(own))
            def _(copy=copy):
                copy.wait_send()

    for target, sem in received:
        pltpu.make_async_copy(target, target, sem).wait()


def tables_kernel(d_ref, f_ref, h_ref, k_ref, do_ref, fo_ref, ho_ref, ko_ref, *sems):
    lay = Layout()
    send_sems, recv_sem = sems[:4], sems[4]
    greet_all(lay)
    sends = []
    for step in range(lay.dp):
        group = lax.rem(lay.d + step, lay.dp)
        flat = group * lay.tensor + lay.user
        own = (lay.user == lay.t) if step == 0 else None
        for item, (source, target) in enumerate(((f_ref, fo_ref), (h_ref, ho_ref))):
            send_or_keep(
                lay,
                sends,
                source.at[group],
                target.at[lax.rem(lay.me, lay.dp)],
                send_sems[item].at[step],
                recv_sem.at[item],
                flat,
                own,
            )
        for extra in range(lay.share):
            user = lay.kv_slice_head * lay.share + extra
            flat = group * lay.tensor + user
            send_or_keep(
                lay,
                sends,
                k_ref.at[group],
                ko_ref.at[lax.rem(lay.me, lay.kv_owners)],
                send_sems[2].at[step, extra],
                recv_sem.at[2],
                flat,
                (user == lay.t) if step == 0 else None,
            )
    pltpu.make_async_copy(d_ref.at[lay.d], do_ref.at[lay.me], recv_sem.at[3]).start()
    for step in range(1, lay.total):
        flat = lax.rem(lay.me + step, lay.total)
        send_or_keep(
            lay,
            sends,
            d_ref.at[flat // lay.tensor],
            do_ref.at[lay.me],
            send_sems[3].at[step],
            recv_sem.at[3],
            flat,
            None,
        )
    finish(
        sends,
        (
            (fo_ref, recv_sem.at[0]),
            (ho_ref, recv_sem.at[1]),
            (ko_ref, recv_sem.at[2]),
            (do_ref, recv_sem.at[3]),
        ),
    )


def grads_kernel(d_ref, f_ref, h_ref, k_ref, do_ref, fo_ref, ho_ref, ko_ref, *sems):
    lay = Layout()
    send_sems, recv_sem = sems[:4], sems[4]
    greet_all(lay)
    sends = []
    for step in range(lay.dp):
        slot = lax.rem(lay.d + step, lay.dp)
        flat = lay.t * lay.dp + slot
        for item, (source, target) in enumerate(((f_ref, fo_ref), (h_ref, ho_ref))):
            send_or_keep(
                lay,
                sends,
                source.at[slot],
                target.at[lay.d],
                send_sems[item].at[step],
                recv_sem.at[item],
                flat,
                flat == lay.me,
            )
    for step in range(lay.kv_owners):
        slot = lax.rem(lay.d + step, lay.kv_owners)
        flat = lay.kv_head * lay.kv_owners + slot
        send_or_keep(
            lay,
            sends,
            k_ref.at[slot],
            ko_ref.at[lay.d * lay.share + lax.rem(lay.t, lay.share)],
            send_sems[2].at[step // lay.share, step % lay.share],
            recv_sem.at[2],
            flat,
            flat == lay.me,
        )
    pltpu.make_async_copy(d_ref.at[lay.me], do_ref.at[lay.me], recv_sem.at[3]).start()
    for step in range(1, lay.total):
        flat = lax.rem(lay.me + step, lay.total)
        send_or_keep(
            lay,
            sends,
            d_ref.at[flat],
            do_ref.at[lay.me],
            send_sems[3].at[step],
            recv_sem.at[3],
            flat,
            None,
        )
    finish(
        sends,
        (
            (fo_ref, recv_sem.at[0]),
            (ho_ref, recv_sem.at[1]),
            (ko_ref, recv_sem.at[2]),
            (do_ref, recv_sem.at[3]),
        ),
    )


def exchange(kernel, name, number, arrays, outs, dp, total, share):
    anywhere = pl.BlockSpec(memory_space=pl.ANY)
    return pl.pallas_call(
        kernel,
        out_shape=tuple(jax.ShapeDtypeStruct(shape, BF16) for shape in outs),
        in_specs=[anywhere] * 4,
        out_specs=(anywhere,) * 4,
        scratch_shapes=[
            pltpu.SemaphoreType.DMA((dp,)),
            pltpu.SemaphoreType.DMA((dp,)),
            pltpu.SemaphoreType.DMA((dp, share)),
            pltpu.SemaphoreType.DMA((total,)),
            pltpu.SemaphoreType.DMA((4,)),
        ],
        compiler_params=pltpu.CompilerParams(
            collective_id=number, has_side_effects=True, vmem_limit_bytes=VMEM_LIMIT
        ),
        name=name,
    )(*arrays)


def chunk_start(sq, chunk, part):
    is_own = (3 - chunk) // 3
    is_far = chunk // 3
    near = 1 - is_own - is_far
    neighbour = sq.down if part == 1 else sq.across
    block = sq.me * is_own + sq.far * is_far + neighbour * near
    other_half = chunk // 2 - is_far
    half = 1 - other_half if part == 1 else other_half
    return pl.multiple_of(block * sq.rows + half * sq.half, sq.half)


def rotate_back(values, cosine, sine):
    first, second = values[:, : HD // 2], values[:, HD // 2 :]
    return jnp.concatenate([first * cosine + second * sine, second * cosine - first * sine], axis=1)


def turned(values):
    return values.astype(F32).T.astype(BF16)


def rotate_rows(values, cosine, sine):
    first, second = values[:, : HD // 2], values[:, HD // 2 :]
    return jnp.concatenate([first * cosine - second * sine, second * cosine + first * sine], axis=1)


def softmax_weights(keys, queries, start, half, length):
    shape = (keys.shape[0], queries.shape[0])
    key_at = lax.broadcasted_iota(jnp.int32, shape, 0)
    query_at = lax.rem(lax.broadcasted_iota(jnp.int32, shape, 1), half) + start
    allowed = (key_at <= query_at) & (key_at < length)
    squash = jnp.tanh(nt(keys, queries) * (1.0 / SOFT_CAP))
    return squash, jnp.where(allowed, jnp.exp(SOFT_CAP * squash), 0.0)


def stack_heads(ref, here, heads):
    return jnp.concatenate([ref[here, h * HD : (h + 1) * HD] for h in range(heads)], axis=0)


def far_first(step):
    return step + 3 * ((3 - step) // 3) - 3 * (step // 3)


def attn_kernel(
    rows,
    length_ref,
    seq_hbm,
    weight_hbm,
    d_table,
    h_table,
    k_table,
    cos_ref,
    sin_ref,
    layer_ref,
    gains_ref,
    q_ref,
    k_ref,
    kt_ref,
    v_ref,
    attended_ref,
    inverse_ref,
    low_ref,
    low_out_ref,
    total_ref,
    resid_ref,
    normed_ref,
    mlp_out,
    w_out_all,
    w_q_all,
    h_all,
    seq,
    weight,
    vt,
    low_sum,
    load_sem,
    own_sem,
    gather_send,
    gather_recv,
    h_send,
    h_recv,
    w_send,
    w_recv,
    *scratch,
):
    sq = Square(rows)
    half = sq.half
    model = total_ref.shape[-1]
    q_width = q_ref.shape[1]
    qkv_width = q_width + 2 * HD
    heads = q_width // HD
    wide = tile_of(model)
    weight_load = pltpu.make_async_copy(weight_hbm, weight, load_sem.at[0])
    seq_load = pltpu.make_async_copy(seq_hbm, seq, load_sem.at[1])
    weight_load.start()
    seq_load.start()
    line = Line(None, None, None)
    greet(
        [{"tensor": peer} for peer in (sq.across, sq.down, sq.far)] + [{"dp": line.sibling}]
    )
    out_spread = HalfSpread(
        sq, line, weight_hbm, qkv_width, w_out_all, w_send.at[0], w_recv.at[0]
    )
    q_spread = HalfSpread(sq, line, weight_hbm, 0, w_q_all, w_send.at[1], w_recv.at[1])
    out_spread.start()
    h_spread = sq.spread(lambda peer: h_table, h_all, h_send, h_recv)
    for copy in h_spread:
        copy.start()
    weight_load.wait()
    seq_load.wait()

    @pl.loop(0, 4)
    def _(block):
        here = pl.ds(pl.multiple_of(block * rows, rows), rows)
        low = band(nn(seq[block], d_table[...]), QUERY, VALUE).astype(BF16)
        low_ref[here, :] = low
        cosine, sine = cos_ref[here, :], sin_ref[here, :]
        for h in range(heads):
            column = slice(h * HD, (h + 1) * HD)
            query = nn(seq[block], weight[:, column]) + nt(
                band(low.astype(F32), QUERY).astype(BF16), h_table[column, :]
            )
            q_ref[here, column] = (rotate_rows(query, cosine, sine) * HD ** (-0.5)).astype(BF16)
        key = nn(seq[block], weight[:, q_width : q_width + HD]) + nt(
            band(low.astype(F32), KEY).astype(BF16), k_table[...]
        )
        key = rotate_rows(key, cosine, sine)
        k_ref[here, :] = key.astype(BF16)
        kt_ref[:, here] = key.T.astype(BF16)
        value = nn(seq[block], weight[:, q_width + HD : qkv_width]) + nt(
            band(low.astype(F32), VALUE).astype(BF16), k_table[...]
        )
        v_ref[here, :] = value.astype(BF16)
        vt[:, here] = value.T.astype(BF16)

    out_spread.forward()
    part, part_low = scratch[0], scratch[5]
    scatters = (ChunkScatter(sq, *scratch[:5]), ChunkScatter(sq, *scratch[5:10]))

    @pl.loop(0, 4)
    def _(step):
        chunk = far_first(step)
        for side in range(2):
            start = chunk_start(sq, chunk, side)
            here = pl.ds(start, half)
            unused, weights = softmax_weights(
                k_ref[...], stack_heads(q_ref, here, heads), start, half, length_ref[0]
            )
            inverse = 1.0 / jnp.sum(weights, axis=0, keepdims=True)
            mixed = nn(vt[...], (weights * inverse).astype(BF16)).T.astype(BF16)
            for h in range(heads):
                inverse_ref[h : h + 1, here] = inverse[:, h * half : (h + 1) * half]
                attended_ref[here, h * HD : (h + 1) * HD] = mixed[h * half : (h + 1) * half]

        attended = jnp.concatenate(
            [attended_ref[pl.ds(chunk_start(sq, chunk, side), half), :] for side in range(2)],
            axis=0,
        )
        part_low[chunk] = band(nn(attended, h_table[...]), OUT).astype(BF16)

        @pl.loop(0, model // wide)
        def _(tile):
            here = columns(tile, wide)
            part[chunk, :, here] = nt(attended, weight[here, qkv_width:]).astype(BF16)

            @pl.when(step == 0)
            def _():
                scatters[0].send(1, tile)

            @pl.when(step == 1)
            def _():
                scatters[0].send(0, tile)

        @pl.when(step == 0)
        def _():
            scatters[1].send_far()

        @pl.when(step == 1)
        def _():
            scatters[1].send_own()

    for scatter in scatters:
        scatter.pass_on()
    scatters[1].collect(low_sum)
    low_out_ref[...] = low_sum[...].astype(BF16)
    scatters[0].collect(total_ref)
    add_lifted(total_ref, low_out_ref, d_table)

    @pl.loop(0, rows // BLOCK)
    def _(step):
        here = pl.ds(pl.multiple_of(step * BLOCK, BLOCK), BLOCK)
        resid = layer_ref[here, :].astype(F32) + rms_norm(total_ref[here, :], gains_ref[1:2, :])
        resid_ref[here, :] = resid
        normed_ref[here, :] = rms_norm(resid, gains_ref[2:3, :]).astype(BF16)

    gather = ChunkGather(sq, normed_ref, mlp_out, gather_send, gather_recv)
    gather.start()
    own = pltpu.make_async_copy(normed_ref, mlp_out.at[0], own_sem)
    own.start()
    gather.wait_chunk(1)
    q_spread.start()
    out_spread.share()
    for chunk in range(2, 4):
        gather.wait_chunk(chunk)
    own.wait()
    q_spread.forward()
    for copy in h_spread:
        copy.wait()
    out_spread.finish()
    q_spread.share()
    q_spread.finish()
    gather.finish()
    for scatter in scatters:
        scatter.finish()


def attn_fused(lengths, seq, weight, d_tab, h_tab, k_tab, cosine, sine, layer_in, gains):
    rows, model = layer_in.shape
    q_width = weight.shape[1] - 2 * HD
    q_width //= 2
    qkv_width = q_width + 2 * HD
    anywhere = pl.BlockSpec(memory_space=pl.ANY)
    vmem = pl.BlockSpec(memory_space=pltpu.VMEM)
    narrow = jax.ShapeDtypeStruct((LEN, HD), BF16)
    return pl.pallas_call(
        functools.partial(attn_kernel, rows),
        out_shape=(
            jax.ShapeDtypeStruct((LEN, q_width), BF16),
            narrow,
            jax.ShapeDtypeStruct((HD, LEN), BF16),
            narrow,
            jax.ShapeDtypeStruct((LEN, q_width), BF16),
            jax.ShapeDtypeStruct((q_width // HD, LEN), F32),
            jax.ShapeDtypeStruct((LEN, LANES), BF16),
            jax.ShapeDtypeStruct((rows, LANES), BF16),
            jax.ShapeDtypeStruct((rows, model), F32),
            jax.ShapeDtypeStruct((rows, model), F32),
            jax.ShapeDtypeStruct((rows, model), BF16),
            jax.ShapeDtypeStruct((4, rows, model), BF16),
            jax.ShapeDtypeStruct((4, model, q_width), BF16),
            jax.ShapeDtypeStruct((4, model, q_width), BF16),
            jax.ShapeDtypeStruct((4, q_width, LANES), BF16),
        ),
        in_specs=[pl.BlockSpec(memory_space=pltpu.SMEM)] + [anywhere] * 2 + [vmem] * 7,
        out_specs=(vmem,) * 11 + (anywhere,) * 4,
        scratch_shapes=[
            pltpu.VMEM((4, rows, model), BF16),
            pltpu.VMEM(weight.shape, BF16),
            pltpu.VMEM((HD, LEN), BF16),
            pltpu.VMEM((rows, LANES), F32),
            pltpu.SemaphoreType.DMA((2,)),
            pltpu.SemaphoreType.DMA,
            pltpu.SemaphoreType.DMA((6,)),
            pltpu.SemaphoreType.DMA((6,)),
            pltpu.SemaphoreType.DMA((3,)),
            pltpu.SemaphoreType.DMA((4,)),
            pltpu.SemaphoreType.DMA((2, 9)),
            pltpu.SemaphoreType.DMA((2, 9)),
        ]
        + scatter_scratch(rows, model, model // tile_of(model))
        + scatter_scratch(rows, LANES),
        compiler_params=pltpu.CompilerParams(
            collective_id=8, has_side_effects=True, vmem_limit_bytes=62 * 1024 * 1024
        ),
        name="attn",
    )(lengths, seq, weight, d_tab, h_tab, k_tab, cosine, sine, layer_in, gains)


def attn_back_kernel(
    rows,
    ids_ref,
    length_ref,
    back_ref,
    low_gu_ref,
    resid_ref,
    total_ref,
    cot_ref,
    layer_hbm,
    gains_ref,
    weight_hbm,
    w_out_hbm,
    w_q_hbm,
    w_kv_hbm,
    seq_hbm,
    q_hbm,
    k_hbm,
    kt_hbm,
    v_hbm,
    attended_hbm,
    inverse_ref,
    cos_hbm,
    sin_hbm,
    low_hbm,
    d_table,
    h_all,
    k_table,
    normed_hbm,
    low_out_ref,
    grad_mlp_hbm,
    low_down_ref,
    f_ref,
    o_ref,
    in_out,
    heads_out,
    hidden_out,
    query_out,
    keyval_out,
    gateup_out,
    resid_out,
    q_ref,
    k_ref,
    kt_ref,
    v_ref,
    attended_ref,
    cos_ref,
    sin_ref,
    low_ref,
    normed_ref,
    grad_mlp_ref,
    layer_ref,
    slots,
    total,
    work,
    g_ref,
    low_sum,
    buf,
    att_send,
    att,
    low_own,
    low_all,
    part_low,
    q_land,
    kv_land,
    low_land,
    q_grad,
    k_sum,
    v_sum,
    kv_grad,
    d_turned,
    h_turned,
    k_turned,
    d_send,
    d_land,
    d_sum,
    d_recv,
    f_recv,
    hk_send,
    hk_land,
    hk_recv,
    load_sem,
    late_sem,
    att_sends,
    att_recvs,
    back_sends,
    back_recvs,
    f_sem,
    d_sem,
    hk_sem,
    group_send,
    group_recv,
    line_recv,
):
    sq = Square(rows)
    dp = lax.axis_size("dp")
    d = lax.axis_index("dp")
    model = o_ref.shape[-1]
    half = sq.half
    wide = tile_of(model)
    q_width = q_ref.shape[1]
    qkv_width = q_width + 2 * HD
    others = (sq.far, sq.across, sq.down)
    arrivals = ((sq.down, 2), (sq.far, 0), (sq.across, 1))
    sources = [w_out_hbm.at[peer] for peer in others]
    sources.append(weight_hbm.at[:, pl.ds(qkv_width, q_width)])
    sources.append(weight_hbm.at[:, pl.ds(0, q_width)])
    sources.append(weight_hbm.at[:, pl.ds(q_width, 2 * HD)])
    for peer, unused in arrivals:
        sources += [w_q_hbm.at[peer], w_kv_hbm.at[peer]]
    loads = [
        pltpu.make_async_copy(source, slots.at[which % 4], load_sem.at[1 + which])
        for which, source in enumerate(sources)
    ]
    seq_load = pltpu.make_async_copy(seq_hbm, buf, load_sem.at[0])
    late = [
        pltpu.make_async_copy(source, target, late_sem.at[which])
        for which, (source, target) in enumerate(
            (
                (q_hbm, q_ref),
                (k_hbm, k_ref),
                (kt_hbm, kt_ref),
                (v_hbm, v_ref),
                (attended_hbm, attended_ref),
                (cos_hbm, cos_ref),
                (sin_hbm, sin_ref),
                (low_hbm, low_ref),
                (normed_hbm, normed_ref),
                (grad_mlp_hbm, grad_mlp_ref),
                (layer_hbm, layer_ref),
            )
        )
    ]
    for copy in loads[:4]:
        copy.start()
    for copy in late:
        copy.start()
    seq_load.start()
    peers = [{"tensor": peer} for peer in (sq.across, sq.down, sq.far)]
    peers += [{"dp": lax.rem(d + step, dp)} for step in range(1, dp)]
    call(peers)

    low_gu = low_gu_ref[...].astype(BF16)

    @pl.loop(0, model // wide)
    def _(step):
        here = columns(step, wide)
        work[:, here] = back_ref[:, here] + nt(low_gu, d_table[here, :])

    @pl.loop(0, rows // BLOCK)
    def _(step):
        here = pl.ds(pl.multiple_of(step * BLOCK, BLOCK), BLOCK)
        at = sq.me * rows + step * BLOCK + lax.broadcasted_iota(jnp.int32, (BLOCK, 1), 0)
        valid = (at < length_ref[0]).astype(F32)
        mid = cot_ref[here, :].astype(F32) * valid + norm_back(
            resid_ref[here, :], gains_ref[2:3, :], work[here, :]
        )
        work[here, :] = mid
        g_ref[here, :] = norm_back(total_ref[here, :], gains_ref[1:2, :], mid).astype(BF16)

    low_out = band(nn(g_ref[...], d_table[...]), OUT).astype(BF16)
    low_own[...] = turned(low_out)[OUT]
    pl.semaphore_wait(pltpu.get_barrier_semaphore(), len(peers))
    heads_out_copies = []
    for which, peer in enumerate(others + (sq.me,)):
        loads[which].wait()
        grads = (nn(g_ref[...], slots[which]) + nt(low_out, h_all[peer])).astype(BF16)
        loads[which + 4].start()
        if which == 3:
            att[sq.me] = grads
            low_all[sq.me] = low_own[...]
            continue
        att_send[which] = grads
        copies = tuple(
            remote(
                source, target.at[sq.me], att_sends.at[which, item], att_recvs.at[which, item], peer
            )
            for item, (source, target) in enumerate(
                ((att_send.at[which], att), (low_own, low_all))
            )
        )
        for copy in copies:
            copy.start()
        heads_out_copies.append(copies)
    line = []
    line += along(lambda k: f_ref.at[k // 2, lax.rem(k, 2)], f_recv, f_sem, line_recv.at[0])
    back = []
    for which, peer in enumerate(others):
        here = pl.ds(pl.multiple_of(peer * rows, rows), rows)
        back.append(
            tuple(
                remote(
                    source,
                    target.at[sq.me],
                    back_sends.at[which, item],
                    back_recvs.at[which, item],
                    peer,
                )
                for item, (source, target) in enumerate(
                    (
                        (q_grad.at[here], q_land),
                        (kv_grad.at[here], kv_land),
                        (part_low.at[peer], low_land),
                    )
                )
            )
        )

    for copy in late:
        copy.wait()
    d_turned[...] = jnp.zeros_like(d_turned)
    low_grads = (
        (turned(low_gu)[GATE.start : UP.stop], normed_ref, slice(GATE.start, UP.stop)),
        (turned(low_out_ref[...])[OUT], g_ref, OUT),
        (turned(low_down_ref[...])[DOWN], grad_mlp_ref, DOWN),
    )

    @pl.loop(0, model // wide)
    def _(step):
        here = columns(step, wide)
        for low, source, place in low_grads:
            d_turned[place, here] = nn(low, source[:, here])

    h_turned[...] = jnp.zeros_like(h_turned)
    k_turned[...] = jnp.zeros_like(k_turned)
    k_sum[...] = jnp.zeros_like(k_sum)
    v_sum[...] = jnp.zeros_like(v_sum)
    heads = q_width // HD
    stacked = heads * half

    @pl.loop(0, 4)
    def _(turn):
        for step, (unused, which) in enumerate(arrivals):

            @pl.when(turn == step + 1)
            def _(which=which):
                for copy in heads_out_copies[which]:
                    copy.wait_recv()

        is_own, is_across = (3 - turn) // 3, turn // 3
        is_far = turn // 2 - is_across
        block = (
            sq.me * is_own
            + sq.far * is_far
            + sq.across * is_across
            + sq.down * (1 - is_own - is_far - is_across)
        )
        low_turned = low_all[block]
        h_turned[:RANK, :] += nn(
            low_turned, attended_ref[pl.ds(pl.multiple_of(block * rows, rows), rows), :]
        )
        for last in range(4):

            @pl.when(block == last)
            def _(last=last):
                seen = slice(0, (last + 1) * rows)

                @pl.loop(0, 2)
                def _(side):
                    start = pl.multiple_of(last * rows + side * half, half)
                    here = pl.ds(start, half)
                    place = pl.ds(pl.multiple_of(side * half, half), half)
                    queries = stack_heads(q_ref, here, heads)
                    grads = jnp.concatenate(
                        [att[last, place, h * HD : (h + 1) * HD] for h in range(heads)], axis=0
                    )
                    inverse = jnp.concatenate(
                        [inverse_ref[h : h + 1, here] for h in range(heads)], axis=1
                    )
                    squash, weights = softmax_weights(
                        k_ref[seen, :], queries, start, half, length_ref[0]
                    )
                    probs = weights * inverse
                    grad_probs = nt(v_ref[seen, :], grads)
                    mean = jnp.sum(probs * grad_probs, axis=0, keepdims=True)
                    grad_raw = (probs * (grad_probs - mean) * (1.0 - squash * squash)).astype(BF16)
                    k_sum[seen, :] += nn(grad_raw, queries)
                    v_sum[seen, :] += nn(probs.astype(BF16), grads)
                    q_back = nn(kt_ref[:, seen], grad_raw).T * HD ** (-0.5)
                    for h in range(heads):
                        q_grad[here, h * HD : (h + 1) * HD] = rotate_back(
                            q_back[h * half : (h + 1) * half], cos_ref[here, :], sin_ref[here, :]
                        ).astype(BF16)

        for step, (unused, which) in enumerate(arrivals):

            @pl.when(turn == step + 1)
            def _(which=which):
                back[which][0].start()

    kv_grad[:, :HD] = rotate_back(k_sum[...], cos_ref[...], sin_ref[...]).astype(BF16)
    kv_grad[:, HD:] = v_sum[...].astype(BF16)
    for copies in back:
        copies[1].start()

    @pl.loop(0, 4)
    def _(block):
        here = pl.ds(pl.multiple_of(block * rows, rows), rows)
        part_low[block] = (
            band(nn(q_grad[here, :], h_all[sq.me]), QUERY)
            + band(nn(kv_grad[here, :HD], k_table[...]), KEY)
            + band(nn(kv_grad[here, HD:], k_table[...]), VALUE)
        ).astype(BF16)

    for copies in back:
        copies[2].start()

    def add_block(queries, keys_values, which, first):
        for item in range(2):
            loads[which + item].wait()
        low_q, low_kv = which % 4, (which + 1) % 4

        @pl.loop(0, model // wide)
        def _(step):
            here = columns(step, wide)
            grad = nt(queries, slots[low_q, here, :]) + nt(keys_values, slots[low_kv, here, :])
            total[:, here] = grad if first else total[:, here] + grad

        for item in range(2):
            if which + item + 4 < len(loads):
                loads[which + item + 4].start()

    own = pl.ds(pl.multiple_of(sq.me * rows, rows), rows)
    add_block(q_grad[own, :], kv_grad[own, :], 4, True)
    seq_load.wait()

    @pl.loop(0, 4)
    def _(block):
        here = pl.ds(pl.multiple_of(block * rows, rows), rows)
        grad_turned = turned(part_low[block])[: VALUE.stop]
        low_turned = turned(low_ref[here, :])
        h_turned[RANK : 2 * RANK, :] += nn(low_turned[QUERY], q_grad[here, :])
        k_turned[:RANK, :] += nn(low_turned[KEY], kv_grad[here, :HD])
        k_turned[RANK : 2 * RANK, :] += nn(low_turned[VALUE], kv_grad[here, HD:])

        @pl.loop(0, model // wide)
        def _(step):
            where = columns(step, wide)
            d_turned[: VALUE.stop, where] += nn(grad_turned, buf[block, :, where])

    @pl.loop(0, model // LANES)
    def _(step):
        here = columns(step, LANES)
        d_send[here, :] = d_turned[:, here].T.astype(BF16)

    d_rows = d_sum.shape[1]
    spread = []
    for k in range(dp):
        spread.append(
            sq.spread(
                lambda peer, k=k: d_send.at[pl.ds(pl.multiple_of((k * 4 + peer) * d_rows, 8), d_rows)],
                d_land.at[k],
                group_send.at[k],
                group_recv.at[k],
            )
        )
    cores = hk_send.shape[0]
    h_size, k_size = q_width // dp, HD // dp
    hk_send[...] = jnp.zeros_like(hk_send)
    for core in range(cores):
        for peer in range(4):
            at = core * 4 + peer
            hk_send[core, peer, : 2 * RANK, :h_size] = h_turned[
                : 2 * RANK, at * h_size : (at + 1) * h_size
            ].astype(BF16)
            hk_send[core, peer, 2 * RANK :, :k_size] = k_turned[
                : 2 * RANK, at * k_size : (at + 1) * k_size
            ].astype(BF16)
    spread.append(
        sq.spread(lambda peer: hk_send.at[:, peer], hk_land, group_send.at[dp], group_recv.at[dp])
    )
    for copies in spread:
        for copy in copies:
            copy.start()
    for step, (peer, which) in enumerate(arrivals):
        for copy in back[which]:
            copy.wait_recv()
        add_block(q_land[peer], kv_land[peer], 6 + 2 * step, False)
    for copies in spread:
        copies[0].wait()
        for copy in copies[1:]:
            copy.wait_recv()
    for k in range(dp):
        d_sum[k] = sum(d_land[k, t].astype(F32) for t in range(4)).astype(BF16)
    line += along(lambda k: d_sum.at[k], d_recv, d_sem, line_recv.at[1])
    line += along(lambda k: hk_land.at[k // 2, lax.rem(k, 2)], hk_recv, hk_sem, line_recv.at[2])
    low_sum[...] = sum(
        low_land[peer].astype(F32) for peer, unused in arrivals
    ) + part_low[sq.me].astype(F32)
    low_qkv = low_sum[...].astype(BF16)

    @pl.loop(0, model // wide)
    def _(step):
        here = columns(step, wide)
        total[:, here] += nt(low_qkv, d_table[here, :])

    @pl.loop(0, rows // BLOCK)
    def _(step):
        here = pl.ds(pl.multiple_of(step * BLOCK, BLOCK), BLOCK)
        o_ref[here, :] = (
            work[here, :]
            + norm_back(layer_ref[here, :].astype(F32), gains_ref[0:1, :], total[here, :])
        ).astype(BF16)

    for item, target in enumerate((f_recv, d_recv, hk_recv)):
        pltpu.make_async_copy(target, target, line_recv.at[item]).wait()

    @pl.loop(0, NA)
    def _(adapter):
        def pick(received):
            total = None
            for group in range(dp):
                mine = jnp.where(
                    ids_ref[group] == adapter, received[group].astype(F32), 0.0
                )
                total = mine if total is None else total + mine
            return total

        d_all = pick(d_recv)
        in_out[adapter] = d_all[:, : 5 * RANK]
        d_flip = d_all.T
        f_all = pick(f_recv)
        hidden_out[adapter] = f_all[:RANK]
        hk_all = pick(hk_recv)
        heads_out[adapter] = hk_all[:RANK, :h_size]
        query_out[adapter] = hk_all[RANK : 2 * RANK, :h_size]
        for which in range(2):
            first = (which + 2) * RANK
            keyval_out[adapter, which] = hk_all[first : first + RANK, :k_size]
            first = (which + 1) * RANK
            gateup_out[adapter, which] = f_all[first : first + RANK]
            first = (which + 5) * RANK
            resid_out[adapter, which] = d_flip[first : first + RANK]

    for copies in spread:
        for copy in copies[1:]:
            copy.wait_send()
    for copies in heads_out_copies + back:
        for copy in copies:
            copy.wait_send()
    for copy in line:
        copy.wait_send()


LATE = (12, 13, 14, 15, 16, 18, 19, 20, 24, 26, 5)


def attn_back_fused(scalars, arrays, grad_shapes, dp, total):
    anywhere = pl.BlockSpec(memory_space=pl.ANY)
    vmem = pl.BlockSpec(memory_space=pltpu.VMEM)
    smem = pl.BlockSpec(memory_space=pltpu.SMEM)
    rows, model = arrays[0].shape
    q, f_in = arrays[12], arrays[-1]
    q_width = q.shape[1]
    specs = [smem, smem] + [vmem] * len(arrays)
    late = [arrays[which] for which in LATE]
    for which in LATE + (7, 8, 9, 10, 11):
        specs[2 + which] = anywhere
    outs = [jax.ShapeDtypeStruct((rows, model), BF16)]
    outs += [jax.ShapeDtypeStruct(shape, F32) for shape in grad_shapes]
    d_rows = model // total
    messages = f_in.shape[2:]
    return pl.pallas_call(
        functools.partial(attn_back_kernel, rows),
        out_shape=tuple(outs),
        in_specs=specs,
        out_specs=(vmem,) * len(outs),
        scratch_shapes=[
            *(pltpu.VMEM(array.shape, array.dtype) for array in late),
            pltpu.VMEM((4, model, q_width), BF16),
            pltpu.VMEM((rows, model), F32),
            pltpu.VMEM((rows, model), F32),
            pltpu.VMEM((rows, model), BF16),
            pltpu.VMEM((rows, LANES), F32),
            pltpu.VMEM((4, rows, model), BF16),
            pltpu.VMEM((3, rows, q_width), BF16),
            pltpu.VMEM((4, rows, q_width), BF16),
            pltpu.VMEM((RANK, rows), BF16),
            pltpu.VMEM((4, RANK, rows), BF16),
            pltpu.VMEM((4, rows, LANES), BF16),
            pltpu.VMEM((4, rows, q_width), BF16),
            pltpu.VMEM((4, rows, 2 * HD), BF16),
            pltpu.VMEM((4, rows, LANES), BF16),
            pltpu.VMEM((LEN, q_width), BF16),
            pltpu.VMEM((LEN, HD), F32),
            pltpu.VMEM((LEN, HD), F32),
            pltpu.VMEM((LEN, 2 * HD), BF16),
            pltpu.VMEM((LANES, model), F32),
            pltpu.VMEM((2 * RANK, q_width), F32),
            pltpu.VMEM((2 * RANK, HD), F32),
            pltpu.VMEM((model, LANES), BF16),
            pltpu.VMEM((dp, 4, d_rows, LANES), BF16),
            pltpu.VMEM((dp, d_rows, LANES), BF16),
            pltpu.VMEM((dp, d_rows, LANES), BF16),
            pltpu.VMEM((dp,) + messages, BF16),
            pltpu.VMEM((dp // 4, 4, 4 * RANK, LANES), BF16),
            pltpu.VMEM((4, dp // 4, 4 * RANK, LANES), BF16),
            pltpu.VMEM((dp, 4 * RANK, LANES), BF16),
            pltpu.SemaphoreType.DMA((13,)),
            pltpu.SemaphoreType.DMA((len(late),)),
            pltpu.SemaphoreType.DMA((3, 2)),
            pltpu.SemaphoreType.DMA((3, 2)),
            pltpu.SemaphoreType.DMA((3, 3)),
            pltpu.SemaphoreType.DMA((3, 3)),
            pltpu.SemaphoreType.DMA((dp,)),
            pltpu.SemaphoreType.DMA((dp,)),
            pltpu.SemaphoreType.DMA((dp,)),
            pltpu.SemaphoreType.DMA((dp + 1, 3)),
            pltpu.SemaphoreType.DMA((dp + 1, 4)),
            pltpu.SemaphoreType.DMA((3,)),
        ],
        compiler_params=pltpu.CompilerParams(
            collective_id=6, has_side_effects=True, vmem_limit_bytes=62 * 1024 * 1024
        ),
        name="attn_back",
    )(*scalars, *arrays)


def per_device(
    layer_in,
    cotangent,
    lengths,
    adapter_ids,
    norm_gains,
    query_weight,
    key_weight,
    value_weight,
    out_weight,
    gate_weight,
    up_weight,
    down_weight,
    adapt_in,
    adapt_heads,
    adapt_hidden,
    lift_query,
    lift_keyval,
    lift_gateup,
    lift_resid,
):
    lay = Layout()
    count = lay.tensor
    rows = layer_in.shape[0]
    group_rows = rows * count
    assert lengths.shape[0] == 1 and group_rows == LEN
    heads_here = lay.heads_here
    head_width = heads_here * HD
    hidden_here = FF // count
    assert lay.ratio % heads_here == 0

    key_cols = lax.dynamic_slice_in_dim(key_weight, lay.kv_head * HD, HD, 1)
    value_cols = lax.dynamic_slice_in_dim(value_weight, lay.kv_head * HD, HD, 1)
    attn_shard = jnp.concatenate([query_weight, key_cols, value_cols, out_weight.T], axis=1)
    gate_up_shard = jnp.concatenate([gate_weight, up_weight], axis=1)
    down_shard = down_weight.T
    attn_shard, gate_up_shard, down_shard = lax.optimization_barrier(
        (attn_shard, gate_up_shard, down_shard)
    )
    qkv_width = head_width + 2 * HD

    cosine, sine = tables(LEN, HD)
    if count == 4 and lay.dp == 8:
        seq_attn, all_ids, d_tab, f_tab, h_tab, k_tab, attn_w = front(
            jnp.broadcast_to(adapter_ids, (8, LANES)),
            layer_in,
            norm_gains,
            jnp.concatenate(
                [
                    lift_gateup.reshape(NA, 2 * RANK, -1),
                    jnp.swapaxes(adapt_hidden, 1, 2),
                ],
                axis=1,
            ),
            jnp.concatenate(
                [jnp.swapaxes(adapt_in, 1, 2), lift_resid.reshape(NA, 2 * RANK, -1)], axis=1
            ),
            jnp.concatenate(
                [
                    jnp.swapaxes(adapt_heads, 1, 2),
                    lift_query,
                    jnp.pad(
                        lift_keyval.reshape(NA, 2 * RANK, -1),
                        ((0, 0), (0, 0), (0, lift_query.shape[2] - lift_keyval.shape[3])),
                    ),
                ],
                axis=1,
            ),
            attn_shard,
            lay.dp,
            (D, hidden_here, head_width, HD),
        )
        attn_w = attn_w.reshape(D, -1)
        gate_up_shard, attn_w = lax.optimization_barrier((gate_up_shard, attn_w))
        gate_up_w = lax.all_gather(gate_up_shard, "dp", axis=0, tiled=True)
        (
            queries,
            keys,
            keys_turned,
            values,
            attended,
            inverse,
            low_qkv,
            low_out,
            attn_total,
            resid_mid,
            normed_mlp,
            seq_mlp,
            w_out_all,
            w_q_all,
            h_all,
        ) = attn_fused(
            lengths,
            seq_attn.reshape(count, rows, D),
            attn_w,
            d_tab,
            h_tab,
            k_tab,
            cosine.reshape(LEN, HD // 2),
            sine.reshape(LEN, HD // 2),
            layer_in,
            norm_gains,
        )
        (
            layer_out,
            grad_mlp,
            low_gu,
            low_down,
            hidden,
            slope,
            gelu,
            down_w,
            w_kv_all,
        ) = mlp_fused(
            lengths,
            seq_mlp,
            gate_up_w,
            down_shard,
            attn_w,
            d_tab,
            f_tab,
            resid_mid,
            cotangent,
            norm_gains,
            lay.dp,
        )
        mlp_back, grad_low_gu, f_grad = mlp_back_fused(
            grad_mlp,
            down_w.reshape(D, hidden_here),
            gate_up_w,
            slope,
            gelu,
            hidden,
            low_gu,
            d_tab,
            f_tab,
            lay.dp,
        )
        grad_shapes = [
            table.shape
            for table in (
                adapt_in,
                adapt_heads,
                adapt_hidden,
                lift_query,
                lift_keyval,
                lift_gateup,
                lift_resid,
            )
        ]
        for which in (1, 2):
            shape = grad_shapes[which]
            grad_shapes[which] = (shape[0], shape[2], shape[1])
        grads = list(
            attn_back_fused(
                (all_ids[:, 0, 0], lengths),
                (
                    mlp_back,
                    grad_low_gu,
                    resid_mid,
                    attn_total,
                    cotangent,
                    layer_in,
                    norm_gains,
                    attn_w,
                    w_out_all,
                    w_q_all,
                    w_kv_all,
                    seq_attn.reshape(count, rows, D),
                    queries,
                    keys,
                    keys_turned,
                    values,
                    attended,
                    inverse,
                    cosine.reshape(LEN, HD // 2),
                    sine.reshape(LEN, HD // 2),
                    low_qkv,
                    d_tab,
                    h_all,
                    k_tab,
                    normed_mlp,
                    low_out,
                    grad_mlp,
                    low_down,
                    f_grad,
                ),
                tuple(grad_shapes),
                lay.dp,
                lay.total,
            )
        )
        for which in (2, 3):
            grads[which] = jnp.swapaxes(grads[which], 1, 2)
        return (layer_out, *grads)

    attn_w = lax.all_gather(attn_shard, "dp", axis=0, tiled=True)
    gate_up_w = lax.all_gather(gate_up_shard, "dp", axis=0, tiled=True)

    all_ids = lax.all_gather(adapter_ids[:, 0], "dp", axis=0, tiled=True)
    group_hot = (all_ids[:, None] == jnp.arange(NA, dtype=jnp.int32)[None, :]).astype(BF16)

    def rows_of(table):
        moved = jnp.moveaxis(table, -1, 1)
        return moved.reshape(NA, moved.shape[1], -1)

    def choose(*parts):
        packed = lanes(*parts)
        return lax.dot_general(
            group_hot, packed, (((1,), (0,)), ((), ())), preferred_element_type=F32
        ).astype(BF16)

    d_send = choose((QUERY, adapt_in), (OUT, rows_of(lift_resid)))
    f_send = choose((GATE, rows_of(lift_gateup)), (DOWN, adapt_hidden))
    h_send = choose((QUERY, rows_of(lift_query)), (OUT, adapt_heads))
    k_send = choose((KEY, rows_of(lift_keyval)))
    d_rows, f_rows, h_rows, k_rows = (item.shape[1] for item in (d_send, f_send, h_send, k_send))
    d_tab, f_tab, h_tab, k_tab = exchange(
        tables_kernel,
        "adapter_tables",
        3,
        (d_send, f_send, h_send, k_send),
        (
            (lay.total, d_rows, LANES),
            (lay.dp, f_rows, LANES),
            (lay.dp, h_rows, LANES),
            (lay.kv_owners, k_rows, LANES),
        ),
        lay.dp,
        lay.total,
        lay.share,
    )
    d_tab = d_tab.reshape(D, LANES)
    f_tab = f_tab.reshape(hidden_here, LANES)
    h_tab = h_tab.reshape(head_width, LANES)
    k_tab = k_tab.reshape(HD, LANES)
    in_qkv, in_gu = d_tab[:, : 3 * RANK], d_tab[:, 3 * RANK : 5 * RANK]
    lift_out, lift_down = d_tab[:, OUT], d_tab[:, DOWN]
    map_hidden, lift_gate, lift_up = f_tab[:, DOWN], f_tab[:, GATE], f_tab[:, UP]
    map_heads, lift_q = h_tab[:, OUT], h_tab[:, QUERY]
    lift_k, lift_v = k_tab[:, KEY], k_tab[:, VALUE]

    row_start = lay.t * rows
    length = lengths[0]
    row_valid = ((row_start + jnp.arange(rows, dtype=jnp.int32)) < length).astype(F32)[:, None]
    place = jnp.arange(LEN, dtype=jnp.int32)
    allowed = (place[:, None] >= place[None, :]) & (place[None, :] < length)

    resid_in = layer_in.astype(F32)
    normed_attn = rms_norm(resid_in, norm_gains[0]).astype(BF16)
    seq_attn = tensor_gather(normed_attn, count)
    low_qkv = nn(seq_attn, in_qkv).astype(BF16)
    low_q, low_k, low_v = (low_qkv[:, i * RANK : (i + 1) * RANK] for i in range(3))
    qkv = nn(seq_attn, attn_w[:, :qkv_width])
    query_pre = (qkv[:, :head_width] + nt(low_q, lift_q)).reshape(LEN, heads_here, HD)
    key_pre = (qkv[:, head_width : head_width + HD] + nt(low_k, lift_k)).reshape(LEN, 1, HD)
    value_pre = qkv[:, head_width + HD :] + nt(low_v, lift_v)
    queries = (rotate(query_pre, cosine, sine) * HD ** (-0.5)).astype(BF16)
    keys = rotate(key_pre, cosine, sine).astype(BF16).reshape(LEN, HD)
    values = value_pre.astype(BF16)

    def scores_of():
        raw = jnp.einsum("qhd,kd->hqk", queries, keys, preferred_element_type=F32)
        squash = jnp.tanh(raw / SOFT_CAP)
        return squash, jnp.where(allowed[None], jnp.exp(SOFT_CAP * squash), 0.0)

    squash, weights = scores_of()
    inverse_total = 1.0 / jnp.sum(weights, axis=-1, keepdims=True)
    attended = jnp.einsum(
        "hqk,kd->qhd", (weights * inverse_total).astype(BF16), values, preferred_element_type=F32
    )
    attended = attended.astype(BF16).reshape(LEN, head_width)
    w_out = attn_w[:, qkv_width:]
    out_part = nt(attended, w_out).astype(BF16)
    low_out_part = pad_lanes(nn(attended, map_heads).astype(BF16))
    attn_main, low_out = tensor_scatter(out_part, low_out_part, count)
    low_out = low_out[:, :RANK].astype(BF16)
    attn_total = attn_main + nt(low_out, lift_out)
    resid_mid = resid_in + rms_norm(attn_total, norm_gains[1])

    normed_mlp = rms_norm(resid_mid, norm_gains[2]).astype(BF16)
    seq_mlp = tensor_gather(normed_mlp, count)
    low_gu = nn(seq_mlp, in_gu).astype(BF16)
    low_g, low_u = low_gu[:, :RANK], low_gu[:, RANK:]
    w_gate, w_up = gate_up_w[:, :hidden_here], gate_up_w[:, hidden_here:]
    gate = nn(seq_mlp, w_gate) + nt(low_g, lift_gate)
    up = nn(seq_mlp, w_up) + nt(low_u, lift_up)
    hidden, slope, gelu = gelu_parts(gate, up)
    down_w = lax.all_gather(down_shard, "dp", axis=0, tiled=True)
    down_part = nt(hidden, down_w).astype(BF16)
    low_down_part = pad_lanes(nn(hidden, map_hidden).astype(BF16))
    mlp_main, low_down = tensor_scatter(down_part, low_down_part, count)
    low_down = low_down[:, :RANK].astype(BF16)
    mlp_total = mlp_main + nt(low_down, lift_down)
    layer_out = (row_valid * (resid_mid + rms_norm(mlp_total, norm_gains[3]))).astype(BF16)

    grad_out = cotangent.astype(F32) * row_valid
    grad_mlp = norm_back(mlp_total, norm_gains[3], grad_out).astype(BF16)
    seq_grad_mlp = tensor_gather(grad_mlp, count)
    grad_low_down = nn(seq_grad_mlp, lift_down).astype(BF16)
    grad_hidden = nn(seq_grad_mlp, down_w) + nt(grad_low_down, map_hidden)
    grad_gate = (grad_hidden * slope.astype(F32)).astype(BF16)
    grad_up = (grad_hidden * gelu.astype(F32)).astype(BF16)
    low_gu_part = pad_lanes(
        jnp.concatenate([nn(grad_gate, lift_gate), nn(grad_up, lift_up)], axis=1).astype(BF16)
    )
    mlp_back_part = (nt(grad_gate, w_gate) + nt(grad_up, w_up)).astype(BF16)
    mlp_back, grad_low_gu = tensor_scatter(mlp_back_part, low_gu_part, count)
    f_parts = [tn(hidden, grad_low_down), tn(grad_gate, low_g), tn(grad_up, low_u)]
    grad_low_gu = grad_low_gu[:, : 2 * RANK].astype(BF16)
    grad_normed_mlp = mlp_back + nt(grad_low_gu, in_gu)
    grad_mid = grad_out + norm_back(resid_mid, norm_gains[2], grad_normed_mlp)

    grad_attn = norm_back(attn_total, norm_gains[1], grad_mid).astype(BF16)
    seq_grad_attn = tensor_gather(grad_attn, count)
    grad_low_out = nn(seq_grad_attn, lift_out).astype(BF16)
    grad_attended = (nn(seq_grad_attn, w_out) + nt(grad_low_out, map_heads)).astype(BF16)
    grad_heads = grad_attended.reshape(LEN, heads_here, HD)
    probs = weights * inverse_total
    probs_low = probs.astype(BF16)
    grad_probs = jnp.einsum("qhd,kd->hqk", grad_heads, values, preferred_element_type=F32)
    grad_value = jnp.einsum("hqk,qhd->kd", probs_low, grad_heads, preferred_element_type=F32)
    grad_capped = probs * (grad_probs - jnp.sum(probs * grad_probs, axis=-1, keepdims=True))
    grad_raw = (grad_capped * (1.0 - squash * squash)).astype(BF16)
    grad_query = jnp.einsum("hqk,kd->qhd", grad_raw, keys, preferred_element_type=F32)
    grad_key = jnp.einsum("hqk,qhd->kd", grad_raw, queries, preferred_element_type=F32)
    grad_q_pre = rotate(grad_query * HD ** (-0.5), cosine, -sine).astype(BF16)
    grad_q_pre = grad_q_pre.reshape(LEN, head_width)
    grad_k_pre = rotate(grad_key.reshape(LEN, 1, HD), cosine, -sine).astype(BF16)
    grad_k_pre = grad_k_pre.reshape(LEN, HD)
    grad_v_pre = grad_value.astype(BF16)
    low_qkv_part = pad_lanes(
        jnp.concatenate(
            [nn(grad_q_pre, lift_q), nn(grad_k_pre, lift_k), nn(grad_v_pre, lift_v)], axis=1
        ).astype(BF16)
    )
    grad_qkv = jnp.concatenate([grad_q_pre, grad_k_pre, grad_v_pre], axis=1)
    attn_back_part = nt(grad_qkv, attn_w[:, :qkv_width]).astype(BF16)
    attn_back, grad_low_qkv = tensor_scatter(attn_back_part, low_qkv_part, count)
    grad_low_qkv = grad_low_qkv[:, : 3 * RANK].astype(BF16)
    grad_normed_attn = attn_back + nt(grad_low_qkv, in_qkv)
    input_grad = (grad_mid + norm_back(resid_in, norm_gains[0], grad_normed_attn)).astype(BF16)

    def packed(parts, blocks):
        return pad_lanes(jnp.concatenate(parts, axis=1).astype(BF16)).reshape(
            blocks, -1, LANES
        )

    d_grad = packed(
        [
            tn(normed_attn, grad_low_qkv),
            tn(normed_mlp, grad_low_gu),
            tn(grad_attn, low_out),
            tn(grad_mlp, low_down),
        ],
        lay.total,
    )
    f_grad = packed(f_parts, lay.dp)
    h_grad = packed([tn(attended, grad_low_out), tn(grad_q_pre, low_q)], lay.dp)
    k_grad = packed([tn(grad_k_pre, low_k), tn(grad_v_pre, low_v)], lay.kv_owners)
    d_all, f_all, h_all, k_all = exchange(
        grads_kernel,
        "adapter_grads",
        4,
        (d_grad, f_grad, h_grad, k_grad),
        (
            (lay.total, d_rows, LANES),
            (lay.dp, f_rows, LANES),
            (lay.dp, h_rows, LANES),
            (lay.dp * lay.share, k_rows, LANES),
        ),
        lay.dp,
        lay.total,
        lay.share,
    )

    def collect(received):
        repeats = received.shape[0] // lay.dp
        hot = jnp.repeat(group_hot, repeats, axis=0)
        return lax.dot_general(
            hot, received, (((0,), (0,)), ((), ())), preferred_element_type=F32
        )

    d_all, f_all, h_all, k_all = (collect(item) for item in (d_all, f_all, h_all, k_all))

    def lift_form(values, shape):
        return jnp.moveaxis(values, 1, 2).reshape(shape)

    return (
        layer_out,
        input_grad,
        d_all[:, :, : 5 * RANK],
        h_all[:, :, :RANK],
        f_all[:, :, :RANK],
        lift_form(h_all[:, :, RANK : 2 * RANK], lift_query.shape),
        lift_form(k_all[:, :, : 2 * RANK], lift_keyval.shape),
        lift_form(f_all[:, :, RANK : 3 * RANK], lift_gateup.shape),
        lift_form(d_all[:, :, 5 * RANK : 7 * RANK], lift_resid.shape),
    )


def solution(mesh):
    return jax.shard_map(
        per_device,
        mesh=mesh,
        in_specs=(
            P(("dp", "tensor"), None),
            P(("dp", "tensor"), None),
            P("dp"),
            P("dp", None),
            P(),
            P("dp", "tensor"),
            P("dp", None),
            P("dp", None),
            P("tensor", "dp"),
            P("dp", "tensor"),
            P("dp", "tensor"),
            P("tensor", "dp"),
            P(None, ("dp", "tensor"), None),
            P(None, ("dp", "tensor"), None),
            P(None, ("dp", "tensor"), None),
            P(None, None, ("dp", "tensor")),
            P(None, None, None, ("dp", "tensor")),
            P(None, None, None, ("dp", "tensor")),
            P(None, None, None, ("dp", "tensor")),
        ),
        out_specs=(
            P(("dp", "tensor"), None),
            P(("dp", "tensor"), None),
            P(None, ("dp", "tensor"), None),
            P(None, ("dp", "tensor"), None),
            P(None, ("dp", "tensor"), None),
            P(None, None, ("dp", "tensor")),
            P(None, None, None, ("dp", "tensor")),
            P(None, None, None, ("dp", "tensor")),
            P(None, None, None, ("dp", "tensor")),
        ),
        check_vma=False,
    )
```

```python
import functools

import jax
import jax.numpy as jnp
from jax import lax
from jax.experimental import pallas as pl
from jax.experimental.pallas import tpu as pltpu
from jax.sharding import PartitionSpec as P

D = 2304
HQ = 8
KV = 4
HD = 256
FF = 9216
NA = 8
RANK = 16
LEN = 1024
LANES = 128

EPSILON = 1e-06
SOFT_CAP = 50.0
MESH = pl.DeviceIdType.MESH
BF16 = jnp.bfloat16
F32 = jnp.float32
VMEM_LIMIT = 48 * 1024 * 1024
BLOCK = 32


def rms_norm(values, gain_row):
    return (
        values * lax.rsqrt(jnp.mean(values * values, axis=-1, keepdims=True) + EPSILON) * gain_row
    )


def norm_back(values, gain_row, gradient):
    inverse = lax.rsqrt(jnp.mean(values * values, axis=-1, keepdims=True) + EPSILON)
    scaled = gradient * gain_row
    normed = values * inverse
    return inverse * (scaled - normed * jnp.mean(scaled * normed, axis=-1, keepdims=True))


def gelu_parts(gate, up):
    scale = (2.0 / jnp.pi) ** 0.5
    square = gate * gate
    bend = jnp.tanh(scale * gate * (1.0 + 0.044715 * square))
    low = 0.5 * (1.0 + bend)
    gelu = gate * low
    slope = low + 0.5 * gate * (1.0 - bend * bend) * (scale * (1.0 + 3.0 * 0.044715 * square))
    return (gelu * up).astype(BF16), (slope * up).astype(BF16), gelu.astype(BF16)


def tables(length, size):
    half_size = size // 2
    frequency = 10000.0 ** (-2.0 * jnp.arange(half_size, dtype=F32) / size)
    angles = jnp.arange(length, dtype=F32)[:, None] * frequency[None, :]
    return (jnp.cos(angles)[:, None, :], jnp.sin(angles)[:, None, :])


def rotate(values, cosine, sine):
    half_size = values.shape[-1] // 2
    first_half = values[..., :half_size]
    second_half = values[..., half_size:]
    return jnp.concatenate(
        [first_half * cosine - second_half * sine, second_half * cosine + first_half * sine],
        axis=-1,
    )


def nn(a, b):
    return lax.dot_general(a, b, (((1,), (0,)), ((), ())), preferred_element_type=F32)


def nt(a, b):
    return lax.dot_general(a, b, (((1,), (1,)), ((), ())), preferred_element_type=F32)


def tn(a, b):
    return lax.dot_general(a, b, (((0,), (0,)), ((), ())), preferred_element_type=F32)


def pad_lanes(values):
    return jnp.pad(values, [(0, 0)] * (values.ndim - 1) + [(0, LANES - values.shape[-1])])


QUERY, KEY, VALUE, GATE, UP, OUT, DOWN = (
    slice(i * RANK, (i + 1) * RANK) for i in range(7)
)


def band(values, first, last=None):
    lane = lax.broadcasted_iota(jnp.int32, values.shape, 1)
    keep = (lane >= first.start) & (lane < (last or first).stop)
    return jnp.where(keep, values, 0.0)


def lanes(*parts):
    pieces, at = [], 0
    for place, values in parts:
        if place.start > at:
            pieces.append(jnp.zeros(values.shape[:-1] + (place.start - at,), values.dtype))
        pieces.append(values)
        at = place.start + values.shape[-1]
    last = parts[-1][1]
    pieces.append(jnp.zeros(last.shape[:-1] + (LANES - at,), last.dtype))
    return jnp.concatenate(pieces, axis=-1)


def call(peers):
    barrier = pltpu.get_barrier_semaphore()
    for peer in peers:
        pl.semaphore_signal(barrier, inc=1, device_id=peer, device_id_type=MESH)


def greet(peers):
    call(peers)
    pl.semaphore_wait(pltpu.get_barrier_semaphore(), len(peers))


def square_peers(index):
    return index + 1 - 2 * lax.rem(index, 2), lax.rem(index + 2, 4), 3 - index


def remote(source, target, send_sem, recv_sem, peer):
    return pltpu.make_async_remote_copy(
        src_ref=source,
        dst_ref=target,
        send_sem=send_sem,
        recv_sem=recv_sem,
        device_id={"tensor": peer},
        device_id_type=MESH,
    )


class PlainGather:
    def __init__(self, me, x_ref, o_ref, local_sem, send_sem, recv_sem):
        rows = x_ref.shape[0]
        half = rows // 2
        links = square_peers(me)[:2]
        self.own = pltpu.make_async_copy(x_ref, o_ref.at[pl.ds(me * rows, rows)], local_sem)
        self.first, self.second, self.onward = [], [], []
        for order, group in enumerate((self.first, self.second)):
            for link in range(2):
                part = link if order == 0 else 1 - link
                group.append(
                    remote(
                        x_ref.at[pl.ds(part * half, half)],
                        o_ref.at[pl.ds(me * rows + part * half, half)],
                        send_sem.at[link, part],
                        recv_sem.at[link, part],
                        links[link],
                    )
                )
        for link in range(2):
            block = o_ref.at[pl.ds(links[link] * rows + link * half, half)]
            self.onward.append(
                remote(block, block, send_sem.at[2, link], recv_sem.at[2, link], links[1 - link])
            )

    def start(self):
        self.own.start()
        for copy in self.first + self.second:
            copy.start()

    def forward(self):
        for copy, onward in zip(self.first, self.onward):
            copy.wait_recv()
            onward.start()

    def finish(self):
        for copy in self.second + self.onward:
            copy.wait_recv()
        self.own.wait()
        for copy in self.first + self.second + self.onward:
            copy.wait_send()


def gather_kernel(count, rows, x_ref, o_ref, local_sem, send_sem, recv_sem):
    me = lax.axis_index("tensor")
    if count == 4:
        across, down, _ = square_peers(me)
        greet([{"tensor": across}, {"tensor": down}])
        gather = PlainGather(me, x_ref, o_ref, local_sem, send_sem, recv_sem)
        gather.start()
        gather.forward()
        gather.finish()
    else:
        peers = [lax.rem(me + step, count) for step in range(1, count)]
        greet([{"tensor": peer} for peer in peers])
        own = pltpu.make_async_copy(x_ref, o_ref.at[pl.ds(me * rows, rows)], local_sem)
        own.start()
        copies = []
        for step, peer in enumerate(peers):
            copy = remote(
                x_ref,
                o_ref.at[pl.ds(me * rows, rows)],
                send_sem.at[0, step],
                recv_sem.at[0, step],
                peer,
            )
            copy.start()
            copies.append(copy)
        own.wait()
        for copy in copies:
            copy.wait()


def tensor_gather(values, count):
    rows, width = values.shape
    slots = max(2, count - 1)
    return pl.pallas_call(
        functools.partial(gather_kernel, count, rows),
        out_shape=jax.ShapeDtypeStruct((count * rows, width), values.dtype),
        in_specs=[pl.BlockSpec(memory_space=pl.ANY)],
        out_specs=pl.BlockSpec(memory_space=pl.ANY),
        scratch_shapes=[
            pltpu.SemaphoreType.DMA,
            pltpu.SemaphoreType.DMA((3, slots)),
            pltpu.SemaphoreType.DMA((3, slots)),
        ],
        compiler_params=pltpu.CompilerParams(
            collective_id=1, has_side_effects=True, vmem_limit_bytes=VMEM_LIMIT
        ),
        name="tensor_gather",
    )(values)


def scatter_kernel(count, rows, p_ref, q_ref, o_ref, l_ref, *scratch):
    me = lax.axis_index("tensor")
    payload = ((p_ref, o_ref), (q_ref, l_ref))
    if count == 4:
        across, down, far = square_peers(me)
        greet([{"tensor": across}, {"tensor": down}])
        half = rows // 2
        first = scratch[0:2]
        sums = scratch[2:4]
        second = scratch[4:6]
        send_sem, recv_sem = scratch[6], scratch[7]
        links = (across, down)
        copies = {}
        for which in (1, 0):
            for link in range(2):
                block = far if which == 1 else links[link]
                for item in range(2):
                    copy = remote(
                        payload[item][0].at[pl.ds(block * rows + link * half, half)],
                        first[item].at[link, which],
                        send_sem.at[item, link, which],
                        recv_sem.at[item, link, which],
                        links[link],
                    )
                    copy.start()
                    copies[item, link, which] = copy
        for link in range(2):
            block = links[1 - link]
            for item in range(2):
                copies[item, link, 1].wait_recv()
                mine = payload[item][0][pl.ds(block * rows + link * half, half), :]
                sums[item][link] = (
                    mine.astype(F32) + first[item][link, 1].astype(F32)
                ).astype(BF16)
                copy = remote(
                    sums[item].at[link],
                    second[item].at[link],
                    send_sem.at[item, link, 2],
                    recv_sem.at[item, link, 2],
                    links[1 - link],
                )
                copy.start()
                copies[item, link, 2] = copy
        for link in range(2):
            for item in range(2):
                copies[item, link, 0].wait_recv()
                mine = payload[item][0][pl.ds(me * rows + link * half, half), :]
                payload[item][1][pl.ds(link * half, half), :] = mine.astype(F32) + first[item][
                    link, 0
                ].astype(F32)
        for link in range(2):
            for item in range(2):
                copies[item, link, 2].wait_recv()
                payload[item][1][pl.ds(link * half, half), :] += second[item][link].astype(F32)
        for copy in copies.values():
            copy.wait_send()
    else:
        peers = [lax.rem(me + step, count) for step in range(1, count)]
        greet([{"tensor": peer} for peer in peers])
        first = scratch[0:2]
        send_sem, recv_sem = scratch[2], scratch[3]
        copies = []
        for step, peer in enumerate(peers):
            for item in range(2):
                copy = remote(
                    payload[item][0].at[pl.ds(peer * rows, rows)],
                    first[item].at[step],
                    send_sem.at[item, step],
                    recv_sem.at[item, step],
                    peer,
                )
                copy.start()
                copies.append((item, step, copy))
        for item in range(2):
            payload[item][1][...] = payload[item][0][pl.ds(me * rows, rows), :].astype(F32)
        for item, step, copy in copies:
            copy.wait()
            payload[item][1][...] += first[item][step].astype(F32)


def tensor_scatter(values, narrow, count):
    rows = values.shape[0] // count
    widths = (values.shape[1], narrow.shape[1])
    if count == 4:
        half = rows // 2
        scratch = [pltpu.VMEM((2, 2, half, width), BF16) for width in widths]
        scratch += [pltpu.VMEM((2, half, width), BF16) for width in widths]
        scratch += [pltpu.VMEM((2, half, width), BF16) for width in widths]
        scratch += [pltpu.SemaphoreType.DMA((2, 2, 3)), pltpu.SemaphoreType.DMA((2, 2, 3))]
    else:
        scratch = [pltpu.VMEM((count - 1, rows, width), BF16) for width in widths]
        scratch += [pltpu.SemaphoreType.DMA((2, count - 1))] * 2
    vmem = pl.BlockSpec(memory_space=pltpu.VMEM)
    return pl.pallas_call(
        functools.partial(scatter_kernel, count, rows),
        out_shape=tuple(jax.ShapeDtypeStruct((rows, width), F32) for width in widths),
        in_specs=[vmem, vmem],
        out_specs=(vmem, vmem),
        scratch_shapes=scratch,
        compiler_params=pltpu.CompilerParams(
            collective_id=2, has_side_effects=True, vmem_limit_bytes=VMEM_LIMIT
        ),
        name="tensor_scatter",
    )(values, narrow)


class Square:
    def __init__(self, rows):
        self.rows = rows
        self.half = rows // 2
        self.me = lax.axis_index("tensor")
        self.across, self.down, self.far = square_peers(self.me)
        self.links = (self.across, self.down)

    def greet(self, far=False):
        greet([{"tensor": peer} for peer in (self.across, self.down) + ((self.far,) if far else ())])

    def spread(self, source_at, target, send_sem, recv_sem):
        copies = [pltpu.make_async_copy(source_at(self.me), target.at[self.me], recv_sem.at[0])]
        for which, peer in enumerate((self.across, self.down, self.far)):
            copies.append(
                remote(
                    source_at(peer),
                    target.at[self.me],
                    send_sem.at[which],
                    recv_sem.at[1 + which],
                    peer,
                )
            )
        return copies


def along(source_at, target, send_sem, recv_sem):
    dp = lax.axis_size("dp")
    d = lax.axis_index("dp")
    pltpu.make_async_copy(source_at(d), target.at[d], recv_sem).start()
    copies = []
    for step in range(1, dp):
        peer = lax.rem(d + step, dp)
        copy = pltpu.make_async_remote_copy(
            src_ref=source_at(peer),
            dst_ref=target.at[d],
            send_sem=send_sem.at[step],
            recv_sem=recv_sem,
            device_id={"dp": peer},
            device_id_type=MESH,
        )
        copy.start()
        copies.append(copy)
    return copies


class ChunkGather:
    def __init__(self, sq, source, buf, send_sem, recv_sem):
        half = sq.half
        self.first, self.second, self.onward = [], [], []
        for link in range(2):
            for order in range(2):
                part = link if order == 0 else 1 - link
                copy = remote(
                    source.at[pl.ds(part * half, half)],
                    buf.at[1 + order, pl.ds(link * half, half)],
                    send_sem.at[2 * order + link],
                    recv_sem.at[2 * order + link],
                    sq.links[link],
                )
                (self.first if order == 0 else self.second).append(copy)
            self.onward.append(
                remote(
                    buf.at[1, pl.ds(link * half, half)],
                    buf.at[3, pl.ds(link * half, half)],
                    send_sem.at[4 + link],
                    recv_sem.at[4 + link],
                    sq.links[1 - link],
                )
            )

    def start(self):
        for copy in self.first + self.second:
            copy.start()

    def wait_chunk(self, chunk):
        if chunk == 1:
            for copy in self.first:
                copy.wait_recv()
            for copy in self.onward:
                copy.start()
        if chunk == 2:
            for copy in self.second:
                copy.wait_recv()
        if chunk == 3:
            for copy in self.onward:
                copy.wait_recv()

    def finish(self):
        for copy in self.first + self.second + self.onward:
            copy.wait_send()


class ChunkScatter:
    def __init__(self, sq, part, landing, passed, send_sem, recv_sem):
        self.sq, self.half = sq, landing.shape[-2]
        self.part, self.landing, self.passed = part, landing, passed
        self.send_sem, self.recv_sem = send_sem, recv_sem
        self.tiles = send_sem.shape[-1]
        self.width = part.shape[-1] // self.tiles

    def columns(self, tile):
        if self.tiles == 1:
            return pl.ds(0, self.width)
        return columns(tile, self.width)

    def copy(self, kind, link, tile):
        rows = pl.ds(link * self.half, self.half)
        cols = self.columns(tile)
        source = (
            self.passed.at[link, :, cols]
            if kind == 2
            else self.part.at[1 + 2 * kind, rows, cols]
        )
        slot = 2 * kind + link
        return remote(
            source,
            self.landing.at[slot, :, cols],
            self.send_sem.at[slot, tile],
            self.recv_sem.at[slot, tile],
            self.sq.links[1 - link if kind == 2 else link],
        )

    def send(self, kind, tile):
        for link in range(2):
            self.copy(kind, link, tile).start()

    def send_own(self):
        for tile in range(self.tiles):
            self.send(0, tile)

    def send_far(self):
        for tile in range(self.tiles):
            self.send(1, tile)

    def pass_on(self):
        for tile in range(self.tiles):
            cols = self.columns(tile)
            for link in range(2):
                self.copy(1, link, tile).wait_recv()
                rows = pl.ds((1 - link) * self.half, self.half)
                mine = self.part[2, rows, cols].astype(F32)
                self.passed[link, :, cols] = (
                    mine + self.landing[2 + link, :, cols].astype(F32)
                ).astype(BF16)
                self.copy(2, link, tile).start()

    def arrived(self):
        for kind in (0, 2):
            for tile in range(self.tiles):
                for link in range(2):
                    self.copy(kind, link, tile).wait_recv()

    def collect(self, out_ref, places=((0, 0),)):
        self.arrived()
        for link in range(2):
            rows = pl.ds(link * self.half, self.half)
            total = (
                self.part[0, rows, :].astype(F32)
                + self.landing[link].astype(F32)
                + self.landing[4 + link].astype(F32)
            )
            size = self.part.shape[-1] // len(places)
            for source, target in places:
                out_ref[rows, target : target + size] = total[:, source : source + size]

    def finish(self):
        for kind in range(3):
            for tile in range(self.tiles):
                for link in range(2):
                    self.copy(kind, link, tile).wait_send()


def scatter_scratch(rows, width, tiles=1):
    half = rows // 2
    return [
        pltpu.VMEM((4, rows, width), BF16),
        pltpu.VMEM((6, half, width), BF16),
        pltpu.VMEM((2, half, width), BF16),
        pltpu.SemaphoreType.DMA((6, tiles)),
        pltpu.SemaphoreType.DMA((6, tiles)),
    ]


def tile_of(width):
    return 768 if width % 768 == 0 else 384


def columns(step, tile, base=0):
    return pl.ds(pl.multiple_of(base + step * tile, LANES), tile)


def pack_rows(low):
    size = low.shape[0] // 8
    return jnp.concatenate(
        [
            jnp.concatenate(
                [
                    low[(4 * half + i) * size : (4 * half + i + 1) * size, GATE.start : UP.stop]
                    for i in range(4)
                ],
                axis=1,
            )
            for half in range(2)
        ],
        axis=0,
    )


def unpack_rows(packed):
    size = packed.shape[0] // 2
    width = UP.stop - GATE.start
    low = jnp.concatenate(
        [
            packed[half * size : (half + 1) * size, i * width : (i + 1) * width]
            for half in range(2)
            for i in range(4)
        ],
        axis=0,
    )
    before = jnp.zeros((low.shape[0], GATE.start), low.dtype)
    after = jnp.zeros((low.shape[0], LANES - UP.stop), low.dtype)
    return jnp.concatenate([before, low, after], axis=1)


def mlp_back_kernel(
    rows,
    g_ref,
    down_hbm,
    gu_hbm,
    slope_hbm,
    gelu_hbm,
    hidden_hbm,
    low_hbm,
    d_ref,
    f_table,
    o_ref,
    l_ref,
    f_send,
    f_ref,
    down_w,
    gu_w,
    buf,
    slope,
    gelu,
    hidden,
    low,
    grads,
    weight_sem,
    load_sem,
    own_sem,
    gather_send,
    gather_recv,
    *scratch,
):
    sq = Square(rows)
    width = hidden.shape[-1]
    model = o_ref.shape[-1]
    down_load = pltpu.make_async_copy(down_hbm, down_w, weight_sem.at[0])
    gu_load = pltpu.make_async_copy(gu_hbm, gu_w, weight_sem.at[1])
    own_load = pltpu.make_async_copy(g_ref, buf.at[0], own_sem)

    def loads(chunk):
        slot = chunk % 2
        return [
            pltpu.make_async_copy(source.at[chunk], target.at[slot], load_sem.at[slot, item])
            for item, (source, target) in enumerate(
                ((slope_hbm, slope), (gelu_hbm, gelu), (hidden_hbm, hidden), (low_hbm, low))
            )
        ]

    down_load.start()
    own_load.start()
    for copy in loads(0):
        copy.start()
    sq.greet()
    gather = ChunkGather(sq, g_ref, buf, gather_send, gather_recv)
    gather.start()
    gu_load.start()
    part, part_low = scratch[0], scratch[5]
    scatters = (ChunkScatter(sq, *scratch[:5]), ChunkScatter(sq, *scratch[5:10]))
    f_ref[...] = jnp.zeros_like(f_ref)
    own_load.wait()
    down_load.wait()

    @pl.loop(0, 4)
    def _(chunk):
        slot = lax.rem(chunk, 2)
        for step in range(4):

            @pl.when(chunk == step)
            def _(step=step):
                gather.wait_chunk(step)
                for copy in loads(step):
                    copy.wait()
                if step < 3:
                    for copy in loads(step + 1):
                        copy.start()

        incoming = buf.at[chunk]
        low_down = band(nn(incoming[...], d_ref[...]), DOWN).astype(BF16)
        tile = tile_of(width)

        @pl.loop(0, width // tile)
        def _(step):
            here = columns(step, tile)
            grad = nn(incoming[...], down_w[:, here]) + nt(low_down, f_table[here, :])
            grads[:, here] = (grad * slope[slot, :, here].astype(F32)).astype(BF16)
            grads[:, columns(step, tile, width)] = (
                grad * gelu[slot, :, here].astype(F32)
            ).astype(BF16)

        @pl.when(chunk == 0)
        def _():
            gu_load.wait()

        wide = tile_of(model)

        @pl.loop(0, model // wide)
        def _(step):
            here = columns(step, wide)
            part[chunk, :, here] = nt(grads[...], gu_w[here, :]).astype(BF16)

            @pl.when(chunk == 1)
            def _():
                scatters[0].send(0, step)

            @pl.when(chunk == 3)
            def _():
                scatters[0].send(1, step)

        part_low[chunk] = pack_rows(
            band(nn(grads[:, :width], f_table[...]), GATE)
            + band(nn(grads[:, width:], f_table[...]), UP)
        ).astype(BF16)

        @pl.when(chunk == 1)
        def _():
            scatters[1].send_own()

        @pl.when(chunk == 3)
        def _():
            scatters[1].send_far()

        low_turned = low_down.astype(F32).T.astype(BF16)
        gu_turned = low[slot].astype(F32).T.astype(BF16)
        f_ref[:RANK, :] += nn(low_turned[DOWN], hidden[slot])
        f_ref[RANK : 2 * RANK, :] += nn(gu_turned[GATE], grads[:, :width])
        f_ref[2 * RANK : 3 * RANK, :] += nn(gu_turned[UP], grads[:, width:])

    for scatter in scatters:
        scatter.pass_on()
    cores, slices = f_send.shape[:2]
    size = width // (cores * slices)
    for core in range(cores):
        for peer in range(slices):
            first = (core * slices + peer) * size
            f_send[core, peer] = f_ref[: 3 * RANK, first : first + size].astype(BF16)
    gather.finish()
    scatters[0].collect(o_ref)
    scatters[1].collect(l_ref)
    for scatter in scatters:
        scatter.finish()


def mlp_back_fused(grad, down_w, gu_w, slope, gelu, hidden, low, d_tab, f_tab, dp):
    rows, model = grad.shape
    width = hidden.shape[2]
    messages = (dp // 4, 4, 3 * RANK, width // dp)
    anywhere = pl.BlockSpec(memory_space=pl.ANY)
    vmem = pl.BlockSpec(memory_space=pltpu.VMEM)
    return pl.pallas_call(
        functools.partial(mlp_back_kernel, rows),
        out_shape=(
            jax.ShapeDtypeStruct((rows, model), F32),
            jax.ShapeDtypeStruct((rows // 4, LANES), F32),
            jax.ShapeDtypeStruct(messages, BF16),
        ),
        in_specs=[vmem] + [anywhere] * 6 + [vmem] * 2,
        out_specs=(vmem,) * 3,
        scratch_shapes=[
            pltpu.VMEM((3 * RANK, width), F32),
            pltpu.VMEM((model, width), BF16),
            pltpu.VMEM((model, 2 * width), BF16),
            pltpu.VMEM((4, rows, model), BF16),
            pltpu.VMEM((2, rows, width), BF16),
            pltpu.VMEM((2, rows, width), BF16),
            pltpu.VMEM((2, rows, width), BF16),
            pltpu.VMEM((2, rows, LANES), BF16),
            pltpu.VMEM((rows, 2 * width), BF16),
            pltpu.SemaphoreType.DMA((2,)),
            pltpu.SemaphoreType.DMA((2, 4)),
            pltpu.SemaphoreType.DMA,
            pltpu.SemaphoreType.DMA((6,)),
            pltpu.SemaphoreType.DMA((6,)),
        ]
        + scatter_scratch(rows, model, model // tile_of(model))
        + scatter_scratch(rows // 4, LANES),
        compiler_params=pltpu.CompilerParams(
            collective_id=5, has_side_effects=True, vmem_limit_bytes=62 * 1024 * 1024
        ),
        name="mlp_back",
    )(grad, down_w, gu_w, slope, gelu, hidden, low, d_tab, f_tab)


def front_kernel(
    ids_ref,
    layer_ref,
    gains_ref,
    gate_up_all,
    hidden_all,
    in_all,
    resid_all,
    heads_all,
    query_all,
    key_value_all,
    query_hbm,
    key_hbm,
    value_hbm,
    output_hbm,
    gate_hbm,
    up_hbm,
    seq_out,
    ids_out,
    d_out,
    f_out,
    h_out,
    k_out,
    weight_out,
    gate_up_out,
    normed,
    shard_pack,
    gate_up_pack,
    ids_own,
    ids_land,
    f_pick,
    d_pick,
    hk_pick,
    f_mid,
    d_mid,
    hk_mid,
    d_join,
    f_land,
    d_land,
    hk_land,
    d_flip,
    f_flip,
    h_flip,
    k_flip,
    local_sem,
    gather_send,
    gather_recv,
    line_send,
    line_recv,
    group_send,
    group_recv,
    shard_sem,
    shard_send,
    shard_recv,
):
    rows = layer_ref.shape[0]
    sq = Square(rows)
    dp = lax.axis_size("dp")
    d = lax.axis_index("dp")
    peers = [{"tensor": peer} for peer in (sq.across, sq.down, sq.far)]
    peers += [{"dp": lax.rem(d + step, dp)} for step in range(1, dp)]
    call(peers)
    shards = Line(weight_out, shard_send, shard_recv)
    q_width, width = query_hbm.shape[1], gate_hbm.shape[1]
    kv_first = pl.multiple_of(sq.me * (q_width // HD) // (HQ // KV) * HD, HD)
    packs = [
        pltpu.make_async_copy(source, target, shard_sem.at[which])
        for which, (source, target) in enumerate(
            (
                (query_hbm, shard_pack.at[:, pl.ds(0, q_width)]),
                (key_hbm.at[:, pl.ds(kv_first, HD)], shard_pack.at[:, pl.ds(q_width, HD)]),
                (
                    value_hbm.at[:, pl.ds(kv_first, HD)],
                    shard_pack.at[:, pl.ds(q_width + HD, HD)],
                ),
                (output_hbm, shard_pack.at[:, pl.ds(q_width + 2 * HD, q_width)]),
                (gate_hbm, gate_up_pack.at[:, pl.ds(0, width)]),
                (up_hbm, gate_up_pack.at[:, pl.ds(width, width)]),
            )
        )
    ]
    for copy in packs:
        copy.start()
    keep_shard = pltpu.make_async_copy(shard_pack, weight_out.at[d], shard_sem.at[6])
    keep_gate_up = pltpu.make_async_copy(gate_up_pack, gate_up_out, shard_sem.at[7])
    ids_own[...] = jnp.full(ids_own.shape, ids_ref[0, 0], jnp.int32)
    for copy in packs[:4]:
        copy.wait()
    keep_shard.start()

    @pl.loop(0, rows // BLOCK)
    def _(step):
        here = pl.ds(pl.multiple_of(step * BLOCK, BLOCK), BLOCK)
        normed[here, :] = rms_norm(layer_ref[here, :].astype(F32), gains_ref[0:1, :]).astype(BF16)

    pl.semaphore_wait(pltpu.get_barrier_semaphore(), len(peers))
    keep_shard.wait()
    shards.start()
    line = along(lambda k: ids_own, ids_land, line_send.at[0], line_recv.at[0])
    for copy in packs[4:]:
        copy.wait()
    keep_gate_up.start()
    gather = PlainGather(sq.me, normed, seq_out, local_sem, gather_send, gather_recv)
    gather.start()
    pltpu.make_async_copy(ids_land, ids_land, line_recv.at[0]).wait()
    ids_out[...] = ids_land[...]

    def pick(source, group):
        total = None
        for adapter in range(NA):
            hit = jnp.broadcast_to(ids_land[group, 0:1, 0:1], source.shape[1:]) == adapter
            mine = jnp.where(hit, source[adapter].astype(F32), 0.0)
            total = mine if total is None else total + mine
        return total

    @pl.loop(0, dp)
    def _(group):
        f_pick[group, : 2 * RANK, :] = pick(gate_up_all, group).astype(BF16)
        f_pick[group, 2 * RANK :, :] = pick(hidden_all, group).astype(BF16)
        d_pick[group, : UP.stop, :] = pick(in_all, group).T.astype(BF16)
        d_pick[group, UP.stop :, :] = pick(resid_all, group).astype(BF16)
        hk_pick[group, :RANK, :] = pick(heads_all, group).astype(BF16)
        hk_pick[group, RANK : 2 * RANK, :] = pick(query_all, group).astype(BF16)
        hk_pick[group, 2 * RANK :, : key_value_all.shape[2]] = pick(key_value_all, group).astype(
            BF16
        )

    lands = (f_mid, d_mid, hk_mid)
    for item, (source, target) in enumerate(zip((f_pick, d_pick, hk_pick), lands)):
        line += along(
            lambda k, source=source: source.at[k],
            target,
            line_send.at[1 + item],
            line_recv.at[1 + item],
        )
    shards.arrive(1, 0)
    gather.forward()
    for flip in (d_flip, f_flip, h_flip, k_flip):
        flip[...] = jnp.zeros_like(flip)
    for item, target in enumerate(lands):
        pltpu.make_async_copy(target, target, line_recv.at[1 + item]).wait()
    shards.arrive(1, 1)
    size = d_mid.shape[2]
    for k in range(dp):
        d_join[:, k * size : (k + 1) * size] = d_mid[k]
    per_user = dp // 4
    spread = [
        sq.spread(lambda peer: d_join, d_land, group_send.at[0], group_recv.at[0]),
        sq.spread(
            lambda peer: f_mid.at[pl.ds(peer * per_user, per_user)],
            f_land,
            group_send.at[1],
            group_recv.at[1],
        ),
        sq.spread(
            lambda peer: hk_mid.at[pl.ds(peer * per_user, per_user)],
            hk_land,
            group_send.at[2],
            group_recv.at[2],
        ),
    ]
    for copies in spread:
        for copy in copies:
            copy.start()
    shards.arrive(2, 0)
    for copies in spread:
        copies[0].wait()
        for copy in copies[1:]:
            copy.wait_recv()
    shards.arrive(2, 1)
    f_size, h_size, k_size = f_mid.shape[2], h_out.shape[0] // dp, k_out.shape[0] // dp
    for t in range(4):
        for k in range(dp):
            at = (k * 4 + t) * size
            d_flip[: DOWN.stop, at : at + size] = d_land[
                t, :, k * size : (k + 1) * size
            ].astype(F32)
        for core in range(per_user):
            at = (core * 4 + t) * f_size
            piece = f_land[t, core].astype(F32)
            f_flip[GATE.start : UP.stop, at : at + f_size] = piece[: 2 * RANK]
            f_flip[DOWN, at : at + f_size] = piece[2 * RANK :]
            piece = hk_land[t, core].astype(F32)
            at = (core * 4 + t) * h_size
            h_flip[OUT, at : at + h_size] = piece[:RANK, :h_size]
            h_flip[QUERY, at : at + h_size] = piece[RANK : 2 * RANK, :h_size]
            at = (core * 4 + t) * k_size
            k_flip[KEY.start : VALUE.stop, at : at + k_size] = piece[2 * RANK :, :k_size]
    for flip, out in ((d_flip, d_out), (f_flip, f_out), (h_flip, h_out), (k_flip, k_out)):

        @pl.loop(0, out.shape[0] // LANES)
        def _(step, flip=flip, out=out):
            here = columns(step, LANES)
            out[here, :] = flip[:, here].T.astype(BF16)

    shards.arrive(3, 0)
    gather.finish()
    shards.arrive(3, 1)
    for place in range(dp // 2):
        for part in range(2):
            shards.wait_sibling(place, part)
    shards.finish()
    keep_gate_up.wait()
    for copies in spread:
        for copy in copies[1:]:
            copy.wait_send()
    for copy in line:
        copy.wait_send()


def front(ids, layer_in, gains, adapters, weights, dp, widths):
    rows, model = layer_in.shape
    anywhere = pl.BlockSpec(memory_space=pl.ANY)
    vmem = pl.BlockSpec(memory_space=pltpu.VMEM)
    gate_up_all, hidden_all, in_all, resid_all, heads_all, query_all, key_value_all = adapters
    tile = (8, LANES)
    shapes = [
        (dp, gate_up_all.shape[1] + RANK, gate_up_all.shape[2]),
        (dp, in_all.shape[2] + resid_all.shape[1], in_all.shape[1]),
        (dp, 2 * RANK + key_value_all.shape[1], query_all.shape[2]),
    ]
    query, key, value, output, gate, up = weights
    shard = (query.shape[0], 2 * query.shape[1] + 2 * HD)
    gate_up = (gate.shape[0], 2 * gate.shape[1])
    joined = (shapes[1][1], dp * shapes[1][2])
    return pl.pallas_call(
        front_kernel,
        out_shape=(
            jax.ShapeDtypeStruct((4 * rows, model), BF16),
            jax.ShapeDtypeStruct((dp,) + tile, jnp.int32),
        )
        + tuple(jax.ShapeDtypeStruct((width, LANES), BF16) for width in widths)
        + (
            jax.ShapeDtypeStruct((dp,) + shard, BF16),
            jax.ShapeDtypeStruct(gate_up, BF16),
        ),
        in_specs=[pl.BlockSpec(memory_space=pltpu.SMEM)] + [vmem] * 9 + [anywhere] * 6,
        out_specs=(anywhere,) + (vmem,) * 5 + (anywhere,) * 2,
        scratch_shapes=[
            pltpu.VMEM((rows, model), BF16),
            pltpu.VMEM(shard, BF16),
            pltpu.VMEM(gate_up, BF16),
            pltpu.VMEM(tile, jnp.int32),
            pltpu.VMEM((dp,) + tile, jnp.int32),
        ]
        + [pltpu.VMEM(shape, BF16) for shape in shapes] * 2
        + [
            pltpu.VMEM(joined, BF16),
            pltpu.VMEM((4, dp // 4) + shapes[0][1:], BF16),
            pltpu.VMEM((4,) + joined, BF16),
            pltpu.VMEM((4, dp // 4) + shapes[2][1:], BF16),
        ]
        + [pltpu.VMEM((LANES, width), F32) for width in widths]
        + [
            pltpu.SemaphoreType.DMA,
            pltpu.SemaphoreType.DMA((3, 2)),
            pltpu.SemaphoreType.DMA((3, 2)),
            pltpu.SemaphoreType.DMA((4, dp)),
            pltpu.SemaphoreType.DMA((4,)),
            pltpu.SemaphoreType.DMA((3, 3)),
            pltpu.SemaphoreType.DMA((3, 4)),
            pltpu.SemaphoreType.DMA((8,)),
            pltpu.SemaphoreType.DMA((3, dp // 2, 2)),
            pltpu.SemaphoreType.DMA((dp, 2)),
        ],
        compiler_params=pltpu.CompilerParams(
            collective_id=9, has_side_effects=True, vmem_limit_bytes=62 * 1024 * 1024
        ),
        name="front",
    )(ids, layer_in, gains, *adapters, *weights)


class Line:
    def __init__(self, slots, send_sem, recv_sem):
        self.d = lax.axis_index("dp")
        self.places = lax.axis_size("dp") // 2
        self.core = lax.rem(self.d, 2)
        self.z = self.d // 2
        self.sibling = self.d + 1 - 2 * self.core
        self.slots, self.send_sem, self.recv_sem = slots, send_sem, recv_sem

    def greet(self, others):
        barrier = pltpu.get_barrier_semaphore()
        for peer in others + [{"dp": self.sibling}]:
            pl.semaphore_signal(barrier, inc=1, device_id=peer, device_id_type=MESH)

        @pl.when(self.z > 0)
        def _():
            pl.semaphore_signal(
                barrier, inc=1, device_id={"dp": self.d - 2}, device_id_type=MESH
            )

        @pl.when(self.z < self.places - 1)
        def _():
            pl.semaphore_signal(
                barrier, inc=1, device_id={"dp": self.d + 2}, device_id_type=MESH
            )

        last = self.places - 1
        ends = (last - self.z) // last + self.z // last
        pl.semaphore_wait(barrier, len(others) + 3 - ends)

    def copy(self, place, kind, part):
        target = (self.d + 2, self.d - 2, self.sibling)[kind]
        slot = 2 * place + self.core
        half = self.slots.shape[1] // 2
        block = self.slots.at[slot, pl.ds(part * half, half)]
        return pltpu.make_async_remote_copy(
            src_ref=block,
            dst_ref=block,
            send_sem=self.send_sem.at[kind, place, part],
            recv_sem=self.recv_sem.at[slot, part],
            device_id={"dp": target},
            device_id_type=MESH,
        )

    def send_up(self, place, part):
        @pl.when(self.z < self.places - 1)
        def _():
            self.copy(place, 0, part).start()

    def send_down(self, place, part):
        @pl.when(self.z > 0)
        def _():
            self.copy(place, 1, part).start()

    def start(self):
        for part in range(2):
            self.send_up(self.z, part)
            self.send_down(self.z, part)
            self.copy(self.z, 2, part).start()

    def arrive(self, distance, part):
        @pl.when(self.z >= distance)
        def _():
            place = self.z - distance
            self.copy(place, 2, part).wait_recv()
            self.send_up(place, part)
            self.copy(place, 2, part).start()

        @pl.when(self.z + distance < self.places)
        def _():
            place = self.z + distance
            self.copy(place, 2, part).wait_recv()
            self.send_down(place, part)
            self.copy(place, 2, part).start()

    def wait_sibling(self, place, part):
        half = self.slots.shape[1] // 2
        other = 2 * place + 1 - self.core
        block = self.slots.at[other, pl.ds(part * half, half)]
        pltpu.make_async_copy(block, block, self.recv_sem.at[other, part]).wait()

    def finish(self):
        for place in range(self.places):
            for part in range(2):

                @pl.when((self.z >= place) & (self.z < self.places - 1))
                def _(place=place, part=part):
                    self.copy(place, 0, part).wait_send()

                @pl.when((self.z <= place) & (self.z > 0))
                def _(place=place, part=part):
                    self.copy(place, 1, part).wait_send()

                self.copy(place, 2, part).wait_send()


class HalfSpread:
    def __init__(self, sq, line, weight, columns_from, target, send_sem, recv_sem):
        model, width = target.shape[1:]
        share, part_rows = model // 2, model // 4
        cols = pl.ds(columns_from, width)

        def rows(part):
            return pl.ds(pl.multiple_of(line.core * share + part * part_rows, 8), part_rows)

        self.first, self.second, self.onward, self.sibling = [], [], [], []
        for order, group in enumerate((self.first, self.second)):
            for link in range(2):
                part = link if order == 0 else 1 - link
                sem = 2 * order + link
                group.append(
                    remote(
                        weight.at[rows(part), cols],
                        target.at[sq.me, rows(part)],
                        send_sem.at[sem],
                        recv_sem.at[sem],
                        sq.links[link],
                    )
                )
        for link in range(2):
            block = target.at[sq.links[link], rows(link)]
            self.onward.append(
                remote(
                    block, block, send_sem.at[4 + link], recv_sem.at[4 + link], sq.links[1 - link]
                )
            )
        mine = pl.ds(pl.multiple_of(line.core * share, 8), share)
        for which, peer in enumerate((sq.across, sq.down, sq.far)):
            block = target.at[peer, mine]
            self.sibling.append(
                pltpu.make_async_remote_copy(
                    src_ref=block,
                    dst_ref=block,
                    send_sem=send_sem.at[6 + which],
                    recv_sem=recv_sem.at[6 + which],
                    device_id={"dp": line.sibling},
                    device_id_type=MESH,
                )
            )

    def start(self):
        for copy in self.first + self.second:
            copy.start()

    def forward(self):
        for copy, onward in zip(self.first, self.onward):
            copy.wait_recv()
            onward.start()

    def share(self):
        for copy in self.second + self.onward:
            copy.wait_recv()
        for copy in self.sibling:
            copy.start()

    def finish(self):
        for copy in self.first + self.second + self.onward:
            copy.wait_send()
        for copy in self.sibling:
            copy.wait()


ARRIVALS = ((0, 1, 2, 3), (1, 0, 2, 3), (2, 1, 3, 0), (3, 2, 1, 0))


def mlp_kernel(
    rows,
    length_ref,
    x_hbm,
    gu_hbm,
    shard_hbm,
    weight_hbm,
    d_ref,
    f_table,
    resid_ref,
    cot_ref,
    gains_ref,
    layer_ref,
    grad_ref,
    low_ref,
    low_down_ref,
    hidden_out,
    slope_out,
    gelu_out,
    down_out,
    w_kv_all,
    work,
    low_sum,
    lows,
    seq,
    tiles,
    hidden,
    slope,
    gelu,
    down,
    load_sem,
    tile_sem,
    store_sem,
    keep_sem,
    line_send,
    line_recv,
    part,
    landing,
    passed,
    part_send,
    part_recv,
    w_send,
    w_recv,
    *low_scratch,
):
    sq = Square(rows)
    line = Line(down, line_send, line_recv)
    width = hidden.shape[-1]
    tile = tiles.shape[-1] // 2
    steps = width // tile
    own_shard = pltpu.make_async_copy(shard_hbm, down.at[line.d], load_sem.at[0])
    seq_load = pltpu.make_async_copy(x_hbm, seq, load_sem.at[1])

    def tile_loads(step, slot):
        return [
            pltpu.make_async_copy(
                gu_hbm.at[:, columns(step, tile, which * width)],
                tiles.at[slot, :, pl.ds(which * tile, tile)],
                tile_sem.at[slot, which],
            )
            for which in range(2)
        ]

    def stores(step, slot):
        here = columns(step, tile)
        return [
            pltpu.make_async_copy(
                source.at[slot], target.at[:, :, here], store_sem.at[slot, which]
            )
            for which, (source, target) in enumerate(((slope, slope_out), (gelu, gelu_out)))
        ]

    own_shard.start()
    seq_load.start()
    for copy in tile_loads(0, 0):
        copy.start()
    line.greet([{"tensor": sq.across}, {"tensor": sq.down}])
    own_shard.wait()
    line.start()
    keys_from = (weight_hbm.shape[1] - w_kv_all.shape[2]) // 2
    spread = HalfSpread(sq, line, weight_hbm, keys_from, w_kv_all, w_send, w_recv)
    spread.start()
    seq_load.wait()

    @pl.loop(0, 4)
    def _(chunk):
        low = nn(seq[chunk], d_ref[...])
        lows[0, chunk] = band(low, GATE).astype(BF16)
        lows[1, chunk] = band(low, UP).astype(BF16)
        low_ref[chunk] = band(low, GATE, UP).astype(BF16)

    @pl.loop(0, steps)
    def _(step):
        slot = lax.rem(step, 2)
        for copy in tile_loads(step, slot):
            copy.wait()

        @pl.when(step + 1 < steps)
        def _():
            for copy in tile_loads(step + 1, 1 - slot):
                copy.start()

        @pl.when(step >= 2)
        def _():
            for copy in stores(step - 2, slot):
                copy.wait()

        here = columns(step, tile)

        @pl.loop(0, 4)
        def _(chunk):
            both = nn(seq[chunk], tiles[slot])
            gate = both[:, :tile] + nt(lows[0, chunk], f_table[here, :])
            up = both[:, tile:] + nt(lows[1, chunk], f_table[here, :])
            hidden[chunk, :, here], slope[slot, chunk], gelu[slot, chunk] = gelu_parts(gate, up)

        for copy in stores(step, slot):
            copy.start()

        for part_at, part_of in ((steps // 2 - 1, 0), (steps - 2, 1)):

            @pl.when(step == part_at)
            def _(part_of=part_of):
                line.arrive(1, part_of)
                if part_of == 0:
                    spread.forward()

    keep_hidden = pltpu.make_async_copy(hidden, hidden_out, keep_sem.at[0])
    keep_hidden.start()
    last = line.places - 1
    is_first, is_last = (last - line.z) // last, line.z // last
    is_third = line.z // 2 - is_last
    is_here = (is_first, 1 - is_first - is_third - is_last, is_third, is_last)
    order = [sum(flag * ARRIVALS[z][i] for z, flag in enumerate(is_here)) for i in range(4)]

    def scatter_at(place, half):
        at = 2 * place + half
        return ChunkScatter(
            sq, part.at[at], landing.at[at], passed.at[at], part_send.at[at], part_recv.at[at]
        )

    low_scatter = ChunkScatter(sq, *low_scratch)

    @pl.loop(0, 4)
    def _(chunk):
        low_scratch[0][chunk] = band(nn(hidden[chunk], f_table[...]), DOWN).astype(BF16)

    low_scatter.send_far()
    low_scatter.send_own()
    keeps = []
    earlier = low_scatter
    half_rows = down.shape[1] // 2
    arrivals = {(1, 0): ((2, 0),), (2, 0): ((2, 1),), (3, 0): ((3, 0),), (3, 1): ((3, 1),)}
    for turn in range(4):
        place = order[turn]
        for half in range(2):
            for distance, piece in arrivals.get((turn, half), ()):
                line.arrive(distance, piece)
            if (turn, half) == (1, 0):
                spread.share()
            line.wait_sibling(place, half)
            scatter = scatter_at(place, half)

            @pl.loop(0, 4)
            def _(step, place=place, half=half, scatter=scatter):
                chunk = far_first(step)
                for core in range(2):
                    part[
                        2 * place + half, chunk, :, core * half_rows : (core + 1) * half_rows
                    ] = nt(
                        hidden[chunk],
                        down[2 * place + core, half * half_rows : (half + 1) * half_rows],
                    ).astype(BF16)

                @pl.when(step == 0)
                def _():
                    scatter.send_far()

                @pl.when(step == 1)
                def _():
                    scatter.send_own()

            earlier.pass_on()
            earlier = scatter
        pair = pl.ds(2 * place, 2)
        keep = pltpu.make_async_copy(down.at[pair], down_out.at[pair], keep_sem.at[1 + turn])
        keep.start()
        keeps.append(keep)
    low_scatter.collect(low_sum)
    low_down_ref[...] = low_sum[...].astype(BF16)
    earlier.pass_on()
    everything = [(place, half) for place in range(4) for half in range(2)]
    for place, half in everything:
        first = 2 * place * down.shape[1] + half * half_rows
        scatter_at(place, half).collect(
            work, ((0, first), (half_rows, first + down.shape[1]))
        )
    add_lifted(work, low_down_ref, d_ref)

    @pl.loop(0, rows // BLOCK)
    def _(step):
        here = pl.ds(pl.multiple_of(step * BLOCK, BLOCK), BLOCK)
        at = sq.me * rows + step * BLOCK + lax.broadcasted_iota(jnp.int32, (BLOCK, 1), 0)
        valid = (at < length_ref[0]).astype(F32)
        total = work[here, :]
        gain = gains_ref[3:4, :]
        layer_ref[here, :] = (valid * (resid_ref[here, :] + rms_norm(total, gain))).astype(BF16)
        grad_ref[here, :] = norm_back(total, gain, cot_ref[here, :].astype(F32) * valid).astype(
            BF16
        )

    for place, half in everything:
        scatter_at(place, half).finish()
    low_scatter.finish()
    line.finish()
    spread.finish()
    for step in (steps - 2, steps - 1):
        for copy in stores(step, step % 2):
            copy.wait()
    keep_hidden.wait()
    for keep in keeps:
        keep.wait()


def add_lifted(work, low, table):
    wide = tile_of(work.shape[1])

    @pl.loop(0, work.shape[1] // wide)
    def _(step):
        here = columns(step, wide)
        work[:, here] += nt(low[...], table[here, :])


def mlp_fused(lengths, seq, gu_w, shard, attn_w, d_tab, f_tab, resid, cotangent, gains, dp):
    chunks, rows, model = seq.shape
    width = shard.shape[1]
    tile = 384
    wide = model // dp
    half = rows // 2
    anywhere = pl.BlockSpec(memory_space=pl.ANY)
    vmem = pl.BlockSpec(memory_space=pltpu.VMEM)
    saved = jax.ShapeDtypeStruct((4, rows, width), BF16)
    return pl.pallas_call(
        functools.partial(mlp_kernel, rows),
        out_shape=(
            jax.ShapeDtypeStruct((rows, model), BF16),
            jax.ShapeDtypeStruct((rows, model), BF16),
            jax.ShapeDtypeStruct((4, rows, LANES), BF16),
            jax.ShapeDtypeStruct((rows, LANES), BF16),
            saved,
            saved,
            saved,
            jax.ShapeDtypeStruct((dp,) + shard.shape, BF16),
            jax.ShapeDtypeStruct((4, model, 2 * HD), BF16),
        ),
        in_specs=[pl.BlockSpec(memory_space=pltpu.SMEM)] + [anywhere] * 4 + [vmem] * 5,
        out_specs=(vmem,) * 4 + (anywhere,) * 5,
        scratch_shapes=[
            pltpu.VMEM((rows, model), F32),
            pltpu.VMEM((rows, LANES), F32),
            pltpu.VMEM((2, 4, rows, LANES), BF16),
            pltpu.VMEM((4, rows, model), BF16),
            pltpu.VMEM((2, model, 2 * tile), BF16),
            pltpu.VMEM((4, rows, width), BF16),
            pltpu.VMEM((2, 4, rows, tile), BF16),
            pltpu.VMEM((2, 4, rows, tile), BF16),
            pltpu.VMEM((dp,) + shard.shape, BF16),
            pltpu.SemaphoreType.DMA((2,)),
            pltpu.SemaphoreType.DMA((2, 2)),
            pltpu.SemaphoreType.DMA((2, 2)),
            pltpu.SemaphoreType.DMA((5,)),
            pltpu.SemaphoreType.DMA((3, dp // 2, 2)),
            pltpu.SemaphoreType.DMA((dp, 2)),
            pltpu.VMEM((dp, 4, rows, wide), BF16),
            pltpu.VMEM((dp, 6, half, wide), BF16),
            pltpu.VMEM((dp, 2, half, wide), BF16),
            pltpu.SemaphoreType.DMA((dp, 6, 1)),
            pltpu.SemaphoreType.DMA((dp, 6, 1)),
            pltpu.SemaphoreType.DMA((9,)),
            pltpu.SemaphoreType.DMA((9,)),
        ]
        + scatter_scratch(rows, LANES),
        compiler_params=pltpu.CompilerParams(
            collective_id=7, has_side_effects=True, vmem_limit_bytes=62 * 1024 * 1024
        ),
        name="mlp",
    )(lengths, seq, gu_w, shard, attn_w, d_tab, f_tab, resid, cotangent, gains)


class Layout:
    def __init__(self):
        self.dp = lax.axis_size("dp")
        self.tensor = lax.axis_size("tensor")
        self.total = self.dp * self.tensor
        self.d = lax.axis_index("dp")
        self.t = lax.axis_index("tensor")
        self.me = self.d * self.tensor + self.t
        self.heads_here = HQ // self.tensor
        self.ratio = HQ // KV
        self.share = max(1, self.tensor // KV)
        self.kv_owners = self.total // KV
        self.kv_head = self.t * self.heads_here // self.ratio
        self.user = self.me // self.dp
        self.kv_slice_head = self.me // self.kv_owners

    def device(self, flat):
        return {"dp": flat // self.tensor, "tensor": lax.rem(flat, self.tensor)}


def greet_all(lay):
    barrier = pltpu.get_barrier_semaphore()

    def signal(step, unused):
        peer = lax.rem(lay.me + step, lay.total)
        pl.semaphore_signal(
            barrier, inc=1, device_id=lay.device(peer), device_id_type=MESH
        )
        return unused

    lax.fori_loop(1, lay.total, signal, 0)
    pl.semaphore_wait(barrier, lay.total - 1)


def send_or_keep(lay, sends, source, target, send_sem, recv_sem, flat, maybe_own):
    def far():
        return pltpu.make_async_remote_copy(
            src_ref=source,
            dst_ref=target,
            send_sem=send_sem,
            recv_sem=recv_sem,
            device_id=lay.device(flat),
            device_id_type=MESH,
        )

    if maybe_own is None:
        copy = far()
        copy.start()
        sends.append((None, copy))
        return

    @pl.when(maybe_own)
    def _():
        pltpu.make_async_copy(source, target, recv_sem).start()

    @pl.when(jnp.logical_not(maybe_own))
    def _():
        far().start()

    sends.append((maybe_own, far()))


def finish(sends, received):
    for own, copy in sends:
        if own is None:
            copy.wait_send()
        else:

            @pl.when(jnp.logical_not(own))
            def _(copy=copy):
                copy.wait_send()

    for target, sem in received:
        pltpu.make_async_copy(target, target, sem).wait()


def tables_kernel(d_ref, f_ref, h_ref, k_ref, do_ref, fo_ref, ho_ref, ko_ref, *sems):
    lay = Layout()
    send_sems, recv_sem = sems[:4], sems[4]
    greet_all(lay)
    sends = []
    for step in range(lay.dp):
        group = lax.rem(lay.d + step, lay.dp)
        flat = group * lay.tensor + lay.user
        own = (lay.user == lay.t) if step == 0 else None
        for item, (source, target) in enumerate(((f_ref, fo_ref), (h_ref, ho_ref))):
            send_or_keep(
                lay,
                sends,
                source.at[group],
                target.at[lax.rem(lay.me, lay.dp)],
                send_sems[item].at[step],
                recv_sem.at[item],
                flat,
                own,
            )
        for extra in range(lay.share):
            user = lay.kv_slice_head * lay.share + extra
            flat = group * lay.tensor + user
            send_or_keep(
                lay,
                sends,
                k_ref.at[group],
                ko_ref.at[lax.rem(lay.me, lay.kv_owners)],
                send_sems[2].at[step, extra],
                recv_sem.at[2],
                flat,
                (user == lay.t) if step == 0 else None,
            )
    pltpu.make_async_copy(d_ref.at[lay.d], do_ref.at[lay.me], recv_sem.at[3]).start()
    for step in range(1, lay.total):
        flat = lax.rem(lay.me + step, lay.total)
        send_or_keep(
            lay,
            sends,
            d_ref.at[flat // lay.tensor],
            do_ref.at[lay.me],
            send_sems[3].at[step],
            recv_sem.at[3],
            flat,
            None,
        )
    finish(
        sends,
        (
            (fo_ref, recv_sem.at[0]),
            (ho_ref, recv_sem.at[1]),
            (ko_ref, recv_sem.at[2]),
            (do_ref, recv_sem.at[3]),
        ),
    )


def grads_kernel(d_ref, f_ref, h_ref, k_ref, do_ref, fo_ref, ho_ref, ko_ref, *sems):
    lay = Layout()
    send_sems, recv_sem = sems[:4], sems[4]
    greet_all(lay)
    sends = []
    for step in range(lay.dp):
        slot = lax.rem(lay.d + step, lay.dp)
        flat = lay.t * lay.dp + slot
        for item, (source, target) in enumerate(((f_ref, fo_ref), (h_ref, ho_ref))):
            send_or_keep(
                lay,
                sends,
                source.at[slot],
                target.at[lay.d],
                send_sems[item].at[step],
                recv_sem.at[item],
                flat,
                flat == lay.me,
            )
    for step in range(lay.kv_owners):
        slot = lax.rem(lay.d + step, lay.kv_owners)
        flat = lay.kv_head * lay.kv_owners + slot
        send_or_keep(
            lay,
            sends,
            k_ref.at[slot],
            ko_ref.at[lay.d * lay.share + lax.rem(lay.t, lay.share)],
            send_sems[2].at[step // lay.share, step % lay.share],
            recv_sem.at[2],
            flat,
            flat == lay.me,
        )
    pltpu.make_async_copy(d_ref.at[lay.me], do_ref.at[lay.me], recv_sem.at[3]).start()
    for step in range(1, lay.total):
        flat = lax.rem(lay.me + step, lay.total)
        send_or_keep(
            lay,
            sends,
            d_ref.at[flat],
            do_ref.at[lay.me],
            send_sems[3].at[step],
            recv_sem.at[3],
            flat,
            None,
        )
    finish(
        sends,
        (
            (fo_ref, recv_sem.at[0]),
            (ho_ref, recv_sem.at[1]),
            (ko_ref, recv_sem.at[2]),
            (do_ref, recv_sem.at[3]),
        ),
    )


def exchange(kernel, name, number, arrays, outs, dp, total, share):
    anywhere = pl.BlockSpec(memory_space=pl.ANY)
    return pl.pallas_call(
        kernel,
        out_shape=tuple(jax.ShapeDtypeStruct(shape, BF16) for shape in outs),
        in_specs=[anywhere] * 4,
        out_specs=(anywhere,) * 4,
        scratch_shapes=[
            pltpu.SemaphoreType.DMA((dp,)),
            pltpu.SemaphoreType.DMA((dp,)),
            pltpu.SemaphoreType.DMA((dp, share)),
            pltpu.SemaphoreType.DMA((total,)),
            pltpu.SemaphoreType.DMA((4,)),
        ],
        compiler_params=pltpu.CompilerParams(
            collective_id=number, has_side_effects=True, vmem_limit_bytes=VMEM_LIMIT
        ),
        name=name,
    )(*arrays)


def chunk_start(sq, chunk, part):
    is_own = (3 - chunk) // 3
    is_far = chunk // 3
    near = 1 - is_own - is_far
    neighbour = sq.down if part == 1 else sq.across
    block = sq.me * is_own + sq.far * is_far + neighbour * near
    other_half = chunk // 2 - is_far
    half = 1 - other_half if part == 1 else other_half
    return pl.multiple_of(block * sq.rows + half * sq.half, sq.half)


def rotate_back(values, cosine, sine):
    first, second = values[:, : HD // 2], values[:, HD // 2 :]
    return jnp.concatenate([first * cosine + second * sine, second * cosine - first * sine], axis=1)


def turned(values):
    return values.astype(F32).T.astype(BF16)


def rotate_rows(values, cosine, sine):
    first, second = values[:, : HD // 2], values[:, HD // 2 :]
    return jnp.concatenate([first * cosine - second * sine, second * cosine + first * sine], axis=1)


def softmax_weights(keys, queries, start, half, length):
    shape = (keys.shape[0], queries.shape[0])
    key_at = lax.broadcasted_iota(jnp.int32, shape, 0)
    query_at = lax.rem(lax.broadcasted_iota(jnp.int32, shape, 1), half) + start
    allowed = (key_at <= query_at) & (key_at < length)
    squash = jnp.tanh(nt(keys, queries) * (1.0 / SOFT_CAP))
    return squash, jnp.where(allowed, jnp.exp(SOFT_CAP * squash), 0.0)


def stack_heads(ref, here, heads):
    return jnp.concatenate([ref[here, h * HD : (h + 1) * HD] for h in range(heads)], axis=0)


def far_first(step):
    return step + 3 * ((3 - step) // 3) - 3 * (step // 3)


def attn_kernel(
    rows,
    length_ref,
    seq_hbm,
    weight_hbm,
    d_table,
    h_table,
    k_table,
    cos_ref,
    sin_ref,
    layer_ref,
    gains_ref,
    q_ref,
    k_ref,
    kt_ref,
    v_ref,
    attended_ref,
    inverse_ref,
    low_ref,
    low_out_ref,
    total_ref,
    resid_ref,
    normed_ref,
    mlp_out,
    w_out_all,
    w_q_all,
    h_all,
    seq,
    weight,
    vt,
    low_sum,
    load_sem,
    own_sem,
    gather_send,
    gather_recv,
    h_send,
    h_recv,
    w_send,
    w_recv,
    *scratch,
):
    sq = Square(rows)
    half = sq.half
    model = total_ref.shape[-1]
    q_width = q_ref.shape[1]
    qkv_width = q_width + 2 * HD
    heads = q_width // HD
    wide = tile_of(model)
    weight_load = pltpu.make_async_copy(weight_hbm, weight, load_sem.at[0])
    seq_load = pltpu.make_async_copy(seq_hbm, seq, load_sem.at[1])
    weight_load.start()
    seq_load.start()
    line = Line(None, None, None)
    greet(
        [{"tensor": peer} for peer in (sq.across, sq.down, sq.far)] + [{"dp": line.sibling}]
    )
    out_spread = HalfSpread(
        sq, line, weight_hbm, qkv_width, w_out_all, w_send.at[0], w_recv.at[0]
    )
    q_spread = HalfSpread(sq, line, weight_hbm, 0, w_q_all, w_send.at[1], w_recv.at[1])
    out_spread.start()
    h_spread = sq.spread(lambda peer: h_table, h_all, h_send, h_recv)
    for copy in h_spread:
        copy.start()
    weight_load.wait()
    seq_load.wait()

    @pl.loop(0, 4)
    def _(block):
        here = pl.ds(pl.multiple_of(block * rows, rows), rows)
        low = band(nn(seq[block], d_table[...]), QUERY, VALUE).astype(BF16)
        low_ref[here, :] = low
        cosine, sine = cos_ref[here, :], sin_ref[here, :]
        for h in range(heads):
            column = slice(h * HD, (h + 1) * HD)
            query = nn(seq[block], weight[:, column]) + nt(
                band(low.astype(F32), QUERY).astype(BF16), h_table[column, :]
            )
            q_ref[here, column] = (rotate_rows(query, cosine, sine) * HD ** (-0.5)).astype(BF16)
        key = nn(seq[block], weight[:, q_width : q_width + HD]) + nt(
            band(low.astype(F32), KEY).astype(BF16), k_table[...]
        )
        key = rotate_rows(key, cosine, sine)
        k_ref[here, :] = key.astype(BF16)
        kt_ref[:, here] = key.T.astype(BF16)
        value = nn(seq[block], weight[:, q_width + HD : qkv_width]) + nt(
            band(low.astype(F32), VALUE).astype(BF16), k_table[...]
        )
        v_ref[here, :] = value.astype(BF16)
        vt[:, here] = value.T.astype(BF16)

    out_spread.forward()
    part, part_low = scratch[0], scratch[5]
    scatters = (ChunkScatter(sq, *scratch[:5]), ChunkScatter(sq, *scratch[5:10]))

    @pl.loop(0, 4)
    def _(step):
        chunk = far_first(step)
        for side in range(2):
            start = chunk_start(sq, chunk, side)
            here = pl.ds(start, half)
            unused, weights = softmax_weights(
                k_ref[...], stack_heads(q_ref, here, heads), start, half, length_ref[0]
            )
            inverse = 1.0 / jnp.sum(weights, axis=0, keepdims=True)
            mixed = nn(vt[...], (weights * inverse).astype(BF16)).T.astype(BF16)
            for h in range(heads):
                inverse_ref[h : h + 1, here] = inverse[:, h * half : (h + 1) * half]
                attended_ref[here, h * HD : (h + 1) * HD] = mixed[h * half : (h + 1) * half]

        attended = jnp.concatenate(
            [attended_ref[pl.ds(chunk_start(sq, chunk, side), half), :] for side in range(2)],
            axis=0,
        )
        part_low[chunk] = band(nn(attended, h_table[...]), OUT).astype(BF16)

        @pl.loop(0, model // wide)
        def _(tile):
            here = columns(tile, wide)
            part[chunk, :, here] = nt(attended, weight[here, qkv_width:]).astype(BF16)

            @pl.when(step == 0)
            def _():
                scatters[0].send(1, tile)

            @pl.when(step == 1)
            def _():
                scatters[0].send(0, tile)

        @pl.when(step == 0)
        def _():
            scatters[1].send_far()

        @pl.when(step == 1)
        def _():
            scatters[1].send_own()

    for scatter in scatters:
        scatter.pass_on()
    scatters[1].collect(low_sum)
    low_out_ref[...] = low_sum[...].astype(BF16)
    scatters[0].collect(total_ref)
    add_lifted(total_ref, low_out_ref, d_table)

    @pl.loop(0, rows // BLOCK)
    def _(step):
        here = pl.ds(pl.multiple_of(step * BLOCK, BLOCK), BLOCK)
        resid = layer_ref[here, :].astype(F32) + rms_norm(total_ref[here, :], gains_ref[1:2, :])
        resid_ref[here, :] = resid
        normed_ref[here, :] = rms_norm(resid, gains_ref[2:3, :]).astype(BF16)

    gather = ChunkGather(sq, normed_ref, mlp_out, gather_send, gather_recv)
    gather.start()
    own = pltpu.make_async_copy(normed_ref, mlp_out.at[0], own_sem)
    own.start()
    gather.wait_chunk(1)
    q_spread.start()
    out_spread.share()
    for chunk in range(2, 4):
        gather.wait_chunk(chunk)
    own.wait()
    q_spread.forward()
    for copy in h_spread:
        copy.wait()
    out_spread.finish()
    q_spread.share()
    q_spread.finish()
    gather.finish()
    for scatter in scatters:
        scatter.finish()


def attn_fused(lengths, seq, weight, d_tab, h_tab, k_tab, cosine, sine, layer_in, gains):
    rows, model = layer_in.shape
    q_width = weight.shape[1] - 2 * HD
    q_width //= 2
    qkv_width = q_width + 2 * HD
    anywhere = pl.BlockSpec(memory_space=pl.ANY)
    vmem = pl.BlockSpec(memory_space=pltpu.VMEM)
    narrow = jax.ShapeDtypeStruct((LEN, HD), BF16)
    return pl.pallas_call(
        functools.partial(attn_kernel, rows),
        out_shape=(
            jax.ShapeDtypeStruct((LEN, q_width), BF16),
            narrow,
            jax.ShapeDtypeStruct((HD, LEN), BF16),
            narrow,
            jax.ShapeDtypeStruct((LEN, q_width), BF16),
            jax.ShapeDtypeStruct((q_width // HD, LEN), F32),
            jax.ShapeDtypeStruct((LEN, LANES), BF16),
            jax.ShapeDtypeStruct((rows, LANES), BF16),
            jax.ShapeDtypeStruct((rows, model), F32),
            jax.ShapeDtypeStruct((rows, model), F32),
            jax.ShapeDtypeStruct((rows, model), BF16),
            jax.ShapeDtypeStruct((4, rows, model), BF16),
            jax.ShapeDtypeStruct((4, model, q_width), BF16),
            jax.ShapeDtypeStruct((4, model, q_width), BF16),
            jax.ShapeDtypeStruct((4, q_width, LANES), BF16),
        ),
        in_specs=[pl.BlockSpec(memory_space=pltpu.SMEM)] + [anywhere] * 2 + [vmem] * 7,
        out_specs=(vmem,) * 11 + (anywhere,) * 4,
        scratch_shapes=[
            pltpu.VMEM((4, rows, model), BF16),
            pltpu.VMEM(weight.shape, BF16),
            pltpu.VMEM((HD, LEN), BF16),
            pltpu.VMEM((rows, LANES), F32),
            pltpu.SemaphoreType.DMA((2,)),
            pltpu.SemaphoreType.DMA,
            pltpu.SemaphoreType.DMA((6,)),
            pltpu.SemaphoreType.DMA((6,)),
            pltpu.SemaphoreType.DMA((3,)),
            pltpu.SemaphoreType.DMA((4,)),
            pltpu.SemaphoreType.DMA((2, 9)),
            pltpu.SemaphoreType.DMA((2, 9)),
        ]
        + scatter_scratch(rows, model, model // tile_of(model))
        + scatter_scratch(rows, LANES),
        compiler_params=pltpu.CompilerParams(
            collective_id=8, has_side_effects=True, vmem_limit_bytes=62 * 1024 * 1024
        ),
        name="attn",
    )(lengths, seq, weight, d_tab, h_tab, k_tab, cosine, sine, layer_in, gains)


def attn_back_kernel(
    rows,
    ids_ref,
    length_ref,
    back_ref,
    low_gu_ref,
    resid_ref,
    total_ref,
    cot_ref,
    layer_hbm,
    gains_ref,
    weight_hbm,
    w_out_hbm,
    w_q_hbm,
    w_kv_hbm,
    seq_hbm,
    q_hbm,
    k_hbm,
    kt_hbm,
    v_hbm,
    attended_hbm,
    inverse_ref,
    cos_hbm,
    sin_hbm,
    low_hbm,
    d_table,
    h_all,
    k_table,
    normed_hbm,
    low_out_ref,
    grad_mlp_hbm,
    low_down_ref,
    f_ref,
    o_ref,
    in_out,
    heads_out,
    hidden_out,
    query_out,
    keyval_out,
    gateup_out,
    resid_out,
    q_ref,
    k_ref,
    kt_ref,
    v_ref,
    attended_ref,
    cos_ref,
    sin_ref,
    low_ref,
    normed_ref,
    grad_mlp_ref,
    layer_ref,
    slots,
    total,
    work,
    g_ref,
    buf,
    att_send,
    att,
    low_own,
    low_all,
    part_low,
    q_land,
    kv_land,
    low_land,
    q_grad,
    k_sum,
    v_sum,
    kv_grad,
    d_turned,
    h_turned,
    k_turned,
    d_send,
    d_land,
    d_sum,
    d_recv,
    f_land,
    f_recv,
    hk_send,
    hk_land,
    hk_recv,
    load_sem,
    late_sem,
    att_sends,
    att_recvs,
    back_sends,
    back_recvs,
    f_sem,
    f_send_sem,
    f_recv_sem,
    d_sem,
    hk_sem,
    group_send,
    group_recv,
    line_recv,
):
    sq = Square(rows)
    dp = lax.axis_size("dp")
    d = lax.axis_index("dp")
    model = o_ref.shape[-1]
    half = sq.half
    wide = tile_of(model)
    q_width = q_ref.shape[1]
    qkv_width = q_width + 2 * HD
    others = (sq.far, sq.across, sq.down)
    arrivals = ((sq.down, 2), (sq.far, 0), (sq.across, 1))
    sources = [w_out_hbm.at[peer] for peer in others]
    sources.append(weight_hbm.at[:, pl.ds(qkv_width, q_width)])
    sources.append(weight_hbm.at[:, pl.ds(0, q_width)])
    sources.append(weight_hbm.at[:, pl.ds(q_width, 2 * HD)])
    for peer, unused in arrivals:
        sources += [w_q_hbm.at[peer], w_kv_hbm.at[peer]]
    loads = [
        pltpu.make_async_copy(source, slots.at[which % 4], load_sem.at[1 + which])
        for which, source in enumerate(sources)
    ]
    seq_load = pltpu.make_async_copy(seq_hbm, buf, load_sem.at[0])
    late = [
        pltpu.make_async_copy(source, target, late_sem.at[which])
        for which, (source, target) in enumerate(
            (
                (q_hbm, q_ref),
                (k_hbm, k_ref),
                (kt_hbm, kt_ref),
                (v_hbm, v_ref),
                (attended_hbm, attended_ref),
                (cos_hbm, cos_ref),
                (sin_hbm, sin_ref),
                (low_hbm, low_ref),
                (normed_hbm, normed_ref),
                (grad_mlp_hbm, grad_mlp_ref),
                (layer_hbm, layer_ref),
            )
        )
    ]
    for copy in loads[:4]:
        copy.start()
    for copy in late:
        copy.start()
    seq_load.start()
    peers = [{"tensor": peer} for peer in (sq.across, sq.down, sq.far)]
    peers += [{"dp": lax.rem(d + step, dp)} for step in range(1, dp)]
    call(peers)

    low_gu = unpack_rows(low_gu_ref[...]).astype(BF16)

    @pl.loop(0, model // wide)
    def _(step):
        here = columns(step, wide)
        work[:, here] = back_ref[:, here] + nt(low_gu, d_table[here, :])

    @pl.loop(0, rows // BLOCK)
    def _(step):
        here = pl.ds(pl.multiple_of(step * BLOCK, BLOCK), BLOCK)
        at = sq.me * rows + step * BLOCK + lax.broadcasted_iota(jnp.int32, (BLOCK, 1), 0)
        valid = (at < length_ref[0]).astype(F32)
        mid = cot_ref[here, :].astype(F32) * valid + norm_back(
            resid_ref[here, :], gains_ref[2:3, :], work[here, :]
        )
        work[here, :] = mid
        g_ref[here, :] = norm_back(total_ref[here, :], gains_ref[1:2, :], mid).astype(BF16)

    low_out = band(nn(g_ref[...], d_table[...]), OUT).astype(BF16)
    low_own[...] = turned(low_out)[OUT]
    pl.semaphore_wait(pltpu.get_barrier_semaphore(), len(peers))
    heads_out_copies = []
    for which, peer in enumerate(others + (sq.me,)):
        loads[which].wait()
        grads = (nn(g_ref[...], slots[which]) + nt(low_out, h_all[peer])).astype(BF16)
        loads[which + 4].start()
        if which == 3:
            att[sq.me] = grads
            low_all[sq.me] = low_own[...]
            continue
        att_send[which] = grads
        copies = tuple(
            remote(
                source, target.at[sq.me], att_sends.at[which, item], att_recvs.at[which, item], peer
            )
            for item, (source, target) in enumerate(
                ((att_send.at[which], att), (low_own, low_all))
            )
        )
        for copy in copies:
            copy.start()
        heads_out_copies.append(copies)
    line = []
    f_spread = sq.spread(lambda peer: f_ref.at[:, peer], f_land, f_send_sem, f_recv_sem)
    for copy in f_spread:
        copy.start()
    back = []
    for which, peer in enumerate(others):
        here = pl.ds(pl.multiple_of(peer * rows, rows), rows)
        back.append(
            tuple(
                remote(
                    source,
                    target.at[sq.me],
                    back_sends.at[which, item],
                    back_recvs.at[which, item],
                    peer,
                )
                for item, (source, target) in enumerate(
                    (
                        (q_grad.at[here], q_land),
                        (kv_grad.at[here], kv_land),
                        (part_low.at[peer], low_land),
                    )
                )
            )
        )

    for copy in late:
        copy.wait()
    d_turned[...] = jnp.zeros_like(d_turned)
    low_grads = (
        (turned(low_gu)[GATE.start : UP.stop], normed_ref, slice(GATE.start, UP.stop)),
        (turned(low_out_ref[...])[OUT], g_ref, OUT),
        (turned(low_down_ref[...])[DOWN], grad_mlp_ref, DOWN),
    )

    @pl.loop(0, model // wide)
    def _(step):
        here = columns(step, wide)
        for low, source, place in low_grads:
            d_turned[place, here] = nn(low, source[:, here])

    h_turned[...] = jnp.zeros_like(h_turned)
    k_turned[...] = jnp.zeros_like(k_turned)
    k_sum[...] = jnp.zeros_like(k_sum)
    v_sum[...] = jnp.zeros_like(v_sum)
    heads = q_width // HD
    stacked = heads * half

    @pl.loop(0, 4)
    def _(turn):
        for step, (unused, which) in enumerate(arrivals):

            @pl.when(turn == step + 1)
            def _(which=which):
                for copy in heads_out_copies[which]:
                    copy.wait_recv()

        is_own, is_across = (3 - turn) // 3, turn // 3
        is_far = turn // 2 - is_across
        block = (
            sq.me * is_own
            + sq.far * is_far
            + sq.across * is_across
            + sq.down * (1 - is_own - is_far - is_across)
        )
        low_turned = low_all[block]
        h_turned[:RANK, :] += nn(
            low_turned, attended_ref[pl.ds(pl.multiple_of(block * rows, rows), rows), :]
        )
        for last in range(4):

            @pl.when(block == last)
            def _(last=last):
                seen = slice(0, (last + 1) * rows)

                @pl.loop(0, 2)
                def _(side):
                    start = pl.multiple_of(last * rows + side * half, half)
                    here = pl.ds(start, half)
                    place = pl.ds(pl.multiple_of(side * half, half), half)
                    queries = stack_heads(q_ref, here, heads)
                    grads = jnp.concatenate(
                        [att[last, place, h * HD : (h + 1) * HD] for h in range(heads)], axis=0
                    )
                    inverse = jnp.concatenate(
                        [inverse_ref[h : h + 1, here] for h in range(heads)], axis=1
                    )
                    squash, weights = softmax_weights(
                        k_ref[seen, :], queries, start, half, length_ref[0]
                    )
                    probs = weights * inverse
                    grad_probs = nt(v_ref[seen, :], grads)
                    mean = jnp.sum(probs * grad_probs, axis=0, keepdims=True)
                    grad_raw = (probs * (grad_probs - mean) * (1.0 - squash * squash)).astype(BF16)
                    k_sum[seen, :] += nn(grad_raw, queries)
                    v_sum[seen, :] += nn(probs.astype(BF16), grads)
                    q_back = nn(kt_ref[:, seen], grad_raw).T * HD ** (-0.5)
                    for h in range(heads):
                        q_grad[here, h * HD : (h + 1) * HD] = rotate_back(
                            q_back[h * half : (h + 1) * half], cos_ref[here, :], sin_ref[here, :]
                        ).astype(BF16)

        for step, (unused, which) in enumerate(arrivals):

            @pl.when(turn == step + 1)
            def _(which=which):
                back[which][0].start()

    kv_grad[:, :HD] = rotate_back(k_sum[...], cos_ref[...], sin_ref[...]).astype(BF16)
    kv_grad[:, HD:] = v_sum[...].astype(BF16)
    for copies in back:
        copies[1].start()
    f_spread[0].wait()
    for copy in f_spread[1:]:
        copy.wait_recv()
    line += along(lambda k: f_land.at[k // 2, lax.rem(k, 2)], f_recv, f_sem, line_recv.at[0])

    @pl.loop(0, 4)
    def _(block):
        here = pl.ds(pl.multiple_of(block * rows, rows), rows)
        low = (
            band(nn(q_grad[here, :], h_all[sq.me]), QUERY)
            + band(nn(kv_grad[here, :HD], k_table[...]), KEY)
            + band(nn(kv_grad[here, HD:], k_table[...]), VALUE)
        )
        part_low[block] = turned(low)[: VALUE.stop]

    for copies in back:
        copies[2].start()

    def add_block(queries, keys_values, which, first):
        for item in range(2):
            loads[which + item].wait()
        low_q, low_kv = which % 4, (which + 1) % 4

        @pl.loop(0, model // wide)
        def _(step):
            here = columns(step, wide)
            grad = nt(queries, slots[low_q, here, :]) + nt(keys_values, slots[low_kv, here, :])
            total[:, here] = grad if first else total[:, here] + grad

        for item in range(2):
            if which + item + 4 < len(loads):
                loads[which + item + 4].start()

    own = pl.ds(pl.multiple_of(sq.me * rows, rows), rows)
    add_block(q_grad[own, :], kv_grad[own, :], 4, True)
    seq_load.wait()

    @pl.loop(0, 4)
    def _(block):
        here = pl.ds(pl.multiple_of(block * rows, rows), rows)
        grad_turned = part_low[block]
        low_turned = turned(low_ref[here, :])
        h_turned[RANK : 2 * RANK, :] += nn(low_turned[QUERY], q_grad[here, :])
        k_turned[:RANK, :] += nn(low_turned[KEY], kv_grad[here, :HD])
        k_turned[RANK : 2 * RANK, :] += nn(low_turned[VALUE], kv_grad[here, HD:])

        @pl.loop(0, model // wide)
        def _(step):
            where = columns(step, wide)
            d_turned[: VALUE.stop, where] += nn(grad_turned, buf[block, :, where])

    @pl.loop(0, model // LANES)
    def _(step):
        here = columns(step, LANES)
        d_send[here, :] = d_turned[:, here].T.astype(BF16)

    d_rows = d_sum.shape[1]
    spread = []
    for k in range(dp):
        spread.append(
            sq.spread(
                lambda peer, k=k: d_send.at[pl.ds(pl.multiple_of((k * 4 + peer) * d_rows, 8), d_rows)],
                d_land.at[k],
                group_send.at[k],
                group_recv.at[k],
            )
        )
    cores = hk_send.shape[0]
    h_size, k_size = q_width // dp, HD // dp
    hk_send[...] = jnp.zeros_like(hk_send)
    for core in range(cores):
        for peer in range(4):
            at = core * 4 + peer
            hk_send[core, peer, : 2 * RANK, :h_size] = h_turned[
                : 2 * RANK, at * h_size : (at + 1) * h_size
            ].astype(BF16)
            hk_send[core, peer, 2 * RANK :, :k_size] = k_turned[
                : 2 * RANK, at * k_size : (at + 1) * k_size
            ].astype(BF16)
    spread.append(
        sq.spread(lambda peer: hk_send.at[:, peer], hk_land, group_send.at[dp], group_recv.at[dp])
    )
    for copies in spread:
        for copy in copies:
            copy.start()
    for step, (peer, which) in enumerate(arrivals):
        for copy in back[which]:
            copy.wait_recv()
        add_block(q_land[peer], kv_land[peer], 6 + 2 * step, False)
    for copies in spread:
        copies[0].wait()
        for copy in copies[1:]:
            copy.wait_recv()
    for k in range(dp):
        d_sum[k] = sum(d_land[k, t].astype(F32) for t in range(4)).astype(BF16)
    line += along(lambda k: d_sum.at[k], d_recv, d_sem, line_recv.at[1])
    line += along(lambda k: hk_land.at[k // 2, lax.rem(k, 2)], hk_recv, hk_sem, line_recv.at[2])
    low_total = sum(
        low_land[peer].astype(F32) for peer, unused in arrivals
    ) + part_low[sq.me].astype(F32)
    rest = jnp.zeros((LANES - VALUE.stop, rows), F32)
    low_qkv = turned(jnp.concatenate([low_total, rest], axis=0))

    @pl.loop(0, model // wide)
    def _(step):
        here = columns(step, wide)
        total[:, here] += nt(low_qkv, d_table[here, :])

    @pl.loop(0, rows // BLOCK)
    def _(step):
        here = pl.ds(pl.multiple_of(step * BLOCK, BLOCK), BLOCK)
        o_ref[here, :] = (
            work[here, :]
            + norm_back(layer_ref[here, :].astype(F32), gains_ref[0:1, :], total[here, :])
        ).astype(BF16)

    for item, target in enumerate((f_recv, d_recv, hk_recv)):
        pltpu.make_async_copy(target, target, line_recv.at[item]).wait()

    @pl.loop(0, NA)
    def _(adapter):
        def pick(received):
            total = None
            for group in range(dp):
                mine = jnp.where(
                    ids_ref[group] == adapter, received[group].astype(F32), 0.0
                )
                total = mine if total is None else total + mine
            return total

        d_all = pick(d_recv)
        in_out[adapter] = d_all[:, : 5 * RANK]
        d_flip = d_all.T
        f_all = pick(f_recv)
        hidden_out[adapter] = f_all[:RANK]
        hk_all = pick(hk_recv)
        heads_out[adapter] = hk_all[:RANK, :h_size]
        query_out[adapter] = hk_all[RANK : 2 * RANK, :h_size]
        for which in range(2):
            first = (which + 2) * RANK
            keyval_out[adapter, which] = hk_all[first : first + RANK, :k_size]
            first = (which + 1) * RANK
            gateup_out[adapter, which] = f_all[first : first + RANK]
            first = (which + 5) * RANK
            resid_out[adapter, which] = d_flip[first : first + RANK]

    for copies in spread + [f_spread]:
        for copy in copies[1:]:
            copy.wait_send()
    for copies in heads_out_copies + back:
        for copy in copies:
            copy.wait_send()
    for copy in line:
        copy.wait_send()


LATE = (12, 13, 14, 15, 16, 18, 19, 20, 24, 26, 5)


def attn_back_fused(scalars, arrays, grad_shapes, dp, total):
    anywhere = pl.BlockSpec(memory_space=pl.ANY)
    vmem = pl.BlockSpec(memory_space=pltpu.VMEM)
    smem = pl.BlockSpec(memory_space=pltpu.SMEM)
    rows, model = arrays[0].shape
    q, f_in = arrays[12], arrays[-1]
    q_width = q.shape[1]
    specs = [smem, smem] + [vmem] * len(arrays)
    late = [arrays[which] for which in LATE]
    for which in LATE + (7, 8, 9, 10, 11):
        specs[2 + which] = anywhere
    outs = [jax.ShapeDtypeStruct((rows, model), BF16)]
    outs += [jax.ShapeDtypeStruct(shape, F32) for shape in grad_shapes]
    d_rows = model // total
    messages = f_in.shape[2:]
    landed = (4, f_in.shape[0]) + messages
    return pl.pallas_call(
        functools.partial(attn_back_kernel, rows),
        out_shape=tuple(outs),
        in_specs=specs,
        out_specs=(vmem,) * len(outs),
        scratch_shapes=[
            *(pltpu.VMEM(array.shape, array.dtype) for array in late),
            pltpu.VMEM((4, model, q_width), BF16),
            pltpu.VMEM((rows, model), F32),
            pltpu.VMEM((rows, model), F32),
            pltpu.VMEM((rows, model), BF16),
            pltpu.VMEM((4, rows, model), BF16),
            pltpu.VMEM((3, rows, q_width), BF16),
            pltpu.VMEM((4, rows, q_width), BF16),
            pltpu.VMEM((RANK, rows), BF16),
            pltpu.VMEM((4, RANK, rows), BF16),
            pltpu.VMEM((4, 3 * RANK, rows), BF16),
            pltpu.VMEM((4, rows, q_width), BF16),
            pltpu.VMEM((4, rows, 2 * HD), BF16),
            pltpu.VMEM((4, 3 * RANK, rows), BF16),
            pltpu.VMEM((LEN, q_width), BF16),
            pltpu.VMEM((LEN, HD), F32),
            pltpu.VMEM((LEN, HD), F32),
            pltpu.VMEM((LEN, 2 * HD), BF16),
            pltpu.VMEM((LANES, model), F32),
            pltpu.VMEM((2 * RANK, q_width), F32),
            pltpu.VMEM((2 * RANK, HD), F32),
            pltpu.VMEM((model, LANES), BF16),
            pltpu.VMEM((dp, 4, d_rows, LANES), BF16),
            pltpu.VMEM((dp, d_rows, LANES), BF16),
            pltpu.VMEM((dp, d_rows, LANES), BF16),
            pltpu.VMEM(landed, BF16),
            pltpu.VMEM((dp,) + messages, BF16),
            pltpu.VMEM((dp // 4, 4, 4 * RANK, LANES), BF16),
            pltpu.VMEM((4, dp // 4, 4 * RANK, LANES), BF16),
            pltpu.VMEM((dp, 4 * RANK, LANES), BF16),
            pltpu.SemaphoreType.DMA((13,)),
            pltpu.SemaphoreType.DMA((len(late),)),
            pltpu.SemaphoreType.DMA((3, 2)),
            pltpu.SemaphoreType.DMA((3, 2)),
            pltpu.SemaphoreType.DMA((3, 3)),
            pltpu.SemaphoreType.DMA((3, 3)),
            pltpu.SemaphoreType.DMA((dp,)),
            pltpu.SemaphoreType.DMA((3,)),
            pltpu.SemaphoreType.DMA((4,)),
            pltpu.SemaphoreType.DMA((dp,)),
            pltpu.SemaphoreType.DMA((dp,)),
            pltpu.SemaphoreType.DMA((dp + 1, 3)),
            pltpu.SemaphoreType.DMA((dp + 1, 4)),
            pltpu.SemaphoreType.DMA((3,)),
        ],
        compiler_params=pltpu.CompilerParams(
            collective_id=6, has_side_effects=True, vmem_limit_bytes=62 * 1024 * 1024
        ),
        name="attn_back",
    )(*scalars, *arrays)


def per_device(
    layer_in,
    cotangent,
    lengths,
    adapter_ids,
    norm_gains,
    query_weight,
    key_weight,
    value_weight,
    out_weight,
    gate_weight,
    up_weight,
    down_weight,
    adapt_in,
    adapt_heads,
    adapt_hidden,
    lift_query,
    lift_keyval,
    lift_gateup,
    lift_resid,
):
    lay = Layout()
    count = lay.tensor
    rows = layer_in.shape[0]
    group_rows = rows * count
    assert lengths.shape[0] == 1 and group_rows == LEN
    heads_here = lay.heads_here
    head_width = heads_here * HD
    hidden_here = FF // count
    assert lay.ratio % heads_here == 0

    qkv_width = head_width + 2 * HD
    cosine, sine = tables(LEN, HD)
    if count == 4 and lay.dp == 8:
        adapters = (
            lift_gateup.reshape(NA, 2 * RANK, -1),
            jnp.swapaxes(adapt_hidden, 1, 2),
            adapt_in,
            lift_resid.reshape(NA, 2 * RANK, -1),
            jnp.swapaxes(adapt_heads, 1, 2),
            lift_query,
            lift_keyval.reshape(NA, 2 * RANK, -1),
        )
        seq_attn, all_ids, d_tab, f_tab, h_tab, k_tab, attn_w, gate_up_shard = front(
            adapter_ids,
            layer_in,
            norm_gains,
            adapters,
            (query_weight, key_weight, value_weight, out_weight.T, gate_weight, up_weight),
            lay.dp,
            (D, hidden_here, head_width, HD),
        )
        attn_w = attn_w.reshape(D, -1)
        down_shard = down_weight.T
        gate_up_w = lax.all_gather(gate_up_shard, "dp", axis=0, tiled=True)
        (
            queries,
            keys,
            keys_turned,
            values,
            attended,
            inverse,
            low_qkv,
            low_out,
            attn_total,
            resid_mid,
            normed_mlp,
            seq_mlp,
            w_out_all,
            w_q_all,
            h_all,
        ) = attn_fused(
            lengths,
            seq_attn.reshape(count, rows, D),
            attn_w,
            d_tab,
            h_tab,
            k_tab,
            cosine.reshape(LEN, HD // 2),
            sine.reshape(LEN, HD // 2),
            layer_in,
            norm_gains,
        )
        (
            layer_out,
            grad_mlp,
            low_gu,
            low_down,
            hidden,
            slope,
            gelu,
            down_w,
            w_kv_all,
        ) = mlp_fused(
            lengths,
            seq_mlp,
            gate_up_w,
            down_shard,
            attn_w,
            d_tab,
            f_tab,
            resid_mid,
            cotangent,
            norm_gains,
            lay.dp,
        )
        mlp_back, grad_low_gu, f_grad = mlp_back_fused(
            grad_mlp,
            down_w.reshape(D, hidden_here),
            gate_up_w,
            slope,
            gelu,
            hidden,
            low_gu,
            d_tab,
            f_tab,
            lay.dp,
        )
        grad_shapes = [
            table.shape
            for table in (
                adapt_in,
                adapt_heads,
                adapt_hidden,
                lift_query,
                lift_keyval,
                lift_gateup,
                lift_resid,
            )
        ]
        for which in (1, 2):
            shape = grad_shapes[which]
            grad_shapes[which] = (shape[0], shape[2], shape[1])
        grads = list(
            attn_back_fused(
                (all_ids[:, 0, 0], lengths),
                (
                    mlp_back,
                    grad_low_gu,
                    resid_mid,
                    attn_total,
                    cotangent,
                    layer_in,
                    norm_gains,
                    attn_w,
                    w_out_all,
                    w_q_all,
                    w_kv_all,
                    seq_attn.reshape(count, rows, D),
                    queries,
                    keys,
                    keys_turned,
                    values,
                    attended,
                    inverse,
                    cosine.reshape(LEN, HD // 2),
                    sine.reshape(LEN, HD // 2),
                    low_qkv,
                    d_tab,
                    h_all,
                    k_tab,
                    normed_mlp,
                    low_out,
                    grad_mlp,
                    low_down,
                    f_grad,
                ),
                tuple(grad_shapes),
                lay.dp,
                lay.total,
            )
        )
        for which in (2, 3):
            grads[which] = jnp.swapaxes(grads[which], 1, 2)
        return (layer_out, *grads)

    key_cols = lax.dynamic_slice_in_dim(key_weight, lay.kv_head * HD, HD, 1)
    value_cols = lax.dynamic_slice_in_dim(value_weight, lay.kv_head * HD, HD, 1)
    attn_shard = jnp.concatenate([query_weight, key_cols, value_cols, out_weight.T], axis=1)
    gate_up_shard = jnp.concatenate([gate_weight, up_weight], axis=1)
    down_shard = down_weight.T
    attn_w = lax.all_gather(attn_shard, "dp", axis=0, tiled=True)
    gate_up_w = lax.all_gather(gate_up_shard, "dp", axis=0, tiled=True)

    all_ids = lax.all_gather(adapter_ids[:, 0], "dp", axis=0, tiled=True)
    group_hot = (all_ids[:, None] == jnp.arange(NA, dtype=jnp.int32)[None, :]).astype(BF16)

    def rows_of(table):
        moved = jnp.moveaxis(table, -1, 1)
        return moved.reshape(NA, moved.shape[1], -1)

    def choose(*parts):
        packed = lanes(*parts)
        return lax.dot_general(
            group_hot, packed, (((1,), (0,)), ((), ())), preferred_element_type=F32
        ).astype(BF16)

    d_send = choose((QUERY, adapt_in), (OUT, rows_of(lift_resid)))
    f_send = choose((GATE, rows_of(lift_gateup)), (DOWN, adapt_hidden))
    h_send = choose((QUERY, rows_of(lift_query)), (OUT, adapt_heads))
    k_send = choose((KEY, rows_of(lift_keyval)))
    d_rows, f_rows, h_rows, k_rows = (item.shape[1] for item in (d_send, f_send, h_send, k_send))
    d_tab, f_tab, h_tab, k_tab = exchange(
        tables_kernel,
        "adapter_tables",
        3,
        (d_send, f_send, h_send, k_send),
        (
            (lay.total, d_rows, LANES),
            (lay.dp, f_rows, LANES),
            (lay.dp, h_rows, LANES),
            (lay.kv_owners, k_rows, LANES),
        ),
        lay.dp,
        lay.total,
        lay.share,
    )
    d_tab = d_tab.reshape(D, LANES)
    f_tab = f_tab.reshape(hidden_here, LANES)
    h_tab = h_tab.reshape(head_width, LANES)
    k_tab = k_tab.reshape(HD, LANES)
    in_qkv, in_gu = d_tab[:, : 3 * RANK], d_tab[:, 3 * RANK : 5 * RANK]
    lift_out, lift_down = d_tab[:, OUT], d_tab[:, DOWN]
    map_hidden, lift_gate, lift_up = f_tab[:, DOWN], f_tab[:, GATE], f_tab[:, UP]
    map_heads, lift_q = h_tab[:, OUT], h_tab[:, QUERY]
    lift_k, lift_v = k_tab[:, KEY], k_tab[:, VALUE]

    row_start = lay.t * rows
    length = lengths[0]
    row_valid = ((row_start + jnp.arange(rows, dtype=jnp.int32)) < length).astype(F32)[:, None]
    place = jnp.arange(LEN, dtype=jnp.int32)
    allowed = (place[:, None] >= place[None, :]) & (place[None, :] < length)

    resid_in = layer_in.astype(F32)
    normed_attn = rms_norm(resid_in, norm_gains[0]).astype(BF16)
    seq_attn = tensor_gather(normed_attn, count)
    low_qkv = nn(seq_attn, in_qkv).astype(BF16)
    low_q, low_k, low_v = (low_qkv[:, i * RANK : (i + 1) * RANK] for i in range(3))
    qkv = nn(seq_attn, attn_w[:, :qkv_width])
    query_pre = (qkv[:, :head_width] + nt(low_q, lift_q)).reshape(LEN, heads_here, HD)
    key_pre = (qkv[:, head_width : head_width + HD] + nt(low_k, lift_k)).reshape(LEN, 1, HD)
    value_pre = qkv[:, head_width + HD :] + nt(low_v, lift_v)
    queries = (rotate(query_pre, cosine, sine) * HD ** (-0.5)).astype(BF16)
    keys = rotate(key_pre, cosine, sine).astype(BF16).reshape(LEN, HD)
    values = value_pre.astype(BF16)

    def scores_of():
        raw = jnp.einsum("qhd,kd->hqk", queries, keys, preferred_element_type=F32)
        squash = jnp.tanh(raw / SOFT_CAP)
        return squash, jnp.where(allowed[None], jnp.exp(SOFT_CAP * squash), 0.0)

    squash, weights = scores_of()
    inverse_total = 1.0 / jnp.sum(weights, axis=-1, keepdims=True)
    attended = jnp.einsum(
        "hqk,kd->qhd", (weights * inverse_total).astype(BF16), values, preferred_element_type=F32
    )
    attended = attended.astype(BF16).reshape(LEN, head_width)
    w_out = attn_w[:, qkv_width:]
    out_part = nt(attended, w_out).astype(BF16)
    low_out_part = pad_lanes(nn(attended, map_heads).astype(BF16))
    attn_main, low_out = tensor_scatter(out_part, low_out_part, count)
    low_out = low_out[:, :RANK].astype(BF16)
    attn_total = attn_main + nt(low_out, lift_out)
    resid_mid = resid_in + rms_norm(attn_total, norm_gains[1])

    normed_mlp = rms_norm(resid_mid, norm_gains[2]).astype(BF16)
    seq_mlp = tensor_gather(normed_mlp, count)
    low_gu = nn(seq_mlp, in_gu).astype(BF16)
    low_g, low_u = low_gu[:, :RANK], low_gu[:, RANK:]
    w_gate, w_up = gate_up_w[:, :hidden_here], gate_up_w[:, hidden_here:]
    gate = nn(seq_mlp, w_gate) + nt(low_g, lift_gate)
    up = nn(seq_mlp, w_up) + nt(low_u, lift_up)
    hidden, slope, gelu = gelu_parts(gate, up)
    down_w = lax.all_gather(down_shard, "dp", axis=0, tiled=True)
    down_part = nt(hidden, down_w).astype(BF16)
    low_down_part = pad_lanes(nn(hidden, map_hidden).astype(BF16))
    mlp_main, low_down = tensor_scatter(down_part, low_down_part, count)
    low_down = low_down[:, :RANK].astype(BF16)
    mlp_total = mlp_main + nt(low_down, lift_down)
    layer_out = (row_valid * (resid_mid + rms_norm(mlp_total, norm_gains[3]))).astype(BF16)

    grad_out = cotangent.astype(F32) * row_valid
    grad_mlp = norm_back(mlp_total, norm_gains[3], grad_out).astype(BF16)
    seq_grad_mlp = tensor_gather(grad_mlp, count)
    grad_low_down = nn(seq_grad_mlp, lift_down).astype(BF16)
    grad_hidden = nn(seq_grad_mlp, down_w) + nt(grad_low_down, map_hidden)
    grad_gate = (grad_hidden * slope.astype(F32)).astype(BF16)
    grad_up = (grad_hidden * gelu.astype(F32)).astype(BF16)
    low_gu_part = pad_lanes(
        jnp.concatenate([nn(grad_gate, lift_gate), nn(grad_up, lift_up)], axis=1).astype(BF16)
    )
    mlp_back_part = (nt(grad_gate, w_gate) + nt(grad_up, w_up)).astype(BF16)
    mlp_back, grad_low_gu = tensor_scatter(mlp_back_part, low_gu_part, count)
    f_parts = [tn(hidden, grad_low_down), tn(grad_gate, low_g), tn(grad_up, low_u)]
    grad_low_gu = grad_low_gu[:, : 2 * RANK].astype(BF16)
    grad_normed_mlp = mlp_back + nt(grad_low_gu, in_gu)
    grad_mid = grad_out + norm_back(resid_mid, norm_gains[2], grad_normed_mlp)

    grad_attn = norm_back(attn_total, norm_gains[1], grad_mid).astype(BF16)
    seq_grad_attn = tensor_gather(grad_attn, count)
    grad_low_out = nn(seq_grad_attn, lift_out).astype(BF16)
    grad_attended = (nn(seq_grad_attn, w_out) + nt(grad_low_out, map_heads)).astype(BF16)
    grad_heads = grad_attended.reshape(LEN, heads_here, HD)
    probs = weights * inverse_total
    probs_low = probs.astype(BF16)
    grad_probs = jnp.einsum("qhd,kd->hqk", grad_heads, values, preferred_element_type=F32)
    grad_value = jnp.einsum("hqk,qhd->kd", probs_low, grad_heads, preferred_element_type=F32)
    grad_capped = probs * (grad_probs - jnp.sum(probs * grad_probs, axis=-1, keepdims=True))
    grad_raw = (grad_capped * (1.0 - squash * squash)).astype(BF16)
    grad_query = jnp.einsum("hqk,kd->qhd", grad_raw, keys, preferred_element_type=F32)
    grad_key = jnp.einsum("hqk,qhd->kd", grad_raw, queries, preferred_element_type=F32)
    grad_q_pre = rotate(grad_query * HD ** (-0.5), cosine, -sine).astype(BF16)
    grad_q_pre = grad_q_pre.reshape(LEN, head_width)
    grad_k_pre = rotate(grad_key.reshape(LEN, 1, HD), cosine, -sine).astype(BF16)
    grad_k_pre = grad_k_pre.reshape(LEN, HD)
    grad_v_pre = grad_value.astype(BF16)
    low_qkv_part = pad_lanes(
        jnp.concatenate(
            [nn(grad_q_pre, lift_q), nn(grad_k_pre, lift_k), nn(grad_v_pre, lift_v)], axis=1
        ).astype(BF16)
    )
    grad_qkv = jnp.concatenate([grad_q_pre, grad_k_pre, grad_v_pre], axis=1)
    attn_back_part = nt(grad_qkv, attn_w[:, :qkv_width]).astype(BF16)
    attn_back, grad_low_qkv = tensor_scatter(attn_back_part, low_qkv_part, count)
    grad_low_qkv = grad_low_qkv[:, : 3 * RANK].astype(BF16)
    grad_normed_attn = attn_back + nt(grad_low_qkv, in_qkv)
    input_grad = (grad_mid + norm_back(resid_in, norm_gains[0], grad_normed_attn)).astype(BF16)

    def packed(parts, blocks):
        return pad_lanes(jnp.concatenate(parts, axis=1).astype(BF16)).reshape(
            blocks, -1, LANES
        )

    d_grad = packed(
        [
            tn(normed_attn, grad_low_qkv),
            tn(normed_mlp, grad_low_gu),
            tn(grad_attn, low_out),
            tn(grad_mlp, low_down),
        ],
        lay.total,
    )
    f_grad = packed(f_parts, lay.dp)
    h_grad = packed([tn(attended, grad_low_out), tn(grad_q_pre, low_q)], lay.dp)
    k_grad = packed([tn(grad_k_pre, low_k), tn(grad_v_pre, low_v)], lay.kv_owners)
    d_all, f_all, h_all, k_all = exchange(
        grads_kernel,
        "adapter_grads",
        4,
        (d_grad, f_grad, h_grad, k_grad),
        (
            (lay.total, d_rows, LANES),
            (lay.dp, f_rows, LANES),
            (lay.dp, h_rows, LANES),
            (lay.dp * lay.share, k_rows, LANES),
        ),
        lay.dp,
        lay.total,
        lay.share,
    )

    def collect(received):
        repeats = received.shape[0] // lay.dp
        hot = jnp.repeat(group_hot, repeats, axis=0)
        return lax.dot_general(
            hot, received, (((0,), (0,)), ((), ())), preferred_element_type=F32
        )

    d_all, f_all, h_all, k_all = (collect(item) for item in (d_all, f_all, h_all, k_all))

    def lift_form(values, shape):
        return jnp.moveaxis(values, 1, 2).reshape(shape)

    return (
        layer_out,
        input_grad,
        d_all[:, :, : 5 * RANK],
        h_all[:, :, :RANK],
        f_all[:, :, :RANK],
        lift_form(h_all[:, :, RANK : 2 * RANK], lift_query.shape),
        lift_form(k_all[:, :, : 2 * RANK], lift_keyval.shape),
        lift_form(f_all[:, :, RANK : 3 * RANK], lift_gateup.shape),
        lift_form(d_all[:, :, 5 * RANK : 7 * RANK], lift_resid.shape),
    )


def solution(mesh):
    return jax.shard_map(
        per_device,
        mesh=mesh,
        in_specs=(
            P(("dp", "tensor"), None),
            P(("dp", "tensor"), None),
            P("dp"),
            P("dp", None),
            P(),
            P("dp", "tensor"),
            P("dp", None),
            P("dp", None),
            P("tensor", "dp"),
            P("dp", "tensor"),
            P("dp", "tensor"),
            P("tensor", "dp"),
            P(None, ("dp", "tensor"), None),
            P(None, ("dp", "tensor"), None),
            P(None, ("dp", "tensor"), None),
            P(None, None, ("dp", "tensor")),
            P(None, None, None, ("dp", "tensor")),
            P(None, None, None, ("dp", "tensor")),
            P(None, None, None, ("dp", "tensor")),
        ),
        out_specs=(
            P(("dp", "tensor"), None),
            P(("dp", "tensor"), None),
            P(None, ("dp", "tensor"), None),
            P(None, ("dp", "tensor"), None),
            P(None, ("dp", "tensor"), None),
            P(None, None, ("dp", "tensor")),
            P(None, None, None, ("dp", "tensor")),
            P(None, None, None, ("dp", "tensor")),
            P(None, None, None, ("dp", "tensor")),
        ),
        check_vma=False,
    )
```

```python
import functools

import jax
import jax.numpy as jnp
from jax import lax
from jax.experimental import pallas as pl
from jax.experimental.pallas import tpu as pltpu
from jax.sharding import PartitionSpec as P

D = 2304
HQ = 8
KV = 4
HD = 256
FF = 9216
NA = 8
RANK = 16
LEN = 1024
LANES = 128

EPSILON = 1e-06
SOFT_CAP = 50.0
MESH = pl.DeviceIdType.MESH
BF16 = jnp.bfloat16
F32 = jnp.float32
VMEM_LIMIT = 48 * 1024 * 1024
BLOCK = 32


def rms_norm(values, gain_row):
    return (
        values * lax.rsqrt(jnp.mean(values * values, axis=-1, keepdims=True) + EPSILON) * gain_row
    )


def norm_back(values, gain_row, gradient):
    inverse = lax.rsqrt(jnp.mean(values * values, axis=-1, keepdims=True) + EPSILON)
    scaled = gradient * gain_row
    normed = values * inverse
    return inverse * (scaled - normed * jnp.mean(scaled * normed, axis=-1, keepdims=True))


def gelu_parts(gate, up):
    scale = (2.0 / jnp.pi) ** 0.5
    square = gate * gate
    bend = jnp.tanh(scale * gate * (1.0 + 0.044715 * square))
    low = 0.5 * (1.0 + bend)
    gelu = gate * low
    slope = low + 0.5 * gate * (1.0 - bend * bend) * (scale * (1.0 + 3.0 * 0.044715 * square))
    return (gelu * up).astype(BF16), (slope * up).astype(BF16), gelu.astype(BF16)


def tables(length, size):
    half_size = size // 2
    frequency = 10000.0 ** (-2.0 * jnp.arange(half_size, dtype=F32) / size)
    angles = jnp.arange(length, dtype=F32)[:, None] * frequency[None, :]
    return (jnp.cos(angles)[:, None, :], jnp.sin(angles)[:, None, :])


def rotate(values, cosine, sine):
    half_size = values.shape[-1] // 2
    first_half = values[..., :half_size]
    second_half = values[..., half_size:]
    return jnp.concatenate(
        [first_half * cosine - second_half * sine, second_half * cosine + first_half * sine],
        axis=-1,
    )


def nn(a, b):
    return lax.dot_general(a, b, (((1,), (0,)), ((), ())), preferred_element_type=F32)


def nt(a, b):
    return lax.dot_general(a, b, (((1,), (1,)), ((), ())), preferred_element_type=F32)


def tn(a, b):
    return lax.dot_general(a, b, (((0,), (0,)), ((), ())), preferred_element_type=F32)


def pad_lanes(values):
    return jnp.pad(values, [(0, 0)] * (values.ndim - 1) + [(0, LANES - values.shape[-1])])


QUERY, KEY, VALUE, GATE, UP, OUT, DOWN = (
    slice(i * RANK, (i + 1) * RANK) for i in range(7)
)


def band(values, first, last=None):
    lane = lax.broadcasted_iota(jnp.int32, values.shape, 1)
    keep = (lane >= first.start) & (lane < (last or first).stop)
    return jnp.where(keep, values, 0.0)


def lanes(*parts):
    pieces, at = [], 0
    for place, values in parts:
        if place.start > at:
            pieces.append(jnp.zeros(values.shape[:-1] + (place.start - at,), values.dtype))
        pieces.append(values)
        at = place.start + values.shape[-1]
    last = parts[-1][1]
    pieces.append(jnp.zeros(last.shape[:-1] + (LANES - at,), last.dtype))
    return jnp.concatenate(pieces, axis=-1)


def call(peers):
    barrier = pltpu.get_barrier_semaphore()
    for peer in peers:
        pl.semaphore_signal(barrier, inc=1, device_id=peer, device_id_type=MESH)


def greet(peers):
    call(peers)
    pl.semaphore_wait(pltpu.get_barrier_semaphore(), len(peers))


def square_peers(index):
    return index + 1 - 2 * lax.rem(index, 2), lax.rem(index + 2, 4), 3 - index


def remote(source, target, send_sem, recv_sem, peer):
    return pltpu.make_async_remote_copy(
        src_ref=source,
        dst_ref=target,
        send_sem=send_sem,
        recv_sem=recv_sem,
        device_id={"tensor": peer},
        device_id_type=MESH,
    )


class PlainGather:
    def __init__(self, me, x_ref, o_ref, local_sem, send_sem, recv_sem):
        rows = x_ref.shape[0]
        half = rows // 2
        links = square_peers(me)[:2]
        self.own = pltpu.make_async_copy(x_ref, o_ref.at[pl.ds(me * rows, rows)], local_sem)
        self.first, self.second, self.onward = [], [], []
        for order, group in enumerate((self.first, self.second)):
            for link in range(2):
                part = link if order == 0 else 1 - link
                group.append(
                    remote(
                        x_ref.at[pl.ds(part * half, half)],
                        o_ref.at[pl.ds(me * rows + part * half, half)],
                        send_sem.at[link, part],
                        recv_sem.at[link, part],
                        links[link],
                    )
                )
        for link in range(2):
            block = o_ref.at[pl.ds(links[link] * rows + link * half, half)]
            self.onward.append(
                remote(block, block, send_sem.at[2, link], recv_sem.at[2, link], links[1 - link])
            )

    def start(self):
        self.own.start()
        for copy in self.first + self.second:
            copy.start()

    def forward(self):
        for copy, onward in zip(self.first, self.onward):
            copy.wait_recv()
            onward.start()

    def finish(self):
        for copy in self.second + self.onward:
            copy.wait_recv()
        self.own.wait()
        for copy in self.first + self.second + self.onward:
            copy.wait_send()


def gather_kernel(count, rows, x_ref, o_ref, local_sem, send_sem, recv_sem):
    me = lax.axis_index("tensor")
    if count == 4:
        across, down, _ = square_peers(me)
        greet([{"tensor": across}, {"tensor": down}])
        gather = PlainGather(me, x_ref, o_ref, local_sem, send_sem, recv_sem)
        gather.start()
        gather.forward()
        gather.finish()
    else:
        peers = [lax.rem(me + step, count) for step in range(1, count)]
        greet([{"tensor": peer} for peer in peers])
        own = pltpu.make_async_copy(x_ref, o_ref.at[pl.ds(me * rows, rows)], local_sem)
        own.start()
        copies = []
        for step, peer in enumerate(peers):
            copy = remote(
                x_ref,
                o_ref.at[pl.ds(me * rows, rows)],
                send_sem.at[0, step],
                recv_sem.at[0, step],
                peer,
            )
            copy.start()
            copies.append(copy)
        own.wait()
        for copy in copies:
            copy.wait()


def tensor_gather(values, count):
    rows, width = values.shape
    slots = max(2, count - 1)
    return pl.pallas_call(
        functools.partial(gather_kernel, count, rows),
        out_shape=jax.ShapeDtypeStruct((count * rows, width), values.dtype),
        in_specs=[pl.BlockSpec(memory_space=pl.ANY)],
        out_specs=pl.BlockSpec(memory_space=pl.ANY),
        scratch_shapes=[
            pltpu.SemaphoreType.DMA,
            pltpu.SemaphoreType.DMA((3, slots)),
            pltpu.SemaphoreType.DMA((3, slots)),
        ],
        compiler_params=pltpu.CompilerParams(
            collective_id=1, has_side_effects=True, vmem_limit_bytes=VMEM_LIMIT
        ),
        name="tensor_gather",
    )(values)


def scatter_kernel(count, rows, p_ref, q_ref, o_ref, l_ref, *scratch):
    me = lax.axis_index("tensor")
    payload = ((p_ref, o_ref), (q_ref, l_ref))
    if count == 4:
        across, down, far = square_peers(me)
        greet([{"tensor": across}, {"tensor": down}])
        half = rows // 2
        first = scratch[0:2]
        sums = scratch[2:4]
        second = scratch[4:6]
        send_sem, recv_sem = scratch[6], scratch[7]
        links = (across, down)
        copies = {}
        for which in (1, 0):
            for link in range(2):
                block = far if which == 1 else links[link]
                for item in range(2):
                    copy = remote(
                        payload[item][0].at[pl.ds(block * rows + link * half, half)],
                        first[item].at[link, which],
                        send_sem.at[item, link, which],
                        recv_sem.at[item, link, which],
                        links[link],
                    )
                    copy.start()
                    copies[item, link, which] = copy
        for link in range(2):
            block = links[1 - link]
            for item in range(2):
                copies[item, link, 1].wait_recv()
                mine = payload[item][0][pl.ds(block * rows + link * half, half), :]
                sums[item][link] = (
                    mine.astype(F32) + first[item][link, 1].astype(F32)
                ).astype(BF16)
                copy = remote(
                    sums[item].at[link],
                    second[item].at[link],
                    send_sem.at[item, link, 2],
                    recv_sem.at[item, link, 2],
                    links[1 - link],
                )
                copy.start()
                copies[item, link, 2] = copy
        for link in range(2):
            for item in range(2):
                copies[item, link, 0].wait_recv()
                mine = payload[item][0][pl.ds(me * rows + link * half, half), :]
                payload[item][1][pl.ds(link * half, half), :] = mine.astype(F32) + first[item][
                    link, 0
                ].astype(F32)
        for link in range(2):
            for item in range(2):
                copies[item, link, 2].wait_recv()
                payload[item][1][pl.ds(link * half, half), :] += second[item][link].astype(F32)
        for copy in copies.values():
            copy.wait_send()
    else:
        peers = [lax.rem(me + step, count) for step in range(1, count)]
        greet([{"tensor": peer} for peer in peers])
        first = scratch[0:2]
        send_sem, recv_sem = scratch[2], scratch[3]
        copies = []
        for step, peer in enumerate(peers):
            for item in range(2):
                copy = remote(
                    payload[item][0].at[pl.ds(peer * rows, rows)],
                    first[item].at[step],
                    send_sem.at[item, step],
                    recv_sem.at[item, step],
                    peer,
                )
                copy.start()
                copies.append((item, step, copy))
        for item in range(2):
            payload[item][1][...] = payload[item][0][pl.ds(me * rows, rows), :].astype(F32)
        for item, step, copy in copies:
            copy.wait()
            payload[item][1][...] += first[item][step].astype(F32)


def tensor_scatter(values, narrow, count):
    rows = values.shape[0] // count
    widths = (values.shape[1], narrow.shape[1])
    if count == 4:
        half = rows // 2
        scratch = [pltpu.VMEM((2, 2, half, width), BF16) for width in widths]
        scratch += [pltpu.VMEM((2, half, width), BF16) for width in widths]
        scratch += [pltpu.VMEM((2, half, width), BF16) for width in widths]
        scratch += [pltpu.SemaphoreType.DMA((2, 2, 3)), pltpu.SemaphoreType.DMA((2, 2, 3))]
    else:
        scratch = [pltpu.VMEM((count - 1, rows, width), BF16) for width in widths]
        scratch += [pltpu.SemaphoreType.DMA((2, count - 1))] * 2
    vmem = pl.BlockSpec(memory_space=pltpu.VMEM)
    return pl.pallas_call(
        functools.partial(scatter_kernel, count, rows),
        out_shape=tuple(jax.ShapeDtypeStruct((rows, width), F32) for width in widths),
        in_specs=[vmem, vmem],
        out_specs=(vmem, vmem),
        scratch_shapes=scratch,
        compiler_params=pltpu.CompilerParams(
            collective_id=2, has_side_effects=True, vmem_limit_bytes=VMEM_LIMIT
        ),
        name="tensor_scatter",
    )(values, narrow)


class Square:
    def __init__(self, rows):
        self.rows = rows
        self.half = rows // 2
        self.me = lax.axis_index("tensor")
        self.across, self.down, self.far = square_peers(self.me)
        self.links = (self.across, self.down)

    def greet(self, far=False):
        greet([{"tensor": peer} for peer in (self.across, self.down) + ((self.far,) if far else ())])

    def spread(self, source_at, target, send_sem, recv_sem):
        copies = [pltpu.make_async_copy(source_at(self.me), target.at[self.me], recv_sem.at[0])]
        for which, peer in enumerate((self.across, self.down, self.far)):
            copies.append(
                remote(
                    source_at(peer),
                    target.at[self.me],
                    send_sem.at[which],
                    recv_sem.at[1 + which],
                    peer,
                )
            )
        return copies


def along(source_at, target, send_sem, recv_sem):
    dp = lax.axis_size("dp")
    d = lax.axis_index("dp")
    pltpu.make_async_copy(source_at(d), target.at[d], recv_sem).start()
    copies = []
    for step in range(1, dp):
        peer = lax.rem(d + step, dp)
        copy = pltpu.make_async_remote_copy(
            src_ref=source_at(peer),
            dst_ref=target.at[d],
            send_sem=send_sem.at[step],
            recv_sem=recv_sem,
            device_id={"dp": peer},
            device_id_type=MESH,
        )
        copy.start()
        copies.append(copy)
    return copies


class ChunkGather:
    def __init__(self, sq, source, buf, send_sem, recv_sem):
        half = sq.half
        self.first, self.second, self.onward = [], [], []
        for link in range(2):
            for order in range(2):
                part = link if order == 0 else 1 - link
                copy = remote(
                    source.at[pl.ds(part * half, half)],
                    buf.at[1 + order, pl.ds(link * half, half)],
                    send_sem.at[2 * order + link],
                    recv_sem.at[2 * order + link],
                    sq.links[link],
                )
                (self.first if order == 0 else self.second).append(copy)
            self.onward.append(
                remote(
                    buf.at[1, pl.ds(link * half, half)],
                    buf.at[3, pl.ds(link * half, half)],
                    send_sem.at[4 + link],
                    recv_sem.at[4 + link],
                    sq.links[1 - link],
                )
            )

    def start(self):
        for copy in self.first + self.second:
            copy.start()

    def wait_chunk(self, chunk):
        if chunk == 1:
            for copy in self.first:
                copy.wait_recv()
            for copy in self.onward:
                copy.start()
        if chunk == 2:
            for copy in self.second:
                copy.wait_recv()
        if chunk == 3:
            for copy in self.onward:
                copy.wait_recv()

    def finish(self):
        for copy in self.first + self.second + self.onward:
            copy.wait_send()


class ChunkScatter:
    def __init__(self, sq, part, landing, passed, send_sem, recv_sem):
        self.sq, self.half = sq, landing.shape[-2]
        self.part, self.landing, self.passed = part, landing, passed
        self.send_sem, self.recv_sem = send_sem, recv_sem
        self.tiles = send_sem.shape[-1]
        self.width = part.shape[-1] // self.tiles

    def columns(self, tile):
        if self.tiles == 1:
            return pl.ds(0, self.width)
        return columns(tile, self.width)

    def copy(self, kind, link, tile):
        rows = pl.ds(link * self.half, self.half)
        cols = self.columns(tile)
        source = (
            self.passed.at[link, :, cols]
            if kind == 2
            else self.part.at[1 + 2 * kind, rows, cols]
        )
        slot = 2 * kind + link
        return remote(
            source,
            self.landing.at[slot, :, cols],
            self.send_sem.at[slot, tile],
            self.recv_sem.at[slot, tile],
            self.sq.links[1 - link if kind == 2 else link],
        )

    def send(self, kind, tile):
        for link in range(2):
            self.copy(kind, link, tile).start()

    def send_own(self):
        for tile in range(self.tiles):
            self.send(0, tile)

    def send_far(self):
        for tile in range(self.tiles):
            self.send(1, tile)

    def pass_on(self):
        for tile in range(self.tiles):
            cols = self.columns(tile)
            for link in range(2):
                self.copy(1, link, tile).wait_recv()
                rows = pl.ds((1 - link) * self.half, self.half)
                mine = self.part[2, rows, cols].astype(F32)
                self.passed[link, :, cols] = (
                    mine + self.landing[2 + link, :, cols].astype(F32)
                ).astype(BF16)
                self.copy(2, link, tile).start()

    def arrived(self):
        for kind in (0, 2):
            for tile in range(self.tiles):
                for link in range(2):
                    self.copy(kind, link, tile).wait_recv()

    def collect(self, out_ref, places=((0, 0),)):
        self.arrived()
        for link in range(2):
            rows = pl.ds(link * self.half, self.half)
            total = (
                self.part[0, rows, :].astype(F32)
                + self.landing[link].astype(F32)
                + self.landing[4 + link].astype(F32)
            )
            size = self.part.shape[-1] // len(places)
            for source, target in places:
                out_ref[rows, target : target + size] = total[:, source : source + size]

    def finish(self):
        for kind in range(3):
            for tile in range(self.tiles):
                for link in range(2):
                    self.copy(kind, link, tile).wait_send()


def scatter_scratch(rows, width, tiles=1):
    half = rows // 2
    return [
        pltpu.VMEM((4, rows, width), BF16),
        pltpu.VMEM((6, half, width), BF16),
        pltpu.VMEM((2, half, width), BF16),
        pltpu.SemaphoreType.DMA((6, tiles)),
        pltpu.SemaphoreType.DMA((6, tiles)),
    ]


def tile_of(width):
    return 768 if width % 768 == 0 else 384


def columns(step, tile, base=0):
    return pl.ds(pl.multiple_of(base + step * tile, LANES), tile)


def pack_rows(low):
    size = low.shape[0] // 8
    return jnp.concatenate(
        [
            jnp.concatenate(
                [
                    low[(4 * half + i) * size : (4 * half + i + 1) * size, GATE.start : UP.stop]
                    for i in range(4)
                ],
                axis=1,
            )
            for half in range(2)
        ],
        axis=0,
    )


def unpack_rows(packed):
    size = packed.shape[0] // 2
    width = UP.stop - GATE.start
    low = jnp.concatenate(
        [
            packed[half * size : (half + 1) * size, i * width : (i + 1) * width]
            for half in range(2)
            for i in range(4)
        ],
        axis=0,
    )
    before = jnp.zeros((low.shape[0], GATE.start), low.dtype)
    after = jnp.zeros((low.shape[0], LANES - UP.stop), low.dtype)
    return jnp.concatenate([before, low, after], axis=1)


def mlp_back_kernel(
    rows,
    g_ref,
    down_hbm,
    gu_hbm,
    slope_hbm,
    gelu_hbm,
    hidden_hbm,
    low_hbm,
    d_ref,
    f_table,
    o_ref,
    l_ref,
    f_send,
    f_ref,
    down_w,
    gu_w,
    buf,
    slope,
    gelu,
    hidden,
    low,
    grads,
    weight_sem,
    load_sem,
    own_sem,
    gather_send,
    gather_recv,
    *scratch,
):
    sq = Square(rows)
    width = hidden.shape[-1]
    model = o_ref.shape[-1]
    down_load = pltpu.make_async_copy(down_hbm, down_w, weight_sem.at[0])
    gu_load = pltpu.make_async_copy(gu_hbm, gu_w, weight_sem.at[1])
    own_load = pltpu.make_async_copy(g_ref, buf.at[0], own_sem)

    def loads(chunk):
        slot = chunk % 2
        return [
            pltpu.make_async_copy(source.at[chunk], target.at[slot], load_sem.at[slot, item])
            for item, (source, target) in enumerate(
                ((slope_hbm, slope), (gelu_hbm, gelu), (hidden_hbm, hidden), (low_hbm, low))
            )
        ]

    down_load.start()
    own_load.start()
    for copy in loads(0):
        copy.start()
    sq.greet()
    gather = ChunkGather(sq, g_ref, buf, gather_send, gather_recv)
    gather.start()
    gu_load.start()
    part, part_low = scratch[0], scratch[5]
    scatters = (ChunkScatter(sq, *scratch[:5]), ChunkScatter(sq, *scratch[5:10]))
    f_ref[...] = jnp.zeros_like(f_ref)
    own_load.wait()
    down_load.wait()

    @pl.loop(0, 4)
    def _(chunk):
        slot = lax.rem(chunk, 2)
        for step in range(4):

            @pl.when(chunk == step)
            def _(step=step):
                gather.wait_chunk(step)
                for copy in loads(step):
                    copy.wait()
                if step < 3:
                    for copy in loads(step + 1):
                        copy.start()

        incoming = buf.at[chunk]
        low_down = band(nn(incoming[...], d_ref[...]), DOWN).astype(BF16)
        tile = tile_of(width)

        @pl.loop(0, width // tile)
        def _(step):
            here = columns(step, tile)
            grad = nn(incoming[...], down_w[:, here]) + nt(low_down, f_table[here, :])
            grads[:, here] = (grad * slope[slot, :, here].astype(F32)).astype(BF16)
            grads[:, columns(step, tile, width)] = (
                grad * gelu[slot, :, here].astype(F32)
            ).astype(BF16)

        @pl.when(chunk == 0)
        def _():
            gu_load.wait()

        wide = tile_of(model)

        @pl.loop(0, model // wide)
        def _(step):
            here = columns(step, wide)
            part[chunk, :, here] = nt(grads[...], gu_w[here, :]).astype(BF16)

            @pl.when(chunk == 1)
            def _():
                scatters[0].send(0, step)

            @pl.when(chunk == 3)
            def _():
                scatters[0].send(1, step)

        part_low[chunk] = pack_rows(
            band(nn(grads[:, :width], f_table[...]), GATE)
            + band(nn(grads[:, width:], f_table[...]), UP)
        ).astype(BF16)

        @pl.when(chunk == 1)
        def _():
            scatters[1].send_own()

        @pl.when(chunk == 3)
        def _():
            scatters[1].send_far()

        low_turned = low_down.astype(F32).T.astype(BF16)
        gu_turned = low[slot].astype(F32).T.astype(BF16)
        f_ref[:RANK, :] += nn(low_turned[DOWN], hidden[slot])
        f_ref[RANK : 2 * RANK, :] += nn(gu_turned[GATE], grads[:, :width])
        f_ref[2 * RANK : 3 * RANK, :] += nn(gu_turned[UP], grads[:, width:])

    for scatter in scatters:
        scatter.pass_on()
    cores, slices = f_send.shape[:2]
    size = width // (cores * slices)
    for core in range(cores):
        for peer in range(slices):
            first = (core * slices + peer) * size
            f_send[core, peer] = f_ref[: 3 * RANK, first : first + size].astype(BF16)
    gather.finish()
    scatters[0].collect(o_ref)
    scatters[1].collect(l_ref)
    for scatter in scatters:
        scatter.finish()


def mlp_back_fused(grad, down_w, gu_w, slope, gelu, hidden, low, d_tab, f_tab, dp):
    rows, model = grad.shape
    width = hidden.shape[2]
    messages = (dp // 4, 4, 3 * RANK, width // dp)
    anywhere = pl.BlockSpec(memory_space=pl.ANY)
    vmem = pl.BlockSpec(memory_space=pltpu.VMEM)
    return pl.pallas_call(
        functools.partial(mlp_back_kernel, rows),
        out_shape=(
            jax.ShapeDtypeStruct((rows, model), F32),
            jax.ShapeDtypeStruct((rows // 4, LANES), F32),
            jax.ShapeDtypeStruct(messages, BF16),
        ),
        in_specs=[vmem] + [anywhere] * 6 + [vmem] * 2,
        out_specs=(vmem,) * 3,
        scratch_shapes=[
            pltpu.VMEM((3 * RANK, width), F32),
            pltpu.VMEM((model, width), BF16),
            pltpu.VMEM((model, 2 * width), BF16),
            pltpu.VMEM((4, rows, model), BF16),
            pltpu.VMEM((2, rows, width), BF16),
            pltpu.VMEM((2, rows, width), BF16),
            pltpu.VMEM((2, rows, width), BF16),
            pltpu.VMEM((2, rows, LANES), BF16),
            pltpu.VMEM((rows, 2 * width), BF16),
            pltpu.SemaphoreType.DMA((2,)),
            pltpu.SemaphoreType.DMA((2, 4)),
            pltpu.SemaphoreType.DMA,
            pltpu.SemaphoreType.DMA((6,)),
            pltpu.SemaphoreType.DMA((6,)),
        ]
        + scatter_scratch(rows, model, model // tile_of(model))
        + scatter_scratch(rows // 4, LANES),
        compiler_params=pltpu.CompilerParams(
            collective_id=5, has_side_effects=True, vmem_limit_bytes=62 * 1024 * 1024
        ),
        name="mlp_back",
    )(grad, down_w, gu_w, slope, gelu, hidden, low, d_tab, f_tab)


def front_kernel(
    ids_ref,
    layer_ref,
    gains_ref,
    gate_up_table_hbm,
    hidden_table_hbm,
    in_table_hbm,
    resid_table_hbm,
    heads_table_hbm,
    query_table_hbm,
    key_value_table_hbm,
    query_hbm,
    key_hbm,
    value_hbm,
    output_hbm,
    gate_hbm,
    up_hbm,
    seq_out,
    ids_out,
    d_out,
    f_out,
    h_out,
    k_out,
    weight_out,
    gate_up_out,
    gate_up_all,
    hidden_all,
    in_all,
    resid_all,
    heads_all,
    query_all,
    key_value_all,
    normed,
    shard_pack,
    gate_up_pack,
    ids_own,
    ids_land,
    f_pick,
    d_pick,
    hk_pick,
    f_mid,
    d_mid,
    hk_mid,
    d_join,
    f_land,
    d_land,
    hk_land,
    d_flip,
    f_flip,
    h_flip,
    k_flip,
    local_sem,
    gather_send,
    gather_recv,
    line_send,
    line_recv,
    group_send,
    group_recv,
    shard_sem,
    table_sem,
    shard_send,
    shard_recv,
):
    rows = layer_ref.shape[0]
    sq = Square(rows)
    dp = lax.axis_size("dp")
    d = lax.axis_index("dp")
    peers = [{"tensor": peer} for peer in (sq.across, sq.down, sq.far)]
    peers += [{"dp": lax.rem(d + step, dp)} for step in range(1, dp)]
    call(peers)
    shards = Line(weight_out, shard_send, shard_recv)
    q_width, width = query_hbm.shape[1], gate_hbm.shape[1]
    kv_first = pl.multiple_of(sq.me * (q_width // HD) // (HQ // KV) * HD, HD)
    packs = [
        pltpu.make_async_copy(source, target, shard_sem.at[which])
        for which, (source, target) in enumerate(
            (
                (query_hbm, shard_pack.at[:, pl.ds(0, q_width)]),
                (key_hbm.at[:, pl.ds(kv_first, HD)], shard_pack.at[:, pl.ds(q_width, HD)]),
                (
                    value_hbm.at[:, pl.ds(kv_first, HD)],
                    shard_pack.at[:, pl.ds(q_width + HD, HD)],
                ),
                (output_hbm, shard_pack.at[:, pl.ds(q_width + 2 * HD, q_width)]),
                (gate_hbm, gate_up_pack.at[:, pl.ds(0, width)]),
                (up_hbm, gate_up_pack.at[:, pl.ds(width, width)]),
            )
        )
    ]
    table_loads = [
        pltpu.make_async_copy(source, target, table_sem.at[which])
        for which, (source, target) in enumerate(
            (
                (gate_up_table_hbm, gate_up_all),
                (hidden_table_hbm, hidden_all),
                (in_table_hbm, in_all),
                (resid_table_hbm, resid_all),
                (heads_table_hbm, heads_all),
                (query_table_hbm, query_all),
                (key_value_table_hbm, key_value_all),
            )
        )
    ]
    for copy in packs + table_loads:
        copy.start()
    keep_shard = pltpu.make_async_copy(shard_pack, weight_out.at[d], shard_sem.at[6])
    keep_gate_up = pltpu.make_async_copy(gate_up_pack, gate_up_out, shard_sem.at[7])
    ids_own[...] = jnp.full(ids_own.shape, ids_ref[0, 0], jnp.int32)
    for copy in packs[:4]:
        copy.wait()
    keep_shard.start()

    @pl.loop(0, rows // BLOCK)
    def _(step):
        here = pl.ds(pl.multiple_of(step * BLOCK, BLOCK), BLOCK)
        normed[here, :] = rms_norm(layer_ref[here, :].astype(F32), gains_ref[0:1, :]).astype(BF16)

    pl.semaphore_wait(pltpu.get_barrier_semaphore(), len(peers))
    keep_shard.wait()
    shards.start()
    line = along(lambda k: ids_own, ids_land, line_send.at[0], line_recv.at[0])
    for copy in packs[4:]:
        copy.wait()
    keep_gate_up.start()
    gather = PlainGather(sq.me, normed, seq_out, local_sem, gather_send, gather_recv)
    gather.start()
    pltpu.make_async_copy(ids_land, ids_land, line_recv.at[0]).wait()
    ids_out[...] = ids_land[...]

    for copy in table_loads:
        copy.wait()

    def pick(source, group):
        total = None
        for adapter in range(NA):
            hit = jnp.broadcast_to(ids_land[group, 0:1, 0:1], source.shape[1:]) == adapter
            mine = jnp.where(hit, source[adapter].astype(F32), 0.0)
            total = mine if total is None else total + mine
        return total

    @pl.loop(0, dp)
    def _(group):
        f_pick[group, : 2 * RANK, :] = pick(gate_up_all, group).astype(BF16)
        f_pick[group, 2 * RANK :, :] = pick(hidden_all, group).astype(BF16)
        d_pick[group, : UP.stop, :] = pick(in_all, group).T.astype(BF16)
        d_pick[group, UP.stop :, :] = pick(resid_all, group).astype(BF16)
        hk_pick[group, :RANK, :] = pick(heads_all, group).astype(BF16)
        hk_pick[group, RANK : 2 * RANK, :] = pick(query_all, group).astype(BF16)
        hk_pick[group, 2 * RANK :, : key_value_all.shape[2]] = pick(key_value_all, group).astype(
            BF16
        )

    lands = (f_mid, d_mid, hk_mid)
    for item, (source, target) in enumerate(zip((f_pick, d_pick, hk_pick), lands)):
        line += along(
            lambda k, source=source: source.at[k],
            target,
            line_send.at[1 + item],
            line_recv.at[1 + item],
        )
    shards.arrive(1, 0)
    gather.forward()
    for flip in (d_flip, f_flip, h_flip, k_flip):
        flip[...] = jnp.zeros_like(flip)
    for item, target in enumerate(lands):
        pltpu.make_async_copy(target, target, line_recv.at[1 + item]).wait()
    shards.arrive(1, 1)
    size = d_mid.shape[2]
    for k in range(dp):
        d_join[:, k * size : (k + 1) * size] = d_mid[k]
    per_user = dp // 4
    spread = [
        sq.spread(lambda peer: d_join, d_land, group_send.at[0], group_recv.at[0]),
        sq.spread(
            lambda peer: f_mid.at[pl.ds(peer * per_user, per_user)],
            f_land,
            group_send.at[1],
            group_recv.at[1],
        ),
        sq.spread(
            lambda peer: hk_mid.at[pl.ds(peer * per_user, per_user)],
            hk_land,
            group_send.at[2],
            group_recv.at[2],
        ),
    ]
    for copies in spread:
        for copy in copies:
            copy.start()
    shards.arrive(2, 0)
    for copies in spread:
        copies[0].wait()
        for copy in copies[1:]:
            copy.wait_recv()
    shards.arrive(2, 1)
    f_size, h_size, k_size = f_mid.shape[2], h_out.shape[0] // dp, k_out.shape[0] // dp
    for t in range(4):
        for k in range(dp):
            at = (k * 4 + t) * size
            d_flip[: DOWN.stop, at : at + size] = d_land[
                t, :, k * size : (k + 1) * size
            ].astype(F32)
        for core in range(per_user):
            at = (core * 4 + t) * f_size
            piece = f_land[t, core].astype(F32)
            f_flip[GATE.start : UP.stop, at : at + f_size] = piece[: 2 * RANK]
            f_flip[DOWN, at : at + f_size] = piece[2 * RANK :]
            piece = hk_land[t, core].astype(F32)
            at = (core * 4 + t) * h_size
            h_flip[OUT, at : at + h_size] = piece[:RANK, :h_size]
            h_flip[QUERY, at : at + h_size] = piece[RANK : 2 * RANK, :h_size]
            at = (core * 4 + t) * k_size
            k_flip[KEY.start : VALUE.stop, at : at + k_size] = piece[2 * RANK :, :k_size]
    for flip, out in ((d_flip, d_out), (f_flip, f_out), (h_flip, h_out), (k_flip, k_out)):

        @pl.loop(0, out.shape[0] // LANES)
        def _(step, flip=flip, out=out):
            here = columns(step, LANES)
            out[here, :] = flip[:, here].T.astype(BF16)

    shards.arrive(3, 0)
    gather.finish()
    shards.arrive(3, 1)
    for place in range(dp // 2):
        for part in range(2):
            shards.wait_sibling(place, part)
    shards.finish()
    keep_gate_up.wait()
    for copies in spread:
        for copy in copies[1:]:
            copy.wait_send()
    for copy in line:
        copy.wait_send()


def front(ids, layer_in, gains, adapters, weights, dp, widths):
    rows, model = layer_in.shape
    anywhere = pl.BlockSpec(memory_space=pl.ANY)
    vmem = pl.BlockSpec(memory_space=pltpu.VMEM)
    gate_up_all, hidden_all, in_all, resid_all, heads_all, query_all, key_value_all = adapters
    tile = (8, LANES)
    shapes = [
        (dp, gate_up_all.shape[1] + RANK, gate_up_all.shape[2]),
        (dp, in_all.shape[2] + resid_all.shape[1], in_all.shape[1]),
        (dp, 2 * RANK + key_value_all.shape[1], query_all.shape[2]),
    ]
    query, key, value, output, gate, up = weights
    shard = (query.shape[0], 2 * query.shape[1] + 2 * HD)
    gate_up = (gate.shape[0], 2 * gate.shape[1])
    joined = (shapes[1][1], dp * shapes[1][2])
    return pl.pallas_call(
        front_kernel,
        out_shape=(
            jax.ShapeDtypeStruct((4 * rows, model), BF16),
            jax.ShapeDtypeStruct((dp,) + tile, jnp.int32),
        )
        + tuple(jax.ShapeDtypeStruct((width, LANES), BF16) for width in widths)
        + (
            jax.ShapeDtypeStruct((dp,) + shard, BF16),
            jax.ShapeDtypeStruct(gate_up, BF16),
        ),
        in_specs=[pl.BlockSpec(memory_space=pltpu.SMEM)] + [vmem] * 2 + [anywhere] * 13,
        out_specs=(anywhere,) + (vmem,) * 5 + (anywhere,) * 2,
        scratch_shapes=[
            *(pltpu.VMEM(table.shape, BF16) for table in adapters),
            pltpu.VMEM((rows, model), BF16),
            pltpu.VMEM(shard, BF16),
            pltpu.VMEM(gate_up, BF16),
            pltpu.VMEM(tile, jnp.int32),
            pltpu.VMEM((dp,) + tile, jnp.int32),
        ]
        + [pltpu.VMEM(shape, BF16) for shape in shapes] * 2
        + [
            pltpu.VMEM(joined, BF16),
            pltpu.VMEM((4, dp // 4) + shapes[0][1:], BF16),
            pltpu.VMEM((4,) + joined, BF16),
            pltpu.VMEM((4, dp // 4) + shapes[2][1:], BF16),
        ]
        + [pltpu.VMEM((LANES, width), F32) for width in widths]
        + [
            pltpu.SemaphoreType.DMA,
            pltpu.SemaphoreType.DMA((3, 2)),
            pltpu.SemaphoreType.DMA((3, 2)),
            pltpu.SemaphoreType.DMA((4, dp)),
            pltpu.SemaphoreType.DMA((4,)),
            pltpu.SemaphoreType.DMA((3, 3)),
            pltpu.SemaphoreType.DMA((3, 4)),
            pltpu.SemaphoreType.DMA((8,)),
            pltpu.SemaphoreType.DMA((7,)),
            pltpu.SemaphoreType.DMA((3, dp // 2, 2)),
            pltpu.SemaphoreType.DMA((dp, 2)),
        ],
        compiler_params=pltpu.CompilerParams(
            collective_id=9, has_side_effects=True, vmem_limit_bytes=62 * 1024 * 1024
        ),
        name="front",
    )(ids, layer_in, gains, *adapters, *weights)


class Line:
    def __init__(self, slots, send_sem, recv_sem):
        self.d = lax.axis_index("dp")
        self.places = lax.axis_size("dp") // 2
        self.core = lax.rem(self.d, 2)
        self.z = self.d // 2
        self.sibling = self.d + 1 - 2 * self.core
        self.slots, self.send_sem, self.recv_sem = slots, send_sem, recv_sem

    def greet(self, others):
        barrier = pltpu.get_barrier_semaphore()
        for peer in others + [{"dp": self.sibling}]:
            pl.semaphore_signal(barrier, inc=1, device_id=peer, device_id_type=MESH)

        @pl.when(self.z > 0)
        def _():
            pl.semaphore_signal(
                barrier, inc=1, device_id={"dp": self.d - 2}, device_id_type=MESH
            )

        @pl.when(self.z < self.places - 1)
        def _():
            pl.semaphore_signal(
                barrier, inc=1, device_id={"dp": self.d + 2}, device_id_type=MESH
            )

        last = self.places - 1
        ends = (last - self.z) // last + self.z // last
        pl.semaphore_wait(barrier, len(others) + 3 - ends)

    def copy(self, place, kind, part):
        target = (self.d + 2, self.d - 2, self.sibling)[kind]
        slot = 2 * place + self.core
        half = self.slots.shape[1] // 2
        block = self.slots.at[slot, pl.ds(part * half, half)]
        return pltpu.make_async_remote_copy(
            src_ref=block,
            dst_ref=block,
            send_sem=self.send_sem.at[kind, place, part],
            recv_sem=self.recv_sem.at[slot, part],
            device_id={"dp": target},
            device_id_type=MESH,
        )

    def send_up(self, place, part):
        @pl.when(self.z < self.places - 1)
        def _():
            self.copy(place, 0, part).start()

    def send_down(self, place, part):
        @pl.when(self.z > 0)
        def _():
            self.copy(place, 1, part).start()

    def start(self):
        for part in range(2):
            self.send_up(self.z, part)
            self.send_down(self.z, part)
            self.copy(self.z, 2, part).start()

    def arrive(self, distance, part):
        @pl.when(self.z >= distance)
        def _():
            place = self.z - distance
            self.copy(place, 2, part).wait_recv()
            self.send_up(place, part)
            self.copy(place, 2, part).start()

        @pl.when(self.z + distance < self.places)
        def _():
            place = self.z + distance
            self.copy(place, 2, part).wait_recv()
            self.send_down(place, part)
            self.copy(place, 2, part).start()

    def wait_sibling(self, place, part):
        half = self.slots.shape[1] // 2
        other = 2 * place + 1 - self.core
        block = self.slots.at[other, pl.ds(part * half, half)]
        pltpu.make_async_copy(block, block, self.recv_sem.at[other, part]).wait()

    def finish(self):
        for place in range(self.places):
            for part in range(2):

                @pl.when((self.z >= place) & (self.z < self.places - 1))
                def _(place=place, part=part):
                    self.copy(place, 0, part).wait_send()

                @pl.when((self.z <= place) & (self.z > 0))
                def _(place=place, part=part):
                    self.copy(place, 1, part).wait_send()

                self.copy(place, 2, part).wait_send()


class HalfSpread:
    def __init__(self, sq, line, weight, columns_from, target, send_sem, recv_sem):
        model, width = target.shape[1:]
        share, part_rows = model // 2, model // 4
        cols = pl.ds(columns_from, width)

        def rows(part):
            return pl.ds(pl.multiple_of(line.core * share + part * part_rows, 8), part_rows)

        self.first, self.second, self.onward, self.sibling = [], [], [], []
        for order, group in enumerate((self.first, self.second)):
            for link in range(2):
                part = link if order == 0 else 1 - link
                sem = 2 * order + link
                group.append(
                    remote(
                        weight.at[rows(part), cols],
                        target.at[sq.me, rows(part)],
                        send_sem.at[sem],
                        recv_sem.at[sem],
                        sq.links[link],
                    )
                )
        for link in range(2):
            block = target.at[sq.links[link], rows(link)]
            self.onward.append(
                remote(
                    block, block, send_sem.at[4 + link], recv_sem.at[4 + link], sq.links[1 - link]
                )
            )
        mine = pl.ds(pl.multiple_of(line.core * share, 8), share)
        for which, peer in enumerate((sq.across, sq.down, sq.far)):
            block = target.at[peer, mine]
            self.sibling.append(
                pltpu.make_async_remote_copy(
                    src_ref=block,
                    dst_ref=block,
                    send_sem=send_sem.at[6 + which],
                    recv_sem=recv_sem.at[6 + which],
                    device_id={"dp": line.sibling},
                    device_id_type=MESH,
                )
            )

    def start(self):
        for copy in self.first + self.second:
            copy.start()

    def forward(self):
        for copy, onward in zip(self.first, self.onward):
            copy.wait_recv()
            onward.start()

    def share(self):
        for copy in self.second + self.onward:
            copy.wait_recv()
        for copy in self.sibling:
            copy.start()

    def finish(self):
        for copy in self.first + self.second + self.onward:
            copy.wait_send()
        for copy in self.sibling:
            copy.wait()


ARRIVALS = ((0, 1, 2, 3), (1, 0, 2, 3), (2, 1, 3, 0), (3, 2, 1, 0))


def mlp_kernel(
    rows,
    length_ref,
    x_hbm,
    gu_hbm,
    shard_hbm,
    weight_hbm,
    d_hbm,
    f_hbm,
    resid_hbm,
    cot_hbm,
    gains_ref,
    layer_ref,
    grad_ref,
    low_ref,
    low_down_ref,
    hidden_out,
    slope_out,
    gelu_out,
    down_out,
    w_kv_all,
    d_ref,
    f_table,
    resid_ref,
    cot_ref,
    work,
    low_sum,
    lows,
    seq,
    tiles,
    hidden,
    slope,
    gelu,
    down,
    load_sem,
    tile_sem,
    store_sem,
    keep_sem,
    line_send,
    line_recv,
    part,
    landing,
    passed,
    part_send,
    part_recv,
    w_send,
    w_recv,
    *low_scratch,
):
    sq = Square(rows)
    line = Line(down, line_send, line_recv)
    width = hidden.shape[-1]
    tile = tiles.shape[-1] // 2
    steps = width // tile
    own_shard = pltpu.make_async_copy(shard_hbm, down.at[line.d], load_sem.at[0])
    seq_load = pltpu.make_async_copy(x_hbm, seq, load_sem.at[1])

    def tile_loads(step, slot):
        return [
            pltpu.make_async_copy(
                gu_hbm.at[:, columns(step, tile, which * width)],
                tiles.at[slot, :, pl.ds(which * tile, tile)],
                tile_sem.at[slot, which],
            )
            for which in range(2)
        ]

    def stores(step, slot):
        here = columns(step, tile)
        return [
            pltpu.make_async_copy(
                source.at[slot], target.at[:, :, here], store_sem.at[slot, which]
            )
            for which, (source, target) in enumerate(((slope, slope_out), (gelu, gelu_out)))
        ]

    late = [
        pltpu.make_async_copy(source, target, load_sem.at[2 + which])
        for which, (source, target) in enumerate(
            ((d_hbm, d_ref), (f_hbm, f_table), (resid_hbm, resid_ref), (cot_hbm, cot_ref))
        )
    ]
    own_shard.start()
    seq_load.start()
    for copy in late:
        copy.start()
    for copy in tile_loads(0, 0):
        copy.start()
    line.greet([{"tensor": sq.across}, {"tensor": sq.down}])
    own_shard.wait()
    line.start()
    keys_from = (weight_hbm.shape[1] - w_kv_all.shape[2]) // 2
    spread = HalfSpread(sq, line, weight_hbm, keys_from, w_kv_all, w_send, w_recv)
    spread.start()
    seq_load.wait()
    for copy in late:
        copy.wait()

    @pl.loop(0, 4)
    def _(chunk):
        low = nn(seq[chunk], d_ref[...])
        lows[0, chunk] = band(low, GATE).astype(BF16)
        lows[1, chunk] = band(low, UP).astype(BF16)
        low_ref[chunk] = band(low, GATE, UP).astype(BF16)

    @pl.loop(0, steps)
    def _(step):
        slot = lax.rem(step, 2)
        for copy in tile_loads(step, slot):
            copy.wait()

        @pl.when(step + 1 < steps)
        def _():
            for copy in tile_loads(step + 1, 1 - slot):
                copy.start()

        @pl.when(step >= 2)
        def _():
            for copy in stores(step - 2, slot):
                copy.wait()

        here = columns(step, tile)

        @pl.loop(0, 4)
        def _(chunk):
            both = nn(seq[chunk], tiles[slot])
            gate = both[:, :tile] + nt(lows[0, chunk], f_table[here, :])
            up = both[:, tile:] + nt(lows[1, chunk], f_table[here, :])
            hidden[chunk, :, here], slope[slot, chunk], gelu[slot, chunk] = gelu_parts(gate, up)

        for copy in stores(step, slot):
            copy.start()

        for part_at, part_of in ((steps // 2 - 1, 0), (steps - 2, 1)):

            @pl.when(step == part_at)
            def _(part_of=part_of):
                line.arrive(1, part_of)
                if part_of == 0:
                    spread.forward()

    keep_hidden = pltpu.make_async_copy(hidden, hidden_out, keep_sem.at[0])
    keep_hidden.start()
    last = line.places - 1
    is_first, is_last = (last - line.z) // last, line.z // last
    is_third = line.z // 2 - is_last
    is_here = (is_first, 1 - is_first - is_third - is_last, is_third, is_last)
    order = [sum(flag * ARRIVALS[z][i] for z, flag in enumerate(is_here)) for i in range(4)]

    def scatter_at(place, half):
        at = 2 * place + half
        return ChunkScatter(
            sq, part.at[at], landing.at[at], passed.at[at], part_send.at[at], part_recv.at[at]
        )

    low_scatter = ChunkScatter(sq, *low_scratch)

    @pl.loop(0, 4)
    def _(chunk):
        low_scratch[0][chunk] = band(nn(hidden[chunk], f_table[...]), DOWN).astype(BF16)

    low_scatter.send_far()
    low_scatter.send_own()
    keeps = []
    earlier = low_scatter
    half_rows = down.shape[1] // 2
    arrivals = {(1, 0): ((2, 0),), (2, 0): ((2, 1),), (3, 0): ((3, 0),), (3, 1): ((3, 1),)}
    for turn in range(4):
        place = order[turn]
        for half in range(2):
            for distance, piece in arrivals.get((turn, half), ()):
                line.arrive(distance, piece)
            if (turn, half) == (1, 0):
                spread.share()
            line.wait_sibling(place, half)
            scatter = scatter_at(place, half)

            @pl.loop(0, 4)
            def _(step, place=place, half=half, scatter=scatter):
                chunk = far_first(step)
                for core in range(2):
                    part[
                        2 * place + half, chunk, :, core * half_rows : (core + 1) * half_rows
                    ] = nt(
                        hidden[chunk],
                        down[2 * place + core, half * half_rows : (half + 1) * half_rows],
                    ).astype(BF16)

                @pl.when(step == 0)
                def _():
                    scatter.send_far()

                @pl.when(step == 1)
                def _():
                    scatter.send_own()

            earlier.pass_on()
            earlier = scatter
        pair = pl.ds(2 * place, 2)
        keep = pltpu.make_async_copy(down.at[pair], down_out.at[pair], keep_sem.at[1 + turn])
        keep.start()
        keeps.append(keep)
    low_scatter.collect(low_sum)
    low_down_ref[...] = low_sum[...].astype(BF16)
    earlier.pass_on()
    everything = [(place, half) for place in range(4) for half in range(2)]
    for place, half in everything:
        first = 2 * place * down.shape[1] + half * half_rows
        scatter_at(place, half).collect(
            work, ((0, first), (half_rows, first + down.shape[1]))
        )
    add_lifted(work, low_down_ref, d_ref)

    @pl.loop(0, rows // BLOCK)
    def _(step):
        here = pl.ds(pl.multiple_of(step * BLOCK, BLOCK), BLOCK)
        at = sq.me * rows + step * BLOCK + lax.broadcasted_iota(jnp.int32, (BLOCK, 1), 0)
        valid = (at < length_ref[0]).astype(F32)
        total = work[here, :]
        gain = gains_ref[3:4, :]
        layer_ref[here, :] = (valid * (resid_ref[here, :] + rms_norm(total, gain))).astype(BF16)
        grad_ref[here, :] = norm_back(total, gain, cot_ref[here, :].astype(F32) * valid).astype(
            BF16
        )

    for place, half in everything:
        scatter_at(place, half).finish()
    low_scatter.finish()
    line.finish()
    spread.finish()
    for step in (steps - 2, steps - 1):
        for copy in stores(step, step % 2):
            copy.wait()
    keep_hidden.wait()
    for keep in keeps:
        keep.wait()


def add_lifted(work, low, table):
    wide = tile_of(work.shape[1])

    @pl.loop(0, work.shape[1] // wide)
    def _(step):
        here = columns(step, wide)
        work[:, here] += nt(low[...], table[here, :])


def mlp_fused(lengths, seq, gu_w, shard, attn_w, d_tab, f_tab, resid, cotangent, gains, dp):
    chunks, rows, model = seq.shape
    width = shard.shape[1]
    tile = 384
    wide = model // dp
    half = rows // 2
    anywhere = pl.BlockSpec(memory_space=pl.ANY)
    vmem = pl.BlockSpec(memory_space=pltpu.VMEM)
    saved = jax.ShapeDtypeStruct((4, rows, width), BF16)
    return pl.pallas_call(
        functools.partial(mlp_kernel, rows),
        out_shape=(
            jax.ShapeDtypeStruct((rows, model), BF16),
            jax.ShapeDtypeStruct((rows, model), BF16),
            jax.ShapeDtypeStruct((4, rows, LANES), BF16),
            jax.ShapeDtypeStruct((rows, LANES), BF16),
            saved,
            saved,
            saved,
            jax.ShapeDtypeStruct((dp,) + shard.shape, BF16),
            jax.ShapeDtypeStruct((4, model, 2 * HD), BF16),
        ),
        in_specs=[pl.BlockSpec(memory_space=pltpu.SMEM)] + [anywhere] * 8 + [vmem],
        out_specs=(vmem,) * 4 + (anywhere,) * 5,
        scratch_shapes=[
            *(pltpu.VMEM(array.shape, array.dtype) for array in (d_tab, f_tab, resid, cotangent)),
            pltpu.VMEM((rows, model), F32),
            pltpu.VMEM((rows, LANES), F32),
            pltpu.VMEM((2, 4, rows, LANES), BF16),
            pltpu.VMEM((4, rows, model), BF16),
            pltpu.VMEM((2, model, 2 * tile), BF16),
            pltpu.VMEM((4, rows, width), BF16),
            pltpu.VMEM((2, 4, rows, tile), BF16),
            pltpu.VMEM((2, 4, rows, tile), BF16),
            pltpu.VMEM((dp,) + shard.shape, BF16),
            pltpu.SemaphoreType.DMA((6,)),
            pltpu.SemaphoreType.DMA((2, 2)),
            pltpu.SemaphoreType.DMA((2, 2)),
            pltpu.SemaphoreType.DMA((5,)),
            pltpu.SemaphoreType.DMA((3, dp // 2, 2)),
            pltpu.SemaphoreType.DMA((dp, 2)),
            pltpu.VMEM((dp, 4, rows, wide), BF16),
            pltpu.VMEM((dp, 6, half, wide), BF16),
            pltpu.VMEM((dp, 2, half, wide), BF16),
            pltpu.SemaphoreType.DMA((dp, 6, 1)),
            pltpu.SemaphoreType.DMA((dp, 6, 1)),
            pltpu.SemaphoreType.DMA((9,)),
            pltpu.SemaphoreType.DMA((9,)),
        ]
        + scatter_scratch(rows, LANES),
        compiler_params=pltpu.CompilerParams(
            collective_id=7, has_side_effects=True, vmem_limit_bytes=62 * 1024 * 1024
        ),
        name="mlp",
    )(lengths, seq, gu_w, shard, attn_w, d_tab, f_tab, resid, cotangent, gains)


class Layout:
    def __init__(self):
        self.dp = lax.axis_size("dp")
        self.tensor = lax.axis_size("tensor")
        self.total = self.dp * self.tensor
        self.d = lax.axis_index("dp")
        self.t = lax.axis_index("tensor")
        self.me = self.d * self.tensor + self.t
        self.heads_here = HQ // self.tensor
        self.ratio = HQ // KV
        self.share = max(1, self.tensor // KV)
        self.kv_owners = self.total // KV
        self.kv_head = self.t * self.heads_here // self.ratio
        self.user = self.me // self.dp
        self.kv_slice_head = self.me // self.kv_owners

    def device(self, flat):
        return {"dp": flat // self.tensor, "tensor": lax.rem(flat, self.tensor)}


def greet_all(lay):
    barrier = pltpu.get_barrier_semaphore()

    def signal(step, unused):
        peer = lax.rem(lay.me + step, lay.total)
        pl.semaphore_signal(
            barrier, inc=1, device_id=lay.device(peer), device_id_type=MESH
        )
        return unused

    lax.fori_loop(1, lay.total, signal, 0)
    pl.semaphore_wait(barrier, lay.total - 1)


def send_or_keep(lay, sends, source, target, send_sem, recv_sem, flat, maybe_own):
    def far():
        return pltpu.make_async_remote_copy(
            src_ref=source,
            dst_ref=target,
            send_sem=send_sem,
            recv_sem=recv_sem,
            device_id=lay.device(flat),
            device_id_type=MESH,
        )

    if maybe_own is None:
        copy = far()
        copy.start()
        sends.append((None, copy))
        return

    @pl.when(maybe_own)
    def _():
        pltpu.make_async_copy(source, target, recv_sem).start()

    @pl.when(jnp.logical_not(maybe_own))
    def _():
        far().start()

    sends.append((maybe_own, far()))


def finish(sends, received):
    for own, copy in sends:
        if own is None:
            copy.wait_send()
        else:

            @pl.when(jnp.logical_not(own))
            def _(copy=copy):
                copy.wait_send()

    for target, sem in received:
        pltpu.make_async_copy(target, target, sem).wait()


def tables_kernel(d_ref, f_ref, h_ref, k_ref, do_ref, fo_ref, ho_ref, ko_ref, *sems):
    lay = Layout()
    send_sems, recv_sem = sems[:4], sems[4]
    greet_all(lay)
    sends = []
    for step in range(lay.dp):
        group = lax.rem(lay.d + step, lay.dp)
        flat = group * lay.tensor + lay.user
        own = (lay.user == lay.t) if step == 0 else None
        for item, (source, target) in enumerate(((f_ref, fo_ref), (h_ref, ho_ref))):
            send_or_keep(
                lay,
                sends,
                source.at[group],
                target.at[lax.rem(lay.me, lay.dp)],
                send_sems[item].at[step],
                recv_sem.at[item],
                flat,
                own,
            )
        for extra in range(lay.share):
            user = lay.kv_slice_head * lay.share + extra
            flat = group * lay.tensor + user
            send_or_keep(
                lay,
                sends,
                k_ref.at[group],
                ko_ref.at[lax.rem(lay.me, lay.kv_owners)],
                send_sems[2].at[step, extra],
                recv_sem.at[2],
                flat,
                (user == lay.t) if step == 0 else None,
            )
    pltpu.make_async_copy(d_ref.at[lay.d], do_ref.at[lay.me], recv_sem.at[3]).start()
    for step in range(1, lay.total):
        flat = lax.rem(lay.me + step, lay.total)
        send_or_keep(
            lay,
            sends,
            d_ref.at[flat // lay.tensor],
            do_ref.at[lay.me],
            send_sems[3].at[step],
            recv_sem.at[3],
            flat,
            None,
        )
    finish(
        sends,
        (
            (fo_ref, recv_sem.at[0]),
            (ho_ref, recv_sem.at[1]),
            (ko_ref, recv_sem.at[2]),
            (do_ref, recv_sem.at[3]),
        ),
    )


def grads_kernel(d_ref, f_ref, h_ref, k_ref, do_ref, fo_ref, ho_ref, ko_ref, *sems):
    lay = Layout()
    send_sems, recv_sem = sems[:4], sems[4]
    greet_all(lay)
    sends = []
    for step in range(lay.dp):
        slot = lax.rem(lay.d + step, lay.dp)
        flat = lay.t * lay.dp + slot
        for item, (source, target) in enumerate(((f_ref, fo_ref), (h_ref, ho_ref))):
            send_or_keep(
                lay,
                sends,
                source.at[slot],
                target.at[lay.d],
                send_sems[item].at[step],
                recv_sem.at[item],
                flat,
                flat == lay.me,
            )
    for step in range(lay.kv_owners):
        slot = lax.rem(lay.d + step, lay.kv_owners)
        flat = lay.kv_head * lay.kv_owners + slot
        send_or_keep(
            lay,
            sends,
            k_ref.at[slot],
            ko_ref.at[lay.d * lay.share + lax.rem(lay.t, lay.share)],
            send_sems[2].at[step // lay.share, step % lay.share],
            recv_sem.at[2],
            flat,
            flat == lay.me,
        )
    pltpu.make_async_copy(d_ref.at[lay.me], do_ref.at[lay.me], recv_sem.at[3]).start()
    for step in range(1, lay.total):
        flat = lax.rem(lay.me + step, lay.total)
        send_or_keep(
            lay,
            sends,
            d_ref.at[flat],
            do_ref.at[lay.me],
            send_sems[3].at[step],
            recv_sem.at[3],
            flat,
            None,
        )
    finish(
        sends,
        (
            (fo_ref, recv_sem.at[0]),
            (ho_ref, recv_sem.at[1]),
            (ko_ref, recv_sem.at[2]),
            (do_ref, recv_sem.at[3]),
        ),
    )


def exchange(kernel, name, number, arrays, outs, dp, total, share):
    anywhere = pl.BlockSpec(memory_space=pl.ANY)
    return pl.pallas_call(
        kernel,
        out_shape=tuple(jax.ShapeDtypeStruct(shape, BF16) for shape in outs),
        in_specs=[anywhere] * 4,
        out_specs=(anywhere,) * 4,
        scratch_shapes=[
            pltpu.SemaphoreType.DMA((dp,)),
            pltpu.SemaphoreType.DMA((dp,)),
            pltpu.SemaphoreType.DMA((dp, share)),
            pltpu.SemaphoreType.DMA((total,)),
            pltpu.SemaphoreType.DMA((4,)),
        ],
        compiler_params=pltpu.CompilerParams(
            collective_id=number, has_side_effects=True, vmem_limit_bytes=VMEM_LIMIT
        ),
        name=name,
    )(*arrays)


def chunk_start(sq, chunk, part):
    is_own = (3 - chunk) // 3
    is_far = chunk // 3
    near = 1 - is_own - is_far
    neighbour = sq.down if part == 1 else sq.across
    block = sq.me * is_own + sq.far * is_far + neighbour * near
    other_half = chunk // 2 - is_far
    half = 1 - other_half if part == 1 else other_half
    return pl.multiple_of(block * sq.rows + half * sq.half, sq.half)


def rotate_back(values, cosine, sine):
    first, second = values[:, : HD // 2], values[:, HD // 2 :]
    return jnp.concatenate([first * cosine + second * sine, second * cosine - first * sine], axis=1)


def turned(values):
    return values.astype(F32).T.astype(BF16)


def rotate_rows(values, cosine, sine):
    first, second = values[:, : HD // 2], values[:, HD // 2 :]
    return jnp.concatenate([first * cosine - second * sine, second * cosine + first * sine], axis=1)


def softmax_weights(keys, queries, start, half, length):
    shape = (keys.shape[0], queries.shape[0])
    key_at = lax.broadcasted_iota(jnp.int32, shape, 0)
    query_at = lax.rem(lax.broadcasted_iota(jnp.int32, shape, 1), half) + start
    allowed = (key_at <= query_at) & (key_at < length)
    squash = jnp.tanh(nt(keys, queries) * (1.0 / SOFT_CAP))
    return squash, jnp.where(allowed, jnp.exp(SOFT_CAP * squash), 0.0)


def stack_heads(ref, here, heads):
    return jnp.concatenate([ref[here, h * HD : (h + 1) * HD] for h in range(heads)], axis=0)


def far_first(step):
    return step + 3 * ((3 - step) // 3) - 3 * (step // 3)


def attn_kernel(
    rows,
    length_ref,
    seq_hbm,
    weight_hbm,
    d_table,
    h_table,
    k_table,
    cos_ref,
    sin_ref,
    layer_ref,
    gains_ref,
    q_ref,
    k_ref,
    kt_ref,
    v_ref,
    attended_ref,
    inverse_ref,
    low_ref,
    low_out_ref,
    total_ref,
    resid_ref,
    normed_ref,
    mlp_out,
    w_out_all,
    w_q_all,
    h_all,
    seq,
    weight,
    vt,
    low_sum,
    load_sem,
    own_sem,
    gather_send,
    gather_recv,
    h_send,
    h_recv,
    w_send,
    w_recv,
    *scratch,
):
    sq = Square(rows)
    half = sq.half
    model = total_ref.shape[-1]
    q_width = q_ref.shape[1]
    qkv_width = q_width + 2 * HD
    heads = q_width // HD
    wide = tile_of(model)
    weight_load = pltpu.make_async_copy(weight_hbm, weight, load_sem.at[0])
    seq_load = pltpu.make_async_copy(seq_hbm, seq, load_sem.at[1])
    weight_load.start()
    seq_load.start()
    line = Line(None, None, None)
    greet(
        [{"tensor": peer} for peer in (sq.across, sq.down, sq.far)] + [{"dp": line.sibling}]
    )
    out_spread = HalfSpread(
        sq, line, weight_hbm, qkv_width, w_out_all, w_send.at[0], w_recv.at[0]
    )
    q_spread = HalfSpread(sq, line, weight_hbm, 0, w_q_all, w_send.at[1], w_recv.at[1])
    out_spread.start()
    h_spread = sq.spread(lambda peer: h_table, h_all, h_send, h_recv)
    for copy in h_spread:
        copy.start()
    weight_load.wait()
    seq_load.wait()

    @pl.loop(0, 4)
    def _(block):
        here = pl.ds(pl.multiple_of(block * rows, rows), rows)
        low = band(nn(seq[block], d_table[...]), QUERY, VALUE).astype(BF16)
        low_ref[here, :] = low
        cosine, sine = cos_ref[here, :], sin_ref[here, :]
        for h in range(heads):
            column = slice(h * HD, (h + 1) * HD)
            query = nn(seq[block], weight[:, column]) + nt(
                band(low.astype(F32), QUERY).astype(BF16), h_table[column, :]
            )
            q_ref[here, column] = (rotate_rows(query, cosine, sine) * HD ** (-0.5)).astype(BF16)
        key = nn(seq[block], weight[:, q_width : q_width + HD]) + nt(
            band(low.astype(F32), KEY).astype(BF16), k_table[...]
        )
        key = rotate_rows(key, cosine, sine)
        k_ref[here, :] = key.astype(BF16)
        kt_ref[:, here] = key.T.astype(BF16)
        value = nn(seq[block], weight[:, q_width + HD : qkv_width]) + nt(
            band(low.astype(F32), VALUE).astype(BF16), k_table[...]
        )
        v_ref[here, :] = value.astype(BF16)
        vt[:, here] = value.T.astype(BF16)

    out_spread.forward()
    part, part_low = scratch[0], scratch[5]
    scatters = (ChunkScatter(sq, *scratch[:5]), ChunkScatter(sq, *scratch[5:10]))

    @pl.loop(0, 4)
    def _(step):
        chunk = far_first(step)
        for side in range(2):
            start = chunk_start(sq, chunk, side)
            here = pl.ds(start, half)
            unused, weights = softmax_weights(
                k_ref[...], stack_heads(q_ref, here, heads), start, half, length_ref[0]
            )
            inverse = 1.0 / jnp.sum(weights, axis=0, keepdims=True)
            mixed = nn(vt[...], (weights * inverse).astype(BF16)).T.astype(BF16)
            for h in range(heads):
                inverse_ref[h : h + 1, here] = inverse[:, h * half : (h + 1) * half]
                attended_ref[here, h * HD : (h + 1) * HD] = mixed[h * half : (h + 1) * half]

        attended = jnp.concatenate(
            [attended_ref[pl.ds(chunk_start(sq, chunk, side), half), :] for side in range(2)],
            axis=0,
        )
        part_low[chunk] = band(nn(attended, h_table[...]), OUT).astype(BF16)

        @pl.loop(0, model // wide)
        def _(tile):
            here = columns(tile, wide)
            part[chunk, :, here] = nt(attended, weight[here, qkv_width:]).astype(BF16)

            @pl.when(step == 0)
            def _():
                scatters[0].send(1, tile)

            @pl.when(step == 1)
            def _():
                scatters[0].send(0, tile)

        @pl.when(step == 0)
        def _():
            scatters[1].send_far()

        @pl.when(step == 1)
        def _():
            scatters[1].send_own()

    for scatter in scatters:
        scatter.pass_on()
    scatters[1].collect(low_sum)
    low_out_ref[...] = low_sum[...].astype(BF16)
    scatters[0].collect(total_ref)
    add_lifted(total_ref, low_out_ref, d_table)

    @pl.loop(0, rows // BLOCK)
    def _(step):
        here = pl.ds(pl.multiple_of(step * BLOCK, BLOCK), BLOCK)
        resid = layer_ref[here, :].astype(F32) + rms_norm(total_ref[here, :], gains_ref[1:2, :])
        resid_ref[here, :] = resid
        normed_ref[here, :] = rms_norm(resid, gains_ref[2:3, :]).astype(BF16)

    gather = ChunkGather(sq, normed_ref, mlp_out, gather_send, gather_recv)
    gather.start()
    own = pltpu.make_async_copy(normed_ref, mlp_out.at[0], own_sem)
    own.start()
    gather.wait_chunk(1)
    q_spread.start()
    out_spread.share()
    for chunk in range(2, 4):
        gather.wait_chunk(chunk)
    own.wait()
    q_spread.forward()
    for copy in h_spread:
        copy.wait()
    out_spread.finish()
    q_spread.share()
    q_spread.finish()
    gather.finish()
    for scatter in scatters:
        scatter.finish()


def attn_fused(lengths, seq, weight, d_tab, h_tab, k_tab, cosine, sine, layer_in, gains):
    rows, model = layer_in.shape
    q_width = weight.shape[1] - 2 * HD
    q_width //= 2
    qkv_width = q_width + 2 * HD
    anywhere = pl.BlockSpec(memory_space=pl.ANY)
    vmem = pl.BlockSpec(memory_space=pltpu.VMEM)
    narrow = jax.ShapeDtypeStruct((LEN, HD), BF16)
    return pl.pallas_call(
        functools.partial(attn_kernel, rows),
        out_shape=(
            jax.ShapeDtypeStruct((LEN, q_width), BF16),
            narrow,
            jax.ShapeDtypeStruct((HD, LEN), BF16),
            narrow,
            jax.ShapeDtypeStruct((LEN, q_width), BF16),
            jax.ShapeDtypeStruct((q_width // HD, LEN), F32),
            jax.ShapeDtypeStruct((LEN, LANES), BF16),
            jax.ShapeDtypeStruct((rows, LANES), BF16),
            jax.ShapeDtypeStruct((rows, model), F32),
            jax.ShapeDtypeStruct((rows, model), F32),
            jax.ShapeDtypeStruct((rows, model), BF16),
            jax.ShapeDtypeStruct((4, rows, model), BF16),
            jax.ShapeDtypeStruct((4, model, q_width), BF16),
            jax.ShapeDtypeStruct((4, model, q_width), BF16),
            jax.ShapeDtypeStruct((4, q_width, LANES), BF16),
        ),
        in_specs=[pl.BlockSpec(memory_space=pltpu.SMEM)] + [anywhere] * 2 + [vmem] * 7,
        out_specs=(vmem,) * 11 + (anywhere,) * 4,
        scratch_shapes=[
            pltpu.VMEM((4, rows, model), BF16),
            pltpu.VMEM(weight.shape, BF16),
            pltpu.VMEM((HD, LEN), BF16),
            pltpu.VMEM((rows, LANES), F32),
            pltpu.SemaphoreType.DMA((2,)),
            pltpu.SemaphoreType.DMA,
            pltpu.SemaphoreType.DMA((6,)),
            pltpu.SemaphoreType.DMA((6,)),
            pltpu.SemaphoreType.DMA((3,)),
            pltpu.SemaphoreType.DMA((4,)),
            pltpu.SemaphoreType.DMA((2, 9)),
            pltpu.SemaphoreType.DMA((2, 9)),
        ]
        + scatter_scratch(rows, model, model // tile_of(model))
        + scatter_scratch(rows, LANES),
        compiler_params=pltpu.CompilerParams(
            collective_id=8, has_side_effects=True, vmem_limit_bytes=62 * 1024 * 1024
        ),
        name="attn",
    )(lengths, seq, weight, d_tab, h_tab, k_tab, cosine, sine, layer_in, gains)


def attn_back_kernel(
    rows,
    ids_ref,
    length_ref,
    back_ref,
    low_gu_ref,
    resid_ref,
    total_ref,
    cot_ref,
    layer_hbm,
    gains_ref,
    weight_hbm,
    w_out_hbm,
    w_q_hbm,
    w_kv_hbm,
    seq_hbm,
    q_hbm,
    k_hbm,
    kt_hbm,
    v_hbm,
    attended_hbm,
    inverse_ref,
    cos_hbm,
    sin_hbm,
    low_hbm,
    d_table,
    h_all,
    k_table,
    normed_hbm,
    low_out_ref,
    grad_mlp_hbm,
    low_down_ref,
    f_ref,
    o_ref,
    in_out,
    heads_out,
    hidden_out,
    query_out,
    keyval_out,
    gateup_out,
    resid_out,
    q_ref,
    k_ref,
    kt_ref,
    v_ref,
    attended_ref,
    cos_ref,
    sin_ref,
    low_ref,
    normed_ref,
    grad_mlp_ref,
    layer_ref,
    slots,
    total,
    work,
    g_ref,
    buf,
    att_send,
    att,
    low_own,
    low_all,
    part_low,
    q_land,
    kv_land,
    low_land,
    q_grad,
    k_sum,
    v_sum,
    kv_grad,
    d_turned,
    h_turned,
    k_turned,
    d_send,
    d_land,
    d_sum,
    d_recv,
    f_land,
    f_recv,
    hk_send,
    hk_land,
    hk_recv,
    load_sem,
    late_sem,
    att_sends,
    att_recvs,
    back_sends,
    back_recvs,
    f_sem,
    f_send_sem,
    f_recv_sem,
    d_sem,
    hk_sem,
    group_send,
    group_recv,
    line_recv,
):
    sq = Square(rows)
    dp = lax.axis_size("dp")
    d = lax.axis_index("dp")
    model = o_ref.shape[-1]
    half = sq.half
    wide = tile_of(model)
    q_width = q_ref.shape[1]
    qkv_width = q_width + 2 * HD
    others = (sq.far, sq.across, sq.down)
    arrivals = ((sq.down, 2), (sq.far, 0), (sq.across, 1))
    sources = [w_out_hbm.at[peer] for peer in others]
    sources.append(weight_hbm.at[:, pl.ds(qkv_width, q_width)])
    sources.append(weight_hbm.at[:, pl.ds(0, q_width)])
    sources.append(weight_hbm.at[:, pl.ds(q_width, 2 * HD)])
    for peer, unused in arrivals:
        sources += [w_q_hbm.at[peer], w_kv_hbm.at[peer]]
    loads = [
        pltpu.make_async_copy(source, slots.at[which % 4], load_sem.at[1 + which])
        for which, source in enumerate(sources)
    ]
    seq_load = pltpu.make_async_copy(seq_hbm, buf, load_sem.at[0])
    late = [
        pltpu.make_async_copy(source, target, late_sem.at[which])
        for which, (source, target) in enumerate(
            (
                (q_hbm, q_ref),
                (k_hbm, k_ref),
                (kt_hbm, kt_ref),
                (v_hbm, v_ref),
                (attended_hbm, attended_ref),
                (cos_hbm, cos_ref),
                (sin_hbm, sin_ref),
                (low_hbm, low_ref),
                (normed_hbm, normed_ref),
                (grad_mlp_hbm, grad_mlp_ref),
                (layer_hbm, layer_ref),
            )
        )
    ]
    for copy in loads[:4]:
        copy.start()
    for copy in late:
        copy.start()
    seq_load.start()
    peers = [{"tensor": peer} for peer in (sq.across, sq.down, sq.far)]
    peers += [{"dp": lax.rem(d + step, dp)} for step in range(1, dp)]
    call(peers)

    low_gu = unpack_rows(low_gu_ref[...]).astype(BF16)

    @pl.loop(0, model // wide)
    def _(step):
        here = columns(step, wide)
        work[:, here] = back_ref[:, here] + nt(low_gu, d_table[here, :])

    @pl.loop(0, rows // BLOCK)
    def _(step):
        here = pl.ds(pl.multiple_of(step * BLOCK, BLOCK), BLOCK)
        at = sq.me * rows + step * BLOCK + lax.broadcasted_iota(jnp.int32, (BLOCK, 1), 0)
        valid = (at < length_ref[0]).astype(F32)
        mid = cot_ref[here, :].astype(F32) * valid + norm_back(
            resid_ref[here, :], gains_ref[2:3, :], work[here, :]
        )
        work[here, :] = mid
        g_ref[here, :] = norm_back(total_ref[here, :], gains_ref[1:2, :], mid).astype(BF16)

    low_out = band(nn(g_ref[...], d_table[...]), OUT).astype(BF16)
    low_own[...] = turned(low_out)[OUT]
    pl.semaphore_wait(pltpu.get_barrier_semaphore(), len(peers))
    heads_out_copies = []
    for which, peer in enumerate(others + (sq.me,)):
        loads[which].wait()
        grads = (nn(g_ref[...], slots[which]) + nt(low_out, h_all[peer])).astype(BF16)
        loads[which + 4].start()
        if which == 3:
            att[sq.me] = grads
            low_all[sq.me] = low_own[...]
            continue
        att_send[which] = grads
        copies = tuple(
            remote(
                source, target.at[sq.me], att_sends.at[which, item], att_recvs.at[which, item], peer
            )
            for item, (source, target) in enumerate(
                ((att_send.at[which], att), (low_own, low_all))
            )
        )
        for copy in copies:
            copy.start()
        heads_out_copies.append(copies)
    line = []
    f_spread = sq.spread(lambda peer: f_ref.at[:, peer], f_land, f_send_sem, f_recv_sem)
    for copy in f_spread:
        copy.start()
    back = []
    for which, peer in enumerate(others):
        here = pl.ds(pl.multiple_of(peer * rows, rows), rows)
        back.append(
            tuple(
                remote(
                    source,
                    target.at[sq.me],
                    back_sends.at[which, item],
                    back_recvs.at[which, item],
                    peer,
                )
                for item, (source, target) in enumerate(
                    (
                        (q_grad.at[here], q_land),
                        (kv_grad.at[here], kv_land),
                        (part_low.at[peer], low_land),
                    )
                )
            )
        )

    for copy in late:
        copy.wait()
    d_turned[...] = jnp.zeros_like(d_turned)
    low_grads = (
        (turned(low_gu)[GATE.start : UP.stop], normed_ref, slice(GATE.start, UP.stop)),
        (turned(low_out_ref[...])[OUT], g_ref, OUT),
        (turned(low_down_ref[...])[DOWN], grad_mlp_ref, DOWN),
    )

    @pl.loop(0, model // wide)
    def _(step):
        here = columns(step, wide)
        for low, source, place in low_grads:
            d_turned[place, here] = nn(low, source[:, here])

    h_turned[...] = jnp.zeros_like(h_turned)
    k_turned[...] = jnp.zeros_like(k_turned)
    k_sum[...] = jnp.zeros_like(k_sum)
    v_sum[...] = jnp.zeros_like(v_sum)
    heads = q_width // HD
    stacked = heads * half

    @pl.loop(0, 4)
    def _(turn):
        for step, (unused, which) in enumerate(arrivals):

            @pl.when(turn == step + 1)
            def _(which=which):
                for copy in heads_out_copies[which]:
                    copy.wait_recv()

        is_own, is_across = (3 - turn) // 3, turn // 3
        is_far = turn // 2 - is_across
        block = (
            sq.me * is_own
            + sq.far * is_far
            + sq.across * is_across
            + sq.down * (1 - is_own - is_far - is_across)
        )
        low_turned = low_all[block]
        h_turned[:RANK, :] += nn(
            low_turned, attended_ref[pl.ds(pl.multiple_of(block * rows, rows), rows), :]
        )
        for last in range(4):

            @pl.when(block == last)
            def _(last=last):
                seen = slice(0, (last + 1) * rows)

                @pl.loop(0, 2)
                def _(side):
                    start = pl.multiple_of(last * rows + side * half, half)
                    here = pl.ds(start, half)
                    place = pl.ds(pl.multiple_of(side * half, half), half)
                    queries = stack_heads(q_ref, here, heads)
                    grads = jnp.concatenate(
                        [att[last, place, h * HD : (h + 1) * HD] for h in range(heads)], axis=0
                    )
                    inverse = jnp.concatenate(
                        [inverse_ref[h : h + 1, here] for h in range(heads)], axis=1
                    )
                    squash, weights = softmax_weights(
                        k_ref[seen, :], queries, start, half, length_ref[0]
                    )
                    probs = weights * inverse
                    grad_probs = nt(v_ref[seen, :], grads)
                    mean = jnp.sum(probs * grad_probs, axis=0, keepdims=True)
                    grad_raw = (probs * (grad_probs - mean) * (1.0 - squash * squash)).astype(BF16)
                    k_sum[seen, :] += nn(grad_raw, queries)
                    v_sum[seen, :] += nn(probs.astype(BF16), grads)
                    q_back = nn(kt_ref[:, seen], grad_raw).T * HD ** (-0.5)
                    for h in range(heads):
                        q_grad[here, h * HD : (h + 1) * HD] = rotate_back(
                            q_back[h * half : (h + 1) * half], cos_ref[here, :], sin_ref[here, :]
                        ).astype(BF16)

        for step, (unused, which) in enumerate(arrivals):

            @pl.when(turn == step + 1)
            def _(which=which):
                back[which][0].start()

    kv_grad[:, :HD] = rotate_back(k_sum[...], cos_ref[...], sin_ref[...]).astype(BF16)
    kv_grad[:, HD:] = v_sum[...].astype(BF16)
    for copies in back:
        copies[1].start()
    f_spread[0].wait()
    for copy in f_spread[1:]:
        copy.wait_recv()
    line += along(lambda k: f_land.at[k // 2, lax.rem(k, 2)], f_recv, f_sem, line_recv.at[0])

    @pl.loop(0, 4)
    def _(block):
        here = pl.ds(pl.multiple_of(block * rows, rows), rows)
        low = (
            band(nn(q_grad[here, :], h_all[sq.me]), QUERY)
            + band(nn(kv_grad[here, :HD], k_table[...]), KEY)
            + band(nn(kv_grad[here, HD:], k_table[...]), VALUE)
        )
        part_low[block] = turned(low)[: VALUE.stop]

    for copies in back:
        copies[2].start()

    def add_block(queries, keys_values, which, first):
        for item in range(2):
            loads[which + item].wait()
        low_q, low_kv = which % 4, (which + 1) % 4

        @pl.loop(0, model // wide)
        def _(step):
            here = columns(step, wide)
            grad = nt(queries, slots[low_q, here, :]) + nt(keys_values, slots[low_kv, here, :])
            total[:, here] = grad if first else total[:, here] + grad

        for item in range(2):
            if which + item + 4 < len(loads):
                loads[which + item + 4].start()

    own = pl.ds(pl.multiple_of(sq.me * rows, rows), rows)
    add_block(q_grad[own, :], kv_grad[own, :], 4, True)
    seq_load.wait()

    @pl.loop(0, 4)
    def _(block):
        here = pl.ds(pl.multiple_of(block * rows, rows), rows)
        grad_turned = part_low[block]
        low_turned = turned(low_ref[here, :])
        h_turned[RANK : 2 * RANK, :] += nn(low_turned[QUERY], q_grad[here, :])
        k_turned[:RANK, :] += nn(low_turned[KEY], kv_grad[here, :HD])
        k_turned[RANK : 2 * RANK, :] += nn(low_turned[VALUE], kv_grad[here, HD:])

        @pl.loop(0, model // wide)
        def _(step):
            where = columns(step, wide)
            d_turned[: VALUE.stop, where] += nn(grad_turned, buf[block, :, where])

    @pl.loop(0, model // LANES)
    def _(step):
        here = columns(step, LANES)
        d_send[here, :] = d_turned[:, here].T.astype(BF16)

    d_rows = d_sum.shape[1]
    spread = []
    for k in range(dp):
        spread.append(
            sq.spread(
                lambda peer, k=k: d_send.at[pl.ds(pl.multiple_of((k * 4 + peer) * d_rows, 8), d_rows)],
                d_land.at[k],
                group_send.at[k],
                group_recv.at[k],
            )
        )
    cores = hk_send.shape[0]
    h_size, k_size = q_width // dp, HD // dp
    hk_send[...] = jnp.zeros_like(hk_send)
    for core in range(cores):
        for peer in range(4):
            at = core * 4 + peer
            hk_send[core, peer, : 2 * RANK, :h_size] = h_turned[
                : 2 * RANK, at * h_size : (at + 1) * h_size
            ].astype(BF16)
            hk_send[core, peer, 2 * RANK :, :k_size] = k_turned[
                : 2 * RANK, at * k_size : (at + 1) * k_size
            ].astype(BF16)
    spread.append(
        sq.spread(lambda peer: hk_send.at[:, peer], hk_land, group_send.at[dp], group_recv.at[dp])
    )
    for copies in spread:
        for copy in copies:
            copy.start()
    for step, (peer, which) in enumerate(arrivals):
        for copy in back[which]:
            copy.wait_recv()
        add_block(q_land[peer], kv_land[peer], 6 + 2 * step, False)
    for copies in spread:
        copies[0].wait()
        for copy in copies[1:]:
            copy.wait_recv()
    for k in range(dp):
        d_sum[k] = sum(d_land[k, t].astype(F32) for t in range(4)).astype(BF16)
    line += along(lambda k: d_sum.at[k], d_recv, d_sem, line_recv.at[1])
    line += along(lambda k: hk_land.at[k // 2, lax.rem(k, 2)], hk_recv, hk_sem, line_recv.at[2])
    low_total = sum(
        low_land[peer].astype(F32) for peer, unused in arrivals
    ) + part_low[sq.me].astype(F32)
    rest = jnp.zeros((LANES - VALUE.stop, rows), F32)
    low_qkv = turned(jnp.concatenate([low_total, rest], axis=0))

    @pl.loop(0, model // wide)
    def _(step):
        here = columns(step, wide)
        total[:, here] += nt(low_qkv, d_table[here, :])

    @pl.loop(0, rows // BLOCK)
    def _(step):
        here = pl.ds(pl.multiple_of(step * BLOCK, BLOCK), BLOCK)
        o_ref[here, :] = (
            work[here, :]
            + norm_back(layer_ref[here, :].astype(F32), gains_ref[0:1, :], total[here, :])
        ).astype(BF16)

    for item, target in enumerate((f_recv, d_recv, hk_recv)):
        pltpu.make_async_copy(target, target, line_recv.at[item]).wait()

    @pl.loop(0, NA)
    def _(adapter):
        def pick(received):
            total = None
            for group in range(dp):
                mine = jnp.where(
                    ids_ref[group] == adapter, received[group].astype(F32), 0.0
                )
                total = mine if total is None else total + mine
            return total

        d_all = pick(d_recv)
        in_out[adapter] = d_all[:, : 5 * RANK]
        d_flip = d_all.T
        f_all = pick(f_recv)
        hidden_out[adapter] = f_all[:RANK]
        hk_all = pick(hk_recv)
        heads_out[adapter] = hk_all[:RANK, :h_size]
        query_out[adapter] = hk_all[RANK : 2 * RANK, :h_size]
        for which in range(2):
            first = (which + 2) * RANK
            keyval_out[adapter, which] = hk_all[first : first + RANK, :k_size]
            first = (which + 1) * RANK
            gateup_out[adapter, which] = f_all[first : first + RANK]
            first = (which + 5) * RANK
            resid_out[adapter, which] = d_flip[first : first + RANK]

    for copies in spread + [f_spread]:
        for copy in copies[1:]:
            copy.wait_send()
    for copies in heads_out_copies + back:
        for copy in copies:
            copy.wait_send()
    for copy in line:
        copy.wait_send()


LATE = (12, 13, 14, 15, 16, 18, 19, 20, 24, 26, 5)


def attn_back_fused(scalars, arrays, grad_shapes, dp, total):
    anywhere = pl.BlockSpec(memory_space=pl.ANY)
    vmem = pl.BlockSpec(memory_space=pltpu.VMEM)
    smem = pl.BlockSpec(memory_space=pltpu.SMEM)
    rows, model = arrays[0].shape
    q, f_in = arrays[12], arrays[-1]
    q_width = q.shape[1]
    specs = [smem, smem] + [vmem] * len(arrays)
    late = [arrays[which] for which in LATE]
    for which in LATE + (7, 8, 9, 10, 11):
        specs[2 + which] = anywhere
    outs = [jax.ShapeDtypeStruct((rows, model), BF16)]
    outs += [jax.ShapeDtypeStruct(shape, F32) for shape in grad_shapes]
    d_rows = model // total
    messages = f_in.shape[2:]
    landed = (4, f_in.shape[0]) + messages
    return pl.pallas_call(
        functools.partial(attn_back_kernel, rows),
        out_shape=tuple(outs),
        in_specs=specs,
        out_specs=(vmem,) * len(outs),
        scratch_shapes=[
            *(pltpu.VMEM(array.shape, array.dtype) for array in late),
            pltpu.VMEM((4, model, q_width), BF16),
            pltpu.VMEM((rows, model), F32),
            pltpu.VMEM((rows, model), F32),
            pltpu.VMEM((rows, model), BF16),
            pltpu.VMEM((4, rows, model), BF16),
            pltpu.VMEM((3, rows, q_width), BF16),
            pltpu.VMEM((4, rows, q_width), BF16),
            pltpu.VMEM((RANK, rows), BF16),
            pltpu.VMEM((4, RANK, rows), BF16),
            pltpu.VMEM((4, 3 * RANK, rows), BF16),
            pltpu.VMEM((4, rows, q_width), BF16),
            pltpu.VMEM((4, rows, 2 * HD), BF16),
            pltpu.VMEM((4, 3 * RANK, rows), BF16),
            pltpu.VMEM((LEN, q_width), BF16),
            pltpu.VMEM((LEN, HD), F32),
            pltpu.VMEM((LEN, HD), F32),
            pltpu.VMEM((LEN, 2 * HD), BF16),
            pltpu.VMEM((LANES, model), F32),
            pltpu.VMEM((2 * RANK, q_width), F32),
            pltpu.VMEM((2 * RANK, HD), F32),
            pltpu.VMEM((model, LANES), BF16),
            pltpu.VMEM((dp, 4, d_rows, LANES), BF16),
            pltpu.VMEM((dp, d_rows, LANES), BF16),
            pltpu.VMEM((dp, d_rows, LANES), BF16),
            pltpu.VMEM(landed, BF16),
            pltpu.VMEM((dp,) + messages, BF16),
            pltpu.VMEM((dp // 4, 4, 4 * RANK, LANES), BF16),
            pltpu.VMEM((4, dp // 4, 4 * RANK, LANES), BF16),
            pltpu.VMEM((dp, 4 * RANK, LANES), BF16),
            pltpu.SemaphoreType.DMA((13,)),
            pltpu.SemaphoreType.DMA((len(late),)),
            pltpu.SemaphoreType.DMA((3, 2)),
            pltpu.SemaphoreType.DMA((3, 2)),
            pltpu.SemaphoreType.DMA((3, 3)),
            pltpu.SemaphoreType.DMA((3, 3)),
            pltpu.SemaphoreType.DMA((dp,)),
            pltpu.SemaphoreType.DMA((3,)),
            pltpu.SemaphoreType.DMA((4,)),
            pltpu.SemaphoreType.DMA((dp,)),
            pltpu.SemaphoreType.DMA((dp,)),
            pltpu.SemaphoreType.DMA((dp + 1, 3)),
            pltpu.SemaphoreType.DMA((dp + 1, 4)),
            pltpu.SemaphoreType.DMA((3,)),
        ],
        compiler_params=pltpu.CompilerParams(
            collective_id=6, has_side_effects=True, vmem_limit_bytes=62 * 1024 * 1024
        ),
        name="attn_back",
    )(*scalars, *arrays)


def per_device(
    layer_in,
    cotangent,
    lengths,
    adapter_ids,
    norm_gains,
    query_weight,
    key_weight,
    value_weight,
    out_weight,
    gate_weight,
    up_weight,
    down_weight,
    adapt_in,
    adapt_heads,
    adapt_hidden,
    lift_query,
    lift_keyval,
    lift_gateup,
    lift_resid,
):
    lay = Layout()
    count = lay.tensor
    rows = layer_in.shape[0]
    group_rows = rows * count
    assert lengths.shape[0] == 1 and group_rows == LEN
    heads_here = lay.heads_here
    head_width = heads_here * HD
    hidden_here = FF // count
    assert lay.ratio % heads_here == 0

    qkv_width = head_width + 2 * HD
    cosine, sine = tables(LEN, HD)
    if count == 4 and lay.dp == 8:
        adapters = (
            lift_gateup.reshape(NA, 2 * RANK, -1),
            jnp.swapaxes(adapt_hidden, 1, 2),
            adapt_in,
            lift_resid.reshape(NA, 2 * RANK, -1),
            jnp.swapaxes(adapt_heads, 1, 2),
            lift_query,
            lift_keyval.reshape(NA, 2 * RANK, -1),
        )
        seq_attn, all_ids, d_tab, f_tab, h_tab, k_tab, attn_w, gate_up_shard = front(
            adapter_ids,
            layer_in,
            norm_gains,
            adapters,
            (query_weight, key_weight, value_weight, out_weight.T, gate_weight, up_weight),
            lay.dp,
            (D, hidden_here, head_width, HD),
        )
        attn_w = attn_w.reshape(D, -1)
        down_shard = down_weight.T
        gate_up_w = lax.all_gather(gate_up_shard, "dp", axis=0, tiled=True)
        (
            queries,
            keys,
            keys_turned,
            values,
            attended,
            inverse,
            low_qkv,
            low_out,
            attn_total,
            resid_mid,
            normed_mlp,
            seq_mlp,
            w_out_all,
            w_q_all,
            h_all,
        ) = attn_fused(
            lengths,
            seq_attn.reshape(count, rows, D),
            attn_w,
            d_tab,
            h_tab,
            k_tab,
            cosine.reshape(LEN, HD // 2),
            sine.reshape(LEN, HD // 2),
            layer_in,
            norm_gains,
        )
        (
            layer_out,
            grad_mlp,
            low_gu,
            low_down,
            hidden,
            slope,
            gelu,
            down_w,
            w_kv_all,
        ) = mlp_fused(
            lengths,
            seq_mlp,
            gate_up_w,
            down_shard,
            attn_w,
            d_tab,
            f_tab,
            resid_mid,
            cotangent,
            norm_gains,
            lay.dp,
        )
        mlp_back, grad_low_gu, f_grad = mlp_back_fused(
            grad_mlp,
            down_w.reshape(D, hidden_here),
            gate_up_w,
            slope,
            gelu,
            hidden,
            low_gu,
            d_tab,
            f_tab,
            lay.dp,
        )
        grad_shapes = [
            table.shape
            for table in (
                adapt_in,
                adapt_heads,
                adapt_hidden,
                lift_query,
                lift_keyval,
                lift_gateup,
                lift_resid,
            )
        ]
        for which in (1, 2):
            shape = grad_shapes[which]
            grad_shapes[which] = (shape[0], shape[2], shape[1])
        grads = list(
            attn_back_fused(
                (all_ids[:, 0, 0], lengths),
                (
                    mlp_back,
                    grad_low_gu,
                    resid_mid,
                    attn_total,
                    cotangent,
                    layer_in,
                    norm_gains,
                    attn_w,
                    w_out_all,
                    w_q_all,
                    w_kv_all,
                    seq_attn.reshape(count, rows, D),
                    queries,
                    keys,
                    keys_turned,
                    values,
                    attended,
                    inverse,
                    cosine.reshape(LEN, HD // 2),
                    sine.reshape(LEN, HD // 2),
                    low_qkv,
                    d_tab,
                    h_all,
                    k_tab,
                    normed_mlp,
                    low_out,
                    grad_mlp,
                    low_down,
                    f_grad,
                ),
                tuple(grad_shapes),
                lay.dp,
                lay.total,
            )
        )
        for which in (2, 3):
            grads[which] = jnp.swapaxes(grads[which], 1, 2)
        return (layer_out, *grads)

    key_cols = lax.dynamic_slice_in_dim(key_weight, lay.kv_head * HD, HD, 1)
    value_cols = lax.dynamic_slice_in_dim(value_weight, lay.kv_head * HD, HD, 1)
    attn_shard = jnp.concatenate([query_weight, key_cols, value_cols, out_weight.T], axis=1)
    gate_up_shard = jnp.concatenate([gate_weight, up_weight], axis=1)
    down_shard = down_weight.T
    attn_w = lax.all_gather(attn_shard, "dp", axis=0, tiled=True)
    gate_up_w = lax.all_gather(gate_up_shard, "dp", axis=0, tiled=True)

    all_ids = lax.all_gather(adapter_ids[:, 0], "dp", axis=0, tiled=True)
    group_hot = (all_ids[:, None] == jnp.arange(NA, dtype=jnp.int32)[None, :]).astype(BF16)

    def rows_of(table):
        moved = jnp.moveaxis(table, -1, 1)
        return moved.reshape(NA, moved.shape[1], -1)

    def choose(*parts):
        packed = lanes(*parts)
        return lax.dot_general(
            group_hot, packed, (((1,), (0,)), ((), ())), preferred_element_type=F32
        ).astype(BF16)

    d_send = choose((QUERY, adapt_in), (OUT, rows_of(lift_resid)))
    f_send = choose((GATE, rows_of(lift_gateup)), (DOWN, adapt_hidden))
    h_send = choose((QUERY, rows_of(lift_query)), (OUT, adapt_heads))
    k_send = choose((KEY, rows_of(lift_keyval)))
    d_rows, f_rows, h_rows, k_rows = (item.shape[1] for item in (d_send, f_send, h_send, k_send))
    d_tab, f_tab, h_tab, k_tab = exchange(
        tables_kernel,
        "adapter_tables",
        3,
        (d_send, f_send, h_send, k_send),
        (
            (lay.total, d_rows, LANES),
            (lay.dp, f_rows, LANES),
            (lay.dp, h_rows, LANES),
            (lay.kv_owners, k_rows, LANES),
        ),
        lay.dp,
        lay.total,
        lay.share,
    )
    d_tab = d_tab.reshape(D, LANES)
    f_tab = f_tab.reshape(hidden_here, LANES)
    h_tab = h_tab.reshape(head_width, LANES)
    k_tab = k_tab.reshape(HD, LANES)
    in_qkv, in_gu = d_tab[:, : 3 * RANK], d_tab[:, 3 * RANK : 5 * RANK]
    lift_out, lift_down = d_tab[:, OUT], d_tab[:, DOWN]
    map_hidden, lift_gate, lift_up = f_tab[:, DOWN], f_tab[:, GATE], f_tab[:, UP]
    map_heads, lift_q = h_tab[:, OUT], h_tab[:, QUERY]
    lift_k, lift_v = k_tab[:, KEY], k_tab[:, VALUE]

    row_start = lay.t * rows
    length = lengths[0]
    row_valid = ((row_start + jnp.arange(rows, dtype=jnp.int32)) < length).astype(F32)[:, None]
    place = jnp.arange(LEN, dtype=jnp.int32)
    allowed = (place[:, None] >= place[None, :]) & (place[None, :] < length)

    resid_in = layer_in.astype(F32)
    normed_attn = rms_norm(resid_in, norm_gains[0]).astype(BF16)
    seq_attn = tensor_gather(normed_attn, count)
    low_qkv = nn(seq_attn, in_qkv).astype(BF16)
    low_q, low_k, low_v = (low_qkv[:, i * RANK : (i + 1) * RANK] for i in range(3))
    qkv = nn(seq_attn, attn_w[:, :qkv_width])
    query_pre = (qkv[:, :head_width] + nt(low_q, lift_q)).reshape(LEN, heads_here, HD)
    key_pre = (qkv[:, head_width : head_width + HD] + nt(low_k, lift_k)).reshape(LEN, 1, HD)
    value_pre = qkv[:, head_width + HD :] + nt(low_v, lift_v)
    queries = (rotate(query_pre, cosine, sine) * HD ** (-0.5)).astype(BF16)
    keys = rotate(key_pre, cosine, sine).astype(BF16).reshape(LEN, HD)
    values = value_pre.astype(BF16)

    def scores_of():
        raw = jnp.einsum("qhd,kd->hqk", queries, keys, preferred_element_type=F32)
        squash = jnp.tanh(raw / SOFT_CAP)
        return squash, jnp.where(allowed[None], jnp.exp(SOFT_CAP * squash), 0.0)

    squash, weights = scores_of()
    inverse_total = 1.0 / jnp.sum(weights, axis=-1, keepdims=True)
    attended = jnp.einsum(
        "hqk,kd->qhd", (weights * inverse_total).astype(BF16), values, preferred_element_type=F32
    )
    attended = attended.astype(BF16).reshape(LEN, head_width)
    w_out = attn_w[:, qkv_width:]
    out_part = nt(attended, w_out).astype(BF16)
    low_out_part = pad_lanes(nn(attended, map_heads).astype(BF16))
    attn_main, low_out = tensor_scatter(out_part, low_out_part, count)
    low_out = low_out[:, :RANK].astype(BF16)
    attn_total = attn_main + nt(low_out, lift_out)
    resid_mid = resid_in + rms_norm(attn_total, norm_gains[1])

    normed_mlp = rms_norm(resid_mid, norm_gains[2]).astype(BF16)
    seq_mlp = tensor_gather(normed_mlp, count)
    low_gu = nn(seq_mlp, in_gu).astype(BF16)
    low_g, low_u = low_gu[:, :RANK], low_gu[:, RANK:]
    w_gate, w_up = gate_up_w[:, :hidden_here], gate_up_w[:, hidden_here:]
    gate = nn(seq_mlp, w_gate) + nt(low_g, lift_gate)
    up = nn(seq_mlp, w_up) + nt(low_u, lift_up)
    hidden, slope, gelu = gelu_parts(gate, up)
    down_w = lax.all_gather(down_shard, "dp", axis=0, tiled=True)
    down_part = nt(hidden, down_w).astype(BF16)
    low_down_part = pad_lanes(nn(hidden, map_hidden).astype(BF16))
    mlp_main, low_down = tensor_scatter(down_part, low_down_part, count)
    low_down = low_down[:, :RANK].astype(BF16)
    mlp_total = mlp_main + nt(low_down, lift_down)
    layer_out = (row_valid * (resid_mid + rms_norm(mlp_total, norm_gains[3]))).astype(BF16)

    grad_out = cotangent.astype(F32) * row_valid
    grad_mlp = norm_back(mlp_total, norm_gains[3], grad_out).astype(BF16)
    seq_grad_mlp = tensor_gather(grad_mlp, count)
    grad_low_down = nn(seq_grad_mlp, lift_down).astype(BF16)
    grad_hidden = nn(seq_grad_mlp, down_w) + nt(grad_low_down, map_hidden)
    grad_gate = (grad_hidden * slope.astype(F32)).astype(BF16)
    grad_up = (grad_hidden * gelu.astype(F32)).astype(BF16)
    low_gu_part = pad_lanes(
        jnp.concatenate([nn(grad_gate, lift_gate), nn(grad_up, lift_up)], axis=1).astype(BF16)
    )
    mlp_back_part = (nt(grad_gate, w_gate) + nt(grad_up, w_up)).astype(BF16)
    mlp_back, grad_low_gu = tensor_scatter(mlp_back_part, low_gu_part, count)
    f_parts = [tn(hidden, grad_low_down), tn(grad_gate, low_g), tn(grad_up, low_u)]
    grad_low_gu = grad_low_gu[:, : 2 * RANK].astype(BF16)
    grad_normed_mlp = mlp_back + nt(grad_low_gu, in_gu)
    grad_mid = grad_out + norm_back(resid_mid, norm_gains[2], grad_normed_mlp)

    grad_attn = norm_back(attn_total, norm_gains[1], grad_mid).astype(BF16)
    seq_grad_attn = tensor_gather(grad_attn, count)
    grad_low_out = nn(seq_grad_attn, lift_out).astype(BF16)
    grad_attended = (nn(seq_grad_attn, w_out) + nt(grad_low_out, map_heads)).astype(BF16)
    grad_heads = grad_attended.reshape(LEN, heads_here, HD)
    probs = weights * inverse_total
    probs_low = probs.astype(BF16)
    grad_probs = jnp.einsum("qhd,kd->hqk", grad_heads, values, preferred_element_type=F32)
    grad_value = jnp.einsum("hqk,qhd->kd", probs_low, grad_heads, preferred_element_type=F32)
    grad_capped = probs * (grad_probs - jnp.sum(probs * grad_probs, axis=-1, keepdims=True))
    grad_raw = (grad_capped * (1.0 - squash * squash)).astype(BF16)
    grad_query = jnp.einsum("hqk,kd->qhd", grad_raw, keys, preferred_element_type=F32)
    grad_key = jnp.einsum("hqk,qhd->kd", grad_raw, queries, preferred_element_type=F32)
    grad_q_pre = rotate(grad_query * HD ** (-0.5), cosine, -sine).astype(BF16)
    grad_q_pre = grad_q_pre.reshape(LEN, head_width)
    grad_k_pre = rotate(grad_key.reshape(LEN, 1, HD), cosine, -sine).astype(BF16)
    grad_k_pre = grad_k_pre.reshape(LEN, HD)
    grad_v_pre = grad_value.astype(BF16)
    low_qkv_part = pad_lanes(
        jnp.concatenate(
            [nn(grad_q_pre, lift_q), nn(grad_k_pre, lift_k), nn(grad_v_pre, lift_v)], axis=1
        ).astype(BF16)
    )
    grad_qkv = jnp.concatenate([grad_q_pre, grad_k_pre, grad_v_pre], axis=1)
    attn_back_part = nt(grad_qkv, attn_w[:, :qkv_width]).astype(BF16)
    attn_back, grad_low_qkv = tensor_scatter(attn_back_part, low_qkv_part, count)
    grad_low_qkv = grad_low_qkv[:, : 3 * RANK].astype(BF16)
    grad_normed_attn = attn_back + nt(grad_low_qkv, in_qkv)
    input_grad = (grad_mid + norm_back(resid_in, norm_gains[0], grad_normed_attn)).astype(BF16)

    def packed(parts, blocks):
        return pad_lanes(jnp.concatenate(parts, axis=1).astype(BF16)).reshape(
            blocks, -1, LANES
        )

    d_grad = packed(
        [
            tn(normed_attn, grad_low_qkv),
            tn(normed_mlp, grad_low_gu),
            tn(grad_attn, low_out),
            tn(grad_mlp, low_down),
        ],
        lay.total,
    )
    f_grad = packed(f_parts, lay.dp)
    h_grad = packed([tn(attended, grad_low_out), tn(grad_q_pre, low_q)], lay.dp)
    k_grad = packed([tn(grad_k_pre, low_k), tn(grad_v_pre, low_v)], lay.kv_owners)
    d_all, f_all, h_all, k_all = exchange(
        grads_kernel,
        "adapter_grads",
        4,
        (d_grad, f_grad, h_grad, k_grad),
        (
            (lay.total, d_rows, LANES),
            (lay.dp, f_rows, LANES),
            (lay.dp, h_rows, LANES),
            (lay.dp * lay.share, k_rows, LANES),
        ),
        lay.dp,
        lay.total,
        lay.share,
    )

    def collect(received):
        repeats = received.shape[0] // lay.dp
        hot = jnp.repeat(group_hot, repeats, axis=0)
        return lax.dot_general(
            hot, received, (((0,), (0,)), ((), ())), preferred_element_type=F32
        )

    d_all, f_all, h_all, k_all = (collect(item) for item in (d_all, f_all, h_all, k_all))

    def lift_form(values, shape):
        return jnp.moveaxis(values, 1, 2).reshape(shape)

    return (
        layer_out,
        input_grad,
        d_all[:, :, : 5 * RANK],
        h_all[:, :, :RANK],
        f_all[:, :, :RANK],
        lift_form(h_all[:, :, RANK : 2 * RANK], lift_query.shape),
        lift_form(k_all[:, :, : 2 * RANK], lift_keyval.shape),
        lift_form(f_all[:, :, RANK : 3 * RANK], lift_gateup.shape),
        lift_form(d_all[:, :, 5 * RANK : 7 * RANK], lift_resid.shape),
    )


def solution(mesh):
    return jax.shard_map(
        per_device,
        mesh=mesh,
        in_specs=(
            P(("dp", "tensor"), None),
            P(("dp", "tensor"), None),
            P("dp"),
            P("dp", None),
            P(),
            P("dp", "tensor"),
            P("dp", None),
            P("dp", None),
            P("tensor", "dp"),
            P("dp", "tensor"),
            P("dp", "tensor"),
            P("tensor", "dp"),
            P(None, ("dp", "tensor"), None),
            P(None, ("dp", "tensor"), None),
            P(None, ("dp", "tensor"), None),
            P(None, None, ("dp", "tensor")),
            P(None, None, None, ("dp", "tensor")),
            P(None, None, None, ("dp", "tensor")),
            P(None, None, None, ("dp", "tensor")),
        ),
        out_specs=(
            P(("dp", "tensor"), None),
            P(("dp", "tensor"), None),
            P(None, ("dp", "tensor"), None),
            P(None, ("dp", "tensor"), None),
            P(None, ("dp", "tensor"), None),
            P(None, None, ("dp", "tensor")),
            P(None, None, None, ("dp", "tensor")),
            P(None, None, None, ("dp", "tensor")),
            P(None, None, None, ("dp", "tensor")),
        ),
        check_vma=False,
    )
```
